32 devices in a mesh: fsdp: 32 (over z, y, x, core).
Axes of the slice: x: 2, y: 2, z: 4, core: 2. Of those that a mesh axis runs over, the one named last changes fastest.
Arguments:
- tokens: bfloat16 [7680, 2304], P('fsdp'), may hold values from -6 to 6
- attn_weights: bfloat16 [2304, 6144], P('fsdp'), may hold values from -0.125 to 0.125
- mlp_weights: bfloat16 [2304, 27648], P('fsdp'), may hold values from -0.125 to 0.125
- norm_gains: bfloat16 [4, 2304], P(None, 'fsdp'), may hold values from -0.5 to 0.5
- seq_lengths: int32 [10], replicated, may hold values from 1 to 1024, 7680 in all
- cotangent: bfloat16 [7680, 2304], P('fsdp'), may hold values from -6 to 6
Outputs:
- layer_output: bfloat16 [7680, 2304], P('fsdp')
- grad_tokens: bfloat16 [7680, 2304], P('fsdp')
- grad_attn: float32 [2304, 6144], P('fsdp')
- grad_mlp: float32 [2304, 27648], P('fsdp')
- grad_gains: float32 [4, 2304], P(None, 'fsdp')
The draws below stay inside these ranges and needn't reach their ends.
Inputs may be any that keep to these rules, and one draw needn't show every extreme that they name: `seq_lengths`: the 10 sequences lie end to end over the 7680 tokens in the order of this array; the longest has exactly 1024 tokens.
All inputs are finite; a program needn't handle non-finite values.
Results may differ from the reference program's by a relative error of at most 0.017.
Values may be sent and summed in bfloat16 or wider, within the bound.
A program may use at most 896 MiB of HBM per device.

```python
import math
import jax
import jax.numpy as jnp
import numpy as np
from jax import lax

D = 2304
H = 8
KVH = 4
HD = 256
FF = 9216
LMAX = 1024
TOK_DEV = 240
TOKENS = 7680
NSEQ = 10


def block_levels(stream_key, extent, pieces, low, largest):
    def one(dim, shards_of):
        steps = jax.random.uniform(jax.random.fold_in(jax.random.fold_in(stream_key, 6), dim), (shards_of,), jnp.float32, low / len(pieces), largest / len(pieces))
        return jnp.repeat(jnp.exp(steps), extent[dim] // shards_of).reshape((-1,) + (1,) * (len(extent) - dim - 1))

    loudness = one(*pieces[0])
    for cut in pieces[1:]:
        loudness = loudness * one(*cut)
    return loudness


def profile(number_of, total, limit, skew):
    loads = [(1 << 20) // math.isqrt(rank ** skew) + 1 for rank in range(2, number_of + 1)]
    rest, counts = total - limit - (number_of - 1), [1] * (number_of - 1)
    while rest > 0:
        free = [i for i in range(number_of - 1) if counts[i] < limit]
        whole, remaining = sum([loads[i] for i in free]), rest
        for i in free:
            extra = min(limit - counts[i], max(1, remaining * loads[i] // whole), rest)
            counts[i] = counts[i] + extra
            rest = rest - extra
    return np.array([limit] + counts)


def ragged(rng, number_of, total, reach, slope):
    if number_of == 2:
        one = jax.random.randint(rng, (), max(1, total - reach), min(reach, total - 1) + 1)
        return jnp.stack([one, total - one])
    tallies = jnp.asarray(profile(number_of, total, reach, slope), jnp.int32)
    pairs = (number_of - 1) // 2
    giver, taker = tallies[1:1 + 2 * pairs:2], tallies[2:2 + 2 * pairs:2]
    margin = jnp.minimum(giver - 1, reach - taker)
    moved = jax.random.randint(jax.random.fold_in(rng, 1), (pairs,), 0, 1 << 20) % (margin + 1)
    tallies = tallies.at[1:1 + 2 * pairs:2].set(giver - moved).at[2:2 + 2 * pairs:2].set(taker + moved)
    return tallies[jax.random.permutation(jax.random.fold_in(rng, 2), number_of)]


def gaussian(own_key, shape, scale, reach, shards=(), kind=jnp.bfloat16):
    result = jax.random.normal(own_key, shape, jnp.float32) * scale
    if len(shards) > 0:
        result = block_levels(own_key, shape, shards, -0.22, 0.18) * result
    return jnp.clip(result, min=-reach, max=reach).astype(kind)


def setup_inputs(seed: int = 0) -> dict:
    arg_keys = jax.random.split(jax.random.key(seed), 7)
    return {
        "tokens": gaussian(arg_keys[0], (TOKENS, D), 1.0, 6.0, ((0, 32),)),
        "attn_weights": gaussian(arg_keys[1], (D, 2 * H * HD + 2 * KVH * HD), D ** -0.5, 0.125, ((0, 32),)),
        "mlp_weights": gaussian(arg_keys[2], (D, 3 * FF), D ** -0.5, 0.125, ((0, 32),)),
        "norm_gains": jnp.clip(jax.random.uniform(arg_keys[3], (4, D), jnp.float32, -0.5, 0.5) * block_levels(arg_keys[3], (4, D), ((1, 32),), -0.4, 0.0), -0.5, 0.5).astype(jnp.bfloat16),
        "seq_lengths": ragged(arg_keys[4], NSEQ, TOKENS, LMAX, 1).astype(jnp.int32),
        "cotangent": gaussian(arg_keys[5], (TOKENS, D), 1.0, 6.0, ((0, 32),)),
    }


EPSILON = 1e-06
SOFT_CAP = 50.0
MASK_VALUE = -1e+30
HIGHEST = lax.Precision.HIGHEST

@jax.custom_vjp
def low(v):
    return lax.optimization_barrier(v.astype(jnp.bfloat16)).astype(jnp.float32)

@jax.custom_vjp
def low_back(v):
    return v

def low_keep(v):
    return (low(v), None)

def low_pass(kept, grad):
    return (grad,)

def back_keep(v):
    return (v, None)

def back_low(kept, grad):
    return (low(grad),)
low.defvjp(low_keep, low_pass)
low_back.defvjp(back_keep, back_low)

def token_tables(seq_lengths, index_vec):
    seq_ends = jnp.cumsum(seq_lengths).astype(jnp.int32)
    after_end = index_vec[:, None] >= seq_ends[None, :]
    segment = lax.optimization_barrier(jnp.sum(after_end.astype(jnp.int32), axis=1)).astype(jnp.int32)
    earlier = lax.optimization_barrier(jnp.sum(jnp.where(after_end, seq_lengths[None, :], 0), axis=1)).astype(jnp.int32)
    return (segment, (index_vec - earlier).astype(jnp.int32))

def rms_scale(value, gain_vec):
    return value * lax.rsqrt(lax.optimization_barrier(jnp.mean(value * value, axis=-1, keepdims=True)) + EPSILON) * (1.0 + gain_vec)

def rotate(value, position, direction):
    half_width = value.shape[-1] // 2
    frequency = 10000.0 ** (-jnp.arange(half_width, dtype=jnp.float32) * 2.0 / value.shape[-1])
    angles = position.astype(jnp.float32)[:, None] * frequency[None, :]
    cosine = jnp.cos(angles)[:, None, :]
    sine_part = direction * jnp.sin(angles)[:, None, :]
    first_half = value[..., :half_width]
    second_half = value[..., half_width:]
    return jnp.concatenate([first_half * cosine - second_half * sine_part, second_half * cosine + first_half * sine_part], axis=-1)

def gelu_product(gate_up):
    half_width = gate_up.shape[-1] // 2
    return jax.nn.gelu(gate_up[:, :half_width], approximate=True) * gate_up[:, half_width:]

def attention(queries, key_rows, value_rows, seq_lengths):
    reach_devs = (LMAX - 2 + TOK_DEV) // TOK_DEV
    span_rows = (reach_devs + 1) * TOK_DEV
    lead_rows = reach_devs * TOK_DEV
    score_scale = HD ** (-0.5)
    padding = jnp.zeros((lead_rows, KVH, HD), jnp.float32)
    key_padded = jnp.concatenate([padding, key_rows], axis=0)
    value_padded = jnp.concatenate([padding, value_rows], axis=0)
    query_blocks = queries.reshape(TOKENS // TOK_DEV, TOK_DEV, KVH, H // KVH, HD)

    def one_block(block_args):
        block_index, query_block = block_args
        start_row = (block_index * TOK_DEV).astype(jnp.int32)
        key_window = lax.dynamic_slice_in_dim(key_padded, start_row, span_rows, 0)
        value_window = lax.dynamic_slice_in_dim(value_padded, start_row, span_rows, 0)
        query_index = start_row + jnp.arange(TOK_DEV, dtype=jnp.int32)
        key_index = start_row - lead_rows + jnp.arange(span_rows, dtype=jnp.int32)
        query_segment, unused_query = token_tables(seq_lengths, query_index)
        key_segment, unused_key = token_tables(seq_lengths, key_index)
        allowed = (key_segment[None, :] == query_segment[:, None]) & (key_index[None, :] <= query_index[:, None]) & (key_index[None, :] >= 0)
        raw_scores = low_back(jnp.einsum('qkgd,pkd->kgqp', query_block, key_window, precision=HIGHEST) * score_scale)
        capped = jnp.where(allowed[None, None], SOFT_CAP * jnp.tanh(raw_scores / SOFT_CAP), MASK_VALUE)
        weights = low(jax.nn.softmax(capped, axis=-1))
        mixed = jnp.einsum('kgqp,pkd->qkgd', weights, value_window, precision=HIGHEST)
        return mixed.reshape(TOK_DEV, H * HD)
    block_ids = jnp.arange(TOKENS // TOK_DEV, dtype=jnp.int32)
    mixed = lax.map(jax.checkpoint(one_block), (block_ids, query_blocks))
    return mixed.reshape(TOKENS, H * HD)

def layer_forward(inputs, attn_full, mlp_full, gain_rows, seq_lengths, position):
    query_width = H * HD
    key_width = KVH * HD
    proj_width = query_width + 2 * key_width
    normed = low(rms_scale(inputs, gain_rows[0]))
    projected = low_back(jnp.dot(normed, attn_full[:, :proj_width], precision=HIGHEST))
    queries = low(rotate(projected[:, :query_width].reshape(TOKENS, H, HD), position, 1.0))
    key_rows = low(rotate(projected[:, query_width:query_width + key_width].reshape(TOKENS, KVH, HD), position, 1.0))
    value_rows = low(projected[:, query_width + key_width:].reshape(TOKENS, KVH, HD))
    attended = low_back(low(attention(queries, key_rows, value_rows, seq_lengths)))
    attn_proj = low_back(jnp.dot(attended, attn_full[:, proj_width:].T, precision=HIGHEST))
    middle = inputs + rms_scale(attn_proj, gain_rows[1])
    normed_mid = low(rms_scale(middle, gain_rows[2]))
    gate_up = low_back(jnp.dot(normed_mid, mlp_full[:, :2 * FF], precision=HIGHEST))
    hidden = low(gelu_product(gate_up))
    mlp_raw = low_back(jnp.dot(hidden, mlp_full[:, 2 * FF:].T, precision=HIGHEST))
    return middle + rms_scale(mlp_raw, gain_rows[3])

def reference(tokens, attn_weights, mlp_weights, norm_gains, seq_lengths, cotangent):
    index_vec = jnp.arange(TOKENS, dtype=jnp.int32)
    unused_segment, position = token_tables(seq_lengths, index_vec)

    def forward(inputs, attn_full, mlp_full, gain_rows):
        return layer_forward(inputs, attn_full, mlp_full, gain_rows, seq_lengths, position)
    output, pullback = jax.vjp(forward, tokens.astype(jnp.float32), attn_weights.astype(jnp.float32), mlp_weights.astype(jnp.float32), norm_gains.astype(jnp.float32))
    grad_tokens, grad_attn, grad_mlp, grad_gains = pullback(cotangent.astype(jnp.float32))
    return (output.astype(jnp.bfloat16), grad_tokens.astype(jnp.bfloat16), grad_attn, grad_mlp, grad_gains)
```

```python
import jax
import jax.numpy as jnp
from jax import lax
from jax.sharding import PartitionSpec as P

H = 8
KVH = 4
HD = 256
LMAX = 1024
PLANE = 8

EPSILON = 1e-06
SOFT_CAP = 50.0
MASK_VALUE = -1e30
AXIS = "fsdp"
F32 = jnp.float32
BF16 = jnp.bfloat16


def token_tables(seq_lengths, index_vec):
    count = seq_lengths.shape[0]
    order = jnp.arange(count, dtype=jnp.int32)
    seq_ends = jnp.sum(
        jnp.where(order[None, :] <= order[:, None], seq_lengths[None, :], 0), axis=1
    )
    after_end = index_vec[:, None] >= seq_ends[None, :]
    segment = jnp.sum(after_end.astype(jnp.int32), axis=1)
    earlier = jnp.sum(jnp.where(after_end, seq_lengths[None, :], 0), axis=1)
    return (segment, index_vec - earlier)


def rms_parts(value):
    return lax.rsqrt(jnp.mean(value * value, axis=-1, keepdims=True) + EPSILON)


def rms_forward(value, gain_vec):
    return value * rms_parts(value) * (1.0 + gain_vec)


def rms_backward(value, gain_vec, grad):
    r = rms_parts(value)
    scaled = (1.0 + gain_vec) * grad
    inner = jnp.mean(value * scaled, axis=-1, keepdims=True)
    return (r * scaled - value * (r * r * r * inner), jnp.sum(grad * value * r, axis=0))


def rotate(value, cosine, sine_part):
    half_width = value.shape[-1] // 2
    first_half = value[..., :half_width]
    second_half = value[..., half_width:]
    return jnp.concatenate(
        [
            first_half * cosine - second_half * sine_part,
            second_half * cosine + first_half * sine_part,
        ],
        axis=-1,
    )


def contract_last(left_side, right_side):
    return lax.dot_general(
        left_side, right_side, (((1,), (1,)), ((), ())), preferred_element_type=F32
    )


def contract_first(left_side, right_side):
    return lax.dot_general(
        left_side, right_side, (((0,), (0,)), ((), ())), preferred_element_type=F32
    )


def matmul(left_side, right_side):
    return jnp.dot(left_side, right_side, preferred_element_type=F32)


def gelu_parts(gate):
    k0 = 0.7978845608028654
    k1 = 0.044715
    t = jnp.tanh(k0 * (gate + k1 * gate * gate * gate))
    value = 0.5 * gate * (1.0 + t)
    slope = 0.5 * (1.0 + t) + 0.5 * gate * (1.0 - t * t) * k0 * (1.0 + 3.0 * k1 * gate * gate)
    return (value, slope)


def windows(rows, block, span, count):
    return jnp.stack([rows[i * block : i * block + span] for i in range(count)])


def local(tokens, attn_weights, mlp_weights, norm_gains, seq_lengths, cotangent):
    tok_rows, width = tokens.shape
    peers = lax.axis_size(AXIS)
    planes = peers // PLANE
    row_share = attn_weights.shape[0]
    ff = mlp_weights.shape[1] // 3
    ffc = ff // PLANE
    plane_rows = PLANE * tok_rows
    halo = LMAX
    in_plane = [[p * PLANE + i for i in range(PLANE)] for p in range(planes)]
    across = [[p * PLANE + i for p in range(planes)] for i in range(PLANE)]
    sibling = [(i, i ^ 1) for i in range(peers)]
    to_next = [(i, i + PLANE) for i in range(peers - PLANE)]
    to_prev = [(i + PLANE, i) for i in range(peers - PLANE)]
    me = lax.axis_index(AXIS)
    is_even = (me % 2) == 0
    plane_start = (me // PLANE) * plane_rows

    def gather_plane(value):
        return lax.all_gather(value, AXIS, axis=0, tiled=True, axis_index_groups=in_plane)

    def scatter_plane(value):
        return lax.psum_scatter(
            value.astype(BF16), AXIS, scatter_dimension=0, tiled=True, axis_index_groups=in_plane
        ).astype(F32)

    def swap_plane(value):
        return lax.all_to_all(
            value, AXIS, split_axis=0, concat_axis=0, tiled=True, axis_index_groups=in_plane
        )

    def gather_across(value):
        return lax.all_gather(value, AXIS, axis=0, tiled=True, axis_index_groups=across)

    def scatter_across(value):
        return lax.psum_scatter(
            value.astype(BF16), AXIS, scatter_dimension=0, tiled=True, axis_index_groups=across
        )

    qw = attn_weights[:, : H * HD].reshape(row_share, PLANE, HD)
    kvw = attn_weights[:, H * HD : (H + 2 * KVH) * HD].reshape(row_share, 2, KVH, HD)
    kvw = kvw.transpose(0, 2, 1, 3).reshape(row_share, PLANE, HD)
    ow = attn_weights[:, (H + 2 * KVH) * HD :].reshape(row_share, PLANE, HD)
    attn_send = jnp.concatenate([qw, kvw, ow], axis=2).transpose(1, 0, 2)
    attn_send = attn_send.reshape(PLANE * row_share, 3 * HD)
    attn_cols = gather_across(swap_plane(attn_send))
    gain_full = lax.all_gather(norm_gains, AXIS, axis=1, tiled=True).astype(F32)
    gu_send = mlp_weights[:, : 2 * ff].reshape(row_share, 2, PLANE, ffc).transpose(2, 0, 1, 3)
    gu_cols = gather_across(swap_plane(gu_send.reshape(PLANE * row_share, 2 * ffc)))
    down_send = mlp_weights[:, 2 * ff :].reshape(row_share, PLANE, ffc).transpose(1, 0, 2)
    down_cols = gather_across(swap_plane(down_send.reshape(PLANE * row_share, ffc)))
    qkv_cols = attn_cols[:, : 2 * HD]
    out_cols = attn_cols[:, 2 * HD :]

    query_index = plane_start + jnp.arange(plane_rows, dtype=jnp.int32)
    key_index = plane_start - halo + jnp.arange(halo + plane_rows, dtype=jnp.int32)
    segment, position = token_tables(seq_lengths, query_index)
    key_segment, unused_key = token_tables(seq_lengths, key_index)
    frequency = 10000.0 ** (-jnp.arange(HD // 2, dtype=F32) * 2.0 / HD)
    angles = position.astype(F32)[:, None] * frequency[None, :]
    cosine, sine_part = jnp.cos(angles), jnp.sin(angles)
    kv_cosine = jnp.where(is_even, cosine, 1.0)
    kv_sine = jnp.where(is_even, sine_part, 0.0)

    inputs = tokens.astype(F32)
    normed = gather_plane(rms_forward(inputs, gain_full[0]).astype(BF16))
    projected = matmul(normed, qkv_cols)
    queries = rotate(projected[:, :HD], cosine, sine_part).astype(BF16)
    kv_own = rotate(projected[:, HD:], kv_cosine, kv_sine).astype(BF16)
    kv_halo = lax.ppermute(kv_own[plane_rows - halo :], AXIS, to_next)
    kv_mine = jnp.concatenate([kv_halo, kv_own], axis=0)
    kv_other = lax.ppermute(kv_mine, AXIS, sibling)
    key_rows = jnp.where(is_even, kv_mine, kv_other)
    value_rows = jnp.where(is_even, kv_other, kv_mine)

    block = tok_rows
    count = plane_rows // block
    span = halo + block
    score_scale = HD ** (-0.5)
    key_win = windows(key_rows, block, span, count)
    value_win = windows(value_rows, block, span, count)
    query_blk = queries.reshape(count, block, HD)
    allowed = (
        (windows(key_segment, block, span, count)[:, None, :] == segment.reshape(count, block, 1))
        & (windows(key_index, block, span, count)[:, None, :] <= query_index.reshape(count, block, 1))
        & (windows(key_index, block, span, count)[:, None, :] >= 0)
    )
    raw_scores = (
        jnp.einsum("bqd,bpd->bqp", query_blk, key_win, preferred_element_type=F32) * score_scale
    )
    bent = jnp.tanh(raw_scores / SOFT_CAP)
    capped = jnp.where(allowed, SOFT_CAP * bent, MASK_VALUE)
    row_max = jnp.max(capped, axis=-1, keepdims=True)
    exponent = jnp.exp(capped - row_max)
    row_total = jnp.sum(exponent, axis=-1, keepdims=True)
    probability = exponent / row_total
    weights = probability.astype(BF16)
    attended = (
        jnp.einsum("bqp,bpd->bqd", weights, value_win, preferred_element_type=F32)
        .reshape(plane_rows, HD)
        .astype(BF16)
    )
    attn_proj = scatter_plane(contract_last(attended, out_cols))

    middle = inputs + rms_forward(attn_proj, gain_full[1])
    mid_low = gather_plane(rms_forward(middle, gain_full[2]).astype(BF16))
    gate_up = matmul(mid_low, gu_cols)
    gate, up = gate_up[:, :ffc], gate_up[:, ffc:]
    gelu, slope = gelu_parts(gate)
    hidden = (gelu * up).astype(BF16)
    mlp_raw = scatter_plane(contract_last(hidden, down_cols))
    layer_output = (middle + rms_forward(mlp_raw, gain_full[3])).astype(BF16)

    grad_out = cotangent.astype(F32)
    grad_raw, gain_four = rms_backward(mlp_raw, gain_full[3], grad_out)
    grad_raw_low = gather_plane(grad_raw.astype(BF16))
    grad_hidden = matmul(grad_raw_low, down_cols)
    grad_gu = jnp.concatenate(
        [(slope * up * grad_hidden).astype(BF16), (gelu * grad_hidden).astype(BF16)], axis=1
    )
    down_term = scatter_across(contract_first(grad_raw_low, hidden))
    grad_normed_mid = scatter_plane(contract_last(grad_gu, gu_cols))
    gu_term = scatter_across(contract_first(mid_low, grad_gu))
    grad_mid_part, gain_three = rms_backward(middle, gain_full[2], grad_normed_mid)
    grad_middle = grad_out + grad_mid_part

    grad_proj, gain_two = rms_backward(attn_proj, gain_full[1], grad_middle)
    grad_proj_low = gather_plane(grad_proj.astype(BF16))
    grad_att = matmul(grad_proj_low, out_cols).astype(BF16)
    out_term = scatter_across(contract_first(grad_proj_low, attended))
    grad_blk = grad_att.reshape(count, block, HD)
    grad_prob = jnp.einsum("bqd,bpd->bqp", grad_blk, value_win, preferred_element_type=F32)
    inner_sum = jnp.sum(probability * grad_prob, axis=-1, keepdims=True)
    grad_scores = (probability * (grad_prob - inner_sum) * (1.0 - bent * bent)).astype(BF16)
    grad_query = (
        jnp.einsum("bqp,bpd->bqd", grad_scores, key_win, preferred_element_type=F32) * score_scale
    ).reshape(plane_rows, HD)
    key_parts = (
        jnp.einsum("bqp,bqd->bpd", grad_scores, query_blk, preferred_element_type=F32) * score_scale
    )
    value_parts = jnp.einsum("bqp,bqd->bpd", weights, grad_blk, preferred_element_type=F32)

    def joined(parts):
        total = jnp.zeros((halo + plane_rows, HD), F32)
        for i in range(count):
            total = total.at[i * block : i * block + span].add(parts[i])
        return total

    grad_keys, grad_values = joined(key_parts), joined(value_parts)
    grad_mine = jnp.where(is_even, grad_keys, grad_values)
    grad_give = jnp.where(is_even, grad_values, grad_keys).astype(BF16)
    grad_kv = grad_mine + lax.ppermute(grad_give, AXIS, sibling).astype(F32)
    grad_back = lax.ppermute(grad_kv[:halo].astype(BF16), AXIS, to_prev).astype(F32)
    grad_kv = grad_kv[halo:] + jnp.pad(grad_back, ((plane_rows - halo, 0), (0, 0)))
    grad_qkv = jnp.concatenate(
        [
            rotate(grad_query, cosine, -sine_part).astype(BF16),
            rotate(grad_kv, kv_cosine, -kv_sine).astype(BF16),
        ],
        axis=1,
    )
    qkv_term = scatter_across(contract_first(normed, grad_qkv))
    grad_normed = scatter_plane(contract_last(grad_qkv, qkv_cols))
    grad_in_part, gain_one = rms_backward(inputs, gain_full[0], grad_normed)
    grad_tokens = (grad_middle + grad_in_part).astype(BF16)

    gu_recv = swap_plane(gu_term).reshape(PLANE, row_share, 2, ffc)
    gu_rows = gu_recv.transpose(1, 2, 0, 3).reshape(row_share, 2 * ff)
    down_recv = swap_plane(down_term).reshape(PLANE, row_share, ffc)
    down_rows = down_recv.transpose(1, 0, 2).reshape(row_share, ff)
    grad_mlp = jnp.concatenate([gu_rows, down_rows], axis=1).astype(F32)
    out_recv = swap_plane(out_term).reshape(PLANE, row_share, HD)
    qkv_recv = swap_plane(qkv_term).reshape(PLANE, row_share, 2, HD)
    kv_recv = qkv_recv[:, :, 1].reshape(KVH, 2, row_share, HD)
    grad_attn = jnp.concatenate(
        [
            qkv_recv[:, :, 0].transpose(1, 0, 2).reshape(row_share, H * HD),
            kv_recv.transpose(2, 1, 0, 3).reshape(row_share, 2 * KVH * HD),
            out_recv.transpose(1, 0, 2).reshape(row_share, H * HD),
        ],
        axis=1,
    ).astype(F32)
    gain_term = jnp.stack([gain_one, gain_two, gain_three, gain_four], axis=0)
    gain_term = gain_term.reshape(4, peers, width // peers).transpose(1, 0, 2)
    gain_recv = lax.all_to_all(gain_term, AXIS, split_axis=0, concat_axis=0, tiled=True)
    grad_gains = jnp.sum(gain_recv, axis=0)
    return (layer_output, grad_tokens, grad_attn, grad_mlp, grad_gains)


def solution(mesh):
    return jax.shard_map(
        local,
        mesh=mesh,
        in_specs=(
            P("fsdp", None),
            P("fsdp", None),
            P("fsdp", None),
            P(None, "fsdp"),
            P(),
            P("fsdp", None),
        ),
        out_specs=(
            P("fsdp", None),
            P("fsdp", None),
            P("fsdp", None),
            P("fsdp", None),
            P(None, "fsdp"),
        ),
        check_vma=False,
    )
```

```python
import jax
import jax.numpy as jnp
from jax import lax
from jax.experimental import pallas as pl
from jax.experimental.pallas import tpu as pltpu
from jax.sharding import PartitionSpec as P

H = 8
KVH = 4
HD = 256
LMAX = 1024
PLANE = 8
QBLK = 128

EPSILON = 1e-06
SOFT_CAP = 50.0
AXIS = "fsdp"
F32 = jnp.float32
BF16 = jnp.bfloat16
MESH = pl.DeviceIdType.MESH
ANY = pl.BlockSpec(memory_space=pl.ANY)
VMEM = pl.BlockSpec(memory_space=pltpu.VMEM)
DMA = pltpu.SemaphoreType.DMA


def flip(index, step):
    return index + step - 2 * step * ((index // step) % 2)


def partner(index, bits):
    for step in (1, 2, 4):
        if bits & step:
            index = flip(index, step)
    return index


def greet(peers):
    barrier = pltpu.get_barrier_semaphore()
    for peer in peers:
        pl.semaphore_signal(barrier, inc=1, device_id=(peer,), device_id_type=MESH)
    pl.semaphore_wait(barrier, len(peers))


class Copies:
    def __init__(self, send_sem, recv_sem):
        self.send_sem, self.recv_sem, self.made = send_sem, recv_sem, []

    def start(self, source, target, device):
        slot = len(self.made)
        copy = pltpu.make_async_remote_copy(
            src_ref=source,
            dst_ref=target,
            send_sem=self.send_sem.at[slot],
            recv_sem=self.recv_sem.at[slot],
            device_id=(device,),
            device_id_type=MESH,
        )
        copy.start()
        self.made.append(copy)
        return copy

    def sent(self):
        for copy in self.made:
            copy.wait_send()


def band(index, size):
    return pl.ds(pl.multiple_of(index * size, 8), size)


def lanes(index, size):
    return pl.ds(pl.multiple_of(index * size, 128), size)


def gather_steps(block_ref, full_ref, copies, own_sem):
    rows, width = block_ref.shape
    half = width // 2
    me = lax.axis_index(AXIS)
    sib, xn, yn = flip(me, 1), flip(me, 2), flip(me, 4)
    diag = flip(xn, 4)

    def at(device, side):
        return full_ref.at[band(device % PLANE, rows), pl.ds(side * half, half)]

    def mine(side):
        return block_ref.at[:, pl.ds(side * half, half)]

    own_rows = full_ref.at[band(me % PLANE, rows)]
    xa = copies.start(mine(0), at(me, 0), xn)
    ya = copies.start(mine(1), at(me, 1), yn)
    xb = copies.start(mine(1), at(me, 1), xn)
    yb = copies.start(mine(0), at(me, 0), yn)
    arriving = [copies.start(block_ref, own_rows, sib)]
    own = pltpu.make_async_copy(block_ref, own_rows, own_sem)
    own.start()

    def finish():
        def to_sibling(device, side):
            arriving.append(copies.start(at(device, side), at(device, side), sib))

        xa.wait_recv()
        yc = copies.start(at(xn, 0), at(xn, 0), yn)
        to_sibling(xn, 0)
        ya.wait_recv()
        xc = copies.start(at(yn, 1), at(yn, 1), xn)
        to_sibling(yn, 1)
        xb.wait_recv()
        to_sibling(xn, 1)
        yb.wait_recv()
        to_sibling(yn, 0)
        yc.wait_recv()
        to_sibling(diag, 0)
        xc.wait_recv()
        to_sibling(diag, 1)
        for copy in arriving:
            copy.wait_recv()
        own.wait()

    return finish


GATHER_COPIES = 13


def gather_kernel(block_ref, full_ref, own_sem, send_sem, recv_sem):
    me = lax.axis_index(AXIS)
    greet((flip(me, 1), flip(me, 2), flip(me, 4)))
    copies = Copies(send_sem, recv_sem)
    gather_steps(block_ref, full_ref, copies, own_sem)()
    copies.sent()


def gather_plane(block):
    rows, width = block.shape
    return pl.pallas_call(
        gather_kernel,
        out_shape=jax.ShapeDtypeStruct((PLANE * rows, width), block.dtype),
        in_specs=[ANY],
        out_specs=ANY,
        scratch_shapes=[DMA(()), DMA((GATHER_COPIES,)), DMA((GATHER_COPIES,))],
        compiler_params=pltpu.CompilerParams(collective_id=1, has_side_effects=True),
        name="gather_plane",
    )(block)


def scatter_kernel(part_ref, out_ref, mine, got, ra, rb, ra2, rb2, load_sem, send_sem, recv_sem):
    rows, width = mine.shape[1:]
    half = width // 2
    step = 16
    me = lax.axis_index(AXIS)
    sib, xn, yn = flip(me, 1), flip(me, 2), flip(me, 4)
    diag = flip(xn, 4)
    left, right = pl.ds(0, half), pl.ds(half, half)
    greet((sib, xn, yn))
    copies = Copies(send_sem, recv_sem)

    def source(device):
        return part_ref.at[band(device % PLANE, rows)]

    loads, crossing = [], []
    for slot, device in enumerate((diag, xn, yn, me)):
        crossing.append(copies.start(source(flip(device, 1)), got.at[slot], sib))
        load = pltpu.make_async_copy(source(device), mine.at[slot], load_sem.at[slot])
        load.start()
        loads.append(load)

    def add(total, other):
        @pl.loop(0, rows // step)
        def _(k):
            r = pl.ds(pl.multiple_of(k * step, step), step)
            total[r] = (total[r].astype(F32) + other[r].astype(F32)).astype(total.dtype)

    def merge(slot):
        crossing[slot].wait_recv()
        loads[slot].wait()
        add(mine.at[slot], got.at[slot])

    merge(0)
    x0 = copies.start(mine.at[0, :, left], ra.at[0], xn)
    y0 = copies.start(mine.at[0, :, right], rb.at[0], yn)
    merge(1)
    x1 = copies.start(mine.at[1, :, left], ra.at[1], xn)
    merge(2)
    y1 = copies.start(mine.at[2, :, right], rb.at[1], yn)
    merge(3)
    x0.wait_recv()
    add(mine.at[2, :, left], ra.at[0])
    y2 = copies.start(mine.at[2, :, left], ra2, yn)
    y0.wait_recv()
    add(mine.at[1, :, right], rb.at[0])
    x2 = copies.start(mine.at[1, :, right], rb2, xn)
    for copy in (x1, y1, y2, x2):
        copy.wait_recv()

    @pl.loop(0, rows // step)
    def _(k):
        r = pl.ds(pl.multiple_of(k * step, step), step)
        out_ref[r, left] = mine[3, r, left].astype(F32) + ra[1, r].astype(F32) + ra2[r].astype(F32)
        out_ref[r, right] = mine[3, r, right].astype(F32) + rb[1, r].astype(F32) + rb2[r].astype(F32)

    copies.sent()


def scatter_plane(part):
    part = part.astype(BF16)
    rows, width = part.shape[0] // PLANE, part.shape[1]
    half = width // 2
    return pl.pallas_call(
        scatter_kernel,
        out_shape=jax.ShapeDtypeStruct((rows, width), F32),
        in_specs=[ANY],
        out_specs=VMEM,
        scratch_shapes=[
            pltpu.VMEM((4, rows, width), BF16),
            pltpu.VMEM((4, rows, width), BF16),
            pltpu.VMEM((2, rows, half), BF16),
            pltpu.VMEM((2, rows, half), BF16),
            pltpu.VMEM((rows, half), BF16),
            pltpu.VMEM((rows, half), BF16),
            DMA((4,)),
            DMA((10,)),
            DMA((10,)),
        ],
        compiler_params=pltpu.CompilerParams(
            collective_id=2, has_side_effects=True, vmem_limit_bytes=40 << 20
        ),
        name="scatter_plane",
    )(part)


def attn_columns(column):
    query_width = H * HD
    key_offset = query_width + (column % 2) * KVH * HD + (column // 2) * HD
    return (column * HD, key_offset, query_width + 2 * KVH * HD + column * HD)


def spread_attn_kernel(weights_ref, gain_ref, part_ref, gains_ref, own_sem, send_sem, recv_sem, gain_send, gain_recv):
    peers = gains_ref.shape[0]
    me = lax.axis_index(AXIS)
    barrier = pltpu.get_barrier_semaphore()

    def other(k):
        return lax.rem(me + k, peers)

    @pl.loop(1, peers)
    def _(k):
        pl.semaphore_signal(barrier, inc=1, device_id=(other(k),), device_id_type=MESH)

    pl.semaphore_wait(barrier, peers - 1)

    def gain_copy(k):
        return pltpu.make_async_remote_copy(
            src_ref=gain_ref,
            dst_ref=gains_ref.at[me],
            send_sem=gain_send.at[k],
            recv_sem=gain_recv.at[k],
            device_id=(other(k),),
            device_id_type=MESH,
        )

    @pl.loop(1, peers)
    def _(k):
        gain_copy(k).start()

    copies = Copies(send_sem, recv_sem)
    target_rows = me % PLANE
    for bits in (6, 2, 4, 7, 3, 5, 1):
        peer = partner(me, bits)
        for slot, offset in enumerate(attn_columns(peer % PLANE)):
            copies.start(
                weights_ref.at[:, pl.ds(pl.multiple_of(offset, 128), HD)],
                part_ref.at[target_rows, :, pl.ds(slot * HD, HD)],
                peer,
            )
    owns = []
    for slot, offset in enumerate(attn_columns(me % PLANE)):
        owns.append(
            pltpu.make_async_copy(
                weights_ref.at[:, pl.ds(pl.multiple_of(offset, 128), HD)],
                part_ref.at[target_rows, :, pl.ds(slot * HD, HD)],
                own_sem.at[slot],
            )
        )
    owns.append(pltpu.make_async_copy(gain_ref, gains_ref.at[me], own_sem.at[3]))
    for own in owns:
        own.start()
    for own in owns:
        own.wait()
    for copy in copies.made:
        copy.wait_recv()
    copies.sent()

    @pl.loop(1, peers)
    def _(k):
        gain_copy(k).wait()


def spread_attn(weights, gain_block, peers):
    rows = weights.shape[0]
    return pl.pallas_call(
        spread_attn_kernel,
        out_shape=(
            jax.ShapeDtypeStruct((PLANE, rows, 3 * HD), BF16),
            jax.ShapeDtypeStruct((peers,) + gain_block.shape, gain_block.dtype),
        ),
        in_specs=[ANY, ANY],
        out_specs=(ANY, ANY),
        scratch_shapes=[DMA((4,)), DMA((21,)), DMA((21,)), DMA((peers,)), DMA((peers,))],
        compiler_params=pltpu.CompilerParams(collective_id=3, has_side_effects=True),
        name="spread_attn",
    )(weights, gain_block)


def spread_mlp_kernel(weights_ref, block_ref, gu_ref, down_ref, full_ref, own_sem, send_sem, recv_sem):
    ffc = down_ref.shape[2]
    me = lax.axis_index(AXIS)
    greet([partner(me, bits) for bits in range(1, PLANE)])
    copies = Copies(send_sem, recv_sem)
    finish = gather_steps(block_ref, full_ref, copies, own_sem.at[3])
    target_rows = me % PLANE
    targets = (
        gu_ref.at[target_rows, :, pl.ds(0, ffc)],
        gu_ref.at[target_rows, :, pl.ds(ffc, ffc)],
        down_ref.at[target_rows],
    )
    owns, moved = [], []
    for bits in (6, 2, 4, 7, 3, 5, 1):
        peer = partner(me, bits)
        for slot in range(3):
            moved.append(
                copies.start(
                    weights_ref.at[:, lanes(slot * PLANE + peer % PLANE, ffc)], targets[slot], peer
                )
            )
    for slot in range(3):
        own = pltpu.make_async_copy(
            weights_ref.at[:, lanes(slot * PLANE + me % PLANE, ffc)],
            targets[slot],
            own_sem.at[slot],
        )
        own.start()
        owns.append(own)
    finish()
    for copy in moved:
        copy.wait_recv()
    for own in owns:
        own.wait()
    copies.sent()


def spread_mlp(weights, block):
    rows = weights.shape[0]
    ffc = weights.shape[1] // 3 // PLANE
    count = GATHER_COPIES + 21
    return pl.pallas_call(
        spread_mlp_kernel,
        out_shape=(
            jax.ShapeDtypeStruct((PLANE, rows, 2 * ffc), BF16),
            jax.ShapeDtypeStruct((PLANE, rows, ffc), BF16),
            jax.ShapeDtypeStruct((PLANE * block.shape[0], block.shape[1]), BF16),
        ),
        in_specs=[ANY, ANY],
        out_specs=(ANY, ANY, ANY),
        scratch_shapes=[DMA((4,)), DMA((count,)), DMA((count,))],
        compiler_params=pltpu.CompilerParams(collective_id=4, has_side_effects=True),
        name="spread_mlp",
    )(weights, block)


def collect_mlp_kernel(gu_ref, down_ref, rows_ref, own_sem, send_sem, recv_sem):
    ffc = down_ref.shape[2]
    me = lax.axis_index(AXIS)
    greet([partner(me, bits) for bits in range(1, PLANE)])
    copies = Copies(send_sem, recv_sem)

    def pieces(device):
        r = device % PLANE
        return (gu_ref.at[r, :, pl.ds(0, ffc)], gu_ref.at[r, :, pl.ds(ffc, ffc)], down_ref.at[r])

    targets = [rows_ref.at[:, lanes(slot * PLANE + me % PLANE, ffc)] for slot in range(3)]
    for bits in (6, 2, 4, 7, 3, 5, 1):
        peer = partner(me, bits)
        for source, target in zip(pieces(peer), targets):
            copies.start(source, target, peer)
    owns = []
    for slot, (source, target) in enumerate(zip(pieces(me), targets)):
        own = pltpu.make_async_copy(source, target, own_sem.at[slot])
        own.start()
        owns.append(own)
    for copy in copies.made:
        copy.wait_recv()
    for own in owns:
        own.wait()
    copies.sent()


def collect_mlp(gu_term, down_term):
    rows, ffc = down_term.shape[1:]
    return pl.pallas_call(
        collect_mlp_kernel,
        out_shape=jax.ShapeDtypeStruct((rows, 3 * PLANE * ffc), BF16),
        in_specs=[ANY, ANY],
        out_specs=ANY,
        scratch_shapes=[DMA((3,)), DMA((21,)), DMA((21,))],
        compiler_params=pltpu.CompilerParams(collective_id=5, has_side_effects=True),
        name="collect_mlp",
    )(gu_term, down_term)


def collect_attn_kernel(qkv_ref, out_ref, gain_ref, rows_ref, gains_ref, own_sem, send_sem, recv_sem, gain_send, gain_recv):
    peers = gain_ref.shape[0]
    me = lax.axis_index(AXIS)
    barrier = pltpu.get_barrier_semaphore()

    def other(k):
        return lax.rem(me + k, peers)

    @pl.loop(1, peers)
    def _(k):
        pl.semaphore_signal(barrier, inc=1, device_id=(other(k),), device_id_type=MESH)

    pl.semaphore_wait(barrier, peers - 1)
    copies = Copies(send_sem, recv_sem)

    def pieces(device):
        r = device % PLANE
        return (qkv_ref.at[r, :, pl.ds(0, HD)], qkv_ref.at[r, :, pl.ds(HD, HD)], out_ref.at[r])

    targets = [
        rows_ref.at[:, pl.ds(pl.multiple_of(offset, 128), HD)]
        for offset in attn_columns(me % PLANE)
    ]
    for bits in (6, 2, 4, 7, 3, 5, 1):
        peer = partner(me, bits)
        for source, target in zip(pieces(peer), targets):
            copies.start(source, target, peer)

    def gain_copy(k):
        return pltpu.make_async_remote_copy(
            src_ref=gain_ref.at[other(k)],
            dst_ref=gains_ref.at[me],
            send_sem=gain_send.at[k],
            recv_sem=gain_recv.at[k],
            device_id=(other(k),),
            device_id_type=MESH,
        )

    @pl.loop(1, peers)
    def _(k):
        gain_copy(k).start()

    owns = []
    for slot, (source, target) in enumerate(zip(pieces(me), targets)):
        owns.append(pltpu.make_async_copy(source, target, own_sem.at[slot]))
    owns.append(pltpu.make_async_copy(gain_ref.at[me], gains_ref.at[me], own_sem.at[3]))
    for own in owns:
        own.start()
    for own in owns:
        own.wait()
    for copy in copies.made:
        copy.wait_recv()
    copies.sent()

    @pl.loop(1, peers)
    def _(k):
        gain_copy(k).wait()


def collect_attn(qkv_term, out_term, gain_blocks):
    rows = qkv_term.shape[1]
    peers = gain_blocks.shape[0]
    return pl.pallas_call(
        collect_attn_kernel,
        out_shape=(
            jax.ShapeDtypeStruct((rows, PLANE * 3 * HD), BF16),
            jax.ShapeDtypeStruct(gain_blocks.shape, gain_blocks.dtype),
        ),
        in_specs=[ANY, ANY, ANY],
        out_specs=(ANY, ANY),
        scratch_shapes=[DMA((4,)), DMA((21,)), DMA((21,)), DMA((peers,)), DMA((peers,))],
        compiler_params=pltpu.CompilerParams(collective_id=6, has_side_effects=True),
        name="collect_attn",
    )(qkv_term, out_term, gain_blocks)


def block_scores(q, k, start, first):
    scores = lax.dot_general(q, k, (((1,), (1,)), ((), ())), preferred_element_type=F32)
    bent = jnp.tanh(scores * (HD ** (-0.5) / SOFT_CAP))
    rows, span = scores.shape
    key_at = lax.broadcasted_iota(jnp.int32, (rows, span), 1)
    row_at = lax.broadcasted_iota(jnp.int32, (rows, span), 0)
    allowed = (key_at + first >= start) & (key_at <= row_at + LMAX)
    return (bent, jnp.where(allowed, jnp.exp(SOFT_CAP * bent), 0.0))


def attend_kernel(q_ref, k_ref, v_ref, start_ref, out_ref, inv_ref):
    first = pl.program_id(0) * QBLK
    keys = pl.ds(pl.multiple_of(first, QBLK), LMAX + QBLK)
    unused_bent, exponent = block_scores(q_ref[...], k_ref[keys], start_ref[...], first)
    inverse = 1.0 / jnp.sum(exponent, axis=-1, keepdims=True)
    weights = (exponent * inverse).astype(BF16)
    out_ref[...] = jnp.dot(weights, v_ref[keys], preferred_element_type=F32).astype(BF16)
    inv_ref[...] = inverse


def attend(queries, key_rows, value_rows, starts):
    rows = queries.shape[0]
    span = key_rows.shape[0]
    row_spec = pl.BlockSpec((QBLK, HD), lambda i: (i, 0))
    one_spec = pl.BlockSpec((QBLK, 1), lambda i: (i, 0))
    all_spec = pl.BlockSpec((span, HD), lambda i: (0, 0))
    return pl.pallas_call(
        attend_kernel,
        out_shape=(
            jax.ShapeDtypeStruct((rows, HD), BF16),
            jax.ShapeDtypeStruct((rows, 1), F32),
        ),
        grid=(rows // QBLK,),
        in_specs=[row_spec, all_spec, all_spec, one_spec],
        out_specs=(row_spec, one_spec),
        compiler_params=pltpu.CompilerParams(vmem_limit_bytes=40 << 20),
        cost_estimate=pl.CostEstimate(
            flops=4 * rows * (LMAX + QBLK) * HD,
            transcendentals=2 * rows * (LMAX + QBLK),
            bytes_accessed=4 * rows * HD * 2,
        ),
        name="attend",
    )(queries, key_rows, value_rows, starts)


def attend_back_kernel(q_ref, k_ref, v_ref, start_ref, inv_ref, grad_ref, gq_ref, gk_ref, gv_ref):
    @pl.when(pl.program_id(0) == 0)
    def _():
        gk_ref[...] = jnp.zeros_like(gk_ref)
        gv_ref[...] = jnp.zeros_like(gv_ref)

    first = pl.program_id(0) * QBLK
    keys = pl.ds(pl.multiple_of(first, QBLK), LMAX + QBLK)
    q, k, v, grad = q_ref[...], k_ref[keys], v_ref[keys], grad_ref[...]
    bent, exponent = block_scores(q, k, start_ref[...], first)
    probability = exponent * inv_ref[...]
    grad_prob = lax.dot_general(grad, v, (((1,), (1,)), ((), ())), preferred_element_type=F32)
    inner = jnp.sum(probability * grad_prob, axis=-1, keepdims=True)
    grad_scores = (probability * (grad_prob - inner) * (1.0 - bent * bent)).astype(BF16)
    scale = HD ** (-0.5)
    gq_ref[...] = jnp.dot(grad_scores, k, preferred_element_type=F32) * scale
    over_rows = (((0,), (0,)), ((), ()))
    gk_ref[keys] += lax.dot_general(grad_scores, q, over_rows, preferred_element_type=F32) * scale
    gv_ref[keys] += lax.dot_general(
        probability.astype(BF16), grad, over_rows, preferred_element_type=F32
    )


def attend_back(queries, key_rows, value_rows, starts, inverse, grad):
    rows = queries.shape[0]
    span = key_rows.shape[0]
    row_spec = pl.BlockSpec((QBLK, HD), lambda i: (i, 0))
    one_spec = pl.BlockSpec((QBLK, 1), lambda i: (i, 0))
    all_spec = pl.BlockSpec((span, HD), lambda i: (0, 0))
    return pl.pallas_call(
        attend_back_kernel,
        out_shape=(
            jax.ShapeDtypeStruct((rows, HD), F32),
            jax.ShapeDtypeStruct((span, HD), F32),
            jax.ShapeDtypeStruct((span, HD), F32),
        ),
        grid=(rows // QBLK,),
        in_specs=[row_spec, all_spec, all_spec, one_spec, one_spec, row_spec],
        out_specs=(row_spec, all_spec, all_spec),
        compiler_params=pltpu.CompilerParams(vmem_limit_bytes=48 << 20),
        cost_estimate=pl.CostEstimate(
            flops=10 * rows * (LMAX + QBLK) * HD,
            transcendentals=2 * rows * (LMAX + QBLK),
            bytes_accessed=12 * rows * HD * 2,
        ),
        name="attend_back",
    )(queries, key_rows, value_rows, starts, inverse, grad)


def token_tables(seq_lengths, index_vec):
    count = seq_lengths.shape[0]
    order = jnp.arange(count, dtype=jnp.int32)
    seq_ends = jnp.sum(
        jnp.where(order[None, :] <= order[:, None], seq_lengths[None, :], 0), axis=1
    )
    after_end = index_vec[:, None] >= seq_ends[None, :]
    return index_vec - jnp.sum(jnp.where(after_end, seq_lengths[None, :], 0), axis=1)


def rms_parts(value):
    return lax.rsqrt(jnp.mean(value * value, axis=-1, keepdims=True) + EPSILON)


def rms_forward(value, gain_vec):
    return value * rms_parts(value) * (1.0 + gain_vec)


def rms_backward(value, gain_vec, grad):
    r = rms_parts(value)
    scaled = (1.0 + gain_vec) * grad
    inner = jnp.mean(value * scaled, axis=-1, keepdims=True)
    return (r * scaled - value * (r * r * r * inner), jnp.sum(grad * value * r, axis=0))


def rotate(value, cosine, sine_part):
    half_width = value.shape[-1] // 2
    first_half = value[..., :half_width]
    second_half = value[..., half_width:]
    return jnp.concatenate(
        [
            first_half * cosine - second_half * sine_part,
            second_half * cosine + first_half * sine_part,
        ],
        axis=-1,
    )


def contract_last(left_side, right_side):
    return lax.dot_general(
        left_side, right_side, (((1,), (1,)), ((), ())), preferred_element_type=F32
    )


def contract_first(left_side, right_side):
    return lax.dot_general(
        left_side, right_side, (((0,), (0,)), ((), ())), preferred_element_type=F32
    )


def matmul(left_side, right_side):
    return jnp.dot(left_side, right_side, preferred_element_type=F32)


def gelu_parts(gate):
    k0 = 0.7978845608028654
    k1 = 0.044715
    t = jnp.tanh(k0 * (gate + k1 * gate * gate * gate))
    value = 0.5 * gate * (1.0 + t)
    slope = 0.5 * (1.0 + t) + 0.5 * gate * (1.0 - t * t) * k0 * (1.0 + 3.0 * k1 * gate * gate)
    return (value, slope)


def local(tokens, attn_weights, mlp_weights, norm_gains, seq_lengths, cotangent):
    tok_rows, width = tokens.shape
    peers = lax.axis_size(AXIS)
    planes = peers // PLANE
    share = width // peers
    ff = mlp_weights.shape[1] // 3
    ffc = ff // PLANE
    plane_rows = PLANE * tok_rows
    halo = LMAX
    across = [[p * PLANE + i for p in range(planes)] for i in range(PLANE)]
    sibling = [(i, i ^ 1) for i in range(peers)]
    to_next = [(i, i + PLANE) for i in range(peers - PLANE)]
    to_prev = [(i + PLANE, i) for i in range(peers - PLANE)]
    me = lax.axis_index(AXIS)
    is_even = (me % 2) == 0
    plane_start = (me // PLANE) * plane_rows

    def gather_across(value):
        return lax.all_gather(value, AXIS, axis=0, tiled=True, axis_index_groups=across)

    def scatter_across(value):
        part = lax.psum_scatter(
            value.astype(BF16), AXIS, scatter_dimension=0, tiled=True, axis_index_groups=across
        )
        return part.reshape(PLANE, -1, part.shape[1])

    gain_block = jnp.pad(norm_gains.astype(F32), ((0, 8 - 4), (0, -share % 128)))
    attn_part, gain_blocks = spread_attn(attn_weights, gain_block, peers)
    attn_cols = gather_across(attn_part.reshape(-1, 3 * HD))
    gain_full = gain_blocks[:, :4, :share].transpose(1, 0, 2).reshape(4, width)
    inputs = tokens.astype(F32)
    gu_part, down_part, normed = spread_mlp(
        mlp_weights, rms_forward(inputs, gain_full[0]).astype(BF16)
    )
    gu_cols = gather_across(gu_part.reshape(-1, 2 * ffc))
    down_cols = gather_across(down_part.reshape(-1, ffc))
    qkv_cols = attn_cols[:, : 2 * HD]
    out_cols = attn_cols[:, 2 * HD :]

    query_index = plane_start + jnp.arange(plane_rows, dtype=jnp.int32)
    position = token_tables(seq_lengths, query_index)
    starts = (jnp.arange(plane_rows, dtype=jnp.int32) + halo - position)[:, None]
    frequency = 10000.0 ** (-jnp.arange(HD // 2, dtype=F32) * 2.0 / HD)
    angles = position.astype(F32)[:, None] * frequency[None, :]
    cosine, sine_part = jnp.cos(angles), jnp.sin(angles)
    kv_cosine = jnp.where(is_even, cosine, 1.0)
    kv_sine = jnp.where(is_even, sine_part, 0.0)

    projected = matmul(normed, qkv_cols)
    queries = rotate(projected[:, :HD], cosine, sine_part).astype(BF16)
    kv_own = rotate(projected[:, HD:], kv_cosine, kv_sine).astype(BF16)
    kv_halo = lax.ppermute(kv_own[plane_rows - halo :], AXIS, to_next)
    kv_mine = jnp.concatenate([kv_halo, kv_own], axis=0)
    kv_other = lax.ppermute(kv_mine, AXIS, sibling)
    key_rows = jnp.where(is_even, kv_mine, kv_other)
    value_rows = jnp.where(is_even, kv_other, kv_mine)
    attended, inverse = attend(queries, key_rows, value_rows, starts)
    attn_proj = scatter_plane(contract_last(attended, out_cols))

    middle = inputs + rms_forward(attn_proj, gain_full[1])
    mid_low = gather_plane(rms_forward(middle, gain_full[2]).astype(BF16))
    gate_up = matmul(mid_low, gu_cols)
    gate, up = gate_up[:, :ffc], gate_up[:, ffc:]
    gelu, slope = gelu_parts(gate)
    hidden = (gelu * up).astype(BF16)
    mlp_raw = scatter_plane(contract_last(hidden, down_cols))
    layer_output = (middle + rms_forward(mlp_raw, gain_full[3])).astype(BF16)

    grad_out = cotangent.astype(F32)
    grad_raw, gain_four = rms_backward(mlp_raw, gain_full[3], grad_out)
    grad_raw_low = gather_plane(grad_raw.astype(BF16))
    grad_hidden = matmul(grad_raw_low, down_cols)
    grad_gu = jnp.concatenate(
        [(slope * up * grad_hidden).astype(BF16), (gelu * grad_hidden).astype(BF16)], axis=1
    )
    down_term = scatter_across(contract_first(grad_raw_low, hidden))
    grad_normed_mid = scatter_plane(contract_last(grad_gu, gu_cols))
    gu_term = scatter_across(contract_first(mid_low, grad_gu))
    grad_mid_part, gain_three = rms_backward(middle, gain_full[2], grad_normed_mid)
    grad_middle = grad_out + grad_mid_part

    grad_proj, gain_two = rms_backward(attn_proj, gain_full[1], grad_middle)
    grad_proj_low = gather_plane(grad_proj.astype(BF16))
    grad_att = matmul(grad_proj_low, out_cols).astype(BF16)
    out_term = scatter_across(contract_first(grad_proj_low, attended))
    grad_query, grad_keys, grad_values = attend_back(
        queries, key_rows, value_rows, starts, inverse, grad_att
    )
    grad_mine = jnp.where(is_even, grad_keys, grad_values)
    grad_give = jnp.where(is_even, grad_values, grad_keys).astype(BF16)
    grad_kv = grad_mine + lax.ppermute(grad_give, AXIS, sibling).astype(F32)
    grad_back = lax.ppermute(grad_kv[:halo].astype(BF16), AXIS, to_prev).astype(F32)
    grad_kv = grad_kv[halo:] + jnp.pad(grad_back, ((plane_rows - halo, 0), (0, 0)))
    grad_qkv = jnp.concatenate(
        [
            rotate(grad_query, cosine, -sine_part).astype(BF16),
            rotate(grad_kv, kv_cosine, -kv_sine).astype(BF16),
        ],
        axis=1,
    )
    qkv_term = scatter_across(contract_first(normed, grad_qkv))
    grad_normed = scatter_plane(contract_last(grad_qkv, qkv_cols))
    grad_in_part, gain_one = rms_backward(inputs, gain_full[0], grad_normed)
    grad_tokens = (grad_middle + grad_in_part).astype(BF16)

    grad_mlp = collect_mlp(gu_term, down_term).astype(F32)
    gain_term = jnp.stack([gain_one, gain_two, gain_three, gain_four], axis=0)
    gain_term = gain_term.reshape(4, peers, share).transpose(1, 0, 2)
    gain_term = jnp.pad(gain_term, ((0, 0), (0, 8 - 4), (0, -share % 128)))
    attn_rows, gain_recv = collect_attn(qkv_term, out_term, gain_term)
    grad_attn = attn_rows.astype(F32)
    grad_gains = jnp.sum(gain_recv[:, :4, :share], axis=0)
    return (layer_output, grad_tokens, grad_attn, grad_mlp, grad_gains)


def solution(mesh):
    return jax.shard_map(
        local,
        mesh=mesh,
        in_specs=(
            P("fsdp", None),
            P("fsdp", None),
            P("fsdp", None),
            P(None, "fsdp"),
            P(),
            P("fsdp", None),
        ),
        out_specs=(
            P("fsdp", None),
            P("fsdp", None),
            P("fsdp", None),
            P("fsdp", None),
            P(None, "fsdp"),
        ),
        check_vma=False,
    )
```

```python
import jax
import jax.numpy as jnp
from jax import lax
from jax.experimental import pallas as pl
from jax.experimental.pallas import tpu as pltpu
from jax.sharding import PartitionSpec as P

H = 8
KVH = 4
HD = 256
LMAX = 1024
PLANE = 8
QBLK = 128

EPSILON = 1e-06
SOFT_CAP = 50.0
AXIS = "fsdp"
F32 = jnp.float32
BF16 = jnp.bfloat16
MESH = pl.DeviceIdType.MESH
ANY = pl.BlockSpec(memory_space=pl.ANY)
VMEM = pl.BlockSpec(memory_space=pltpu.VMEM)
DMA = pltpu.SemaphoreType.DMA


def flip(index, step):
    return index + step - 2 * step * ((index // step) % 2)


def partner(index, bits):
    for step in (1, 2, 4):
        if bits & step:
            index = flip(index, step)
    return index


def greet(peers):
    barrier = pltpu.get_barrier_semaphore()
    for peer in peers:
        pl.semaphore_signal(barrier, inc=1, device_id=(peer,), device_id_type=MESH)
    pl.semaphore_wait(barrier, len(peers))


class Copies:
    def __init__(self, send_sem, recv_sem):
        self.send_sem, self.recv_sem, self.made = send_sem, recv_sem, []

    def start(self, source, target, device):
        slot = len(self.made)
        copy = pltpu.make_async_remote_copy(
            src_ref=source,
            dst_ref=target,
            send_sem=self.send_sem.at[slot],
            recv_sem=self.recv_sem.at[slot],
            device_id=(device,),
            device_id_type=MESH,
        )
        copy.start()
        self.made.append(copy)
        return copy

    def sent(self):
        for copy in self.made:
            copy.wait_send()


def band(index, size):
    return pl.ds(pl.multiple_of(index * size, 8), size)


def lanes(index, size):
    return pl.ds(pl.multiple_of(index * size, 128), size)


def gather_steps(block_ref, full_ref, copies, own_sem):
    rows, width = block_ref.shape
    half = width // 2
    me = lax.axis_index(AXIS)
    sib, xn, yn = flip(me, 1), flip(me, 2), flip(me, 4)
    diag = flip(xn, 4)

    def at(device, side):
        return full_ref.at[band(device % PLANE, rows), pl.ds(side * half, half)]

    def mine(side):
        return block_ref.at[:, pl.ds(side * half, half)]

    own_rows = full_ref.at[band(me % PLANE, rows)]
    xa = copies.start(mine(0), at(me, 0), xn)
    ya = copies.start(mine(1), at(me, 1), yn)
    xb = copies.start(mine(1), at(me, 1), xn)
    yb = copies.start(mine(0), at(me, 0), yn)
    arriving = [copies.start(block_ref, own_rows, sib)]
    own = pltpu.make_async_copy(block_ref, own_rows, own_sem)
    own.start()

    def finish():
        def to_sibling(device, side):
            arriving.append(copies.start(at(device, side), at(device, side), sib))

        xa.wait_recv()
        yc = copies.start(at(xn, 0), at(xn, 0), yn)
        to_sibling(xn, 0)
        ya.wait_recv()
        xc = copies.start(at(yn, 1), at(yn, 1), xn)
        to_sibling(yn, 1)
        xb.wait_recv()
        to_sibling(xn, 1)
        yb.wait_recv()
        to_sibling(yn, 0)
        yc.wait_recv()
        to_sibling(diag, 0)
        xc.wait_recv()
        to_sibling(diag, 1)
        for copy in arriving:
            copy.wait_recv()
        own.wait()

    return finish


GATHER_COPIES = 13


def gather_kernel(block_ref, full_ref, own_sem, send_sem, recv_sem):
    me = lax.axis_index(AXIS)
    greet((flip(me, 1), flip(me, 2), flip(me, 4)))
    copies = Copies(send_sem, recv_sem)
    gather_steps(block_ref, full_ref, copies, own_sem)()
    copies.sent()


def gather_plane(block):
    rows, width = block.shape
    return pl.pallas_call(
        gather_kernel,
        out_shape=jax.ShapeDtypeStruct((PLANE * rows, width), block.dtype),
        in_specs=[ANY],
        out_specs=ANY,
        scratch_shapes=[DMA(()), DMA((GATHER_COPIES,)), DMA((GATHER_COPIES,))],
        compiler_params=pltpu.CompilerParams(collective_id=1, has_side_effects=True),
        name="gather_plane",
    )(block)


def scatter_kernel(part_ref, out_ref, mine, got, ra, rb, ra2, rb2, load_sem, send_sem, recv_sem):
    rows, width = mine.shape[1:]
    half = width // 2
    step = 16
    me = lax.axis_index(AXIS)
    sib, xn, yn = flip(me, 1), flip(me, 2), flip(me, 4)
    diag = flip(xn, 4)
    left, right = pl.ds(0, half), pl.ds(half, half)
    greet((sib, xn, yn))
    copies = Copies(send_sem, recv_sem)

    def source(device):
        return part_ref.at[band(device % PLANE, rows)]

    loads, crossing = [], []
    for slot, device in enumerate((diag, xn, yn, me)):
        crossing.append(copies.start(source(flip(device, 1)), got.at[slot], sib))
        load = pltpu.make_async_copy(source(device), mine.at[slot], load_sem.at[slot])
        load.start()
        loads.append(load)

    def add(total, other):
        @pl.loop(0, rows // step)
        def _(k):
            r = pl.ds(pl.multiple_of(k * step, step), step)
            total[r] = (total[r].astype(F32) + other[r].astype(F32)).astype(total.dtype)

    def merge(slot):
        crossing[slot].wait_recv()
        loads[slot].wait()
        add(mine.at[slot], got.at[slot])

    merge(0)
    x0 = copies.start(mine.at[0, :, left], ra.at[0], xn)
    y0 = copies.start(mine.at[0, :, right], rb.at[0], yn)
    merge(1)
    x1 = copies.start(mine.at[1, :, left], ra.at[1], xn)
    merge(2)
    y1 = copies.start(mine.at[2, :, right], rb.at[1], yn)
    merge(3)
    x0.wait_recv()
    add(mine.at[2, :, left], ra.at[0])
    y2 = copies.start(mine.at[2, :, left], ra2, yn)
    y0.wait_recv()
    add(mine.at[1, :, right], rb.at[0])
    x2 = copies.start(mine.at[1, :, right], rb2, xn)
    for copy in (x1, y1, y2, x2):
        copy.wait_recv()

    @pl.loop(0, rows // step)
    def _(k):
        r = pl.ds(pl.multiple_of(k * step, step), step)
        out_ref[r, left] = mine[3, r, left].astype(F32) + ra[1, r].astype(F32) + ra2[r].astype(F32)
        out_ref[r, right] = mine[3, r, right].astype(F32) + rb[1, r].astype(F32) + rb2[r].astype(F32)

    copies.sent()


def scatter_plane(part):
    part = part.astype(BF16)
    rows, width = part.shape[0] // PLANE, part.shape[1]
    half = width // 2
    return pl.pallas_call(
        scatter_kernel,
        out_shape=jax.ShapeDtypeStruct((rows, width), F32),
        in_specs=[ANY],
        out_specs=VMEM,
        scratch_shapes=[
            pltpu.VMEM((4, rows, width), BF16),
            pltpu.VMEM((4, rows, width), BF16),
            pltpu.VMEM((2, rows, half), BF16),
            pltpu.VMEM((2, rows, half), BF16),
            pltpu.VMEM((rows, half), BF16),
            pltpu.VMEM((rows, half), BF16),
            DMA((4,)),
            DMA((10,)),
            DMA((10,)),
        ],
        compiler_params=pltpu.CompilerParams(
            collective_id=2, has_side_effects=True, vmem_limit_bytes=40 << 20
        ),
        name="scatter_plane",
    )(part)


def attn_columns(column):
    query_width = H * HD
    key_offset = query_width + (column % 2) * KVH * HD + (column // 2) * HD
    return (column * HD, key_offset, query_width + 2 * KVH * HD + column * HD)


def greet_all(peers):
    me = lax.axis_index(AXIS)
    barrier = pltpu.get_barrier_semaphore()

    @pl.loop(1, peers)
    def _(k):
        device = lax.rem(me + k, peers)
        pl.semaphore_signal(barrier, inc=1, device_id=(device,), device_id_type=MESH)

    pl.semaphore_wait(barrier, peers - 1)


def exchange_all(source_of, target_ref, send_sem, recv_sem):
    peers = target_ref.shape[0]
    me = lax.axis_index(AXIS)

    def copy(k):
        device = lax.rem(me + k, peers)
        return pltpu.make_async_remote_copy(
            src_ref=source_of(device),
            dst_ref=target_ref.at[me],
            send_sem=send_sem.at[k],
            recv_sem=recv_sem.at[k],
            device_id=(device,),
            device_id_type=MESH,
        )

    @pl.loop(1, peers)
    def _(k):
        copy(k).start()

    def finish():
        @pl.loop(1, peers)
        def _(k):
            copy(k).wait()

    return finish


ORDER = (6, 7, 2, 3, 4, 5, 1)


def swap_steps(pieces_of, targets, copies, own_sem):
    me = lax.axis_index(AXIS)
    moved = []
    for bits in ORDER:
        peer = partner(me, bits)
        for source, target in zip(pieces_of(peer % PLANE), targets):
            moved.append(copies.start(source, target, peer))
    owns = []
    for slot, (source, target) in enumerate(zip(pieces_of(me % PLANE), targets)):
        own = pltpu.make_async_copy(source, target, own_sem.at[slot])
        own.start()
        owns.append(own)

    def finish():
        for own in owns:
            own.wait()
        for copy in moved:
            copy.wait_recv()

    return finish


def greet_plane():
    me = lax.axis_index(AXIS)
    greet([partner(me, bits) for bits in ORDER])


def wide(offset):
    return pl.ds(pl.multiple_of(offset, 128), HD)


def spread_attn_kernel(weights_ref, part_ref, own_sem, send_sem, recv_sem):
    me = lax.axis_index(AXIS)
    greet_plane()
    copies = Copies(send_sem, recv_sem)
    swap_steps(
        lambda c: [weights_ref.at[:, wide(offset)] for offset in attn_columns(c)],
        [part_ref.at[me % PLANE, :, pl.ds(slot * HD, HD)] for slot in range(3)],
        copies,
        own_sem,
    )()
    copies.sent()


def spread_attn(weights):
    rows = weights.shape[0]
    return pl.pallas_call(
        spread_attn_kernel,
        out_shape=jax.ShapeDtypeStruct((PLANE, rows, 3 * HD), BF16),
        in_specs=[ANY],
        out_specs=ANY,
        scratch_shapes=[DMA((3,)), DMA((21,)), DMA((21,))],
        compiler_params=pltpu.CompilerParams(collective_id=3, has_side_effects=True),
        name="spread_attn",
    )(weights)


def spread_gu_kernel(
    weights_ref, gain_ref, gu_ref, gains_ref, own_sem, send_sem, recv_sem, gain_send, gain_recv
):
    peers = gains_ref.shape[0]
    ffc = gu_ref.shape[2] // 2
    me = lax.axis_index(AXIS)
    greet_all(peers)
    gains_done = exchange_all(lambda device: gain_ref, gains_ref, gain_send, gain_recv)
    own = pltpu.make_async_copy(gain_ref, gains_ref.at[me], own_sem.at[2])
    own.start()
    copies = Copies(send_sem, recv_sem)
    swap_steps(
        lambda c: [weights_ref.at[:, lanes(slot * PLANE + c, ffc)] for slot in range(2)],
        [gu_ref.at[me % PLANE, :, pl.ds(slot * ffc, ffc)] for slot in range(2)],
        copies,
        own_sem,
    )()
    own.wait()
    gains_done()
    copies.sent()


def spread_gu(weights, gain_block, peers):
    rows = weights.shape[0]
    ffc = weights.shape[1] // 3 // PLANE
    return pl.pallas_call(
        spread_gu_kernel,
        out_shape=(
            jax.ShapeDtypeStruct((PLANE, rows, 2 * ffc), BF16),
            jax.ShapeDtypeStruct((peers,) + gain_block.shape, gain_block.dtype),
        ),
        in_specs=[ANY, ANY],
        out_specs=(ANY, ANY),
        scratch_shapes=[DMA((3,)), DMA((14,)), DMA((14,)), DMA((peers,)), DMA((peers,))],
        compiler_params=pltpu.CompilerParams(collective_id=4, has_side_effects=True),
        name="spread_gu",
    )(weights, gain_block)


def spread_down_kernel(weights_ref, block_ref, down_ref, full_ref, own_sem, send_sem, recv_sem):
    ffc = down_ref.shape[2]
    me = lax.axis_index(AXIS)
    greet_plane()
    copies = Copies(send_sem, recv_sem)
    gathered = gather_steps(block_ref, full_ref, copies, own_sem.at[1])
    spread = swap_steps(
        lambda c: [weights_ref.at[:, lanes(2 * PLANE + c, ffc)]],
        [down_ref.at[me % PLANE]],
        copies,
        own_sem,
    )
    gathered()
    spread()
    copies.sent()


def spread_down(weights, block):
    rows = weights.shape[0]
    ffc = weights.shape[1] // 3 // PLANE
    count = GATHER_COPIES + 7
    return pl.pallas_call(
        spread_down_kernel,
        out_shape=(
            jax.ShapeDtypeStruct((PLANE, rows, ffc), BF16),
            jax.ShapeDtypeStruct((PLANE * block.shape[0], block.shape[1]), BF16),
        ),
        in_specs=[ANY, ANY],
        out_specs=(ANY, ANY),
        scratch_shapes=[DMA((2,)), DMA((count,)), DMA((count,))],
        compiler_params=pltpu.CompilerParams(collective_id=5, has_side_effects=True),
        name="spread_down",
    )(weights, block)


def collect_mlp_kernel(gu_ref, down_ref, rows_ref, own_sem, send_sem, recv_sem):
    ffc = down_ref.shape[2]
    me = lax.axis_index(AXIS)
    greet_plane()
    copies = Copies(send_sem, recv_sem)
    swap_steps(
        lambda c: [gu_ref.at[c, :, pl.ds(0, ffc)], gu_ref.at[c, :, pl.ds(ffc, ffc)], down_ref.at[c]],
        [rows_ref.at[:, lanes(slot * PLANE + me % PLANE, ffc)] for slot in range(3)],
        copies,
        own_sem,
    )()
    copies.sent()


def collect_mlp(gu_term, down_term):
    rows, ffc = down_term.shape[1:]
    return pl.pallas_call(
        collect_mlp_kernel,
        out_shape=jax.ShapeDtypeStruct((rows, 3 * PLANE * ffc), BF16),
        in_specs=[ANY, ANY],
        out_specs=ANY,
        scratch_shapes=[DMA((3,)), DMA((21,)), DMA((21,))],
        compiler_params=pltpu.CompilerParams(collective_id=6, has_side_effects=True),
        name="collect_mlp",
    )(gu_term, down_term)


def collect_qkv_kernel(
    qkv_ref, gain_ref, rows_ref, gains_ref, own_sem, send_sem, recv_sem, gain_send, gain_recv
):
    me = lax.axis_index(AXIS)
    greet_all(gain_ref.shape[0])
    copies = Copies(send_sem, recv_sem)
    moved = swap_steps(
        lambda c: [qkv_ref.at[c, :, pl.ds(0, HD)], qkv_ref.at[c, :, pl.ds(HD, HD)]],
        [rows_ref.at[:, wide(offset)] for offset in attn_columns(me % PLANE)[:2]],
        copies,
        own_sem,
    )
    gains_done = exchange_all(lambda device: gain_ref.at[device], gains_ref, gain_send, gain_recv)
    own = pltpu.make_async_copy(gain_ref.at[me], gains_ref.at[me], own_sem.at[2])
    own.start()
    moved()
    own.wait()
    gains_done()
    copies.sent()


def collect_qkv(qkv_term, gain_blocks):
    rows = qkv_term.shape[1]
    peers = gain_blocks.shape[0]
    return pl.pallas_call(
        collect_qkv_kernel,
        out_shape=(
            jax.ShapeDtypeStruct((rows, (H + 2 * KVH) * HD), BF16),
            jax.ShapeDtypeStruct(gain_blocks.shape, gain_blocks.dtype),
        ),
        in_specs=[ANY, ANY],
        out_specs=(ANY, ANY),
        scratch_shapes=[DMA((3,)), DMA((14,)), DMA((14,)), DMA((peers,)), DMA((peers,))],
        compiler_params=pltpu.CompilerParams(collective_id=7, has_side_effects=True),
        name="collect_qkv",
    )(qkv_term, gain_blocks)


def collect_out_kernel(out_ref, rows_ref, own_sem, send_sem, recv_sem):
    me = lax.axis_index(AXIS)
    greet_plane()
    copies = Copies(send_sem, recv_sem)
    swap_steps(
        lambda c: [out_ref.at[c]], [rows_ref.at[:, lanes(me % PLANE, HD)]], copies, own_sem
    )()
    copies.sent()


def collect_out(out_term):
    rows = out_term.shape[1]
    return pl.pallas_call(
        collect_out_kernel,
        out_shape=jax.ShapeDtypeStruct((rows, H * HD), BF16),
        in_specs=[ANY],
        out_specs=ANY,
        scratch_shapes=[DMA((1,)), DMA((7,)), DMA((7,))],
        compiler_params=pltpu.CompilerParams(collective_id=8, has_side_effects=True),
        name="collect_out",
    )(out_term)


def block_scores(q, k, start, first):
    scores = lax.dot_general(q, k, (((1,), (1,)), ((), ())), preferred_element_type=F32)
    bent = jnp.tanh(scores * (HD ** (-0.5) / SOFT_CAP))
    rows, span = scores.shape
    key_at = lax.broadcasted_iota(jnp.int32, (rows, span), 1)
    row_at = lax.broadcasted_iota(jnp.int32, (rows, span), 0)
    allowed = (key_at + first >= start) & (key_at <= row_at + LMAX)
    return (bent, jnp.where(allowed, jnp.exp(SOFT_CAP * bent), 0.0))


def attend_kernel(q_ref, k_ref, v_ref, start_ref, out_ref, inv_ref):
    first = pl.program_id(0) * QBLK
    keys = pl.ds(pl.multiple_of(first, QBLK), LMAX + QBLK)
    unused_bent, exponent = block_scores(q_ref[...], k_ref[keys], start_ref[...], first)
    inverse = 1.0 / jnp.sum(exponent, axis=-1, keepdims=True)
    weights = (exponent * inverse).astype(BF16)
    out_ref[...] = jnp.dot(weights, v_ref[keys], preferred_element_type=F32).astype(BF16)
    inv_ref[...] = inverse


def attend(queries, key_rows, value_rows, starts):
    rows = queries.shape[0]
    span = key_rows.shape[0]
    row_spec = pl.BlockSpec((QBLK, HD), lambda i: (i, 0))
    one_spec = pl.BlockSpec((QBLK, 1), lambda i: (i, 0))
    all_spec = pl.BlockSpec((span, HD), lambda i: (0, 0))
    return pl.pallas_call(
        attend_kernel,
        out_shape=(
            jax.ShapeDtypeStruct((rows, HD), BF16),
            jax.ShapeDtypeStruct((rows, 1), F32),
        ),
        grid=(rows // QBLK,),
        in_specs=[row_spec, all_spec, all_spec, one_spec],
        out_specs=(row_spec, one_spec),
        compiler_params=pltpu.CompilerParams(vmem_limit_bytes=40 << 20),
        cost_estimate=pl.CostEstimate(
            flops=4 * rows * (LMAX + QBLK) * HD,
            transcendentals=2 * rows * (LMAX + QBLK),
            bytes_accessed=4 * rows * HD * 2,
        ),
        name="attend",
    )(queries, key_rows, value_rows, starts)


def attend_back_kernel(q_ref, k_ref, v_ref, start_ref, inv_ref, grad_ref, gq_ref, gk_ref, gv_ref):
    @pl.when(pl.program_id(0) == 0)
    def _():
        gk_ref[...] = jnp.zeros_like(gk_ref)
        gv_ref[...] = jnp.zeros_like(gv_ref)

    first = pl.program_id(0) * QBLK
    keys = pl.ds(pl.multiple_of(first, QBLK), LMAX + QBLK)
    q, k, v, grad = q_ref[...], k_ref[keys], v_ref[keys], grad_ref[...]
    bent, exponent = block_scores(q, k, start_ref[...], first)
    probability = exponent * inv_ref[...]
    grad_prob = lax.dot_general(grad, v, (((1,), (1,)), ((), ())), preferred_element_type=F32)
    inner = jnp.sum(probability * grad_prob, axis=-1, keepdims=True)
    grad_scores = (probability * (grad_prob - inner) * (1.0 - bent * bent)).astype(BF16)
    scale = HD ** (-0.5)
    gq_ref[...] = jnp.dot(grad_scores, k, preferred_element_type=F32) * scale
    over_rows = (((0,), (0,)), ((), ()))
    gk_ref[keys] += lax.dot_general(grad_scores, q, over_rows, preferred_element_type=F32) * scale
    gv_ref[keys] += lax.dot_general(
        probability.astype(BF16), grad, over_rows, preferred_element_type=F32
    )


def attend_back(queries, key_rows, value_rows, starts, inverse, grad):
    rows = queries.shape[0]
    span = key_rows.shape[0]
    row_spec = pl.BlockSpec((QBLK, HD), lambda i: (i, 0))
    one_spec = pl.BlockSpec((QBLK, 1), lambda i: (i, 0))
    all_spec = pl.BlockSpec((span, HD), lambda i: (0, 0))
    return pl.pallas_call(
        attend_back_kernel,
        out_shape=(
            jax.ShapeDtypeStruct((rows, HD), F32),
            jax.ShapeDtypeStruct((span, HD), F32),
            jax.ShapeDtypeStruct((span, HD), F32),
        ),
        grid=(rows // QBLK,),
        in_specs=[row_spec, all_spec, all_spec, one_spec, one_spec, row_spec],
        out_specs=(row_spec, all_spec, all_spec),
        compiler_params=pltpu.CompilerParams(vmem_limit_bytes=48 << 20),
        cost_estimate=pl.CostEstimate(
            flops=10 * rows * (LMAX + QBLK) * HD,
            transcendentals=2 * rows * (LMAX + QBLK),
            bytes_accessed=12 * rows * HD * 2,
        ),
        name="attend_back",
    )(queries, key_rows, value_rows, starts, inverse, grad)


def token_tables(seq_lengths, index_vec):
    count = seq_lengths.shape[0]
    order = jnp.arange(count, dtype=jnp.int32)
    seq_ends = jnp.sum(
        jnp.where(order[None, :] <= order[:, None], seq_lengths[None, :], 0), axis=1
    )
    after_end = index_vec[:, None] >= seq_ends[None, :]
    return index_vec - jnp.sum(jnp.where(after_end, seq_lengths[None, :], 0), axis=1)


def rms_parts(value):
    return lax.rsqrt(jnp.mean(value * value, axis=-1, keepdims=True) + EPSILON)


def rms_forward(value, gain_vec):
    return value * rms_parts(value) * (1.0 + gain_vec)


def rms_backward(value, gain_vec, grad):
    r = rms_parts(value)
    scaled = (1.0 + gain_vec) * grad
    inner = jnp.mean(value * scaled, axis=-1, keepdims=True)
    return (r * scaled - value * (r * r * r * inner), jnp.sum(grad * value * r, axis=0))


def rotate(value, cosine, sine_part):
    half_width = value.shape[-1] // 2
    first_half = value[..., :half_width]
    second_half = value[..., half_width:]
    return jnp.concatenate(
        [
            first_half * cosine - second_half * sine_part,
            second_half * cosine + first_half * sine_part,
        ],
        axis=-1,
    )


def contract_last(left_side, right_side):
    return lax.dot_general(
        left_side, right_side, (((1,), (1,)), ((), ())), preferred_element_type=F32
    )


def contract_first(left_side, right_side):
    return lax.dot_general(
        left_side, right_side, (((0,), (0,)), ((), ())), preferred_element_type=F32
    )


def matmul(left_side, right_side):
    return jnp.dot(left_side, right_side, preferred_element_type=F32)


def gelu_parts(gate):
    k0 = 0.7978845608028654
    k1 = 0.044715
    t = jnp.tanh(k0 * (gate + k1 * gate * gate * gate))
    value = 0.5 * gate * (1.0 + t)
    slope = 0.5 * (1.0 + t) + 0.5 * gate * (1.0 - t * t) * k0 * (1.0 + 3.0 * k1 * gate * gate)
    return (value, slope)


def local(tokens, attn_weights, mlp_weights, norm_gains, seq_lengths, cotangent):
    tok_rows, width = tokens.shape
    peers = lax.axis_size(AXIS)
    planes = peers // PLANE
    share = width // peers
    ff = mlp_weights.shape[1] // 3
    ffc = ff // PLANE
    plane_rows = PLANE * tok_rows
    halo = LMAX
    across = [[p * PLANE + i for p in range(planes)] for i in range(PLANE)]
    sibling = [(i, i ^ 1) for i in range(peers)]
    to_next = [(i, i + PLANE) for i in range(peers - PLANE)]
    to_prev = [(i + PLANE, i) for i in range(peers - PLANE)]
    me = lax.axis_index(AXIS)
    is_even = (me % 2) == 0
    plane_start = (me // PLANE) * plane_rows

    def gather_across(value):
        return lax.all_gather(value, AXIS, axis=0, tiled=True, axis_index_groups=across)

    def scatter_across(value):
        part = lax.psum_scatter(
            value.astype(BF16), AXIS, scatter_dimension=0, tiled=True, axis_index_groups=across
        )
        return part.reshape(PLANE, -1, part.shape[1])

    gain_block = jnp.pad(norm_gains.astype(F32), ((0, 8 - 4), (0, -share % 128)))
    attn_part, gain_block = lax.optimization_barrier((spread_attn(attn_weights), gain_block))
    attn_cols = gather_across(attn_part.reshape(-1, 3 * HD))
    gu_part, gain_blocks = spread_gu(mlp_weights, gain_block, peers)
    gain_full = gain_blocks[:, :4, :share].transpose(1, 0, 2).reshape(4, width)
    inputs = tokens.astype(F32)
    down_part, normed = spread_down(
        mlp_weights, rms_forward(inputs, gain_full[0]).astype(BF16)
    )
    gu_cols = gather_across(gu_part.reshape(-1, 2 * ffc))
    down_cols = gather_across(down_part.reshape(-1, ffc))
    qkv_cols = attn_cols[:, : 2 * HD]
    out_cols = attn_cols[:, 2 * HD :]

    query_index = plane_start + jnp.arange(plane_rows, dtype=jnp.int32)
    position = token_tables(seq_lengths, query_index)
    starts = (jnp.arange(plane_rows, dtype=jnp.int32) + halo - position)[:, None]
    frequency = 10000.0 ** (-jnp.arange(HD // 2, dtype=F32) * 2.0 / HD)
    angles = position.astype(F32)[:, None] * frequency[None, :]
    cosine, sine_part = jnp.cos(angles), jnp.sin(angles)
    kv_cosine = jnp.where(is_even, cosine, 1.0)
    kv_sine = jnp.where(is_even, sine_part, 0.0)

    projected = matmul(normed, qkv_cols)
    queries = rotate(projected[:, :HD], cosine, sine_part).astype(BF16)
    kv_own = rotate(projected[:, HD:], kv_cosine, kv_sine).astype(BF16)
    kv_halo = lax.ppermute(kv_own[plane_rows - halo :], AXIS, to_next)
    kv_mine = jnp.concatenate([kv_halo, kv_own], axis=0)
    kv_other = lax.ppermute(kv_mine, AXIS, sibling)
    key_rows = jnp.where(is_even, kv_mine, kv_other)
    value_rows = jnp.where(is_even, kv_other, kv_mine)
    attended, inverse = attend(queries, key_rows, value_rows, starts)
    attn_proj = scatter_plane(contract_last(attended, out_cols))

    middle = inputs + rms_forward(attn_proj, gain_full[1])
    mid_low = gather_plane(rms_forward(middle, gain_full[2]).astype(BF16))
    gate_up = matmul(mid_low, gu_cols)
    gate, up = gate_up[:, :ffc], gate_up[:, ffc:]
    gelu, slope = gelu_parts(gate)
    hidden = (gelu * up).astype(BF16)
    mlp_raw = scatter_plane(contract_last(hidden, down_cols))
    layer_output = (middle + rms_forward(mlp_raw, gain_full[3])).astype(BF16)

    grad_out = cotangent.astype(F32)
    grad_raw, gain_four = rms_backward(mlp_raw, gain_full[3], grad_out)
    grad_raw_low = gather_plane(grad_raw.astype(BF16))
    down_grad = contract_first(grad_raw_low, hidden).astype(BF16)
    down_grad, grad_raw_low = lax.optimization_barrier((down_grad, grad_raw_low))
    down_term = scatter_across(down_grad)
    grad_hidden = matmul(grad_raw_low, down_cols)
    grad_gu = jnp.concatenate(
        [(slope * up * grad_hidden).astype(BF16), (gelu * grad_hidden).astype(BF16)], axis=1
    )
    gu_grad = contract_first(mid_low, grad_gu).astype(BF16)
    gu_grad, grad_gu = lax.optimization_barrier((gu_grad, grad_gu))
    gu_term = scatter_across(gu_grad)
    grad_normed_mid = scatter_plane(contract_last(grad_gu, gu_cols))
    grad_mid_part, gain_three = rms_backward(middle, gain_full[2], grad_normed_mid)
    grad_middle = grad_out + grad_mid_part

    grad_proj, gain_two = rms_backward(attn_proj, gain_full[1], grad_middle)
    grad_proj_own, down_term = lax.optimization_barrier((grad_proj.astype(BF16), down_term))
    grad_proj_low = gather_plane(grad_proj_own)
    grad_att = matmul(grad_proj_low, out_cols).astype(BF16)
    grad_query, grad_keys, grad_values = attend_back(
        queries, key_rows, value_rows, starts, inverse, grad_att
    )
    grad_mine = jnp.where(is_even, grad_keys, grad_values)
    grad_give = jnp.where(is_even, grad_values, grad_keys).astype(BF16)
    grad_kv = grad_mine + lax.ppermute(grad_give, AXIS, sibling).astype(F32)
    grad_back = lax.ppermute(grad_kv[:halo].astype(BF16), AXIS, to_prev).astype(F32)
    grad_kv = grad_kv[halo:] + jnp.pad(grad_back, ((plane_rows - halo, 0), (0, 0)))
    grad_qkv = jnp.concatenate(
        [
            rotate(grad_query, cosine, -sine_part).astype(BF16),
            rotate(grad_kv, kv_cosine, -kv_sine).astype(BF16),
        ],
        axis=1,
    )
    qkv_grad = contract_first(normed, grad_qkv).astype(BF16)
    qkv_grad, grad_qkv, grad_proj_low = lax.optimization_barrier(
        (qkv_grad, grad_qkv, grad_proj_low)
    )
    qkv_term = scatter_across(qkv_grad)
    out_grad = contract_first(grad_proj_low, attended).astype(BF16)
    out_grad, grad_qkv = lax.optimization_barrier((out_grad, grad_qkv))
    out_term = scatter_across(out_grad)
    grad_normed = scatter_plane(contract_last(grad_qkv, qkv_cols))
    grad_in_part, gain_one = rms_backward(inputs, gain_full[0], grad_normed)
    grad_tokens = (grad_middle + grad_in_part).astype(BF16)

    gain_term = jnp.stack([gain_one, gain_two, gain_three, gain_four], axis=0)
    gain_term = gain_term.reshape(4, peers, share).transpose(1, 0, 2)
    gain_term = jnp.pad(gain_term, ((0, 0), (0, 8 - 4), (0, -share % 128)))
    gu_term, gain_term = lax.optimization_barrier((gu_term, gain_term))
    mlp_rows = collect_mlp(gu_term, down_term)
    mlp_rows, qkv_term = lax.optimization_barrier((mlp_rows, qkv_term))
    grad_mlp = mlp_rows.astype(F32)
    qkv_rows, gain_recv = collect_qkv(qkv_term, gain_term)
    qkv_rows, out_term = lax.optimization_barrier((qkv_rows, out_term))
    out_rows = collect_out(out_term)
    grad_attn = jnp.concatenate([qkv_rows, out_rows], axis=1).astype(F32)
    grad_gains = jnp.sum(gain_recv[:, :4, :share], axis=0)
    return (layer_output, grad_tokens, grad_attn, grad_mlp, grad_gains)


def solution(mesh):
    return jax.shard_map(
        local,
        mesh=mesh,
        in_specs=(
            P("fsdp", None),
            P("fsdp", None),
            P("fsdp", None),
            P(None, "fsdp"),
            P(),
            P("fsdp", None),
        ),
        out_specs=(
            P("fsdp", None),
            P("fsdp", None),
            P("fsdp", None),
            P("fsdp", None),
            P(None, "fsdp"),
        ),
        check_vma=False,
    )
```

```python
from functools import partial

import jax
import jax.numpy as jnp
from jax import lax
from jax.experimental import pallas as pl
from jax.experimental.pallas import tpu as pltpu
from jax.sharding import PartitionSpec as P

H = 8
KVH = 4
HD = 256
LMAX = 1024
PLANE = 8
QBLK = 128

EPSILON = 1e-06
SOFT_CAP = 50.0
AXIS = "fsdp"
F32 = jnp.float32
BF16 = jnp.bfloat16
MESH = pl.DeviceIdType.MESH
ANY = pl.BlockSpec(memory_space=pl.ANY)
VMEM = pl.BlockSpec(memory_space=pltpu.VMEM)
DMA = pltpu.SemaphoreType.DMA


def flip(index, step):
    return index + step - 2 * step * ((index // step) % 2)


PLANE_STEP = 4
BLOCK_STEP = 8


def partner(index, bits, step):
    for bit, by in ((1, 1), (2, 2), (4, step)):
        if bits & bit:
            index = flip(index, by)
    return index


def place(device, step):
    return device % 4 + 4 * ((device // step) % 2)


def greet(peers):
    barrier = pltpu.get_barrier_semaphore()
    for peer in peers:
        pl.semaphore_signal(barrier, inc=1, device_id=(peer,), device_id_type=MESH)
    pl.semaphore_wait(barrier, len(peers))


class Copies:
    def __init__(self, send_sem, recv_sem):
        self.send_sem, self.recv_sem, self.made = send_sem, recv_sem, []

    def start(self, source, target, device):
        slot = len(self.made)
        copy = pltpu.make_async_remote_copy(
            src_ref=source,
            dst_ref=target,
            send_sem=self.send_sem.at[slot],
            recv_sem=self.recv_sem.at[slot],
            device_id=(device,),
            device_id_type=MESH,
        )
        copy.start()
        self.made.append(copy)
        return copy

    def sent(self):
        for copy in self.made:
            copy.wait_send()


def band(index, size):
    return pl.ds(pl.multiple_of(index * size, 8), size)


def lanes(index, size):
    return pl.ds(pl.multiple_of(index * size, 128), size)


def gather_steps(block_ref, full_ref, copies, own_sem, step):
    rows, width = block_ref.shape
    half = width // 2
    me = lax.axis_index(AXIS)
    sib, xn, yn = flip(me, 1), flip(me, 2), flip(me, step)
    diag = flip(xn, step)

    def at(device, side):
        return full_ref.at[band(place(device, step), rows), pl.ds(side * half, half)]

    def mine(side):
        return block_ref.at[:, pl.ds(side * half, half)]

    own_rows = full_ref.at[band(place(me, step), rows)]
    xa = copies.start(mine(0), at(me, 0), xn)
    ya = copies.start(mine(1), at(me, 1), yn)
    xb = copies.start(mine(1), at(me, 1), xn)
    yb = copies.start(mine(0), at(me, 0), yn)
    arriving = [copies.start(block_ref, own_rows, sib)]
    own = pltpu.make_async_copy(block_ref, own_rows, own_sem)
    own.start()

    def finish():
        def to_sibling(device, side):
            arriving.append(copies.start(at(device, side), at(device, side), sib))

        xa.wait_recv()
        yc = copies.start(at(xn, 0), at(xn, 0), yn)
        to_sibling(xn, 0)
        ya.wait_recv()
        xc = copies.start(at(yn, 1), at(yn, 1), xn)
        to_sibling(yn, 1)
        xb.wait_recv()
        to_sibling(xn, 1)
        yb.wait_recv()
        to_sibling(yn, 0)
        yc.wait_recv()
        to_sibling(diag, 0)
        xc.wait_recv()
        to_sibling(diag, 1)
        for copy in arriving:
            copy.wait_recv()
        own.wait()

    return finish


GATHER_COPIES = 13


def cost(microseconds):
    return pl.CostEstimate(
        flops=int(microseconds * 1.1e9), transcendentals=0, bytes_accessed=int(microseconds * 3.3e6)
    )


def gather_kernel(block_ref, full_ref, own_sem, send_sem, recv_sem, *, step):
    me = lax.axis_index(AXIS)
    greet((flip(me, 1), flip(me, 2), flip(me, step)))
    copies = Copies(send_sem, recv_sem)
    gather_steps(block_ref, full_ref, copies, own_sem, step)()
    copies.sent()


def gather_square(block, step, collective_id):
    rows, width = block.shape
    return pl.pallas_call(
        partial(gather_kernel, step=step),
        out_shape=jax.ShapeDtypeStruct((PLANE * rows, width), block.dtype),
        in_specs=[ANY],
        out_specs=ANY,
        scratch_shapes=[DMA(()), DMA((GATHER_COPIES,)), DMA((GATHER_COPIES,))],
        compiler_params=pltpu.CompilerParams(collective_id=collective_id, has_side_effects=True),
        cost_estimate=cost(42),
        name="gather_square",
    )(block)


W_TILES = 3


def product_scatter_kernel(*refs, pairs, step):
    left_refs, right_refs, out_ref = refs[:pairs], refs[pairs : 2 * pairs], refs[2 * pairs]
    left_bufs = refs[2 * pairs + 1 : 3 * pairs + 1]
    right_bufs = refs[3 * pairs + 1 : 4 * pairs + 1]
    both, got, ra, rb, ra2, rb2, load_sem, send_sem, recv_sem = refs[4 * pairs + 1 :]
    rows, width = got.shape[1:]
    half = width // 2
    tile = width // W_TILES
    chunk = 16
    me = lax.axis_index(AXIS)
    core = me % 2
    sib, xn, yn = flip(me, 1), flip(me, 2), flip(me, step)
    order = (flip(xn, step), xn, yn, me)
    first, second = pl.ds(0, half), pl.ds(half, half)

    def chip_rows(device):
        return pl.ds(pl.multiple_of((place(device, step) // 2) * 2 * rows, 16), 2 * rows)

    def right_load(j, t):
        r = pl.ds(t * tile, tile)
        return pltpu.make_async_copy(right_refs[j].at[r], right_bufs[j].at[r], load_sem.at[j, t])

    def left_load(j, i):
        r = chip_rows(order[i])
        return pltpu.make_async_copy(
            left_refs[j].at[r], left_bufs[j].at[r], load_sem.at[j, W_TILES + i]
        )

    for j in range(pairs):
        left_load(j, 0).start()
    for t in range(W_TILES):
        for j in range(pairs):
            right_load(j, t).start()
    for i in range(1, 4):
        for j in range(pairs):
            left_load(j, i).start()
    greet((sib, xn, yn))
    copies = Copies(send_sem, recv_sem)

    def product(i):
        r = chip_rows(order[i])
        for j in range(pairs):
            left_load(j, i).wait()

        def columns(w):
            total = None
            for j in range(pairs):
                term = contract_last(left_bufs[j][r], right_bufs[j][w])
                total = term if total is None else total + term
            both[i, :, w] = total.astype(BF16)

        if i == 0:
            for t in range(W_TILES):
                for j in range(pairs):
                    right_load(j, t).wait()
                columns(pl.ds(t * tile, tile))
        else:

            @pl.loop(0, W_TILES)
            def _(t):
                columns(pl.ds(pl.multiple_of(t * tile, tile), tile))

    def mine(i, cols=None):
        if cols is None:
            return both.at[i, band(core, rows)]
        return both.at[i, band(core, rows), cols]

    def add(total, other):
        @pl.loop(0, rows // chunk)
        def _(k):
            r = pl.ds(pl.multiple_of(k * chunk, chunk), chunk)
            total[r] = (total[r].astype(F32) + other[r].astype(F32)).astype(total.dtype)

    def make(i):
        product(i)
        crossing = copies.start(both.at[i, band(1 - core, rows)], got.at[i], sib)
        crossing.wait_recv()
        add(mine(i), got.at[i])

    make(0)
    x0 = copies.start(mine(0, first), ra.at[0], xn)
    y0 = copies.start(mine(0, second), rb.at[0], yn)
    make(1)
    x1 = copies.start(mine(1, first), ra.at[1], xn)
    make(2)
    y1 = copies.start(mine(2, second), rb.at[1], yn)
    x0.wait_recv()
    add(mine(2, first), ra.at[0])
    y2 = copies.start(mine(2, first), ra2, yn)
    y0.wait_recv()
    add(mine(1, second), rb.at[0])
    x2 = copies.start(mine(1, second), rb2, xn)
    make(3)
    for copy in (x1, y1, y2, x2):
        copy.wait_recv()
    own = mine(3)

    @pl.loop(0, rows // chunk)
    def _(k):
        r = pl.ds(pl.multiple_of(k * chunk, chunk), chunk)
        out_ref[r, first] = own[r, first].astype(F32) + ra[1, r].astype(F32) + ra2[r].astype(F32)
        out_ref[r, second] = own[r, second].astype(F32) + rb[1, r].astype(F32) + rb2[r].astype(F32)

    copies.sent()


def product_scatter(lefts, rights, step, collective_id, microseconds=50):
    pairs = len(lefts)
    rows, width = lefts[0].shape[0] // PLANE, rights[0].shape[0]
    half = width // 2
    return pl.pallas_call(
        partial(product_scatter_kernel, pairs=pairs, step=step),
        out_shape=jax.ShapeDtypeStruct((rows, width), F32),
        in_specs=[ANY] * (2 * pairs),
        out_specs=VMEM,
        scratch_shapes=[
            *[pltpu.VMEM(value.shape, BF16) for value in lefts],
            *[pltpu.VMEM(value.shape, BF16) for value in rights],
            pltpu.VMEM((4, 2 * rows, width), BF16),
            pltpu.VMEM((4, rows, width), BF16),
            pltpu.VMEM((2, rows, half), BF16),
            pltpu.VMEM((2, rows, half), BF16),
            pltpu.VMEM((rows, half), BF16),
            pltpu.VMEM((rows, half), BF16),
            DMA((pairs, W_TILES + 4)),
            DMA((10,)),
            DMA((10,)),
        ],
        compiler_params=pltpu.CompilerParams(
            collective_id=collective_id, has_side_effects=True, vmem_limit_bytes=56 << 20
        ),
        cost_estimate=cost(microseconds),
        name="product_scatter",
    )(*lefts, *rights)


def attn_columns(column):
    query_width = H * HD
    key_offset = query_width + (column % 2) * KVH * HD + (column // 2) * HD
    return (column * HD, key_offset, query_width + 2 * KVH * HD + column * HD)


def greet_all(peers):
    me = lax.axis_index(AXIS)
    barrier = pltpu.get_barrier_semaphore()

    @pl.loop(1, peers)
    def _(k):
        device = lax.rem(me + k, peers)
        pl.semaphore_signal(barrier, inc=1, device_id=(device,), device_id_type=MESH)

    pl.semaphore_wait(barrier, peers - 1)


def exchange_all(source_of, target_ref, send_sem, recv_sem):
    peers = target_ref.shape[0]
    me = lax.axis_index(AXIS)

    def copy(k):
        device = lax.rem(me + k, peers)
        return pltpu.make_async_remote_copy(
            src_ref=source_of(device),
            dst_ref=target_ref.at[me],
            send_sem=send_sem.at[k],
            recv_sem=recv_sem.at[k],
            device_id=(device,),
            device_id_type=MESH,
        )

    @pl.loop(1, peers)
    def _(k):
        copy(k).start()

    def finish():
        @pl.loop(1, peers)
        def _(k):
            copy(k).wait()

    return finish


ORDER = (6, 7, 2, 3, 4, 5, 1)


def swap_steps(pieces_of, targets, copies, own_sem, step):
    me = lax.axis_index(AXIS)
    moved = []
    for bits in ORDER:
        peer = partner(me, bits, step)
        for source, target in zip(pieces_of(place(peer, step)), targets):
            moved.append(copies.start(source, target, peer))
    owns = []
    for slot, (source, target) in enumerate(zip(pieces_of(place(me, step)), targets)):
        own = pltpu.make_async_copy(source, target, own_sem.at[slot])
        own.start()
        owns.append(own)

    def finish():
        for own in owns:
            own.wait()
        for copy in moved:
            copy.wait_recv()

    return finish


def square(step):
    me = lax.axis_index(AXIS)
    return [partner(me, bits, step) for bits in ORDER]


def wide(offset):
    return pl.ds(pl.multiple_of(offset, 128), HD)


def spread_attn_kernel(weights_ref, part_ref, own_sem, send_sem, recv_sem):
    here = place(lax.axis_index(AXIS), PLANE_STEP)
    greet(square(PLANE_STEP))
    copies = Copies(send_sem, recv_sem)
    swap_steps(
        lambda c: [weights_ref.at[:, wide(offset)] for offset in attn_columns(c)],
        [part_ref.at[here, :, pl.ds(slot * HD, HD)] for slot in range(3)],
        copies,
        own_sem,
        PLANE_STEP,
    )()
    copies.sent()


def spread_attn(weights):
    rows = weights.shape[0]
    return pl.pallas_call(
        spread_attn_kernel,
        out_shape=jax.ShapeDtypeStruct((PLANE, rows, 3 * HD), BF16),
        in_specs=[ANY],
        out_specs=ANY,
        scratch_shapes=[DMA((3,)), DMA((21,)), DMA((21,))],
        compiler_params=pltpu.CompilerParams(collective_id=3, has_side_effects=True),
        name="spread_attn",
    )(weights)


def spread_gu_kernel(
    weights_ref, gain_ref, gate_ref, up_ref, gains_ref, own_sem, send_sem, recv_sem, gain_send, gain_recv
):
    peers = gains_ref.shape[0]
    ffc = gate_ref.shape[2]
    me = lax.axis_index(AXIS)
    here = place(me, BLOCK_STEP)
    greet_all(peers)
    gains_done = exchange_all(lambda device: gain_ref, gains_ref, gain_send, gain_recv)
    own = pltpu.make_async_copy(gain_ref, gains_ref.at[me], own_sem.at[2])
    own.start()
    copies = Copies(send_sem, recv_sem)
    swap_steps(
        lambda c: [weights_ref.at[:, lanes(slot * PLANE + c, ffc)] for slot in range(2)],
        [gate_ref.at[here], up_ref.at[here]],
        copies,
        own_sem,
        BLOCK_STEP,
    )()
    own.wait()
    gains_done()
    copies.sent()


def spread_gu(weights, gain_block, peers):
    rows = weights.shape[0]
    ffc = weights.shape[1] // 3 // PLANE
    return pl.pallas_call(
        spread_gu_kernel,
        out_shape=(
            jax.ShapeDtypeStruct((PLANE, rows, ffc), BF16),
            jax.ShapeDtypeStruct((PLANE, rows, ffc), BF16),
            jax.ShapeDtypeStruct((peers,) + gain_block.shape, gain_block.dtype),
        ),
        in_specs=[ANY, ANY],
        out_specs=(ANY, ANY, ANY),
        scratch_shapes=[DMA((3,)), DMA((14,)), DMA((14,)), DMA((peers,)), DMA((peers,))],
        compiler_params=pltpu.CompilerParams(collective_id=4, has_side_effects=True),
        cost_estimate=cost(38),
        name="spread_gu",
    )(weights, gain_block)


def spread_down_kernel(weights_ref, block_ref, down_ref, full_ref, own_sem, send_sem, recv_sem):
    ffc = down_ref.shape[2]
    me = lax.axis_index(AXIS)
    greet(square(BLOCK_STEP) + [flip(me, PLANE_STEP)])
    copies = Copies(send_sem, recv_sem)
    gathered = gather_steps(block_ref, full_ref, copies, own_sem.at[1], PLANE_STEP)
    spread = swap_steps(
        lambda c: [weights_ref.at[:, lanes(2 * PLANE + c, ffc)]],
        [down_ref.at[place(me, BLOCK_STEP)]],
        copies,
        own_sem,
        BLOCK_STEP,
    )
    gathered()
    spread()
    copies.sent()


def spread_down(weights, block):
    rows = weights.shape[0]
    ffc = weights.shape[1] // 3 // PLANE
    count = GATHER_COPIES + 7
    return pl.pallas_call(
        spread_down_kernel,
        out_shape=(
            jax.ShapeDtypeStruct((PLANE, rows, ffc), BF16),
            jax.ShapeDtypeStruct((PLANE * block.shape[0], block.shape[1]), BF16),
        ),
        in_specs=[ANY, ANY],
        out_specs=(ANY, ANY),
        scratch_shapes=[DMA((2,)), DMA((count,)), DMA((count,))],
        compiler_params=pltpu.CompilerParams(collective_id=5, has_side_effects=True),
        cost_estimate=cost(1),
        name="spread_down",
    )(weights, block)


def assemble_kernel(near_ref, far_ref, side_ref, far_side_ref, full_ref, sem):
    me = lax.axis_index(AXIS)
    block, column = (me // 16) % 2, (me // 4) % 2
    copies = []
    for slot, (source, b, c) in enumerate(
        (
            (near_ref, block, column),
            (far_ref, 1 - block, column),
            (side_ref, block, 1 - column),
            (far_side_ref, 1 - block, 1 - column),
        )
    ):
        copies.append(pltpu.make_async_copy(source, full_ref.at[b, :, c], sem.at[slot]))
    for copy in copies:
        copy.start()
    for copy in copies:
        copy.wait()


def assemble(near, far, side, far_side):
    return pl.pallas_call(
        assemble_kernel,
        out_shape=jax.ShapeDtypeStruct((2, 2, 2) + near.shape[1:], near.dtype),
        in_specs=[ANY] * 4,
        out_specs=ANY,
        scratch_shapes=[DMA((4,))],
        cost_estimate=cost(5),
        name="assemble",
    )(near, far, side, far_side)


def collect_mlp_kernel(gate_ref, up_ref, down_ref, rows_ref, own_sem, send_sem, recv_sem):
    ffc = down_ref.shape[2]
    here = place(lax.axis_index(AXIS), BLOCK_STEP)
    greet(square(BLOCK_STEP))
    copies = Copies(send_sem, recv_sem)
    swap_steps(
        lambda c: [gate_ref.at[c], up_ref.at[c], down_ref.at[c]],
        [rows_ref.at[:, lanes(slot * PLANE + here, ffc)] for slot in range(3)],
        copies,
        own_sem,
        BLOCK_STEP,
    )()
    copies.sent()


def collect_mlp(gate_term, up_term, down_term):
    rows, ffc = down_term.shape[1:]
    return pl.pallas_call(
        collect_mlp_kernel,
        out_shape=jax.ShapeDtypeStruct((rows, 3 * PLANE * ffc), BF16),
        in_specs=[ANY, ANY, ANY],
        out_specs=ANY,
        scratch_shapes=[DMA((3,)), DMA((21,)), DMA((21,))],
        compiler_params=pltpu.CompilerParams(collective_id=6, has_side_effects=True),
        cost_estimate=cost(46),
        name="collect_mlp",
    )(gate_term, up_term, down_term)


def collect_qkv_kernel(
    qkv_ref, gain_ref, rows_ref, gains_ref, own_sem, send_sem, recv_sem, gain_send, gain_recv
):
    me = lax.axis_index(AXIS)
    greet_all(gain_ref.shape[0])
    copies = Copies(send_sem, recv_sem)
    moved = swap_steps(
        lambda c: [qkv_ref.at[c, :, pl.ds(0, HD)], qkv_ref.at[c, :, pl.ds(HD, HD)]],
        [rows_ref.at[:, wide(offset)] for offset in attn_columns(place(me, PLANE_STEP))[:2]],
        copies,
        own_sem,
        PLANE_STEP,
    )
    gains_done = exchange_all(lambda device: gain_ref.at[device], gains_ref, gain_send, gain_recv)
    own = pltpu.make_async_copy(gain_ref.at[me], gains_ref.at[me], own_sem.at[2])
    own.start()
    moved()
    own.wait()
    gains_done()
    copies.sent()


def collect_qkv(qkv_term, gain_blocks):
    rows = qkv_term.shape[1]
    peers = gain_blocks.shape[0]
    return pl.pallas_call(
        collect_qkv_kernel,
        out_shape=(
            jax.ShapeDtypeStruct((rows, (H + 2 * KVH) * HD), BF16),
            jax.ShapeDtypeStruct(gain_blocks.shape, gain_blocks.dtype),
        ),
        in_specs=[ANY, ANY],
        out_specs=(ANY, ANY),
        scratch_shapes=[DMA((3,)), DMA((14,)), DMA((14,)), DMA((peers,)), DMA((peers,))],
        compiler_params=pltpu.CompilerParams(collective_id=7, has_side_effects=True),
        name="collect_qkv",
    )(qkv_term, gain_blocks)


def collect_out_kernel(out_ref, rows_ref, own_sem, send_sem, recv_sem):
    here = place(lax.axis_index(AXIS), PLANE_STEP)
    greet(square(PLANE_STEP))
    copies = Copies(send_sem, recv_sem)
    swap_steps(
        lambda c: [out_ref.at[c]], [rows_ref.at[:, lanes(here, HD)]], copies, own_sem, PLANE_STEP
    )()
    copies.sent()


def collect_out(out_term):
    rows = out_term.shape[1]
    return pl.pallas_call(
        collect_out_kernel,
        out_shape=jax.ShapeDtypeStruct((rows, H * HD), BF16),
        in_specs=[ANY],
        out_specs=ANY,
        scratch_shapes=[DMA((1,)), DMA((7,)), DMA((7,))],
        compiler_params=pltpu.CompilerParams(collective_id=8, has_side_effects=True),
        name="collect_out",
    )(out_term)


def block_scores(q, k, start, first):
    scores = lax.dot_general(q, k, (((1,), (1,)), ((), ())), preferred_element_type=F32)
    bent = jnp.tanh(scores * (HD ** (-0.5) / SOFT_CAP))
    rows, span = scores.shape
    key_at = lax.broadcasted_iota(jnp.int32, (rows, span), 1)
    row_at = lax.broadcasted_iota(jnp.int32, (rows, span), 0)
    allowed = (key_at + first >= start) & (key_at <= row_at + LMAX)
    return (bent, jnp.where(allowed, jnp.exp(SOFT_CAP * bent), 0.0))


def attend_kernel(q_ref, k_ref, v_ref, start_ref, out_ref, inv_ref):
    first = pl.program_id(0) * QBLK
    keys = pl.ds(pl.multiple_of(first, QBLK), LMAX + QBLK)
    unused_bent, exponent = block_scores(q_ref[...], k_ref[keys], start_ref[...], first)
    inverse = 1.0 / jnp.sum(exponent, axis=-1, keepdims=True)
    weights = (exponent * inverse).astype(BF16)
    out_ref[...] = jnp.dot(weights, v_ref[keys], preferred_element_type=F32).astype(BF16)
    inv_ref[...] = inverse


def attend(queries, key_rows, value_rows, starts):
    rows = queries.shape[0]
    span = key_rows.shape[0]
    row_spec = pl.BlockSpec((QBLK, HD), lambda i: (i, 0))
    one_spec = pl.BlockSpec((QBLK, 1), lambda i: (i, 0))
    all_spec = pl.BlockSpec((span, HD), lambda i: (0, 0))
    return pl.pallas_call(
        attend_kernel,
        out_shape=(
            jax.ShapeDtypeStruct((rows, HD), BF16),
            jax.ShapeDtypeStruct((rows, 1), F32),
        ),
        grid=(rows // QBLK,),
        in_specs=[row_spec, all_spec, all_spec, one_spec],
        out_specs=(row_spec, one_spec),
        compiler_params=pltpu.CompilerParams(vmem_limit_bytes=40 << 20),
        cost_estimate=cost(1),
        name="attend",
    )(queries, key_rows, value_rows, starts)


def attend_back_kernel(q_ref, k_ref, v_ref, start_ref, inv_ref, grad_ref, gq_ref, gk_ref, gv_ref):
    @pl.when(pl.program_id(0) == 0)
    def _():
        gk_ref[...] = jnp.zeros_like(gk_ref)
        gv_ref[...] = jnp.zeros_like(gv_ref)

    first = pl.program_id(0) * QBLK
    keys = pl.ds(pl.multiple_of(first, QBLK), LMAX + QBLK)
    q, k, v, grad = q_ref[...], k_ref[keys], v_ref[keys], grad_ref[...]
    bent, exponent = block_scores(q, k, start_ref[...], first)
    probability = exponent * inv_ref[...]
    grad_prob = lax.dot_general(grad, v, (((1,), (1,)), ((), ())), preferred_element_type=F32)
    inner = jnp.sum(probability * grad_prob, axis=-1, keepdims=True)
    grad_scores = (probability * (grad_prob - inner) * (1.0 - bent * bent)).astype(BF16)
    scale = HD ** (-0.5)
    gq_ref[...] = jnp.dot(grad_scores, k, preferred_element_type=F32) * scale
    over_rows = (((0,), (0,)), ((), ()))
    gk_ref[keys] += lax.dot_general(grad_scores, q, over_rows, preferred_element_type=F32) * scale
    gv_ref[keys] += lax.dot_general(
        probability.astype(BF16), grad, over_rows, preferred_element_type=F32
    )


def attend_back(queries, key_rows, value_rows, starts, inverse, grad):
    rows = queries.shape[0]
    span = key_rows.shape[0]
    row_spec = pl.BlockSpec((QBLK, HD), lambda i: (i, 0))
    one_spec = pl.BlockSpec((QBLK, 1), lambda i: (i, 0))
    all_spec = pl.BlockSpec((span, HD), lambda i: (0, 0))
    return pl.pallas_call(
        attend_back_kernel,
        out_shape=(
            jax.ShapeDtypeStruct((rows, HD), F32),
            jax.ShapeDtypeStruct((span, HD), F32),
            jax.ShapeDtypeStruct((span, HD), F32),
        ),
        grid=(rows // QBLK,),
        in_specs=[row_spec, all_spec, all_spec, one_spec, one_spec, row_spec],
        out_specs=(row_spec, all_spec, all_spec),
        compiler_params=pltpu.CompilerParams(vmem_limit_bytes=48 << 20),
        cost_estimate=pl.CostEstimate(
            flops=10 * rows * (LMAX + QBLK) * HD,
            transcendentals=2 * rows * (LMAX + QBLK),
            bytes_accessed=12 * rows * HD * 2,
        ),
        name="attend_back",
    )(queries, key_rows, value_rows, starts, inverse, grad)


def token_tables(seq_lengths, index_vec):
    count = seq_lengths.shape[0]
    order = jnp.arange(count, dtype=jnp.int32)
    seq_ends = jnp.sum(
        jnp.where(order[None, :] <= order[:, None], seq_lengths[None, :], 0), axis=1
    )
    after_end = index_vec[:, None] >= seq_ends[None, :]
    return index_vec - jnp.sum(jnp.where(after_end, seq_lengths[None, :], 0), axis=1)


def rms_parts(value):
    return lax.rsqrt(jnp.mean(value * value, axis=-1, keepdims=True) + EPSILON)


def rms_forward(value, gain_vec):
    return value * rms_parts(value) * (1.0 + gain_vec)


def rms_backward(value, gain_vec, grad):
    r = rms_parts(value)
    scaled = (1.0 + gain_vec) * grad
    inner = jnp.mean(value * scaled, axis=-1, keepdims=True)
    return (r * scaled - value * (r * r * r * inner), jnp.sum(grad * value * r, axis=0))


def rotate(value, cosine, sine_part):
    half_width = value.shape[-1] // 2
    first_half = value[..., :half_width]
    second_half = value[..., half_width:]
    return jnp.concatenate(
        [
            first_half * cosine - second_half * sine_part,
            second_half * cosine + first_half * sine_part,
        ],
        axis=-1,
    )


def contract_last(left_side, right_side):
    return lax.dot_general(
        left_side, right_side, (((1,), (1,)), ((), ())), preferred_element_type=F32
    )


def contract_first(left_side, right_side):
    return lax.dot_general(
        left_side, right_side, (((0,), (0,)), ((), ())), preferred_element_type=F32
    )


def matmul(left_side, right_side):
    return jnp.dot(left_side, right_side, preferred_element_type=F32)


def gelu_parts(gate):
    k0 = 0.7978845608028654
    k1 = 0.044715
    t = jnp.tanh(k0 * (gate + k1 * gate * gate * gate))
    value = 0.5 * gate * (1.0 + t)
    slope = 0.5 * (1.0 + t) + 0.5 * gate * (1.0 - t * t) * k0 * (1.0 + 3.0 * k1 * gate * gate)
    return (value, slope)


def local(tokens, attn_weights, mlp_weights, norm_gains, seq_lengths, cotangent):
    tok_rows, width = tokens.shape
    peers = lax.axis_size(AXIS)
    planes = peers // PLANE
    share = width // peers
    row_share = attn_weights.shape[0]
    ff = mlp_weights.shape[1] // 3
    ffc = ff // PLANE
    plane_rows = PLANE * tok_rows
    halo = LMAX
    blocks = peers // 16
    over_blocks = [[k * 16 + i for k in range(blocks)] for i in range(16)]
    to_side = [(i, i ^ 4) for i in range(peers)]
    to_far = [(i, i ^ 16) for i in range(peers)]
    across = [[p * PLANE + i for p in range(planes)] for i in range(PLANE)]
    sibling = [(i, i ^ 1) for i in range(peers)]
    to_next = [(i, i + PLANE) for i in range(peers - PLANE)]
    to_prev = [(i + PLANE, i) for i in range(peers - PLANE)]
    me = lax.axis_index(AXIS)
    is_even = (me % 2) == 0
    plane_start = (me // PLANE) * plane_rows

    def gather_across(value):
        return lax.all_gather(value, AXIS, axis=0, tiled=True, axis_index_groups=across)

    def scatter_across(value):
        part = lax.psum_scatter(
            value.astype(BF16), AXIS, scatter_dimension=0, tiled=True, axis_index_groups=across
        )
        return part.reshape(PLANE, -1, part.shape[1])

    column = (me // 4) % 2
    block = (me // 16) % 2

    def send_far(part):
        part = part.reshape(2, 4 * row_share, ffc)
        if blocks == 2:
            return (part, lax.ppermute(part, AXIS, to_far))
        return (
            part,
            lax.all_gather(part, AXIS, axis=0, tiled=False, axis_index_groups=over_blocks),
        )

    def join(part, far, side, far_side):
        if blocks == 2:
            full = assemble(part, far, side, far_side)
        else:
            full = jnp.where(
                column == 0, jnp.stack([far, far_side], axis=2), jnp.stack([far_side, far], axis=2)
            )
        return full.reshape(width, ffc)

    def pick(value, index, axis):
        return lax.dynamic_index_in_dim(value, index, axis, keepdims=False)

    def halve_side(grad):
        grad = grad.reshape(blocks, 2, 2, 4 * row_share, ffc)
        got = lax.ppermute(pick(grad, 1 - column, 2), AXIS, to_side)
        return (pick(grad, column, 2).astype(F32) + got.astype(F32)).astype(BF16)

    def halve_far(part):
        if blocks == 2:
            got = lax.ppermute(pick(part, 1 - block, 0), AXIS, to_far)
            part = (pick(part, block, 0).astype(F32) + got.astype(F32)).astype(BF16)
        else:
            part = lax.psum_scatter(
                part, AXIS, scatter_dimension=0, tiled=True, axis_index_groups=over_blocks
            )
        return part.reshape(PLANE, row_share, ffc)

    gain_block = jnp.pad(norm_gains.astype(F32), ((0, 8 - 4), (0, -share % 128)))
    attn_part, gain_block = lax.optimization_barrier((spread_attn(attn_weights), gain_block))
    attn_cols = gather_across(attn_part.reshape(-1, 3 * HD))
    gate_part, up_part, gain_blocks = spread_gu(mlp_weights, gain_block, peers)
    gain_full = gain_blocks[:, :4, :share].transpose(1, 0, 2).reshape(4, width)
    inputs = tokens.astype(F32)
    down_part, normed = spread_down(
        mlp_weights, rms_forward(inputs, gain_full[0]).astype(BF16)
    )
    gate_part, gate_far = send_far(gate_part)
    up_part, up_far = send_far(up_part)
    down_part, gate_far = lax.optimization_barrier((down_part, gate_far))
    down_part, down_far = send_far(down_part)
    gate_side, up_side, down_side = [
        lax.ppermute(part, AXIS, to_side) for part in (gate_part, up_part, down_part)
    ]
    qkv_cols = attn_cols[:, : 2 * HD]
    out_cols = attn_cols[:, 2 * HD :]

    query_index = plane_start + jnp.arange(plane_rows, dtype=jnp.int32)
    position = token_tables(seq_lengths, query_index)
    starts = (jnp.arange(plane_rows, dtype=jnp.int32) + halo - position)[:, None]
    frequency = 10000.0 ** (-jnp.arange(HD // 2, dtype=F32) * 2.0 / HD)
    angles = position.astype(F32)[:, None] * frequency[None, :]
    cosine, sine_part = jnp.cos(angles), jnp.sin(angles)
    kv_cosine = jnp.where(is_even, cosine, 1.0)
    kv_sine = jnp.where(is_even, sine_part, 0.0)

    projected = matmul(normed, qkv_cols)
    queries = rotate(projected[:, :HD], cosine, sine_part).astype(BF16)
    kv_own = rotate(projected[:, HD:], kv_cosine, kv_sine).astype(BF16)
    kv_halo = lax.ppermute(kv_own[plane_rows - halo :], AXIS, to_next)
    kv_mine = jnp.concatenate([kv_halo, kv_own], axis=0)
    kv_other = lax.ppermute(kv_mine, AXIS, sibling)
    key_rows = jnp.where(is_even, kv_mine, kv_other)
    value_rows = jnp.where(is_even, kv_other, kv_mine)
    attended, inverse = attend(queries, key_rows, value_rows, starts)
    gate_far, attended = lax.optimization_barrier((gate_far, attended))
    gate_far_side = lax.ppermute(gate_far, AXIS, to_side)
    attn_proj = product_scatter([attended], [out_cols], PLANE_STEP, 11, 1)

    middle = inputs + rms_forward(attn_proj, gain_full[1])
    mid_own, up_far = lax.optimization_barrier(
        (rms_forward(middle, gain_full[2]).astype(BF16), up_far)
    )
    up_far_side = lax.ppermute(up_far, AXIS, to_side)
    mid_low = gather_square(mid_own, BLOCK_STEP, 2)
    mid_low, down_far, gate_far_side, up_far_side = lax.optimization_barrier(
        (mid_low, down_far, gate_far_side, up_far_side)
    )
    down_far_side = lax.ppermute(down_far, AXIS, to_side)
    gate_cols = join(gate_part, gate_far, gate_side, gate_far_side)
    gate = matmul(mid_low, gate_cols)
    up_cols = join(up_part, up_far, up_side, up_far_side)
    up = matmul(mid_low, up_cols)
    gelu, slope = gelu_parts(gate)
    hidden = (gelu * up).astype(BF16)
    down_cols = join(down_part, down_far, down_side, down_far_side)
    mlp_raw = product_scatter([hidden], [down_cols], BLOCK_STEP, 9)
    layer_output = (middle + rms_forward(mlp_raw, gain_full[3])).astype(BF16)

    grad_out = cotangent.astype(F32)
    grad_raw, gain_four = rms_backward(mlp_raw, gain_full[3], grad_out)
    grad_raw_low = gather_square(grad_raw.astype(BF16), BLOCK_STEP, 2)
    down_grad = contract_first(grad_raw_low, hidden).astype(BF16)
    down_grad, grad_raw_low = lax.optimization_barrier((down_grad, grad_raw_low))
    down_half = halve_side(down_grad)
    grad_hidden = matmul(grad_raw_low, down_cols)
    grad_gate = (slope * up * grad_hidden).astype(BF16)
    grad_up = (gelu * grad_hidden).astype(BF16)
    gate_grad = contract_first(mid_low, grad_gate).astype(BF16)
    gate_grad, grad_up = lax.optimization_barrier((gate_grad, grad_up))
    gate_half = halve_side(gate_grad)
    up_grad = contract_first(mid_low, grad_up).astype(BF16)
    up_grad, grad_up, down_half = lax.optimization_barrier((up_grad, grad_up, down_half))
    up_half = halve_side(up_grad)
    down_term = halve_far(down_half)
    grad_normed_mid = product_scatter([grad_gate, grad_up], [gate_cols, up_cols], BLOCK_STEP, 10)
    gate_half, grad_normed_mid = lax.optimization_barrier((gate_half, grad_normed_mid))
    gate_term = halve_far(gate_half)
    grad_mid_part, gain_three = rms_backward(middle, gain_full[2], grad_normed_mid)
    grad_middle = grad_out + grad_mid_part

    grad_proj, gain_two = rms_backward(attn_proj, gain_full[1], grad_middle)
    grad_proj_own, up_half = lax.optimization_barrier((grad_proj.astype(BF16), up_half))
    up_term = halve_far(up_half)
    grad_proj_low = gather_square(grad_proj_own, PLANE_STEP, 1)
    grad_att = matmul(grad_proj_low, out_cols).astype(BF16)
    grad_query, grad_keys, grad_values = attend_back(
        queries, key_rows, value_rows, starts, inverse, grad_att
    )
    grad_mine = jnp.where(is_even, grad_keys, grad_values)
    grad_give = jnp.where(is_even, grad_values, grad_keys).astype(BF16)
    grad_kv = grad_mine + lax.ppermute(grad_give, AXIS, sibling).astype(F32)
    grad_back = lax.ppermute(grad_kv[:halo].astype(BF16), AXIS, to_prev).astype(F32)
    grad_kv = grad_kv[halo:] + jnp.pad(grad_back, ((plane_rows - halo, 0), (0, 0)))
    grad_qkv = jnp.concatenate(
        [
            rotate(grad_query, cosine, -sine_part).astype(BF16),
            rotate(grad_kv, kv_cosine, -kv_sine).astype(BF16),
        ],
        axis=1,
    )
    qkv_grad = contract_first(normed, grad_qkv).astype(BF16)
    qkv_grad, grad_qkv, grad_proj_low = lax.optimization_barrier(
        (qkv_grad, grad_qkv, grad_proj_low)
    )
    qkv_term = scatter_across(qkv_grad)
    out_grad = contract_first(grad_proj_low, attended).astype(BF16)
    out_grad, grad_qkv = lax.optimization_barrier((out_grad, grad_qkv))
    out_term = scatter_across(out_grad)
    grad_normed = product_scatter([grad_qkv], [qkv_cols], PLANE_STEP, 12)
    grad_in_part, gain_one = rms_backward(inputs, gain_full[0], grad_normed)
    grad_tokens = (grad_middle + grad_in_part).astype(BF16)

    gain_term = jnp.stack([gain_one, gain_two, gain_three, gain_four], axis=0)
    gain_term = gain_term.reshape(4, peers, share).transpose(1, 0, 2)
    gain_term = jnp.pad(gain_term, ((0, 0), (0, 8 - 4), (0, -share % 128)))
    up_term, gain_term = lax.optimization_barrier((up_term, gain_term))
    mlp_rows = collect_mlp(gate_term, up_term, down_term)
    mlp_rows, qkv_term = lax.optimization_barrier((mlp_rows, qkv_term))
    grad_mlp = mlp_rows.astype(F32)
    qkv_rows, gain_recv = collect_qkv(qkv_term, gain_term)
    qkv_rows, out_term = lax.optimization_barrier((qkv_rows, out_term))
    out_rows = collect_out(out_term)
    grad_attn = jnp.concatenate([qkv_rows, out_rows], axis=1).astype(F32)
    grad_gains = jnp.sum(gain_recv[:, :4, :share], axis=0)
    return (layer_output, grad_tokens, grad_attn, grad_mlp, grad_gains)


def solution(mesh):
    return jax.shard_map(
        local,
        mesh=mesh,
        in_specs=(
            P("fsdp", None),
            P("fsdp", None),
            P("fsdp", None),
            P(None, "fsdp"),
            P(),
            P("fsdp", None),
        ),
        out_specs=(
            P("fsdp", None),
            P("fsdp", None),
            P("fsdp", None),
            P("fsdp", None),
            P(None, "fsdp"),
        ),
        check_vma=False,
    )
```

```python
from functools import partial

import jax
import jax.numpy as jnp
from jax import lax
from jax.experimental import pallas as pl
from jax.experimental.pallas import tpu as pltpu
from jax.sharding import PartitionSpec as P

H = 8
KVH = 4
HD = 256
LMAX = 1024
PLANE = 8
QBLK = 128

EPSILON = 1e-06
SOFT_CAP = 50.0
AXIS = "fsdp"
F32 = jnp.float32
BF16 = jnp.bfloat16
MESH = pl.DeviceIdType.MESH
ANY = pl.BlockSpec(memory_space=pl.ANY)
VMEM = pl.BlockSpec(memory_space=pltpu.VMEM)
DMA = pltpu.SemaphoreType.DMA


def flip(index, step):
    return index + step - 2 * step * ((index // step) % 2)


PLANE_STEP = 4


def partner(index, bits, step):
    for bit, by in ((1, 1), (2, 2), (4, step)):
        if bits & bit:
            index = flip(index, by)
    return index


def place(device, step):
    return device % 4 + 4 * ((device // step) % 2)


def greet(peers):
    barrier = pltpu.get_barrier_semaphore()
    for peer in peers:
        pl.semaphore_signal(barrier, inc=1, device_id=(peer,), device_id_type=MESH)
    pl.semaphore_wait(barrier, len(peers))


class Copies:
    def __init__(self, send_sem, recv_sem):
        self.send_sem, self.recv_sem, self.made = send_sem, recv_sem, []

    def start(self, source, target, device):
        slot = len(self.made)
        copy = pltpu.make_async_remote_copy(
            src_ref=source,
            dst_ref=target,
            send_sem=self.send_sem.at[slot],
            recv_sem=self.recv_sem.at[slot],
            device_id=(device,),
            device_id_type=MESH,
        )
        copy.start()
        self.made.append(copy)
        return copy

    def sent(self):
        for copy in self.made:
            copy.wait_send()


def band(index, size):
    return pl.ds(pl.multiple_of(index * size, 8), size)


def lanes(index, size):
    return pl.ds(pl.multiple_of(index * size, 128), size)


def gather_steps(block_ref, full_ref, copies, own_sem, step):
    rows, width = block_ref.shape
    half = width // 2
    me = lax.axis_index(AXIS)
    sib, xn, yn = flip(me, 1), flip(me, 2), flip(me, step)
    diag = flip(xn, step)

    def at(device, side):
        return full_ref.at[band(place(device, step), rows), pl.ds(side * half, half)]

    def mine(side):
        return block_ref.at[:, pl.ds(side * half, half)]

    own_rows = full_ref.at[band(place(me, step), rows)]
    xa = copies.start(mine(0), at(me, 0), xn)
    ya = copies.start(mine(1), at(me, 1), yn)
    xb = copies.start(mine(1), at(me, 1), xn)
    yb = copies.start(mine(0), at(me, 0), yn)
    arriving = [copies.start(block_ref, own_rows, sib)]
    own = pltpu.make_async_copy(block_ref, own_rows, own_sem)
    own.start()

    def finish():
        def to_sibling(device, side):
            arriving.append(copies.start(at(device, side), at(device, side), sib))

        xa.wait_recv()
        yc = copies.start(at(xn, 0), at(xn, 0), yn)
        to_sibling(xn, 0)
        ya.wait_recv()
        xc = copies.start(at(yn, 1), at(yn, 1), xn)
        to_sibling(yn, 1)
        xb.wait_recv()
        to_sibling(xn, 1)
        yb.wait_recv()
        to_sibling(yn, 0)
        yc.wait_recv()
        to_sibling(diag, 0)
        xc.wait_recv()
        to_sibling(diag, 1)
        for copy in arriving:
            copy.wait_recv()
        own.wait()

    return finish


GATHER_COPIES = 13


def cost(microseconds):
    return pl.CostEstimate(
        flops=int(microseconds * 1.1e9), transcendentals=0, bytes_accessed=int(microseconds * 3.3e6)
    )


def gather_kernel(block_ref, full_ref, own_sem, send_sem, recv_sem, *, step):
    me = lax.axis_index(AXIS)
    greet((flip(me, 1), flip(me, 2), flip(me, step)))
    copies = Copies(send_sem, recv_sem)
    gather_steps(block_ref, full_ref, copies, own_sem, step)()
    copies.sent()


def gather_square(block, step, collective_id):
    rows, width = block.shape
    return pl.pallas_call(
        partial(gather_kernel, step=step),
        out_shape=jax.ShapeDtypeStruct((PLANE * rows, width), block.dtype),
        in_specs=[ANY],
        out_specs=ANY,
        scratch_shapes=[DMA(()), DMA((GATHER_COPIES,)), DMA((GATHER_COPIES,))],
        compiler_params=pltpu.CompilerParams(collective_id=collective_id, has_side_effects=True),
        cost_estimate=cost(42),
        name="gather_square",
    )(block)


W_TILES = 3


def product_scatter_kernel(*refs, pairs, offsets, step):
    left_refs, right_refs, out_ref = refs[:pairs], refs[pairs : 2 * pairs], refs[2 * pairs]
    left_bufs = refs[2 * pairs + 1 : 3 * pairs + 1]
    right_bufs = refs[3 * pairs + 1 : 4 * pairs + 1]
    both, got, ra, rb, ra2, rb2, load_sem, send_sem, recv_sem = refs[4 * pairs + 1 :]
    rows, width = got.shape[1:]
    half = width // 2
    tile = width // W_TILES
    chunk = 16
    me = lax.axis_index(AXIS)
    core = me % 2
    sib, xn, yn = flip(me, 1), flip(me, 2), flip(me, step)
    order = (flip(xn, step), xn, yn, me)
    first, second = pl.ds(0, half), pl.ds(half, half)

    def chip_rows(device):
        return pl.ds(pl.multiple_of((place(device, step) // 2) * 2 * rows, 16), 2 * rows)

    def right_load(j, t):
        r = pl.ds(t * tile, tile)
        source = right_refs[j].at[r, pl.ds(offsets[j], right_bufs[j].shape[1])]
        return pltpu.make_async_copy(source, right_bufs[j].at[r], load_sem.at[j, t])

    def left_load(j, i):
        r = chip_rows(order[i])
        return pltpu.make_async_copy(
            left_refs[j].at[r], left_bufs[j].at[r], load_sem.at[j, W_TILES + i]
        )

    for j in range(pairs):
        left_load(j, 0).start()
    for t in range(W_TILES):
        for j in range(pairs):
            right_load(j, t).start()
    for i in range(1, 4):
        for j in range(pairs):
            left_load(j, i).start()
    greet((sib, xn, yn))
    copies = Copies(send_sem, recv_sem)

    def product(i):
        r = chip_rows(order[i])
        for j in range(pairs):
            left_load(j, i).wait()

        def columns(w):
            total = None
            for j in range(pairs):
                term = contract_last(left_bufs[j][r], right_bufs[j][w])
                total = term if total is None else total + term
            both[i, :, w] = total.astype(BF16)

        if i == 0:
            for t in range(W_TILES):
                for j in range(pairs):
                    right_load(j, t).wait()
                columns(pl.ds(t * tile, tile))
        else:

            @pl.loop(0, W_TILES)
            def _(t):
                columns(pl.ds(pl.multiple_of(t * tile, tile), tile))

    def mine(i, cols=None):
        if cols is None:
            return both.at[i, band(core, rows)]
        return both.at[i, band(core, rows), cols]

    def add(total, other):
        @pl.loop(0, rows // chunk)
        def _(k):
            r = pl.ds(pl.multiple_of(k * chunk, chunk), chunk)
            total[r] = (total[r].astype(F32) + other[r].astype(F32)).astype(total.dtype)

    def make(i):
        product(i)
        crossing = copies.start(both.at[i, band(1 - core, rows)], got.at[i], sib)
        crossing.wait_recv()
        add(mine(i), got.at[i])

    make(0)
    x0 = copies.start(mine(0, first), ra.at[0], xn)
    y0 = copies.start(mine(0, second), rb.at[0], yn)
    make(1)
    x1 = copies.start(mine(1, first), ra.at[1], xn)
    make(2)
    y1 = copies.start(mine(2, second), rb.at[1], yn)
    x0.wait_recv()
    add(mine(2, first), ra.at[0])
    y2 = copies.start(mine(2, first), ra2, yn)
    y0.wait_recv()
    add(mine(1, second), rb.at[0])
    x2 = copies.start(mine(1, second), rb2, xn)
    make(3)
    for copy in (x1, y1, y2, x2):
        copy.wait_recv()
    own = mine(3)

    @pl.loop(0, rows // chunk)
    def _(k):
        r = pl.ds(pl.multiple_of(k * chunk, chunk), chunk)
        out_ref[r, first] = own[r, first].astype(F32) + ra[1, r].astype(F32) + ra2[r].astype(F32)
        out_ref[r, second] = own[r, second].astype(F32) + rb[1, r].astype(F32) + rb2[r].astype(F32)

    copies.sent()


def product_scatter(lefts, rights, offsets, step, collective_id):
    pairs = len(lefts)
    rows, width = lefts[0].shape[0] // PLANE, rights[0].shape[0]
    half = width // 2
    return pl.pallas_call(
        partial(product_scatter_kernel, pairs=pairs, offsets=offsets, step=step),
        out_shape=jax.ShapeDtypeStruct((rows, width), F32),
        in_specs=[ANY] * (2 * pairs),
        out_specs=VMEM,
        scratch_shapes=[
            *[pltpu.VMEM(value.shape, BF16) for value in lefts],
            *[pltpu.VMEM((width, value.shape[1]), BF16) for value in lefts],
            pltpu.VMEM((4, 2 * rows, width), BF16),
            pltpu.VMEM((4, rows, width), BF16),
            pltpu.VMEM((2, rows, half), BF16),
            pltpu.VMEM((2, rows, half), BF16),
            pltpu.VMEM((rows, half), BF16),
            pltpu.VMEM((rows, half), BF16),
            DMA((pairs, W_TILES + 4)),
            DMA((10,)),
            DMA((10,)),
        ],
        compiler_params=pltpu.CompilerParams(
            collective_id=collective_id, has_side_effects=True, vmem_limit_bytes=56 << 20
        ),
        cost_estimate=cost(50),
        name="product_scatter",
    )(*lefts, *rights)


def attn_columns(column):
    query_width = H * HD
    key_offset = query_width + (column % 2) * KVH * HD + (column // 2) * HD
    return (column * HD, key_offset, query_width + 2 * KVH * HD + column * HD)


def greet_all(peers):
    me = lax.axis_index(AXIS)
    barrier = pltpu.get_barrier_semaphore()

    @pl.loop(1, peers)
    def _(k):
        device = lax.rem(me + k, peers)
        pl.semaphore_signal(barrier, inc=1, device_id=(device,), device_id_type=MESH)

    pl.semaphore_wait(barrier, peers - 1)


def exchange_all(source_of, target_ref, send_sem, recv_sem):
    peers = target_ref.shape[0]
    me = lax.axis_index(AXIS)

    def copy(k):
        device = lax.rem(me + k, peers)
        return pltpu.make_async_remote_copy(
            src_ref=source_of(device),
            dst_ref=target_ref.at[me],
            send_sem=send_sem.at[k],
            recv_sem=recv_sem.at[k],
            device_id=(device,),
            device_id_type=MESH,
        )

    @pl.loop(1, peers)
    def _(k):
        copy(k).start()

    def finish():
        @pl.loop(1, peers)
        def _(k):
            copy(k).wait()

    return finish


ORDER = (6, 7, 2, 3, 4, 5, 1)


def swap_steps(pieces_of, targets, copies, own_sem, step):
    me = lax.axis_index(AXIS)
    moved = []
    for bits in ORDER:
        peer = partner(me, bits, step)
        for source, target in zip(pieces_of(place(peer, step)), targets):
            moved.append(copies.start(source, target, peer))
    owns = []
    for slot, (source, target) in enumerate(zip(pieces_of(place(me, step)), targets)):
        own = pltpu.make_async_copy(source, target, own_sem.at[slot])
        own.start()
        owns.append(own)

    def finish():
        for own in owns:
            own.wait()
        for copy in moved:
            copy.wait_recv()

    return finish


def square(step):
    me = lax.axis_index(AXIS)
    return [partner(me, bits, step) for bits in ORDER]


def wide(offset):
    return pl.ds(pl.multiple_of(offset, 128), HD)


def spread_attn_kernel(weights_ref, part_ref, own_sem, send_sem, recv_sem):
    here = place(lax.axis_index(AXIS), PLANE_STEP)
    greet(square(PLANE_STEP))
    copies = Copies(send_sem, recv_sem)
    swap_steps(
        lambda c: [weights_ref.at[:, wide(offset)] for offset in attn_columns(c)],
        [part_ref.at[here, :, pl.ds(slot * HD, HD)] for slot in range(3)],
        copies,
        own_sem,
        PLANE_STEP,
    )()
    copies.sent()


def spread_attn(weights):
    rows = weights.shape[0]
    return pl.pallas_call(
        spread_attn_kernel,
        out_shape=jax.ShapeDtypeStruct((PLANE, rows, 3 * HD), BF16),
        in_specs=[ANY],
        out_specs=ANY,
        scratch_shapes=[DMA((3,)), DMA((21,)), DMA((21,))],
        compiler_params=pltpu.CompilerParams(collective_id=3, has_side_effects=True),
        name="spread_attn",
    )(weights)


def spread_gu_kernel(
    weights_ref, gain_ref, gu_ref, gains_ref, own_sem, send_sem, recv_sem, gain_send, gain_recv
):
    peers = gains_ref.shape[0]
    ffc = gu_ref.shape[2] // 2
    me = lax.axis_index(AXIS)
    here = place(me, PLANE_STEP)
    greet_all(peers)
    gains_done = exchange_all(lambda device: gain_ref, gains_ref, gain_send, gain_recv)
    own = pltpu.make_async_copy(gain_ref, gains_ref.at[me], own_sem.at[2])
    own.start()
    copies = Copies(send_sem, recv_sem)
    swap_steps(
        lambda c: [weights_ref.at[:, lanes(slot * PLANE + c, ffc)] for slot in range(2)],
        [gu_ref.at[here, :, pl.ds(slot * ffc, ffc)] for slot in range(2)],
        copies,
        own_sem,
        PLANE_STEP,
    )()
    own.wait()
    gains_done()
    copies.sent()


def spread_gu(weights, gain_block, peers):
    rows = weights.shape[0]
    ffc = weights.shape[1] // 3 // PLANE
    return pl.pallas_call(
        spread_gu_kernel,
        out_shape=(
            jax.ShapeDtypeStruct((PLANE, rows, 2 * ffc), BF16),
            jax.ShapeDtypeStruct((peers,) + gain_block.shape, gain_block.dtype),
        ),
        in_specs=[ANY, ANY],
        out_specs=(ANY, ANY),
        scratch_shapes=[DMA((3,)), DMA((14,)), DMA((14,)), DMA((peers,)), DMA((peers,))],
        compiler_params=pltpu.CompilerParams(collective_id=4, has_side_effects=True),
        cost_estimate=cost(38),
        name="spread_gu",
    )(weights, gain_block)


def spread_down_kernel(weights_ref, block_ref, down_ref, full_ref, own_sem, send_sem, recv_sem):
    ffc = down_ref.shape[2]
    me = lax.axis_index(AXIS)
    greet(square(PLANE_STEP))
    copies = Copies(send_sem, recv_sem)
    gathered = gather_steps(block_ref, full_ref, copies, own_sem.at[1], PLANE_STEP)
    spread = swap_steps(
        lambda c: [weights_ref.at[:, lanes(2 * PLANE + c, ffc)]],
        [down_ref.at[place(me, PLANE_STEP)]],
        copies,
        own_sem,
        PLANE_STEP,
    )
    gathered()
    spread()
    copies.sent()


def spread_down(weights, block):
    rows = weights.shape[0]
    ffc = weights.shape[1] // 3 // PLANE
    count = GATHER_COPIES + 7
    return pl.pallas_call(
        spread_down_kernel,
        out_shape=(
            jax.ShapeDtypeStruct((PLANE, rows, ffc), BF16),
            jax.ShapeDtypeStruct((PLANE * block.shape[0], block.shape[1]), BF16),
        ),
        in_specs=[ANY, ANY],
        out_specs=(ANY, ANY),
        scratch_shapes=[DMA((2,)), DMA((count,)), DMA((count,))],
        compiler_params=pltpu.CompilerParams(collective_id=5, has_side_effects=True),
        cost_estimate=cost(1),
        name="spread_down",
    )(weights, block)


def collect_kernel(*refs, count):
    term_refs, rows_ref = refs[:count], refs[count]
    own_sem, send_sem, recv_sem = refs[count + 1 :]
    ffc = term_refs[0].shape[2]
    here = place(lax.axis_index(AXIS), PLANE_STEP)
    greet(square(PLANE_STEP))
    copies = Copies(send_sem, recv_sem)
    swap_steps(
        lambda c: [term.at[c] for term in term_refs],
        [rows_ref.at[:, lanes(slot * PLANE + here, ffc)] for slot in range(count)],
        copies,
        own_sem,
        PLANE_STEP,
    )()
    copies.sent()


def collect(terms, collective_id):
    count = len(terms)
    rows, ffc = terms[0].shape[1:]
    return pl.pallas_call(
        partial(collect_kernel, count=count),
        out_shape=jax.ShapeDtypeStruct((rows, count * PLANE * ffc), BF16),
        in_specs=[ANY] * count,
        out_specs=ANY,
        scratch_shapes=[DMA((count,)), DMA((7 * count,)), DMA((7 * count,))],
        compiler_params=pltpu.CompilerParams(collective_id=collective_id, has_side_effects=True),
        cost_estimate=cost(15 * count),
        name="collect",
    )(*terms)


def collect_qkv_kernel(
    qkv_ref, gain_ref, rows_ref, gains_ref, own_sem, send_sem, recv_sem, gain_send, gain_recv
):
    me = lax.axis_index(AXIS)
    greet_all(gain_ref.shape[0])
    copies = Copies(send_sem, recv_sem)
    moved = swap_steps(
        lambda c: [qkv_ref.at[c, :, pl.ds(0, HD)], qkv_ref.at[c, :, pl.ds(HD, HD)]],
        [rows_ref.at[:, wide(offset)] for offset in attn_columns(place(me, PLANE_STEP))[:2]],
        copies,
        own_sem,
        PLANE_STEP,
    )
    gains_done = exchange_all(lambda device: gain_ref.at[device], gains_ref, gain_send, gain_recv)
    own = pltpu.make_async_copy(gain_ref.at[me], gains_ref.at[me], own_sem.at[2])
    own.start()
    moved()
    own.wait()
    gains_done()
    copies.sent()


def collect_qkv(qkv_term, gain_blocks):
    rows = qkv_term.shape[1]
    peers = gain_blocks.shape[0]
    return pl.pallas_call(
        collect_qkv_kernel,
        out_shape=(
            jax.ShapeDtypeStruct((rows, (H + 2 * KVH) * HD), BF16),
            jax.ShapeDtypeStruct(gain_blocks.shape, gain_blocks.dtype),
        ),
        in_specs=[ANY, ANY],
        out_specs=(ANY, ANY),
        scratch_shapes=[DMA((3,)), DMA((14,)), DMA((14,)), DMA((peers,)), DMA((peers,))],
        compiler_params=pltpu.CompilerParams(collective_id=7, has_side_effects=True),
        name="collect_qkv",
    )(qkv_term, gain_blocks)


def block_scores(q, k, start, first):
    scores = lax.dot_general(q, k, (((1,), (1,)), ((), ())), preferred_element_type=F32)
    bent = jnp.tanh(scores * (HD ** (-0.5) / SOFT_CAP))
    rows, span = scores.shape
    key_at = lax.broadcasted_iota(jnp.int32, (rows, span), 1)
    row_at = lax.broadcasted_iota(jnp.int32, (rows, span), 0)
    allowed = (key_at + first >= start) & (key_at <= row_at + LMAX)
    return (bent, jnp.where(allowed, jnp.exp(SOFT_CAP * bent), 0.0))


def attend_kernel(q_ref, k_ref, v_ref, start_ref, out_ref, inv_ref):
    first = pl.program_id(0) * QBLK
    keys = pl.ds(pl.multiple_of(first, QBLK), LMAX + QBLK)
    unused_bent, exponent = block_scores(q_ref[...], k_ref[keys], start_ref[...], first)
    inverse = 1.0 / jnp.sum(exponent, axis=-1, keepdims=True)
    weights = (exponent * inverse).astype(BF16)
    out_ref[...] = jnp.dot(weights, v_ref[keys], preferred_element_type=F32).astype(BF16)
    inv_ref[...] = inverse


def attend(queries, key_rows, value_rows, starts):
    rows = queries.shape[0]
    span = key_rows.shape[0]
    row_spec = pl.BlockSpec((QBLK, HD), lambda i: (i, 0))
    one_spec = pl.BlockSpec((QBLK, 1), lambda i: (i, 0))
    all_spec = pl.BlockSpec((span, HD), lambda i: (0, 0))
    return pl.pallas_call(
        attend_kernel,
        out_shape=(
            jax.ShapeDtypeStruct((rows, HD), BF16),
            jax.ShapeDtypeStruct((rows, 1), F32),
        ),
        grid=(rows // QBLK,),
        in_specs=[row_spec, all_spec, all_spec, one_spec],
        out_specs=(row_spec, one_spec),
        compiler_params=pltpu.CompilerParams(vmem_limit_bytes=40 << 20),
        cost_estimate=cost(1),
        name="attend",
    )(queries, key_rows, value_rows, starts)


def attend_back_kernel(q_ref, k_ref, v_ref, start_ref, inv_ref, grad_ref, gq_ref, gk_ref, gv_ref):
    @pl.when(pl.program_id(0) == 0)
    def _():
        gk_ref[...] = jnp.zeros_like(gk_ref)
        gv_ref[...] = jnp.zeros_like(gv_ref)

    first = pl.program_id(0) * QBLK
    keys = pl.ds(pl.multiple_of(first, QBLK), LMAX + QBLK)
    q, k, v, grad = q_ref[...], k_ref[keys], v_ref[keys], grad_ref[...]
    bent, exponent = block_scores(q, k, start_ref[...], first)
    probability = exponent * inv_ref[...]
    grad_prob = lax.dot_general(grad, v, (((1,), (1,)), ((), ())), preferred_element_type=F32)
    inner = jnp.sum(probability * grad_prob, axis=-1, keepdims=True)
    grad_scores = (probability * (grad_prob - inner) * (1.0 - bent * bent)).astype(BF16)
    scale = HD ** (-0.5)
    gq_ref[...] = jnp.dot(grad_scores, k, preferred_element_type=F32) * scale
    over_rows = (((0,), (0,)), ((), ()))
    gk_ref[keys] += lax.dot_general(grad_scores, q, over_rows, preferred_element_type=F32) * scale
    gv_ref[keys] += lax.dot_general(
        probability.astype(BF16), grad, over_rows, preferred_element_type=F32
    )


def attend_back(queries, key_rows, value_rows, starts, inverse, grad):
    rows = queries.shape[0]
    span = key_rows.shape[0]
    row_spec = pl.BlockSpec((QBLK, HD), lambda i: (i, 0))
    one_spec = pl.BlockSpec((QBLK, 1), lambda i: (i, 0))
    all_spec = pl.BlockSpec((span, HD), lambda i: (0, 0))
    return pl.pallas_call(
        attend_back_kernel,
        out_shape=(
            jax.ShapeDtypeStruct((rows, HD), F32),
            jax.ShapeDtypeStruct((span, HD), F32),
            jax.ShapeDtypeStruct((span, HD), F32),
        ),
        grid=(rows // QBLK,),
        in_specs=[row_spec, all_spec, all_spec, one_spec, one_spec, row_spec],
        out_specs=(row_spec, all_spec, all_spec),
        compiler_params=pltpu.CompilerParams(vmem_limit_bytes=48 << 20),
        cost_estimate=pl.CostEstimate(
            flops=10 * rows * (LMAX + QBLK) * HD,
            transcendentals=2 * rows * (LMAX + QBLK),
            bytes_accessed=12 * rows * HD * 2,
        ),
        name="attend_back",
    )(queries, key_rows, value_rows, starts, inverse, grad)


def token_tables(seq_lengths, index_vec):
    count = seq_lengths.shape[0]
    order = jnp.arange(count, dtype=jnp.int32)
    seq_ends = jnp.sum(
        jnp.where(order[None, :] <= order[:, None], seq_lengths[None, :], 0), axis=1
    )
    after_end = index_vec[:, None] >= seq_ends[None, :]
    return index_vec - jnp.sum(jnp.where(after_end, seq_lengths[None, :], 0), axis=1)


def rms_parts(value):
    return lax.rsqrt(jnp.mean(value * value, axis=-1, keepdims=True) + EPSILON)


def rms_forward(value, gain_vec):
    return value * rms_parts(value) * (1.0 + gain_vec)


def rms_backward(value, gain_vec, grad):
    r = rms_parts(value)
    scaled = (1.0 + gain_vec) * grad
    inner = jnp.mean(value * scaled, axis=-1, keepdims=True)
    return (r * scaled - value * (r * r * r * inner), jnp.sum(grad * value * r, axis=0))


def rotate(value, cosine, sine_part):
    half_width = value.shape[-1] // 2
    first_half = value[..., :half_width]
    second_half = value[..., half_width:]
    return jnp.concatenate(
        [
            first_half * cosine - second_half * sine_part,
            second_half * cosine + first_half * sine_part,
        ],
        axis=-1,
    )


def contract_last(left_side, right_side):
    return lax.dot_general(
        left_side, right_side, (((1,), (1,)), ((), ())), preferred_element_type=F32
    )


def contract_first(left_side, right_side):
    return lax.dot_general(
        left_side, right_side, (((0,), (0,)), ((), ())), preferred_element_type=F32
    )


def matmul(left_side, right_side):
    return jnp.dot(left_side, right_side, preferred_element_type=F32)


def gelu_parts(gate):
    k0 = 0.7978845608028654
    k1 = 0.044715
    t = jnp.tanh(k0 * (gate + k1 * gate * gate * gate))
    value = 0.5 * gate * (1.0 + t)
    slope = 0.5 * (1.0 + t) + 0.5 * gate * (1.0 - t * t) * k0 * (1.0 + 3.0 * k1 * gate * gate)
    return (value, slope)


def local(tokens, attn_weights, mlp_weights, norm_gains, seq_lengths, cotangent):
    tok_rows, width = tokens.shape
    peers = lax.axis_size(AXIS)
    planes = peers // PLANE
    share = width // peers
    row_share = attn_weights.shape[0]
    ff = mlp_weights.shape[1] // 3
    ffc = ff // PLANE
    plane_rows = PLANE * tok_rows
    halo = LMAX
    across = [[p * PLANE + i for p in range(planes)] for i in range(PLANE)]
    sibling = [(i, i ^ 1) for i in range(peers)]
    to_next = [(i, i + PLANE) for i in range(peers - PLANE)]
    to_prev = [(i + PLANE, i) for i in range(peers - PLANE)]
    me = lax.axis_index(AXIS)
    is_even = (me % 2) == 0
    plane_start = (me // PLANE) * plane_rows

    def gather_across(value):
        return lax.all_gather(value, AXIS, axis=0, tiled=True, axis_index_groups=across)

    def scatter_across(value):
        part = lax.psum_scatter(
            value.astype(BF16), AXIS, scatter_dimension=0, tiled=True, axis_index_groups=across
        )
        return part.reshape(PLANE, -1, part.shape[1])

    gain_block = jnp.pad(norm_gains.astype(F32), ((0, 8 - 4), (0, -share % 128)))
    attn_part, gain_block = lax.optimization_barrier((spread_attn(attn_weights), gain_block))
    attn_cols = gather_across(attn_part.reshape(-1, 3 * HD))
    gu_part, gain_blocks = spread_gu(mlp_weights, gain_block, peers)
    gain_full = gain_blocks[:, :4, :share].transpose(1, 0, 2).reshape(4, width)
    inputs = tokens.astype(F32)
    down_part, normed = spread_down(
        mlp_weights, rms_forward(inputs, gain_full[0]).astype(BF16)
    )
    gu_cols = gather_across(gu_part.reshape(-1, 2 * ffc))
    down_cols = gather_across(down_part.reshape(-1, ffc))
    qkv_cols = attn_cols[:, : 2 * HD]
    out_cols = attn_cols[:, 2 * HD :]

    query_index = plane_start + jnp.arange(plane_rows, dtype=jnp.int32)
    position = token_tables(seq_lengths, query_index)
    starts = (jnp.arange(plane_rows, dtype=jnp.int32) + halo - position)[:, None]
    frequency = 10000.0 ** (-jnp.arange(HD // 2, dtype=F32) * 2.0 / HD)
    angles = position.astype(F32)[:, None] * frequency[None, :]
    cosine, sine_part = jnp.cos(angles), jnp.sin(angles)
    kv_cosine = jnp.where(is_even, cosine, 1.0)
    kv_sine = jnp.where(is_even, sine_part, 0.0)

    projected = matmul(normed, qkv_cols)
    queries = rotate(projected[:, :HD], cosine, sine_part).astype(BF16)
    kv_own = rotate(projected[:, HD:], kv_cosine, kv_sine).astype(BF16)
    kv_halo = lax.ppermute(kv_own[plane_rows - halo :], AXIS, to_next)
    kv_mine = jnp.concatenate([kv_halo, kv_own], axis=0)
    kv_other = lax.ppermute(kv_mine, AXIS, sibling)
    key_rows = jnp.where(is_even, kv_mine, kv_other)
    value_rows = jnp.where(is_even, kv_other, kv_mine)
    attended, inverse = attend(queries, key_rows, value_rows, starts)
    attn_proj = product_scatter([attended], [out_cols], [0], PLANE_STEP, 11)

    middle = inputs + rms_forward(attn_proj, gain_full[1])
    mid_low = gather_square(rms_forward(middle, gain_full[2]).astype(BF16), PLANE_STEP, 1)
    gate_up = matmul(mid_low, gu_cols)
    gate, up = gate_up[:, :ffc], gate_up[:, ffc:]
    gelu, slope = gelu_parts(gate)
    hidden = (gelu * up).astype(BF16)
    mlp_raw = product_scatter([hidden], [down_cols], [0], PLANE_STEP, 9)
    layer_output = (middle + rms_forward(mlp_raw, gain_full[3])).astype(BF16)

    grad_out = cotangent.astype(F32)
    grad_raw, gain_four = rms_backward(mlp_raw, gain_full[3], grad_out)
    grad_raw_low = gather_square(grad_raw.astype(BF16), PLANE_STEP, 1)
    down_grad = contract_first(grad_raw_low, hidden).astype(BF16)
    down_grad, grad_raw_low = lax.optimization_barrier((down_grad, grad_raw_low))
    down_term = scatter_across(down_grad)
    grad_hidden = matmul(grad_raw_low, down_cols)
    grad_gate = (slope * up * grad_hidden).astype(BF16)
    grad_up = (gelu * grad_hidden).astype(BF16)
    gate_grad = contract_first(mid_low, grad_gate).astype(BF16)
    gate_grad, grad_up = lax.optimization_barrier((gate_grad, grad_up))
    gate_term = scatter_across(gate_grad)
    up_grad = contract_first(mid_low, grad_up).astype(BF16)
    up_grad, grad_up = lax.optimization_barrier((up_grad, grad_up))
    up_term = scatter_across(up_grad)
    grad_normed_mid = product_scatter(
        [grad_gate, grad_up], [gu_cols, gu_cols], [0, ffc], PLANE_STEP, 10
    )
    grad_mid_part, gain_three = rms_backward(middle, gain_full[2], grad_normed_mid)
    grad_middle = grad_out + grad_mid_part

    grad_proj, gain_two = rms_backward(attn_proj, gain_full[1], grad_middle)
    grad_proj_own, down_term = lax.optimization_barrier((grad_proj.astype(BF16), down_term))
    grad_proj_low = gather_square(grad_proj_own, PLANE_STEP, 1)
    grad_att = matmul(grad_proj_low, out_cols).astype(BF16)
    grad_query, grad_keys, grad_values = attend_back(
        queries, key_rows, value_rows, starts, inverse, grad_att
    )
    grad_mine = jnp.where(is_even, grad_keys, grad_values)
    grad_give = jnp.where(is_even, grad_values, grad_keys).astype(BF16)
    grad_kv = grad_mine + lax.ppermute(grad_give, AXIS, sibling).astype(F32)
    grad_back = lax.ppermute(grad_kv[:halo].astype(BF16), AXIS, to_prev).astype(F32)
    down_term, gate_term, grad_kv = lax.optimization_barrier((down_term, gate_term, grad_kv))
    gate_rows, down_rows = jnp.split(collect([gate_term, down_term], 6), 2, axis=1)
    gate_rows, down_rows, grad_back = lax.optimization_barrier((gate_rows, down_rows, grad_back))
    grad_kv = grad_kv[halo:] + jnp.pad(grad_back, ((plane_rows - halo, 0), (0, 0)))
    grad_qkv = jnp.concatenate(
        [
            rotate(grad_query, cosine, -sine_part).astype(BF16),
            rotate(grad_kv, kv_cosine, -kv_sine).astype(BF16),
        ],
        axis=1,
    )
    qkv_grad = contract_first(normed, grad_qkv).astype(BF16)
    qkv_grad, grad_qkv, grad_proj_low = lax.optimization_barrier(
        (qkv_grad, grad_qkv, grad_proj_low)
    )
    qkv_term = scatter_across(qkv_grad)
    out_grad = contract_first(grad_proj_low, attended).astype(BF16)
    out_grad, grad_qkv = lax.optimization_barrier((out_grad, grad_qkv))
    out_term = scatter_across(out_grad)
    grad_normed = product_scatter([grad_qkv], [qkv_cols], [0], PLANE_STEP, 12)
    grad_in_part, gain_one = rms_backward(inputs, gain_full[0], grad_normed)
    grad_tokens = (grad_middle + grad_in_part).astype(BF16)

    gain_term = jnp.stack([gain_one, gain_two, gain_three, gain_four], axis=0)
    gain_term = gain_term.reshape(4, peers, share).transpose(1, 0, 2)
    gain_term = jnp.pad(gain_term, ((0, 0), (0, 8 - 4), (0, -share % 128)))
    up_term, gain_term = lax.optimization_barrier((up_term, gain_term))
    up_rows = collect([up_term], 13)
    up_rows, qkv_term = lax.optimization_barrier((up_rows, qkv_term))
    grad_mlp = jnp.concatenate([gate_rows, up_rows, down_rows], axis=1).astype(F32)
    qkv_rows, gain_recv = collect_qkv(qkv_term, gain_term)
    qkv_rows, out_term = lax.optimization_barrier((qkv_rows, out_term))
    out_rows = collect([out_term], 8)
    grad_attn = jnp.concatenate([qkv_rows, out_rows], axis=1).astype(F32)
    grad_gains = jnp.sum(gain_recv[:, :4, :share], axis=0)
    return (layer_output, grad_tokens, grad_attn, grad_mlp, grad_gains)


def solution(mesh):
    return jax.shard_map(
        local,
        mesh=mesh,
        in_specs=(
            P("fsdp", None),
            P("fsdp", None),
            P("fsdp", None),
            P(None, "fsdp"),
            P(),
            P("fsdp", None),
        ),
        out_specs=(
            P("fsdp", None),
            P("fsdp", None),
            P("fsdp", None),
            P("fsdp", None),
            P(None, "fsdp"),
        ),
        check_vma=False,
    )
```

```python
from functools import partial

import jax
import jax.numpy as jnp
from jax import lax
from jax.experimental import pallas as pl
from jax.experimental.pallas import tpu as pltpu
from jax.sharding import PartitionSpec as P

H = 8
KVH = 4
HD = 256
LMAX = 1024
PLANE = 8
QBLK = 128

EPSILON = 1e-06
SOFT_CAP = 50.0
AXIS = "fsdp"
F32 = jnp.float32
BF16 = jnp.bfloat16
MESH = pl.DeviceIdType.MESH
ANY = pl.BlockSpec(memory_space=pl.ANY)
VMEM = pl.BlockSpec(memory_space=pltpu.VMEM)
DMA = pltpu.SemaphoreType.DMA


def flip(index, step):
    return index + step - 2 * step * ((index // step) % 2)


PLANE_STEP = 4


def partner(index, bits, step):
    for bit, by in ((1, 1), (2, 2), (4, step)):
        if bits & bit:
            index = flip(index, by)
    return index


def place(device, step):
    return device % 4 + 4 * ((device // step) % 2)


def greet(peers):
    barrier = pltpu.get_barrier_semaphore()
    for peer in peers:
        pl.semaphore_signal(barrier, inc=1, device_id=(peer,), device_id_type=MESH)
    pl.semaphore_wait(barrier, len(peers))


class Copies:
    def __init__(self, send_sem, recv_sem):
        self.send_sem, self.recv_sem, self.made = send_sem, recv_sem, []

    def start(self, source, target, device):
        slot = len(self.made)
        copy = pltpu.make_async_remote_copy(
            src_ref=source,
            dst_ref=target,
            send_sem=self.send_sem.at[slot],
            recv_sem=self.recv_sem.at[slot],
            device_id=(device,),
            device_id_type=MESH,
        )
        copy.start()
        self.made.append(copy)
        return copy

    def sent(self):
        for copy in self.made:
            copy.wait_send()


def band(index, size):
    return pl.ds(pl.multiple_of(index * size, 8), size)


def lanes(index, size):
    return pl.ds(pl.multiple_of(index * size, 128), size)


def gather_steps(block_ref, full_ref, copies, own_sem, step):
    rows, width = block_ref.shape
    half = width // 2
    me = lax.axis_index(AXIS)
    sib, xn, yn = flip(me, 1), flip(me, 2), flip(me, step)
    diag = flip(xn, step)

    def at(device, side):
        return full_ref.at[band(place(device, step), rows), pl.ds(side * half, half)]

    def mine(side):
        return block_ref.at[:, pl.ds(side * half, half)]

    own_rows = full_ref.at[band(place(me, step), rows)]
    xa = copies.start(mine(0), at(me, 0), xn)
    ya = copies.start(mine(1), at(me, 1), yn)
    xb = copies.start(mine(1), at(me, 1), xn)
    yb = copies.start(mine(0), at(me, 0), yn)
    arriving = [copies.start(block_ref, own_rows, sib)]
    own = pltpu.make_async_copy(block_ref, own_rows, own_sem)
    own.start()

    def finish():
        def to_sibling(device, side):
            arriving.append(copies.start(at(device, side), at(device, side), sib))

        xa.wait_recv()
        yc = copies.start(at(xn, 0), at(xn, 0), yn)
        to_sibling(xn, 0)
        ya.wait_recv()
        xc = copies.start(at(yn, 1), at(yn, 1), xn)
        to_sibling(yn, 1)
        xb.wait_recv()
        to_sibling(xn, 1)
        yb.wait_recv()
        to_sibling(yn, 0)
        yc.wait_recv()
        to_sibling(diag, 0)
        xc.wait_recv()
        to_sibling(diag, 1)
        for copy in arriving:
            copy.wait_recv()
        own.wait()

    return finish


GATHER_COPIES = 13


def cost(microseconds):
    return pl.CostEstimate(
        flops=int(microseconds * 1e7), transcendentals=0, bytes_accessed=int(microseconds * 3e4)
    )


def gather_kernel(block_ref, full_ref, own_sem, send_sem, recv_sem, *, step):
    me = lax.axis_index(AXIS)
    greet((flip(me, 1), flip(me, 2), flip(me, step)))
    copies = Copies(send_sem, recv_sem)
    gather_steps(block_ref, full_ref, copies, own_sem, step)()
    copies.sent()


def gather_square(block, step, collective_id):
    rows, width = block.shape
    return pl.pallas_call(
        partial(gather_kernel, step=step),
        out_shape=jax.ShapeDtypeStruct((PLANE * rows, width), block.dtype),
        in_specs=[ANY],
        out_specs=ANY,
        scratch_shapes=[DMA(()), DMA((GATHER_COPIES,)), DMA((GATHER_COPIES,))],
        compiler_params=pltpu.CompilerParams(collective_id=collective_id, has_side_effects=True),
        cost_estimate=cost(42),
        name="gather_square",
    )(block)


W_TILES = 3


def product_scatter_kernel(*refs, pairs, offsets, step):
    left_refs, right_refs, out_ref = refs[:pairs], refs[pairs : 2 * pairs], refs[2 * pairs]
    left_bufs = refs[2 * pairs + 1 : 3 * pairs + 1]
    right_bufs = refs[3 * pairs + 1 : 4 * pairs + 1]
    both, got, ra, rb, ra2, rb2, load_sem, send_sem, recv_sem = refs[4 * pairs + 1 :]
    rows, width = got.shape[1:]
    half = width // 2
    tile = width // W_TILES
    chunk = 16
    me = lax.axis_index(AXIS)
    core = me % 2
    sib, xn, yn = flip(me, 1), flip(me, 2), flip(me, step)
    order = (flip(xn, step), xn, yn, me)
    first, second = pl.ds(0, half), pl.ds(half, half)

    def chip_rows(device):
        return pl.ds(pl.multiple_of((place(device, step) // 2) * 2 * rows, 16), 2 * rows)

    def right_load(j, t):
        r = pl.ds(t * tile, tile)
        source = right_refs[j].at[r, pl.ds(offsets[j], right_bufs[j].shape[1])]
        return pltpu.make_async_copy(source, right_bufs[j].at[r], load_sem.at[j, t])

    def left_load(j, i):
        r = chip_rows(order[i])
        return pltpu.make_async_copy(
            left_refs[j].at[r], left_bufs[j].at[r], load_sem.at[j, W_TILES + i]
        )

    for j in range(pairs):
        left_load(j, 0).start()
    for t in range(W_TILES):
        for j in range(pairs):
            right_load(j, t).start()
    for i in range(1, 4):
        for j in range(pairs):
            left_load(j, i).start()
    greet((sib, xn, yn))
    copies = Copies(send_sem, recv_sem)

    def product(i):
        r = chip_rows(order[i])
        for j in range(pairs):
            left_load(j, i).wait()

        def columns(w):
            total = None
            for j in range(pairs):
                term = contract_last(left_bufs[j][r], right_bufs[j][w])
                total = term if total is None else total + term
            both[i, :, w] = total.astype(BF16)

        if i == 0:
            for t in range(W_TILES):
                for j in range(pairs):
                    right_load(j, t).wait()
                columns(pl.ds(t * tile, tile))
        else:

            @pl.loop(0, W_TILES)
            def _(t):
                columns(pl.ds(pl.multiple_of(t * tile, tile), tile))

    def mine(i, cols=None):
        if cols is None:
            return both.at[i, band(core, rows)]
        return both.at[i, band(core, rows), cols]

    def add(total, other):
        @pl.loop(0, rows // chunk)
        def _(k):
            r = pl.ds(pl.multiple_of(k * chunk, chunk), chunk)
            total[r] = (total[r].astype(F32) + other[r].astype(F32)).astype(total.dtype)

    def make(i):
        product(i)
        crossing = copies.start(both.at[i, band(1 - core, rows)], got.at[i], sib)
        crossing.wait_recv()
        add(mine(i), got.at[i])

    make(0)
    x0 = copies.start(mine(0, first), ra.at[0], xn)
    y0 = copies.start(mine(0, second), rb.at[0], yn)
    make(1)
    x1 = copies.start(mine(1, first), ra.at[1], xn)
    make(2)
    y1 = copies.start(mine(2, second), rb.at[1], yn)
    x0.wait_recv()
    add(mine(2, first), ra.at[0])
    y2 = copies.start(mine(2, first), ra2, yn)
    y0.wait_recv()
    add(mine(1, second), rb.at[0])
    x2 = copies.start(mine(1, second), rb2, xn)
    make(3)
    for copy in (x1, y1, y2, x2):
        copy.wait_recv()
    own = mine(3)

    @pl.loop(0, rows // chunk)
    def _(k):
        r = pl.ds(pl.multiple_of(k * chunk, chunk), chunk)
        out_ref[r, first] = own[r, first].astype(F32) + ra[1, r].astype(F32) + ra2[r].astype(F32)
        out_ref[r, second] = own[r, second].astype(F32) + rb[1, r].astype(F32) + rb2[r].astype(F32)

    copies.sent()


def product_scatter(lefts, rights, offsets, step, collective_id):
    pairs = len(lefts)
    rows, width = lefts[0].shape[0] // PLANE, rights[0].shape[0]
    half = width // 2
    return pl.pallas_call(
        partial(product_scatter_kernel, pairs=pairs, offsets=offsets, step=step),
        out_shape=jax.ShapeDtypeStruct((rows, width), F32),
        in_specs=[ANY] * (2 * pairs),
        out_specs=VMEM,
        scratch_shapes=[
            *[pltpu.VMEM(value.shape, BF16) for value in lefts],
            *[pltpu.VMEM((width, value.shape[1]), BF16) for value in lefts],
            pltpu.VMEM((4, 2 * rows, width), BF16),
            pltpu.VMEM((4, rows, width), BF16),
            pltpu.VMEM((2, rows, half), BF16),
            pltpu.VMEM((2, rows, half), BF16),
            pltpu.VMEM((rows, half), BF16),
            pltpu.VMEM((rows, half), BF16),
            DMA((pairs, W_TILES + 4)),
            DMA((10,)),
            DMA((10,)),
        ],
        compiler_params=pltpu.CompilerParams(
            collective_id=collective_id, has_side_effects=True, vmem_limit_bytes=56 << 20
        ),
        cost_estimate=cost(50),
        name="product_scatter",
    )(*lefts, *rights)


def attn_columns(column):
    query_width = H * HD
    key_offset = query_width + (column % 2) * KVH * HD + (column // 2) * HD
    return (column * HD, key_offset, query_width + 2 * KVH * HD + column * HD)


def greet_all(peers):
    me = lax.axis_index(AXIS)
    barrier = pltpu.get_barrier_semaphore()

    @pl.loop(1, peers)
    def _(k):
        device = lax.rem(me + k, peers)
        pl.semaphore_signal(barrier, inc=1, device_id=(device,), device_id_type=MESH)

    pl.semaphore_wait(barrier, peers - 1)


def exchange_all(source_of, target_ref, send_sem, recv_sem):
    peers = target_ref.shape[0]
    me = lax.axis_index(AXIS)

    def copy(k):
        device = lax.rem(me + k, peers)
        return pltpu.make_async_remote_copy(
            src_ref=source_of(device),
            dst_ref=target_ref.at[me],
            send_sem=send_sem.at[k],
            recv_sem=recv_sem.at[k],
            device_id=(device,),
            device_id_type=MESH,
        )

    @pl.loop(1, peers)
    def _(k):
        copy(k).start()

    def finish():
        @pl.loop(1, peers)
        def _(k):
            copy(k).wait()

    return finish


ORDER = (6, 7, 2, 3, 4, 5, 1)


def swap_steps(pieces_of, targets, copies, own_sem, step):
    me = lax.axis_index(AXIS)
    moved = []
    for bits in ORDER:
        peer = partner(me, bits, step)
        for source, target in zip(pieces_of(place(peer, step)), targets):
            moved.append(copies.start(source, target, peer))
    owns = []
    for slot, (source, target) in enumerate(zip(pieces_of(place(me, step)), targets)):
        own = pltpu.make_async_copy(source, target, own_sem.at[slot])
        own.start()
        owns.append(own)

    def finish():
        for own in owns:
            own.wait()
        for copy in moved:
            copy.wait_recv()

    return finish


def square(step):
    me = lax.axis_index(AXIS)
    return [partner(me, bits, step) for bits in ORDER]


def wide(offset):
    return pl.ds(pl.multiple_of(offset, 128), HD)


def spread_attn_kernel(weights_ref, part_ref, own_sem, send_sem, recv_sem):
    here = place(lax.axis_index(AXIS), PLANE_STEP)
    greet(square(PLANE_STEP))
    copies = Copies(send_sem, recv_sem)
    swap_steps(
        lambda c: [weights_ref.at[:, wide(offset)] for offset in attn_columns(c)],
        [part_ref.at[here, :, pl.ds(slot * HD, HD)] for slot in range(3)],
        copies,
        own_sem,
        PLANE_STEP,
    )()
    copies.sent()


def spread_attn(weights):
    rows = weights.shape[0]
    return pl.pallas_call(
        spread_attn_kernel,
        out_shape=jax.ShapeDtypeStruct((PLANE, rows, 3 * HD), BF16),
        in_specs=[ANY],
        out_specs=ANY,
        scratch_shapes=[DMA((3,)), DMA((21,)), DMA((21,))],
        compiler_params=pltpu.CompilerParams(collective_id=3, has_side_effects=True),
        name="spread_attn",
    )(weights)


def spread_gu_kernel(
    weights_ref, gain_ref, gu_ref, gains_ref, own_sem, send_sem, recv_sem, gain_send, gain_recv
):
    peers = gains_ref.shape[0]
    ffc = gu_ref.shape[2] // 2
    me = lax.axis_index(AXIS)
    here = place(me, PLANE_STEP)
    greet_all(peers)
    gains_done = exchange_all(lambda device: gain_ref, gains_ref, gain_send, gain_recv)
    own = pltpu.make_async_copy(gain_ref, gains_ref.at[me], own_sem.at[2])
    own.start()
    copies = Copies(send_sem, recv_sem)
    swap_steps(
        lambda c: [weights_ref.at[:, lanes(slot * PLANE + c, ffc)] for slot in range(2)],
        [gu_ref.at[here, :, pl.ds(slot * ffc, ffc)] for slot in range(2)],
        copies,
        own_sem,
        PLANE_STEP,
    )()
    own.wait()
    gains_done()
    copies.sent()


def spread_gu(weights, gain_block, peers):
    rows = weights.shape[0]
    ffc = weights.shape[1] // 3 // PLANE
    return pl.pallas_call(
        spread_gu_kernel,
        out_shape=(
            jax.ShapeDtypeStruct((PLANE, rows, 2 * ffc), BF16),
            jax.ShapeDtypeStruct((peers,) + gain_block.shape, gain_block.dtype),
        ),
        in_specs=[ANY, ANY],
        out_specs=(ANY, ANY),
        scratch_shapes=[DMA((3,)), DMA((14,)), DMA((14,)), DMA((peers,)), DMA((peers,))],
        compiler_params=pltpu.CompilerParams(collective_id=4, has_side_effects=True),
        cost_estimate=cost(38),
        name="spread_gu",
    )(weights, gain_block)


def spread_down_kernel(weights_ref, block_ref, down_ref, full_ref, own_sem, send_sem, recv_sem):
    ffc = down_ref.shape[2]
    me = lax.axis_index(AXIS)
    greet(square(PLANE_STEP))
    copies = Copies(send_sem, recv_sem)
    gathered = gather_steps(block_ref, full_ref, copies, own_sem.at[1], PLANE_STEP)
    spread = swap_steps(
        lambda c: [weights_ref.at[:, lanes(2 * PLANE + c, ffc)]],
        [down_ref.at[place(me, PLANE_STEP)]],
        copies,
        own_sem,
        PLANE_STEP,
    )
    gathered()
    spread()
    copies.sent()


def spread_down(weights, block):
    rows = weights.shape[0]
    ffc = weights.shape[1] // 3 // PLANE
    count = GATHER_COPIES + 7
    return pl.pallas_call(
        spread_down_kernel,
        out_shape=(
            jax.ShapeDtypeStruct((PLANE, rows, ffc), BF16),
            jax.ShapeDtypeStruct((PLANE * block.shape[0], block.shape[1]), BF16),
        ),
        in_specs=[ANY, ANY],
        out_specs=(ANY, ANY),
        scratch_shapes=[DMA((2,)), DMA((count,)), DMA((count,))],
        compiler_params=pltpu.CompilerParams(collective_id=5, has_side_effects=True),
        cost_estimate=cost(1),
        name="spread_down",
    )(weights, block)


def collect_kernel(*refs, count):
    term_refs, rows_ref = refs[:count], refs[count]
    own_sem, send_sem, recv_sem = refs[count + 1 :]
    ffc = term_refs[0].shape[2]
    here = place(lax.axis_index(AXIS), PLANE_STEP)
    greet(square(PLANE_STEP))
    copies = Copies(send_sem, recv_sem)
    swap_steps(
        lambda c: [term.at[c] for term in term_refs],
        [rows_ref.at[:, lanes(slot * PLANE + here, ffc)] for slot in range(count)],
        copies,
        own_sem,
        PLANE_STEP,
    )()
    copies.sent()


def collect(terms, collective_id):
    count = len(terms)
    rows, ffc = terms[0].shape[1:]
    return pl.pallas_call(
        partial(collect_kernel, count=count),
        out_shape=jax.ShapeDtypeStruct((rows, count * PLANE * ffc), BF16),
        in_specs=[ANY] * count,
        out_specs=ANY,
        scratch_shapes=[DMA((count,)), DMA((7 * count,)), DMA((7 * count,))],
        compiler_params=pltpu.CompilerParams(collective_id=collective_id, has_side_effects=True),
        cost_estimate=cost(0.1),
        name="collect",
    )(*terms)


def collect_attn_kernel(
    term_ref, gain_ref, rows_ref, gains_ref, own_sem, send_sem, recv_sem, gain_send, gain_recv
):
    me = lax.axis_index(AXIS)
    greet_all(gain_ref.shape[0])
    copies = Copies(send_sem, recv_sem)
    moved = swap_steps(
        lambda c: [term_ref.at[c, :, pl.ds(slot * HD, HD)] for slot in range(3)],
        [rows_ref.at[:, wide(offset)] for offset in attn_columns(place(me, PLANE_STEP))],
        copies,
        own_sem,
        PLANE_STEP,
    )
    gains_done = exchange_all(lambda device: gain_ref.at[device], gains_ref, gain_send, gain_recv)
    own = pltpu.make_async_copy(gain_ref.at[me], gains_ref.at[me], own_sem.at[3])
    own.start()
    moved()
    own.wait()
    gains_done()
    copies.sent()


def collect_attn(term, gain_blocks):
    rows = term.shape[1]
    peers = gain_blocks.shape[0]
    return pl.pallas_call(
        collect_attn_kernel,
        out_shape=(
            jax.ShapeDtypeStruct((rows, PLANE * 3 * HD), BF16),
            jax.ShapeDtypeStruct(gain_blocks.shape, gain_blocks.dtype),
        ),
        in_specs=[ANY, ANY],
        out_specs=(ANY, ANY),
        scratch_shapes=[DMA((4,)), DMA((21,)), DMA((21,)), DMA((peers,)), DMA((peers,))],
        compiler_params=pltpu.CompilerParams(collective_id=7, has_side_effects=True),
        name="collect_attn",
    )(term, gain_blocks)


def block_scores(q, k, start, first):
    scores = lax.dot_general(q, k, (((1,), (1,)), ((), ())), preferred_element_type=F32)
    bent = jnp.tanh(scores * (HD ** (-0.5) / SOFT_CAP))
    rows, span = scores.shape
    key_at = lax.broadcasted_iota(jnp.int32, (rows, span), 1)
    row_at = lax.broadcasted_iota(jnp.int32, (rows, span), 0)
    allowed = (key_at + first >= start) & (key_at <= row_at + LMAX)
    return (bent, jnp.where(allowed, jnp.exp(SOFT_CAP * bent), 0.0))


def attend_kernel(q_ref, k_ref, v_ref, start_ref, out_ref, inv_ref):
    first = pl.program_id(0) * QBLK
    keys = pl.ds(pl.multiple_of(first, QBLK), LMAX + QBLK)
    unused_bent, exponent = block_scores(q_ref[...], k_ref[keys], start_ref[...], first)
    inverse = 1.0 / jnp.sum(exponent, axis=-1, keepdims=True)
    weights = (exponent * inverse).astype(BF16)
    out_ref[...] = jnp.dot(weights, v_ref[keys], preferred_element_type=F32).astype(BF16)
    inv_ref[...] = inverse


def attend(queries, key_rows, value_rows, starts):
    rows = queries.shape[0]
    span = key_rows.shape[0]
    row_spec = pl.BlockSpec((QBLK, HD), lambda i: (i, 0))
    one_spec = pl.BlockSpec((QBLK, 1), lambda i: (i, 0))
    all_spec = pl.BlockSpec((span, HD), lambda i: (0, 0))
    return pl.pallas_call(
        attend_kernel,
        out_shape=(
            jax.ShapeDtypeStruct((rows, HD), BF16),
            jax.ShapeDtypeStruct((rows, 1), F32),
        ),
        grid=(rows // QBLK,),
        in_specs=[row_spec, all_spec, all_spec, one_spec],
        out_specs=(row_spec, one_spec),
        compiler_params=pltpu.CompilerParams(vmem_limit_bytes=40 << 20),
        cost_estimate=cost(1),
        name="attend",
    )(queries, key_rows, value_rows, starts)


def attend_back_kernel(q_ref, k_ref, v_ref, start_ref, inv_ref, grad_ref, gq_ref, gk_ref, gv_ref):
    @pl.when(pl.program_id(0) == 0)
    def _():
        gk_ref[...] = jnp.zeros_like(gk_ref)
        gv_ref[...] = jnp.zeros_like(gv_ref)

    first = pl.program_id(0) * QBLK
    keys = pl.ds(pl.multiple_of(first, QBLK), LMAX + QBLK)
    q, k, v, grad = q_ref[...], k_ref[keys], v_ref[keys], grad_ref[...]
    bent, exponent = block_scores(q, k, start_ref[...], first)
    probability = exponent * inv_ref[...]
    grad_prob = lax.dot_general(grad, v, (((1,), (1,)), ((), ())), preferred_element_type=F32)
    inner = jnp.sum(probability * grad_prob, axis=-1, keepdims=True)
    grad_scores = (probability * (grad_prob - inner) * (1.0 - bent * bent)).astype(BF16)
    scale = HD ** (-0.5)
    gq_ref[...] = jnp.dot(grad_scores, k, preferred_element_type=F32) * scale
    over_rows = (((0,), (0,)), ((), ()))
    gk_ref[keys] += lax.dot_general(grad_scores, q, over_rows, preferred_element_type=F32) * scale
    gv_ref[keys] += lax.dot_general(
        probability.astype(BF16), grad, over_rows, preferred_element_type=F32
    )


def attend_back(queries, key_rows, value_rows, starts, inverse, grad):
    rows = queries.shape[0]
    span = key_rows.shape[0]
    row_spec = pl.BlockSpec((QBLK, HD), lambda i: (i, 0))
    one_spec = pl.BlockSpec((QBLK, 1), lambda i: (i, 0))
    all_spec = pl.BlockSpec((span, HD), lambda i: (0, 0))
    return pl.pallas_call(
        attend_back_kernel,
        out_shape=(
            jax.ShapeDtypeStruct((rows, HD), F32),
            jax.ShapeDtypeStruct((span, HD), F32),
            jax.ShapeDtypeStruct((span, HD), F32),
        ),
        grid=(rows // QBLK,),
        in_specs=[row_spec, all_spec, all_spec, one_spec, one_spec, row_spec],
        out_specs=(row_spec, all_spec, all_spec),
        compiler_params=pltpu.CompilerParams(vmem_limit_bytes=48 << 20),
        cost_estimate=cost(20),
        name="attend_back",
    )(queries, key_rows, value_rows, starts, inverse, grad)


def token_tables(seq_lengths, index_vec):
    count = seq_lengths.shape[0]
    order = jnp.arange(count, dtype=jnp.int32)
    seq_ends = jnp.sum(
        jnp.where(order[None, :] <= order[:, None], seq_lengths[None, :], 0), axis=1
    )
    after_end = index_vec[:, None] >= seq_ends[None, :]
    return index_vec - jnp.sum(jnp.where(after_end, seq_lengths[None, :], 0), axis=1)


def rms_parts(value):
    return lax.rsqrt(jnp.mean(value * value, axis=-1, keepdims=True) + EPSILON)


def rms_forward(value, gain_vec):
    return value * rms_parts(value) * (1.0 + gain_vec)


def rms_backward(value, gain_vec, grad):
    r = rms_parts(value)
    scaled = (1.0 + gain_vec) * grad
    inner = jnp.mean(value * scaled, axis=-1, keepdims=True)
    return (r * scaled - value * (r * r * r * inner), jnp.sum(grad * value * r, axis=0))


def rotate(value, cosine, sine_part):
    half_width = value.shape[-1] // 2
    first_half = value[..., :half_width]
    second_half = value[..., half_width:]
    return jnp.concatenate(
        [
            first_half * cosine - second_half * sine_part,
            second_half * cosine + first_half * sine_part,
        ],
        axis=-1,
    )


def contract_last(left_side, right_side):
    return lax.dot_general(
        left_side, right_side, (((1,), (1,)), ((), ())), preferred_element_type=F32
    )


def contract_first(left_side, right_side):
    return lax.dot_general(
        left_side, right_side, (((0,), (0,)), ((), ())), preferred_element_type=F32
    )


def matmul(left_side, right_side):
    return jnp.dot(left_side, right_side, preferred_element_type=F32)


def gelu_parts(gate):
    k0 = 0.7978845608028654
    k1 = 0.044715
    t = jnp.tanh(k0 * (gate + k1 * gate * gate * gate))
    value = 0.5 * gate * (1.0 + t)
    slope = 0.5 * (1.0 + t) + 0.5 * gate * (1.0 - t * t) * k0 * (1.0 + 3.0 * k1 * gate * gate)
    return (value, slope)


def local(tokens, attn_weights, mlp_weights, norm_gains, seq_lengths, cotangent):
    tok_rows, width = tokens.shape
    peers = lax.axis_size(AXIS)
    planes = peers // PLANE
    share = width // peers
    row_share = attn_weights.shape[0]
    ff = mlp_weights.shape[1] // 3
    ffc = ff // PLANE
    plane_rows = PLANE * tok_rows
    halo = LMAX
    across = [[p * PLANE + i for p in range(planes)] for i in range(PLANE)]
    sibling = [(i, i ^ 1) for i in range(peers)]
    to_next = [(i, i + PLANE) for i in range(peers - PLANE)]
    to_prev = [(i + PLANE, i) for i in range(peers - PLANE)]
    me = lax.axis_index(AXIS)
    is_even = (me % 2) == 0
    plane_start = (me // PLANE) * plane_rows

    def gather_across(value):
        return lax.all_gather(value, AXIS, axis=0, tiled=True, axis_index_groups=across)

    def scatter_across(value):
        part = lax.psum_scatter(
            value.astype(BF16), AXIS, scatter_dimension=0, tiled=True, axis_index_groups=across
        )
        return part.reshape(PLANE, -1, part.shape[1])

    gain_block = jnp.pad(norm_gains.astype(F32), ((0, 8 - 4), (0, -share % 128)))
    attn_part, gain_block = lax.optimization_barrier((spread_attn(attn_weights), gain_block))
    attn_cols = gather_across(attn_part.reshape(-1, 3 * HD))
    gu_part, gain_blocks = spread_gu(mlp_weights, gain_block, peers)
    gain_full = gain_blocks[:, :4, :share].transpose(1, 0, 2).reshape(4, width)
    inputs = tokens.astype(F32)
    down_part, normed = spread_down(
        mlp_weights, rms_forward(inputs, gain_full[0]).astype(BF16)
    )
    gu_cols = gather_across(gu_part.reshape(-1, 2 * ffc))
    down_cols = gather_across(down_part.reshape(-1, ffc))
    qkv_cols = attn_cols[:, : 2 * HD]
    out_cols = attn_cols[:, 2 * HD :]

    query_index = plane_start + jnp.arange(plane_rows, dtype=jnp.int32)
    position = token_tables(seq_lengths, query_index)
    starts = (jnp.arange(plane_rows, dtype=jnp.int32) + halo - position)[:, None]
    frequency = 10000.0 ** (-jnp.arange(HD // 2, dtype=F32) * 2.0 / HD)
    angles = position.astype(F32)[:, None] * frequency[None, :]
    cosine, sine_part = jnp.cos(angles), jnp.sin(angles)
    kv_cosine = jnp.where(is_even, cosine, 1.0)
    kv_sine = jnp.where(is_even, sine_part, 0.0)

    projected = matmul(normed, qkv_cols)
    queries = rotate(projected[:, :HD], cosine, sine_part).astype(BF16)
    kv_own = rotate(projected[:, HD:], kv_cosine, kv_sine).astype(BF16)
    kv_halo = lax.ppermute(kv_own[plane_rows - halo :], AXIS, to_next)
    kv_mine = jnp.concatenate([kv_halo, kv_own], axis=0)
    kv_other = lax.ppermute(kv_mine, AXIS, sibling)
    key_rows = jnp.where(is_even, kv_mine, kv_other)
    value_rows = jnp.where(is_even, kv_other, kv_mine)
    attended, inverse = attend(queries, key_rows, value_rows, starts)
    attn_proj = product_scatter([attended], [out_cols], [0], PLANE_STEP, 11)

    middle = inputs + rms_forward(attn_proj, gain_full[1])
    mid_low = gather_square(rms_forward(middle, gain_full[2]).astype(BF16), PLANE_STEP, 1)
    gate_up = matmul(mid_low, gu_cols)
    gate, up = gate_up[:, :ffc], gate_up[:, ffc:]
    gelu, slope = gelu_parts(gate)
    hidden = (gelu * up).astype(BF16)
    mlp_raw = product_scatter([hidden], [down_cols], [0], PLANE_STEP, 9)
    layer_output = (middle + rms_forward(mlp_raw, gain_full[3])).astype(BF16)

    grad_out = cotangent.astype(F32)
    grad_raw, gain_four = rms_backward(mlp_raw, gain_full[3], grad_out)
    grad_raw_low = gather_square(grad_raw.astype(BF16), PLANE_STEP, 1)
    down_grad = contract_first(grad_raw_low, hidden).astype(BF16)
    down_grad, grad_raw_low = lax.optimization_barrier((down_grad, grad_raw_low))
    down_term = scatter_across(down_grad)
    grad_hidden = matmul(grad_raw_low, down_cols)
    grad_gate = (slope * up * grad_hidden).astype(BF16)
    grad_up = (gelu * grad_hidden).astype(BF16)
    gate_grad = contract_first(mid_low, grad_gate).astype(BF16)
    gate_grad, grad_up = lax.optimization_barrier((gate_grad, grad_up))
    gate_term = scatter_across(gate_grad)
    up_grad = contract_first(mid_low, grad_up).astype(BF16)
    up_grad, grad_up = lax.optimization_barrier((up_grad, grad_up))
    up_term = scatter_across(up_grad)
    grad_normed_mid = product_scatter(
        [grad_gate, grad_up], [gu_cols, gu_cols], [0, ffc], PLANE_STEP, 10
    )
    grad_mid_part, gain_three = rms_backward(middle, gain_full[2], grad_normed_mid)
    grad_middle = grad_out + grad_mid_part

    grad_proj, gain_two = rms_backward(attn_proj, gain_full[1], grad_middle)
    grad_proj_own, down_term = lax.optimization_barrier((grad_proj.astype(BF16), down_term))
    grad_proj_low = gather_square(grad_proj_own, PLANE_STEP, 1)
    grad_att = matmul(grad_proj_low, out_cols).astype(BF16)
    grad_query, grad_keys, grad_values = attend_back(
        queries, key_rows, value_rows, starts, inverse, grad_att
    )
    grad_mine = jnp.where(is_even, grad_keys, grad_values)
    grad_give = jnp.where(is_even, grad_values, grad_keys).astype(BF16)
    grad_kv = grad_mine + lax.ppermute(grad_give, AXIS, sibling).astype(F32)
    grad_back = lax.ppermute(grad_kv[:halo].astype(BF16), AXIS, to_prev).astype(F32)
    down_term, gate_term, grad_kv = lax.optimization_barrier((down_term, gate_term, grad_kv))
    gate_rows, down_rows = jnp.split(collect([gate_term, down_term], 6), 2, axis=1)
    gate_rows, down_rows, grad_back = lax.optimization_barrier((gate_rows, down_rows, grad_back))
    grad_kv = grad_kv[halo:] + jnp.pad(grad_back, ((plane_rows - halo, 0), (0, 0)))
    grad_qkv = jnp.concatenate(
        [
            rotate(grad_query, cosine, -sine_part).astype(BF16),
            rotate(grad_kv, kv_cosine, -kv_sine).astype(BF16),
        ],
        axis=1,
    )
    attn_grad = jnp.concatenate(
        [contract_first(normed, grad_qkv), contract_first(grad_proj_low, attended)], axis=1
    ).astype(BF16)
    attn_grad, grad_qkv = lax.optimization_barrier((attn_grad, grad_qkv))
    attn_term = scatter_across(attn_grad)
    grad_normed = product_scatter([grad_qkv], [qkv_cols], [0], PLANE_STEP, 12)
    grad_in_part, gain_one = rms_backward(inputs, gain_full[0], grad_normed)
    grad_tokens = (grad_middle + grad_in_part).astype(BF16)

    gain_term = jnp.stack([gain_one, gain_two, gain_three, gain_four], axis=0)
    gain_term = gain_term.reshape(4, peers, share).transpose(1, 0, 2)
    gain_term = jnp.pad(gain_term, ((0, 0), (0, 8 - 4), (0, -share % 128)))
    up_term, gain_term = lax.optimization_barrier((up_term, gain_term))
    up_rows = collect([up_term], 13)
    grad_mlp = jnp.concatenate([gate_rows, up_rows, down_rows], axis=1).astype(F32)
    grad_mlp, attn_term = lax.optimization_barrier((grad_mlp, attn_term))
    attn_rows, gain_recv = collect_attn(attn_term, gain_term)
    grad_attn = attn_rows.astype(F32)
    grad_gains = jnp.sum(gain_recv[:, :4, :share], axis=0)
    return (layer_output, grad_tokens, grad_attn, grad_mlp, grad_gains)


def solution(mesh):
    return jax.shard_map(
        local,
        mesh=mesh,
        in_specs=(
            P("fsdp", None),
            P("fsdp", None),
            P("fsdp", None),
            P(None, "fsdp"),
            P(),
            P("fsdp", None),
        ),
        out_specs=(
            P("fsdp", None),
            P("fsdp", None),
            P("fsdp", None),
            P("fsdp", None),
            P(None, "fsdp"),
        ),
        check_vma=False,
    )
```

```python
from functools import partial

import jax
import jax.numpy as jnp
from jax import lax
from jax.experimental import pallas as pl
from jax.experimental.pallas import tpu as pltpu
from jax.sharding import PartitionSpec as P

H = 8
KVH = 4
HD = 256
LMAX = 1024
PLANE = 8
QBLK = 128

EPSILON = 1e-06
SOFT_CAP = 50.0
AXIS = "fsdp"
F32 = jnp.float32
BF16 = jnp.bfloat16
MESH = pl.DeviceIdType.MESH
ANY = pl.BlockSpec(memory_space=pl.ANY)
VMEM = pl.BlockSpec(memory_space=pltpu.VMEM)
DMA = pltpu.SemaphoreType.DMA


def flip(index, step):
    return index + step - 2 * step * ((index // step) % 2)


PLANE_STEP = 4


def partner(index, bits, step):
    for bit, by in ((1, 1), (2, 2), (4, step)):
        if bits & bit:
            index = flip(index, by)
    return index


def place(device, step):
    return device % 4 + 4 * ((device // step) % 2)


def greet(peers):
    barrier = pltpu.get_barrier_semaphore()
    for peer in peers:
        pl.semaphore_signal(barrier, inc=1, device_id=(peer,), device_id_type=MESH)
    pl.semaphore_wait(barrier, len(peers))


class Copies:
    def __init__(self, send_sem, recv_sem):
        self.send_sem, self.recv_sem, self.made = send_sem, recv_sem, []

    def start(self, source, target, device):
        slot = len(self.made)
        copy = pltpu.make_async_remote_copy(
            src_ref=source,
            dst_ref=target,
            send_sem=self.send_sem.at[slot],
            recv_sem=self.recv_sem.at[slot],
            device_id=(device,),
            device_id_type=MESH,
        )
        copy.start()
        self.made.append(copy)
        return copy

    def sent(self):
        for copy in self.made:
            copy.wait_send()


def band(index, size):
    return pl.ds(pl.multiple_of(index * size, 8), size)


def lanes(index, size):
    return pl.ds(pl.multiple_of(index * size, 128), size)


def gather_steps(block_ref, full_ref, copies, own_sem, step):
    rows, width = block_ref.shape
    half = width // 2
    me = lax.axis_index(AXIS)
    sib, xn, yn = flip(me, 1), flip(me, 2), flip(me, step)
    diag = flip(xn, step)

    def at(device, side):
        return full_ref.at[band(place(device, step), rows), pl.ds(side * half, half)]

    def mine(side):
        return block_ref.at[:, pl.ds(side * half, half)]

    own_rows = full_ref.at[band(place(me, step), rows)]
    xa = copies.start(mine(0), at(me, 0), xn)
    ya = copies.start(mine(1), at(me, 1), yn)
    xb = copies.start(mine(1), at(me, 1), xn)
    yb = copies.start(mine(0), at(me, 0), yn)
    arriving = [copies.start(block_ref, own_rows, sib)]
    own = pltpu.make_async_copy(block_ref, own_rows, own_sem)
    own.start()

    def finish(on_rows=None):
        def to_sibling(device, side):
            arriving.append(copies.start(at(device, side), at(device, side), sib))

        def arrived(first, last, *devices):
            for copy in arriving[first:last]:
                copy.wait_recv()
            for device in devices:
                on_rows(device)

        if on_rows is not None:
            own.wait()
            arrived(0, 1, me)
        xa.wait_recv()
        yc = copies.start(at(xn, 0), at(xn, 0), yn)
        to_sibling(xn, 0)
        ya.wait_recv()
        xc = copies.start(at(yn, 1), at(yn, 1), xn)
        to_sibling(yn, 1)
        xb.wait_recv()
        to_sibling(xn, 1)
        yb.wait_recv()
        to_sibling(yn, 0)
        if on_rows is not None:
            arrived(1, 5, xn, yn)
        yc.wait_recv()
        to_sibling(diag, 0)
        xc.wait_recv()
        to_sibling(diag, 1)
        if on_rows is not None:
            arrived(5, 7, diag)
        else:
            arrived(0, 7)
            own.wait()

    return finish


GATHER_COPIES = 13


def cost(microseconds):
    return pl.CostEstimate(
        flops=int(microseconds * 1e7), transcendentals=0, bytes_accessed=int(microseconds * 3e4)
    )


def gather_kernel(block_ref, full_ref, own_sem, send_sem, recv_sem, *, step):
    me = lax.axis_index(AXIS)
    greet((flip(me, 1), flip(me, 2), flip(me, step)))
    copies = Copies(send_sem, recv_sem)
    gather_steps(block_ref, full_ref, copies, own_sem, step)()
    copies.sent()


def gather_square(block, step, collective_id):
    rows, width = block.shape
    return pl.pallas_call(
        partial(gather_kernel, step=step),
        out_shape=jax.ShapeDtypeStruct((PLANE * rows, width), block.dtype),
        in_specs=[ANY],
        out_specs=ANY,
        scratch_shapes=[DMA(()), DMA((GATHER_COPIES,)), DMA((GATHER_COPIES,))],
        compiler_params=pltpu.CompilerParams(collective_id=collective_id, has_side_effects=True),
        cost_estimate=cost(42),
        name="gather_square",
    )(block)


W_TILES = 3


def product_scatter_steps(
    left_refs, right_refs, left_bufs, right_bufs, buffers, load_sem, copies, offsets, step
):
    both, got, ra, rb, ra2, rb2 = buffers
    pairs = len(left_refs)
    rows, width = got.shape[1:]
    half = width // 2
    tile = width // W_TILES
    chunk = 16
    me = lax.axis_index(AXIS)
    core = me % 2
    sib, xn, yn = flip(me, 1), flip(me, 2), flip(me, step)
    order = (flip(xn, step), xn, yn, me)
    first, second = pl.ds(0, half), pl.ds(half, half)

    def chip_rows(device):
        return pl.ds(pl.multiple_of((place(device, step) // 2) * 2 * rows, 16), 2 * rows)

    def right_load(j, t):
        r = pl.ds(t * tile, tile)
        source = right_refs[j].at[r, pl.ds(offsets[j], right_bufs[j].shape[1])]
        return pltpu.make_async_copy(source, right_bufs[j].at[r], load_sem.at[j, t])

    def left_load(j, i):
        r = chip_rows(order[i])
        return pltpu.make_async_copy(
            left_refs[j].at[r], left_bufs[j].at[r], load_sem.at[j, W_TILES + i]
        )

    for j in range(pairs):
        left_load(j, 0).start()
    for t in range(W_TILES):
        for j in range(pairs):
            right_load(j, t).start()
    for i in range(1, 4):
        for j in range(pairs):
            left_load(j, i).start()
    greet((sib, xn, yn))

    def product(i):
        r = chip_rows(order[i])
        for j in range(pairs):
            left_load(j, i).wait()

        def columns(w):
            total = None
            for j in range(pairs):
                term = contract_last(left_bufs[j][r], right_bufs[j][w])
                total = term if total is None else total + term
            both[i, :, w] = total.astype(BF16)

        if i == 0:
            for t in range(W_TILES):
                for j in range(pairs):
                    right_load(j, t).wait()
                columns(pl.ds(t * tile, tile))
        else:

            @pl.loop(0, W_TILES)
            def _(t):
                columns(pl.ds(pl.multiple_of(t * tile, tile), tile))

    def mine(i, cols=None):
        if cols is None:
            return both.at[i, band(core, rows)]
        return both.at[i, band(core, rows), cols]

    def add(total, other):
        @pl.loop(0, rows // chunk)
        def _(k):
            r = pl.ds(pl.multiple_of(k * chunk, chunk), chunk)
            total[r] = (total[r].astype(F32) + other[r].astype(F32)).astype(total.dtype)

    def make(i):
        product(i)
        crossing = copies.start(both.at[i, band(1 - core, rows)], got.at[i], sib)
        crossing.wait_recv()
        add(mine(i), got.at[i])

    make(0)
    x0 = copies.start(mine(0, first), ra.at[0], xn)
    y0 = copies.start(mine(0, second), rb.at[0], yn)
    make(1)
    x1 = copies.start(mine(1, first), ra.at[1], xn)
    make(2)
    y1 = copies.start(mine(2, second), rb.at[1], yn)
    x0.wait_recv()
    add(mine(2, first), ra.at[0])
    y2 = copies.start(mine(2, first), ra2, yn)
    y0.wait_recv()
    add(mine(1, second), rb.at[0])
    x2 = copies.start(mine(1, second), rb2, xn)
    make(3)
    for copy in (x1, y1, y2, x2):
        copy.wait_recv()
    own = mine(3)

    def summed(r):
        return jnp.concatenate(
            [
                own[r, first].astype(F32) + ra[1, r].astype(F32) + ra2[r].astype(F32),
                own[r, second].astype(F32) + rb[1, r].astype(F32) + rb2[r].astype(F32),
            ],
            axis=1,
        )

    return summed


ROW_CHUNK = 16


def product_scatter_kernel(*refs, pairs, offsets, step):
    left_refs, right_refs, out_ref = refs[:pairs], refs[pairs : 2 * pairs], refs[2 * pairs]
    left_bufs = refs[2 * pairs + 1 : 3 * pairs + 1]
    right_bufs = refs[3 * pairs + 1 : 4 * pairs + 1]
    buffers, (load_sem, send_sem, recv_sem) = refs[4 * pairs + 1 : -3], refs[-3:]
    copies = Copies(send_sem, recv_sem)
    summed = product_scatter_steps(
        left_refs, right_refs, left_bufs, right_bufs, buffers, load_sem, copies, offsets, step
    )

    @pl.loop(0, out_ref.shape[0] // ROW_CHUNK)
    def _(k):
        r = pl.ds(pl.multiple_of(k * ROW_CHUNK, ROW_CHUNK), ROW_CHUNK)
        out_ref[r] = summed(r)

    copies.sent()


def scatter_buffers(rows, width):
    half = width // 2
    return [
        pltpu.VMEM((4, 2 * rows, width), BF16),
        pltpu.VMEM((4, rows, width), BF16),
        pltpu.VMEM((2, rows, half), BF16),
        pltpu.VMEM((2, rows, half), BF16),
        pltpu.VMEM((rows, half), BF16),
        pltpu.VMEM((rows, half), BF16),
    ]


def product_scatter(lefts, rights, offsets, step, collective_id):
    pairs = len(lefts)
    rows, width = lefts[0].shape[0] // PLANE, rights[0].shape[0]
    return pl.pallas_call(
        partial(product_scatter_kernel, pairs=pairs, offsets=offsets, step=step),
        out_shape=jax.ShapeDtypeStruct((rows, width), F32),
        in_specs=[ANY] * (2 * pairs),
        out_specs=VMEM,
        scratch_shapes=[
            *[pltpu.VMEM(value.shape, BF16) for value in lefts],
            *[pltpu.VMEM((width, value.shape[1]), BF16) for value in lefts],
            *scatter_buffers(rows, width),
            DMA((pairs, W_TILES + 4)),
            DMA((10,)),
            DMA((10,)),
        ],
        compiler_params=pltpu.CompilerParams(
            collective_id=collective_id, has_side_effects=True, vmem_limit_bytes=56 << 20
        ),
        cost_estimate=cost(50),
        name="product_scatter",
    )(*lefts, *rights)


TURN_TILE = 768


def turn_kernel(
    left_ref, right_ref, gain_ref, grad_ref, raw_ref, full_ref, term_ref, *refs, step
):
    left_buf, right_buf, gathered, total, grad_own = refs[:5]
    buffers, (load_sem, own_sem, store_sem, send_sem, recv_sem) = refs[5:-5], refs[-5:]
    rows, width = grad_ref.shape
    copies = Copies(send_sem, recv_sem)
    summed = product_scatter_steps(
        [left_ref], [right_ref], [left_buf], [right_buf], buffers, load_sem, copies, [0], step
    )
    gain = gain_ref[...]

    @pl.loop(0, rows // ROW_CHUNK)
    def _(k):
        r = pl.ds(pl.multiple_of(k * ROW_CHUNK, ROW_CHUNK), ROW_CHUNK)
        value = summed(r)
        raw_ref[r] = value
        scale = lax.rsqrt(jnp.mean(value * value, axis=1, keepdims=True) + EPSILON)
        scaled = (1.0 + gain) * grad_ref[r].astype(F32)
        inner = jnp.mean(value * scaled, axis=1, keepdims=True)
        grad_own[r] = (scale * scaled - value * (scale * scale * scale * inner)).astype(BF16)

    stores = []

    def on_rows(device):
        slot = len(stores)
        r = pl.ds(pl.multiple_of((place(device, step) // 2) * 2 * rows, 16), 2 * rows)
        store = pltpu.make_async_copy(gathered.at[r], full_ref.at[r], store_sem.at[slot])
        store.start()
        stores.append(store)
        right = left_buf[r]

        @pl.loop(0, width // TURN_TILE)
        def _(t):
            w = pl.ds(pl.multiple_of(t * TURN_TILE, TURN_TILE), TURN_TILE)
            term = contract_first(gathered[r, w], right)
            if slot == 0:
                total[w] = term
            elif slot < 3:
                total[w] += term
            else:
                right_buf[w] = (total[w] + term).astype(BF16)
                pltpu.make_async_copy(right_buf.at[w], term_ref.at[w], store_sem.at[4]).start()

    gather_steps(grad_own, gathered, copies, own_sem, step)(on_rows)
    pltpu.make_async_copy(right_buf, term_ref, store_sem.at[4]).wait()
    for store in stores:
        store.wait()
    copies.sent()


def turn(left, right, gain_row, grad, step, collective_id):
    rows, width = grad.shape
    count = 10 + GATHER_COPIES
    return pl.pallas_call(
        partial(turn_kernel, step=step),
        out_shape=(
            jax.ShapeDtypeStruct((rows, width), F32),
            jax.ShapeDtypeStruct((PLANE * rows, width), BF16),
            jax.ShapeDtypeStruct((width, left.shape[1]), BF16),
        ),
        in_specs=[ANY, ANY, VMEM, VMEM],
        out_specs=(VMEM, ANY, ANY),
        scratch_shapes=[
            pltpu.VMEM(left.shape, BF16),
            pltpu.VMEM(right.shape, BF16),
            pltpu.VMEM((PLANE * rows, width), BF16),
            pltpu.VMEM((width, left.shape[1]), F32),
            pltpu.VMEM((rows, width), BF16),
            *scatter_buffers(rows, width),
            DMA((1, W_TILES + 4)),
            DMA(()),
            DMA((5,)),
            DMA((count,)),
            DMA((count,)),
        ],
        compiler_params=pltpu.CompilerParams(
            collective_id=collective_id, has_side_effects=True, vmem_limit_bytes=60 << 20
        ),
        cost_estimate=cost(50),
        name="turn",
    )(left, right, gain_row, grad)


def attn_columns(column):
    query_width = H * HD
    key_offset = query_width + (column % 2) * KVH * HD + (column // 2) * HD
    return (column * HD, key_offset, query_width + 2 * KVH * HD + column * HD)


def greet_all(peers):
    me = lax.axis_index(AXIS)
    barrier = pltpu.get_barrier_semaphore()

    @pl.loop(1, peers)
    def _(k):
        device = lax.rem(me + k, peers)
        pl.semaphore_signal(barrier, inc=1, device_id=(device,), device_id_type=MESH)

    pl.semaphore_wait(barrier, peers - 1)


def exchange_all(source_of, target_ref, send_sem, recv_sem):
    peers = target_ref.shape[0]
    me = lax.axis_index(AXIS)

    def copy(k):
        device = lax.rem(me + k, peers)
        return pltpu.make_async_remote_copy(
            src_ref=source_of(device),
            dst_ref=target_ref.at[me],
            send_sem=send_sem.at[k],
            recv_sem=recv_sem.at[k],
            device_id=(device,),
            device_id_type=MESH,
        )

    @pl.loop(1, peers)
    def _(k):
        copy(k).start()

    def finish():
        @pl.loop(1, peers)
        def _(k):
            copy(k).wait()

    return finish


ORDER = (6, 7, 2, 3, 4, 5, 1)


def swap_steps(pieces_of, targets, copies, own_sem, step):
    me = lax.axis_index(AXIS)
    moved = []
    for bits in ORDER:
        peer = partner(me, bits, step)
        for source, target in zip(pieces_of(place(peer, step)), targets):
            moved.append(copies.start(source, target, peer))
    owns = []
    for slot, (source, target) in enumerate(zip(pieces_of(place(me, step)), targets)):
        own = pltpu.make_async_copy(source, target, own_sem.at[slot])
        own.start()
        owns.append(own)

    def finish():
        for own in owns:
            own.wait()
        for copy in moved:
            copy.wait_recv()

    return finish


def square(step):
    me = lax.axis_index(AXIS)
    return [partner(me, bits, step) for bits in ORDER]


def wide(offset):
    return pl.ds(pl.multiple_of(offset, 128), HD)


def spread_attn_kernel(weights_ref, part_ref, own_sem, send_sem, recv_sem):
    here = place(lax.axis_index(AXIS), PLANE_STEP)
    greet(square(PLANE_STEP))
    copies = Copies(send_sem, recv_sem)
    swap_steps(
        lambda c: [weights_ref.at[:, wide(offset)] for offset in attn_columns(c)],
        [part_ref.at[here, :, pl.ds(slot * HD, HD)] for slot in range(3)],
        copies,
        own_sem,
        PLANE_STEP,
    )()
    copies.sent()


def spread_attn(weights):
    rows = weights.shape[0]
    return pl.pallas_call(
        spread_attn_kernel,
        out_shape=jax.ShapeDtypeStruct((PLANE, rows, 3 * HD), BF16),
        in_specs=[ANY],
        out_specs=ANY,
        scratch_shapes=[DMA((3,)), DMA((21,)), DMA((21,))],
        compiler_params=pltpu.CompilerParams(collective_id=3, has_side_effects=True),
        name="spread_attn",
    )(weights)


def spread_gu_kernel(
    weights_ref, gain_ref, gu_ref, gains_ref, own_sem, send_sem, recv_sem, gain_send, gain_recv
):
    peers = gains_ref.shape[0]
    ffc = gu_ref.shape[2] // 2
    me = lax.axis_index(AXIS)
    here = place(me, PLANE_STEP)
    greet_all(peers)
    gains_done = exchange_all(lambda device: gain_ref, gains_ref, gain_send, gain_recv)
    own = pltpu.make_async_copy(gain_ref, gains_ref.at[me], own_sem.at[2])
    own.start()
    copies = Copies(send_sem, recv_sem)
    swap_steps(
        lambda c: [weights_ref.at[:, lanes(slot * PLANE + c, ffc)] for slot in range(2)],
        [gu_ref.at[here, :, pl.ds(slot * ffc, ffc)] for slot in range(2)],
        copies,
        own_sem,
        PLANE_STEP,
    )()
    own.wait()
    gains_done()
    copies.sent()


def spread_gu(weights, gain_block, peers):
    rows = weights.shape[0]
    ffc = weights.shape[1] // 3 // PLANE
    return pl.pallas_call(
        spread_gu_kernel,
        out_shape=(
            jax.ShapeDtypeStruct((PLANE, rows, 2 * ffc), BF16),
            jax.ShapeDtypeStruct((peers,) + gain_block.shape, gain_block.dtype),
        ),
        in_specs=[ANY, ANY],
        out_specs=(ANY, ANY),
        scratch_shapes=[DMA((3,)), DMA((14,)), DMA((14,)), DMA((peers,)), DMA((peers,))],
        compiler_params=pltpu.CompilerParams(collective_id=4, has_side_effects=True),
        cost_estimate=cost(38),
        name="spread_gu",
    )(weights, gain_block)


def spread_down_kernel(weights_ref, block_ref, down_ref, full_ref, own_sem, send_sem, recv_sem):
    ffc = down_ref.shape[2]
    me = lax.axis_index(AXIS)
    greet(square(PLANE_STEP))
    copies = Copies(send_sem, recv_sem)
    gathered = gather_steps(block_ref, full_ref, copies, own_sem.at[1], PLANE_STEP)
    spread = swap_steps(
        lambda c: [weights_ref.at[:, lanes(2 * PLANE + c, ffc)]],
        [down_ref.at[place(me, PLANE_STEP)]],
        copies,
        own_sem,
        PLANE_STEP,
    )
    gathered()
    spread()
    copies.sent()


def spread_down(weights, block):
    rows = weights.shape[0]
    ffc = weights.shape[1] // 3 // PLANE
    count = GATHER_COPIES + 7
    return pl.pallas_call(
        spread_down_kernel,
        out_shape=(
            jax.ShapeDtypeStruct((PLANE, rows, ffc), BF16),
            jax.ShapeDtypeStruct((PLANE * block.shape[0], block.shape[1]), BF16),
        ),
        in_specs=[ANY, ANY],
        out_specs=(ANY, ANY),
        scratch_shapes=[DMA((2,)), DMA((count,)), DMA((count,))],
        compiler_params=pltpu.CompilerParams(collective_id=5, has_side_effects=True),
        cost_estimate=cost(1),
        name="spread_down",
    )(weights, block)


def collect_kernel(*refs, count):
    term_refs, rows_ref = refs[:count], refs[count]
    own_sem, send_sem, recv_sem = refs[count + 1 :]
    ffc = term_refs[0].shape[2]
    here = place(lax.axis_index(AXIS), PLANE_STEP)
    greet(square(PLANE_STEP))
    copies = Copies(send_sem, recv_sem)
    swap_steps(
        lambda c: [term.at[c] for term in term_refs],
        [rows_ref.at[:, lanes(slot * PLANE + here, ffc)] for slot in range(count)],
        copies,
        own_sem,
        PLANE_STEP,
    )()
    copies.sent()


def collect(terms, collective_id):
    count = len(terms)
    rows, ffc = terms[0].shape[1:]
    return pl.pallas_call(
        partial(collect_kernel, count=count),
        out_shape=jax.ShapeDtypeStruct((rows, count * PLANE * ffc), BF16),
        in_specs=[ANY] * count,
        out_specs=ANY,
        scratch_shapes=[DMA((count,)), DMA((7 * count,)), DMA((7 * count,))],
        compiler_params=pltpu.CompilerParams(collective_id=collective_id, has_side_effects=True),
        cost_estimate=cost(0.1),
        name="collect",
    )(*terms)


def collect_attn_kernel(
    term_ref, gain_ref, rows_ref, gains_ref, own_sem, send_sem, recv_sem, gain_send, gain_recv
):
    me = lax.axis_index(AXIS)
    greet_all(gain_ref.shape[0])
    copies = Copies(send_sem, recv_sem)
    moved = swap_steps(
        lambda c: [term_ref.at[c, :, pl.ds(slot * HD, HD)] for slot in range(3)],
        [rows_ref.at[:, wide(offset)] for offset in attn_columns(place(me, PLANE_STEP))],
        copies,
        own_sem,
        PLANE_STEP,
    )
    gains_done = exchange_all(lambda device: gain_ref.at[device], gains_ref, gain_send, gain_recv)
    own = pltpu.make_async_copy(gain_ref.at[me], gains_ref.at[me], own_sem.at[3])
    own.start()
    moved()
    own.wait()
    gains_done()
    copies.sent()


def collect_attn(term, gain_blocks):
    rows = term.shape[1]
    peers = gain_blocks.shape[0]
    return pl.pallas_call(
        collect_attn_kernel,
        out_shape=(
            jax.ShapeDtypeStruct((rows, PLANE * 3 * HD), BF16),
            jax.ShapeDtypeStruct(gain_blocks.shape, gain_blocks.dtype),
        ),
        in_specs=[ANY, ANY],
        out_specs=(ANY, ANY),
        scratch_shapes=[DMA((4,)), DMA((21,)), DMA((21,)), DMA((peers,)), DMA((peers,))],
        compiler_params=pltpu.CompilerParams(collective_id=7, has_side_effects=True),
        name="collect_attn",
    )(term, gain_blocks)


def block_scores(q, k, start, first):
    scores = lax.dot_general(q, k, (((1,), (1,)), ((), ())), preferred_element_type=F32)
    bent = jnp.tanh(scores * (HD ** (-0.5) / SOFT_CAP))
    rows, span = scores.shape
    key_at = lax.broadcasted_iota(jnp.int32, (rows, span), 1)
    row_at = lax.broadcasted_iota(jnp.int32, (rows, span), 0)
    allowed = (key_at + first >= start) & (key_at <= row_at + LMAX)
    return (bent, jnp.where(allowed, jnp.exp(SOFT_CAP * bent), 0.0))


def attend_kernel(q_ref, k_ref, v_ref, start_ref, out_ref, inv_ref):
    first = pl.program_id(0) * QBLK
    keys = pl.ds(pl.multiple_of(first, QBLK), LMAX + QBLK)
    unused_bent, exponent = block_scores(q_ref[...], k_ref[keys], start_ref[...], first)
    inverse = 1.0 / jnp.sum(exponent, axis=-1, keepdims=True)
    weights = (exponent * inverse).astype(BF16)
    out_ref[...] = jnp.dot(weights, v_ref[keys], preferred_element_type=F32).astype(BF16)
    inv_ref[...] = inverse


def attend(queries, key_rows, value_rows, starts):
    rows = queries.shape[0]
    span = key_rows.shape[0]
    row_spec = pl.BlockSpec((QBLK, HD), lambda i: (i, 0))
    one_spec = pl.BlockSpec((QBLK, 1), lambda i: (i, 0))
    all_spec = pl.BlockSpec((span, HD), lambda i: (0, 0))
    return pl.pallas_call(
        attend_kernel,
        out_shape=(
            jax.ShapeDtypeStruct((rows, HD), BF16),
            jax.ShapeDtypeStruct((rows, 1), F32),
        ),
        grid=(rows // QBLK,),
        in_specs=[row_spec, all_spec, all_spec, one_spec],
        out_specs=(row_spec, one_spec),
        compiler_params=pltpu.CompilerParams(vmem_limit_bytes=40 << 20),
        cost_estimate=cost(1),
        name="attend",
    )(queries, key_rows, value_rows, starts)


def attend_back_kernel(q_ref, k_ref, v_ref, start_ref, inv_ref, grad_ref, gq_ref, gk_ref, gv_ref):
    @pl.when(pl.program_id(0) == 0)
    def _():
        gk_ref[...] = jnp.zeros_like(gk_ref)
        gv_ref[...] = jnp.zeros_like(gv_ref)

    first = pl.program_id(0) * QBLK
    keys = pl.ds(pl.multiple_of(first, QBLK), LMAX + QBLK)
    q, k, v, grad = q_ref[...], k_ref[keys], v_ref[keys], grad_ref[...]
    bent, exponent = block_scores(q, k, start_ref[...], first)
    probability = exponent * inv_ref[...]
    grad_prob = lax.dot_general(grad, v, (((1,), (1,)), ((), ())), preferred_element_type=F32)
    inner = jnp.sum(probability * grad_prob, axis=-1, keepdims=True)
    grad_scores = (probability * (grad_prob - inner) * (1.0 - bent * bent)).astype(BF16)
    scale = HD ** (-0.5)
    gq_ref[...] = jnp.dot(grad_scores, k, preferred_element_type=F32) * scale
    over_rows = (((0,), (0,)), ((), ()))
    gk_ref[keys] += lax.dot_general(grad_scores, q, over_rows, preferred_element_type=F32) * scale
    gv_ref[keys] += lax.dot_general(
        probability.astype(BF16), grad, over_rows, preferred_element_type=F32
    )


def attend_back(queries, key_rows, value_rows, starts, inverse, grad):
    rows = queries.shape[0]
    span = key_rows.shape[0]
    row_spec = pl.BlockSpec((QBLK, HD), lambda i: (i, 0))
    one_spec = pl.BlockSpec((QBLK, 1), lambda i: (i, 0))
    all_spec = pl.BlockSpec((span, HD), lambda i: (0, 0))
    return pl.pallas_call(
        attend_back_kernel,
        out_shape=(
            jax.ShapeDtypeStruct((rows, HD), F32),
            jax.ShapeDtypeStruct((span, HD), F32),
            jax.ShapeDtypeStruct((span, HD), F32),
        ),
        grid=(rows // QBLK,),
        in_specs=[row_spec, all_spec, all_spec, one_spec, one_spec, row_spec],
        out_specs=(row_spec, all_spec, all_spec),
        compiler_params=pltpu.CompilerParams(vmem_limit_bytes=48 << 20),
        cost_estimate=cost(20),
        name="attend_back",
    )(queries, key_rows, value_rows, starts, inverse, grad)


def token_tables(seq_lengths, index_vec):
    count = seq_lengths.shape[0]
    order = jnp.arange(count, dtype=jnp.int32)
    seq_ends = jnp.sum(
        jnp.where(order[None, :] <= order[:, None], seq_lengths[None, :], 0), axis=1
    )
    after_end = index_vec[:, None] >= seq_ends[None, :]
    return index_vec - jnp.sum(jnp.where(after_end, seq_lengths[None, :], 0), axis=1)


def rms_parts(value):
    return lax.rsqrt(jnp.mean(value * value, axis=-1, keepdims=True) + EPSILON)


def rms_forward(value, gain_vec):
    return value * rms_parts(value) * (1.0 + gain_vec)


def rms_backward(value, gain_vec, grad):
    r = rms_parts(value)
    scaled = (1.0 + gain_vec) * grad
    inner = jnp.mean(value * scaled, axis=-1, keepdims=True)
    return (r * scaled - value * (r * r * r * inner), jnp.sum(grad * value * r, axis=0))


def rotate(value, cosine, sine_part):
    half_width = value.shape[-1] // 2
    first_half = value[..., :half_width]
    second_half = value[..., half_width:]
    return jnp.concatenate(
        [
            first_half * cosine - second_half * sine_part,
            second_half * cosine + first_half * sine_part,
        ],
        axis=-1,
    )


def contract_last(left_side, right_side):
    return lax.dot_general(
        left_side, right_side, (((1,), (1,)), ((), ())), preferred_element_type=F32
    )


def contract_first(left_side, right_side):
    return lax.dot_general(
        left_side, right_side, (((0,), (0,)), ((), ())), preferred_element_type=F32
    )


def matmul(left_side, right_side):
    return jnp.dot(left_side, right_side, preferred_element_type=F32)


def gelu_parts(gate):
    k0 = 0.7978845608028654
    k1 = 0.044715
    t = jnp.tanh(k0 * (gate + k1 * gate * gate * gate))
    value = 0.5 * gate * (1.0 + t)
    slope = 0.5 * (1.0 + t) + 0.5 * gate * (1.0 - t * t) * k0 * (1.0 + 3.0 * k1 * gate * gate)
    return (value, slope)


def local(tokens, attn_weights, mlp_weights, norm_gains, seq_lengths, cotangent):
    tok_rows, width = tokens.shape
    peers = lax.axis_size(AXIS)
    planes = peers // PLANE
    share = width // peers
    row_share = attn_weights.shape[0]
    ff = mlp_weights.shape[1] // 3
    ffc = ff // PLANE
    plane_rows = PLANE * tok_rows
    halo = LMAX
    across = [[p * PLANE + i for p in range(planes)] for i in range(PLANE)]
    sibling = [(i, i ^ 1) for i in range(peers)]
    to_next = [(i, i + PLANE) for i in range(peers - PLANE)]
    to_prev = [(i + PLANE, i) for i in range(peers - PLANE)]
    me = lax.axis_index(AXIS)
    is_even = (me % 2) == 0
    plane_start = (me // PLANE) * plane_rows

    def gather_across(value):
        return lax.all_gather(value, AXIS, axis=0, tiled=True, axis_index_groups=across)

    def scatter_across(value):
        part = lax.psum_scatter(
            value.astype(BF16), AXIS, scatter_dimension=0, tiled=True, axis_index_groups=across
        )
        return part.reshape(PLANE, -1, part.shape[1])

    gain_block = jnp.pad(norm_gains.astype(F32), ((0, 8 - 4), (0, -share % 128)))
    attn_part, gain_block = lax.optimization_barrier((spread_attn(attn_weights), gain_block))
    attn_cols = gather_across(attn_part.reshape(-1, 3 * HD))
    gu_part, gain_blocks = spread_gu(mlp_weights, gain_block, peers)
    gain_full = gain_blocks[:, :4, :share].transpose(1, 0, 2).reshape(4, width)
    inputs = tokens.astype(F32)
    down_part, normed = spread_down(
        mlp_weights, rms_forward(inputs, gain_full[0]).astype(BF16)
    )
    gu_cols = gather_across(gu_part.reshape(-1, 2 * ffc))
    down_cols = gather_across(down_part.reshape(-1, ffc))
    qkv_cols = attn_cols[:, : 2 * HD]
    out_cols = attn_cols[:, 2 * HD :]

    query_index = plane_start + jnp.arange(plane_rows, dtype=jnp.int32)
    position = token_tables(seq_lengths, query_index)
    starts = (jnp.arange(plane_rows, dtype=jnp.int32) + halo - position)[:, None]
    frequency = 10000.0 ** (-jnp.arange(HD // 2, dtype=F32) * 2.0 / HD)
    angles = position.astype(F32)[:, None] * frequency[None, :]
    cosine, sine_part = jnp.cos(angles), jnp.sin(angles)
    kv_cosine = jnp.where(is_even, cosine, 1.0)
    kv_sine = jnp.where(is_even, sine_part, 0.0)

    projected = matmul(normed, qkv_cols)
    queries = rotate(projected[:, :HD], cosine, sine_part).astype(BF16)
    kv_own = rotate(projected[:, HD:], kv_cosine, kv_sine).astype(BF16)
    kv_halo = lax.ppermute(kv_own[plane_rows - halo :], AXIS, to_next)
    kv_mine = jnp.concatenate([kv_halo, kv_own], axis=0)
    kv_other = lax.ppermute(kv_mine, AXIS, sibling)
    key_rows = jnp.where(is_even, kv_mine, kv_other)
    value_rows = jnp.where(is_even, kv_other, kv_mine)
    attended, inverse = attend(queries, key_rows, value_rows, starts)
    attn_proj = product_scatter([attended], [out_cols], [0], PLANE_STEP, 11)

    middle = inputs + rms_forward(attn_proj, gain_full[1])
    mid_low = gather_square(rms_forward(middle, gain_full[2]).astype(BF16), PLANE_STEP, 1)
    gate_up = matmul(mid_low, gu_cols)
    gate, up = gate_up[:, :ffc], gate_up[:, ffc:]
    gelu, slope = gelu_parts(gate)
    hidden = (gelu * up).astype(BF16)
    mlp_raw, grad_raw_low, down_grad = turn(
        hidden, down_cols, gain_full[3:4], cotangent, PLANE_STEP, 9
    )
    layer_output = (middle + rms_forward(mlp_raw, gain_full[3])).astype(BF16)

    grad_out = cotangent.astype(F32)
    gain_four = jnp.sum(grad_out * mlp_raw * rms_parts(mlp_raw), axis=0)
    down_term = scatter_across(down_grad)
    grad_hidden = matmul(grad_raw_low, down_cols)
    grad_gate = (slope * up * grad_hidden).astype(BF16)
    grad_up = (gelu * grad_hidden).astype(BF16)
    gate_grad = contract_first(mid_low, grad_gate).astype(BF16)
    gate_grad, grad_up = lax.optimization_barrier((gate_grad, grad_up))
    gate_term = scatter_across(gate_grad)
    up_grad = contract_first(mid_low, grad_up).astype(BF16)
    up_grad, grad_up = lax.optimization_barrier((up_grad, grad_up))
    up_term = scatter_across(up_grad)
    grad_normed_mid = product_scatter(
        [grad_gate, grad_up], [gu_cols, gu_cols], [0, ffc], PLANE_STEP, 10
    )
    grad_mid_part, gain_three = rms_backward(middle, gain_full[2], grad_normed_mid)
    grad_middle = grad_out + grad_mid_part

    grad_proj, gain_two = rms_backward(attn_proj, gain_full[1], grad_middle)
    grad_proj_own, down_term = lax.optimization_barrier((grad_proj.astype(BF16), down_term))
    grad_proj_low = gather_square(grad_proj_own, PLANE_STEP, 1)
    grad_att = matmul(grad_proj_low, out_cols).astype(BF16)
    grad_query, grad_keys, grad_values = attend_back(
        queries, key_rows, value_rows, starts, inverse, grad_att
    )
    grad_mine = jnp.where(is_even, grad_keys, grad_values)
    grad_give = jnp.where(is_even, grad_values, grad_keys).astype(BF16)
    grad_kv = grad_mine + lax.ppermute(grad_give, AXIS, sibling).astype(F32)
    grad_back = lax.ppermute(grad_kv[:halo].astype(BF16), AXIS, to_prev).astype(F32)
    down_term, gate_term, grad_kv = lax.optimization_barrier((down_term, gate_term, grad_kv))
    gate_rows, down_rows = jnp.split(collect([gate_term, down_term], 6), 2, axis=1)
    gate_rows, down_rows, grad_back = lax.optimization_barrier((gate_rows, down_rows, grad_back))
    grad_kv = grad_kv[halo:] + jnp.pad(grad_back, ((plane_rows - halo, 0), (0, 0)))
    grad_qkv = jnp.concatenate(
        [
            rotate(grad_query, cosine, -sine_part).astype(BF16),
            rotate(grad_kv, kv_cosine, -kv_sine).astype(BF16),
        ],
        axis=1,
    )
    attn_grad = jnp.concatenate(
        [contract_first(normed, grad_qkv), contract_first(grad_proj_low, attended)], axis=1
    ).astype(BF16)
    attn_grad, grad_qkv = lax.optimization_barrier((attn_grad, grad_qkv))
    attn_term = scatter_across(attn_grad)
    grad_normed = product_scatter([grad_qkv], [qkv_cols], [0], PLANE_STEP, 12)
    grad_in_part, gain_one = rms_backward(inputs, gain_full[0], grad_normed)
    grad_tokens = (grad_middle + grad_in_part).astype(BF16)

    gain_term = jnp.stack([gain_one, gain_two, gain_three, gain_four], axis=0)
    gain_term = gain_term.reshape(4, peers, share).transpose(1, 0, 2)
    gain_term = jnp.pad(gain_term, ((0, 0), (0, 8 - 4), (0, -share % 128)))
    up_term, gain_term = lax.optimization_barrier((up_term, gain_term))
    up_rows = collect([up_term], 13)
    grad_mlp = jnp.concatenate([gate_rows, up_rows, down_rows], axis=1).astype(F32)
    grad_mlp, attn_term = lax.optimization_barrier((grad_mlp, attn_term))
    attn_rows, gain_recv = collect_attn(attn_term, gain_term)
    grad_attn = attn_rows.astype(F32)
    grad_gains = jnp.sum(gain_recv[:, :4, :share], axis=0)
    return (layer_output, grad_tokens, grad_attn, grad_mlp, grad_gains)


def solution(mesh):
    return jax.shard_map(
        local,
        mesh=mesh,
        in_specs=(
            P("fsdp", None),
            P("fsdp", None),
            P("fsdp", None),
            P(None, "fsdp"),
            P(),
            P("fsdp", None),
        ),
        out_specs=(
            P("fsdp", None),
            P("fsdp", None),
            P("fsdp", None),
            P("fsdp", None),
            P(None, "fsdp"),
        ),
        check_vma=False,
    )
```

```python
from functools import partial

import jax
import jax.numpy as jnp
from jax import lax
from jax.experimental import pallas as pl
from jax.experimental.pallas import tpu as pltpu
from jax.sharding import PartitionSpec as P

H = 8
KVH = 4
HD = 256
LMAX = 1024
PLANE = 8
QBLK = 128

EPSILON = 1e-06
SOFT_CAP = 50.0
AXIS = "fsdp"
F32 = jnp.float32
BF16 = jnp.bfloat16
MESH = pl.DeviceIdType.MESH
ANY = pl.BlockSpec(memory_space=pl.ANY)
VMEM = pl.BlockSpec(memory_space=pltpu.VMEM)
DMA = pltpu.SemaphoreType.DMA


def flip(index, step):
    return index + step - 2 * step * ((index // step) % 2)


PLANE_STEP = 4


def partner(index, bits, step):
    for bit, by in ((1, 1), (2, 2), (4, step)):
        if bits & bit:
            index = flip(index, by)
    return index


def place(device, step):
    return device % 4 + 4 * ((device // step) % 2)


def greet(peers):
    barrier = pltpu.get_barrier_semaphore()
    for peer in peers:
        pl.semaphore_signal(barrier, inc=1, device_id=(peer,), device_id_type=MESH)
    pl.semaphore_wait(barrier, len(peers))


class Copies:
    def __init__(self, send_sem, recv_sem):
        self.send_sem, self.recv_sem, self.made = send_sem, recv_sem, []

    def start(self, source, target, device):
        slot = len(self.made)
        copy = pltpu.make_async_remote_copy(
            src_ref=source,
            dst_ref=target,
            send_sem=self.send_sem.at[slot],
            recv_sem=self.recv_sem.at[slot],
            device_id=(device,),
            device_id_type=MESH,
        )
        copy.start()
        self.made.append(copy)
        return copy

    def sent(self):
        for copy in self.made:
            copy.wait_send()


def band(index, size):
    return pl.ds(pl.multiple_of(index * size, 8), size)


def lanes(index, size):
    return pl.ds(pl.multiple_of(index * size, 128), size)


def gather_steps(block_ref, full_ref, copies, own_sem, step):
    rows, width = block_ref.shape
    half = width // 2
    me = lax.axis_index(AXIS)
    sib, xn, yn = flip(me, 1), flip(me, 2), flip(me, step)
    diag = flip(xn, step)

    def at(device, side):
        return full_ref.at[band(place(device, step), rows), pl.ds(side * half, half)]

    def mine(side):
        return block_ref.at[:, pl.ds(side * half, half)]

    own_rows = full_ref.at[band(place(me, step), rows)]
    xa = copies.start(mine(0), at(me, 0), xn)
    ya = copies.start(mine(1), at(me, 1), yn)
    xb = copies.start(mine(1), at(me, 1), xn)
    yb = copies.start(mine(0), at(me, 0), yn)
    arriving = [copies.start(block_ref, own_rows, sib)]
    own = pltpu.make_async_copy(block_ref, own_rows, own_sem)
    own.start()

    def finish(on_rows=None):
        def to_sibling(device, side):
            arriving.append(copies.start(at(device, side), at(device, side), sib))

        def arrived(first, last, *devices):
            for copy in arriving[first:last]:
                copy.wait_recv()
            for device in devices:
                on_rows(device)

        if on_rows is not None:
            own.wait()
            arrived(0, 1, me)
        xa.wait_recv()
        yc = copies.start(at(xn, 0), at(xn, 0), yn)
        to_sibling(xn, 0)
        ya.wait_recv()
        xc = copies.start(at(yn, 1), at(yn, 1), xn)
        to_sibling(yn, 1)
        xb.wait_recv()
        to_sibling(xn, 1)
        yb.wait_recv()
        to_sibling(yn, 0)
        if on_rows is not None:
            arrived(1, 5, xn, yn)
        yc.wait_recv()
        to_sibling(diag, 0)
        xc.wait_recv()
        to_sibling(diag, 1)
        if on_rows is not None:
            arrived(5, 7, diag)
        else:
            arrived(0, 7)
            own.wait()

    return finish


GATHER_COPIES = 13


def cost(microseconds):
    return pl.CostEstimate(
        flops=int(microseconds * 1e7), transcendentals=0, bytes_accessed=int(microseconds * 3e4)
    )


def gather_kernel(block_ref, full_ref, own_sem, send_sem, recv_sem, *, step):
    me = lax.axis_index(AXIS)
    greet((flip(me, 1), flip(me, 2), flip(me, step)))
    copies = Copies(send_sem, recv_sem)
    gather_steps(block_ref, full_ref, copies, own_sem, step)()
    copies.sent()


def gather_square(block, step, collective_id):
    rows, width = block.shape
    return pl.pallas_call(
        partial(gather_kernel, step=step),
        out_shape=jax.ShapeDtypeStruct((PLANE * rows, width), block.dtype),
        in_specs=[ANY],
        out_specs=ANY,
        scratch_shapes=[DMA(()), DMA((GATHER_COPIES,)), DMA((GATHER_COPIES,))],
        compiler_params=pltpu.CompilerParams(collective_id=collective_id, has_side_effects=True),
        cost_estimate=cost(42),
        name="gather_square",
    )(block)


W_TILES = 3


def product_scatter_steps(
    left_refs, right_refs, left_bufs, right_bufs, buffers, load_sem, copies, offsets, step
):
    both, got, ra, rb, ra2, rb2 = buffers
    pairs = len(left_refs)
    rows, width = got.shape[1:]
    half = width // 2
    tile = width // W_TILES
    chunk = 16
    me = lax.axis_index(AXIS)
    core = me % 2
    sib, xn, yn = flip(me, 1), flip(me, 2), flip(me, step)
    order = (flip(xn, step), xn, yn, me)
    first, second = pl.ds(0, half), pl.ds(half, half)

    def chip_rows(device):
        return pl.ds(pl.multiple_of((place(device, step) // 2) * 2 * rows, 16), 2 * rows)

    def right_load(j, t):
        r = pl.ds(t * tile, tile)
        source = right_refs[j].at[r, pl.ds(offsets[j], right_bufs[j].shape[1])]
        return pltpu.make_async_copy(source, right_bufs[j].at[r], load_sem.at[j, t])

    def left_load(j, i):
        r = chip_rows(order[i])
        return pltpu.make_async_copy(
            left_refs[j].at[r], left_bufs[j].at[r], load_sem.at[j, W_TILES + i]
        )

    for j in range(pairs):
        left_load(j, 0).start()
    for t in range(W_TILES):
        for j in range(pairs):
            right_load(j, t).start()
    for i in range(1, 4):
        for j in range(pairs):
            left_load(j, i).start()
    greet((sib, xn, yn))

    def product(i):
        r = chip_rows(order[i])
        for j in range(pairs):
            left_load(j, i).wait()

        def columns(w):
            total = None
            for j in range(pairs):
                term = contract_last(left_bufs[j][r], right_bufs[j][w])
                total = term if total is None else total + term
            both[i, :, w] = total.astype(BF16)

        if i == 0:
            for t in range(W_TILES):
                for j in range(pairs):
                    right_load(j, t).wait()
                columns(pl.ds(t * tile, tile))
        else:

            @pl.loop(0, W_TILES)
            def _(t):
                columns(pl.ds(pl.multiple_of(t * tile, tile), tile))

    def mine(i, cols=None):
        if cols is None:
            return both.at[i, band(core, rows)]
        return both.at[i, band(core, rows), cols]

    def add(total, other):
        @pl.loop(0, rows // chunk)
        def _(k):
            r = pl.ds(pl.multiple_of(k * chunk, chunk), chunk)
            total[r] = (total[r].astype(F32) + other[r].astype(F32)).astype(total.dtype)

    def make(i):
        product(i)
        crossing = copies.start(both.at[i, band(1 - core, rows)], got.at[i], sib)
        crossing.wait_recv()
        add(mine(i), got.at[i])

    make(0)
    x0 = copies.start(mine(0, first), ra.at[0], xn)
    y0 = copies.start(mine(0, second), rb.at[0], yn)
    make(1)
    x1 = copies.start(mine(1, first), ra.at[1], xn)
    make(2)
    y1 = copies.start(mine(2, second), rb.at[1], yn)
    x0.wait_recv()
    add(mine(2, first), ra.at[0])
    y2 = copies.start(mine(2, first), ra2, yn)
    y0.wait_recv()
    add(mine(1, second), rb.at[0])
    x2 = copies.start(mine(1, second), rb2, xn)
    make(3)
    for copy in (x1, y1, y2, x2):
        copy.wait_recv()
    own = mine(3)

    def summed(r):
        return jnp.concatenate(
            [
                own[r, first].astype(F32) + ra[1, r].astype(F32) + ra2[r].astype(F32),
                own[r, second].astype(F32) + rb[1, r].astype(F32) + rb2[r].astype(F32),
            ],
            axis=1,
        )

    return summed


ROW_CHUNK = 16


def product_scatter_kernel(*refs, pairs, offsets, step):
    left_refs, right_refs, out_ref = refs[:pairs], refs[pairs : 2 * pairs], refs[2 * pairs]
    left_bufs = refs[2 * pairs + 1 : 3 * pairs + 1]
    right_bufs = refs[3 * pairs + 1 : 4 * pairs + 1]
    buffers, (load_sem, send_sem, recv_sem) = refs[4 * pairs + 1 : -3], refs[-3:]
    copies = Copies(send_sem, recv_sem)
    summed = product_scatter_steps(
        left_refs, right_refs, left_bufs, right_bufs, buffers, load_sem, copies, offsets, step
    )

    @pl.loop(0, out_ref.shape[0] // ROW_CHUNK)
    def _(k):
        r = pl.ds(pl.multiple_of(k * ROW_CHUNK, ROW_CHUNK), ROW_CHUNK)
        out_ref[r] = summed(r)

    copies.sent()


def scatter_buffers(rows, width):
    half = width // 2
    return [
        pltpu.VMEM((4, 2 * rows, width), BF16),
        pltpu.VMEM((4, rows, width), BF16),
        pltpu.VMEM((2, rows, half), BF16),
        pltpu.VMEM((2, rows, half), BF16),
        pltpu.VMEM((rows, half), BF16),
        pltpu.VMEM((rows, half), BF16),
    ]


def product_scatter(lefts, rights, offsets, step, collective_id):
    pairs = len(lefts)
    rows, width = lefts[0].shape[0] // PLANE, rights[0].shape[0]
    return pl.pallas_call(
        partial(product_scatter_kernel, pairs=pairs, offsets=offsets, step=step),
        out_shape=jax.ShapeDtypeStruct((rows, width), F32),
        in_specs=[ANY] * (2 * pairs),
        out_specs=VMEM,
        scratch_shapes=[
            *[pltpu.VMEM(value.shape, BF16) for value in lefts],
            *[pltpu.VMEM((width, value.shape[1]), BF16) for value in lefts],
            *scatter_buffers(rows, width),
            DMA((pairs, W_TILES + 4)),
            DMA((10,)),
            DMA((10,)),
        ],
        compiler_params=pltpu.CompilerParams(
            collective_id=collective_id, has_side_effects=True, vmem_limit_bytes=56 << 20
        ),
        cost_estimate=cost(50),
        name="product_scatter",
    )(*lefts, *rights)


TURN_TILE = 768


def turn_kernel(
    left_ref, right_ref, gain_ref, grad_ref, raw_ref, full_ref, term_ref, *refs, step
):
    left_buf, right_buf, gathered, total, grad_own = refs[:5]
    buffers, (load_sem, own_sem, store_sem, send_sem, recv_sem) = refs[5:-5], refs[-5:]
    rows, width = grad_ref.shape
    copies = Copies(send_sem, recv_sem)
    summed = product_scatter_steps(
        [left_ref], [right_ref], [left_buf], [right_buf], buffers, load_sem, copies, [0], step
    )
    gain = gain_ref[...]

    @pl.loop(0, rows // ROW_CHUNK)
    def _(k):
        r = pl.ds(pl.multiple_of(k * ROW_CHUNK, ROW_CHUNK), ROW_CHUNK)
        value = summed(r)
        raw_ref[r] = value
        scale = lax.rsqrt(jnp.mean(value * value, axis=1, keepdims=True) + EPSILON)
        scaled = (1.0 + gain) * grad_ref[r].astype(F32)
        inner = jnp.mean(value * scaled, axis=1, keepdims=True)
        grad_own[r] = (scale * scaled - value * (scale * scale * scale * inner)).astype(BF16)

    stores = []

    def on_rows(device):
        slot = len(stores)
        r = pl.ds(pl.multiple_of((place(device, step) // 2) * 2 * rows, 16), 2 * rows)
        store = pltpu.make_async_copy(gathered.at[r], full_ref.at[r], store_sem.at[slot])
        store.start()
        stores.append(store)
        right = left_buf[r]

        @pl.loop(0, width // TURN_TILE)
        def _(t):
            w = pl.ds(pl.multiple_of(t * TURN_TILE, TURN_TILE), TURN_TILE)
            term = contract_first(gathered[r, w], right)
            if slot == 0:
                total[w] = term
            elif slot < 3:
                total[w] += term
            else:
                right_buf[w] = (total[w] + term).astype(BF16)
                pltpu.make_async_copy(right_buf.at[w], term_ref.at[w], store_sem.at[4]).start()

    gather_steps(grad_own, gathered, copies, own_sem, step)(on_rows)
    pltpu.make_async_copy(right_buf, term_ref, store_sem.at[4]).wait()
    for store in stores:
        store.wait()
    copies.sent()


def turn(left, right, gain_row, grad, step, collective_id):
    rows, width = grad.shape
    count = 10 + GATHER_COPIES
    return pl.pallas_call(
        partial(turn_kernel, step=step),
        out_shape=(
            jax.ShapeDtypeStruct((rows, width), F32),
            jax.ShapeDtypeStruct((PLANE * rows, width), BF16),
            jax.ShapeDtypeStruct((width, left.shape[1]), BF16),
        ),
        in_specs=[ANY, ANY, VMEM, VMEM],
        out_specs=(VMEM, ANY, ANY),
        scratch_shapes=[
            pltpu.VMEM(left.shape, BF16),
            pltpu.VMEM(right.shape, BF16),
            pltpu.VMEM((PLANE * rows, width), BF16),
            pltpu.VMEM((width, left.shape[1]), F32),
            pltpu.VMEM((rows, width), BF16),
            *scatter_buffers(rows, width),
            DMA((1, W_TILES + 4)),
            DMA(()),
            DMA((5,)),
            DMA((count,)),
            DMA((count,)),
        ],
        compiler_params=pltpu.CompilerParams(
            collective_id=collective_id, has_side_effects=True, vmem_limit_bytes=60 << 20
        ),
        cost_estimate=cost(50),
        name="turn",
    )(left, right, gain_row, grad)


def attn_columns(column):
    query_width = H * HD
    key_offset = query_width + (column % 2) * KVH * HD + (column // 2) * HD
    return (column * HD, key_offset, query_width + 2 * KVH * HD + column * HD)


def greet_all(peers):
    me = lax.axis_index(AXIS)
    barrier = pltpu.get_barrier_semaphore()

    @pl.loop(1, peers)
    def _(k):
        device = lax.rem(me + k, peers)
        pl.semaphore_signal(barrier, inc=1, device_id=(device,), device_id_type=MESH)

    pl.semaphore_wait(barrier, peers - 1)


def exchange_all(source_of, target_ref, send_sem, recv_sem):
    peers = target_ref.shape[0]
    me = lax.axis_index(AXIS)

    def copy(k):
        device = lax.rem(me + k, peers)
        return pltpu.make_async_remote_copy(
            src_ref=source_of(device),
            dst_ref=target_ref.at[me],
            send_sem=send_sem.at[k],
            recv_sem=recv_sem.at[k],
            device_id=(device,),
            device_id_type=MESH,
        )

    @pl.loop(1, peers)
    def _(k):
        copy(k).start()

    def finish():
        @pl.loop(1, peers)
        def _(k):
            copy(k).wait()

    return finish


ORDER = (6, 7, 2, 3, 4, 5, 1)


def swap_steps(pieces_of, targets, copies, own_sem, step):
    me = lax.axis_index(AXIS)
    moved = []
    for bits in ORDER:
        peer = partner(me, bits, step)
        for source, target in zip(pieces_of(place(peer, step)), targets):
            moved.append(copies.start(source, target, peer))
    owns = []
    for slot, (source, target) in enumerate(zip(pieces_of(place(me, step)), targets)):
        own = pltpu.make_async_copy(source, target, own_sem.at[slot])
        own.start()
        owns.append(own)

    def finish():
        for own in owns:
            own.wait()
        for copy in moved:
            copy.wait_recv()

    return finish


def square(step):
    me = lax.axis_index(AXIS)
    return [partner(me, bits, step) for bits in ORDER]


def wide(offset):
    return pl.ds(pl.multiple_of(offset, 128), HD)


def spread_attn_kernel(weights_ref, part_ref, own_sem, send_sem, recv_sem):
    here = place(lax.axis_index(AXIS), PLANE_STEP)
    greet(square(PLANE_STEP))
    copies = Copies(send_sem, recv_sem)
    swap_steps(
        lambda c: [weights_ref.at[:, wide(offset)] for offset in attn_columns(c)],
        [part_ref.at[here, :, pl.ds(slot * HD, HD)] for slot in range(3)],
        copies,
        own_sem,
        PLANE_STEP,
    )()
    copies.sent()


def spread_attn(weights):
    rows = weights.shape[0]
    return pl.pallas_call(
        spread_attn_kernel,
        out_shape=jax.ShapeDtypeStruct((PLANE, rows, 3 * HD), BF16),
        in_specs=[ANY],
        out_specs=ANY,
        scratch_shapes=[DMA((3,)), DMA((21,)), DMA((21,))],
        compiler_params=pltpu.CompilerParams(collective_id=3, has_side_effects=True),
        name="spread_attn",
    )(weights)


def spread_gu_kernel(
    weights_ref, gain_ref, gu_ref, gains_ref, own_sem, send_sem, recv_sem, gain_send, gain_recv
):
    peers = gains_ref.shape[0]
    ffc = gu_ref.shape[2] // 2
    me = lax.axis_index(AXIS)
    here = place(me, PLANE_STEP)
    greet_all(peers)
    gains_done = exchange_all(lambda device: gain_ref, gains_ref, gain_send, gain_recv)
    own = pltpu.make_async_copy(gain_ref, gains_ref.at[me], own_sem.at[2])
    own.start()
    copies = Copies(send_sem, recv_sem)
    swap_steps(
        lambda c: [weights_ref.at[:, lanes(slot * PLANE + c, ffc)] for slot in range(2)],
        [gu_ref.at[here, :, pl.ds(slot * ffc, ffc)] for slot in range(2)],
        copies,
        own_sem,
        PLANE_STEP,
    )()
    own.wait()
    gains_done()
    copies.sent()


def spread_gu(weights, gain_block, peers):
    rows = weights.shape[0]
    ffc = weights.shape[1] // 3 // PLANE
    return pl.pallas_call(
        spread_gu_kernel,
        out_shape=(
            jax.ShapeDtypeStruct((PLANE, rows, 2 * ffc), BF16),
            jax.ShapeDtypeStruct((peers,) + gain_block.shape, gain_block.dtype),
        ),
        in_specs=[ANY, ANY],
        out_specs=(ANY, ANY),
        scratch_shapes=[DMA((3,)), DMA((14,)), DMA((14,)), DMA((peers,)), DMA((peers,))],
        compiler_params=pltpu.CompilerParams(collective_id=4, has_side_effects=True),
        cost_estimate=cost(38),
        name="spread_gu",
    )(weights, gain_block)


def spread_down_kernel(weights_ref, block_ref, down_ref, full_ref, own_sem, send_sem, recv_sem):
    ffc = down_ref.shape[2]
    me = lax.axis_index(AXIS)
    greet(square(PLANE_STEP))
    copies = Copies(send_sem, recv_sem)
    gathered = gather_steps(block_ref, full_ref, copies, own_sem.at[1], PLANE_STEP)
    spread = swap_steps(
        lambda c: [weights_ref.at[:, lanes(2 * PLANE + c, ffc)]],
        [down_ref.at[place(me, PLANE_STEP)]],
        copies,
        own_sem,
        PLANE_STEP,
    )
    gathered()
    spread()
    copies.sent()


def spread_down(weights, block):
    rows = weights.shape[0]
    ffc = weights.shape[1] // 3 // PLANE
    count = GATHER_COPIES + 7
    return pl.pallas_call(
        spread_down_kernel,
        out_shape=(
            jax.ShapeDtypeStruct((PLANE, rows, ffc), BF16),
            jax.ShapeDtypeStruct((PLANE * block.shape[0], block.shape[1]), BF16),
        ),
        in_specs=[ANY, ANY],
        out_specs=(ANY, ANY),
        scratch_shapes=[DMA((2,)), DMA((count,)), DMA((count,))],
        compiler_params=pltpu.CompilerParams(collective_id=5, has_side_effects=True),
        cost_estimate=cost(1),
        name="spread_down",
    )(weights, block)


def collect_kernel(term_ref, rows_ref, own_sem, send_sem, recv_sem):
    here = place(lax.axis_index(AXIS), PLANE_STEP)
    count = own_sem.shape[0]
    ffc = term_ref.shape[2] // count
    greet(square(PLANE_STEP))
    copies = Copies(send_sem, recv_sem)
    swap_steps(
        lambda c: [term_ref.at[c, :, pl.ds(slot * ffc, ffc)] for slot in range(count)],
        [rows_ref.at[:, lanes(slot * PLANE + here, ffc)] for slot in range(count)],
        copies,
        own_sem,
        PLANE_STEP,
    )()
    copies.sent()


def collect(term, count, collective_id):
    rows, columns = term.shape[1:]
    return pl.pallas_call(
        collect_kernel,
        out_shape=jax.ShapeDtypeStruct((rows, PLANE * columns), BF16),
        in_specs=[ANY],
        out_specs=ANY,
        scratch_shapes=[DMA((count,)), DMA((7 * count,)), DMA((7 * count,))],
        compiler_params=pltpu.CompilerParams(collective_id=collective_id, has_side_effects=True),
        cost_estimate=cost(0.1),
        name="collect",
    )(term)


def collect_attn_kernel(term_ref, rows_ref, own_sem, send_sem, recv_sem):
    here = place(lax.axis_index(AXIS), PLANE_STEP)
    greet(square(PLANE_STEP))
    copies = Copies(send_sem, recv_sem)
    swap_steps(
        lambda c: [term_ref.at[c, :, pl.ds(slot * HD, HD)] for slot in range(3)],
        [rows_ref.at[:, wide(offset)] for offset in attn_columns(here)],
        copies,
        own_sem,
        PLANE_STEP,
    )()
    copies.sent()


def collect_attn(term):
    rows = term.shape[1]
    return pl.pallas_call(
        collect_attn_kernel,
        out_shape=jax.ShapeDtypeStruct((rows, PLANE * 3 * HD), BF16),
        in_specs=[ANY],
        out_specs=ANY,
        scratch_shapes=[DMA((3,)), DMA((21,)), DMA((21,))],
        compiler_params=pltpu.CompilerParams(collective_id=7, has_side_effects=True),
        name="collect_attn",
    )(term)


def collect_gains_kernel(gain_ref, gains_ref, own_sem, gain_send, gain_recv):
    me = lax.axis_index(AXIS)
    greet_all(gain_ref.shape[0])
    done = exchange_all(lambda device: gain_ref.at[device], gains_ref, gain_send, gain_recv)
    own = pltpu.make_async_copy(gain_ref.at[me], gains_ref.at[me], own_sem)
    own.start()
    own.wait()
    done()


def collect_gains(gain_blocks):
    peers = gain_blocks.shape[0]
    return pl.pallas_call(
        collect_gains_kernel,
        out_shape=jax.ShapeDtypeStruct(gain_blocks.shape, gain_blocks.dtype),
        in_specs=[ANY],
        out_specs=ANY,
        scratch_shapes=[DMA(()), DMA((peers,)), DMA((peers,))],
        compiler_params=pltpu.CompilerParams(collective_id=8, has_side_effects=True),
        name="collect_gains",
    )(gain_blocks)


def block_scores(q, k, start, first):
    scores = lax.dot_general(q, k, (((1,), (1,)), ((), ())), preferred_element_type=F32)
    bent = jnp.tanh(scores * (HD ** (-0.5) / SOFT_CAP))
    rows, span = scores.shape
    key_at = lax.broadcasted_iota(jnp.int32, (rows, span), 1)
    row_at = lax.broadcasted_iota(jnp.int32, (rows, span), 0)
    allowed = (key_at + first >= start) & (key_at <= row_at + LMAX)
    return (bent, jnp.where(allowed, jnp.exp(SOFT_CAP * bent), 0.0))


def attend_kernel(q_ref, k_ref, v_ref, start_ref, out_ref, inv_ref):
    first = pl.program_id(0) * QBLK
    keys = pl.ds(pl.multiple_of(first, QBLK), LMAX + QBLK)
    unused_bent, exponent = block_scores(q_ref[...], k_ref[keys], start_ref[...], first)
    inverse = 1.0 / jnp.sum(exponent, axis=-1, keepdims=True)
    weights = (exponent * inverse).astype(BF16)
    out_ref[...] = jnp.dot(weights, v_ref[keys], preferred_element_type=F32).astype(BF16)
    inv_ref[...] = inverse


def attend(queries, key_rows, value_rows, starts):
    rows = queries.shape[0]
    span = key_rows.shape[0]
    row_spec = pl.BlockSpec((QBLK, HD), lambda i: (i, 0))
    one_spec = pl.BlockSpec((QBLK, 1), lambda i: (i, 0))
    all_spec = pl.BlockSpec((span, HD), lambda i: (0, 0))
    return pl.pallas_call(
        attend_kernel,
        out_shape=(
            jax.ShapeDtypeStruct((rows, HD), BF16),
            jax.ShapeDtypeStruct((rows, 1), F32),
        ),
        grid=(rows // QBLK,),
        in_specs=[row_spec, all_spec, all_spec, one_spec],
        out_specs=(row_spec, one_spec),
        compiler_params=pltpu.CompilerParams(vmem_limit_bytes=40 << 20),
        cost_estimate=cost(1),
        name="attend",
    )(queries, key_rows, value_rows, starts)


def attend_back_kernel(q_ref, k_ref, v_ref, start_ref, inv_ref, grad_ref, gq_ref, gk_ref, gv_ref):
    @pl.when(pl.program_id(0) == 0)
    def _():
        gk_ref[...] = jnp.zeros_like(gk_ref)
        gv_ref[...] = jnp.zeros_like(gv_ref)

    first = pl.program_id(0) * QBLK
    keys = pl.ds(pl.multiple_of(first, QBLK), LMAX + QBLK)
    q, k, v, grad = q_ref[...], k_ref[keys], v_ref[keys], grad_ref[...]
    bent, exponent = block_scores(q, k, start_ref[...], first)
    probability = exponent * inv_ref[...]
    grad_prob = lax.dot_general(grad, v, (((1,), (1,)), ((), ())), preferred_element_type=F32)
    inner = jnp.sum(probability * grad_prob, axis=-1, keepdims=True)
    grad_scores = (probability * (grad_prob - inner) * (1.0 - bent * bent)).astype(BF16)
    scale = HD ** (-0.5)
    gq_ref[...] = jnp.dot(grad_scores, k, preferred_element_type=F32) * scale
    over_rows = (((0,), (0,)), ((), ()))
    gk_ref[keys] += lax.dot_general(grad_scores, q, over_rows, preferred_element_type=F32) * scale
    gv_ref[keys] += lax.dot_general(
        probability.astype(BF16), grad, over_rows, preferred_element_type=F32
    )


def attend_back(queries, key_rows, value_rows, starts, inverse, grad):
    rows = queries.shape[0]
    span = key_rows.shape[0]
    row_spec = pl.BlockSpec((QBLK, HD), lambda i: (i, 0))
    one_spec = pl.BlockSpec((QBLK, 1), lambda i: (i, 0))
    all_spec = pl.BlockSpec((span, HD), lambda i: (0, 0))
    return pl.pallas_call(
        attend_back_kernel,
        out_shape=(
            jax.ShapeDtypeStruct((rows, HD), F32),
            jax.ShapeDtypeStruct((span, HD), F32),
            jax.ShapeDtypeStruct((span, HD), F32),
        ),
        grid=(rows // QBLK,),
        in_specs=[row_spec, all_spec, all_spec, one_spec, one_spec, row_spec],
        out_specs=(row_spec, all_spec, all_spec),
        compiler_params=pltpu.CompilerParams(vmem_limit_bytes=48 << 20),
        cost_estimate=cost(20),
        name="attend_back",
    )(queries, key_rows, value_rows, starts, inverse, grad)


def token_tables(seq_lengths, index_vec):
    count = seq_lengths.shape[0]
    order = jnp.arange(count, dtype=jnp.int32)
    seq_ends = jnp.sum(
        jnp.where(order[None, :] <= order[:, None], seq_lengths[None, :], 0), axis=1
    )
    after_end = index_vec[:, None] >= seq_ends[None, :]
    return index_vec - jnp.sum(jnp.where(after_end, seq_lengths[None, :], 0), axis=1)


def rms_parts(value):
    return lax.rsqrt(jnp.mean(value * value, axis=-1, keepdims=True) + EPSILON)


def rms_forward(value, gain_vec):
    return value * rms_parts(value) * (1.0 + gain_vec)


def rms_backward(value, gain_vec, grad):
    r = rms_parts(value)
    scaled = (1.0 + gain_vec) * grad
    inner = jnp.mean(value * scaled, axis=-1, keepdims=True)
    return (r * scaled - value * (r * r * r * inner), jnp.sum(grad * value * r, axis=0))


def rotate(value, cosine, sine_part):
    half_width = value.shape[-1] // 2
    first_half = value[..., :half_width]
    second_half = value[..., half_width:]
    return jnp.concatenate(
        [
            first_half * cosine - second_half * sine_part,
            second_half * cosine + first_half * sine_part,
        ],
        axis=-1,
    )


def contract_last(left_side, right_side):
    return lax.dot_general(
        left_side, right_side, (((1,), (1,)), ((), ())), preferred_element_type=F32
    )


def contract_first(left_side, right_side):
    return lax.dot_general(
        left_side, right_side, (((0,), (0,)), ((), ())), preferred_element_type=F32
    )


def matmul(left_side, right_side):
    return jnp.dot(left_side, right_side, preferred_element_type=F32)


def gelu_parts(gate):
    k0 = 0.7978845608028654
    k1 = 0.044715
    t = jnp.tanh(k0 * (gate + k1 * gate * gate * gate))
    value = 0.5 * gate * (1.0 + t)
    slope = 0.5 * (1.0 + t) + 0.5 * gate * (1.0 - t * t) * k0 * (1.0 + 3.0 * k1 * gate * gate)
    return (value, slope)


def local(tokens, attn_weights, mlp_weights, norm_gains, seq_lengths, cotangent):
    tok_rows, width = tokens.shape
    peers = lax.axis_size(AXIS)
    planes = peers // PLANE
    share = width // peers
    row_share = attn_weights.shape[0]
    ff = mlp_weights.shape[1] // 3
    ffc = ff // PLANE
    plane_rows = PLANE * tok_rows
    halo = LMAX
    across = [[p * PLANE + i for p in range(planes)] for i in range(PLANE)]
    sibling = [(i, i ^ 1) for i in range(peers)]
    to_next = [(i, i + PLANE) for i in range(peers - PLANE)]
    to_prev = [(i + PLANE, i) for i in range(peers - PLANE)]
    me = lax.axis_index(AXIS)
    is_even = (me % 2) == 0
    plane_start = (me // PLANE) * plane_rows

    def gather_across(value):
        return lax.all_gather(value, AXIS, axis=0, tiled=True, axis_index_groups=across)

    def scatter_across(value):
        part = lax.psum_scatter(
            value.astype(BF16), AXIS, scatter_dimension=0, tiled=True, axis_index_groups=across
        )
        return part.reshape(PLANE, -1, part.shape[1])

    gain_block = jnp.pad(norm_gains.astype(F32), ((0, 8 - 4), (0, -share % 128)))
    attn_part, gain_block = lax.optimization_barrier((spread_attn(attn_weights), gain_block))
    attn_cols = gather_across(attn_part.reshape(-1, 3 * HD))
    gu_part, gain_blocks = spread_gu(mlp_weights, gain_block, peers)
    gain_full = gain_blocks[:, :4, :share].transpose(1, 0, 2).reshape(4, width)
    inputs = tokens.astype(F32)
    down_part, normed = spread_down(
        mlp_weights, rms_forward(inputs, gain_full[0]).astype(BF16)
    )
    gu_cols = gather_across(gu_part.reshape(-1, 2 * ffc))
    down_cols = gather_across(down_part.reshape(-1, ffc))
    qkv_cols = attn_cols[:, : 2 * HD]
    out_cols = attn_cols[:, 2 * HD :]

    query_index = plane_start + jnp.arange(plane_rows, dtype=jnp.int32)
    position = token_tables(seq_lengths, query_index)
    starts = (jnp.arange(plane_rows, dtype=jnp.int32) + halo - position)[:, None]
    frequency = 10000.0 ** (-jnp.arange(HD // 2, dtype=F32) * 2.0 / HD)
    angles = position.astype(F32)[:, None] * frequency[None, :]
    cosine, sine_part = jnp.cos(angles), jnp.sin(angles)
    kv_cosine = jnp.where(is_even, cosine, 1.0)
    kv_sine = jnp.where(is_even, sine_part, 0.0)

    projected = matmul(normed, qkv_cols)
    queries = rotate(projected[:, :HD], cosine, sine_part).astype(BF16)
    kv_own = rotate(projected[:, HD:], kv_cosine, kv_sine).astype(BF16)
    kv_halo = lax.ppermute(kv_own[plane_rows - halo :], AXIS, to_next)
    kv_mine = jnp.concatenate([kv_halo, kv_own], axis=0)
    kv_other = lax.ppermute(kv_mine, AXIS, sibling)
    key_rows = jnp.where(is_even, kv_mine, kv_other)
    value_rows = jnp.where(is_even, kv_other, kv_mine)
    attended, inverse = attend(queries, key_rows, value_rows, starts)
    attn_proj = product_scatter([attended], [out_cols], [0], PLANE_STEP, 11)

    middle = inputs + rms_forward(attn_proj, gain_full[1])
    mid_low = gather_square(rms_forward(middle, gain_full[2]).astype(BF16), PLANE_STEP, 1)
    gate_up = matmul(mid_low, gu_cols)
    gate, up = gate_up[:, :ffc], gate_up[:, ffc:]
    gelu, slope = gelu_parts(gate)
    hidden = (gelu * up).astype(BF16)
    mlp_raw, grad_raw_low, down_grad = turn(
        hidden, down_cols, gain_full[3:4], cotangent, PLANE_STEP, 9
    )
    layer_output = (middle + rms_forward(mlp_raw, gain_full[3])).astype(BF16)

    grad_out = cotangent.astype(F32)
    gain_four = jnp.sum(grad_out * mlp_raw * rms_parts(mlp_raw), axis=0)
    down_term = scatter_across(down_grad)
    grad_hidden = matmul(grad_raw_low, down_cols)
    grad_gu = jnp.concatenate(
        [(slope * up * grad_hidden).astype(BF16), (gelu * grad_hidden).astype(BF16)], axis=1
    )
    gu_grad = contract_first(mid_low, grad_gu).astype(BF16)
    gu_grad, grad_gu = lax.optimization_barrier((gu_grad, grad_gu))
    gu_term = scatter_across(gu_grad)
    grad_normed_mid = product_scatter([grad_gu], [gu_cols], [0], PLANE_STEP, 10)
    grad_mid_part, gain_three = rms_backward(middle, gain_full[2], grad_normed_mid)
    grad_middle = grad_out + grad_mid_part

    grad_proj, gain_two = rms_backward(attn_proj, gain_full[1], grad_middle)
    grad_proj_own, down_term = lax.optimization_barrier((grad_proj.astype(BF16), down_term))
    grad_proj_low = gather_square(grad_proj_own, PLANE_STEP, 1)
    grad_att = matmul(grad_proj_low, out_cols).astype(BF16)
    grad_query, grad_keys, grad_values = attend_back(
        queries, key_rows, value_rows, starts, inverse, grad_att
    )
    grad_mine = jnp.where(is_even, grad_keys, grad_values)
    grad_give = jnp.where(is_even, grad_values, grad_keys).astype(BF16)
    grad_kv = grad_mine + lax.ppermute(grad_give, AXIS, sibling).astype(F32)
    grad_back = lax.ppermute(grad_kv[:halo].astype(BF16), AXIS, to_prev).astype(F32)
    down_term, grad_kv = lax.optimization_barrier((down_term, grad_kv))
    down_rows = collect(down_term, 1, 6)
    down_rows, grad_back = lax.optimization_barrier((down_rows, grad_back))
    grad_kv = grad_kv[halo:] + jnp.pad(grad_back, ((plane_rows - halo, 0), (0, 0)))
    grad_qkv = jnp.concatenate(
        [
            rotate(grad_query, cosine, -sine_part).astype(BF16),
            rotate(grad_kv, kv_cosine, -kv_sine).astype(BF16),
        ],
        axis=1,
    )
    attn_grad = jnp.concatenate(
        [contract_first(normed, grad_qkv), contract_first(grad_proj_low, attended)], axis=1
    ).astype(BF16)
    attn_grad, grad_qkv = lax.optimization_barrier((attn_grad, grad_qkv))
    attn_term = scatter_across(attn_grad)
    grad_normed = product_scatter([grad_qkv], [qkv_cols], [0], PLANE_STEP, 12)
    grad_in_part, gain_one = rms_backward(inputs, gain_full[0], grad_normed)
    grad_tokens = (grad_middle + grad_in_part).astype(BF16)

    gain_term = jnp.stack([gain_one, gain_two, gain_three, gain_four], axis=0)
    gain_term = gain_term.reshape(4, peers, share).transpose(1, 0, 2)
    gain_term = jnp.pad(gain_term, ((0, 0), (0, 8 - 4), (0, -share % 128)))
    gain_recv = collect_gains(gain_term)
    gu_term, gain_recv = lax.optimization_barrier((gu_term, gain_recv))
    gu_rows = collect(gu_term, 2, 13)
    grad_mlp = jnp.concatenate([gu_rows, down_rows], axis=1).astype(F32)
    grad_mlp, attn_term = lax.optimization_barrier((grad_mlp, attn_term))
    grad_attn = collect_attn(attn_term).astype(F32)
    grad_gains = jnp.sum(gain_recv[:, :4, :share], axis=0)
    return (layer_output, grad_tokens, grad_attn, grad_mlp, grad_gains)


def solution(mesh):
    return jax.shard_map(
        local,
        mesh=mesh,
        in_specs=(
            P("fsdp", None),
            P("fsdp", None),
            P("fsdp", None),
            P(None, "fsdp"),
            P(),
            P("fsdp", None),
        ),
        out_specs=(
            P("fsdp", None),
            P("fsdp", None),
            P("fsdp", None),
            P("fsdp", None),
            P(None, "fsdp"),
        ),
        check_vma=False,
    )
```

```python
from functools import partial

import jax
import jax.numpy as jnp
from jax import lax
from jax.experimental import pallas as pl
from jax.experimental.pallas import tpu as pltpu
from jax.sharding import PartitionSpec as P

H = 8
KVH = 4
HD = 256
LMAX = 1024
PLANE = 8
QBLK = 128

EPSILON = 1e-06
SOFT_CAP = 50.0
AXIS = "fsdp"
F32 = jnp.float32
BF16 = jnp.bfloat16
MESH = pl.DeviceIdType.MESH
ANY = pl.BlockSpec(memory_space=pl.ANY)
VMEM = pl.BlockSpec(memory_space=pltpu.VMEM)
DMA = pltpu.SemaphoreType.DMA


def flip(index, step):
    return index + step - 2 * step * ((index // step) % 2)


PLANE_STEP = 4


def partner(index, bits, step):
    for bit, by in ((1, 1), (2, 2), (4, step)):
        if bits & bit:
            index = flip(index, by)
    return index


def place(device, step):
    return device % 4 + 4 * ((device // step) % 2)


def greet(peers):
    barrier = pltpu.get_barrier_semaphore()
    for peer in peers:
        pl.semaphore_signal(barrier, inc=1, device_id=(peer,), device_id_type=MESH)
    pl.semaphore_wait(barrier, len(peers))


class Copies:
    def __init__(self, send_sem, recv_sem):
        self.send_sem, self.recv_sem, self.made = send_sem, recv_sem, []

    def start(self, source, target, device):
        slot = len(self.made)
        copy = pltpu.make_async_remote_copy(
            src_ref=source,
            dst_ref=target,
            send_sem=self.send_sem.at[slot],
            recv_sem=self.recv_sem.at[slot],
            device_id=(device,),
            device_id_type=MESH,
        )
        copy.start()
        self.made.append(copy)
        return copy

    def sent(self):
        for copy in self.made:
            copy.wait_send()


def band(index, size):
    return pl.ds(pl.multiple_of(index * size, 8), size)


def lanes(index, size):
    return pl.ds(pl.multiple_of(index * size, 128), size)


def gather_steps(block_ref, full_ref, copies, own_sem, step):
    rows, width = block_ref.shape
    half = width // 2
    me = lax.axis_index(AXIS)
    sib, xn, yn = flip(me, 1), flip(me, 2), flip(me, step)
    diag = flip(xn, step)

    def at(device, side):
        return full_ref.at[band(place(device, step), rows), pl.ds(side * half, half)]

    def mine(side):
        return block_ref.at[:, pl.ds(side * half, half)]

    own_rows = full_ref.at[band(place(me, step), rows)]
    xa = copies.start(mine(0), at(me, 0), xn)
    ya = copies.start(mine(1), at(me, 1), yn)
    xb = copies.start(mine(1), at(me, 1), xn)
    yb = copies.start(mine(0), at(me, 0), yn)
    arriving = [copies.start(block_ref, own_rows, sib)]
    own = pltpu.make_async_copy(block_ref, own_rows, own_sem)
    own.start()

    def finish(on_rows=None):
        def to_sibling(device, side):
            arriving.append(copies.start(at(device, side), at(device, side), sib))

        def arrived(first, last, *devices):
            for copy in arriving[first:last]:
                copy.wait_recv()
            for device in devices:
                on_rows(device)

        if on_rows is not None:
            own.wait()
            arrived(0, 1, me)
        xa.wait_recv()
        yc = copies.start(at(xn, 0), at(xn, 0), yn)
        to_sibling(xn, 0)
        ya.wait_recv()
        xc = copies.start(at(yn, 1), at(yn, 1), xn)
        to_sibling(yn, 1)
        xb.wait_recv()
        to_sibling(xn, 1)
        yb.wait_recv()
        to_sibling(yn, 0)
        if on_rows is not None:
            arrived(1, 5, xn, yn)
        yc.wait_recv()
        to_sibling(diag, 0)
        xc.wait_recv()
        to_sibling(diag, 1)
        if on_rows is not None:
            arrived(5, 7, diag)
        else:
            arrived(0, 7)
            own.wait()

    return finish


GATHER_COPIES = 13


def cost(microseconds):
    return pl.CostEstimate(
        flops=int(microseconds * 1e7), transcendentals=0, bytes_accessed=int(microseconds * 3e4)
    )


def gather_kernel(block_ref, full_ref, own_sem, send_sem, recv_sem, *, step):
    me = lax.axis_index(AXIS)
    greet((flip(me, 1), flip(me, 2), flip(me, step)))
    copies = Copies(send_sem, recv_sem)
    gather_steps(block_ref, full_ref, copies, own_sem, step)()
    copies.sent()


def gather_square(block, step, collective_id):
    rows, width = block.shape
    return pl.pallas_call(
        partial(gather_kernel, step=step),
        out_shape=jax.ShapeDtypeStruct((PLANE * rows, width), block.dtype),
        in_specs=[ANY],
        out_specs=ANY,
        scratch_shapes=[DMA(()), DMA((GATHER_COPIES,)), DMA((GATHER_COPIES,))],
        compiler_params=pltpu.CompilerParams(collective_id=collective_id, has_side_effects=True),
        cost_estimate=cost(42),
        name="gather_square",
    )(block)


W_TILES = 3


def product_scatter_steps(
    left_refs, right_refs, left_bufs, right_bufs, buffers, load_sem, copies, offsets, step, beside=None
):
    both, got, ra, rb, ra2, rb2 = buffers
    pairs = len(left_refs)
    rows, width = got.shape[1:]
    half = width // 2
    tile = width // W_TILES
    chunk = 16
    me = lax.axis_index(AXIS)
    core = me % 2
    sib, xn, yn = flip(me, 1), flip(me, 2), flip(me, step)
    order = (flip(xn, step), xn, yn, me)
    first, second = pl.ds(0, half), pl.ds(half, half)

    def chip_rows(device):
        return pl.ds(pl.multiple_of((place(device, step) // 2) * 2 * rows, 16), 2 * rows)

    def right_load(j, t):
        r = pl.ds(t * tile, tile)
        source = right_refs[j].at[r, pl.ds(offsets[j], right_bufs[j].shape[1])]
        return pltpu.make_async_copy(source, right_bufs[j].at[r], load_sem.at[j, t])

    def left_load(j, i):
        r = chip_rows(order[i])
        return pltpu.make_async_copy(
            left_refs[j].at[r], left_bufs[j].at[r], load_sem.at[j, W_TILES + i]
        )

    for j in range(pairs):
        left_load(j, 0).start()
    for t in range(W_TILES):
        for j in range(pairs):
            right_load(j, t).start()
    for i in range(1, 4):
        for j in range(pairs):
            left_load(j, i).start()
    if beside is not None:
        beside[0]()
    greet((sib, xn, yn))

    def product(i):
        r = chip_rows(order[i])
        for j in range(pairs):
            left_load(j, i).wait()

        def columns(w):
            total = None
            for j in range(pairs):
                term = contract_last(left_bufs[j][r], right_bufs[j][w])
                total = term if total is None else total + term
            both[i, :, w] = total.astype(BF16)

        if i == 0:
            for t in range(W_TILES):
                for j in range(pairs):
                    right_load(j, t).wait()
                columns(pl.ds(t * tile, tile))
        else:

            @pl.loop(0, W_TILES)
            def _(t):
                columns(pl.ds(pl.multiple_of(t * tile, tile), tile))

    def mine(i, cols=None):
        if cols is None:
            return both.at[i, band(core, rows)]
        return both.at[i, band(core, rows), cols]

    def add(total, other):
        @pl.loop(0, rows // chunk)
        def _(k):
            r = pl.ds(pl.multiple_of(k * chunk, chunk), chunk)
            total[r] = (total[r].astype(F32) + other[r].astype(F32)).astype(total.dtype)

    def make(i):
        product(i)
        crossing = copies.start(both.at[i, band(1 - core, rows)], got.at[i], sib)
        crossing.wait_recv()
        add(mine(i), got.at[i])

    make(0)
    x0 = copies.start(mine(0, first), ra.at[0], xn)
    y0 = copies.start(mine(0, second), rb.at[0], yn)
    make(1)
    x1 = copies.start(mine(1, first), ra.at[1], xn)
    make(2)
    y1 = copies.start(mine(2, second), rb.at[1], yn)
    x0.wait_recv()
    add(mine(2, first), ra.at[0])
    y2 = copies.start(mine(2, first), ra2, yn)
    y0.wait_recv()
    add(mine(1, second), rb.at[0])
    x2 = copies.start(mine(1, second), rb2, xn)
    make(3)
    if beside is not None:
        beside[1]()
    for copy in (x1, y1, y2, x2):
        copy.wait_recv()
    own = mine(3)

    def summed(r):
        return jnp.concatenate(
            [
                own[r, first].astype(F32) + ra[1, r].astype(F32) + ra2[r].astype(F32),
                own[r, second].astype(F32) + rb[1, r].astype(F32) + rb2[r].astype(F32),
            ],
            axis=1,
        )

    return summed


ROW_CHUNK = 16


def product_scatter_kernel(*refs, pairs, offsets, step):
    left_refs, right_refs, out_ref = refs[:pairs], refs[pairs : 2 * pairs], refs[2 * pairs]
    left_bufs = refs[2 * pairs + 1 : 3 * pairs + 1]
    right_bufs = refs[3 * pairs + 1 : 4 * pairs + 1]
    buffers, (load_sem, send_sem, recv_sem) = refs[4 * pairs + 1 : -3], refs[-3:]
    copies = Copies(send_sem, recv_sem)
    summed = product_scatter_steps(
        left_refs, right_refs, left_bufs, right_bufs, buffers, load_sem, copies, offsets, step
    )

    @pl.loop(0, out_ref.shape[0] // ROW_CHUNK)
    def _(k):
        r = pl.ds(pl.multiple_of(k * ROW_CHUNK, ROW_CHUNK), ROW_CHUNK)
        out_ref[r] = summed(r)

    copies.sent()


def scatter_buffers(rows, width):
    half = width // 2
    return [
        pltpu.VMEM((4, 2 * rows, width), BF16),
        pltpu.VMEM((4, rows, width), BF16),
        pltpu.VMEM((2, rows, half), BF16),
        pltpu.VMEM((2, rows, half), BF16),
        pltpu.VMEM((rows, half), BF16),
        pltpu.VMEM((rows, half), BF16),
    ]


def product_scatter(lefts, rights, offsets, step, collective_id):
    pairs = len(lefts)
    rows, width = lefts[0].shape[0] // PLANE, rights[0].shape[0]
    return pl.pallas_call(
        partial(product_scatter_kernel, pairs=pairs, offsets=offsets, step=step),
        out_shape=jax.ShapeDtypeStruct((rows, width), F32),
        in_specs=[ANY] * (2 * pairs),
        out_specs=VMEM,
        scratch_shapes=[
            *[pltpu.VMEM(value.shape, BF16) for value in lefts],
            *[pltpu.VMEM((width, value.shape[1]), BF16) for value in lefts],
            *scatter_buffers(rows, width),
            DMA((pairs, W_TILES + 4)),
            DMA((10,)),
            DMA((10,)),
        ],
        compiler_params=pltpu.CompilerParams(
            collective_id=collective_id, has_side_effects=True, vmem_limit_bytes=56 << 20
        ),
        cost_estimate=cost(50),
        name="product_scatter",
    )(*lefts, *rights)


BACK_TILE = 384


def back_kernel(*refs, pairs, offsets, step):
    left_refs, right_refs, rows_ref = refs[:pairs], refs[pairs : 2 * pairs], refs[2 * pairs]
    out_ref, term_ref = refs[2 * pairs + 1 : 2 * pairs + 3]
    scratch = refs[2 * pairs + 3 :]
    left_bufs, right_bufs = scratch[:pairs], scratch[pairs : 2 * pairs]
    rows_buf, stage = scratch[2 * pairs : 2 * pairs + 2]
    buffers = scratch[2 * pairs + 2 : -5]
    load_sem, rows_sem, store_sem, send_sem, recv_sem = scratch[-5:]
    copies = Copies(send_sem, recv_sem)
    rows_load = pltpu.make_async_copy(rows_ref, rows_buf, rows_sem)
    tiles = rows_ref.shape[1] // BACK_TILE
    width = left_refs[0].shape[1]

    def store(t):
        return pltpu.make_async_copy(
            stage.at[t % 2],
            term_ref.at[pl.ds(pl.multiple_of(t * BACK_TILE, 16), BACK_TILE)],
            store_sem.at[t % 2],
        )

    def beside():
        rows_load.wait()

        @pl.loop(0, tiles)
        def _(t):
            @pl.when(t >= 2)
            def _():
                store(t - 2).wait()

            columns = rows_buf[:, pl.ds(pl.multiple_of(t * BACK_TILE, BACK_TILE), BACK_TILE)]
            for j in range(pairs):
                term = contract_first(columns, left_bufs[j][...])
                stage[t % 2, :, pl.ds(j * width, width)] = term.astype(BF16)
            store(t).start()

    def start_rows():
        rows_load.start()

    summed = product_scatter_steps(
        left_refs,
        right_refs,
        left_bufs,
        right_bufs,
        buffers,
        load_sem,
        copies,
        offsets,
        step,
        (start_rows, beside),
    )

    @pl.loop(0, out_ref.shape[0] // ROW_CHUNK)
    def _(k):
        r = pl.ds(pl.multiple_of(k * ROW_CHUNK, ROW_CHUNK), ROW_CHUNK)
        out_ref[r] = summed(r)

    for t in range(tiles - 2, tiles):
        store(t).wait()
    copies.sent()


def product_scatter_back(lefts, rights, offsets, rows, step, collective_id):
    pairs = len(lefts)
    count, width = lefts[0].shape[0] // PLANE, rights[0].shape[0]
    columns = sum(value.shape[1] for value in lefts)
    return pl.pallas_call(
        partial(back_kernel, pairs=pairs, offsets=offsets, step=step),
        out_shape=(
            jax.ShapeDtypeStruct((count, width), F32),
            jax.ShapeDtypeStruct((rows.shape[1], columns), BF16),
        ),
        in_specs=[ANY] * (2 * pairs + 1),
        out_specs=(VMEM, ANY),
        scratch_shapes=[
            *[pltpu.VMEM(value.shape, BF16) for value in lefts],
            *[pltpu.VMEM((width, value.shape[1]), BF16) for value in lefts],
            pltpu.VMEM(rows.shape, BF16),
            pltpu.VMEM((2, BACK_TILE, columns), BF16),
            *scatter_buffers(count, width),
            DMA((pairs, W_TILES + 4)),
            DMA(()),
            DMA((2,)),
            DMA((10,)),
            DMA((10,)),
        ],
        compiler_params=pltpu.CompilerParams(
            collective_id=collective_id, has_side_effects=True, vmem_limit_bytes=62 << 20
        ),
        cost_estimate=cost(60),
        name="product_scatter_back",
    )(*lefts, *rights, rows)


TURN_TILE = 768


def turn_kernel(
    left_ref, right_ref, gain_ref, grad_ref, raw_ref, full_ref, term_ref, *refs, step
):
    left_buf, right_buf, gathered, total, grad_own = refs[:5]
    buffers, (load_sem, own_sem, store_sem, send_sem, recv_sem) = refs[5:-5], refs[-5:]
    rows, width = grad_ref.shape
    copies = Copies(send_sem, recv_sem)
    summed = product_scatter_steps(
        [left_ref], [right_ref], [left_buf], [right_buf], buffers, load_sem, copies, [0], step
    )
    gain = gain_ref[...]

    @pl.loop(0, rows // ROW_CHUNK)
    def _(k):
        r = pl.ds(pl.multiple_of(k * ROW_CHUNK, ROW_CHUNK), ROW_CHUNK)
        value = summed(r)
        raw_ref[r] = value
        scale = lax.rsqrt(jnp.mean(value * value, axis=1, keepdims=True) + EPSILON)
        scaled = (1.0 + gain) * grad_ref[r].astype(F32)
        inner = jnp.mean(value * scaled, axis=1, keepdims=True)
        grad_own[r] = (scale * scaled - value * (scale * scale * scale * inner)).astype(BF16)

    stores = []

    def on_rows(device):
        slot = len(stores)
        r = pl.ds(pl.multiple_of((place(device, step) // 2) * 2 * rows, 16), 2 * rows)
        store = pltpu.make_async_copy(gathered.at[r], full_ref.at[r], store_sem.at[slot])
        store.start()
        stores.append(store)
        right = left_buf[r]

        @pl.loop(0, width // TURN_TILE)
        def _(t):
            w = pl.ds(pl.multiple_of(t * TURN_TILE, TURN_TILE), TURN_TILE)
            term = contract_first(gathered[r, w], right)
            if slot == 0:
                total[w] = term
            elif slot < 3:
                total[w] += term
            else:
                right_buf[w] = (total[w] + term).astype(BF16)
                pltpu.make_async_copy(right_buf.at[w], term_ref.at[w], store_sem.at[4]).start()

    gather_steps(grad_own, gathered, copies, own_sem, step)(on_rows)
    pltpu.make_async_copy(right_buf, term_ref, store_sem.at[4]).wait()
    for store in stores:
        store.wait()
    copies.sent()


def turn(left, right, gain_row, grad, step, collective_id):
    rows, width = grad.shape
    count = 10 + GATHER_COPIES
    return pl.pallas_call(
        partial(turn_kernel, step=step),
        out_shape=(
            jax.ShapeDtypeStruct((rows, width), F32),
            jax.ShapeDtypeStruct((PLANE * rows, width), BF16),
            jax.ShapeDtypeStruct((width, left.shape[1]), BF16),
        ),
        in_specs=[ANY, ANY, VMEM, VMEM],
        out_specs=(VMEM, ANY, ANY),
        scratch_shapes=[
            pltpu.VMEM(left.shape, BF16),
            pltpu.VMEM(right.shape, BF16),
            pltpu.VMEM((PLANE * rows, width), BF16),
            pltpu.VMEM((width, left.shape[1]), F32),
            pltpu.VMEM((rows, width), BF16),
            *scatter_buffers(rows, width),
            DMA((1, W_TILES + 4)),
            DMA(()),
            DMA((5,)),
            DMA((count,)),
            DMA((count,)),
        ],
        compiler_params=pltpu.CompilerParams(
            collective_id=collective_id, has_side_effects=True, vmem_limit_bytes=60 << 20
        ),
        cost_estimate=cost(50),
        name="turn",
    )(left, right, gain_row, grad)


def attn_columns(column):
    query_width = H * HD
    key_offset = query_width + (column % 2) * KVH * HD + (column // 2) * HD
    return (column * HD, key_offset, query_width + 2 * KVH * HD + column * HD)


def greet_all(peers):
    me = lax.axis_index(AXIS)
    barrier = pltpu.get_barrier_semaphore()

    @pl.loop(1, peers)
    def _(k):
        device = lax.rem(me + k, peers)
        pl.semaphore_signal(barrier, inc=1, device_id=(device,), device_id_type=MESH)

    pl.semaphore_wait(barrier, peers - 1)


def exchange_all(source_of, target_ref, send_sem, recv_sem):
    peers = target_ref.shape[0]
    me = lax.axis_index(AXIS)

    def copy(k):
        device = lax.rem(me + k, peers)
        return pltpu.make_async_remote_copy(
            src_ref=source_of(device),
            dst_ref=target_ref.at[me],
            send_sem=send_sem.at[k],
            recv_sem=recv_sem.at[k],
            device_id=(device,),
            device_id_type=MESH,
        )

    @pl.loop(1, peers)
    def _(k):
        copy(k).start()

    def finish():
        @pl.loop(1, peers)
        def _(k):
            copy(k).wait()

    return finish


ORDER = (6, 7, 2, 3, 4, 5, 1)


def swap_steps(pieces_of, targets, copies, own_sem, step):
    me = lax.axis_index(AXIS)
    moved = []
    for bits in ORDER:
        peer = partner(me, bits, step)
        for source, target in zip(pieces_of(place(peer, step)), targets):
            moved.append(copies.start(source, target, peer))
    owns = []
    for slot, (source, target) in enumerate(zip(pieces_of(place(me, step)), targets)):
        own = pltpu.make_async_copy(source, target, own_sem.at[slot])
        own.start()
        owns.append(own)

    def finish():
        for own in owns:
            own.wait()
        for copy in moved:
            copy.wait_recv()

    return finish


def square(step):
    me = lax.axis_index(AXIS)
    return [partner(me, bits, step) for bits in ORDER]


def wide(offset):
    return pl.ds(pl.multiple_of(offset, 128), HD)


def spread_attn_kernel(weights_ref, part_ref, own_sem, send_sem, recv_sem):
    here = place(lax.axis_index(AXIS), PLANE_STEP)
    greet(square(PLANE_STEP))
    copies = Copies(send_sem, recv_sem)
    swap_steps(
        lambda c: [weights_ref.at[:, wide(offset)] for offset in attn_columns(c)],
        [part_ref.at[here, :, pl.ds(slot * HD, HD)] for slot in range(3)],
        copies,
        own_sem,
        PLANE_STEP,
    )()
    copies.sent()


def spread_attn(weights):
    rows = weights.shape[0]
    return pl.pallas_call(
        spread_attn_kernel,
        out_shape=jax.ShapeDtypeStruct((PLANE, rows, 3 * HD), BF16),
        in_specs=[ANY],
        out_specs=ANY,
        scratch_shapes=[DMA((3,)), DMA((21,)), DMA((21,))],
        compiler_params=pltpu.CompilerParams(collective_id=3, has_side_effects=True),
        name="spread_attn",
    )(weights)


def spread_gu_kernel(
    weights_ref, gain_ref, gu_ref, gains_ref, own_sem, send_sem, recv_sem, gain_send, gain_recv
):
    peers = gains_ref.shape[0]
    ffc = gu_ref.shape[2] // 2
    me = lax.axis_index(AXIS)
    here = place(me, PLANE_STEP)
    greet_all(peers)
    gains_done = exchange_all(lambda device: gain_ref, gains_ref, gain_send, gain_recv)
    own = pltpu.make_async_copy(gain_ref, gains_ref.at[me], own_sem.at[2])
    own.start()
    copies = Copies(send_sem, recv_sem)
    swap_steps(
        lambda c: [weights_ref.at[:, lanes(slot * PLANE + c, ffc)] for slot in range(2)],
        [gu_ref.at[here, :, pl.ds(slot * ffc, ffc)] for slot in range(2)],
        copies,
        own_sem,
        PLANE_STEP,
    )()
    own.wait()
    gains_done()
    copies.sent()


def spread_gu(weights, gain_block, peers):
    rows = weights.shape[0]
    ffc = weights.shape[1] // 3 // PLANE
    return pl.pallas_call(
        spread_gu_kernel,
        out_shape=(
            jax.ShapeDtypeStruct((PLANE, rows, 2 * ffc), BF16),
            jax.ShapeDtypeStruct((peers,) + gain_block.shape, gain_block.dtype),
        ),
        in_specs=[ANY, ANY],
        out_specs=(ANY, ANY),
        scratch_shapes=[DMA((3,)), DMA((14,)), DMA((14,)), DMA((peers,)), DMA((peers,))],
        compiler_params=pltpu.CompilerParams(collective_id=4, has_side_effects=True),
        cost_estimate=cost(38),
        name="spread_gu",
    )(weights, gain_block)


def spread_down_kernel(weights_ref, block_ref, down_ref, full_ref, own_sem, send_sem, recv_sem):
    ffc = down_ref.shape[2]
    me = lax.axis_index(AXIS)
    greet(square(PLANE_STEP))
    copies = Copies(send_sem, recv_sem)
    gathered = gather_steps(block_ref, full_ref, copies, own_sem.at[1], PLANE_STEP)
    spread = swap_steps(
        lambda c: [weights_ref.at[:, lanes(2 * PLANE + c, ffc)]],
        [down_ref.at[place(me, PLANE_STEP)]],
        copies,
        own_sem,
        PLANE_STEP,
    )
    gathered()
    spread()
    copies.sent()


def spread_down(weights, block):
    rows = weights.shape[0]
    ffc = weights.shape[1] // 3 // PLANE
    count = GATHER_COPIES + 7
    return pl.pallas_call(
        spread_down_kernel,
        out_shape=(
            jax.ShapeDtypeStruct((PLANE, rows, ffc), BF16),
            jax.ShapeDtypeStruct((PLANE * block.shape[0], block.shape[1]), BF16),
        ),
        in_specs=[ANY, ANY],
        out_specs=(ANY, ANY),
        scratch_shapes=[DMA((2,)), DMA((count,)), DMA((count,))],
        compiler_params=pltpu.CompilerParams(collective_id=5, has_side_effects=True),
        cost_estimate=cost(1),
        name="spread_down",
    )(weights, block)


def collect_kernel(term_ref, rows_ref, own_sem, send_sem, recv_sem):
    here = place(lax.axis_index(AXIS), PLANE_STEP)
    count = own_sem.shape[0]
    ffc = term_ref.shape[2] // count
    greet(square(PLANE_STEP))
    copies = Copies(send_sem, recv_sem)
    swap_steps(
        lambda c: [term_ref.at[c, :, pl.ds(slot * ffc, ffc)] for slot in range(count)],
        [rows_ref.at[:, lanes(slot * PLANE + here, ffc)] for slot in range(count)],
        copies,
        own_sem,
        PLANE_STEP,
    )()
    copies.sent()


def collect(term, count, collective_id):
    rows, columns = term.shape[1:]
    return pl.pallas_call(
        collect_kernel,
        out_shape=jax.ShapeDtypeStruct((rows, PLANE * columns), BF16),
        in_specs=[ANY],
        out_specs=ANY,
        scratch_shapes=[DMA((count,)), DMA((7 * count,)), DMA((7 * count,))],
        compiler_params=pltpu.CompilerParams(collective_id=collective_id, has_side_effects=True),
        cost_estimate=cost(0.1),
        name="collect",
    )(term)


def collect_attn_kernel(term_ref, rows_ref, own_sem, send_sem, recv_sem):
    here = place(lax.axis_index(AXIS), PLANE_STEP)
    greet(square(PLANE_STEP))
    copies = Copies(send_sem, recv_sem)
    swap_steps(
        lambda c: [term_ref.at[c, :, pl.ds(slot * HD, HD)] for slot in range(3)],
        [rows_ref.at[:, wide(offset)] for offset in attn_columns(here)],
        copies,
        own_sem,
        PLANE_STEP,
    )()
    copies.sent()


def collect_attn(term):
    rows = term.shape[1]
    return pl.pallas_call(
        collect_attn_kernel,
        out_shape=jax.ShapeDtypeStruct((rows, PLANE * 3 * HD), BF16),
        in_specs=[ANY],
        out_specs=ANY,
        scratch_shapes=[DMA((3,)), DMA((21,)), DMA((21,))],
        compiler_params=pltpu.CompilerParams(collective_id=7, has_side_effects=True),
        name="collect_attn",
    )(term)


def collect_gains_kernel(gain_ref, gains_ref, own_sem, gain_send, gain_recv):
    me = lax.axis_index(AXIS)
    greet_all(gain_ref.shape[0])
    done = exchange_all(lambda device: gain_ref.at[device], gains_ref, gain_send, gain_recv)
    own = pltpu.make_async_copy(gain_ref.at[me], gains_ref.at[me], own_sem)
    own.start()
    own.wait()
    done()


def collect_gains(gain_blocks):
    peers = gain_blocks.shape[0]
    return pl.pallas_call(
        collect_gains_kernel,
        out_shape=jax.ShapeDtypeStruct(gain_blocks.shape, gain_blocks.dtype),
        in_specs=[ANY],
        out_specs=ANY,
        scratch_shapes=[DMA(()), DMA((peers,)), DMA((peers,))],
        compiler_params=pltpu.CompilerParams(collective_id=8, has_side_effects=True),
        name="collect_gains",
    )(gain_blocks)


def block_scores(q, k, start, first):
    scores = lax.dot_general(q, k, (((1,), (1,)), ((), ())), preferred_element_type=F32)
    bent = jnp.tanh(scores * (HD ** (-0.5) / SOFT_CAP))
    rows, span = scores.shape
    key_at = lax.broadcasted_iota(jnp.int32, (rows, span), 1)
    row_at = lax.broadcasted_iota(jnp.int32, (rows, span), 0)
    allowed = (key_at + first >= start) & (key_at <= row_at + LMAX)
    return (bent, jnp.where(allowed, jnp.exp(SOFT_CAP * bent), 0.0))


def attend_kernel(q_ref, k_ref, v_ref, start_ref, out_ref, inv_ref):
    first = pl.program_id(0) * QBLK
    keys = pl.ds(pl.multiple_of(first, QBLK), LMAX + QBLK)
    unused_bent, exponent = block_scores(q_ref[...], k_ref[keys], start_ref[...], first)
    inverse = 1.0 / jnp.sum(exponent, axis=-1, keepdims=True)
    weights = (exponent * inverse).astype(BF16)
    out_ref[...] = jnp.dot(weights, v_ref[keys], preferred_element_type=F32).astype(BF16)
    inv_ref[...] = inverse


def attend(queries, key_rows, value_rows, starts):
    rows = queries.shape[0]
    span = key_rows.shape[0]
    row_spec = pl.BlockSpec((QBLK, HD), lambda i: (i, 0))
    one_spec = pl.BlockSpec((QBLK, 1), lambda i: (i, 0))
    all_spec = pl.BlockSpec((span, HD), lambda i: (0, 0))
    return pl.pallas_call(
        attend_kernel,
        out_shape=(
            jax.ShapeDtypeStruct((rows, HD), BF16),
            jax.ShapeDtypeStruct((rows, 1), F32),
        ),
        grid=(rows // QBLK,),
        in_specs=[row_spec, all_spec, all_spec, one_spec],
        out_specs=(row_spec, one_spec),
        compiler_params=pltpu.CompilerParams(vmem_limit_bytes=40 << 20),
        cost_estimate=cost(1),
        name="attend",
    )(queries, key_rows, value_rows, starts)


def attend_back_kernel(q_ref, k_ref, v_ref, start_ref, inv_ref, grad_ref, gq_ref, gk_ref, gv_ref):
    @pl.when(pl.program_id(0) == 0)
    def _():
        gk_ref[...] = jnp.zeros_like(gk_ref)
        gv_ref[...] = jnp.zeros_like(gv_ref)

    first = pl.program_id(0) * QBLK
    keys = pl.ds(pl.multiple_of(first, QBLK), LMAX + QBLK)
    q, k, v, grad = q_ref[...], k_ref[keys], v_ref[keys], grad_ref[...]
    bent, exponent = block_scores(q, k, start_ref[...], first)
    probability = exponent * inv_ref[...]
    grad_prob = lax.dot_general(grad, v, (((1,), (1,)), ((), ())), preferred_element_type=F32)
    inner = jnp.sum(probability * grad_prob, axis=-1, keepdims=True)
    grad_scores = (probability * (grad_prob - inner) * (1.0 - bent * bent)).astype(BF16)
    scale = HD ** (-0.5)
    gq_ref[...] = jnp.dot(grad_scores, k, preferred_element_type=F32) * scale
    over_rows = (((0,), (0,)), ((), ()))
    gk_ref[keys] += lax.dot_general(grad_scores, q, over_rows, preferred_element_type=F32) * scale
    gv_ref[keys] += lax.dot_general(
        probability.astype(BF16), grad, over_rows, preferred_element_type=F32
    )


def attend_back(queries, key_rows, value_rows, starts, inverse, grad):
    rows = queries.shape[0]
    span = key_rows.shape[0]
    row_spec = pl.BlockSpec((QBLK, HD), lambda i: (i, 0))
    one_spec = pl.BlockSpec((QBLK, 1), lambda i: (i, 0))
    all_spec = pl.BlockSpec((span, HD), lambda i: (0, 0))
    return pl.pallas_call(
        attend_back_kernel,
        out_shape=(
            jax.ShapeDtypeStruct((rows, HD), F32),
            jax.ShapeDtypeStruct((span, HD), F32),
            jax.ShapeDtypeStruct((span, HD), F32),
        ),
        grid=(rows // QBLK,),
        in_specs=[row_spec, all_spec, all_spec, one_spec, one_spec, row_spec],
        out_specs=(row_spec, all_spec, all_spec),
        compiler_params=pltpu.CompilerParams(vmem_limit_bytes=48 << 20),
        cost_estimate=cost(20),
        name="attend_back",
    )(queries, key_rows, value_rows, starts, inverse, grad)


def token_tables(seq_lengths, index_vec):
    count = seq_lengths.shape[0]
    order = jnp.arange(count, dtype=jnp.int32)
    seq_ends = jnp.sum(
        jnp.where(order[None, :] <= order[:, None], seq_lengths[None, :], 0), axis=1
    )
    after_end = index_vec[:, None] >= seq_ends[None, :]
    return index_vec - jnp.sum(jnp.where(after_end, seq_lengths[None, :], 0), axis=1)


def rms_parts(value):
    return lax.rsqrt(jnp.mean(value * value, axis=-1, keepdims=True) + EPSILON)


def rms_forward(value, gain_vec):
    return value * rms_parts(value) * (1.0 + gain_vec)


def rms_backward(value, gain_vec, grad):
    r = rms_parts(value)
    scaled = (1.0 + gain_vec) * grad
    inner = jnp.mean(value * scaled, axis=-1, keepdims=True)
    return (r * scaled - value * (r * r * r * inner), jnp.sum(grad * value * r, axis=0))


def rotate(value, cosine, sine_part):
    half_width = value.shape[-1] // 2
    first_half = value[..., :half_width]
    second_half = value[..., half_width:]
    return jnp.concatenate(
        [
            first_half * cosine - second_half * sine_part,
            second_half * cosine + first_half * sine_part,
        ],
        axis=-1,
    )


def contract_last(left_side, right_side):
    return lax.dot_general(
        left_side, right_side, (((1,), (1,)), ((), ())), preferred_element_type=F32
    )


def contract_first(left_side, right_side):
    return lax.dot_general(
        left_side, right_side, (((0,), (0,)), ((), ())), preferred_element_type=F32
    )


def matmul(left_side, right_side):
    return jnp.dot(left_side, right_side, preferred_element_type=F32)


def gelu_parts(gate):
    k0 = 0.7978845608028654
    k1 = 0.044715
    t = jnp.tanh(k0 * (gate + k1 * gate * gate * gate))
    value = 0.5 * gate * (1.0 + t)
    slope = 0.5 * (1.0 + t) + 0.5 * gate * (1.0 - t * t) * k0 * (1.0 + 3.0 * k1 * gate * gate)
    return (value, slope)


def local(tokens, attn_weights, mlp_weights, norm_gains, seq_lengths, cotangent):
    tok_rows, width = tokens.shape
    peers = lax.axis_size(AXIS)
    planes = peers // PLANE
    share = width // peers
    row_share = attn_weights.shape[0]
    ff = mlp_weights.shape[1] // 3
    ffc = ff // PLANE
    plane_rows = PLANE * tok_rows
    halo = LMAX
    across = [[p * PLANE + i for p in range(planes)] for i in range(PLANE)]
    sibling = [(i, i ^ 1) for i in range(peers)]
    to_next = [(i, i + PLANE) for i in range(peers - PLANE)]
    to_prev = [(i + PLANE, i) for i in range(peers - PLANE)]
    me = lax.axis_index(AXIS)
    is_even = (me % 2) == 0
    plane_start = (me // PLANE) * plane_rows

    def gather_across(value):
        return lax.all_gather(value, AXIS, axis=0, tiled=True, axis_index_groups=across)

    def scatter_across(value):
        part = lax.psum_scatter(
            value.astype(BF16), AXIS, scatter_dimension=0, tiled=True, axis_index_groups=across
        )
        return part.reshape(PLANE, -1, part.shape[1])

    gain_block = jnp.pad(norm_gains.astype(F32), ((0, 8 - 4), (0, -share % 128)))
    attn_part, gain_block = lax.optimization_barrier((spread_attn(attn_weights), gain_block))
    attn_cols = gather_across(attn_part.reshape(-1, 3 * HD))
    gu_part, gain_blocks = spread_gu(mlp_weights, gain_block, peers)
    gain_full = gain_blocks[:, :4, :share].transpose(1, 0, 2).reshape(4, width)
    inputs = tokens.astype(F32)
    down_part, normed = spread_down(
        mlp_weights, rms_forward(inputs, gain_full[0]).astype(BF16)
    )
    gu_cols = gather_across(gu_part.reshape(-1, 2 * ffc))
    down_cols = gather_across(down_part.reshape(-1, ffc))
    qkv_cols = attn_cols[:, : 2 * HD]
    out_cols = attn_cols[:, 2 * HD :]

    query_index = plane_start + jnp.arange(plane_rows, dtype=jnp.int32)
    position = token_tables(seq_lengths, query_index)
    starts = (jnp.arange(plane_rows, dtype=jnp.int32) + halo - position)[:, None]
    frequency = 10000.0 ** (-jnp.arange(HD // 2, dtype=F32) * 2.0 / HD)
    angles = position.astype(F32)[:, None] * frequency[None, :]
    cosine, sine_part = jnp.cos(angles), jnp.sin(angles)
    kv_cosine = jnp.where(is_even, cosine, 1.0)
    kv_sine = jnp.where(is_even, sine_part, 0.0)

    projected = matmul(normed, qkv_cols)
    queries = rotate(projected[:, :HD], cosine, sine_part).astype(BF16)
    kv_own = rotate(projected[:, HD:], kv_cosine, kv_sine).astype(BF16)
    kv_halo = lax.ppermute(kv_own[plane_rows - halo :], AXIS, to_next)
    kv_mine = jnp.concatenate([kv_halo, kv_own], axis=0)
    kv_other = lax.ppermute(kv_mine, AXIS, sibling)
    key_rows = jnp.where(is_even, kv_mine, kv_other)
    value_rows = jnp.where(is_even, kv_other, kv_mine)
    attended, inverse = attend(queries, key_rows, value_rows, starts)
    attn_proj = product_scatter([attended], [out_cols], [0], PLANE_STEP, 11)

    middle = inputs + rms_forward(attn_proj, gain_full[1])
    mid_low = gather_square(rms_forward(middle, gain_full[2]).astype(BF16), PLANE_STEP, 1)
    gate_up = matmul(mid_low, gu_cols)
    gate, up = gate_up[:, :ffc], gate_up[:, ffc:]
    gelu, slope = gelu_parts(gate)
    hidden = (gelu * up).astype(BF16)
    mlp_raw, grad_raw_low, down_grad = turn(
        hidden, down_cols, gain_full[3:4], cotangent, PLANE_STEP, 9
    )
    layer_output = (middle + rms_forward(mlp_raw, gain_full[3])).astype(BF16)

    grad_out = cotangent.astype(F32)
    gain_four = jnp.sum(grad_out * mlp_raw * rms_parts(mlp_raw), axis=0)
    down_term = scatter_across(down_grad)
    grad_hidden = matmul(grad_raw_low, down_cols)
    grad_normed_mid, gu_grad = product_scatter_back(
        [(slope * up * grad_hidden).astype(BF16), (gelu * grad_hidden).astype(BF16)],
        [gu_cols, gu_cols],
        [0, ffc],
        mid_low,
        PLANE_STEP,
        10,
    )
    gu_term = scatter_across(gu_grad)
    grad_mid_part, gain_three = rms_backward(middle, gain_full[2], grad_normed_mid)
    grad_middle = grad_out + grad_mid_part

    grad_proj, gain_two = rms_backward(attn_proj, gain_full[1], grad_middle)
    grad_proj_own, down_term = lax.optimization_barrier((grad_proj.astype(BF16), down_term))
    grad_proj_low = gather_square(grad_proj_own, PLANE_STEP, 1)
    grad_att = matmul(grad_proj_low, out_cols).astype(BF16)
    grad_query, grad_keys, grad_values = attend_back(
        queries, key_rows, value_rows, starts, inverse, grad_att
    )
    grad_mine = jnp.where(is_even, grad_keys, grad_values)
    grad_give = jnp.where(is_even, grad_values, grad_keys).astype(BF16)
    grad_kv = grad_mine + lax.ppermute(grad_give, AXIS, sibling).astype(F32)
    grad_back = lax.ppermute(grad_kv[:halo].astype(BF16), AXIS, to_prev).astype(F32)
    down_term, grad_kv = lax.optimization_barrier((down_term, grad_kv))
    down_rows = collect(down_term, 1, 6)
    down_rows, grad_back = lax.optimization_barrier((down_rows, grad_back))
    grad_kv = grad_kv[halo:] + jnp.pad(grad_back, ((plane_rows - halo, 0), (0, 0)))
    grad_qkv = jnp.concatenate(
        [
            rotate(grad_query, cosine, -sine_part).astype(BF16),
            rotate(grad_kv, kv_cosine, -kv_sine).astype(BF16),
        ],
        axis=1,
    )
    attn_grad = jnp.concatenate(
        [contract_first(normed, grad_qkv), contract_first(grad_proj_low, attended)], axis=1
    ).astype(BF16)
    attn_grad, grad_qkv = lax.optimization_barrier((attn_grad, grad_qkv))
    attn_term = scatter_across(attn_grad)
    grad_normed = product_scatter([grad_qkv], [qkv_cols], [0], PLANE_STEP, 12)
    grad_in_part, gain_one = rms_backward(inputs, gain_full[0], grad_normed)
    grad_tokens = (grad_middle + grad_in_part).astype(BF16)

    gain_term = jnp.stack([gain_one, gain_two, gain_three, gain_four], axis=0)
    gain_term = gain_term.reshape(4, peers, share).transpose(1, 0, 2)
    gain_term = jnp.pad(gain_term, ((0, 0), (0, 8 - 4), (0, -share % 128)))
    gain_recv = collect_gains(gain_term)
    gu_term, gain_recv = lax.optimization_barrier((gu_term, gain_recv))
    gu_rows = collect(gu_term, 2, 13)
    grad_mlp = jnp.concatenate([gu_rows, down_rows], axis=1).astype(F32)
    grad_mlp, attn_term = lax.optimization_barrier((grad_mlp, attn_term))
    grad_attn = collect_attn(attn_term).astype(F32)
    grad_gains = jnp.sum(gain_recv[:, :4, :share], axis=0)
    return (layer_output, grad_tokens, grad_attn, grad_mlp, grad_gains)


def solution(mesh):
    return jax.shard_map(
        local,
        mesh=mesh,
        in_specs=(
            P("fsdp", None),
            P("fsdp", None),
            P("fsdp", None),
            P(None, "fsdp"),
            P(),
            P("fsdp", None),
        ),
        out_specs=(
            P("fsdp", None),
            P("fsdp", None),
            P("fsdp", None),
            P("fsdp", None),
            P(None, "fsdp"),
        ),
        check_vma=False,
    )
```

```python
from functools import partial

import jax
import jax.numpy as jnp
from jax import lax
from jax.experimental import pallas as pl
from jax.experimental.pallas import tpu as pltpu
from jax.sharding import PartitionSpec as P

H = 8
KVH = 4
HD = 256
LMAX = 1024
PLANE = 8
QBLK = 128

EPSILON = 1e-06
SOFT_CAP = 50.0
AXIS = "fsdp"
F32 = jnp.float32
BF16 = jnp.bfloat16
MESH = pl.DeviceIdType.MESH
ANY = pl.BlockSpec(memory_space=pl.ANY)
VMEM = pl.BlockSpec(memory_space=pltpu.VMEM)
DMA = pltpu.SemaphoreType.DMA


def flip(index, step):
    return index + step - 2 * step * ((index // step) % 2)


PLANE_STEP = 4


def partner(index, bits, step):
    for bit, by in ((1, 1), (2, 2), (4, step)):
        if bits & bit:
            index = flip(index, by)
    return index


def place(device, step):
    return device % 4 + 4 * ((device // step) % 2)


def greet(peers):
    barrier = pltpu.get_barrier_semaphore()
    for peer in peers:
        pl.semaphore_signal(barrier, inc=1, device_id=(peer,), device_id_type=MESH)
    pl.semaphore_wait(barrier, len(peers))


class Copies:
    def __init__(self, send_sem, recv_sem):
        self.send_sem, self.recv_sem, self.made = send_sem, recv_sem, []

    def start(self, source, target, device):
        slot = len(self.made)
        copy = pltpu.make_async_remote_copy(
            src_ref=source,
            dst_ref=target,
            send_sem=self.send_sem.at[slot],
            recv_sem=self.recv_sem.at[slot],
            device_id=(device,),
            device_id_type=MESH,
        )
        copy.start()
        self.made.append(copy)
        return copy

    def sent(self):
        for copy in self.made:
            copy.wait_send()


def band(index, size):
    return pl.ds(pl.multiple_of(index * size, 8), size)


def lanes(index, size):
    return pl.ds(pl.multiple_of(index * size, 128), size)


def gather_steps(block_ref, full_ref, copies, own_sem, step):
    rows, width = block_ref.shape
    half = width // 2
    me = lax.axis_index(AXIS)
    sib, xn, yn = flip(me, 1), flip(me, 2), flip(me, step)
    diag = flip(xn, step)

    def at(device, side):
        return full_ref.at[band(place(device, step), rows), pl.ds(side * half, half)]

    def mine(side):
        return block_ref.at[:, pl.ds(side * half, half)]

    own_rows = full_ref.at[band(place(me, step), rows)]
    xa = copies.start(mine(0), at(me, 0), xn)
    ya = copies.start(mine(1), at(me, 1), yn)
    xb = copies.start(mine(1), at(me, 1), xn)
    yb = copies.start(mine(0), at(me, 0), yn)
    arriving = [copies.start(block_ref, own_rows, sib)]
    own = pltpu.make_async_copy(block_ref, own_rows, own_sem)
    own.start()

    def finish(on_rows=None):
        def to_sibling(device, side):
            arriving.append(copies.start(at(device, side), at(device, side), sib))

        def arrived(first, last, *devices):
            for copy in arriving[first:last]:
                copy.wait_recv()
            for device in devices:
                on_rows(device)

        if on_rows is not None:
            own.wait()
            arrived(0, 1, me)
        xa.wait_recv()
        yc = copies.start(at(xn, 0), at(xn, 0), yn)
        to_sibling(xn, 0)
        ya.wait_recv()
        xc = copies.start(at(yn, 1), at(yn, 1), xn)
        to_sibling(yn, 1)
        xb.wait_recv()
        to_sibling(xn, 1)
        yb.wait_recv()
        to_sibling(yn, 0)
        if on_rows is not None:
            arrived(1, 5, xn, yn)
        yc.wait_recv()
        to_sibling(diag, 0)
        xc.wait_recv()
        to_sibling(diag, 1)
        if on_rows is not None:
            arrived(5, 7, diag)
        else:
            arrived(0, 7)
            own.wait()

    return finish


GATHER_COPIES = 13


def cost(microseconds):
    return pl.CostEstimate(
        flops=int(microseconds * 1e7), transcendentals=0, bytes_accessed=int(microseconds * 3e4)
    )


def gather_kernel(block_ref, full_ref, own_sem, send_sem, recv_sem, *, step):
    me = lax.axis_index(AXIS)
    greet((flip(me, 1), flip(me, 2), flip(me, step)))
    copies = Copies(send_sem, recv_sem)
    gather_steps(block_ref, full_ref, copies, own_sem, step)()
    copies.sent()


def gather_square(block, step, collective_id):
    rows, width = block.shape
    return pl.pallas_call(
        partial(gather_kernel, step=step),
        out_shape=jax.ShapeDtypeStruct((PLANE * rows, width), block.dtype),
        in_specs=[ANY],
        out_specs=ANY,
        scratch_shapes=[DMA(()), DMA((GATHER_COPIES,)), DMA((GATHER_COPIES,))],
        compiler_params=pltpu.CompilerParams(collective_id=collective_id, has_side_effects=True),
        cost_estimate=cost(42),
        name="gather_square",
    )(block)


W_TILES = 3


def product_scatter_steps(
    left_refs, right_refs, left_bufs, right_bufs, buffers, load_sem, copies, offsets, step, beside=None
):
    both, got, ra, rb, ra2, rb2 = buffers
    pairs = len(left_refs)
    rows, width = got.shape[1:]
    half = width // 2
    tile = width // W_TILES
    chunk = 16
    me = lax.axis_index(AXIS)
    core = me % 2
    sib, xn, yn = flip(me, 1), flip(me, 2), flip(me, step)
    order = (flip(xn, step), xn, yn, me)
    first, second = pl.ds(0, half), pl.ds(half, half)

    def chip_rows(device):
        return pl.ds(pl.multiple_of((place(device, step) // 2) * 2 * rows, 16), 2 * rows)

    def right_load(j, t):
        r = pl.ds(t * tile, tile)
        source = right_refs[j].at[r, pl.ds(offsets[j], right_bufs[j].shape[1])]
        return pltpu.make_async_copy(source, right_bufs[j].at[r], load_sem.at[j, t])

    def left_load(j, i):
        r = chip_rows(order[i])
        return pltpu.make_async_copy(
            left_refs[j].at[r], left_bufs[j].at[r], load_sem.at[j, W_TILES + i]
        )

    for j in range(pairs):
        left_load(j, 0).start()
    for t in range(W_TILES):
        for j in range(pairs):
            right_load(j, t).start()
    for i in range(1, 4):
        for j in range(pairs):
            left_load(j, i).start()
    if beside is not None:
        beside[0]()
    greet((sib, xn, yn))

    def product(i):
        r = chip_rows(order[i])
        for j in range(pairs):
            left_load(j, i).wait()

        def columns(w):
            total = None
            for j in range(pairs):
                term = contract_last(left_bufs[j][r], right_bufs[j][w])
                total = term if total is None else total + term
            both[i, :, w] = total.astype(BF16)

        if i == 0:
            for t in range(W_TILES):
                for j in range(pairs):
                    right_load(j, t).wait()
                columns(pl.ds(t * tile, tile))
        else:

            @pl.loop(0, W_TILES)
            def _(t):
                columns(pl.ds(pl.multiple_of(t * tile, tile), tile))

    def mine(i, cols=None):
        if cols is None:
            return both.at[i, band(core, rows)]
        return both.at[i, band(core, rows), cols]

    def add(total, other):
        @pl.loop(0, rows // chunk)
        def _(k):
            r = pl.ds(pl.multiple_of(k * chunk, chunk), chunk)
            total[r] = (total[r].astype(F32) + other[r].astype(F32)).astype(total.dtype)

    def make(i):
        product(i)
        crossing = copies.start(both.at[i, band(1 - core, rows)], got.at[i], sib)
        crossing.wait_recv()
        add(mine(i), got.at[i])

    make(0)
    x0 = copies.start(mine(0, first), ra.at[0], xn)
    y0 = copies.start(mine(0, second), rb.at[0], yn)
    make(1)
    x1 = copies.start(mine(1, first), ra.at[1], xn)
    make(2)
    y1 = copies.start(mine(2, second), rb.at[1], yn)
    x0.wait_recv()
    add(mine(2, first), ra.at[0])
    y2 = copies.start(mine(2, first), ra2, yn)
    y0.wait_recv()
    add(mine(1, second), rb.at[0])
    x2 = copies.start(mine(1, second), rb2, xn)
    make(3)
    if beside is not None:
        beside[1]()
    for copy in (x1, y1, y2, x2):
        copy.wait_recv()
    own = mine(3)

    def summed(r):
        return jnp.concatenate(
            [
                own[r, first].astype(F32) + ra[1, r].astype(F32) + ra2[r].astype(F32),
                own[r, second].astype(F32) + rb[1, r].astype(F32) + rb2[r].astype(F32),
            ],
            axis=1,
        )

    return summed


ROW_CHUNK = 16


def product_scatter_kernel(*refs, pairs, offsets, step):
    left_refs, right_refs, out_ref = refs[:pairs], refs[pairs : 2 * pairs], refs[2 * pairs]
    left_bufs = refs[2 * pairs + 1 : 3 * pairs + 1]
    right_bufs = refs[3 * pairs + 1 : 4 * pairs + 1]
    buffers, (load_sem, send_sem, recv_sem) = refs[4 * pairs + 1 : -3], refs[-3:]
    copies = Copies(send_sem, recv_sem)
    summed = product_scatter_steps(
        left_refs, right_refs, left_bufs, right_bufs, buffers, load_sem, copies, offsets, step
    )

    @pl.loop(0, out_ref.shape[0] // ROW_CHUNK)
    def _(k):
        r = pl.ds(pl.multiple_of(k * ROW_CHUNK, ROW_CHUNK), ROW_CHUNK)
        out_ref[r] = summed(r)

    copies.sent()


def scatter_buffers(rows, width):
    half = width // 2
    return [
        pltpu.VMEM((4, 2 * rows, width), BF16),
        pltpu.VMEM((4, rows, width), BF16),
        pltpu.VMEM((2, rows, half), BF16),
        pltpu.VMEM((2, rows, half), BF16),
        pltpu.VMEM((rows, half), BF16),
        pltpu.VMEM((rows, half), BF16),
    ]


def product_scatter(lefts, rights, offsets, step, collective_id):
    pairs = len(lefts)
    rows, width = lefts[0].shape[0] // PLANE, rights[0].shape[0]
    return pl.pallas_call(
        partial(product_scatter_kernel, pairs=pairs, offsets=offsets, step=step),
        out_shape=jax.ShapeDtypeStruct((rows, width), F32),
        in_specs=[ANY] * (2 * pairs),
        out_specs=VMEM,
        scratch_shapes=[
            *[pltpu.VMEM(value.shape, BF16) for value in lefts],
            *[pltpu.VMEM((width, value.shape[1]), BF16) for value in lefts],
            *scatter_buffers(rows, width),
            DMA((pairs, W_TILES + 4)),
            DMA((10,)),
            DMA((10,)),
        ],
        compiler_params=pltpu.CompilerParams(
            collective_id=collective_id, has_side_effects=True, vmem_limit_bytes=56 << 20
        ),
        cost_estimate=cost(50),
        name="product_scatter",
    )(*lefts, *rights)


BACK_TILE = 384


def back_kernel(*refs, pairs, offsets, step):
    left_refs, right_refs, rows_ref = refs[:pairs], refs[pairs : 2 * pairs], refs[2 * pairs]
    out_ref, term_ref = refs[2 * pairs + 1 : 2 * pairs + 3]
    scratch = refs[2 * pairs + 3 :]
    left_bufs, right_bufs = scratch[:pairs], scratch[pairs : 2 * pairs]
    rows_buf, stage = scratch[2 * pairs : 2 * pairs + 2]
    buffers = scratch[2 * pairs + 2 : -5]
    load_sem, rows_sem, store_sem, send_sem, recv_sem = scratch[-5:]
    copies = Copies(send_sem, recv_sem)
    rows_load = pltpu.make_async_copy(rows_ref, rows_buf, rows_sem)
    tiles = rows_ref.shape[1] // BACK_TILE
    width = left_refs[0].shape[1]

    def store(t):
        return pltpu.make_async_copy(
            stage.at[t % 2],
            term_ref.at[pl.ds(pl.multiple_of(t * BACK_TILE, 16), BACK_TILE)],
            store_sem.at[t % 2],
        )

    def beside():
        rows_load.wait()

        @pl.loop(0, tiles)
        def _(t):
            @pl.when(t >= 2)
            def _():
                store(t - 2).wait()

            columns = rows_buf[:, pl.ds(pl.multiple_of(t * BACK_TILE, BACK_TILE), BACK_TILE)]
            for j in range(pairs):
                term = contract_first(columns, left_bufs[j][...])
                stage[t % 2, :, pl.ds(j * width, width)] = term.astype(BF16)
            store(t).start()

    def start_rows():
        rows_load.start()

    summed = product_scatter_steps(
        left_refs,
        right_refs,
        left_bufs,
        right_bufs,
        buffers,
        load_sem,
        copies,
        offsets,
        step,
        (start_rows, beside),
    )

    @pl.loop(0, out_ref.shape[0] // ROW_CHUNK)
    def _(k):
        r = pl.ds(pl.multiple_of(k * ROW_CHUNK, ROW_CHUNK), ROW_CHUNK)
        out_ref[r] = summed(r)

    for t in range(tiles - 2, tiles):
        store(t).wait()
    copies.sent()


def product_scatter_back(lefts, rights, offsets, rows, step, collective_id):
    pairs = len(lefts)
    count, width = lefts[0].shape[0] // PLANE, rights[0].shape[0]
    columns = sum(value.shape[1] for value in lefts)
    return pl.pallas_call(
        partial(back_kernel, pairs=pairs, offsets=offsets, step=step),
        out_shape=(
            jax.ShapeDtypeStruct((count, width), F32),
            jax.ShapeDtypeStruct((rows.shape[1], columns), BF16),
        ),
        in_specs=[ANY] * (2 * pairs + 1),
        out_specs=(VMEM, ANY),
        scratch_shapes=[
            *[pltpu.VMEM(value.shape, BF16) for value in lefts],
            *[pltpu.VMEM((width, value.shape[1]), BF16) for value in lefts],
            pltpu.VMEM(rows.shape, BF16),
            pltpu.VMEM((2, BACK_TILE, columns), BF16),
            *scatter_buffers(count, width),
            DMA((pairs, W_TILES + 4)),
            DMA(()),
            DMA((2,)),
            DMA((10,)),
            DMA((10,)),
        ],
        compiler_params=pltpu.CompilerParams(
            collective_id=collective_id, has_side_effects=True, vmem_limit_bytes=62 << 20
        ),
        cost_estimate=cost(60),
        name="product_scatter_back",
    )(*lefts, *rights, rows)


TURN_TILE = 768


def turn_kernel(
    left_ref, right_ref, gain_ref, grad_ref, raw_ref, full_ref, term_ref, *refs, step
):
    left_buf, right_buf, gathered, total, grad_own = refs[:5]
    buffers, (load_sem, own_sem, store_sem, send_sem, recv_sem) = refs[5:-5], refs[-5:]
    rows, width = grad_ref.shape
    copies = Copies(send_sem, recv_sem)
    summed = product_scatter_steps(
        [left_ref], [right_ref], [left_buf], [right_buf], buffers, load_sem, copies, [0], step
    )
    gain = gain_ref[...]

    @pl.loop(0, rows // ROW_CHUNK)
    def _(k):
        r = pl.ds(pl.multiple_of(k * ROW_CHUNK, ROW_CHUNK), ROW_CHUNK)
        value = summed(r)
        raw_ref[r] = value
        scale = lax.rsqrt(jnp.mean(value * value, axis=1, keepdims=True) + EPSILON)
        scaled = (1.0 + gain) * grad_ref[r].astype(F32)
        inner = jnp.mean(value * scaled, axis=1, keepdims=True)
        grad_own[r] = (scale * scaled - value * (scale * scale * scale * inner)).astype(BF16)

    stores = []

    def on_rows(device):
        slot = len(stores)
        r = pl.ds(pl.multiple_of((place(device, step) // 2) * 2 * rows, 16), 2 * rows)
        store = pltpu.make_async_copy(gathered.at[r], full_ref.at[r], store_sem.at[slot])
        store.start()
        stores.append(store)
        right = left_buf[r]

        @pl.loop(0, width // TURN_TILE)
        def _(t):
            w = pl.ds(pl.multiple_of(t * TURN_TILE, TURN_TILE), TURN_TILE)
            term = contract_first(gathered[r, w], right)
            if slot == 0:
                total[w] = term
            elif slot < 3:
                total[w] += term
            else:
                right_buf[w] = (total[w] + term).astype(BF16)
                pltpu.make_async_copy(right_buf.at[w], term_ref.at[w], store_sem.at[4]).start()

    gather_steps(grad_own, gathered, copies, own_sem, step)(on_rows)
    pltpu.make_async_copy(right_buf, term_ref, store_sem.at[4]).wait()
    for store in stores:
        store.wait()
    copies.sent()


def turn(left, right, gain_row, grad, step, collective_id):
    rows, width = grad.shape
    count = 10 + GATHER_COPIES
    return pl.pallas_call(
        partial(turn_kernel, step=step),
        out_shape=(
            jax.ShapeDtypeStruct((rows, width), F32),
            jax.ShapeDtypeStruct((PLANE * rows, width), BF16),
            jax.ShapeDtypeStruct((width, left.shape[1]), BF16),
        ),
        in_specs=[ANY, ANY, VMEM, VMEM],
        out_specs=(VMEM, ANY, ANY),
        scratch_shapes=[
            pltpu.VMEM(left.shape, BF16),
            pltpu.VMEM(right.shape, BF16),
            pltpu.VMEM((PLANE * rows, width), BF16),
            pltpu.VMEM((width, left.shape[1]), F32),
            pltpu.VMEM((rows, width), BF16),
            *scatter_buffers(rows, width),
            DMA((1, W_TILES + 4)),
            DMA(()),
            DMA((5,)),
            DMA((count,)),
            DMA((count,)),
        ],
        compiler_params=pltpu.CompilerParams(
            collective_id=collective_id, has_side_effects=True, vmem_limit_bytes=60 << 20
        ),
        cost_estimate=cost(50),
        name="turn",
    )(left, right, gain_row, grad)


def attn_columns(column):
    query_width = H * HD
    key_offset = query_width + (column % 2) * KVH * HD + (column // 2) * HD
    return (column * HD, key_offset, query_width + 2 * KVH * HD + column * HD)


def greet_all(peers):
    me = lax.axis_index(AXIS)
    barrier = pltpu.get_barrier_semaphore()

    @pl.loop(1, peers)
    def _(k):
        device = lax.rem(me + k, peers)
        pl.semaphore_signal(barrier, inc=1, device_id=(device,), device_id_type=MESH)

    pl.semaphore_wait(barrier, peers - 1)


def exchange_all(source_of, target_ref, send_sem, recv_sem):
    peers = target_ref.shape[0]
    me = lax.axis_index(AXIS)

    def copy(k):
        device = lax.rem(me + k, peers)
        return pltpu.make_async_remote_copy(
            src_ref=source_of(device),
            dst_ref=target_ref.at[me],
            send_sem=send_sem.at[k],
            recv_sem=recv_sem.at[k],
            device_id=(device,),
            device_id_type=MESH,
        )

    @pl.loop(1, peers)
    def _(k):
        copy(k).start()

    def finish():
        @pl.loop(1, peers)
        def _(k):
            copy(k).wait()

    return finish


ORDER = (6, 7, 2, 3, 4, 5, 1)


def swap_steps(pieces_of, targets, copies, own_sem, step):
    me = lax.axis_index(AXIS)
    moved = []
    for bits in ORDER:
        peer = partner(me, bits, step)
        for source, target in zip(pieces_of(place(peer, step)), targets):
            moved.append(copies.start(source, target, peer))
    owns = []
    for slot, (source, target) in enumerate(zip(pieces_of(place(me, step)), targets)):
        own = pltpu.make_async_copy(source, target, own_sem.at[slot])
        own.start()
        owns.append(own)

    def finish():
        for own in owns:
            own.wait()
        for copy in moved:
            copy.wait_recv()

    return finish


def square(step):
    me = lax.axis_index(AXIS)
    return [partner(me, bits, step) for bits in ORDER]


def wide(offset):
    return pl.ds(pl.multiple_of(offset, 128), HD)


class Line:
    def __init__(self, full_ref, send_sem, recv_sem):
        me = lax.axis_index(AXIS)
        self.full, self.planes = full_ref, full_ref.shape[0]
        self.send_sem, self.recv_sem = send_sem, recv_sem
        self.plane = me // PLANE
        peers = self.planes * PLANE
        self.devices = (lax.rem(me + PLANE, peers), lax.rem(me + peers - PLANE, peers))

    def copy(self, way, slot, source):
        return pltpu.make_async_remote_copy(
            src_ref=self.full.at[source],
            dst_ref=self.full.at[source],
            send_sem=self.send_sem.at[way, slot],
            recv_sem=self.recv_sem.at[way, slot],
            device_id=(self.devices[way],),
            device_id_type=MESH,
        )

    def sends(self, way, hop):
        if way == 0:
            source = self.plane - (hop - 1)
            return (self.plane + 1 < self.planes) & (source >= 0), source
        source = self.plane + (hop - 1)
        return (self.plane >= 1) & (source < self.planes), source

    def greet(self):
        barrier = pltpu.get_barrier_semaphore()
        count = 0
        for way, there in enumerate((self.plane + 1 < self.planes, self.plane >= 1)):

            @pl.when(there)
            def _():
                pl.semaphore_signal(
                    barrier, inc=1, device_id=(self.devices[way],), device_id_type=MESH
                )

            count = count + there.astype(jnp.int32)
        return count

    def start(self, hop, slot):
        for way in range(2):
            there, source = self.sends(way, hop)

            @pl.when(there)
            def _():
                self.copy(way, slot, source).start()

    def arrived(self, hop, slot):
        for way in range(2):
            source = self.plane - hop if way == 0 else self.plane + hop

            @pl.when((source >= 0) & (source < self.planes))
            def _():
                self.copy(way, slot, source).wait_recv()

    def sent(self, hop, slot):
        for way in range(2):
            there, source = self.sends(way, hop)

            @pl.when(there)
            def _():
                self.copy(way, slot, source).wait_send()


def line_hops(planes):
    hops = list(range(1, planes))
    first = (2 * len(hops) + 2) // 3
    return hops[:first], hops[first:]


def spread_attn_kernel(weights_ref, part_ref, own_sem, send_sem, recv_sem):
    me = lax.axis_index(AXIS)
    plane, here = me // PLANE, place(me, PLANE_STEP)
    greet(square(PLANE_STEP))
    copies = Copies(send_sem, recv_sem)
    swap_steps(
        lambda c: [weights_ref.at[:, wide(offset)] for offset in attn_columns(c)],
        [part_ref.at[plane, here, :, pl.ds(slot * HD, HD)] for slot in range(3)],
        copies,
        own_sem,
        PLANE_STEP,
    )()
    copies.sent()


def spread_attn(weights, planes):
    rows = weights.shape[0]
    return pl.pallas_call(
        spread_attn_kernel,
        out_shape=jax.ShapeDtypeStruct((planes, PLANE, rows, 3 * HD), BF16),
        in_specs=[ANY],
        out_specs=ANY,
        scratch_shapes=[DMA((3,)), DMA((21,)), DMA((21,))],
        compiler_params=pltpu.CompilerParams(collective_id=3, has_side_effects=True),
        name="spread_attn",
    )(weights)


def spread_gu_kernel(
    weights_ref,
    gain_ref,
    attn_in,
    gu_ref,
    gains_ref,
    attn_ref,
    own_sem,
    send_sem,
    recv_sem,
    gain_send,
    gain_recv,
    line_send,
    line_recv,
):
    peers = gains_ref.shape[0]
    ffc = gu_ref.shape[2] // 2
    me = lax.axis_index(AXIS)
    here = place(me, PLANE_STEP)
    line = Line(attn_ref, line_send, line_recv)
    hops = line_hops(line.planes)[0]
    greet_all(peers)
    line.start(hops[0], 0)
    gains_done = exchange_all(lambda device: gain_ref, gains_ref, gain_send, gain_recv)
    own = pltpu.make_async_copy(gain_ref, gains_ref.at[me], own_sem.at[2])
    own.start()
    copies = Copies(send_sem, recv_sem)
    spread = swap_steps(
        lambda c: [weights_ref.at[:, lanes(slot * PLANE + c, ffc)] for slot in range(2)],
        [gu_ref.at[here, :, pl.ds(slot * ffc, ffc)] for slot in range(2)],
        copies,
        own_sem,
        PLANE_STEP,
    )
    for slot, hop in enumerate(hops):
        line.arrived(hop, slot)
        if slot + 1 < len(hops):
            line.start(hop + 1, slot + 1)
    spread()
    own.wait()
    gains_done()
    for slot, hop in enumerate(hops):
        line.sent(hop, slot)
    copies.sent()


def spread_gu(weights, gain_block, attn_full, peers):
    rows = weights.shape[0]
    ffc = weights.shape[1] // 3 // PLANE
    hops = len(line_hops(attn_full.shape[0])[0])
    return pl.pallas_call(
        spread_gu_kernel,
        out_shape=(
            jax.ShapeDtypeStruct((PLANE, rows, 2 * ffc), BF16),
            jax.ShapeDtypeStruct((peers,) + gain_block.shape, gain_block.dtype),
            jax.ShapeDtypeStruct(attn_full.shape, attn_full.dtype),
        ),
        in_specs=[ANY, ANY, ANY],
        out_specs=(ANY, ANY, ANY),
        scratch_shapes=[
            DMA((3,)),
            DMA((14,)),
            DMA((14,)),
            DMA((peers,)),
            DMA((peers,)),
            DMA((2, hops)),
            DMA((2, hops)),
        ],
        input_output_aliases={2: 2},
        compiler_params=pltpu.CompilerParams(collective_id=4, has_side_effects=True),
        cost_estimate=cost(38),
        name="spread_gu",
    )(weights, gain_block, attn_full)


def spread_down_kernel(
    weights_ref,
    block_ref,
    attn_in,
    down_ref,
    full_ref,
    attn_ref,
    own_sem,
    send_sem,
    recv_sem,
    line_send,
    line_recv,
):
    ffc = down_ref.shape[2]
    me = lax.axis_index(AXIS)
    line = Line(attn_ref, line_send, line_recv)
    hops = line_hops(line.planes)[1]
    barrier = pltpu.get_barrier_semaphore()
    in_square = square(PLANE_STEP)
    for peer in in_square:
        pl.semaphore_signal(barrier, inc=1, device_id=(peer,), device_id_type=MESH)
    pl.semaphore_wait(barrier, len(in_square) + line.greet())
    line.start(hops[0], 0)
    copies = Copies(send_sem, recv_sem)
    gathered = gather_steps(block_ref, full_ref, copies, own_sem.at[1], PLANE_STEP)
    spread = swap_steps(
        lambda c: [weights_ref.at[:, lanes(2 * PLANE + c, ffc)]],
        [down_ref.at[place(me, PLANE_STEP)]],
        copies,
        own_sem,
        PLANE_STEP,
    )
    gathered()
    for slot, hop in enumerate(hops):
        line.arrived(hop, slot)
        if slot + 1 < len(hops):
            line.start(hop + 1, slot + 1)
    spread()
    for slot, hop in enumerate(hops):
        line.sent(hop, slot)
    copies.sent()


def spread_down(weights, block, attn_full):
    rows = weights.shape[0]
    ffc = weights.shape[1] // 3 // PLANE
    count = GATHER_COPIES + 7
    hops = len(line_hops(attn_full.shape[0])[1])
    return pl.pallas_call(
        spread_down_kernel,
        out_shape=(
            jax.ShapeDtypeStruct((PLANE, rows, ffc), BF16),
            jax.ShapeDtypeStruct((PLANE * block.shape[0], block.shape[1]), BF16),
            jax.ShapeDtypeStruct(attn_full.shape, attn_full.dtype),
        ),
        in_specs=[ANY, ANY, ANY],
        out_specs=(ANY, ANY, ANY),
        scratch_shapes=[
            DMA((2,)),
            DMA((count,)),
            DMA((count,)),
            DMA((2, hops)),
            DMA((2, hops)),
        ],
        input_output_aliases={2: 2},
        compiler_params=pltpu.CompilerParams(collective_id=5, has_side_effects=True),
        cost_estimate=cost(1),
        name="spread_down",
    )(weights, block, attn_full)


def collect_kernel(term_ref, rows_ref, own_sem, send_sem, recv_sem):
    here = place(lax.axis_index(AXIS), PLANE_STEP)
    count = own_sem.shape[0]
    ffc = term_ref.shape[2] // count
    greet(square(PLANE_STEP))
    copies = Copies(send_sem, recv_sem)
    swap_steps(
        lambda c: [term_ref.at[c, :, pl.ds(slot * ffc, ffc)] for slot in range(count)],
        [rows_ref.at[:, lanes(slot * PLANE + here, ffc)] for slot in range(count)],
        copies,
        own_sem,
        PLANE_STEP,
    )()
    copies.sent()


def collect(term, count, collective_id):
    rows, columns = term.shape[1:]
    return pl.pallas_call(
        collect_kernel,
        out_shape=jax.ShapeDtypeStruct((rows, PLANE * columns), BF16),
        in_specs=[ANY],
        out_specs=ANY,
        scratch_shapes=[DMA((count,)), DMA((7 * count,)), DMA((7 * count,))],
        compiler_params=pltpu.CompilerParams(collective_id=collective_id, has_side_effects=True),
        cost_estimate=cost(0.1),
        name="collect",
    )(term)


def collect_attn_kernel(term_ref, rows_ref, own_sem, send_sem, recv_sem):
    here = place(lax.axis_index(AXIS), PLANE_STEP)
    greet(square(PLANE_STEP))
    copies = Copies(send_sem, recv_sem)
    swap_steps(
        lambda c: [term_ref.at[c, :, pl.ds(slot * HD, HD)] for slot in range(3)],
        [rows_ref.at[:, wide(offset)] for offset in attn_columns(here)],
        copies,
        own_sem,
        PLANE_STEP,
    )()
    copies.sent()


def collect_attn(term):
    rows = term.shape[1]
    return pl.pallas_call(
        collect_attn_kernel,
        out_shape=jax.ShapeDtypeStruct((rows, PLANE * 3 * HD), BF16),
        in_specs=[ANY],
        out_specs=ANY,
        scratch_shapes=[DMA((3,)), DMA((21,)), DMA((21,))],
        compiler_params=pltpu.CompilerParams(collective_id=7, has_side_effects=True),
        name="collect_attn",
    )(term)


def collect_gains_kernel(gain_ref, gains_ref, own_sem, gain_send, gain_recv):
    me = lax.axis_index(AXIS)
    greet_all(gain_ref.shape[0])
    done = exchange_all(lambda device: gain_ref.at[device], gains_ref, gain_send, gain_recv)
    own = pltpu.make_async_copy(gain_ref.at[me], gains_ref.at[me], own_sem)
    own.start()
    own.wait()
    done()


def collect_gains(gain_blocks):
    peers = gain_blocks.shape[0]
    return pl.pallas_call(
        collect_gains_kernel,
        out_shape=jax.ShapeDtypeStruct(gain_blocks.shape, gain_blocks.dtype),
        in_specs=[ANY],
        out_specs=ANY,
        scratch_shapes=[DMA(()), DMA((peers,)), DMA((peers,))],
        compiler_params=pltpu.CompilerParams(collective_id=8, has_side_effects=True),
        name="collect_gains",
    )(gain_blocks)


def block_scores(q, k, start, first):
    scores = lax.dot_general(q, k, (((1,), (1,)), ((), ())), preferred_element_type=F32)
    bent = jnp.tanh(scores * (HD ** (-0.5) / SOFT_CAP))
    rows, span = scores.shape
    key_at = lax.broadcasted_iota(jnp.int32, (rows, span), 1)
    row_at = lax.broadcasted_iota(jnp.int32, (rows, span), 0)
    allowed = (key_at + first >= start) & (key_at <= row_at + LMAX)
    return (bent, jnp.where(allowed, jnp.exp(SOFT_CAP * bent), 0.0))


def attend_kernel(q_ref, k_ref, v_ref, start_ref, out_ref, inv_ref):
    first = pl.program_id(0) * QBLK
    keys = pl.ds(pl.multiple_of(first, QBLK), LMAX + QBLK)
    unused_bent, exponent = block_scores(q_ref[...], k_ref[keys], start_ref[...], first)
    inverse = 1.0 / jnp.sum(exponent, axis=-1, keepdims=True)
    weights = (exponent * inverse).astype(BF16)
    out_ref[...] = jnp.dot(weights, v_ref[keys], preferred_element_type=F32).astype(BF16)
    inv_ref[...] = inverse


def attend(queries, key_rows, value_rows, starts):
    rows = queries.shape[0]
    span = key_rows.shape[0]
    row_spec = pl.BlockSpec((QBLK, HD), lambda i: (i, 0))
    one_spec = pl.BlockSpec((QBLK, 1), lambda i: (i, 0))
    all_spec = pl.BlockSpec((span, HD), lambda i: (0, 0))
    return pl.pallas_call(
        attend_kernel,
        out_shape=(
            jax.ShapeDtypeStruct((rows, HD), BF16),
            jax.ShapeDtypeStruct((rows, 1), F32),
        ),
        grid=(rows // QBLK,),
        in_specs=[row_spec, all_spec, all_spec, one_spec],
        out_specs=(row_spec, one_spec),
        compiler_params=pltpu.CompilerParams(vmem_limit_bytes=40 << 20),
        cost_estimate=cost(1),
        name="attend",
    )(queries, key_rows, value_rows, starts)


def attend_back_kernel(q_ref, k_ref, v_ref, start_ref, inv_ref, grad_ref, gq_ref, gk_ref, gv_ref):
    @pl.when(pl.program_id(0) == 0)
    def _():
        gk_ref[...] = jnp.zeros_like(gk_ref)
        gv_ref[...] = jnp.zeros_like(gv_ref)

    first = pl.program_id(0) * QBLK
    keys = pl.ds(pl.multiple_of(first, QBLK), LMAX + QBLK)
    q, k, v, grad = q_ref[...], k_ref[keys], v_ref[keys], grad_ref[...]
    bent, exponent = block_scores(q, k, start_ref[...], first)
    probability = exponent * inv_ref[...]
    grad_prob = lax.dot_general(grad, v, (((1,), (1,)), ((), ())), preferred_element_type=F32)
    inner = jnp.sum(probability * grad_prob, axis=-1, keepdims=True)
    grad_scores = (probability * (grad_prob - inner) * (1.0 - bent * bent)).astype(BF16)
    scale = HD ** (-0.5)
    gq_ref[...] = jnp.dot(grad_scores, k, preferred_element_type=F32) * scale
    over_rows = (((0,), (0,)), ((), ()))
    gk_ref[keys] += lax.dot_general(grad_scores, q, over_rows, preferred_element_type=F32) * scale
    gv_ref[keys] += lax.dot_general(
        probability.astype(BF16), grad, over_rows, preferred_element_type=F32
    )


def attend_back(queries, key_rows, value_rows, starts, inverse, grad):
    rows = queries.shape[0]
    span = key_rows.shape[0]
    row_spec = pl.BlockSpec((QBLK, HD), lambda i: (i, 0))
    one_spec = pl.BlockSpec((QBLK, 1), lambda i: (i, 0))
    all_spec = pl.BlockSpec((span, HD), lambda i: (0, 0))
    return pl.pallas_call(
        attend_back_kernel,
        out_shape=(
            jax.ShapeDtypeStruct((rows, HD), F32),
            jax.ShapeDtypeStruct((span, HD), F32),
            jax.ShapeDtypeStruct((span, HD), F32),
        ),
        grid=(rows // QBLK,),
        in_specs=[row_spec, all_spec, all_spec, one_spec, one_spec, row_spec],
        out_specs=(row_spec, all_spec, all_spec),
        compiler_params=pltpu.CompilerParams(vmem_limit_bytes=48 << 20),
        cost_estimate=cost(20),
        name="attend_back",
    )(queries, key_rows, value_rows, starts, inverse, grad)


def token_tables(seq_lengths, index_vec):
    count = seq_lengths.shape[0]
    order = jnp.arange(count, dtype=jnp.int32)
    seq_ends = jnp.sum(
        jnp.where(order[None, :] <= order[:, None], seq_lengths[None, :], 0), axis=1
    )
    after_end = index_vec[:, None] >= seq_ends[None, :]
    return index_vec - jnp.sum(jnp.where(after_end, seq_lengths[None, :], 0), axis=1)


def rms_parts(value):
    return lax.rsqrt(jnp.mean(value * value, axis=-1, keepdims=True) + EPSILON)


def rms_forward(value, gain_vec):
    return value * rms_parts(value) * (1.0 + gain_vec)


def rms_backward(value, gain_vec, grad):
    r = rms_parts(value)
    scaled = (1.0 + gain_vec) * grad
    inner = jnp.mean(value * scaled, axis=-1, keepdims=True)
    return (r * scaled - value * (r * r * r * inner), jnp.sum(grad * value * r, axis=0))


def rotate(value, cosine, sine_part):
    half_width = value.shape[-1] // 2
    first_half = value[..., :half_width]
    second_half = value[..., half_width:]
    return jnp.concatenate(
        [
            first_half * cosine - second_half * sine_part,
            second_half * cosine + first_half * sine_part,
        ],
        axis=-1,
    )


def contract_last(left_side, right_side):
    return lax.dot_general(
        left_side, right_side, (((1,), (1,)), ((), ())), preferred_element_type=F32
    )


def contract_first(left_side, right_side):
    return lax.dot_general(
        left_side, right_side, (((0,), (0,)), ((), ())), preferred_element_type=F32
    )


def matmul(left_side, right_side):
    return jnp.dot(left_side, right_side, preferred_element_type=F32)


def gelu_parts(gate):
    k0 = 0.7978845608028654
    k1 = 0.044715
    t = jnp.tanh(k0 * (gate + k1 * gate * gate * gate))
    value = 0.5 * gate * (1.0 + t)
    slope = 0.5 * (1.0 + t) + 0.5 * gate * (1.0 - t * t) * k0 * (1.0 + 3.0 * k1 * gate * gate)
    return (value, slope)


def local(tokens, attn_weights, mlp_weights, norm_gains, seq_lengths, cotangent):
    tok_rows, width = tokens.shape
    peers = lax.axis_size(AXIS)
    planes = peers // PLANE
    share = width // peers
    row_share = attn_weights.shape[0]
    ff = mlp_weights.shape[1] // 3
    ffc = ff // PLANE
    plane_rows = PLANE * tok_rows
    halo = LMAX
    across = [[p * PLANE + i for p in range(planes)] for i in range(PLANE)]
    sibling = [(i, i ^ 1) for i in range(peers)]
    to_next = [(i, i + PLANE) for i in range(peers - PLANE)]
    to_prev = [(i + PLANE, i) for i in range(peers - PLANE)]
    me = lax.axis_index(AXIS)
    is_even = (me % 2) == 0
    plane_start = (me // PLANE) * plane_rows

    def gather_across(value):
        return lax.all_gather(value, AXIS, axis=0, tiled=True, axis_index_groups=across)

    def scatter_across(value):
        part = lax.psum_scatter(
            value.astype(BF16), AXIS, scatter_dimension=0, tiled=True, axis_index_groups=across
        )
        return part.reshape(PLANE, -1, part.shape[1])

    gain_block = jnp.pad(norm_gains.astype(F32), ((0, 8 - 4), (0, -share % 128)))
    attn_full, gain_block = lax.optimization_barrier(
        (spread_attn(attn_weights, planes), gain_block)
    )
    gu_part, gain_blocks, attn_full = spread_gu(mlp_weights, gain_block, attn_full, peers)
    gain_full = gain_blocks[:, :4, :share].transpose(1, 0, 2).reshape(4, width)
    inputs = tokens.astype(F32)
    down_part, normed, attn_full = spread_down(
        mlp_weights, rms_forward(inputs, gain_full[0]).astype(BF16), attn_full
    )
    attn_cols = attn_full.reshape(width, 3 * HD)
    gu_cols = gather_across(gu_part.reshape(-1, 2 * ffc))
    down_cols = gather_across(down_part.reshape(-1, ffc))
    qkv_cols = attn_cols[:, : 2 * HD]
    out_cols = attn_cols[:, 2 * HD :]

    query_index = plane_start + jnp.arange(plane_rows, dtype=jnp.int32)
    position = token_tables(seq_lengths, query_index)
    starts = (jnp.arange(plane_rows, dtype=jnp.int32) + halo - position)[:, None]
    frequency = 10000.0 ** (-jnp.arange(HD // 2, dtype=F32) * 2.0 / HD)
    angles = position.astype(F32)[:, None] * frequency[None, :]
    cosine, sine_part = jnp.cos(angles), jnp.sin(angles)
    kv_cosine = jnp.where(is_even, cosine, 1.0)
    kv_sine = jnp.where(is_even, sine_part, 0.0)

    projected = matmul(normed, qkv_cols)
    queries = rotate(projected[:, :HD], cosine, sine_part).astype(BF16)
    kv_own = rotate(projected[:, HD:], kv_cosine, kv_sine).astype(BF16)
    kv_halo = lax.ppermute(kv_own[plane_rows - halo :], AXIS, to_next)
    kv_mine = jnp.concatenate([kv_halo, kv_own], axis=0)
    kv_other = lax.ppermute(kv_mine, AXIS, sibling)
    key_rows = jnp.where(is_even, kv_mine, kv_other)
    value_rows = jnp.where(is_even, kv_other, kv_mine)
    attended, inverse = attend(queries, key_rows, value_rows, starts)
    attn_proj = product_scatter([attended], [out_cols], [0], PLANE_STEP, 11)

    middle = inputs + rms_forward(attn_proj, gain_full[1])
    mid_low = gather_square(rms_forward(middle, gain_full[2]).astype(BF16), PLANE_STEP, 1)
    gate_up = matmul(mid_low, gu_cols)
    gate, up = gate_up[:, :ffc], gate_up[:, ffc:]
    gelu, slope = gelu_parts(gate)
    hidden = (gelu * up).astype(BF16)
    mlp_raw, grad_raw_low, down_grad = turn(
        hidden, down_cols, gain_full[3:4], cotangent, PLANE_STEP, 9
    )
    layer_output = (middle + rms_forward(mlp_raw, gain_full[3])).astype(BF16)

    grad_out = cotangent.astype(F32)
    gain_four = jnp.sum(grad_out * mlp_raw * rms_parts(mlp_raw), axis=0)
    down_term = scatter_across(down_grad)
    grad_hidden = matmul(grad_raw_low, down_cols)
    grad_normed_mid, gu_grad = product_scatter_back(
        [(slope * up * grad_hidden).astype(BF16), (gelu * grad_hidden).astype(BF16)],
        [gu_cols, gu_cols],
        [0, ffc],
        mid_low,
        PLANE_STEP,
        10,
    )
    gu_term = scatter_across(gu_grad)
    grad_mid_part, gain_three = rms_backward(middle, gain_full[2], grad_normed_mid)
    grad_middle = grad_out + grad_mid_part

    grad_proj, gain_two = rms_backward(attn_proj, gain_full[1], grad_middle)
    grad_proj_own, down_term = lax.optimization_barrier((grad_proj.astype(BF16), down_term))
    grad_proj_low = gather_square(grad_proj_own, PLANE_STEP, 1)
    grad_att = matmul(grad_proj_low, out_cols).astype(BF16)
    grad_query, grad_keys, grad_values = attend_back(
        queries, key_rows, value_rows, starts, inverse, grad_att
    )
    grad_mine = jnp.where(is_even, grad_keys, grad_values)
    grad_give = jnp.where(is_even, grad_values, grad_keys).astype(BF16)
    grad_kv = grad_mine + lax.ppermute(grad_give, AXIS, sibling).astype(F32)
    grad_back = lax.ppermute(grad_kv[:halo].astype(BF16), AXIS, to_prev).astype(F32)
    down_term, grad_kv = lax.optimization_barrier((down_term, grad_kv))
    down_rows = collect(down_term, 1, 6)
    down_rows, grad_back = lax.optimization_barrier((down_rows, grad_back))
    grad_kv = grad_kv[halo:] + jnp.pad(grad_back, ((plane_rows - halo, 0), (0, 0)))
    grad_qkv = jnp.concatenate(
        [
            rotate(grad_query, cosine, -sine_part).astype(BF16),
            rotate(grad_kv, kv_cosine, -kv_sine).astype(BF16),
        ],
        axis=1,
    )
    attn_grad = jnp.concatenate(
        [contract_first(normed, grad_qkv), contract_first(grad_proj_low, attended)], axis=1
    ).astype(BF16)
    attn_grad, grad_qkv = lax.optimization_barrier((attn_grad, grad_qkv))
    attn_term = scatter_across(attn_grad)
    grad_normed = product_scatter([grad_qkv], [qkv_cols], [0], PLANE_STEP, 12)
    grad_in_part, gain_one = rms_backward(inputs, gain_full[0], grad_normed)
    grad_tokens = (grad_middle + grad_in_part).astype(BF16)

    gain_term = jnp.stack([gain_one, gain_two, gain_three, gain_four], axis=0)
    gain_term = gain_term.reshape(4, peers, share).transpose(1, 0, 2)
    gain_term = jnp.pad(gain_term, ((0, 0), (0, 8 - 4), (0, -share % 128)))
    gain_recv = collect_gains(gain_term)
    gu_term, gain_recv = lax.optimization_barrier((gu_term, gain_recv))
    gu_rows = collect(gu_term, 2, 13)
    grad_mlp = jnp.concatenate([gu_rows, down_rows], axis=1).astype(F32)
    grad_mlp, attn_term = lax.optimization_barrier((grad_mlp, attn_term))
    grad_attn = collect_attn(attn_term).astype(F32)
    grad_gains = jnp.sum(gain_recv[:, :4, :share], axis=0)
    return (layer_output, grad_tokens, grad_attn, grad_mlp, grad_gains)


def solution(mesh):
    return jax.shard_map(
        local,
        mesh=mesh,
        in_specs=(
            P("fsdp", None),
            P("fsdp", None),
            P("fsdp", None),
            P(None, "fsdp"),
            P(),
            P("fsdp", None),
        ),
        out_specs=(
            P("fsdp", None),
            P("fsdp", None),
            P("fsdp", None),
            P("fsdp", None),
            P(None, "fsdp"),
        ),
        check_vma=False,
    )
```

```python
from functools import partial

import jax
import jax.numpy as jnp
from jax import lax
from jax.experimental import pallas as pl
from jax.experimental.pallas import tpu as pltpu
from jax.sharding import PartitionSpec as P

H = 8
KVH = 4
HD = 256
LMAX = 1024
PLANE = 8
QBLK = 128

EPSILON = 1e-06
SOFT_CAP = 50.0
AXIS = "fsdp"
F32 = jnp.float32
BF16 = jnp.bfloat16
MESH = pl.DeviceIdType.MESH
ANY = pl.BlockSpec(memory_space=pl.ANY)
VMEM = pl.BlockSpec(memory_space=pltpu.VMEM)
DMA = pltpu.SemaphoreType.DMA


def flip(index, step):
    return index + step - 2 * step * ((index // step) % 2)


PLANE_STEP = 4


def partner(index, bits, step):
    for bit, by in ((1, 1), (2, 2), (4, step)):
        if bits & bit:
            index = flip(index, by)
    return index


def place(device, step):
    return device % 4 + 4 * ((device // step) % 2)


def greet(peers):
    barrier = pltpu.get_barrier_semaphore()
    for peer in peers:
        pl.semaphore_signal(barrier, inc=1, device_id=(peer,), device_id_type=MESH)
    pl.semaphore_wait(barrier, len(peers))


class Copies:
    def __init__(self, send_sem, recv_sem):
        self.send_sem, self.recv_sem, self.made = send_sem, recv_sem, []

    def start(self, source, target, device):
        slot = len(self.made)
        copy = pltpu.make_async_remote_copy(
            src_ref=source,
            dst_ref=target,
            send_sem=self.send_sem.at[slot],
            recv_sem=self.recv_sem.at[slot],
            device_id=(device,),
            device_id_type=MESH,
        )
        copy.start()
        self.made.append(copy)
        return copy

    def sent(self):
        for copy in self.made:
            copy.wait_send()


def band(index, size):
    return pl.ds(pl.multiple_of(index * size, 8), size)


def lanes(index, size):
    return pl.ds(pl.multiple_of(index * size, 128), size)


def gather_steps(block_ref, full_ref, copies, own_sem, step):
    rows, width = block_ref.shape
    half = width // 2
    me = lax.axis_index(AXIS)
    sib, xn, yn = flip(me, 1), flip(me, 2), flip(me, step)
    diag = flip(xn, step)

    def at(device, side):
        return full_ref.at[band(place(device, step), rows), pl.ds(side * half, half)]

    def mine(side):
        return block_ref.at[:, pl.ds(side * half, half)]

    own_rows = full_ref.at[band(place(me, step), rows)]
    xa = copies.start(mine(0), at(me, 0), xn)
    ya = copies.start(mine(1), at(me, 1), yn)
    xb = copies.start(mine(1), at(me, 1), xn)
    yb = copies.start(mine(0), at(me, 0), yn)
    arriving = [copies.start(block_ref, own_rows, sib)]
    own = pltpu.make_async_copy(block_ref, own_rows, own_sem)
    own.start()

    def finish(on_rows=None):
        def to_sibling(device, side):
            arriving.append(copies.start(at(device, side), at(device, side), sib))

        def arrived(first, last, *devices):
            for copy in arriving[first:last]:
                copy.wait_recv()
            for device in devices:
                on_rows(device)

        if on_rows is not None:
            own.wait()
            arrived(0, 1, me)
        xa.wait_recv()
        yc = copies.start(at(xn, 0), at(xn, 0), yn)
        to_sibling(xn, 0)
        ya.wait_recv()
        xc = copies.start(at(yn, 1), at(yn, 1), xn)
        to_sibling(yn, 1)
        xb.wait_recv()
        to_sibling(xn, 1)
        yb.wait_recv()
        to_sibling(yn, 0)
        if on_rows is not None:
            arrived(1, 5, xn, yn)
        yc.wait_recv()
        to_sibling(diag, 0)
        xc.wait_recv()
        to_sibling(diag, 1)
        if on_rows is not None:
            arrived(5, 7, diag)
        else:
            arrived(0, 7)
            own.wait()

    return finish


GATHER_COPIES = 13


def cost(microseconds):
    return pl.CostEstimate(
        flops=int(microseconds * 1e7), transcendentals=0, bytes_accessed=int(microseconds * 3e4)
    )


def gather_kernel(block_ref, full_ref, own_sem, send_sem, recv_sem, *, step):
    me = lax.axis_index(AXIS)
    greet((flip(me, 1), flip(me, 2), flip(me, step)))
    copies = Copies(send_sem, recv_sem)
    gather_steps(block_ref, full_ref, copies, own_sem, step)()
    copies.sent()


def gather_square(block, step, collective_id):
    rows, width = block.shape
    return pl.pallas_call(
        partial(gather_kernel, step=step),
        out_shape=jax.ShapeDtypeStruct((PLANE * rows, width), block.dtype),
        in_specs=[ANY],
        out_specs=ANY,
        scratch_shapes=[DMA(()), DMA((GATHER_COPIES,)), DMA((GATHER_COPIES,))],
        compiler_params=pltpu.CompilerParams(collective_id=collective_id, has_side_effects=True),
        cost_estimate=cost(42),
        name="gather_square",
    )(block)


W_TILES = 2
SCATTER_COPIES = 14


def product_scatter_steps(
    left_refs, right_refs, left_bufs, right_bufs, buffers, load_sem, copies, offsets, step, beside=None
):
    both, got, ra, rb, ra2, rb2 = buffers
    pairs = len(left_refs)
    rows, width = got.shape[1:]
    half = width // 2
    tile = width // W_TILES
    chunk = 16
    me = lax.axis_index(AXIS)
    core = me % 2
    sib, xn, yn = flip(me, 1), flip(me, 2), flip(me, step)
    order = (flip(xn, step), xn, yn, me)
    first, second = pl.ds(0, half), pl.ds(half, half)

    def chip_rows(device):
        return pl.ds(pl.multiple_of((place(device, step) // 2) * 2 * rows, 16), 2 * rows)

    def right_load(j, t):
        r = pl.ds(t * tile, tile)
        source = right_refs[j].at[r, pl.ds(offsets[j], right_bufs[j].shape[1])]
        return pltpu.make_async_copy(source, right_bufs[j].at[r], load_sem.at[j, t])

    def left_load(j, i):
        r = chip_rows(order[i])
        return pltpu.make_async_copy(
            left_refs[j].at[r], left_bufs[j].at[r], load_sem.at[j, W_TILES + i]
        )

    for j in range(pairs):
        left_load(j, 0).start()
    for t in range(W_TILES):
        for j in range(pairs):
            right_load(j, t).start()
    for i in range(1, 4):
        for j in range(pairs):
            left_load(j, i).start()
    if beside is not None:
        beside[0]()
    greet((sib, xn, yn))

    def mine(i, cols):
        return both.at[i, band(core, rows), cols]

    def add(total, other):
        @pl.loop(0, rows // chunk)
        def _(k):
            r = pl.ds(pl.multiple_of(k * chunk, chunk), chunk)
            total[r] = (total[r].astype(F32) + other[r].astype(F32)).astype(total.dtype)

    loaded = set()

    def make(i, side):
        for j in range(pairs):
            if i not in loaded:
                left_load(j, i).wait()
            if i == 0:
                right_load(j, side).wait()
        loaded.add(i)
        r, cols = chip_rows(order[i]), pl.ds(side * half, half)
        total = None
        for j in range(pairs):
            term = contract_last(left_bufs[j][r], right_bufs[j][cols])
            total = term if total is None else total + term
        both[i, :, cols] = total.astype(BF16)
        return copies.start(both.at[i, band(1 - core, rows), cols], got.at[i, :, cols], sib)

    def merge(crossing, i, side):
        cols = pl.ds(side * half, half)
        crossing.wait_recv()
        add(mine(i, cols), got.at[i, :, cols])

    c0 = make(0, 0)
    c1 = make(0, 1)
    merge(c0, 0, 0)
    x0 = copies.start(mine(0, first), ra.at[0], xn)
    c2 = make(1, 0)
    merge(c1, 0, 1)
    y0 = copies.start(mine(0, second), rb.at[0], yn)
    c3 = make(2, 1)
    merge(c2, 1, 0)
    x1 = copies.start(mine(1, first), ra.at[1], xn)
    c4 = make(2, 0)
    merge(c3, 2, 1)
    y1 = copies.start(mine(2, second), rb.at[1], yn)
    c5 = make(1, 1)
    merge(c4, 2, 0)
    x0.wait_recv()
    add(mine(2, first), ra.at[0])
    y2 = copies.start(mine(2, first), ra2, yn)
    c6 = make(3, 0)
    merge(c5, 1, 1)
    y0.wait_recv()
    add(mine(1, second), rb.at[0])
    x2 = copies.start(mine(1, second), rb2, xn)
    c7 = make(3, 1)
    merge(c6, 3, 0)
    merge(c7, 3, 1)
    if beside is not None:
        beside[1]()
    for copy in (x1, y1, y2, x2):
        copy.wait_recv()
    own = both.at[3, band(core, rows)]

    def summed(r):
        return jnp.concatenate(
            [
                own[r, first].astype(F32) + ra[1, r].astype(F32) + ra2[r].astype(F32),
                own[r, second].astype(F32) + rb[1, r].astype(F32) + rb2[r].astype(F32),
            ],
            axis=1,
        )

    return summed


ROW_CHUNK = 16


def product_scatter_kernel(*refs, pairs, offsets, step):
    left_refs, right_refs, out_ref = refs[:pairs], refs[pairs : 2 * pairs], refs[2 * pairs]
    left_bufs = refs[2 * pairs + 1 : 3 * pairs + 1]
    right_bufs = refs[3 * pairs + 1 : 4 * pairs + 1]
    buffers, (load_sem, send_sem, recv_sem) = refs[4 * pairs + 1 : -3], refs[-3:]
    copies = Copies(send_sem, recv_sem)
    summed = product_scatter_steps(
        left_refs, right_refs, left_bufs, right_bufs, buffers, load_sem, copies, offsets, step
    )

    @pl.loop(0, out_ref.shape[0] // ROW_CHUNK)
    def _(k):
        r = pl.ds(pl.multiple_of(k * ROW_CHUNK, ROW_CHUNK), ROW_CHUNK)
        out_ref[r] = summed(r)

    copies.sent()


def scatter_buffers(rows, width):
    half = width // 2
    return [
        pltpu.VMEM((4, 2 * rows, width), BF16),
        pltpu.VMEM((4, rows, width), BF16),
        pltpu.VMEM((2, rows, half), BF16),
        pltpu.VMEM((2, rows, half), BF16),
        pltpu.VMEM((rows, half), BF16),
        pltpu.VMEM((rows, half), BF16),
    ]


def product_scatter(lefts, rights, offsets, step, collective_id):
    pairs = len(lefts)
    rows, width = lefts[0].shape[0] // PLANE, rights[0].shape[0]
    return pl.pallas_call(
        partial(product_scatter_kernel, pairs=pairs, offsets=offsets, step=step),
        out_shape=jax.ShapeDtypeStruct((rows, width), F32),
        in_specs=[ANY] * (2 * pairs),
        out_specs=VMEM,
        scratch_shapes=[
            *[pltpu.VMEM(value.shape, BF16) for value in lefts],
            *[pltpu.VMEM((width, value.shape[1]), BF16) for value in lefts],
            *scatter_buffers(rows, width),
            DMA((pairs, W_TILES + 4)),
            DMA((SCATTER_COPIES,)),
            DMA((SCATTER_COPIES,)),
        ],
        compiler_params=pltpu.CompilerParams(
            collective_id=collective_id, has_side_effects=True, vmem_limit_bytes=56 << 20
        ),
        cost_estimate=cost(50),
        name="product_scatter",
    )(*lefts, *rights)


BACK_TILE = 384


def back_kernel(*refs, pairs, offsets, step):
    left_refs, right_refs, rows_ref = refs[:pairs], refs[pairs : 2 * pairs], refs[2 * pairs]
    out_ref, term_ref = refs[2 * pairs + 1 : 2 * pairs + 3]
    scratch = refs[2 * pairs + 3 :]
    left_bufs, right_bufs = scratch[:pairs], scratch[pairs : 2 * pairs]
    rows_buf, stage = scratch[2 * pairs : 2 * pairs + 2]
    buffers = scratch[2 * pairs + 2 : -5]
    load_sem, rows_sem, store_sem, send_sem, recv_sem = scratch[-5:]
    copies = Copies(send_sem, recv_sem)
    rows_load = pltpu.make_async_copy(rows_ref, rows_buf, rows_sem)
    tiles = rows_ref.shape[1] // BACK_TILE
    width = left_refs[0].shape[1]

    def store(t):
        return pltpu.make_async_copy(
            stage.at[t % 2],
            term_ref.at[pl.ds(pl.multiple_of(t * BACK_TILE, 16), BACK_TILE)],
            store_sem.at[t % 2],
        )

    def beside():
        rows_load.wait()

        @pl.loop(0, tiles)
        def _(t):
            @pl.when(t >= 2)
            def _():
                store(t - 2).wait()

            columns = rows_buf[:, pl.ds(pl.multiple_of(t * BACK_TILE, BACK_TILE), BACK_TILE)]
            for j in range(pairs):
                term = contract_first(columns, left_bufs[j][...])
                stage[t % 2, :, pl.ds(j * width, width)] = term.astype(BF16)
            store(t).start()

    def start_rows():
        rows_load.start()

    summed = product_scatter_steps(
        left_refs,
        right_refs,
        left_bufs,
        right_bufs,
        buffers,
        load_sem,
        copies,
        offsets,
        step,
        (start_rows, beside),
    )

    @pl.loop(0, out_ref.shape[0] // ROW_CHUNK)
    def _(k):
        r = pl.ds(pl.multiple_of(k * ROW_CHUNK, ROW_CHUNK), ROW_CHUNK)
        out_ref[r] = summed(r)

    for t in range(tiles - 2, tiles):
        store(t).wait()
    copies.sent()


def product_scatter_back(lefts, rights, offsets, rows, step, collective_id):
    pairs = len(lefts)
    count, width = lefts[0].shape[0] // PLANE, rights[0].shape[0]
    columns = sum(value.shape[1] for value in lefts)
    return pl.pallas_call(
        partial(back_kernel, pairs=pairs, offsets=offsets, step=step),
        out_shape=(
            jax.ShapeDtypeStruct((count, width), F32),
            jax.ShapeDtypeStruct((rows.shape[1], columns), BF16),
        ),
        in_specs=[ANY] * (2 * pairs + 1),
        out_specs=(VMEM, ANY),
        scratch_shapes=[
            *[pltpu.VMEM(value.shape, BF16) for value in lefts],
            *[pltpu.VMEM((width, value.shape[1]), BF16) for value in lefts],
            pltpu.VMEM(rows.shape, BF16),
            pltpu.VMEM((2, BACK_TILE, columns), BF16),
            *scatter_buffers(count, width),
            DMA((pairs, W_TILES + 4)),
            DMA(()),
            DMA((2,)),
            DMA((SCATTER_COPIES,)),
            DMA((SCATTER_COPIES,)),
        ],
        compiler_params=pltpu.CompilerParams(
            collective_id=collective_id, has_side_effects=True, vmem_limit_bytes=62 << 20
        ),
        cost_estimate=cost(60),
        name="product_scatter_back",
    )(*lefts, *rights, rows)


TURN_TILE = 768


def turn_kernel(
    left_ref, right_ref, gain_ref, grad_ref, raw_ref, full_ref, term_ref, *refs, step
):
    left_buf, right_buf, gathered, total, grad_own = refs[:5]
    buffers, (load_sem, own_sem, store_sem, send_sem, recv_sem) = refs[5:-5], refs[-5:]
    rows, width = grad_ref.shape
    copies = Copies(send_sem, recv_sem)
    summed = product_scatter_steps(
        [left_ref], [right_ref], [left_buf], [right_buf], buffers, load_sem, copies, [0], step
    )
    gain = gain_ref[...]

    @pl.loop(0, rows // ROW_CHUNK)
    def _(k):
        r = pl.ds(pl.multiple_of(k * ROW_CHUNK, ROW_CHUNK), ROW_CHUNK)
        value = summed(r)
        raw_ref[r] = value
        scale = lax.rsqrt(jnp.mean(value * value, axis=1, keepdims=True) + EPSILON)
        scaled = (1.0 + gain) * grad_ref[r].astype(F32)
        inner = jnp.mean(value * scaled, axis=1, keepdims=True)
        grad_own[r] = (scale * scaled - value * (scale * scale * scale * inner)).astype(BF16)

    stores = []

    def on_rows(device):
        slot = len(stores)
        r = pl.ds(pl.multiple_of((place(device, step) // 2) * 2 * rows, 16), 2 * rows)
        store = pltpu.make_async_copy(gathered.at[r], full_ref.at[r], store_sem.at[slot])
        store.start()
        stores.append(store)
        right = left_buf[r]

        @pl.loop(0, width // TURN_TILE)
        def _(t):
            w = pl.ds(pl.multiple_of(t * TURN_TILE, TURN_TILE), TURN_TILE)
            term = contract_first(gathered[r, w], right)
            if slot == 0:
                total[w] = term
            elif slot < 3:
                total[w] += term
            else:
                right_buf[w] = (total[w] + term).astype(BF16)
                pltpu.make_async_copy(right_buf.at[w], term_ref.at[w], store_sem.at[4]).start()

    gather_steps(grad_own, gathered, copies, own_sem, step)(on_rows)
    pltpu.make_async_copy(right_buf, term_ref, store_sem.at[4]).wait()
    for store in stores:
        store.wait()
    copies.sent()


def turn(left, right, gain_row, grad, step, collective_id):
    rows, width = grad.shape
    count = SCATTER_COPIES + GATHER_COPIES
    return pl.pallas_call(
        partial(turn_kernel, step=step),
        out_shape=(
            jax.ShapeDtypeStruct((rows, width), F32),
            jax.ShapeDtypeStruct((PLANE * rows, width), BF16),
            jax.ShapeDtypeStruct((width, left.shape[1]), BF16),
        ),
        in_specs=[ANY, ANY, VMEM, VMEM],
        out_specs=(VMEM, ANY, ANY),
        scratch_shapes=[
            pltpu.VMEM(left.shape, BF16),
            pltpu.VMEM(right.shape, BF16),
            pltpu.VMEM((PLANE * rows, width), BF16),
            pltpu.VMEM((width, left.shape[1]), F32),
            pltpu.VMEM((rows, width), BF16),
            *scatter_buffers(rows, width),
            DMA((1, W_TILES + 4)),
            DMA(()),
            DMA((5,)),
            DMA((count,)),
            DMA((count,)),
        ],
        compiler_params=pltpu.CompilerParams(
            collective_id=collective_id, has_side_effects=True, vmem_limit_bytes=60 << 20
        ),
        cost_estimate=cost(50),
        name="turn",
    )(left, right, gain_row, grad)


def attn_columns(column):
    query_width = H * HD
    key_offset = query_width + (column % 2) * KVH * HD + (column // 2) * HD
    return (column * HD, key_offset, query_width + 2 * KVH * HD + column * HD)


def greet_all(peers):
    me = lax.axis_index(AXIS)
    barrier = pltpu.get_barrier_semaphore()

    @pl.loop(1, peers)
    def _(k):
        device = lax.rem(me + k, peers)
        pl.semaphore_signal(barrier, inc=1, device_id=(device,), device_id_type=MESH)

    pl.semaphore_wait(barrier, peers - 1)


def exchange_all(source_of, target_ref, send_sem, recv_sem):
    peers = target_ref.shape[0]
    me = lax.axis_index(AXIS)

    def copy(k):
        device = lax.rem(me + k, peers)
        return pltpu.make_async_remote_copy(
            src_ref=source_of(device),
            dst_ref=target_ref.at[me],
            send_sem=send_sem.at[k],
            recv_sem=recv_sem.at[k],
            device_id=(device,),
            device_id_type=MESH,
        )

    @pl.loop(1, peers)
    def _(k):
        copy(k).start()

    def finish():
        @pl.loop(1, peers)
        def _(k):
            copy(k).wait()

    return finish


ORDER = (6, 7, 2, 3, 4, 5, 1)


def swap_steps(pieces_of, targets, copies, own_sem, step):
    me = lax.axis_index(AXIS)
    moved = []
    for bits in ORDER:
        peer = partner(me, bits, step)
        for source, target in zip(pieces_of(place(peer, step)), targets):
            moved.append(copies.start(source, target, peer))
    owns = []
    for slot, (source, target) in enumerate(zip(pieces_of(place(me, step)), targets)):
        own = pltpu.make_async_copy(source, target, own_sem.at[slot])
        own.start()
        owns.append(own)

    def finish():
        for own in owns:
            own.wait()
        for copy in moved:
            copy.wait_recv()

    return finish


def square(step):
    me = lax.axis_index(AXIS)
    return [partner(me, bits, step) for bits in ORDER]


def wide(offset):
    return pl.ds(pl.multiple_of(offset, 128), HD)


class Line:
    def __init__(self, full_ref, send_sem, recv_sem):
        me = lax.axis_index(AXIS)
        self.full, self.planes = full_ref, full_ref.shape[0]
        self.send_sem, self.recv_sem = send_sem, recv_sem
        self.plane = me // PLANE
        peers = self.planes * PLANE
        self.devices = (lax.rem(me + PLANE, peers), lax.rem(me + peers - PLANE, peers))

    def copy(self, way, slot, source):
        return pltpu.make_async_remote_copy(
            src_ref=self.full.at[source],
            dst_ref=self.full.at[source],
            send_sem=self.send_sem.at[way, slot],
            recv_sem=self.recv_sem.at[way, slot],
            device_id=(self.devices[way],),
            device_id_type=MESH,
        )

    def sends(self, way, hop):
        if way == 0:
            source = self.plane - (hop - 1)
            return (self.plane + 1 < self.planes) & (source >= 0), source
        source = self.plane + (hop - 1)
        return (self.plane >= 1) & (source < self.planes), source

    def greet(self):
        barrier = pltpu.get_barrier_semaphore()
        count = 0
        for way, there in enumerate((self.plane + 1 < self.planes, self.plane >= 1)):

            @pl.when(there)
            def _():
                pl.semaphore_signal(
                    barrier, inc=1, device_id=(self.devices[way],), device_id_type=MESH
                )

            count = count + there.astype(jnp.int32)
        return count

    def start(self, hop, slot):
        for way in range(2):
            there, source = self.sends(way, hop)

            @pl.when(there)
            def _():
                self.copy(way, slot, source).start()

    def arrived(self, hop, slot):
        for way in range(2):
            source = self.plane - hop if way == 0 else self.plane + hop

            @pl.when((source >= 0) & (source < self.planes))
            def _():
                self.copy(way, slot, source).wait_recv()

    def sent(self, hop, slot):
        for way in range(2):
            there, source = self.sends(way, hop)

            @pl.when(there)
            def _():
                self.copy(way, slot, source).wait_send()


def line_hops(planes):
    hops = list(range(1, planes))
    first = (2 * len(hops) + 2) // 3
    return hops[:first], hops[first:]


def spread_attn_kernel(weights_ref, part_ref, own_sem, send_sem, recv_sem):
    me = lax.axis_index(AXIS)
    plane, here = me // PLANE, place(me, PLANE_STEP)
    greet(square(PLANE_STEP))
    copies = Copies(send_sem, recv_sem)
    swap_steps(
        lambda c: [weights_ref.at[:, wide(offset)] for offset in attn_columns(c)],
        [part_ref.at[plane, here, :, pl.ds(slot * HD, HD)] for slot in range(3)],
        copies,
        own_sem,
        PLANE_STEP,
    )()
    copies.sent()


def spread_attn(weights, planes):
    rows = weights.shape[0]
    return pl.pallas_call(
        spread_attn_kernel,
        out_shape=jax.ShapeDtypeStruct((planes, PLANE, rows, 3 * HD), BF16),
        in_specs=[ANY],
        out_specs=ANY,
        scratch_shapes=[DMA((3,)), DMA((21,)), DMA((21,))],
        compiler_params=pltpu.CompilerParams(collective_id=3, has_side_effects=True),
        name="spread_attn",
    )(weights)


def spread_gu_kernel(
    weights_ref,
    gain_ref,
    attn_in,
    gu_ref,
    gains_ref,
    attn_ref,
    own_sem,
    send_sem,
    recv_sem,
    gain_send,
    gain_recv,
    line_send,
    line_recv,
):
    peers = gains_ref.shape[0]
    ffc = gu_ref.shape[2] // 2
    me = lax.axis_index(AXIS)
    here = place(me, PLANE_STEP)
    line = Line(attn_ref, line_send, line_recv)
    hops = line_hops(line.planes)[0]
    greet_all(peers)
    line.start(hops[0], 0)
    gains_done = exchange_all(lambda device: gain_ref, gains_ref, gain_send, gain_recv)
    own = pltpu.make_async_copy(gain_ref, gains_ref.at[me], own_sem.at[2])
    own.start()
    copies = Copies(send_sem, recv_sem)
    spread = swap_steps(
        lambda c: [weights_ref.at[:, lanes(slot * PLANE + c, ffc)] for slot in range(2)],
        [gu_ref.at[here, :, pl.ds(slot * ffc, ffc)] for slot in range(2)],
        copies,
        own_sem,
        PLANE_STEP,
    )
    for slot, hop in enumerate(hops):
        line.arrived(hop, slot)
        if slot + 1 < len(hops):
            line.start(hop + 1, slot + 1)
    spread()
    own.wait()
    gains_done()
    for slot, hop in enumerate(hops):
        line.sent(hop, slot)
    copies.sent()


def spread_gu(weights, gain_block, attn_full, peers):
    rows = weights.shape[0]
    ffc = weights.shape[1] // 3 // PLANE
    hops = len(line_hops(attn_full.shape[0])[0])
    return pl.pallas_call(
        spread_gu_kernel,
        out_shape=(
            jax.ShapeDtypeStruct((PLANE, rows, 2 * ffc), BF16),
            jax.ShapeDtypeStruct((peers,) + gain_block.shape, gain_block.dtype),
            jax.ShapeDtypeStruct(attn_full.shape, attn_full.dtype),
        ),
        in_specs=[ANY, ANY, ANY],
        out_specs=(ANY, ANY, ANY),
        scratch_shapes=[
            DMA((3,)),
            DMA((14,)),
            DMA((14,)),
            DMA((peers,)),
            DMA((peers,)),
            DMA((2, hops)),
            DMA((2, hops)),
        ],
        input_output_aliases={2: 2},
        compiler_params=pltpu.CompilerParams(collective_id=4, has_side_effects=True),
        cost_estimate=cost(38),
        name="spread_gu",
    )(weights, gain_block, attn_full)


def spread_down_kernel(
    weights_ref,
    block_ref,
    attn_in,
    down_ref,
    full_ref,
    attn_ref,
    own_sem,
    send_sem,
    recv_sem,
    line_send,
    line_recv,
):
    ffc = down_ref.shape[2]
    me = lax.axis_index(AXIS)
    line = Line(attn_ref, line_send, line_recv)
    hops = line_hops(line.planes)[1]
    barrier = pltpu.get_barrier_semaphore()
    in_square = square(PLANE_STEP)
    for peer in in_square:
        pl.semaphore_signal(barrier, inc=1, device_id=(peer,), device_id_type=MESH)
    pl.semaphore_wait(barrier, len(in_square) + line.greet())
    line.start(hops[0], 0)
    copies = Copies(send_sem, recv_sem)
    gathered = gather_steps(block_ref, full_ref, copies, own_sem.at[1], PLANE_STEP)
    spread = swap_steps(
        lambda c: [weights_ref.at[:, lanes(2 * PLANE + c, ffc)]],
        [down_ref.at[place(me, PLANE_STEP)]],
        copies,
        own_sem,
        PLANE_STEP,
    )
    gathered()
    for slot, hop in enumerate(hops):
        line.arrived(hop, slot)
        if slot + 1 < len(hops):
            line.start(hop + 1, slot + 1)
    spread()
    for slot, hop in enumerate(hops):
        line.sent(hop, slot)
    copies.sent()


def spread_down(weights, block, attn_full):
    rows = weights.shape[0]
    ffc = weights.shape[1] // 3 // PLANE
    count = GATHER_COPIES + 7
    hops = len(line_hops(attn_full.shape[0])[1])
    return pl.pallas_call(
        spread_down_kernel,
        out_shape=(
            jax.ShapeDtypeStruct((PLANE, rows, ffc), BF16),
            jax.ShapeDtypeStruct((PLANE * block.shape[0], block.shape[1]), BF16),
            jax.ShapeDtypeStruct(attn_full.shape, attn_full.dtype),
        ),
        in_specs=[ANY, ANY, ANY],
        out_specs=(ANY, ANY, ANY),
        scratch_shapes=[
            DMA((2,)),
            DMA((count,)),
            DMA((count,)),
            DMA((2, hops)),
            DMA((2, hops)),
        ],
        input_output_aliases={2: 2},
        compiler_params=pltpu.CompilerParams(collective_id=5, has_side_effects=True),
        cost_estimate=cost(1),
        name="spread_down",
    )(weights, block, attn_full)


def collect_kernel(term_ref, rows_ref, own_sem, send_sem, recv_sem):
    here = place(lax.axis_index(AXIS), PLANE_STEP)
    count = own_sem.shape[0]
    ffc = term_ref.shape[2] // count
    greet(square(PLANE_STEP))
    copies = Copies(send_sem, recv_sem)
    swap_steps(
        lambda c: [term_ref.at[c, :, pl.ds(slot * ffc, ffc)] for slot in range(count)],
        [rows_ref.at[:, lanes(slot * PLANE + here, ffc)] for slot in range(count)],
        copies,
        own_sem,
        PLANE_STEP,
    )()
    copies.sent()


def collect(term, count, collective_id):
    rows, columns = term.shape[1:]
    return pl.pallas_call(
        collect_kernel,
        out_shape=jax.ShapeDtypeStruct((rows, PLANE * columns), BF16),
        in_specs=[ANY],
        out_specs=ANY,
        scratch_shapes=[DMA((count,)), DMA((7 * count,)), DMA((7 * count,))],
        compiler_params=pltpu.CompilerParams(collective_id=collective_id, has_side_effects=True),
        cost_estimate=cost(0.1),
        name="collect",
    )(term)


def collect_attn_kernel(term_ref, rows_ref, own_sem, send_sem, recv_sem):
    here = place(lax.axis_index(AXIS), PLANE_STEP)
    greet(square(PLANE_STEP))
    copies = Copies(send_sem, recv_sem)
    swap_steps(
        lambda c: [term_ref.at[c, :, pl.ds(slot * HD, HD)] for slot in range(3)],
        [rows_ref.at[:, wide(offset)] for offset in attn_columns(here)],
        copies,
        own_sem,
        PLANE_STEP,
    )()
    copies.sent()


def collect_attn(term):
    rows = term.shape[1]
    return pl.pallas_call(
        collect_attn_kernel,
        out_shape=jax.ShapeDtypeStruct((rows, PLANE * 3 * HD), BF16),
        in_specs=[ANY],
        out_specs=ANY,
        scratch_shapes=[DMA((3,)), DMA((21,)), DMA((21,))],
        compiler_params=pltpu.CompilerParams(collective_id=7, has_side_effects=True),
        name="collect_attn",
    )(term)


def collect_gains_kernel(gain_ref, gains_ref, own_sem, gain_send, gain_recv):
    me = lax.axis_index(AXIS)
    greet_all(gain_ref.shape[0])
    done = exchange_all(lambda device: gain_ref.at[device], gains_ref, gain_send, gain_recv)
    own = pltpu.make_async_copy(gain_ref.at[me], gains_ref.at[me], own_sem)
    own.start()
    own.wait()
    done()


def collect_gains(gain_blocks):
    peers = gain_blocks.shape[0]
    return pl.pallas_call(
        collect_gains_kernel,
        out_shape=jax.ShapeDtypeStruct(gain_blocks.shape, gain_blocks.dtype),
        in_specs=[ANY],
        out_specs=ANY,
        scratch_shapes=[DMA(()), DMA((peers,)), DMA((peers,))],
        compiler_params=pltpu.CompilerParams(collective_id=8, has_side_effects=True),
        name="collect_gains",
    )(gain_blocks)


def block_scores(q, k, start, first):
    scores = lax.dot_general(q, k, (((1,), (1,)), ((), ())), preferred_element_type=F32)
    bent = jnp.tanh(scores * (HD ** (-0.5) / SOFT_CAP))
    rows, span = scores.shape
    key_at = lax.broadcasted_iota(jnp.int32, (rows, span), 1)
    row_at = lax.broadcasted_iota(jnp.int32, (rows, span), 0)
    allowed = (key_at + first >= start) & (key_at <= row_at + LMAX)
    return (bent, jnp.where(allowed, jnp.exp(SOFT_CAP * bent), 0.0))


def attend_kernel(q_ref, k_ref, v_ref, start_ref, out_ref, inv_ref):
    first = pl.program_id(0) * QBLK
    keys = pl.ds(pl.multiple_of(first, QBLK), LMAX + QBLK)
    unused_bent, exponent = block_scores(q_ref[...], k_ref[keys], start_ref[...], first)
    inverse = 1.0 / jnp.sum(exponent, axis=-1, keepdims=True)
    weights = (exponent * inverse).astype(BF16)
    out_ref[...] = jnp.dot(weights, v_ref[keys], preferred_element_type=F32).astype(BF16)
    inv_ref[...] = inverse


def attend(queries, key_rows, value_rows, starts):
    rows = queries.shape[0]
    span = key_rows.shape[0]
    row_spec = pl.BlockSpec((QBLK, HD), lambda i: (i, 0))
    one_spec = pl.BlockSpec((QBLK, 1), lambda i: (i, 0))
    all_spec = pl.BlockSpec((span, HD), lambda i: (0, 0))
    return pl.pallas_call(
        attend_kernel,
        out_shape=(
            jax.ShapeDtypeStruct((rows, HD), BF16),
            jax.ShapeDtypeStruct((rows, 1), F32),
        ),
        grid=(rows // QBLK,),
        in_specs=[row_spec, all_spec, all_spec, one_spec],
        out_specs=(row_spec, one_spec),
        compiler_params=pltpu.CompilerParams(vmem_limit_bytes=40 << 20),
        cost_estimate=cost(1),
        name="attend",
    )(queries, key_rows, value_rows, starts)


GRAD_TILE = 256


def attn_grad_kernel(rows_ref, qkv_ref, proj_ref, attended_ref, out_ref):
    width = qkv_ref.shape[1]
    out_ref[:, pl.ds(0, width)] = contract_first(rows_ref[...], qkv_ref[...]).astype(BF16)
    out_ref[:, pl.ds(width, attended_ref.shape[1])] = contract_first(
        proj_ref[...], attended_ref[...]
    ).astype(BF16)


def attn_grad(rows, grad_qkv, grad_proj, attended):
    count, width = rows.shape
    columns = grad_qkv.shape[1] + attended.shape[1]
    tile = pl.BlockSpec((count, GRAD_TILE), lambda i: (0, i))
    return pl.pallas_call(
        attn_grad_kernel,
        out_shape=jax.ShapeDtypeStruct((width, columns), BF16),
        grid=(width // GRAD_TILE,),
        in_specs=[
            tile,
            pl.BlockSpec(grad_qkv.shape, lambda i: (0, 0)),
            tile,
            pl.BlockSpec(attended.shape, lambda i: (0, 0)),
        ],
        out_specs=pl.BlockSpec((GRAD_TILE, columns), lambda i: (i, 0)),
        compiler_params=pltpu.CompilerParams(vmem_limit_bytes=48 << 20),
        cost_estimate=cost(10),
        name="attn_grad",
    )(rows, grad_qkv, grad_proj, attended)


def attend_back_kernel(q_ref, k_ref, v_ref, start_ref, inv_ref, grad_ref, gq_ref, gk_ref, gv_ref):
    @pl.when(pl.program_id(0) == 0)
    def _():
        gk_ref[...] = jnp.zeros_like(gk_ref)
        gv_ref[...] = jnp.zeros_like(gv_ref)

    first = pl.program_id(0) * QBLK
    keys = pl.ds(pl.multiple_of(first, QBLK), LMAX + QBLK)
    q, k, v, grad = q_ref[...], k_ref[keys], v_ref[keys], grad_ref[...]
    bent, exponent = block_scores(q, k, start_ref[...], first)
    probability = exponent * inv_ref[...]
    grad_prob = lax.dot_general(grad, v, (((1,), (1,)), ((), ())), preferred_element_type=F32)
    inner = jnp.sum(probability * grad_prob, axis=-1, keepdims=True)
    grad_scores = (probability * (grad_prob - inner) * (1.0 - bent * bent)).astype(BF16)
    scale = HD ** (-0.5)
    gq_ref[...] = jnp.dot(grad_scores, k, preferred_element_type=F32) * scale
    over_rows = (((0,), (0,)), ((), ()))
    gk_ref[keys] += lax.dot_general(grad_scores, q, over_rows, preferred_element_type=F32) * scale
    gv_ref[keys] += lax.dot_general(
        probability.astype(BF16), grad, over_rows, preferred_element_type=F32
    )


def attend_back(queries, key_rows, value_rows, starts, inverse, grad):
    rows = queries.shape[0]
    span = key_rows.shape[0]
    row_spec = pl.BlockSpec((QBLK, HD), lambda i: (i, 0))
    one_spec = pl.BlockSpec((QBLK, 1), lambda i: (i, 0))
    all_spec = pl.BlockSpec((span, HD), lambda i: (0, 0))
    return pl.pallas_call(
        attend_back_kernel,
        out_shape=(
            jax.ShapeDtypeStruct((rows, HD), F32),
            jax.ShapeDtypeStruct((span, HD), F32),
            jax.ShapeDtypeStruct((span, HD), F32),
        ),
        grid=(rows // QBLK,),
        in_specs=[row_spec, all_spec, all_spec, one_spec, one_spec, row_spec],
        out_specs=(row_spec, all_spec, all_spec),
        compiler_params=pltpu.CompilerParams(vmem_limit_bytes=48 << 20),
        cost_estimate=cost(20),
        name="attend_back",
    )(queries, key_rows, value_rows, starts, inverse, grad)


def token_tables(seq_lengths, index_vec):
    count = seq_lengths.shape[0]
    order = jnp.arange(count, dtype=jnp.int32)
    seq_ends = jnp.sum(
        jnp.where(order[None, :] <= order[:, None], seq_lengths[None, :], 0), axis=1
    )
    after_end = index_vec[:, None] >= seq_ends[None, :]
    return index_vec - jnp.sum(jnp.where(after_end, seq_lengths[None, :], 0), axis=1)


def rms_parts(value):
    return lax.rsqrt(jnp.mean(value * value, axis=-1, keepdims=True) + EPSILON)


def rms_forward(value, gain_vec):
    return value * rms_parts(value) * (1.0 + gain_vec)


def rms_backward(value, gain_vec, grad):
    r = rms_parts(value)
    scaled = (1.0 + gain_vec) * grad
    inner = jnp.mean(value * scaled, axis=-1, keepdims=True)
    return (r * scaled - value * (r * r * r * inner), jnp.sum(grad * value * r, axis=0))


def rotate(value, cosine, sine_part):
    half_width = value.shape[-1] // 2
    first_half = value[..., :half_width]
    second_half = value[..., half_width:]
    return jnp.concatenate(
        [
            first_half * cosine - second_half * sine_part,
            second_half * cosine + first_half * sine_part,
        ],
        axis=-1,
    )


def contract_last(left_side, right_side):
    return lax.dot_general(
        left_side, right_side, (((1,), (1,)), ((), ())), preferred_element_type=F32
    )


def contract_first(left_side, right_side):
    return lax.dot_general(
        left_side, right_side, (((0,), (0,)), ((), ())), preferred_element_type=F32
    )


def matmul(left_side, right_side):
    return jnp.dot(left_side, right_side, preferred_element_type=F32)


def gelu_parts(gate):
    k0 = 0.7978845608028654
    k1 = 0.044715
    t = jnp.tanh(k0 * (gate + k1 * gate * gate * gate))
    value = 0.5 * gate * (1.0 + t)
    slope = 0.5 * (1.0 + t) + 0.5 * gate * (1.0 - t * t) * k0 * (1.0 + 3.0 * k1 * gate * gate)
    return (value, slope)


def local(tokens, attn_weights, mlp_weights, norm_gains, seq_lengths, cotangent):
    tok_rows, width = tokens.shape
    peers = lax.axis_size(AXIS)
    planes = peers // PLANE
    share = width // peers
    row_share = attn_weights.shape[0]
    ff = mlp_weights.shape[1] // 3
    ffc = ff // PLANE
    plane_rows = PLANE * tok_rows
    halo = LMAX
    across = [[p * PLANE + i for p in range(planes)] for i in range(PLANE)]
    sibling = [(i, i ^ 1) for i in range(peers)]
    to_next = [(i, i + PLANE) for i in range(peers - PLANE)]
    to_prev = [(i + PLANE, i) for i in range(peers - PLANE)]
    me = lax.axis_index(AXIS)
    is_even = (me % 2) == 0
    plane_start = (me // PLANE) * plane_rows

    def gather_across(value):
        return lax.all_gather(value, AXIS, axis=0, tiled=True, axis_index_groups=across)

    def scatter_across(value):
        part = lax.psum_scatter(
            value.astype(BF16), AXIS, scatter_dimension=0, tiled=True, axis_index_groups=across
        )
        return part.reshape(PLANE, -1, part.shape[1])

    gain_block = jnp.pad(norm_gains.astype(F32), ((0, 8 - 4), (0, -share % 128)))
    attn_full, gain_block = lax.optimization_barrier(
        (spread_attn(attn_weights, planes), gain_block)
    )
    gu_part, gain_blocks, attn_full = spread_gu(mlp_weights, gain_block, attn_full, peers)
    gain_full = gain_blocks[:, :4, :share].transpose(1, 0, 2).reshape(4, width)
    inputs = tokens.astype(F32)
    down_part, normed, attn_full = spread_down(
        mlp_weights, rms_forward(inputs, gain_full[0]).astype(BF16), attn_full
    )
    attn_cols = attn_full.reshape(width, 3 * HD)
    gu_cols = gather_across(gu_part.reshape(-1, 2 * ffc))
    down_cols = gather_across(down_part.reshape(-1, ffc))
    qkv_cols = attn_cols[:, : 2 * HD]
    out_cols = attn_cols[:, 2 * HD :]

    query_index = plane_start + jnp.arange(plane_rows, dtype=jnp.int32)
    position = token_tables(seq_lengths, query_index)
    starts = (jnp.arange(plane_rows, dtype=jnp.int32) + halo - position)[:, None]
    frequency = 10000.0 ** (-jnp.arange(HD // 2, dtype=F32) * 2.0 / HD)
    angles = position.astype(F32)[:, None] * frequency[None, :]
    cosine, sine_part = jnp.cos(angles), jnp.sin(angles)
    kv_cosine = jnp.where(is_even, cosine, 1.0)
    kv_sine = jnp.where(is_even, sine_part, 0.0)

    projected = matmul(normed, qkv_cols)
    queries = rotate(projected[:, :HD], cosine, sine_part).astype(BF16)
    kv_own = rotate(projected[:, HD:], kv_cosine, kv_sine).astype(BF16)
    kv_halo = lax.ppermute(kv_own[plane_rows - halo :], AXIS, to_next)
    kv_mine = jnp.concatenate([kv_halo, kv_own], axis=0)
    kv_other = lax.ppermute(kv_mine, AXIS, sibling)
    key_rows = jnp.where(is_even, kv_mine, kv_other)
    value_rows = jnp.where(is_even, kv_other, kv_mine)
    attended, inverse = attend(queries, key_rows, value_rows, starts)
    attn_proj = product_scatter([attended], [out_cols], [0], PLANE_STEP, 11)

    middle = inputs + rms_forward(attn_proj, gain_full[1])
    mid_low = gather_square(rms_forward(middle, gain_full[2]).astype(BF16), PLANE_STEP, 1)
    gate_up = matmul(mid_low, gu_cols)
    gate, up = gate_up[:, :ffc], gate_up[:, ffc:]
    gelu, slope = gelu_parts(gate)
    hidden = (gelu * up).astype(BF16)
    mlp_raw, grad_raw_low, down_grad = turn(
        hidden, down_cols, gain_full[3:4], cotangent, PLANE_STEP, 9
    )
    layer_output = (middle + rms_forward(mlp_raw, gain_full[3])).astype(BF16)

    grad_out = cotangent.astype(F32)
    gain_four = jnp.sum(grad_out * mlp_raw * rms_parts(mlp_raw), axis=0)
    down_term = scatter_across(down_grad)
    grad_hidden = matmul(grad_raw_low, down_cols)
    grad_normed_mid, gu_grad = product_scatter_back(
        [(slope * up * grad_hidden).astype(BF16), (gelu * grad_hidden).astype(BF16)],
        [gu_cols, gu_cols],
        [0, ffc],
        mid_low,
        PLANE_STEP,
        10,
    )
    gu_term = scatter_across(gu_grad)
    grad_mid_part, gain_three = rms_backward(middle, gain_full[2], grad_normed_mid)
    grad_middle = grad_out + grad_mid_part

    grad_proj, gain_two = rms_backward(attn_proj, gain_full[1], grad_middle)
    grad_proj_own, down_term = lax.optimization_barrier((grad_proj.astype(BF16), down_term))
    grad_proj_low = gather_square(grad_proj_own, PLANE_STEP, 1)
    grad_att = matmul(grad_proj_low, out_cols).astype(BF16)
    grad_query, grad_keys, grad_values = attend_back(
        queries, key_rows, value_rows, starts, inverse, grad_att
    )
    grad_mine = jnp.where(is_even, grad_keys, grad_values)
    grad_give = jnp.where(is_even, grad_values, grad_keys).astype(BF16)
    grad_kv = grad_mine + lax.ppermute(grad_give, AXIS, sibling).astype(F32)
    grad_back = lax.ppermute(grad_kv[:halo].astype(BF16), AXIS, to_prev).astype(F32)
    down_term, grad_kv = lax.optimization_barrier((down_term, grad_kv))
    down_rows = collect(down_term, 1, 6)
    down_rows, grad_back = lax.optimization_barrier((down_rows, grad_back))
    grad_kv = grad_kv[halo:] + jnp.pad(grad_back, ((plane_rows - halo, 0), (0, 0)))
    grad_qkv = jnp.concatenate(
        [
            rotate(grad_query, cosine, -sine_part).astype(BF16),
            rotate(grad_kv, kv_cosine, -kv_sine).astype(BF16),
        ],
        axis=1,
    )
    attn_term, grad_qkv = lax.optimization_barrier(
        (attn_grad(normed, grad_qkv, grad_proj_low, attended), grad_qkv)
    )
    attn_term = scatter_across(attn_term)
    grad_normed = product_scatter([grad_qkv], [qkv_cols], [0], PLANE_STEP, 12)
    grad_in_part, gain_one = rms_backward(inputs, gain_full[0], grad_normed)
    grad_tokens = (grad_middle + grad_in_part).astype(BF16)

    gain_term = jnp.stack([gain_one, gain_two, gain_three, gain_four], axis=0)
    gain_term = gain_term.reshape(4, peers, share).transpose(1, 0, 2)
    gain_term = jnp.pad(gain_term, ((0, 0), (0, 8 - 4), (0, -share % 128)))
    gain_recv = collect_gains(gain_term)
    gu_term, gain_recv = lax.optimization_barrier((gu_term, gain_recv))
    gu_rows = collect(gu_term, 2, 13)
    grad_mlp = jnp.concatenate([gu_rows, down_rows], axis=1).astype(F32)
    grad_mlp, attn_term = lax.optimization_barrier((grad_mlp, attn_term))
    grad_attn = collect_attn(attn_term).astype(F32)
    grad_gains = jnp.sum(gain_recv[:, :4, :share], axis=0)
    return (layer_output, grad_tokens, grad_attn, grad_mlp, grad_gains)


def solution(mesh):
    return jax.shard_map(
        local,
        mesh=mesh,
        in_specs=(
            P("fsdp", None),
            P("fsdp", None),
            P("fsdp", None),
            P(None, "fsdp"),
            P(),
            P("fsdp", None),
        ),
        out_specs=(
            P("fsdp", None),
            P("fsdp", None),
            P("fsdp", None),
            P("fsdp", None),
            P(None, "fsdp"),
        ),
        check_vma=False,
    )
```

```python
from functools import partial

import jax
import jax.numpy as jnp
from jax import lax
from jax.experimental import pallas as pl
from jax.experimental.pallas import tpu as pltpu
from jax.sharding import PartitionSpec as P

H = 8
KVH = 4
HD = 256
LMAX = 1024
PLANE = 8
QBLK = 128

EPSILON = 1e-06
SOFT_CAP = 50.0
AXIS = "fsdp"
F32 = jnp.float32
BF16 = jnp.bfloat16
MESH = pl.DeviceIdType.MESH
ANY = pl.BlockSpec(memory_space=pl.ANY)
VMEM = pl.BlockSpec(memory_space=pltpu.VMEM)
DMA = pltpu.SemaphoreType.DMA


def flip(index, step):
    return index + step - 2 * step * ((index // step) % 2)


PLANE_STEP = 4


def partner(index, bits, step):
    for bit, by in ((1, 1), (2, 2), (4, step)):
        if bits & bit:
            index = flip(index, by)
    return index


def place(device, step):
    return device % 4 + 4 * ((device // step) % 2)


def greet(peers):
    barrier = pltpu.get_barrier_semaphore()
    for peer in peers:
        pl.semaphore_signal(barrier, inc=1, device_id=(peer,), device_id_type=MESH)
    pl.semaphore_wait(barrier, len(peers))


class Copies:
    def __init__(self, send_sem, recv_sem):
        self.send_sem, self.recv_sem, self.made = send_sem, recv_sem, []

    def start(self, source, target, device):
        slot = len(self.made)
        copy = pltpu.make_async_remote_copy(
            src_ref=source,
            dst_ref=target,
            send_sem=self.send_sem.at[slot],
            recv_sem=self.recv_sem.at[slot],
            device_id=(device,),
            device_id_type=MESH,
        )
        copy.start()
        self.made.append(copy)
        return copy

    def sent(self):
        for copy in self.made:
            copy.wait_send()


def band(index, size):
    return pl.ds(pl.multiple_of(index * size, 8), size)


def lanes(index, size):
    return pl.ds(pl.multiple_of(index * size, 128), size)


def gather_steps(block_ref, full_ref, copies, own_sem, step):
    rows, width = block_ref.shape
    half = width // 2
    me = lax.axis_index(AXIS)
    sib, xn, yn = flip(me, 1), flip(me, 2), flip(me, step)
    diag = flip(xn, step)

    def at(device, side):
        return full_ref.at[band(place(device, step), rows), pl.ds(side * half, half)]

    def mine(side):
        return block_ref.at[:, pl.ds(side * half, half)]

    own_rows = full_ref.at[band(place(me, step), rows)]
    xa = copies.start(mine(0), at(me, 0), xn)
    ya = copies.start(mine(1), at(me, 1), yn)
    xb = copies.start(mine(1), at(me, 1), xn)
    yb = copies.start(mine(0), at(me, 0), yn)
    arriving = [copies.start(block_ref, own_rows, sib)]
    own = pltpu.make_async_copy(block_ref, own_rows, own_sem)
    own.start()

    def finish(on_rows=None):
        def to_sibling(device, side):
            arriving.append(copies.start(at(device, side), at(device, side), sib))

        def arrived(first, last, *devices):
            for copy in arriving[first:last]:
                copy.wait_recv()
            for device in devices:
                on_rows(device)

        if on_rows is not None:
            own.wait()
            arrived(0, 1, me)
        xa.wait_recv()
        yc = copies.start(at(xn, 0), at(xn, 0), yn)
        to_sibling(xn, 0)
        ya.wait_recv()
        xc = copies.start(at(yn, 1), at(yn, 1), xn)
        to_sibling(yn, 1)
        xb.wait_recv()
        to_sibling(xn, 1)
        yb.wait_recv()
        to_sibling(yn, 0)
        if on_rows is not None:
            arrived(1, 5, xn, yn)
        yc.wait_recv()
        to_sibling(diag, 0)
        xc.wait_recv()
        to_sibling(diag, 1)
        if on_rows is not None:
            arrived(5, 7, diag)
        else:
            arrived(0, 7)
            own.wait()

    return finish


GATHER_COPIES = 13


def cost(microseconds):
    return pl.CostEstimate(
        flops=int(microseconds * 1e7), transcendentals=0, bytes_accessed=int(microseconds * 3e4)
    )


def gather_kernel(block_ref, full_ref, own_sem, send_sem, recv_sem, *, step):
    me = lax.axis_index(AXIS)
    greet((flip(me, 1), flip(me, 2), flip(me, step)))
    copies = Copies(send_sem, recv_sem)
    gather_steps(block_ref, full_ref, copies, own_sem, step)()
    copies.sent()


def gather_square(block, step, collective_id):
    rows, width = block.shape
    return pl.pallas_call(
        partial(gather_kernel, step=step),
        out_shape=jax.ShapeDtypeStruct((PLANE * rows, width), block.dtype),
        in_specs=[ANY],
        out_specs=ANY,
        scratch_shapes=[DMA(()), DMA((GATHER_COPIES,)), DMA((GATHER_COPIES,))],
        compiler_params=pltpu.CompilerParams(collective_id=collective_id, has_side_effects=True),
        cost_estimate=cost(42),
        name="gather_square",
    )(block)


W_TILES = 2
SCATTER_COPIES = 14


def product_scatter_steps(
    left_refs, right_refs, left_bufs, right_bufs, buffers, load_sem, copies, offsets, step, beside=None
):
    both, got, ra, rb, ra2, rb2 = buffers
    pairs = len(left_refs)
    rows, width = got.shape[1:]
    half = width // 2
    tile = width // W_TILES
    chunk = 16
    me = lax.axis_index(AXIS)
    core = me % 2
    sib, xn, yn = flip(me, 1), flip(me, 2), flip(me, step)
    order = (flip(xn, step), xn, yn, me)
    first, second = pl.ds(0, half), pl.ds(half, half)

    def chip_rows(device):
        return pl.ds(pl.multiple_of((place(device, step) // 2) * 2 * rows, 16), 2 * rows)

    def right_load(j, t):
        r = pl.ds(t * tile, tile)
        source = right_refs[j].at[r, pl.ds(offsets[j], right_bufs[j].shape[1])]
        return pltpu.make_async_copy(source, right_bufs[j].at[r], load_sem.at[j, t])

    def left_load(j, i):
        r = chip_rows(order[i])
        return pltpu.make_async_copy(
            left_refs[j].at[r], left_bufs[j].at[r], load_sem.at[j, W_TILES + i]
        )

    for j in range(pairs):
        left_load(j, 0).start()
    for t in range(W_TILES):
        for j in range(pairs):
            right_load(j, t).start()
    for i in range(1, 4):
        for j in range(pairs):
            left_load(j, i).start()
    if beside is not None:
        beside[0]()
    greet((sib, xn, yn))

    def mine(i, cols):
        return both.at[i, band(core, rows), cols]

    def add(total, other):
        @pl.loop(0, rows // chunk)
        def _(k):
            r = pl.ds(pl.multiple_of(k * chunk, chunk), chunk)
            total[r] = (total[r].astype(F32) + other[r].astype(F32)).astype(total.dtype)

    loaded = set()

    def make(i, side):
        for j in range(pairs):
            if i not in loaded:
                left_load(j, i).wait()
            if i == 0:
                right_load(j, side).wait()
        loaded.add(i)
        r, cols = chip_rows(order[i]), pl.ds(side * half, half)
        total = None
        for j in range(pairs):
            term = contract_last(left_bufs[j][r], right_bufs[j][cols])
            total = term if total is None else total + term
        both[i, :, cols] = total.astype(BF16)
        return copies.start(both.at[i, band(1 - core, rows), cols], got.at[i, :, cols], sib)

    def merge(crossing, i, side):
        cols = pl.ds(side * half, half)
        crossing.wait_recv()
        add(mine(i, cols), got.at[i, :, cols])

    c0 = make(0, 0)
    c1 = make(0, 1)
    merge(c0, 0, 0)
    x0 = copies.start(mine(0, first), ra.at[0], xn)
    c2 = make(1, 0)
    merge(c1, 0, 1)
    y0 = copies.start(mine(0, second), rb.at[0], yn)
    c3 = make(2, 1)
    merge(c2, 1, 0)
    x1 = copies.start(mine(1, first), ra.at[1], xn)
    c4 = make(2, 0)
    merge(c3, 2, 1)
    y1 = copies.start(mine(2, second), rb.at[1], yn)
    c5 = make(1, 1)
    merge(c4, 2, 0)
    x0.wait_recv()
    add(mine(2, first), ra.at[0])
    y2 = copies.start(mine(2, first), ra2, yn)
    c6 = make(3, 0)
    merge(c5, 1, 1)
    y0.wait_recv()
    add(mine(1, second), rb.at[0])
    x2 = copies.start(mine(1, second), rb2, xn)
    c7 = make(3, 1)
    merge(c6, 3, 0)
    merge(c7, 3, 1)
    if beside is not None:
        beside[1]()
    for copy in (x1, y1, y2, x2):
        copy.wait_recv()
    own = both.at[3, band(core, rows)]

    def summed(r):
        return jnp.concatenate(
            [
                own[r, first].astype(F32) + ra[1, r].astype(F32) + ra2[r].astype(F32),
                own[r, second].astype(F32) + rb[1, r].astype(F32) + rb2[r].astype(F32),
            ],
            axis=1,
        )

    return summed


ROW_CHUNK = 16


def product_scatter_kernel(*refs, pairs, offsets, step):
    left_refs, right_refs, out_ref = refs[:pairs], refs[pairs : 2 * pairs], refs[2 * pairs]
    left_bufs = refs[2 * pairs + 1 : 3 * pairs + 1]
    right_bufs = refs[3 * pairs + 1 : 4 * pairs + 1]
    buffers, (load_sem, send_sem, recv_sem) = refs[4 * pairs + 1 : -3], refs[-3:]
    copies = Copies(send_sem, recv_sem)
    summed = product_scatter_steps(
        left_refs, right_refs, left_bufs, right_bufs, buffers, load_sem, copies, offsets, step
    )

    @pl.loop(0, out_ref.shape[0] // ROW_CHUNK)
    def _(k):
        r = pl.ds(pl.multiple_of(k * ROW_CHUNK, ROW_CHUNK), ROW_CHUNK)
        out_ref[r] = summed(r)

    copies.sent()


def scatter_buffers(rows, width):
    half = width // 2
    return [
        pltpu.VMEM((4, 2 * rows, width), BF16),
        pltpu.VMEM((4, rows, width), BF16),
        pltpu.VMEM((2, rows, half), BF16),
        pltpu.VMEM((2, rows, half), BF16),
        pltpu.VMEM((rows, half), BF16),
        pltpu.VMEM((rows, half), BF16),
    ]


def product_scatter(lefts, rights, offsets, step, collective_id):
    pairs = len(lefts)
    rows, width = lefts[0].shape[0] // PLANE, rights[0].shape[0]
    return pl.pallas_call(
        partial(product_scatter_kernel, pairs=pairs, offsets=offsets, step=step),
        out_shape=jax.ShapeDtypeStruct((rows, width), F32),
        in_specs=[ANY] * (2 * pairs),
        out_specs=VMEM,
        scratch_shapes=[
            *[pltpu.VMEM(value.shape, BF16) for value in lefts],
            *[pltpu.VMEM((width, value.shape[1]), BF16) for value in lefts],
            *scatter_buffers(rows, width),
            DMA((pairs, W_TILES + 4)),
            DMA((SCATTER_COPIES,)),
            DMA((SCATTER_COPIES,)),
        ],
        compiler_params=pltpu.CompilerParams(
            collective_id=collective_id, has_side_effects=True, vmem_limit_bytes=56 << 20
        ),
        cost_estimate=cost(50),
        name="product_scatter",
    )(*lefts, *rights)


BACK_TILE = 384


def back_kernel(*refs, pairs, offsets, step):
    left_refs, right_refs, rows_ref = refs[:pairs], refs[pairs : 2 * pairs], refs[2 * pairs]
    out_ref, term_ref = refs[2 * pairs + 1 : 2 * pairs + 3]
    scratch = refs[2 * pairs + 3 :]
    left_bufs, right_bufs = scratch[:pairs], scratch[pairs : 2 * pairs]
    rows_buf, stage = scratch[2 * pairs : 2 * pairs + 2]
    buffers = scratch[2 * pairs + 2 : -5]
    load_sem, rows_sem, store_sem, send_sem, recv_sem = scratch[-5:]
    copies = Copies(send_sem, recv_sem)
    rows_load = pltpu.make_async_copy(rows_ref, rows_buf, rows_sem)
    tiles = rows_ref.shape[1] // BACK_TILE
    width = left_refs[0].shape[1]

    def store(t):
        return pltpu.make_async_copy(
            stage.at[t % 2],
            term_ref.at[pl.ds(pl.multiple_of(t * BACK_TILE, 16), BACK_TILE)],
            store_sem.at[t % 2],
        )

    def beside():
        rows_load.wait()

        @pl.loop(0, tiles)
        def _(t):
            @pl.when(t >= 2)
            def _():
                store(t - 2).wait()

            columns = rows_buf[:, pl.ds(pl.multiple_of(t * BACK_TILE, BACK_TILE), BACK_TILE)]
            for j in range(pairs):
                term = contract_first(columns, left_bufs[j][...])
                stage[t % 2, :, pl.ds(j * width, width)] = term.astype(BF16)
            store(t).start()

    def start_rows():
        rows_load.start()

    summed = product_scatter_steps(
        left_refs,
        right_refs,
        left_bufs,
        right_bufs,
        buffers,
        load_sem,
        copies,
        offsets,
        step,
        (start_rows, beside),
    )

    @pl.loop(0, out_ref.shape[0] // ROW_CHUNK)
    def _(k):
        r = pl.ds(pl.multiple_of(k * ROW_CHUNK, ROW_CHUNK), ROW_CHUNK)
        out_ref[r] = summed(r)

    for t in range(tiles - 2, tiles):
        store(t).wait()
    copies.sent()


def product_scatter_back(lefts, rights, offsets, rows, step, collective_id):
    pairs = len(lefts)
    count, width = lefts[0].shape[0] // PLANE, rights[0].shape[0]
    columns = sum(value.shape[1] for value in lefts)
    return pl.pallas_call(
        partial(back_kernel, pairs=pairs, offsets=offsets, step=step),
        out_shape=(
            jax.ShapeDtypeStruct((count, width), F32),
            jax.ShapeDtypeStruct((rows.shape[1], columns), BF16),
        ),
        in_specs=[ANY] * (2 * pairs + 1),
        out_specs=(VMEM, ANY),
        scratch_shapes=[
            *[pltpu.VMEM(value.shape, BF16) for value in lefts],
            *[pltpu.VMEM((width, value.shape[1]), BF16) for value in lefts],
            pltpu.VMEM(rows.shape, BF16),
            pltpu.VMEM((2, BACK_TILE, columns), BF16),
            *scatter_buffers(count, width),
            DMA((pairs, W_TILES + 4)),
            DMA(()),
            DMA((2,)),
            DMA((SCATTER_COPIES,)),
            DMA((SCATTER_COPIES,)),
        ],
        compiler_params=pltpu.CompilerParams(
            collective_id=collective_id, has_side_effects=True, vmem_limit_bytes=62 << 20
        ),
        cost_estimate=cost(60),
        name="product_scatter_back",
    )(*lefts, *rights, rows)


TURN_TILE = 768


def turn_kernel(
    left_ref, right_ref, gain_ref, grad_ref, raw_ref, full_ref, term_ref, *refs, step
):
    left_buf, right_buf, gathered, total, grad_own = refs[:5]
    buffers, (load_sem, own_sem, store_sem, send_sem, recv_sem) = refs[5:-5], refs[-5:]
    rows, width = grad_ref.shape
    copies = Copies(send_sem, recv_sem)
    summed = product_scatter_steps(
        [left_ref], [right_ref], [left_buf], [right_buf], buffers, load_sem, copies, [0], step
    )
    gain = gain_ref[...]

    @pl.loop(0, rows // ROW_CHUNK)
    def _(k):
        r = pl.ds(pl.multiple_of(k * ROW_CHUNK, ROW_CHUNK), ROW_CHUNK)
        value = summed(r)
        raw_ref[r] = value
        scale = lax.rsqrt(jnp.mean(value * value, axis=1, keepdims=True) + EPSILON)
        scaled = (1.0 + gain) * grad_ref[r].astype(F32)
        inner = jnp.mean(value * scaled, axis=1, keepdims=True)
        grad_own[r] = (scale * scaled - value * (scale * scale * scale * inner)).astype(BF16)

    stores = []

    def on_rows(device):
        slot = len(stores)
        r = pl.ds(pl.multiple_of((place(device, step) // 2) * 2 * rows, 16), 2 * rows)
        store = pltpu.make_async_copy(gathered.at[r], full_ref.at[r], store_sem.at[slot])
        store.start()
        stores.append(store)
        right = left_buf[r]

        @pl.loop(0, width // TURN_TILE)
        def _(t):
            w = pl.ds(pl.multiple_of(t * TURN_TILE, TURN_TILE), TURN_TILE)
            term = contract_first(gathered[r, w], right)
            if slot == 0:
                total[w] = term
            elif slot < 3:
                total[w] += term
            else:
                right_buf[w] = (total[w] + term).astype(BF16)
                pltpu.make_async_copy(right_buf.at[w], term_ref.at[w], store_sem.at[4]).start()

    gather_steps(grad_own, gathered, copies, own_sem, step)(on_rows)
    pltpu.make_async_copy(right_buf, term_ref, store_sem.at[4]).wait()
    for store in stores:
        store.wait()
    copies.sent()


def turn(left, right, gain_row, grad, step, collective_id):
    rows, width = grad.shape
    count = SCATTER_COPIES + GATHER_COPIES
    return pl.pallas_call(
        partial(turn_kernel, step=step),
        out_shape=(
            jax.ShapeDtypeStruct((rows, width), F32),
            jax.ShapeDtypeStruct((PLANE * rows, width), BF16),
            jax.ShapeDtypeStruct((width, left.shape[1]), BF16),
        ),
        in_specs=[ANY, ANY, VMEM, VMEM],
        out_specs=(VMEM, ANY, ANY),
        scratch_shapes=[
            pltpu.VMEM(left.shape, BF16),
            pltpu.VMEM(right.shape, BF16),
            pltpu.VMEM((PLANE * rows, width), BF16),
            pltpu.VMEM((width, left.shape[1]), F32),
            pltpu.VMEM((rows, width), BF16),
            *scatter_buffers(rows, width),
            DMA((1, W_TILES + 4)),
            DMA(()),
            DMA((5,)),
            DMA((count,)),
            DMA((count,)),
        ],
        compiler_params=pltpu.CompilerParams(
            collective_id=collective_id, has_side_effects=True, vmem_limit_bytes=60 << 20
        ),
        cost_estimate=cost(50),
        name="turn",
    )(left, right, gain_row, grad)


def attn_columns(column):
    query_width = H * HD
    key_offset = query_width + (column % 2) * KVH * HD + (column // 2) * HD
    return (column * HD, key_offset, query_width + 2 * KVH * HD + column * HD)


def greet_all(peers):
    me = lax.axis_index(AXIS)
    barrier = pltpu.get_barrier_semaphore()

    @pl.loop(1, peers)
    def _(k):
        device = lax.rem(me + k, peers)
        pl.semaphore_signal(barrier, inc=1, device_id=(device,), device_id_type=MESH)

    pl.semaphore_wait(barrier, peers - 1)


def exchange_all(source_of, target_ref, send_sem, recv_sem):
    peers = target_ref.shape[0]
    me = lax.axis_index(AXIS)

    def copy(k):
        device = lax.rem(me + k, peers)
        return pltpu.make_async_remote_copy(
            src_ref=source_of(device),
            dst_ref=target_ref.at[me],
            send_sem=send_sem.at[k],
            recv_sem=recv_sem.at[k],
            device_id=(device,),
            device_id_type=MESH,
        )

    @pl.loop(1, peers)
    def _(k):
        copy(k).start()

    def finish():
        @pl.loop(1, peers)
        def _(k):
            copy(k).wait()

    return finish


ORDER = (6, 7, 2, 3, 4, 5, 1)


def swap_steps(pieces_of, targets, copies, own_sem, step):
    me = lax.axis_index(AXIS)
    moved = []
    for bits in ORDER:
        peer = partner(me, bits, step)
        for source, target in zip(pieces_of(place(peer, step)), targets):
            moved.append(copies.start(source, target, peer))
    owns = []
    for slot, (source, target) in enumerate(zip(pieces_of(place(me, step)), targets)):
        own = pltpu.make_async_copy(source, target, own_sem.at[slot])
        own.start()
        owns.append(own)

    def finish():
        for own in owns:
            own.wait()
        for copy in moved:
            copy.wait_recv()

    return finish


def square(step):
    me = lax.axis_index(AXIS)
    return [partner(me, bits, step) for bits in ORDER]


def wide(offset):
    return pl.ds(pl.multiple_of(offset, 128), HD)


class Line:
    def __init__(self, full_ref, send_sem, recv_sem, own_ref=None):
        me = lax.axis_index(AXIS)
        self.own = own_ref
        self.full, self.planes = full_ref, full_ref.shape[0]
        self.send_sem, self.recv_sem = send_sem, recv_sem
        self.plane = me // PLANE
        peers = self.planes * PLANE
        self.devices = (lax.rem(me + PLANE, peers), lax.rem(me + peers - PLANE, peers))

    def copy(self, way, slot, source, first=False):
        return pltpu.make_async_remote_copy(
            src_ref=self.own if first and self.own is not None else self.full.at[source],
            dst_ref=self.full.at[source],
            send_sem=self.send_sem.at[way, slot],
            recv_sem=self.recv_sem.at[way, slot],
            device_id=(self.devices[way],),
            device_id_type=MESH,
        )

    def sends(self, way, hop):
        if way == 0:
            source = self.plane - (hop - 1)
            return (self.plane + 1 < self.planes) & (source >= 0), source
        source = self.plane + (hop - 1)
        return (self.plane >= 1) & (source < self.planes), source

    def greet(self):
        barrier = pltpu.get_barrier_semaphore()
        count = 0
        for way, there in enumerate((self.plane + 1 < self.planes, self.plane >= 1)):

            @pl.when(there)
            def _():
                pl.semaphore_signal(
                    barrier, inc=1, device_id=(self.devices[way],), device_id_type=MESH
                )

            count = count + there.astype(jnp.int32)
        return count

    def start(self, hop, slot):
        for way in range(2):
            there, source = self.sends(way, hop)

            @pl.when(there)
            def _():
                self.copy(way, slot, source, hop == 1).start()

    def arrived(self, hop, slot):
        for way in range(2):
            source = self.plane - hop if way == 0 else self.plane + hop

            @pl.when((source >= 0) & (source < self.planes))
            def _():
                self.copy(way, slot, source).wait_recv()

    def sent(self, hop, slot):
        for way in range(2):
            there, source = self.sends(way, hop)

            @pl.when(there)
            def _():
                self.copy(way, slot, source, hop == 1).wait_send()

    def begin(self, hops):
        if hops:
            self.start(hops[0], 0)

    def run(self, hops):
        for slot, hop in enumerate(hops):
            self.arrived(hop, slot)
            if slot + 1 < len(hops):
                self.start(hop + 1, slot + 1)

    def end(self, hops):
        for slot, hop in enumerate(hops):
            self.sent(hop, slot)


def line_hops(planes):
    hops = list(range(1, planes))
    first = (2 * len(hops) + 2) // 3
    return hops[:first], hops[first:]


def line_semaphores(planes, part):
    count = max(1, len(line_hops(planes)[part]))
    return [DMA((2, count)), DMA((2, count))]


def greet_line(line, peers):
    barrier = pltpu.get_barrier_semaphore()
    for peer in peers:
        pl.semaphore_signal(barrier, inc=1, device_id=(peer,), device_id_type=MESH)
    pl.semaphore_wait(barrier, len(peers) + line.greet())


def spread_attn_kernel(
    weights_ref, qkv_ref, rows_ref, own_sem, send_sem, recv_sem, line_send, line_recv
):
    me = lax.axis_index(AXIS)
    plane, here = me // PLANE, place(me, PLANE_STEP)
    out_rows = weights_ref.at[:, pl.ds((H + 2 * KVH) * HD, H * HD)]
    line = Line(rows_ref, line_send, line_recv, out_rows)
    hops = line_hops(line.planes)[0]
    greet_line(line, square(PLANE_STEP))
    line.begin(hops)
    own = pltpu.make_async_copy(out_rows, rows_ref.at[plane], own_sem.at[2])
    own.start()
    copies = Copies(send_sem, recv_sem)
    spread = swap_steps(
        lambda c: [weights_ref.at[:, wide(offset)] for offset in attn_columns(c)[:2]],
        [qkv_ref.at[plane, here, :, pl.ds(slot * HD, HD)] for slot in range(2)],
        copies,
        own_sem,
        PLANE_STEP,
    )
    line.run(hops)
    spread()
    own.wait()
    line.end(hops)
    copies.sent()


def spread_attn(weights, planes):
    rows = weights.shape[0]
    return pl.pallas_call(
        spread_attn_kernel,
        out_shape=(
            jax.ShapeDtypeStruct((planes, PLANE, rows, 2 * HD), BF16),
            jax.ShapeDtypeStruct((planes, rows, H * HD), BF16),
        ),
        in_specs=[ANY],
        out_specs=(ANY, ANY),
        scratch_shapes=[DMA((3,)), DMA((14,)), DMA((14,)), *line_semaphores(planes, 0)],
        compiler_params=pltpu.CompilerParams(collective_id=3, has_side_effects=True),
        name="spread_attn",
    )(weights)


def spread_gu_kernel(
    weights_ref,
    gain_ref,
    qkv_in,
    rows_in,
    gu_ref,
    gains_ref,
    qkv_ref,
    rows_ref,
    own_sem,
    send_sem,
    recv_sem,
    gain_send,
    gain_recv,
    qkv_send,
    qkv_recv,
    rows_send,
    rows_recv,
):
    peers = gains_ref.shape[0]
    ffc = gu_ref.shape[2] // 2
    me = lax.axis_index(AXIS)
    here = place(me, PLANE_STEP)
    qkv_line = Line(qkv_ref, qkv_send, qkv_recv)
    rows_line = Line(rows_ref, rows_send, rows_recv)
    qkv_hops, rows_hops = line_hops(qkv_line.planes)
    greet_all(peers)
    rows_line.begin(rows_hops)
    qkv_line.begin(qkv_hops)
    gains_done = exchange_all(lambda device: gain_ref, gains_ref, gain_send, gain_recv)
    own = pltpu.make_async_copy(gain_ref, gains_ref.at[me], own_sem.at[2])
    own.start()
    copies = Copies(send_sem, recv_sem)
    spread = swap_steps(
        lambda c: [weights_ref.at[:, lanes(slot * PLANE + c, ffc)] for slot in range(2)],
        [gu_ref.at[here, :, pl.ds(slot * ffc, ffc)] for slot in range(2)],
        copies,
        own_sem,
        PLANE_STEP,
    )
    rows_line.run(rows_hops)
    qkv_line.run(qkv_hops)
    spread()
    own.wait()
    gains_done()
    rows_line.end(rows_hops)
    qkv_line.end(qkv_hops)
    copies.sent()


def spread_gu(weights, gain_block, qkv_full, rows_full, peers):
    rows = weights.shape[0]
    ffc = weights.shape[1] // 3 // PLANE
    planes = qkv_full.shape[0]
    return pl.pallas_call(
        spread_gu_kernel,
        out_shape=(
            jax.ShapeDtypeStruct((PLANE, rows, 2 * ffc), BF16),
            jax.ShapeDtypeStruct((peers,) + gain_block.shape, gain_block.dtype),
            jax.ShapeDtypeStruct(qkv_full.shape, qkv_full.dtype),
            jax.ShapeDtypeStruct(rows_full.shape, rows_full.dtype),
        ),
        in_specs=[ANY, ANY, ANY, ANY],
        out_specs=(ANY, ANY, ANY, ANY),
        scratch_shapes=[
            DMA((3,)),
            DMA((14,)),
            DMA((14,)),
            DMA((peers,)),
            DMA((peers,)),
            *line_semaphores(planes, 0),
            *line_semaphores(planes, 1),
        ],
        input_output_aliases={2: 2, 3: 3},
        compiler_params=pltpu.CompilerParams(collective_id=4, has_side_effects=True),
        cost_estimate=cost(38),
        name="spread_gu",
    )(weights, gain_block, qkv_full, rows_full)


def spread_down_kernel(
    weights_ref,
    block_ref,
    qkv_in,
    rows_ref,
    down_ref,
    full_ref,
    qkv_ref,
    out_ref,
    own_sem,
    send_sem,
    recv_sem,
    line_send,
    line_recv,
):
    ffc = down_ref.shape[2]
    here = place(lax.axis_index(AXIS), PLANE_STEP)
    line = Line(qkv_ref, line_send, line_recv)
    hops = line_hops(line.planes)[1]
    greet_line(line, square(PLANE_STEP))
    line.begin(hops)
    copies = Copies(send_sem, recv_sem)
    gathered = gather_steps(block_ref, full_ref, copies, own_sem.at[2], PLANE_STEP)
    spread = swap_steps(
        lambda c: [
            rows_ref.at[:, :, lanes(c, HD)],
            weights_ref.at[:, lanes(2 * PLANE + c, ffc)],
        ],
        [out_ref.at[:, here], down_ref.at[here]],
        copies,
        own_sem,
        PLANE_STEP,
    )
    gathered()
    line.run(hops)
    spread()
    line.end(hops)
    copies.sent()


def spread_down(weights, block, qkv_full, rows_full):
    rows = weights.shape[0]
    ffc = weights.shape[1] // 3 // PLANE
    planes = qkv_full.shape[0]
    count = GATHER_COPIES + 14
    return pl.pallas_call(
        spread_down_kernel,
        out_shape=(
            jax.ShapeDtypeStruct((PLANE, rows, ffc), BF16),
            jax.ShapeDtypeStruct((PLANE * block.shape[0], block.shape[1]), BF16),
            jax.ShapeDtypeStruct(qkv_full.shape, qkv_full.dtype),
            jax.ShapeDtypeStruct((planes, PLANE, rows, HD), BF16),
        ),
        in_specs=[ANY, ANY, ANY, ANY],
        out_specs=(ANY, ANY, ANY, ANY),
        scratch_shapes=[
            DMA((3,)),
            DMA((count,)),
            DMA((count,)),
            *line_semaphores(planes, 1),
        ],
        input_output_aliases={2: 2},
        compiler_params=pltpu.CompilerParams(collective_id=5, has_side_effects=True),
        cost_estimate=cost(1),
        name="spread_down",
    )(weights, block, qkv_full, rows_full)


def collect_kernel(term_ref, rows_ref, own_sem, send_sem, recv_sem):
    here = place(lax.axis_index(AXIS), PLANE_STEP)
    count = own_sem.shape[0]
    ffc = term_ref.shape[2] // count
    greet(square(PLANE_STEP))
    copies = Copies(send_sem, recv_sem)
    swap_steps(
        lambda c: [term_ref.at[c, :, pl.ds(slot * ffc, ffc)] for slot in range(count)],
        [rows_ref.at[:, lanes(slot * PLANE + here, ffc)] for slot in range(count)],
        copies,
        own_sem,
        PLANE_STEP,
    )()
    copies.sent()


def collect(term, count, collective_id):
    rows, columns = term.shape[1:]
    return pl.pallas_call(
        collect_kernel,
        out_shape=jax.ShapeDtypeStruct((rows, PLANE * columns), BF16),
        in_specs=[ANY],
        out_specs=ANY,
        scratch_shapes=[DMA((count,)), DMA((7 * count,)), DMA((7 * count,))],
        compiler_params=pltpu.CompilerParams(collective_id=collective_id, has_side_effects=True),
        cost_estimate=cost(0.1),
        name="collect",
    )(term)


def collect_attn_kernel(term_ref, rows_ref, own_sem, send_sem, recv_sem):
    here = place(lax.axis_index(AXIS), PLANE_STEP)
    greet(square(PLANE_STEP))
    copies = Copies(send_sem, recv_sem)
    swap_steps(
        lambda c: [term_ref.at[c, :, pl.ds(slot * HD, HD)] for slot in range(3)],
        [rows_ref.at[:, wide(offset)] for offset in attn_columns(here)],
        copies,
        own_sem,
        PLANE_STEP,
    )()
    copies.sent()


def collect_attn(term):
    rows = term.shape[1]
    return pl.pallas_call(
        collect_attn_kernel,
        out_shape=jax.ShapeDtypeStruct((rows, PLANE * 3 * HD), BF16),
        in_specs=[ANY],
        out_specs=ANY,
        scratch_shapes=[DMA((3,)), DMA((21,)), DMA((21,))],
        compiler_params=pltpu.CompilerParams(collective_id=7, has_side_effects=True),
        name="collect_attn",
    )(term)


def collect_gains_kernel(gain_ref, gains_ref, own_sem, gain_send, gain_recv):
    me = lax.axis_index(AXIS)
    greet_all(gain_ref.shape[0])
    done = exchange_all(lambda device: gain_ref.at[device], gains_ref, gain_send, gain_recv)
    own = pltpu.make_async_copy(gain_ref.at[me], gains_ref.at[me], own_sem)
    own.start()
    own.wait()
    done()


def collect_gains(gain_blocks):
    peers = gain_blocks.shape[0]
    return pl.pallas_call(
        collect_gains_kernel,
        out_shape=jax.ShapeDtypeStruct(gain_blocks.shape, gain_blocks.dtype),
        in_specs=[ANY],
        out_specs=ANY,
        scratch_shapes=[DMA(()), DMA((peers,)), DMA((peers,))],
        compiler_params=pltpu.CompilerParams(collective_id=8, has_side_effects=True),
        name="collect_gains",
    )(gain_blocks)


def block_scores(q, k, start, first):
    scores = lax.dot_general(q, k, (((1,), (1,)), ((), ())), preferred_element_type=F32)
    bent = jnp.tanh(scores * (HD ** (-0.5) / SOFT_CAP))
    rows, span = scores.shape
    key_at = lax.broadcasted_iota(jnp.int32, (rows, span), 1)
    row_at = lax.broadcasted_iota(jnp.int32, (rows, span), 0)
    allowed = (key_at + first >= start) & (key_at <= row_at + LMAX)
    return (bent, jnp.where(allowed, jnp.exp(SOFT_CAP * bent), 0.0))


def attend_kernel(q_ref, k_ref, v_ref, start_ref, out_ref, inv_ref):
    first = pl.program_id(0) * QBLK
    keys = pl.ds(pl.multiple_of(first, QBLK), LMAX + QBLK)
    unused_bent, exponent = block_scores(q_ref[...], k_ref[keys], start_ref[...], first)
    inverse = 1.0 / jnp.sum(exponent, axis=-1, keepdims=True)
    weights = (exponent * inverse).astype(BF16)
    out_ref[...] = jnp.dot(weights, v_ref[keys], preferred_element_type=F32).astype(BF16)
    inv_ref[...] = inverse


def attend(queries, key_rows, value_rows, starts):
    rows = queries.shape[0]
    span = key_rows.shape[0]
    row_spec = pl.BlockSpec((QBLK, HD), lambda i: (i, 0))
    one_spec = pl.BlockSpec((QBLK, 1), lambda i: (i, 0))
    all_spec = pl.BlockSpec((span, HD), lambda i: (0, 0))
    return pl.pallas_call(
        attend_kernel,
        out_shape=(
            jax.ShapeDtypeStruct((rows, HD), BF16),
            jax.ShapeDtypeStruct((rows, 1), F32),
        ),
        grid=(rows // QBLK,),
        in_specs=[row_spec, all_spec, all_spec, one_spec],
        out_specs=(row_spec, one_spec),
        compiler_params=pltpu.CompilerParams(vmem_limit_bytes=40 << 20),
        cost_estimate=cost(1),
        name="attend",
    )(queries, key_rows, value_rows, starts)


GRAD_TILE = 256


def attn_grad_kernel(rows_ref, qkv_ref, proj_ref, attended_ref, out_ref):
    width = qkv_ref.shape[1]
    out_ref[:, pl.ds(0, width)] = contract_first(rows_ref[...], qkv_ref[...]).astype(BF16)
    out_ref[:, pl.ds(width, attended_ref.shape[1])] = contract_first(
        proj_ref[...], attended_ref[...]
    ).astype(BF16)


def attn_grad(rows, grad_qkv, grad_proj, attended):
    count, width = rows.shape
    columns = grad_qkv.shape[1] + attended.shape[1]
    tile = pl.BlockSpec((count, GRAD_TILE), lambda i: (0, i))
    return pl.pallas_call(
        attn_grad_kernel,
        out_shape=jax.ShapeDtypeStruct((width, columns), BF16),
        grid=(width // GRAD_TILE,),
        in_specs=[
            tile,
            pl.BlockSpec(grad_qkv.shape, lambda i: (0, 0)),
            tile,
            pl.BlockSpec(attended.shape, lambda i: (0, 0)),
        ],
        out_specs=pl.BlockSpec((GRAD_TILE, columns), lambda i: (i, 0)),
        compiler_params=pltpu.CompilerParams(vmem_limit_bytes=48 << 20),
        cost_estimate=cost(10),
        name="attn_grad",
    )(rows, grad_qkv, grad_proj, attended)


def attend_back_kernel(q_ref, k_ref, v_ref, start_ref, inv_ref, grad_ref, gq_ref, gk_ref, gv_ref):
    @pl.when(pl.program_id(0) == 0)
    def _():
        gk_ref[...] = jnp.zeros_like(gk_ref)
        gv_ref[...] = jnp.zeros_like(gv_ref)

    first = pl.program_id(0) * QBLK
    keys = pl.ds(pl.multiple_of(first, QBLK), LMAX + QBLK)
    q, k, v, grad = q_ref[...], k_ref[keys], v_ref[keys], grad_ref[...]
    bent, exponent = block_scores(q, k, start_ref[...], first)
    probability = exponent * inv_ref[...]
    grad_prob = lax.dot_general(grad, v, (((1,), (1,)), ((), ())), preferred_element_type=F32)
    inner = jnp.sum(probability * grad_prob, axis=-1, keepdims=True)
    grad_scores = (probability * (grad_prob - inner) * (1.0 - bent * bent)).astype(BF16)
    scale = HD ** (-0.5)
    gq_ref[...] = jnp.dot(grad_scores, k, preferred_element_type=F32) * scale
    over_rows = (((0,), (0,)), ((), ()))
    gk_ref[keys] += lax.dot_general(grad_scores, q, over_rows, preferred_element_type=F32) * scale
    gv_ref[keys] += lax.dot_general(
        probability.astype(BF16), grad, over_rows, preferred_element_type=F32
    )


def attend_back(queries, key_rows, value_rows, starts, inverse, grad):
    rows = queries.shape[0]
    span = key_rows.shape[0]
    row_spec = pl.BlockSpec((QBLK, HD), lambda i: (i, 0))
    one_spec = pl.BlockSpec((QBLK, 1), lambda i: (i, 0))
    all_spec = pl.BlockSpec((span, HD), lambda i: (0, 0))
    return pl.pallas_call(
        attend_back_kernel,
        out_shape=(
            jax.ShapeDtypeStruct((rows, HD), F32),
            jax.ShapeDtypeStruct((span, HD), F32),
            jax.ShapeDtypeStruct((span, HD), F32),
        ),
        grid=(rows // QBLK,),
        in_specs=[row_spec, all_spec, all_spec, one_spec, one_spec, row_spec],
        out_specs=(row_spec, all_spec, all_spec),
        compiler_params=pltpu.CompilerParams(vmem_limit_bytes=48 << 20),
        cost_estimate=cost(20),
        name="attend_back",
    )(queries, key_rows, value_rows, starts, inverse, grad)


def token_tables(seq_lengths, index_vec):
    count = seq_lengths.shape[0]
    order = jnp.arange(count, dtype=jnp.int32)
    seq_ends = jnp.sum(
        jnp.where(order[None, :] <= order[:, None], seq_lengths[None, :], 0), axis=1
    )
    after_end = index_vec[:, None] >= seq_ends[None, :]
    return index_vec - jnp.sum(jnp.where(after_end, seq_lengths[None, :], 0), axis=1)


def rms_parts(value):
    return lax.rsqrt(jnp.mean(value * value, axis=-1, keepdims=True) + EPSILON)


def rms_forward(value, gain_vec):
    return value * rms_parts(value) * (1.0 + gain_vec)


def rms_backward(value, gain_vec, grad):
    r = rms_parts(value)
    scaled = (1.0 + gain_vec) * grad
    inner = jnp.mean(value * scaled, axis=-1, keepdims=True)
    return (r * scaled - value * (r * r * r * inner), jnp.sum(grad * value * r, axis=0))


def rotate(value, cosine, sine_part):
    half_width = value.shape[-1] // 2
    first_half = value[..., :half_width]
    second_half = value[..., half_width:]
    return jnp.concatenate(
        [
            first_half * cosine - second_half * sine_part,
            second_half * cosine + first_half * sine_part,
        ],
        axis=-1,
    )


def contract_last(left_side, right_side):
    return lax.dot_general(
        left_side, right_side, (((1,), (1,)), ((), ())), preferred_element_type=F32
    )


def contract_first(left_side, right_side):
    return lax.dot_general(
        left_side, right_side, (((0,), (0,)), ((), ())), preferred_element_type=F32
    )


def matmul(left_side, right_side):
    return jnp.dot(left_side, right_side, preferred_element_type=F32)


def gelu_parts(gate):
    k0 = 0.7978845608028654
    k1 = 0.044715
    t = jnp.tanh(k0 * (gate + k1 * gate * gate * gate))
    value = 0.5 * gate * (1.0 + t)
    slope = 0.5 * (1.0 + t) + 0.5 * gate * (1.0 - t * t) * k0 * (1.0 + 3.0 * k1 * gate * gate)
    return (value, slope)


def local(tokens, attn_weights, mlp_weights, norm_gains, seq_lengths, cotangent):
    tok_rows, width = tokens.shape
    peers = lax.axis_size(AXIS)
    planes = peers // PLANE
    share = width // peers
    row_share = attn_weights.shape[0]
    ff = mlp_weights.shape[1] // 3
    ffc = ff // PLANE
    plane_rows = PLANE * tok_rows
    halo = LMAX
    across = [[p * PLANE + i for p in range(planes)] for i in range(PLANE)]
    sibling = [(i, i ^ 1) for i in range(peers)]
    to_next = [(i, i + PLANE) for i in range(peers - PLANE)]
    to_prev = [(i + PLANE, i) for i in range(peers - PLANE)]
    me = lax.axis_index(AXIS)
    is_even = (me % 2) == 0
    plane_start = (me // PLANE) * plane_rows

    def gather_across(value):
        return lax.all_gather(value, AXIS, axis=0, tiled=True, axis_index_groups=across)

    def scatter_across(value):
        part = lax.psum_scatter(
            value.astype(BF16), AXIS, scatter_dimension=0, tiled=True, axis_index_groups=across
        )
        return part.reshape(PLANE, -1, part.shape[1])

    qkv_full, rows_full, gain_rows = lax.optimization_barrier(
        (*spread_attn(attn_weights, planes), norm_gains)
    )
    gain_block = jnp.pad(gain_rows.astype(F32), ((0, 8 - 4), (0, -share % 128)))
    gu_part, gain_blocks, qkv_full, rows_full = spread_gu(
        mlp_weights, gain_block, qkv_full, rows_full, peers
    )
    gain_full = gain_blocks[:, :4, :share].transpose(1, 0, 2).reshape(4, width)
    inputs = tokens.astype(F32)
    down_part, normed, qkv_full, out_full = spread_down(
        mlp_weights, rms_forward(inputs, gain_full[0]).astype(BF16), qkv_full, rows_full
    )
    qkv_cols = qkv_full.reshape(width, 2 * HD)
    out_cols = out_full.reshape(width, HD)
    gu_cols = gather_across(gu_part.reshape(-1, 2 * ffc))
    down_cols = gather_across(down_part.reshape(-1, ffc))

    query_index = plane_start + jnp.arange(plane_rows, dtype=jnp.int32)
    position = token_tables(seq_lengths, query_index)
    starts = (jnp.arange(plane_rows, dtype=jnp.int32) + halo - position)[:, None]
    frequency = 10000.0 ** (-jnp.arange(HD // 2, dtype=F32) * 2.0 / HD)
    angles = position.astype(F32)[:, None] * frequency[None, :]
    cosine, sine_part = jnp.cos(angles), jnp.sin(angles)
    kv_cosine = jnp.where(is_even, cosine, 1.0)
    kv_sine = jnp.where(is_even, sine_part, 0.0)

    projected = matmul(normed, qkv_cols)
    queries = rotate(projected[:, :HD], cosine, sine_part).astype(BF16)
    kv_own = rotate(projected[:, HD:], kv_cosine, kv_sine).astype(BF16)
    kv_halo = lax.ppermute(kv_own[plane_rows - halo :], AXIS, to_next)
    kv_mine = jnp.concatenate([kv_halo, kv_own], axis=0)
    kv_other = lax.ppermute(kv_mine, AXIS, sibling)
    key_rows = jnp.where(is_even, kv_mine, kv_other)
    value_rows = jnp.where(is_even, kv_other, kv_mine)
    attended, inverse = attend(queries, key_rows, value_rows, starts)
    attn_proj = product_scatter([attended], [out_cols], [0], PLANE_STEP, 11)

    middle = inputs + rms_forward(attn_proj, gain_full[1])
    mid_low = gather_square(rms_forward(middle, gain_full[2]).astype(BF16), PLANE_STEP, 1)
    gate_up = matmul(mid_low, gu_cols)
    gate, up = gate_up[:, :ffc], gate_up[:, ffc:]
    gelu, slope = gelu_parts(gate)
    hidden = (gelu * up).astype(BF16)
    mlp_raw, grad_raw_low, down_grad = turn(
        hidden, down_cols, gain_full[3:4], cotangent, PLANE_STEP, 9
    )
    layer_output = (middle + rms_forward(mlp_raw, gain_full[3])).astype(BF16)

    grad_out = cotangent.astype(F32)
    gain_four = jnp.sum(grad_out * mlp_raw * rms_parts(mlp_raw), axis=0)
    down_term = scatter_across(down_grad)
    grad_hidden = matmul(grad_raw_low, down_cols)
    grad_normed_mid, gu_grad = product_scatter_back(
        [(slope * up * grad_hidden).astype(BF16), (gelu * grad_hidden).astype(BF16)],
        [gu_cols, gu_cols],
        [0, ffc],
        mid_low,
        PLANE_STEP,
        10,
    )
    gu_term = scatter_across(gu_grad)
    grad_mid_part, gain_three = rms_backward(middle, gain_full[2], grad_normed_mid)
    grad_middle = grad_out + grad_mid_part

    grad_proj, gain_two = rms_backward(attn_proj, gain_full[1], grad_middle)
    grad_proj_own, down_term = lax.optimization_barrier((grad_proj.astype(BF16), down_term))
    grad_proj_low = gather_square(grad_proj_own, PLANE_STEP, 1)
    grad_att = matmul(grad_proj_low, out_cols).astype(BF16)
    grad_query, grad_keys, grad_values = attend_back(
        queries, key_rows, value_rows, starts, inverse, grad_att
    )
    grad_mine = jnp.where(is_even, grad_keys, grad_values)
    grad_give = jnp.where(is_even, grad_values, grad_keys).astype(BF16)
    grad_kv = grad_mine + lax.ppermute(grad_give, AXIS, sibling).astype(F32)
    grad_back = lax.ppermute(grad_kv[:halo].astype(BF16), AXIS, to_prev).astype(F32)
    down_term, grad_kv = lax.optimization_barrier((down_term, grad_kv))
    down_rows = collect(down_term, 1, 6)
    down_rows, grad_back = lax.optimization_barrier((down_rows, grad_back))
    grad_kv = grad_kv[halo:] + jnp.pad(grad_back, ((plane_rows - halo, 0), (0, 0)))
    grad_qkv = jnp.concatenate(
        [
            rotate(grad_query, cosine, -sine_part).astype(BF16),
            rotate(grad_kv, kv_cosine, -kv_sine).astype(BF16),
        ],
        axis=1,
    )
    attn_term, grad_qkv = lax.optimization_barrier(
        (attn_grad(normed, grad_qkv, grad_proj_low, attended), grad_qkv)
    )
    attn_term = scatter_across(attn_term)
    grad_normed = product_scatter([grad_qkv], [qkv_cols], [0], PLANE_STEP, 12)
    grad_in_part, gain_one = rms_backward(inputs, gain_full[0], grad_normed)
    grad_tokens = (grad_middle + grad_in_part).astype(BF16)

    gain_term = jnp.stack([gain_one, gain_two, gain_three, gain_four], axis=0)
    gain_term = gain_term.reshape(4, peers, share).transpose(1, 0, 2)
    gain_term = jnp.pad(gain_term, ((0, 0), (0, 8 - 4), (0, -share % 128)))
    gain_recv = collect_gains(gain_term)
    gu_term, gain_recv = lax.optimization_barrier((gu_term, gain_recv))
    gu_rows = collect(gu_term, 2, 13)
    grad_mlp = jnp.concatenate([gu_rows, down_rows], axis=1).astype(F32)
    grad_mlp, attn_term = lax.optimization_barrier((grad_mlp, attn_term))
    grad_attn = collect_attn(attn_term).astype(F32)
    grad_gains = jnp.sum(gain_recv[:, :4, :share], axis=0)
    return (layer_output, grad_tokens, grad_attn, grad_mlp, grad_gains)


def solution(mesh):
    return jax.shard_map(
        local,
        mesh=mesh,
        in_specs=(
            P("fsdp", None),
            P("fsdp", None),
            P("fsdp", None),
            P(None, "fsdp"),
            P(),
            P("fsdp", None),
        ),
        out_specs=(
            P("fsdp", None),
            P("fsdp", None),
            P("fsdp", None),
            P("fsdp", None),
            P(None, "fsdp"),
        ),
        check_vma=False,
    )
```

```python
from functools import partial

import jax
import jax.numpy as jnp
from jax import lax
from jax.experimental import pallas as pl
from jax.experimental.pallas import tpu as pltpu
from jax.sharding import PartitionSpec as P

H = 8
KVH = 4
HD = 256
LMAX = 1024
PLANE = 8
QBLK = 128

EPSILON = 1e-06
SOFT_CAP = 50.0
AXIS = "fsdp"
F32 = jnp.float32
BF16 = jnp.bfloat16
MESH = pl.DeviceIdType.MESH
ANY = pl.BlockSpec(memory_space=pl.ANY)
VMEM = pl.BlockSpec(memory_space=pltpu.VMEM)
DMA = pltpu.SemaphoreType.DMA


def flip(index, step):
    return index + step - 2 * step * ((index // step) % 2)


PLANE_STEP = 4


def partner(index, bits, step):
    for bit, by in ((1, 1), (2, 2), (4, step)):
        if bits & bit:
            index = flip(index, by)
    return index


def place(device, step):
    return device % 4 + 4 * ((device // step) % 2)


def greet(peers):
    barrier = pltpu.get_barrier_semaphore()
    for peer in peers:
        pl.semaphore_signal(barrier, inc=1, device_id=(peer,), device_id_type=MESH)
    pl.semaphore_wait(barrier, len(peers))


class Copies:
    def __init__(self, send_sem, recv_sem):
        self.send_sem, self.recv_sem, self.made = send_sem, recv_sem, []

    def start(self, source, target, device):
        slot = len(self.made)
        copy = pltpu.make_async_remote_copy(
            src_ref=source,
            dst_ref=target,
            send_sem=self.send_sem.at[slot],
            recv_sem=self.recv_sem.at[slot],
            device_id=(device,),
            device_id_type=MESH,
        )
        copy.start()
        self.made.append(copy)
        return copy

    def sent(self):
        for copy in self.made:
            copy.wait_send()


def band(index, size):
    return pl.ds(pl.multiple_of(index * size, 8), size)


def lanes(index, size):
    return pl.ds(pl.multiple_of(index * size, 128), size)


def gather_steps(block_ref, full_ref, copies, own_sem, step):
    rows, width = block_ref.shape
    half = width // 2
    me = lax.axis_index(AXIS)
    sib, xn, yn = flip(me, 1), flip(me, 2), flip(me, step)
    diag = flip(xn, step)

    def at(device, side):
        return full_ref.at[band(place(device, step), rows), pl.ds(side * half, half)]

    def mine(side):
        return block_ref.at[:, pl.ds(side * half, half)]

    own_rows = full_ref.at[band(place(me, step), rows)]
    xa = copies.start(mine(0), at(me, 0), xn)
    ya = copies.start(mine(1), at(me, 1), yn)
    xb = copies.start(mine(1), at(me, 1), xn)
    yb = copies.start(mine(0), at(me, 0), yn)
    arriving = [copies.start(block_ref, own_rows, sib)]
    own = pltpu.make_async_copy(block_ref, own_rows, own_sem)
    own.start()

    def finish(on_rows=None):
        def to_sibling(device, side):
            arriving.append(copies.start(at(device, side), at(device, side), sib))

        def arrived(first, last, *devices):
            for copy in arriving[first:last]:
                copy.wait_recv()
            for device in devices:
                on_rows(device)

        if on_rows is not None:
            own.wait()
            arrived(0, 1, me)
        xa.wait_recv()
        yc = copies.start(at(xn, 0), at(xn, 0), yn)
        to_sibling(xn, 0)
        ya.wait_recv()
        xc = copies.start(at(yn, 1), at(yn, 1), xn)
        to_sibling(yn, 1)
        xb.wait_recv()
        to_sibling(xn, 1)
        yb.wait_recv()
        to_sibling(yn, 0)
        if on_rows is not None:
            arrived(1, 5, xn, yn)
        yc.wait_recv()
        to_sibling(diag, 0)
        xc.wait_recv()
        to_sibling(diag, 1)
        if on_rows is not None:
            arrived(5, 7, diag)
        else:
            arrived(0, 7)
            own.wait()

    return finish


GATHER_COPIES = 13


def cost(microseconds):
    return pl.CostEstimate(
        flops=int(microseconds * 1e7), transcendentals=0, bytes_accessed=int(microseconds * 3e4)
    )


def gather_kernel(block_ref, full_ref, own_sem, send_sem, recv_sem, *, step):
    me = lax.axis_index(AXIS)
    greet((flip(me, 1), flip(me, 2), flip(me, step)))
    copies = Copies(send_sem, recv_sem)
    gather_steps(block_ref, full_ref, copies, own_sem, step)()
    copies.sent()


def gather_square(block, step, collective_id):
    rows, width = block.shape
    return pl.pallas_call(
        partial(gather_kernel, step=step),
        out_shape=jax.ShapeDtypeStruct((PLANE * rows, width), block.dtype),
        in_specs=[ANY],
        out_specs=ANY,
        scratch_shapes=[DMA(()), DMA((GATHER_COPIES,)), DMA((GATHER_COPIES,))],
        compiler_params=pltpu.CompilerParams(collective_id=collective_id, has_side_effects=True),
        cost_estimate=cost(42),
        name="gather_square",
    )(block)


W_TILES = 2
SCATTER_COPIES = 14


def product_scatter_steps(
    left_refs, right_refs, left_bufs, right_bufs, buffers, load_sem, copies, offsets, step, beside=None
):
    both, got, ra, rb, ra2, rb2 = buffers
    pairs = len(left_refs)
    rows, width = got.shape[1:]
    half = width // 2
    tile = width // W_TILES
    chunk = 16
    me = lax.axis_index(AXIS)
    core = me % 2
    sib, xn, yn = flip(me, 1), flip(me, 2), flip(me, step)
    order = (flip(xn, step), xn, yn, me)
    first, second = pl.ds(0, half), pl.ds(half, half)

    def chip_rows(device):
        return pl.ds(pl.multiple_of((place(device, step) // 2) * 2 * rows, 16), 2 * rows)

    def right_load(j, t):
        r = pl.ds(t * tile, tile)
        source = right_refs[j].at[r, pl.ds(offsets[j], right_bufs[j].shape[1])]
        return pltpu.make_async_copy(source, right_bufs[j].at[r], load_sem.at[j, t])

    def left_load(j, i):
        r = chip_rows(order[i])
        return pltpu.make_async_copy(
            left_refs[j].at[r], left_bufs[j].at[r], load_sem.at[j, W_TILES + i]
        )

    for j in range(pairs):
        left_load(j, 0).start()
    for t in range(W_TILES):
        for j in range(pairs):
            right_load(j, t).start()
    for i in range(1, 4):
        for j in range(pairs):
            left_load(j, i).start()
    if beside is not None:
        beside[0]()
    greet((sib, xn, yn))

    def mine(i, cols):
        return both.at[i, band(core, rows), cols]

    def add(total, other):
        @pl.loop(0, rows // chunk)
        def _(k):
            r = pl.ds(pl.multiple_of(k * chunk, chunk), chunk)
            total[r] = (total[r].astype(F32) + other[r].astype(F32)).astype(total.dtype)

    loaded = set()

    def make(i, side):
        for j in range(pairs):
            if i not in loaded:
                left_load(j, i).wait()
            if i == 0:
                right_load(j, side).wait()
        loaded.add(i)
        r, cols = chip_rows(order[i]), pl.ds(side * half, half)
        total = None
        for j in range(pairs):
            term = contract_last(left_bufs[j][r], right_bufs[j][cols])
            total = term if total is None else total + term
        both[i, :, cols] = total.astype(BF16)
        return copies.start(both.at[i, band(1 - core, rows), cols], got.at[i, :, cols], sib)

    def merge(crossing, i, side):
        cols = pl.ds(side * half, half)
        crossing.wait_recv()
        add(mine(i, cols), got.at[i, :, cols])

    c0 = make(0, 0)
    c1 = make(0, 1)
    merge(c0, 0, 0)
    x0 = copies.start(mine(0, first), ra.at[0], xn)
    c2 = make(1, 0)
    merge(c1, 0, 1)
    y0 = copies.start(mine(0, second), rb.at[0], yn)
    c3 = make(2, 1)
    merge(c2, 1, 0)
    x1 = copies.start(mine(1, first), ra.at[1], xn)
    c4 = make(2, 0)
    merge(c3, 2, 1)
    y1 = copies.start(mine(2, second), rb.at[1], yn)
    c5 = make(1, 1)
    merge(c4, 2, 0)
    x0.wait_recv()
    add(mine(2, first), ra.at[0])
    y2 = copies.start(mine(2, first), ra2, yn)
    c6 = make(3, 0)
    merge(c5, 1, 1)
    y0.wait_recv()
    add(mine(1, second), rb.at[0])
    x2 = copies.start(mine(1, second), rb2, xn)
    c7 = make(3, 1)
    merge(c6, 3, 0)
    merge(c7, 3, 1)
    if beside is not None:
        beside[1]()
    for copy in (x1, y1, y2, x2):
        copy.wait_recv()
    own = both.at[3, band(core, rows)]

    def summed(r):
        return jnp.concatenate(
            [
                own[r, first].astype(F32) + ra[1, r].astype(F32) + ra2[r].astype(F32),
                own[r, second].astype(F32) + rb[1, r].astype(F32) + rb2[r].astype(F32),
            ],
            axis=1,
        )

    return summed


ROW_CHUNK = 16


def product_scatter_kernel(*refs, pairs, offsets, step):
    left_refs, right_refs, out_ref = refs[:pairs], refs[pairs : 2 * pairs], refs[2 * pairs]
    left_bufs = refs[2 * pairs + 1 : 3 * pairs + 1]
    right_bufs = refs[3 * pairs + 1 : 4 * pairs + 1]
    buffers, (load_sem, send_sem, recv_sem) = refs[4 * pairs + 1 : -3], refs[-3:]
    copies = Copies(send_sem, recv_sem)
    summed = product_scatter_steps(
        left_refs, right_refs, left_bufs, right_bufs, buffers, load_sem, copies, offsets, step
    )

    @pl.loop(0, out_ref.shape[0] // ROW_CHUNK)
    def _(k):
        r = pl.ds(pl.multiple_of(k * ROW_CHUNK, ROW_CHUNK), ROW_CHUNK)
        out_ref[r] = summed(r)

    copies.sent()


def scatter_buffers(rows, width):
    half = width // 2
    return [
        pltpu.VMEM((4, 2 * rows, width), BF16),
        pltpu.VMEM((4, rows, width), BF16),
        pltpu.VMEM((2, rows, half), BF16),
        pltpu.VMEM((2, rows, half), BF16),
        pltpu.VMEM((rows, half), BF16),
        pltpu.VMEM((rows, half), BF16),
    ]


def product_scatter(lefts, rights, offsets, step, collective_id):
    pairs = len(lefts)
    rows, width = lefts[0].shape[0] // PLANE, rights[0].shape[0]
    return pl.pallas_call(
        partial(product_scatter_kernel, pairs=pairs, offsets=offsets, step=step),
        out_shape=jax.ShapeDtypeStruct((rows, width), F32),
        in_specs=[ANY] * (2 * pairs),
        out_specs=VMEM,
        scratch_shapes=[
            *[pltpu.VMEM(value.shape, BF16) for value in lefts],
            *[pltpu.VMEM((width, value.shape[1]), BF16) for value in lefts],
            *scatter_buffers(rows, width),
            DMA((pairs, W_TILES + 4)),
            DMA((SCATTER_COPIES,)),
            DMA((SCATTER_COPIES,)),
        ],
        compiler_params=pltpu.CompilerParams(
            collective_id=collective_id, has_side_effects=True, vmem_limit_bytes=56 << 20
        ),
        cost_estimate=cost(50),
        name="product_scatter",
    )(*lefts, *rights)


BACK_TILE = 384


def back_kernel(*refs, pairs, offsets, step):
    left_refs, right_refs, rows_ref = refs[:pairs], refs[pairs : 2 * pairs], refs[2 * pairs]
    out_ref, term_ref = refs[2 * pairs + 1 : 2 * pairs + 3]
    scratch = refs[2 * pairs + 3 :]
    left_bufs, right_bufs = scratch[:pairs], scratch[pairs : 2 * pairs]
    rows_buf, stage = scratch[2 * pairs : 2 * pairs + 2]
    buffers = scratch[2 * pairs + 2 : -5]
    load_sem, rows_sem, store_sem, send_sem, recv_sem = scratch[-5:]
    copies = Copies(send_sem, recv_sem)
    rows_load = pltpu.make_async_copy(rows_ref, rows_buf, rows_sem)
    tiles = rows_ref.shape[1] // BACK_TILE
    width = left_refs[0].shape[1]

    def store(t):
        return pltpu.make_async_copy(
            stage.at[t % 2],
            term_ref.at[pl.ds(pl.multiple_of(t * BACK_TILE, 16), BACK_TILE)],
            store_sem.at[t % 2],
        )

    def beside():
        rows_load.wait()

        @pl.loop(0, tiles)
        def _(t):
            @pl.when(t >= 2)
            def _():
                store(t - 2).wait()

            columns = rows_buf[:, pl.ds(pl.multiple_of(t * BACK_TILE, BACK_TILE), BACK_TILE)]
            for j in range(pairs):
                term = contract_first(columns, left_bufs[j][...])
                stage[t % 2, :, pl.ds(j * width, width)] = term.astype(BF16)
            store(t).start()

    def start_rows():
        rows_load.start()

    summed = product_scatter_steps(
        left_refs,
        right_refs,
        left_bufs,
        right_bufs,
        buffers,
        load_sem,
        copies,
        offsets,
        step,
        (start_rows, beside),
    )

    @pl.loop(0, out_ref.shape[0] // ROW_CHUNK)
    def _(k):
        r = pl.ds(pl.multiple_of(k * ROW_CHUNK, ROW_CHUNK), ROW_CHUNK)
        out_ref[r] = summed(r)

    for t in range(tiles - 2, tiles):
        store(t).wait()
    copies.sent()


def product_scatter_back(lefts, rights, offsets, rows, step, collective_id):
    pairs = len(lefts)
    count, width = lefts[0].shape[0] // PLANE, rights[0].shape[0]
    columns = sum(value.shape[1] for value in lefts)
    return pl.pallas_call(
        partial(back_kernel, pairs=pairs, offsets=offsets, step=step),
        out_shape=(
            jax.ShapeDtypeStruct((count, width), F32),
            jax.ShapeDtypeStruct((rows.shape[1], columns), BF16),
        ),
        in_specs=[ANY] * (2 * pairs + 1),
        out_specs=(VMEM, ANY),
        scratch_shapes=[
            *[pltpu.VMEM(value.shape, BF16) for value in lefts],
            *[pltpu.VMEM((width, value.shape[1]), BF16) for value in lefts],
            pltpu.VMEM(rows.shape, BF16),
            pltpu.VMEM((2, BACK_TILE, columns), BF16),
            *scatter_buffers(count, width),
            DMA((pairs, W_TILES + 4)),
            DMA(()),
            DMA((2,)),
            DMA((SCATTER_COPIES,)),
            DMA((SCATTER_COPIES,)),
        ],
        compiler_params=pltpu.CompilerParams(
            collective_id=collective_id, has_side_effects=True, vmem_limit_bytes=62 << 20
        ),
        cost_estimate=cost(60),
        name="product_scatter_back",
    )(*lefts, *rights, rows)


TURN_TILE = 768


def turn_kernel(
    left_ref, right_ref, gain_ref, grad_ref, raw_ref, full_ref, term_ref, *refs, step
):
    left_buf, right_buf, gathered, total, grad_own = refs[:5]
    buffers, (load_sem, own_sem, store_sem, send_sem, recv_sem) = refs[5:-5], refs[-5:]
    rows, width = grad_ref.shape
    copies = Copies(send_sem, recv_sem)
    summed = product_scatter_steps(
        [left_ref], [right_ref], [left_buf], [right_buf], buffers, load_sem, copies, [0], step
    )
    gain = gain_ref[...]

    @pl.loop(0, rows // ROW_CHUNK)
    def _(k):
        r = pl.ds(pl.multiple_of(k * ROW_CHUNK, ROW_CHUNK), ROW_CHUNK)
        value = summed(r)
        raw_ref[r] = value
        scale = lax.rsqrt(jnp.mean(value * value, axis=1, keepdims=True) + EPSILON)
        scaled = (1.0 + gain) * grad_ref[r].astype(F32)
        inner = jnp.mean(value * scaled, axis=1, keepdims=True)
        grad_own[r] = (scale * scaled - value * (scale * scale * scale * inner)).astype(BF16)

    stores = []

    def on_rows(device):
        slot = len(stores)
        r = pl.ds(pl.multiple_of((place(device, step) // 2) * 2 * rows, 16), 2 * rows)
        store = pltpu.make_async_copy(gathered.at[r], full_ref.at[r], store_sem.at[slot])
        store.start()
        stores.append(store)
        right = left_buf[r]

        @pl.loop(0, width // TURN_TILE)
        def _(t):
            w = pl.ds(pl.multiple_of(t * TURN_TILE, TURN_TILE), TURN_TILE)
            term = contract_first(gathered[r, w], right)
            if slot == 0:
                total[w] = term
            elif slot < 3:
                total[w] += term
            else:
                right_buf[w] = (total[w] + term).astype(BF16)
                pltpu.make_async_copy(right_buf.at[w], term_ref.at[w], store_sem.at[4]).start()

    gather_steps(grad_own, gathered, copies, own_sem, step)(on_rows)
    pltpu.make_async_copy(right_buf, term_ref, store_sem.at[4]).wait()
    for store in stores:
        store.wait()
    copies.sent()


def turn(left, right, gain_row, grad, step, collective_id):
    rows, width = grad.shape
    count = SCATTER_COPIES + GATHER_COPIES
    return pl.pallas_call(
        partial(turn_kernel, step=step),
        out_shape=(
            jax.ShapeDtypeStruct((rows, width), F32),
            jax.ShapeDtypeStruct((PLANE * rows, width), BF16),
            jax.ShapeDtypeStruct((width, left.shape[1]), BF16),
        ),
        in_specs=[ANY, ANY, VMEM, VMEM],
        out_specs=(VMEM, ANY, ANY),
        scratch_shapes=[
            pltpu.VMEM(left.shape, BF16),
            pltpu.VMEM(right.shape, BF16),
            pltpu.VMEM((PLANE * rows, width), BF16),
            pltpu.VMEM((width, left.shape[1]), F32),
            pltpu.VMEM((rows, width), BF16),
            *scatter_buffers(rows, width),
            DMA((1, W_TILES + 4)),
            DMA(()),
            DMA((5,)),
            DMA((count,)),
            DMA((count,)),
        ],
        compiler_params=pltpu.CompilerParams(
            collective_id=collective_id, has_side_effects=True, vmem_limit_bytes=60 << 20
        ),
        cost_estimate=cost(50),
        name="turn",
    )(left, right, gain_row, grad)


def attn_columns(column):
    query_width = H * HD
    key_offset = query_width + (column % 2) * KVH * HD + (column // 2) * HD
    return (column * HD, key_offset, query_width + 2 * KVH * HD + column * HD)


def greet_all(peers):
    me = lax.axis_index(AXIS)
    barrier = pltpu.get_barrier_semaphore()

    @pl.loop(1, peers)
    def _(k):
        device = lax.rem(me + k, peers)
        pl.semaphore_signal(barrier, inc=1, device_id=(device,), device_id_type=MESH)

    pl.semaphore_wait(barrier, peers - 1)


def exchange_all(source_of, target_ref, send_sem, recv_sem):
    peers = target_ref.shape[0]
    me = lax.axis_index(AXIS)

    def copy(k):
        device = lax.rem(me + k, peers)
        return pltpu.make_async_remote_copy(
            src_ref=source_of(device),
            dst_ref=target_ref.at[me],
            send_sem=send_sem.at[k],
            recv_sem=recv_sem.at[k],
            device_id=(device,),
            device_id_type=MESH,
        )

    @pl.loop(1, peers)
    def _(k):
        copy(k).start()

    def finish():
        @pl.loop(1, peers)
        def _(k):
            copy(k).wait()

    return finish


ORDER = (6, 7, 2, 3, 4, 5, 1)


def swap_steps(pieces_of, targets, copies, own_sem, step):
    me = lax.axis_index(AXIS)
    moved = []
    for bits in ORDER:
        peer = partner(me, bits, step)
        for source, target in zip(pieces_of(place(peer, step)), targets):
            moved.append(copies.start(source, target, peer))
    owns = []
    for slot, (source, target) in enumerate(zip(pieces_of(place(me, step)), targets)):
        own = pltpu.make_async_copy(source, target, own_sem.at[slot])
        own.start()
        owns.append(own)

    def finish():
        for own in owns:
            own.wait()
        for copy in moved:
            copy.wait_recv()

    return finish


def square(step):
    me = lax.axis_index(AXIS)
    return [partner(me, bits, step) for bits in ORDER]


def wide(offset):
    return pl.ds(pl.multiple_of(offset, 128), HD)


class Line:
    def __init__(self, full_ref, send_sem, recv_sem, own_ref=None):
        me = lax.axis_index(AXIS)
        self.own = own_ref
        self.full, self.planes = full_ref, full_ref.shape[0]
        self.send_sem, self.recv_sem = send_sem, recv_sem
        self.plane = me // PLANE
        peers = self.planes * PLANE
        self.devices = (lax.rem(me + PLANE, peers), lax.rem(me + peers - PLANE, peers))

    def copy(self, way, slot, source, first=False):
        return pltpu.make_async_remote_copy(
            src_ref=self.own if first and self.own is not None else self.full.at[source],
            dst_ref=self.full.at[source],
            send_sem=self.send_sem.at[way, slot],
            recv_sem=self.recv_sem.at[way, slot],
            device_id=(self.devices[way],),
            device_id_type=MESH,
        )

    def sends(self, way, hop):
        if way == 0:
            source = self.plane - (hop - 1)
            return (self.plane + 1 < self.planes) & (source >= 0), source
        source = self.plane + (hop - 1)
        return (self.plane >= 1) & (source < self.planes), source

    def greet(self):
        barrier = pltpu.get_barrier_semaphore()
        count = 0
        for way, there in enumerate((self.plane + 1 < self.planes, self.plane >= 1)):

            @pl.when(there)
            def _():
                pl.semaphore_signal(
                    barrier, inc=1, device_id=(self.devices[way],), device_id_type=MESH
                )

            count = count + there.astype(jnp.int32)
        return count

    def start(self, hop, slot):
        for way in range(2):
            there, source = self.sends(way, hop)

            @pl.when(there)
            def _():
                self.copy(way, slot, source, hop == 1).start()

    def arrived(self, hop, slot):
        for way in range(2):
            source = self.plane - hop if way == 0 else self.plane + hop

            @pl.when((source >= 0) & (source < self.planes))
            def _():
                self.copy(way, slot, source).wait_recv()

    def sent(self, hop, slot):
        for way in range(2):
            there, source = self.sends(way, hop)

            @pl.when(there)
            def _():
                self.copy(way, slot, source, hop == 1).wait_send()

    def begin(self, hops):
        if hops:
            self.start(hops[0], 0)

    def run(self, hops):
        for slot, hop in enumerate(hops):
            self.arrived(hop, slot)
            if slot + 1 < len(hops):
                self.start(hop + 1, slot + 1)

    def end(self, hops):
        for slot, hop in enumerate(hops):
            self.sent(hop, slot)


def line_hops(planes):
    hops = list(range(1, planes))
    first = (2 * len(hops) + 2) // 3
    return hops[:first], hops[first:]


def line_semaphores(hops):
    count = max(1, len(hops))
    return [DMA((2, count)), DMA((2, count))]


def greet_line(line, peers):
    barrier = pltpu.get_barrier_semaphore()
    for peer in peers:
        pl.semaphore_signal(barrier, inc=1, device_id=(peer,), device_id_type=MESH)
    pl.semaphore_wait(barrier, len(peers) + line.greet())


def row_bands(weights_ref):
    return [weights_ref.at[:, pl.ds(start * HD, H * HD)] for start in (0, H + 2 * KVH)]


def spread_attn_kernel(weights_ref, kv_ref, q_ref, out_ref, own_sem, send_sem, recv_sem, *sems):
    me = lax.axis_index(AXIS)
    plane, here = me // PLANE, place(me, PLANE_STEP)
    q_rows, out_rows = row_bands(weights_ref)
    q_line = Line(q_ref, sems[0], sems[1], q_rows)
    out_line = Line(out_ref, sems[2], sems[3], out_rows)
    hops = line_hops(out_line.planes)[0]
    greet_line(out_line, square(PLANE_STEP))
    out_line.begin(hops)
    q_line.begin([1])
    owns = []
    for slot, (source, target) in enumerate(((q_rows, q_ref), (out_rows, out_ref))):
        own = pltpu.make_async_copy(source, target.at[plane], own_sem.at[1 + slot])
        own.start()
        owns.append(own)
    copies = Copies(send_sem, recv_sem)
    spread = swap_steps(
        lambda c: [weights_ref.at[:, wide(attn_columns(c)[1])]],
        [kv_ref.at[plane, here]],
        copies,
        own_sem,
        PLANE_STEP,
    )
    out_line.run(hops)
    q_line.run([1])
    spread()
    for own in owns:
        own.wait()
    out_line.end(hops)
    q_line.end([1])
    copies.sent()


def spread_attn(weights, planes):
    rows = weights.shape[0]
    return pl.pallas_call(
        spread_attn_kernel,
        out_shape=(
            jax.ShapeDtypeStruct((planes, PLANE, rows, HD), BF16),
            jax.ShapeDtypeStruct((planes, rows, H * HD), BF16),
            jax.ShapeDtypeStruct((planes, rows, H * HD), BF16),
        ),
        in_specs=[ANY],
        out_specs=(ANY, ANY, ANY),
        scratch_shapes=[
            DMA((3,)),
            DMA((7,)),
            DMA((7,)),
            *line_semaphores([1]),
            *line_semaphores(line_hops(planes)[0]),
        ],
        compiler_params=pltpu.CompilerParams(collective_id=3, has_side_effects=True),
        name="spread_attn",
    )(weights)


def spread_gu_kernel(
    weights_ref,
    gain_ref,
    kv_in,
    q_in,
    out_in,
    gu_ref,
    gains_ref,
    kv_ref,
    q_ref,
    out_ref,
    own_sem,
    send_sem,
    recv_sem,
    gain_send,
    gain_recv,
    *sems,
):
    peers = gains_ref.shape[0]
    ffc = gu_ref.shape[2] // 2
    me = lax.axis_index(AXIS)
    here = place(me, PLANE_STEP)
    kv_line = Line(kv_ref, sems[0], sems[1])
    q_line = Line(q_ref, sems[2], sems[3])
    out_line = Line(out_ref, sems[4], sems[5])
    kv_hops, out_hops = line_hops(kv_line.planes)
    q_hops = list(range(2, kv_line.planes))
    greet_all(peers)
    q_line.begin(q_hops)
    out_line.begin(out_hops)
    kv_line.begin(kv_hops)
    gains_done = exchange_all(lambda device: gain_ref, gains_ref, gain_send, gain_recv)
    own = pltpu.make_async_copy(gain_ref, gains_ref.at[me], own_sem.at[2])
    own.start()
    copies = Copies(send_sem, recv_sem)
    spread = swap_steps(
        lambda c: [weights_ref.at[:, lanes(slot * PLANE + c, ffc)] for slot in range(2)],
        [gu_ref.at[here, :, pl.ds(slot * ffc, ffc)] for slot in range(2)],
        copies,
        own_sem,
        PLANE_STEP,
    )
    q_line.run(q_hops)
    out_line.run(out_hops)
    kv_line.run(kv_hops)
    spread()
    own.wait()
    gains_done()
    for line, hops in ((q_line, q_hops), (out_line, out_hops), (kv_line, kv_hops)):
        line.end(hops)
    copies.sent()


def spread_gu(weights, gain_block, kv_full, q_rows, out_rows, peers):
    rows = weights.shape[0]
    ffc = weights.shape[1] // 3 // PLANE
    planes = kv_full.shape[0]
    kv_hops, out_hops = line_hops(planes)
    return pl.pallas_call(
        spread_gu_kernel,
        out_shape=(
            jax.ShapeDtypeStruct((PLANE, rows, 2 * ffc), BF16),
            jax.ShapeDtypeStruct((peers,) + gain_block.shape, gain_block.dtype),
            jax.ShapeDtypeStruct(kv_full.shape, kv_full.dtype),
            jax.ShapeDtypeStruct(q_rows.shape, q_rows.dtype),
            jax.ShapeDtypeStruct(out_rows.shape, out_rows.dtype),
        ),
        in_specs=[ANY] * 5,
        out_specs=(ANY,) * 5,
        scratch_shapes=[
            DMA((3,)),
            DMA((14,)),
            DMA((14,)),
            DMA((peers,)),
            DMA((peers,)),
            *line_semaphores(kv_hops),
            *line_semaphores(range(2, planes)),
            *line_semaphores(out_hops),
        ],
        input_output_aliases={2: 2, 3: 3, 4: 4},
        compiler_params=pltpu.CompilerParams(collective_id=4, has_side_effects=True),
        cost_estimate=cost(38),
        name="spread_gu",
    )(weights, gain_block, kv_full, q_rows, out_rows)


def spread_down_kernel(
    weights_ref,
    block_ref,
    kv_in,
    rows_ref,
    down_ref,
    full_ref,
    kv_ref,
    q_ref,
    own_sem,
    send_sem,
    recv_sem,
    line_send,
    line_recv,
):
    ffc = down_ref.shape[2]
    here = place(lax.axis_index(AXIS), PLANE_STEP)
    line = Line(kv_ref, line_send, line_recv)
    hops = line_hops(line.planes)[1]
    greet_line(line, square(PLANE_STEP))
    line.begin(hops)
    copies = Copies(send_sem, recv_sem)
    gathered = gather_steps(block_ref, full_ref, copies, own_sem.at[2], PLANE_STEP)
    spread = swap_steps(
        lambda c: [
            rows_ref.at[:, :, lanes(c, HD)],
            weights_ref.at[:, lanes(2 * PLANE + c, ffc)],
        ],
        [q_ref.at[:, here], down_ref.at[here]],
        copies,
        own_sem,
        PLANE_STEP,
    )
    gathered()
    line.run(hops)
    spread()
    line.end(hops)
    copies.sent()


def spread_down(weights, block, kv_full, q_rows):
    rows = weights.shape[0]
    ffc = weights.shape[1] // 3 // PLANE
    planes = kv_full.shape[0]
    count = GATHER_COPIES + 14
    return pl.pallas_call(
        spread_down_kernel,
        out_shape=(
            jax.ShapeDtypeStruct((PLANE, rows, ffc), BF16),
            jax.ShapeDtypeStruct((PLANE * block.shape[0], block.shape[1]), BF16),
            jax.ShapeDtypeStruct(kv_full.shape, kv_full.dtype),
            jax.ShapeDtypeStruct((planes, PLANE, rows, HD), BF16),
        ),
        in_specs=[ANY] * 4,
        out_specs=(ANY,) * 4,
        scratch_shapes=[
            DMA((3,)),
            DMA((count,)),
            DMA((count,)),
            *line_semaphores(line_hops(planes)[1]),
        ],
        input_output_aliases={2: 2},
        compiler_params=pltpu.CompilerParams(collective_id=5, has_side_effects=True),
        cost_estimate=cost(1),
        name="spread_down",
    )(weights, block, kv_full, q_rows)


def spread_out_kernel(rows_ref, full_ref, own_sem, send_sem, recv_sem):
    here = place(lax.axis_index(AXIS), PLANE_STEP)
    greet(square(PLANE_STEP))
    copies = Copies(send_sem, recv_sem)
    swap_steps(
        lambda c: [rows_ref.at[:, :, lanes(c, HD)]],
        [full_ref.at[:, here]],
        copies,
        own_sem,
        PLANE_STEP,
    )()
    copies.sent()


def spread_out(out_rows):
    planes, rows = out_rows.shape[:2]
    return pl.pallas_call(
        spread_out_kernel,
        out_shape=jax.ShapeDtypeStruct((planes, PLANE, rows, HD), BF16),
        in_specs=[ANY],
        out_specs=ANY,
        scratch_shapes=[DMA((1,)), DMA((7,)), DMA((7,))],
        compiler_params=pltpu.CompilerParams(collective_id=11, has_side_effects=True),
        cost_estimate=cost(0.1),
        name="spread_out",
    )(out_rows)


def collect_kernel(term_ref, rows_ref, own_sem, send_sem, recv_sem):
    here = place(lax.axis_index(AXIS), PLANE_STEP)
    count = own_sem.shape[0]
    ffc = term_ref.shape[2] // count
    greet(square(PLANE_STEP))
    copies = Copies(send_sem, recv_sem)
    swap_steps(
        lambda c: [term_ref.at[c, :, pl.ds(slot * ffc, ffc)] for slot in range(count)],
        [rows_ref.at[:, lanes(slot * PLANE + here, ffc)] for slot in range(count)],
        copies,
        own_sem,
        PLANE_STEP,
    )()
    copies.sent()


def collect(term, count, collective_id):
    rows, columns = term.shape[1:]
    return pl.pallas_call(
        collect_kernel,
        out_shape=jax.ShapeDtypeStruct((rows, PLANE * columns), BF16),
        in_specs=[ANY],
        out_specs=ANY,
        scratch_shapes=[DMA((count,)), DMA((7 * count,)), DMA((7 * count,))],
        compiler_params=pltpu.CompilerParams(collective_id=collective_id, has_side_effects=True),
        cost_estimate=cost(0.1),
        name="collect",
    )(term)


def collect_attn_kernel(term_ref, rows_ref, own_sem, send_sem, recv_sem):
    here = place(lax.axis_index(AXIS), PLANE_STEP)
    greet(square(PLANE_STEP))
    copies = Copies(send_sem, recv_sem)
    swap_steps(
        lambda c: [term_ref.at[c, :, pl.ds(slot * HD, HD)] for slot in range(3)],
        [rows_ref.at[:, wide(offset)] for offset in attn_columns(here)],
        copies,
        own_sem,
        PLANE_STEP,
    )()
    copies.sent()


def collect_attn(term):
    rows = term.shape[1]
    return pl.pallas_call(
        collect_attn_kernel,
        out_shape=jax.ShapeDtypeStruct((rows, PLANE * 3 * HD), BF16),
        in_specs=[ANY],
        out_specs=ANY,
        scratch_shapes=[DMA((3,)), DMA((21,)), DMA((21,))],
        compiler_params=pltpu.CompilerParams(collective_id=7, has_side_effects=True),
        name="collect_attn",
    )(term)


def collect_gains_kernel(gain_ref, gains_ref, own_sem, gain_send, gain_recv):
    me = lax.axis_index(AXIS)
    greet_all(gain_ref.shape[0])
    done = exchange_all(lambda device: gain_ref.at[device], gains_ref, gain_send, gain_recv)
    own = pltpu.make_async_copy(gain_ref.at[me], gains_ref.at[me], own_sem)
    own.start()
    own.wait()
    done()


def collect_gains(gain_blocks):
    peers = gain_blocks.shape[0]
    return pl.pallas_call(
        collect_gains_kernel,
        out_shape=jax.ShapeDtypeStruct(gain_blocks.shape, gain_blocks.dtype),
        in_specs=[ANY],
        out_specs=ANY,
        scratch_shapes=[DMA(()), DMA((peers,)), DMA((peers,))],
        compiler_params=pltpu.CompilerParams(collective_id=8, has_side_effects=True),
        name="collect_gains",
    )(gain_blocks)


def block_scores(q, k, start, first):
    scores = lax.dot_general(q, k, (((1,), (1,)), ((), ())), preferred_element_type=F32)
    bent = jnp.tanh(scores * (HD ** (-0.5) / SOFT_CAP))
    rows, span = scores.shape
    key_at = lax.broadcasted_iota(jnp.int32, (rows, span), 1)
    row_at = lax.broadcasted_iota(jnp.int32, (rows, span), 0)
    allowed = (key_at + first >= start) & (key_at <= row_at + LMAX)
    return (bent, jnp.where(allowed, jnp.exp(SOFT_CAP * bent), 0.0))


def attend_kernel(q_ref, k_ref, v_ref, start_ref, out_ref, inv_ref):
    first = pl.program_id(0) * QBLK
    keys = pl.ds(pl.multiple_of(first, QBLK), LMAX + QBLK)
    unused_bent, exponent = block_scores(q_ref[...], k_ref[keys], start_ref[...], first)
    inverse = 1.0 / jnp.sum(exponent, axis=-1, keepdims=True)
    weights = (exponent * inverse).astype(BF16)
    out_ref[...] = jnp.dot(weights, v_ref[keys], preferred_element_type=F32).astype(BF16)
    inv_ref[...] = inverse


def attend(queries, key_rows, value_rows, starts):
    rows = queries.shape[0]
    span = key_rows.shape[0]
    row_spec = pl.BlockSpec((QBLK, HD), lambda i: (i, 0))
    one_spec = pl.BlockSpec((QBLK, 1), lambda i: (i, 0))
    all_spec = pl.BlockSpec((span, HD), lambda i: (0, 0))
    return pl.pallas_call(
        attend_kernel,
        out_shape=(
            jax.ShapeDtypeStruct((rows, HD), BF16),
            jax.ShapeDtypeStruct((rows, 1), F32),
        ),
        grid=(rows // QBLK,),
        in_specs=[row_spec, all_spec, all_spec, one_spec],
        out_specs=(row_spec, one_spec),
        compiler_params=pltpu.CompilerParams(vmem_limit_bytes=40 << 20),
        cost_estimate=cost(1),
        name="attend",
    )(queries, key_rows, value_rows, starts)


GRAD_TILE = 256


def attn_grad_kernel(rows_ref, q_ref, kv_ref, proj_ref, attended_ref, out_ref):
    for slot, (left, right) in enumerate(
        ((rows_ref, q_ref), (rows_ref, kv_ref), (proj_ref, attended_ref))
    ):
        out_ref[:, pl.ds(slot * HD, HD)] = contract_first(left[...], right[...]).astype(BF16)


def attn_grad(rows, grad_q, grad_kv, grad_proj, attended):
    count, width = rows.shape
    tile = pl.BlockSpec((count, GRAD_TILE), lambda i: (0, i))
    whole = pl.BlockSpec((count, HD), lambda i: (0, 0))
    return pl.pallas_call(
        attn_grad_kernel,
        out_shape=jax.ShapeDtypeStruct((width, 3 * HD), BF16),
        grid=(width // GRAD_TILE,),
        in_specs=[tile, whole, whole, tile, whole],
        out_specs=pl.BlockSpec((GRAD_TILE, 3 * HD), lambda i: (i, 0)),
        compiler_params=pltpu.CompilerParams(vmem_limit_bytes=48 << 20),
        cost_estimate=cost(10),
        name="attn_grad",
    )(rows, grad_q, grad_kv, grad_proj, attended)


def attend_back_kernel(q_ref, k_ref, v_ref, start_ref, inv_ref, grad_ref, gq_ref, gk_ref, gv_ref):
    @pl.when(pl.program_id(0) == 0)
    def _():
        gk_ref[...] = jnp.zeros_like(gk_ref)
        gv_ref[...] = jnp.zeros_like(gv_ref)

    first = pl.program_id(0) * QBLK
    keys = pl.ds(pl.multiple_of(first, QBLK), LMAX + QBLK)
    q, k, v, grad = q_ref[...], k_ref[keys], v_ref[keys], grad_ref[...]
    bent, exponent = block_scores(q, k, start_ref[...], first)
    probability = exponent * inv_ref[...]
    grad_prob = lax.dot_general(grad, v, (((1,), (1,)), ((), ())), preferred_element_type=F32)
    inner = jnp.sum(probability * grad_prob, axis=-1, keepdims=True)
    grad_scores = (probability * (grad_prob - inner) * (1.0 - bent * bent)).astype(BF16)
    scale = HD ** (-0.5)
    gq_ref[...] = jnp.dot(grad_scores, k, preferred_element_type=F32) * scale
    over_rows = (((0,), (0,)), ((), ()))
    gk_ref[keys] += lax.dot_general(grad_scores, q, over_rows, preferred_element_type=F32) * scale
    gv_ref[keys] += lax.dot_general(
        probability.astype(BF16), grad, over_rows, preferred_element_type=F32
    )


def attend_back(queries, key_rows, value_rows, starts, inverse, grad):
    rows = queries.shape[0]
    span = key_rows.shape[0]
    row_spec = pl.BlockSpec((QBLK, HD), lambda i: (i, 0))
    one_spec = pl.BlockSpec((QBLK, 1), lambda i: (i, 0))
    all_spec = pl.BlockSpec((span, HD), lambda i: (0, 0))
    return pl.pallas_call(
        attend_back_kernel,
        out_shape=(
            jax.ShapeDtypeStruct((rows, HD), F32),
            jax.ShapeDtypeStruct((span, HD), F32),
            jax.ShapeDtypeStruct((span, HD), F32),
        ),
        grid=(rows // QBLK,),
        in_specs=[row_spec, all_spec, all_spec, one_spec, one_spec, row_spec],
        out_specs=(row_spec, all_spec, all_spec),
        compiler_params=pltpu.CompilerParams(vmem_limit_bytes=48 << 20),
        cost_estimate=cost(20),
        name="attend_back",
    )(queries, key_rows, value_rows, starts, inverse, grad)


def token_tables(seq_lengths, index_vec):
    count = seq_lengths.shape[0]
    order = jnp.arange(count, dtype=jnp.int32)
    seq_ends = jnp.sum(
        jnp.where(order[None, :] <= order[:, None], seq_lengths[None, :], 0), axis=1
    )
    after_end = index_vec[:, None] >= seq_ends[None, :]
    return index_vec - jnp.sum(jnp.where(after_end, seq_lengths[None, :], 0), axis=1)


def rms_parts(value):
    return lax.rsqrt(jnp.mean(value * value, axis=-1, keepdims=True) + EPSILON)


def rms_forward(value, gain_vec):
    return value * rms_parts(value) * (1.0 + gain_vec)


def rms_backward(value, gain_vec, grad):
    r = rms_parts(value)
    scaled = (1.0 + gain_vec) * grad
    inner = jnp.mean(value * scaled, axis=-1, keepdims=True)
    return (r * scaled - value * (r * r * r * inner), jnp.sum(grad * value * r, axis=0))


def rotate(value, cosine, sine_part):
    half_width = value.shape[-1] // 2
    first_half = value[..., :half_width]
    second_half = value[..., half_width:]
    return jnp.concatenate(
        [
            first_half * cosine - second_half * sine_part,
            second_half * cosine + first_half * sine_part,
        ],
        axis=-1,
    )


def contract_last(left_side, right_side):
    return lax.dot_general(
        left_side, right_side, (((1,), (1,)), ((), ())), preferred_element_type=F32
    )


def contract_first(left_side, right_side):
    return lax.dot_general(
        left_side, right_side, (((0,), (0,)), ((), ())), preferred_element_type=F32
    )


def matmul(left_side, right_side):
    return jnp.dot(left_side, right_side, preferred_element_type=F32)


def gelu_parts(gate):
    k0 = 0.7978845608028654
    k1 = 0.044715
    t = jnp.tanh(k0 * (gate + k1 * gate * gate * gate))
    value = 0.5 * gate * (1.0 + t)
    slope = 0.5 * (1.0 + t) + 0.5 * gate * (1.0 - t * t) * k0 * (1.0 + 3.0 * k1 * gate * gate)
    return (value, slope)


def local(tokens, attn_weights, mlp_weights, norm_gains, seq_lengths, cotangent):
    tok_rows, width = tokens.shape
    peers = lax.axis_size(AXIS)
    planes = peers // PLANE
    share = width // peers
    row_share = attn_weights.shape[0]
    ff = mlp_weights.shape[1] // 3
    ffc = ff // PLANE
    plane_rows = PLANE * tok_rows
    halo = LMAX
    across = [[p * PLANE + i for p in range(planes)] for i in range(PLANE)]
    sibling = [(i, i ^ 1) for i in range(peers)]
    to_next = [(i, i + PLANE) for i in range(peers - PLANE)]
    to_prev = [(i + PLANE, i) for i in range(peers - PLANE)]
    me = lax.axis_index(AXIS)
    is_even = (me % 2) == 0
    plane_start = (me // PLANE) * plane_rows

    def gather_across(value):
        return lax.all_gather(value, AXIS, axis=0, tiled=True, axis_index_groups=across)

    def scatter_across(value):
        part = lax.psum_scatter(
            value.astype(BF16), AXIS, scatter_dimension=0, tiled=True, axis_index_groups=across
        )
        return part.reshape(PLANE, -1, part.shape[1])

    kv_full, q_rows, out_rows, gain_rows = lax.optimization_barrier(
        (*spread_attn(attn_weights, planes), norm_gains)
    )
    gain_block = jnp.pad(gain_rows.astype(F32), ((0, 8 - 4), (0, -share % 128)))
    gu_part, gain_blocks, kv_full, q_rows, out_rows = spread_gu(
        mlp_weights, gain_block, kv_full, q_rows, out_rows, peers
    )
    gain_full = gain_blocks[:, :4, :share].transpose(1, 0, 2).reshape(4, width)
    inputs = tokens.astype(F32)
    down_part, normed, kv_full, q_full = spread_down(
        mlp_weights, rms_forward(inputs, gain_full[0]).astype(BF16), kv_full, q_rows
    )
    q_cols, kv_cols = q_full.reshape(width, HD), kv_full.reshape(width, HD)
    gu_cols = gather_across(gu_part.reshape(-1, 2 * ffc))
    down_cols = gather_across(down_part.reshape(-1, ffc))

    query_index = plane_start + jnp.arange(plane_rows, dtype=jnp.int32)
    position = token_tables(seq_lengths, query_index)
    starts = (jnp.arange(plane_rows, dtype=jnp.int32) + halo - position)[:, None]
    frequency = 10000.0 ** (-jnp.arange(HD // 2, dtype=F32) * 2.0 / HD)
    angles = position.astype(F32)[:, None] * frequency[None, :]
    cosine, sine_part = jnp.cos(angles), jnp.sin(angles)
    kv_cosine = jnp.where(is_even, cosine, 1.0)
    kv_sine = jnp.where(is_even, sine_part, 0.0)

    kv_own = rotate(matmul(normed, kv_cols), kv_cosine, kv_sine).astype(BF16)
    kv_halo = lax.ppermute(kv_own[plane_rows - halo :], AXIS, to_next)
    kv_own, out_rows, q_cols = lax.optimization_barrier((kv_own, out_rows, q_cols))
    out_cols = spread_out(out_rows).reshape(width, HD)
    queries = rotate(matmul(normed, q_cols), cosine, sine_part).astype(BF16)
    kv_halo, out_cols, queries = lax.optimization_barrier((kv_halo, out_cols, queries))
    kv_mine = jnp.concatenate([kv_halo, kv_own], axis=0)
    kv_other = lax.ppermute(kv_mine, AXIS, sibling)
    key_rows = jnp.where(is_even, kv_mine, kv_other)
    value_rows = jnp.where(is_even, kv_other, kv_mine)
    attended, inverse = attend(queries, key_rows, value_rows, starts)
    attn_proj = product_scatter([attended], [out_cols], [0], PLANE_STEP, 2)

    middle = inputs + rms_forward(attn_proj, gain_full[1])
    mid_low = gather_square(rms_forward(middle, gain_full[2]).astype(BF16), PLANE_STEP, 1)
    gate_up = matmul(mid_low, gu_cols)
    gate, up = gate_up[:, :ffc], gate_up[:, ffc:]
    gelu, slope = gelu_parts(gate)
    hidden = (gelu * up).astype(BF16)
    mlp_raw, grad_raw_low, down_grad = turn(
        hidden, down_cols, gain_full[3:4], cotangent, PLANE_STEP, 9
    )
    layer_output = (middle + rms_forward(mlp_raw, gain_full[3])).astype(BF16)

    grad_out = cotangent.astype(F32)
    gain_four = jnp.sum(grad_out * mlp_raw * rms_parts(mlp_raw), axis=0)
    down_term = scatter_across(down_grad)
    grad_hidden = matmul(grad_raw_low, down_cols)
    grad_normed_mid, gu_grad = product_scatter_back(
        [(slope * up * grad_hidden).astype(BF16), (gelu * grad_hidden).astype(BF16)],
        [gu_cols, gu_cols],
        [0, ffc],
        mid_low,
        PLANE_STEP,
        10,
    )
    gu_term = scatter_across(gu_grad)
    grad_mid_part, gain_three = rms_backward(middle, gain_full[2], grad_normed_mid)
    grad_middle = grad_out + grad_mid_part

    grad_proj, gain_two = rms_backward(attn_proj, gain_full[1], grad_middle)
    grad_proj_own, down_term = lax.optimization_barrier((grad_proj.astype(BF16), down_term))
    grad_proj_low = gather_square(grad_proj_own, PLANE_STEP, 1)
    grad_att = matmul(grad_proj_low, out_cols).astype(BF16)
    grad_query, grad_keys, grad_values = attend_back(
        queries, key_rows, value_rows, starts, inverse, grad_att
    )
    grad_mine = jnp.where(is_even, grad_keys, grad_values)
    grad_give = jnp.where(is_even, grad_values, grad_keys).astype(BF16)
    grad_kv = grad_mine + lax.ppermute(grad_give, AXIS, sibling).astype(F32)
    grad_back = lax.ppermute(grad_kv[:halo].astype(BF16), AXIS, to_prev).astype(F32)
    down_term, grad_kv = lax.optimization_barrier((down_term, grad_kv))
    down_rows = collect(down_term, 1, 6)
    down_rows, grad_back = lax.optimization_barrier((down_rows, grad_back))
    grad_kv = grad_kv[halo:] + jnp.pad(grad_back, ((plane_rows - halo, 0), (0, 0)))
    grad_q = rotate(grad_query, cosine, -sine_part).astype(BF16)
    grad_kv = rotate(grad_kv, kv_cosine, -kv_sine).astype(BF16)
    attn_term, grad_q, grad_kv = lax.optimization_barrier(
        (attn_grad(normed, grad_q, grad_kv, grad_proj_low, attended), grad_q, grad_kv)
    )
    attn_term = scatter_across(attn_term)
    grad_normed = product_scatter([grad_q, grad_kv], [q_cols, kv_cols], [0, 0], PLANE_STEP, 12)
    grad_in_part, gain_one = rms_backward(inputs, gain_full[0], grad_normed)
    grad_tokens = (grad_middle + grad_in_part).astype(BF16)

    gain_term = jnp.stack([gain_one, gain_two, gain_three, gain_four], axis=0)
    gain_term = gain_term.reshape(4, peers, share).transpose(1, 0, 2)
    gain_term = jnp.pad(gain_term, ((0, 0), (0, 8 - 4), (0, -share % 128)))
    gain_recv = collect_gains(gain_term)
    gu_term, gain_recv = lax.optimization_barrier((gu_term, gain_recv))
    gu_rows = collect(gu_term, 2, 13)
    grad_mlp = jnp.concatenate([gu_rows, down_rows], axis=1).astype(F32)
    grad_mlp, attn_term = lax.optimization_barrier((grad_mlp, attn_term))
    grad_attn = collect_attn(attn_term).astype(F32)
    grad_gains = jnp.sum(gain_recv[:, :4, :share], axis=0)
    return (layer_output, grad_tokens, grad_attn, grad_mlp, grad_gains)


def solution(mesh):
    return jax.shard_map(
        local,
        mesh=mesh,
        in_specs=(
            P("fsdp", None),
            P("fsdp", None),
            P("fsdp", None),
            P(None, "fsdp"),
            P(),
            P("fsdp", None),
        ),
        out_specs=(
            P("fsdp", None),
            P("fsdp", None),
            P("fsdp", None),
            P("fsdp", None),
            P(None, "fsdp"),
        ),
        check_vma=False,
    )
```

```python
from functools import partial

import jax
import jax.numpy as jnp
from jax import lax
from jax.experimental import pallas as pl
from jax.experimental.pallas import tpu as pltpu
from jax.sharding import PartitionSpec as P

H = 8
KVH = 4
HD = 256
LMAX = 1024
PLANE = 8
QBLK = 128

EPSILON = 1e-06
SOFT_CAP = 50.0
AXIS = "fsdp"
F32 = jnp.float32
BF16 = jnp.bfloat16
MESH = pl.DeviceIdType.MESH
ANY = pl.BlockSpec(memory_space=pl.ANY)
VMEM = pl.BlockSpec(memory_space=pltpu.VMEM)
DMA = pltpu.SemaphoreType.DMA


def flip(index, step):
    return index + step - 2 * step * ((index // step) % 2)


PLANE_STEP = 4


def partner(index, bits, step):
    for bit, by in ((1, 1), (2, 2), (4, step)):
        if bits & bit:
            index = flip(index, by)
    return index


def place(device, step):
    return device % 4 + 4 * ((device // step) % 2)


def greet(peers):
    barrier = pltpu.get_barrier_semaphore()
    for peer in peers:
        pl.semaphore_signal(barrier, inc=1, device_id=(peer,), device_id_type=MESH)
    pl.semaphore_wait(barrier, len(peers))


class Copies:
    def __init__(self, send_sem, recv_sem):
        self.send_sem, self.recv_sem, self.made = send_sem, recv_sem, []

    def start(self, source, target, device):
        slot = len(self.made)
        copy = pltpu.make_async_remote_copy(
            src_ref=source,
            dst_ref=target,
            send_sem=self.send_sem.at[slot],
            recv_sem=self.recv_sem.at[slot],
            device_id=(device,),
            device_id_type=MESH,
        )
        copy.start()
        self.made.append(copy)
        return copy

    def sent(self):
        for copy in self.made:
            copy.wait_send()


def band(index, size):
    return pl.ds(pl.multiple_of(index * size, 8), size)


def lanes(index, size):
    return pl.ds(pl.multiple_of(index * size, 128), size)


def gather_steps(block_ref, full_ref, copies, own_sem, step):
    rows, width = block_ref.shape
    half = width // 2
    me = lax.axis_index(AXIS)
    sib, xn, yn = flip(me, 1), flip(me, 2), flip(me, step)
    diag = flip(xn, step)

    def at(device, side):
        return full_ref.at[band(place(device, step), rows), pl.ds(side * half, half)]

    def mine(side):
        return block_ref.at[:, pl.ds(side * half, half)]

    own_rows = full_ref.at[band(place(me, step), rows)]
    xa = copies.start(mine(0), at(me, 0), xn)
    ya = copies.start(mine(1), at(me, 1), yn)
    xb = copies.start(mine(1), at(me, 1), xn)
    yb = copies.start(mine(0), at(me, 0), yn)
    arriving = [copies.start(block_ref, own_rows, sib)]
    own = pltpu.make_async_copy(block_ref, own_rows, own_sem)
    own.start()

    def finish(on_rows=None):
        def to_sibling(device, side):
            arriving.append(copies.start(at(device, side), at(device, side), sib))

        def arrived(first, last, *devices):
            for copy in arriving[first:last]:
                copy.wait_recv()
            for device in devices:
                on_rows(device)

        if on_rows is not None:
            own.wait()
            arrived(0, 1, me)
        xa.wait_recv()
        yc = copies.start(at(xn, 0), at(xn, 0), yn)
        to_sibling(xn, 0)
        ya.wait_recv()
        xc = copies.start(at(yn, 1), at(yn, 1), xn)
        to_sibling(yn, 1)
        xb.wait_recv()
        to_sibling(xn, 1)
        yb.wait_recv()
        to_sibling(yn, 0)
        if on_rows is not None:
            arrived(1, 5, xn, yn)
        yc.wait_recv()
        to_sibling(diag, 0)
        xc.wait_recv()
        to_sibling(diag, 1)
        if on_rows is not None:
            arrived(5, 7, diag)
        else:
            arrived(0, 7)
            own.wait()

    return finish


GATHER_COPIES = 13


def cost(microseconds):
    return pl.CostEstimate(
        flops=int(microseconds * 1e7), transcendentals=0, bytes_accessed=int(microseconds * 3e4)
    )


def gather_kernel(block_ref, full_ref, own_sem, send_sem, recv_sem, *, step):
    me = lax.axis_index(AXIS)
    greet((flip(me, 1), flip(me, 2), flip(me, step)))
    copies = Copies(send_sem, recv_sem)
    gather_steps(block_ref, full_ref, copies, own_sem, step)()
    copies.sent()


def gather_square(block, step, collective_id):
    rows, width = block.shape
    return pl.pallas_call(
        partial(gather_kernel, step=step),
        out_shape=jax.ShapeDtypeStruct((PLANE * rows, width), block.dtype),
        in_specs=[ANY],
        out_specs=ANY,
        scratch_shapes=[DMA(()), DMA((GATHER_COPIES,)), DMA((GATHER_COPIES,))],
        compiler_params=pltpu.CompilerParams(collective_id=collective_id, has_side_effects=True),
        cost_estimate=cost(42),
        name="gather_square",
    )(block)


W_TILES = 2
SCATTER_COPIES = 14


def split_columns(width):
    left = (width // 2 + 127) // 128 * 128
    return pl.ds(0, left), pl.ds(left, width - left)


def product_scatter_steps(
    left_refs, right_refs, left_bufs, right_bufs, buffers, load_sem, copies, offsets, step, beside=None
):
    both, got, ra, rb, ra2, rb2 = buffers
    pairs = len(left_refs)
    rows, width = got.shape[1:]
    sides = split_columns(width)
    chunk = 48
    me = lax.axis_index(AXIS)
    core = me % 2
    sib, xn, yn = flip(me, 1), flip(me, 2), flip(me, step)
    order = (flip(xn, step), xn, yn, me)
    first, second = sides

    def chip_rows(device):
        return pl.ds(pl.multiple_of((place(device, step) // 2) * 2 * rows, 16), 2 * rows)

    def right_load(j, t):
        r = sides[t]
        source = right_refs[j].at[r, pl.ds(offsets[j], right_bufs[j].shape[1])]
        return pltpu.make_async_copy(source, right_bufs[j].at[r], load_sem.at[j, t])

    def left_load(j, i):
        r = chip_rows(order[i])
        return pltpu.make_async_copy(
            left_refs[j].at[r], left_bufs[j].at[r], load_sem.at[j, W_TILES + i]
        )

    for j in range(pairs):
        left_load(j, 0).start()
    for t in range(W_TILES):
        for j in range(pairs):
            right_load(j, t).start()
    for i in range(1, 4):
        for j in range(pairs):
            left_load(j, i).start()
    if beside is not None:
        beside[0]()
    greet((sib, xn, yn))

    def mine(i, cols):
        return both.at[i, band(core, rows), cols]

    def add(total, other):
        @pl.loop(0, rows // chunk)
        def _(k):
            r = pl.ds(pl.multiple_of(k * chunk, chunk), chunk)
            total[r] = (total[r].astype(F32) + other[r].astype(F32)).astype(total.dtype)

    loaded = set()

    def make(i, side):
        for j in range(pairs):
            if i not in loaded:
                left_load(j, i).wait()
            if i == 0:
                right_load(j, side).wait()
        loaded.add(i)
        r, cols = chip_rows(order[i]), sides[side]
        total = None
        for j in range(pairs):
            term = contract_last(left_bufs[j][r], right_bufs[j][cols])
            total = term if total is None else total + term
        both[i, :, cols] = total.astype(BF16)
        return copies.start(both.at[i, band(1 - core, rows), cols], got.at[i, :, cols], sib)

    def merge(crossing, i, side):
        cols = sides[side]
        crossing.wait_recv()
        add(mine(i, cols), got.at[i, :, cols])

    c0 = make(0, 0)
    c1 = make(0, 1)
    merge(c0, 0, 0)
    x0 = copies.start(mine(0, first), ra.at[0], xn)
    c2 = make(1, 0)
    merge(c1, 0, 1)
    y0 = copies.start(mine(0, second), rb.at[0], yn)
    c3 = make(2, 1)
    merge(c2, 1, 0)
    x1 = copies.start(mine(1, first), ra.at[1], xn)
    c4 = make(2, 0)
    merge(c3, 2, 1)
    y1 = copies.start(mine(2, second), rb.at[1], yn)
    c5 = make(1, 1)
    merge(c4, 2, 0)
    x0.wait_recv()
    add(mine(2, first), ra.at[0])
    y2 = copies.start(mine(2, first), ra2, yn)
    c6 = make(3, 0)
    merge(c5, 1, 1)
    y0.wait_recv()
    add(mine(1, second), rb.at[0])
    x2 = copies.start(mine(1, second), rb2, xn)
    c7 = make(3, 1)
    merge(c6, 3, 0)
    merge(c7, 3, 1)
    if beside is not None:
        beside[1]()
    for copy in (x1, y1, y2, x2):
        copy.wait_recv()
    own = both.at[3, band(core, rows)]

    def summed(r):
        return jnp.concatenate(
            [
                own[r, first].astype(F32) + ra[1, r].astype(F32) + ra2[r].astype(F32),
                own[r, second].astype(F32) + rb[1, r].astype(F32) + rb2[r].astype(F32),
            ],
            axis=1,
        )

    return summed


ROW_CHUNK = 48


def product_scatter_kernel(*refs, pairs, offsets, step):
    left_refs, right_refs, out_ref = refs[:pairs], refs[pairs : 2 * pairs], refs[2 * pairs]
    left_bufs = refs[2 * pairs + 1 : 3 * pairs + 1]
    right_bufs = refs[3 * pairs + 1 : 4 * pairs + 1]
    buffers, (load_sem, send_sem, recv_sem) = refs[4 * pairs + 1 : -3], refs[-3:]
    copies = Copies(send_sem, recv_sem)
    summed = product_scatter_steps(
        left_refs, right_refs, left_bufs, right_bufs, buffers, load_sem, copies, offsets, step
    )

    @pl.loop(0, out_ref.shape[0] // ROW_CHUNK)
    def _(k):
        r = pl.ds(pl.multiple_of(k * ROW_CHUNK, ROW_CHUNK), ROW_CHUNK)
        out_ref[r] = summed(r)

    copies.sent()


def scatter_buffers(rows, width):
    left, right = [side.size for side in split_columns(width)]
    return [
        pltpu.VMEM((4, 2 * rows, width), BF16),
        pltpu.VMEM((4, rows, width), BF16),
        pltpu.VMEM((2, rows, left), BF16),
        pltpu.VMEM((2, rows, right), BF16),
        pltpu.VMEM((rows, left), BF16),
        pltpu.VMEM((rows, right), BF16),
    ]


def product_scatter(lefts, rights, offsets, step, collective_id):
    pairs = len(lefts)
    rows, width = lefts[0].shape[0] // PLANE, rights[0].shape[0]
    return pl.pallas_call(
        partial(product_scatter_kernel, pairs=pairs, offsets=offsets, step=step),
        out_shape=jax.ShapeDtypeStruct((rows, width), F32),
        in_specs=[ANY] * (2 * pairs),
        out_specs=VMEM,
        scratch_shapes=[
            *[pltpu.VMEM(value.shape, BF16) for value in lefts],
            *[pltpu.VMEM((width, value.shape[1]), BF16) for value in lefts],
            *scatter_buffers(rows, width),
            DMA((pairs, W_TILES + 4)),
            DMA((SCATTER_COPIES,)),
            DMA((SCATTER_COPIES,)),
        ],
        compiler_params=pltpu.CompilerParams(
            collective_id=collective_id, has_side_effects=True, vmem_limit_bytes=56 << 20
        ),
        cost_estimate=cost(50),
        name="product_scatter",
    )(*lefts, *rights)


BACK_TILE = 384


def back_kernel(*refs, pairs, offsets, step):
    left_refs, right_refs, rows_ref = refs[:pairs], refs[pairs : 2 * pairs], refs[2 * pairs]
    out_ref, term_ref = refs[2 * pairs + 1 : 2 * pairs + 3]
    scratch = refs[2 * pairs + 3 :]
    left_bufs, right_bufs = scratch[:pairs], scratch[pairs : 2 * pairs]
    rows_buf, stage = scratch[2 * pairs : 2 * pairs + 2]
    buffers = scratch[2 * pairs + 2 : -5]
    load_sem, rows_sem, store_sem, send_sem, recv_sem = scratch[-5:]
    copies = Copies(send_sem, recv_sem)
    rows_load = pltpu.make_async_copy(rows_ref, rows_buf, rows_sem)
    tiles = rows_ref.shape[1] // BACK_TILE
    width = left_refs[0].shape[1]

    def store(t):
        return pltpu.make_async_copy(
            stage.at[t % 2],
            term_ref.at[pl.ds(pl.multiple_of(t * BACK_TILE, 16), BACK_TILE)],
            store_sem.at[t % 2],
        )

    def beside():
        rows_load.wait()

        @pl.loop(0, tiles)
        def _(t):
            @pl.when(t >= 2)
            def _():
                store(t - 2).wait()

            columns = rows_buf[:, pl.ds(pl.multiple_of(t * BACK_TILE, BACK_TILE), BACK_TILE)]
            for j in range(pairs):
                term = contract_first(columns, left_bufs[j][...])
                stage[t % 2, :, pl.ds(j * width, width)] = term.astype(BF16)
            store(t).start()

    def start_rows():
        rows_load.start()

    summed = product_scatter_steps(
        left_refs,
        right_refs,
        left_bufs,
        right_bufs,
        buffers,
        load_sem,
        copies,
        offsets,
        step,
        (start_rows, beside),
    )

    @pl.loop(0, out_ref.shape[0] // ROW_CHUNK)
    def _(k):
        r = pl.ds(pl.multiple_of(k * ROW_CHUNK, ROW_CHUNK), ROW_CHUNK)
        out_ref[r] = summed(r)

    for t in range(tiles - 2, tiles):
        store(t).wait()
    copies.sent()


def product_scatter_back(lefts, rights, offsets, rows, step, collective_id):
    pairs = len(lefts)
    count, width = lefts[0].shape[0] // PLANE, rights[0].shape[0]
    columns = sum(value.shape[1] for value in lefts)
    return pl.pallas_call(
        partial(back_kernel, pairs=pairs, offsets=offsets, step=step),
        out_shape=(
            jax.ShapeDtypeStruct((count, width), F32),
            jax.ShapeDtypeStruct((rows.shape[1], columns), BF16),
        ),
        in_specs=[ANY] * (2 * pairs + 1),
        out_specs=(VMEM, ANY),
        scratch_shapes=[
            *[pltpu.VMEM(value.shape, BF16) for value in lefts],
            *[pltpu.VMEM((width, value.shape[1]), BF16) for value in lefts],
            pltpu.VMEM(rows.shape, BF16),
            pltpu.VMEM((2, BACK_TILE, columns), BF16),
            *scatter_buffers(count, width),
            DMA((pairs, W_TILES + 4)),
            DMA(()),
            DMA((2,)),
            DMA((SCATTER_COPIES,)),
            DMA((SCATTER_COPIES,)),
        ],
        compiler_params=pltpu.CompilerParams(
            collective_id=collective_id, has_side_effects=True, vmem_limit_bytes=62 << 20
        ),
        cost_estimate=cost(60),
        name="product_scatter_back",
    )(*lefts, *rights, rows)


TURN_TILE = 768


def in_place(rows):
    return rows % 16 == 0


def turn_kernel(
    left_ref,
    right_ref,
    near_ref,
    gain_ref,
    grad_ref,
    raw_ref,
    full_ref,
    term_ref,
    *refs,
    planes,
    step,
):
    left_buf, right_buf, gathered, total, grad_own, stage = refs[:6]
    buffers, (load_sem, own_sem, store_sem, send_sem, recv_sem) = refs[6:-5], refs[-5:]
    rows, width = grad_ref.shape
    half = width // 2
    piece = half // planes
    copies = Copies(send_sem, recv_sem)
    summed = product_scatter_steps(
        [left_ref], [right_ref], [left_buf], [right_buf], buffers, load_sem, copies, [0], step
    )
    gain = gain_ref[...]

    @pl.loop(0, rows // ROW_CHUNK)
    def _(k):
        r = pl.ds(pl.multiple_of(k * ROW_CHUNK, ROW_CHUNK), ROW_CHUNK)
        far = summed(r)
        raw_ref[r] = far
        value = jnp.concatenate([near_ref[r], far], axis=1)
        scale = lax.rsqrt(jnp.mean(value * value, axis=1, keepdims=True) + EPSILON)
        scaled = (1.0 + gain) * grad_ref[r].astype(F32)
        inner = jnp.mean(value * scaled, axis=1, keepdims=True)
        grad_own[r] = (scale * scaled - value * (scale * scale * scale * inner)).astype(BF16)

    stores = []

    def store_term(side):
        for plane in range(planes):
            start = side * half + plane * piece
            target = plane * 2 * piece + side * piece if in_place(piece) else start
            pltpu.make_async_copy(
                stage.at[pl.ds(start, piece)] if in_place(piece) else stage.at[pl.ds(side * half, half)],
                term_ref.at[pl.ds(target, piece)]
                if in_place(piece)
                else term_ref.at[pl.ds(side * half, half)],
                store_sem.at[4],
            ).start()
            if not in_place(piece):
                break

    def on_rows(device):
        slot = len(stores)
        r = pl.ds(pl.multiple_of((place(device, step) // 2) * 2 * rows, 16), 2 * rows)
        store = pltpu.make_async_copy(gathered.at[r], full_ref.at[r], store_sem.at[slot])
        store.start()
        stores.append(store)
        right = left_buf[r]
        if slot < 3:

            @pl.loop(0, width // TURN_TILE)
            def _(t):
                w = pl.ds(pl.multiple_of(t * TURN_TILE, TURN_TILE), TURN_TILE)
                term = contract_first(gathered[r, w], right)
                if slot == 0:
                    total[w] = term
                else:
                    total[w] += term
        else:
            for side in range(2):

                @pl.loop(0, 3)
                def _(t):
                    w = pl.ds(
                        pl.multiple_of(side * half + t * (half // 3), half // 3), half // 3
                    )
                    term = contract_first(gathered[r, w], right)
                    stage[w] = (total[w] + term).astype(BF16)

                store_term(side)

    gather_steps(grad_own, gathered, copies, own_sem, step)(on_rows)
    pltpu.make_async_copy(stage, term_ref, store_sem.at[4]).wait()
    for store in stores:
        store.wait()
    copies.sent()


def turn(left, right, near, gain_row, grad, planes, step, collective_id):
    rows, width = grad.shape
    count = SCATTER_COPIES + GATHER_COPIES
    return pl.pallas_call(
        partial(turn_kernel, planes=planes, step=step),
        out_shape=(
            jax.ShapeDtypeStruct((rows, width // 2), F32),
            jax.ShapeDtypeStruct((PLANE * rows, width), BF16),
            jax.ShapeDtypeStruct((width, left.shape[1]), BF16),
        ),
        in_specs=[ANY, ANY, VMEM, VMEM, VMEM],
        out_specs=(VMEM, ANY, ANY),
        scratch_shapes=[
            pltpu.VMEM(left.shape, BF16),
            pltpu.VMEM(right.shape, BF16),
            pltpu.VMEM((PLANE * rows, width), BF16),
            pltpu.VMEM((width, left.shape[1]), F32),
            pltpu.VMEM((rows, width), BF16),
            pltpu.VMEM((width, left.shape[1]), BF16),
            *scatter_buffers(rows, width // 2),
            DMA((1, W_TILES + 4)),
            DMA(()),
            DMA((5,)),
            DMA((count,)),
            DMA((count,)),
        ],
        compiler_params=pltpu.CompilerParams(
            collective_id=collective_id, has_side_effects=True, vmem_limit_bytes=60 << 20
        ),
        cost_estimate=cost(50),
        name="turn",
    )(left, right, near, gain_row, grad)


def attn_columns(column):
    query_width = H * HD
    key_offset = query_width + (column % 2) * KVH * HD + (column // 2) * HD
    return (column * HD, key_offset, query_width + 2 * KVH * HD + column * HD)


def greet_all(peers):
    me = lax.axis_index(AXIS)
    barrier = pltpu.get_barrier_semaphore()

    @pl.loop(1, peers)
    def _(k):
        device = lax.rem(me + k, peers)
        pl.semaphore_signal(barrier, inc=1, device_id=(device,), device_id_type=MESH)

    pl.semaphore_wait(barrier, peers - 1)


def exchange_all(source_of, target_ref, send_sem, recv_sem):
    peers = target_ref.shape[0]
    me = lax.axis_index(AXIS)

    def copy(k):
        device = lax.rem(me + k, peers)
        return pltpu.make_async_remote_copy(
            src_ref=source_of(device),
            dst_ref=target_ref.at[me],
            send_sem=send_sem.at[k],
            recv_sem=recv_sem.at[k],
            device_id=(device,),
            device_id_type=MESH,
        )

    @pl.loop(1, peers)
    def _(k):
        copy(k).start()

    def finish():
        @pl.loop(1, peers)
        def _(k):
            copy(k).wait()

    return finish


ORDER = (6, 7, 2, 3, 4, 5, 1)


def swap_steps(pieces_of, targets, copies, own_sem, step):
    me = lax.axis_index(AXIS)
    moved = []
    for bits in ORDER:
        peer = partner(me, bits, step)
        for source, target in zip(pieces_of(place(peer, step)), targets):
            moved.append(copies.start(source, target, peer))
    owns = []
    for slot, (source, target) in enumerate(zip(pieces_of(place(me, step)), targets)):
        own = pltpu.make_async_copy(source, target, own_sem.at[slot])
        own.start()
        owns.append(own)

    def finish():
        for own in owns:
            own.wait()
        for copy in moved:
            copy.wait_recv()

    return finish


def square(step):
    me = lax.axis_index(AXIS)
    return [partner(me, bits, step) for bits in ORDER]


def wide(offset):
    return pl.ds(pl.multiple_of(offset, 128), HD)


class Line:
    def __init__(self, full_ref, send_sem, recv_sem, own_ref=None):
        me = lax.axis_index(AXIS)
        self.own = own_ref
        self.full, self.planes = full_ref, full_ref.shape[0]
        self.send_sem, self.recv_sem = send_sem, recv_sem
        self.plane = me // PLANE
        peers = self.planes * PLANE
        self.devices = (lax.rem(me + PLANE, peers), lax.rem(me + peers - PLANE, peers))

    def copy(self, way, slot, source, first=False):
        return pltpu.make_async_remote_copy(
            src_ref=self.own if first and self.own is not None else self.full.at[source],
            dst_ref=self.full.at[source],
            send_sem=self.send_sem.at[way, slot],
            recv_sem=self.recv_sem.at[way, slot],
            device_id=(self.devices[way],),
            device_id_type=MESH,
        )

    def sends(self, way, hop):
        if way == 0:
            source = self.plane - (hop - 1)
            return (self.plane + 1 < self.planes) & (source >= 0), source
        source = self.plane + (hop - 1)
        return (self.plane >= 1) & (source < self.planes), source

    def greet(self):
        barrier = pltpu.get_barrier_semaphore()
        count = 0
        for way, there in enumerate((self.plane + 1 < self.planes, self.plane >= 1)):

            @pl.when(there)
            def _():
                pl.semaphore_signal(
                    barrier, inc=1, device_id=(self.devices[way],), device_id_type=MESH
                )

            count = count + there.astype(jnp.int32)
        return count

    def start(self, hop, slot):
        for way in range(2):
            there, source = self.sends(way, hop)

            @pl.when(there)
            def _():
                self.copy(way, slot, source, hop == 1).start()

    def arrived(self, hop, slot):
        for way in range(2):
            source = self.plane - hop if way == 0 else self.plane + hop

            @pl.when((source >= 0) & (source < self.planes))
            def _():
                self.copy(way, slot, source).wait_recv()

    def sent(self, hop, slot):
        for way in range(2):
            there, source = self.sends(way, hop)

            @pl.when(there)
            def _():
                self.copy(way, slot, source, hop == 1).wait_send()

    def begin(self, hops):
        if hops:
            self.start(hops[0], 0)

    def run(self, hops):
        for slot, hop in enumerate(hops):
            self.arrived(hop, slot)
            if slot + 1 < len(hops):
                self.start(hop + 1, slot + 1)

    def end(self, hops):
        for slot, hop in enumerate(hops):
            self.sent(hop, slot)


def line_hops(planes):
    hops = list(range(1, planes))
    first = (2 * len(hops) + 2) // 3
    return hops[:first], hops[first:]


def line_semaphores(hops):
    count = max(1, len(hops))
    return [DMA((2, count)), DMA((2, count))]


def greet_line(line, peers):
    barrier = pltpu.get_barrier_semaphore()
    for peer in peers:
        pl.semaphore_signal(barrier, inc=1, device_id=(peer,), device_id_type=MESH)
    pl.semaphore_wait(barrier, len(peers) + line.greet())


def row_bands(weights_ref):
    return [weights_ref.at[:, pl.ds(start * HD, H * HD)] for start in (0, H + 2 * KVH)]


def spread_attn_kernel(weights_ref, kv_ref, q_ref, out_ref, own_sem, send_sem, recv_sem, *sems):
    me = lax.axis_index(AXIS)
    plane, here = me // PLANE, place(me, PLANE_STEP)
    q_rows, out_rows = row_bands(weights_ref)
    q_line = Line(q_ref, sems[0], sems[1], q_rows)
    out_line = Line(out_ref, sems[2], sems[3], out_rows)
    hops = line_hops(out_line.planes)[0]
    greet_line(out_line, square(PLANE_STEP))
    out_line.begin(hops)
    q_line.begin([1])
    owns = []
    for slot, (source, target) in enumerate(((q_rows, q_ref), (out_rows, out_ref))):
        own = pltpu.make_async_copy(source, target.at[plane], own_sem.at[1 + slot])
        own.start()
        owns.append(own)
    copies = Copies(send_sem, recv_sem)
    spread = swap_steps(
        lambda c: [weights_ref.at[:, wide(attn_columns(c)[1])]],
        [kv_ref.at[plane, here]],
        copies,
        own_sem,
        PLANE_STEP,
    )
    out_line.run(hops)
    q_line.run([1])
    spread()
    for own in owns:
        own.wait()
    out_line.end(hops)
    q_line.end([1])
    copies.sent()


def spread_attn(weights, planes):
    rows = weights.shape[0]
    return pl.pallas_call(
        spread_attn_kernel,
        out_shape=(
            jax.ShapeDtypeStruct((planes, PLANE, rows, HD), BF16),
            jax.ShapeDtypeStruct((planes, rows, H * HD), BF16),
            jax.ShapeDtypeStruct((planes, rows, H * HD), BF16),
        ),
        in_specs=[ANY],
        out_specs=(ANY, ANY, ANY),
        scratch_shapes=[
            DMA((3,)),
            DMA((7,)),
            DMA((7,)),
            *line_semaphores([1]),
            *line_semaphores(line_hops(planes)[0]),
        ],
        compiler_params=pltpu.CompilerParams(collective_id=3, has_side_effects=True),
        name="spread_attn",
    )(weights)


def spread_gu_kernel(
    weights_ref,
    gain_ref,
    kv_in,
    q_in,
    out_in,
    gu_ref,
    gains_ref,
    kv_ref,
    q_ref,
    out_ref,
    own_sem,
    send_sem,
    recv_sem,
    gain_send,
    gain_recv,
    *sems,
):
    peers = gains_ref.shape[0]
    ffc = gu_ref.shape[2] // 2
    me = lax.axis_index(AXIS)
    here = place(me, PLANE_STEP)
    kv_line = Line(kv_ref, sems[0], sems[1])
    q_line = Line(q_ref, sems[2], sems[3])
    out_line = Line(out_ref, sems[4], sems[5])
    kv_hops, out_hops = line_hops(kv_line.planes)
    q_hops = list(range(2, kv_line.planes))
    greet_all(peers)
    q_line.begin(q_hops)
    out_line.begin(out_hops)
    kv_line.begin(kv_hops)
    gains_done = exchange_all(lambda device: gain_ref, gains_ref, gain_send, gain_recv)
    own = pltpu.make_async_copy(gain_ref, gains_ref.at[me], own_sem.at[2])
    own.start()
    copies = Copies(send_sem, recv_sem)
    spread = swap_steps(
        lambda c: [weights_ref.at[:, lanes(slot * PLANE + c, ffc)] for slot in range(2)],
        [gu_ref.at[here, :, pl.ds(slot * ffc, ffc)] for slot in range(2)],
        copies,
        own_sem,
        PLANE_STEP,
    )
    q_line.run(q_hops)
    out_line.run(out_hops)
    kv_line.run(kv_hops)
    spread()
    own.wait()
    gains_done()
    for line, hops in ((q_line, q_hops), (out_line, out_hops), (kv_line, kv_hops)):
        line.end(hops)
    copies.sent()


def spread_gu(weights, gain_block, kv_full, q_rows, out_rows, peers):
    rows = weights.shape[0]
    ffc = weights.shape[1] // 3 // PLANE
    planes = kv_full.shape[0]
    kv_hops, out_hops = line_hops(planes)
    return pl.pallas_call(
        spread_gu_kernel,
        out_shape=(
            jax.ShapeDtypeStruct((PLANE, rows, 2 * ffc), BF16),
            jax.ShapeDtypeStruct((peers,) + gain_block.shape, gain_block.dtype),
            jax.ShapeDtypeStruct(kv_full.shape, kv_full.dtype),
            jax.ShapeDtypeStruct(q_rows.shape, q_rows.dtype),
            jax.ShapeDtypeStruct(out_rows.shape, out_rows.dtype),
        ),
        in_specs=[ANY] * 5,
        out_specs=(ANY,) * 5,
        scratch_shapes=[
            DMA((3,)),
            DMA((14,)),
            DMA((14,)),
            DMA((peers,)),
            DMA((peers,)),
            *line_semaphores(kv_hops),
            *line_semaphores(range(2, planes)),
            *line_semaphores(out_hops),
        ],
        input_output_aliases={2: 2, 3: 3, 4: 4},
        compiler_params=pltpu.CompilerParams(collective_id=4, has_side_effects=True),
        cost_estimate=cost(38),
        name="spread_gu",
    )(weights, gain_block, kv_full, q_rows, out_rows)


def spread_down_kernel(
    weights_ref,
    block_ref,
    kv_in,
    rows_ref,
    down_ref,
    full_ref,
    kv_ref,
    q_ref,
    own_sem,
    send_sem,
    recv_sem,
    line_send,
    line_recv,
):
    ffc = down_ref.shape[2]
    here = place(lax.axis_index(AXIS), PLANE_STEP)
    line = Line(kv_ref, line_send, line_recv)
    hops = line_hops(line.planes)[1]
    greet_line(line, square(PLANE_STEP))
    line.begin(hops)
    copies = Copies(send_sem, recv_sem)
    gathered = gather_steps(block_ref, full_ref, copies, own_sem.at[2], PLANE_STEP)
    spread = swap_steps(
        lambda c: [
            rows_ref.at[:, :, lanes(c, HD)],
            weights_ref.at[:, lanes(2 * PLANE + c, ffc)],
        ],
        [q_ref.at[:, here], down_ref.at[here]],
        copies,
        own_sem,
        PLANE_STEP,
    )
    gathered()
    line.run(hops)
    spread()
    line.end(hops)
    copies.sent()


def spread_down(weights, block, kv_full, q_rows):
    rows = weights.shape[0]
    ffc = weights.shape[1] // 3 // PLANE
    planes = kv_full.shape[0]
    count = GATHER_COPIES + 14
    return pl.pallas_call(
        spread_down_kernel,
        out_shape=(
            jax.ShapeDtypeStruct((PLANE, rows, ffc), BF16),
            jax.ShapeDtypeStruct((PLANE * block.shape[0], block.shape[1]), BF16),
            jax.ShapeDtypeStruct(kv_full.shape, kv_full.dtype),
            jax.ShapeDtypeStruct((planes, PLANE, rows, HD), BF16),
        ),
        in_specs=[ANY] * 4,
        out_specs=(ANY,) * 4,
        scratch_shapes=[
            DMA((3,)),
            DMA((count,)),
            DMA((count,)),
            *line_semaphores(line_hops(planes)[1]),
        ],
        input_output_aliases={2: 2},
        compiler_params=pltpu.CompilerParams(collective_id=5, has_side_effects=True),
        cost_estimate=cost(1),
        name="spread_down",
    )(weights, block, kv_full, q_rows)


def spread_out_kernel(rows_ref, full_ref, own_sem, send_sem, recv_sem):
    here = place(lax.axis_index(AXIS), PLANE_STEP)
    greet(square(PLANE_STEP))
    copies = Copies(send_sem, recv_sem)
    swap_steps(
        lambda c: [rows_ref.at[:, :, lanes(c, HD)]],
        [full_ref.at[:, here]],
        copies,
        own_sem,
        PLANE_STEP,
    )()
    copies.sent()


def spread_out(out_rows):
    planes, rows = out_rows.shape[:2]
    return pl.pallas_call(
        spread_out_kernel,
        out_shape=jax.ShapeDtypeStruct((planes, PLANE, rows, HD), BF16),
        in_specs=[ANY],
        out_specs=ANY,
        scratch_shapes=[DMA((1,)), DMA((7,)), DMA((7,))],
        compiler_params=pltpu.CompilerParams(collective_id=11, has_side_effects=True),
        cost_estimate=cost(0.1),
        name="spread_out",
    )(out_rows)


def collect_kernel(term_ref, rows_ref, own_sem, send_sem, recv_sem):
    here = place(lax.axis_index(AXIS), PLANE_STEP)
    count = own_sem.shape[0]
    ffc = term_ref.shape[2] // count
    greet(square(PLANE_STEP))
    copies = Copies(send_sem, recv_sem)
    swap_steps(
        lambda c: [term_ref.at[c, :, pl.ds(slot * ffc, ffc)] for slot in range(count)],
        [rows_ref.at[:, lanes(slot * PLANE + here, ffc)] for slot in range(count)],
        copies,
        own_sem,
        PLANE_STEP,
    )()
    copies.sent()


def collect(term, count, collective_id):
    rows, columns = term.shape[1:]
    return pl.pallas_call(
        collect_kernel,
        out_shape=jax.ShapeDtypeStruct((rows, PLANE * columns), BF16),
        in_specs=[ANY],
        out_specs=ANY,
        scratch_shapes=[DMA((count,)), DMA((7 * count,)), DMA((7 * count,))],
        compiler_params=pltpu.CompilerParams(collective_id=collective_id, has_side_effects=True),
        cost_estimate=cost(0.1),
        name="collect",
    )(term)


def collect_attn_kernel(term_ref, rows_ref, own_sem, send_sem, recv_sem):
    here = place(lax.axis_index(AXIS), PLANE_STEP)
    greet(square(PLANE_STEP))
    copies = Copies(send_sem, recv_sem)
    swap_steps(
        lambda c: [term_ref.at[c, :, pl.ds(slot * HD, HD)] for slot in range(3)],
        [rows_ref.at[:, wide(offset)] for offset in attn_columns(here)],
        copies,
        own_sem,
        PLANE_STEP,
    )()
    copies.sent()


def collect_attn(term):
    rows = term.shape[1]
    return pl.pallas_call(
        collect_attn_kernel,
        out_shape=jax.ShapeDtypeStruct((rows, PLANE * 3 * HD), BF16),
        in_specs=[ANY],
        out_specs=ANY,
        scratch_shapes=[DMA((3,)), DMA((21,)), DMA((21,))],
        compiler_params=pltpu.CompilerParams(collective_id=7, has_side_effects=True),
        name="collect_attn",
    )(term)


def collect_gains_kernel(gain_ref, gains_ref, own_sem, gain_send, gain_recv):
    me = lax.axis_index(AXIS)
    greet_all(gain_ref.shape[0])
    done = exchange_all(lambda device: gain_ref.at[device], gains_ref, gain_send, gain_recv)
    own = pltpu.make_async_copy(gain_ref.at[me], gains_ref.at[me], own_sem)
    own.start()
    own.wait()
    done()


def collect_gains(gain_blocks):
    peers = gain_blocks.shape[0]
    return pl.pallas_call(
        collect_gains_kernel,
        out_shape=jax.ShapeDtypeStruct(gain_blocks.shape, gain_blocks.dtype),
        in_specs=[ANY],
        out_specs=ANY,
        scratch_shapes=[DMA(()), DMA((peers,)), DMA((peers,))],
        compiler_params=pltpu.CompilerParams(collective_id=8, has_side_effects=True),
        name="collect_gains",
    )(gain_blocks)


def block_scores(q, k, start, first):
    scores = lax.dot_general(q, k, (((1,), (1,)), ((), ())), preferred_element_type=F32)
    bent = jnp.tanh(scores * (HD ** (-0.5) / SOFT_CAP))
    rows, span = scores.shape
    key_at = lax.broadcasted_iota(jnp.int32, (rows, span), 1)
    row_at = lax.broadcasted_iota(jnp.int32, (rows, span), 0)
    allowed = (key_at + first >= start) & (key_at <= row_at + LMAX)
    return (bent, jnp.where(allowed, jnp.exp(SOFT_CAP * bent), 0.0))


def attend_kernel(q_ref, k_ref, v_ref, start_ref, out_ref, inv_ref):
    first = pl.program_id(0) * QBLK
    keys = pl.ds(pl.multiple_of(first, QBLK), LMAX + QBLK)
    unused_bent, exponent = block_scores(q_ref[...], k_ref[keys], start_ref[...], first)
    inverse = 1.0 / jnp.sum(exponent, axis=-1, keepdims=True)
    weights = (exponent * inverse).astype(BF16)
    out_ref[...] = jnp.dot(weights, v_ref[keys], preferred_element_type=F32).astype(BF16)
    inv_ref[...] = inverse


def attend(queries, key_rows, value_rows, starts):
    rows = queries.shape[0]
    span = key_rows.shape[0]
    row_spec = pl.BlockSpec((QBLK, HD), lambda i: (i, 0))
    one_spec = pl.BlockSpec((QBLK, 1), lambda i: (i, 0))
    all_spec = pl.BlockSpec((span, HD), lambda i: (0, 0))
    return pl.pallas_call(
        attend_kernel,
        out_shape=(
            jax.ShapeDtypeStruct((rows, HD), BF16),
            jax.ShapeDtypeStruct((rows, 1), F32),
        ),
        grid=(rows // QBLK,),
        in_specs=[row_spec, all_spec, all_spec, one_spec],
        out_specs=(row_spec, one_spec),
        compiler_params=pltpu.CompilerParams(vmem_limit_bytes=40 << 20),
        cost_estimate=cost(1),
        name="attend",
    )(queries, key_rows, value_rows, starts)


GRAD_TILE = 256


def attn_grad_kernel(rows_ref, q_ref, kv_ref, proj_ref, attended_ref, out_ref):
    for slot, (left, right) in enumerate(
        ((rows_ref, q_ref), (rows_ref, kv_ref), (proj_ref, attended_ref))
    ):
        out_ref[:, pl.ds(slot * HD, HD)] = contract_first(left[...], right[...]).astype(BF16)


def attn_grad(rows, grad_q, grad_kv, grad_proj, attended):
    count, width = rows.shape
    tile = pl.BlockSpec((count, GRAD_TILE), lambda i: (0, i))
    whole = pl.BlockSpec((count, HD), lambda i: (0, 0))
    return pl.pallas_call(
        attn_grad_kernel,
        out_shape=jax.ShapeDtypeStruct((width, 3 * HD), BF16),
        grid=(width // GRAD_TILE,),
        in_specs=[tile, whole, whole, tile, whole],
        out_specs=pl.BlockSpec((GRAD_TILE, 3 * HD), lambda i: (i, 0)),
        compiler_params=pltpu.CompilerParams(vmem_limit_bytes=48 << 20),
        cost_estimate=cost(10),
        name="attn_grad",
    )(rows, grad_q, grad_kv, grad_proj, attended)


def attend_back_kernel(q_ref, k_ref, v_ref, start_ref, inv_ref, grad_ref, gq_ref, gk_ref, gv_ref):
    @pl.when(pl.program_id(0) == 0)
    def _():
        gk_ref[...] = jnp.zeros_like(gk_ref)
        gv_ref[...] = jnp.zeros_like(gv_ref)

    first = pl.program_id(0) * QBLK
    keys = pl.ds(pl.multiple_of(first, QBLK), LMAX + QBLK)
    q, k, v, grad = q_ref[...], k_ref[keys], v_ref[keys], grad_ref[...]
    bent, exponent = block_scores(q, k, start_ref[...], first)
    probability = exponent * inv_ref[...]
    grad_prob = lax.dot_general(grad, v, (((1,), (1,)), ((), ())), preferred_element_type=F32)
    inner = jnp.sum(probability * grad_prob, axis=-1, keepdims=True)
    grad_scores = (probability * (grad_prob - inner) * (1.0 - bent * bent)).astype(BF16)
    scale = HD ** (-0.5)
    gq_ref[...] = jnp.dot(grad_scores, k, preferred_element_type=F32) * scale
    over_rows = (((0,), (0,)), ((), ()))
    gk_ref[keys] += lax.dot_general(grad_scores, q, over_rows, preferred_element_type=F32) * scale
    gv_ref[keys] += lax.dot_general(
        probability.astype(BF16), grad, over_rows, preferred_element_type=F32
    )


def attend_back(queries, key_rows, value_rows, starts, inverse, grad):
    rows = queries.shape[0]
    span = key_rows.shape[0]
    row_spec = pl.BlockSpec((QBLK, HD), lambda i: (i, 0))
    one_spec = pl.BlockSpec((QBLK, 1), lambda i: (i, 0))
    all_spec = pl.BlockSpec((span, HD), lambda i: (0, 0))
    return pl.pallas_call(
        attend_back_kernel,
        out_shape=(
            jax.ShapeDtypeStruct((rows, HD), F32),
            jax.ShapeDtypeStruct((span, HD), F32),
            jax.ShapeDtypeStruct((span, HD), F32),
        ),
        grid=(rows // QBLK,),
        in_specs=[row_spec, all_spec, all_spec, one_spec, one_spec, row_spec],
        out_specs=(row_spec, all_spec, all_spec),
        compiler_params=pltpu.CompilerParams(vmem_limit_bytes=48 << 20),
        cost_estimate=cost(20),
        name="attend_back",
    )(queries, key_rows, value_rows, starts, inverse, grad)


def token_tables(seq_lengths, index_vec):
    count = seq_lengths.shape[0]
    order = jnp.arange(count, dtype=jnp.int32)
    seq_ends = jnp.sum(
        jnp.where(order[None, :] <= order[:, None], seq_lengths[None, :], 0), axis=1
    )
    after_end = index_vec[:, None] >= seq_ends[None, :]
    return index_vec - jnp.sum(jnp.where(after_end, seq_lengths[None, :], 0), axis=1)


def rms_parts(value):
    return lax.rsqrt(jnp.mean(value * value, axis=-1, keepdims=True) + EPSILON)


def rms_forward(value, gain_vec):
    return value * rms_parts(value) * (1.0 + gain_vec)


def rms_backward(value, gain_vec, grad):
    r = rms_parts(value)
    scaled = (1.0 + gain_vec) * grad
    inner = jnp.mean(value * scaled, axis=-1, keepdims=True)
    return (r * scaled - value * (r * r * r * inner), jnp.sum(grad * value * r, axis=0))


def rotate(value, cosine, sine_part):
    half_width = value.shape[-1] // 2
    first_half = value[..., :half_width]
    second_half = value[..., half_width:]
    return jnp.concatenate(
        [
            first_half * cosine - second_half * sine_part,
            second_half * cosine + first_half * sine_part,
        ],
        axis=-1,
    )


def contract_last(left_side, right_side):
    return lax.dot_general(
        left_side, right_side, (((1,), (1,)), ((), ())), preferred_element_type=F32
    )


def contract_first(left_side, right_side):
    return lax.dot_general(
        left_side, right_side, (((0,), (0,)), ((), ())), preferred_element_type=F32
    )


def matmul(left_side, right_side):
    return jnp.dot(left_side, right_side, preferred_element_type=F32)


def gelu_parts(gate):
    k0 = 0.7978845608028654
    k1 = 0.044715
    t = jnp.tanh(k0 * (gate + k1 * gate * gate * gate))
    value = 0.5 * gate * (1.0 + t)
    slope = 0.5 * (1.0 + t) + 0.5 * gate * (1.0 - t * t) * k0 * (1.0 + 3.0 * k1 * gate * gate)
    return (value, slope)


def local(tokens, attn_weights, mlp_weights, norm_gains, seq_lengths, cotangent):
    tok_rows, width = tokens.shape
    peers = lax.axis_size(AXIS)
    planes = peers // PLANE
    share = width // peers
    row_share = attn_weights.shape[0]
    ff = mlp_weights.shape[1] // 3
    ffc = ff // PLANE
    plane_rows = PLANE * tok_rows
    halo = LMAX
    across = [[p * PLANE + i for p in range(planes)] for i in range(PLANE)]
    sibling = [(i, i ^ 1) for i in range(peers)]
    to_next = [(i, i + PLANE) for i in range(peers - PLANE)]
    to_prev = [(i + PLANE, i) for i in range(peers - PLANE)]
    me = lax.axis_index(AXIS)
    is_even = (me % 2) == 0
    plane_start = (me // PLANE) * plane_rows

    def split_features(value):
        value = value.reshape(value.shape[0], planes, 2, width // planes // 2)
        return value.transpose(0, 2, 1, 3).reshape(value.shape[0], width)

    def join_features(value):
        value = value.reshape(value.shape[0], 2, planes, width // planes // 2)
        return value.transpose(0, 2, 1, 3).reshape(value.shape[0], width)

    def gather_across(value):
        return lax.all_gather(value, AXIS, axis=0, tiled=True, axis_index_groups=across)

    def scatter_across(value):
        part = lax.psum_scatter(
            value.astype(BF16), AXIS, scatter_dimension=0, tiled=True, axis_index_groups=across
        )
        return part.reshape(PLANE, -1, part.shape[1])

    kv_full, q_rows, out_rows, gain_rows = lax.optimization_barrier(
        (*spread_attn(attn_weights, planes), norm_gains)
    )
    gain_block = jnp.pad(gain_rows.astype(F32), ((0, 8 - 4), (0, -share % 128)))
    gu_part, gain_blocks, kv_full, q_rows, out_rows = spread_gu(
        mlp_weights, gain_block, kv_full, q_rows, out_rows, peers
    )
    gain_full = gain_blocks[:, :4, :share].transpose(1, 0, 2).reshape(4, width)
    inputs = tokens.astype(F32)
    down_part, normed, kv_full, q_full = spread_down(
        mlp_weights, rms_forward(inputs, gain_full[0]).astype(BF16), kv_full, q_rows
    )
    q_cols, kv_cols = q_full.reshape(width, HD), kv_full.reshape(width, HD)
    gu_cols = gather_across(gu_part.reshape(-1, 2 * ffc))
    down_near = gather_across(down_part[: PLANE // 2].reshape(-1, ffc))
    down_far = gather_across(down_part[PLANE // 2 :].reshape(-1, ffc))

    query_index = plane_start + jnp.arange(plane_rows, dtype=jnp.int32)
    position = token_tables(seq_lengths, query_index)
    starts = (jnp.arange(plane_rows, dtype=jnp.int32) + halo - position)[:, None]
    frequency = 10000.0 ** (-jnp.arange(HD // 2, dtype=F32) * 2.0 / HD)
    angles = position.astype(F32)[:, None] * frequency[None, :]
    cosine, sine_part = jnp.cos(angles), jnp.sin(angles)
    kv_cosine = jnp.where(is_even, cosine, 1.0)
    kv_sine = jnp.where(is_even, sine_part, 0.0)

    kv_own = rotate(matmul(normed, kv_cols), kv_cosine, kv_sine).astype(BF16)
    kv_halo = lax.ppermute(kv_own[plane_rows - halo :], AXIS, to_next)
    kv_own, out_rows, q_cols = lax.optimization_barrier((kv_own, out_rows, q_cols))
    out_cols = spread_out(out_rows).reshape(width, HD)
    queries = rotate(matmul(normed, q_cols), cosine, sine_part).astype(BF16)
    kv_halo, out_cols, queries = lax.optimization_barrier((kv_halo, out_cols, queries))
    kv_mine = jnp.concatenate([kv_halo, kv_own], axis=0)
    kv_other = lax.ppermute(kv_mine, AXIS, sibling)
    key_rows = jnp.where(is_even, kv_mine, kv_other)
    value_rows = jnp.where(is_even, kv_other, kv_mine)
    attended, inverse = attend(queries, key_rows, value_rows, starts)
    attn_proj = product_scatter([attended], [out_cols], [0], PLANE_STEP, 2)

    middle = inputs + rms_forward(attn_proj, gain_full[1])
    mid_low = gather_square(rms_forward(middle, gain_full[2]).astype(BF16), PLANE_STEP, 1)
    gate_up = matmul(mid_low, gu_cols)
    gate, up = gate_up[:, :ffc], gate_up[:, ffc:]
    gelu, slope = gelu_parts(gate)
    hidden = (gelu * up).astype(BF16)
    hidden, gain_split, grad_split = lax.optimization_barrier(
        (hidden, split_features(gain_full[3:4]), split_features(cotangent))
    )
    raw_near = product_scatter([hidden], [down_near], [0], PLANE_STEP, 14)
    raw_far, grad_raw_low, down_grad = turn(
        hidden, down_far, raw_near, gain_split, grad_split, planes, PLANE_STEP, 9
    )
    mlp_raw = join_features(jnp.concatenate([raw_near, raw_far], axis=1))
    if not in_place(width // planes // 2):
        down_grad = join_features(down_grad.T).T
    layer_output = (middle + rms_forward(mlp_raw, gain_full[3])).astype(BF16)

    grad_out = cotangent.astype(F32)
    gain_four = jnp.sum(grad_out * mlp_raw * rms_parts(mlp_raw), axis=0)
    down_term = scatter_across(down_grad)
    grad_hidden = matmul(grad_raw_low, jnp.concatenate([down_near, down_far], axis=0))
    grad_normed_mid, gu_grad = product_scatter_back(
        [(slope * up * grad_hidden).astype(BF16), (gelu * grad_hidden).astype(BF16)],
        [gu_cols, gu_cols],
        [0, ffc],
        mid_low,
        PLANE_STEP,
        10,
    )
    gu_term = scatter_across(gu_grad)
    grad_mid_part, gain_three = rms_backward(middle, gain_full[2], grad_normed_mid)
    grad_middle = grad_out + grad_mid_part

    grad_proj, gain_two = rms_backward(attn_proj, gain_full[1], grad_middle)
    grad_proj_own, down_term = lax.optimization_barrier((grad_proj.astype(BF16), down_term))
    grad_proj_low = gather_square(grad_proj_own, PLANE_STEP, 1)
    grad_att = matmul(grad_proj_low, out_cols).astype(BF16)
    grad_query, grad_keys, grad_values = attend_back(
        queries, key_rows, value_rows, starts, inverse, grad_att
    )
    grad_mine = jnp.where(is_even, grad_keys, grad_values)
    grad_give = jnp.where(is_even, grad_values, grad_keys).astype(BF16)
    grad_kv = grad_mine + lax.ppermute(grad_give, AXIS, sibling).astype(F32)
    grad_back = lax.ppermute(grad_kv[:halo].astype(BF16), AXIS, to_prev).astype(F32)
    down_term, grad_kv = lax.optimization_barrier((down_term, grad_kv))
    down_rows = collect(down_term, 1, 6)
    down_rows, grad_back = lax.optimization_barrier((down_rows, grad_back))
    grad_kv = grad_kv[halo:] + jnp.pad(grad_back, ((plane_rows - halo, 0), (0, 0)))
    grad_q = rotate(grad_query, cosine, -sine_part).astype(BF16)
    grad_kv = rotate(grad_kv, kv_cosine, -kv_sine).astype(BF16)
    attn_term, grad_q, grad_kv = lax.optimization_barrier(
        (attn_grad(normed, grad_q, grad_kv, grad_proj_low, attended), grad_q, grad_kv)
    )
    attn_term = scatter_across(attn_term)
    grad_normed = product_scatter([grad_q, grad_kv], [q_cols, kv_cols], [0, 0], PLANE_STEP, 12)
    grad_in_part, gain_one = rms_backward(inputs, gain_full[0], grad_normed)
    grad_tokens = (grad_middle + grad_in_part).astype(BF16)

    gain_term = jnp.stack([gain_one, gain_two, gain_three, gain_four], axis=0)
    gain_term = gain_term.reshape(4, peers, share).transpose(1, 0, 2)
    gain_term = jnp.pad(gain_term, ((0, 0), (0, 8 - 4), (0, -share % 128)))
    gain_recv = collect_gains(gain_term)
    gu_term, gain_recv = lax.optimization_barrier((gu_term, gain_recv))
    gu_rows = collect(gu_term, 2, 13)
    grad_mlp = jnp.concatenate([gu_rows, down_rows], axis=1).astype(F32)
    grad_mlp, attn_term = lax.optimization_barrier((grad_mlp, attn_term))
    grad_attn = collect_attn(attn_term).astype(F32)
    grad_gains = jnp.sum(gain_recv[:, :4, :share], axis=0)
    return (layer_output, grad_tokens, grad_attn, grad_mlp, grad_gains)


def solution(mesh):
    return jax.shard_map(
        local,
        mesh=mesh,
        in_specs=(
            P("fsdp", None),
            P("fsdp", None),
            P("fsdp", None),
            P(None, "fsdp"),
            P(),
            P("fsdp", None),
        ),
        out_specs=(
            P("fsdp", None),
            P("fsdp", None),
            P("fsdp", None),
            P("fsdp", None),
            P(None, "fsdp"),
        ),
        check_vma=False,
    )
```

```python
from functools import partial

import jax
import jax.numpy as jnp
from jax import lax
from jax.experimental import pallas as pl
from jax.experimental.pallas import tpu as pltpu
from jax.sharding import PartitionSpec as P

H = 8
KVH = 4
HD = 256
LMAX = 1024
PLANE = 8
QBLK = 128

EPSILON = 1e-06
SOFT_CAP = 50.0
AXIS = "fsdp"
F32 = jnp.float32
BF16 = jnp.bfloat16
MESH = pl.DeviceIdType.MESH
ANY = pl.BlockSpec(memory_space=pl.ANY)
VMEM = pl.BlockSpec(memory_space=pltpu.VMEM)
DMA = pltpu.SemaphoreType.DMA


def flip(index, step):
    return index + step - 2 * step * ((index // step) % 2)


PLANE_STEP = 4


def partner(index, bits, step):
    for bit, by in ((1, 1), (2, 2), (4, step)):
        if bits & bit:
            index = flip(index, by)
    return index


def place(device, step):
    return device % 4 + 4 * ((device // step) % 2)


def greet(peers):
    barrier = pltpu.get_barrier_semaphore()
    for peer in peers:
        pl.semaphore_signal(barrier, inc=1, device_id=(peer,), device_id_type=MESH)
    pl.semaphore_wait(barrier, len(peers))


class Copies:
    def __init__(self, send_sem, recv_sem):
        self.send_sem, self.recv_sem, self.made, self.slots = send_sem, recv_sem, [], 0

    def prepare(self, source, target, device):
        slot = self.slots
        self.slots += 1
        return pltpu.make_async_remote_copy(
            src_ref=source,
            dst_ref=target,
            send_sem=self.send_sem.at[slot],
            recv_sem=self.recv_sem.at[slot],
            device_id=(device,),
            device_id_type=MESH,
        )

    def start(self, source, target, device):
        copy = self.prepare(source, target, device)
        copy.start()
        self.made.append(copy)
        return copy

    def sent(self):
        for copy in self.made:
            copy.wait_send()


def band(index, size):
    return pl.ds(pl.multiple_of(index * size, 8), size)


def lanes(index, size):
    return pl.ds(pl.multiple_of(index * size, 128), size)


def gather_steps(block_ref, full_ref, copies, own_sem, step):
    rows, width = block_ref.shape
    half = width // 2
    me = lax.axis_index(AXIS)
    sib, xn, yn = flip(me, 1), flip(me, 2), flip(me, step)
    diag = flip(xn, step)

    def at(device, side):
        return full_ref.at[band(place(device, step), rows), pl.ds(side * half, half)]

    def mine(side):
        return block_ref.at[:, pl.ds(side * half, half)]

    own_rows = full_ref.at[band(place(me, step), rows)]
    xa = copies.start(mine(0), at(me, 0), xn)
    ya = copies.start(mine(1), at(me, 1), yn)
    xb = copies.start(mine(1), at(me, 1), xn)
    yb = copies.start(mine(0), at(me, 0), yn)
    arriving = [copies.start(block_ref, own_rows, sib)]
    own = pltpu.make_async_copy(block_ref, own_rows, own_sem)
    own.start()

    def finish(on_rows=None):
        def to_sibling(device, side):
            arriving.append(copies.start(at(device, side), at(device, side), sib))

        def arrived(first, last, *devices):
            for copy in arriving[first:last]:
                copy.wait_recv()
            for device in devices:
                on_rows(device)

        if on_rows is not None:
            own.wait()
            arrived(0, 1, me)
        xa.wait_recv()
        yc = copies.start(at(xn, 0), at(xn, 0), yn)
        to_sibling(xn, 0)
        ya.wait_recv()
        xc = copies.start(at(yn, 1), at(yn, 1), xn)
        to_sibling(yn, 1)
        xb.wait_recv()
        to_sibling(xn, 1)
        yb.wait_recv()
        to_sibling(yn, 0)
        if on_rows is not None:
            arrived(1, 5, xn, yn)
        yc.wait_recv()
        to_sibling(diag, 0)
        xc.wait_recv()
        to_sibling(diag, 1)
        if on_rows is not None:
            arrived(5, 7, diag)
        else:
            arrived(0, 7)
            own.wait()

    return finish


GATHER_COPIES = 13


def cost(microseconds):
    return pl.CostEstimate(
        flops=int(microseconds * 1e7), transcendentals=0, bytes_accessed=int(microseconds * 3e4)
    )


def gather_kernel(block_ref, full_ref, own_sem, send_sem, recv_sem, *, step):
    me = lax.axis_index(AXIS)
    greet((flip(me, 1), flip(me, 2), flip(me, step)))
    copies = Copies(send_sem, recv_sem)
    gather_steps(block_ref, full_ref, copies, own_sem, step)()
    copies.sent()


def gather_square(block, step, collective_id):
    rows, width = block.shape
    return pl.pallas_call(
        partial(gather_kernel, step=step),
        out_shape=jax.ShapeDtypeStruct((PLANE * rows, width), block.dtype),
        in_specs=[ANY],
        out_specs=ANY,
        scratch_shapes=[DMA(()), DMA((GATHER_COPIES,)), DMA((GATHER_COPIES,))],
        compiler_params=pltpu.CompilerParams(collective_id=collective_id, has_side_effects=True),
        cost_estimate=cost(42),
        name="gather_square",
    )(block)


W_TILES = 2
SCATTER_COPIES = 14


def split_columns(width):
    left = (width // 2 + 127) // 128 * 128
    return pl.ds(0, left), pl.ds(left, width - left)


def product_scatter_steps(
    left_refs, right_refs, left_bufs, right_bufs, buffers, load_sem, copies, offsets, step, beside=None, line=None
):
    both, got, ra, rb, ra2, rb2 = buffers
    pairs = len(left_refs)
    rows, width = got.shape[1:]
    sides = split_columns(width)
    chunk = 48
    me = lax.axis_index(AXIS)
    core = me % 2
    sib, xn, yn = flip(me, 1), flip(me, 2), flip(me, step)
    order = (flip(xn, step), xn, yn, me)
    first, second = sides

    def chip_rows(device):
        return pl.ds(pl.multiple_of((place(device, step) // 2) * 2 * rows, 16), 2 * rows)

    def right_load(j, t):
        r = sides[t]
        source = right_refs[j].at[r, pl.ds(offsets[j], right_bufs[j].shape[1])]
        return pltpu.make_async_copy(source, right_bufs[j].at[r], load_sem.at[j, t])

    def left_load(j, i):
        r = chip_rows(order[i])
        return pltpu.make_async_copy(
            left_refs[j].at[r], left_bufs[j].at[r], load_sem.at[j, W_TILES + i]
        )

    for j in range(pairs):
        left_load(j, 0).start()
    for t in range(W_TILES):
        for j in range(pairs):
            right_load(j, t).start()
    for i in range(1, 4):
        for j in range(pairs):
            left_load(j, i).start()
    if beside is not None:
        beside[0]()
    if line is None:
        greet((sib, xn, yn))
    else:
        line[0].greet_with((sib, xn, yn))
        line[0].begin(line[1])

    def mine(i, cols):
        return both.at[i, band(core, rows), cols]

    def add(total, other):
        @pl.loop(0, rows // chunk)
        def _(k):
            r = pl.ds(pl.multiple_of(k * chunk, chunk), chunk)
            total[r] = (total[r].astype(F32) + other[r].astype(F32)).astype(total.dtype)

    loaded = set()

    def make(i, side):
        for j in range(pairs):
            if i not in loaded:
                left_load(j, i).wait()
            if i == 0:
                right_load(j, side).wait()
        loaded.add(i)
        r, cols = chip_rows(order[i]), sides[side]
        total = None
        for j in range(pairs):
            term = contract_last(left_bufs[j][r], right_bufs[j][cols])
            total = term if total is None else total + term
        both[i, :, cols] = total.astype(BF16)
        return copies.start(both.at[i, band(1 - core, rows), cols], got.at[i, :, cols], sib)

    def merge(crossing, i, side):
        cols = sides[side]
        crossing.wait_recv()
        add(mine(i, cols), got.at[i, :, cols])

    c0 = make(0, 0)
    c1 = make(0, 1)
    merge(c0, 0, 0)
    x0 = copies.start(mine(0, first), ra.at[0], xn)
    c2 = make(1, 0)
    merge(c1, 0, 1)
    y0 = copies.start(mine(0, second), rb.at[0], yn)
    c3 = make(2, 1)
    merge(c2, 1, 0)
    x1 = copies.start(mine(1, first), ra.at[1], xn)
    c4 = make(2, 0)
    merge(c3, 2, 1)
    y1 = copies.start(mine(2, second), rb.at[1], yn)
    c5 = make(1, 1)
    merge(c4, 2, 0)
    x0.wait_recv()
    add(mine(2, first), ra.at[0])
    y2 = copies.start(mine(2, first), ra2, yn)
    c6 = make(3, 0)
    merge(c5, 1, 1)
    y0.wait_recv()
    add(mine(1, second), rb.at[0])
    x2 = copies.start(mine(1, second), rb2, xn)
    c7 = make(3, 1)
    merge(c6, 3, 0)
    merge(c7, 3, 1)
    if beside is not None:
        beside[1]()
    if line is not None:
        line[0].run(line[1])
        line[0].end(line[1])
    for copy in (x1, y1, y2, x2):
        copy.wait_recv()
    own = both.at[3, band(core, rows)]

    def summed(r):
        return jnp.concatenate(
            [
                own[r, first].astype(F32) + ra[1, r].astype(F32) + ra2[r].astype(F32),
                own[r, second].astype(F32) + rb[1, r].astype(F32) + rb2[r].astype(F32),
            ],
            axis=1,
        )

    return summed


ROW_CHUNK = 48


def product_scatter_kernel(*refs, pairs, offsets, step):
    left_refs, right_refs, out_ref = refs[:pairs], refs[pairs : 2 * pairs], refs[2 * pairs]
    left_bufs = refs[2 * pairs + 1 : 3 * pairs + 1]
    right_bufs = refs[3 * pairs + 1 : 4 * pairs + 1]
    buffers, (load_sem, send_sem, recv_sem) = refs[4 * pairs + 1 : -3], refs[-3:]
    copies = Copies(send_sem, recv_sem)
    summed = product_scatter_steps(
        left_refs, right_refs, left_bufs, right_bufs, buffers, load_sem, copies, offsets, step
    )

    @pl.loop(0, out_ref.shape[0] // ROW_CHUNK)
    def _(k):
        r = pl.ds(pl.multiple_of(k * ROW_CHUNK, ROW_CHUNK), ROW_CHUNK)
        out_ref[r] = summed(r)

    copies.sent()


def scatter_buffers(rows, width):
    left, right = [side.size for side in split_columns(width)]
    return [
        pltpu.VMEM((4, 2 * rows, width), BF16),
        pltpu.VMEM((4, rows, width), BF16),
        pltpu.VMEM((2, rows, left), BF16),
        pltpu.VMEM((2, rows, right), BF16),
        pltpu.VMEM((rows, left), BF16),
        pltpu.VMEM((rows, right), BF16),
    ]


def product_scatter(lefts, rights, offsets, step, collective_id):
    pairs = len(lefts)
    rows, width = lefts[0].shape[0] // PLANE, rights[0].shape[0]
    return pl.pallas_call(
        partial(product_scatter_kernel, pairs=pairs, offsets=offsets, step=step),
        out_shape=jax.ShapeDtypeStruct((rows, width), F32),
        in_specs=[ANY] * (2 * pairs),
        out_specs=VMEM,
        scratch_shapes=[
            *[pltpu.VMEM(value.shape, BF16) for value in lefts],
            *[pltpu.VMEM((width, value.shape[1]), BF16) for value in lefts],
            *scatter_buffers(rows, width),
            DMA((pairs, W_TILES + 4)),
            DMA((SCATTER_COPIES,)),
            DMA((SCATTER_COPIES,)),
        ],
        compiler_params=pltpu.CompilerParams(
            collective_id=collective_id, has_side_effects=True, vmem_limit_bytes=56 << 20
        ),
        cost_estimate=cost(50),
        name="product_scatter",
    )(*lefts, *rights)


BACK_TILE = 384


def back_kernel(*refs, pairs, offsets, step):
    left_refs, right_refs, rows_ref = refs[:pairs], refs[pairs : 2 * pairs], refs[2 * pairs]
    out_ref, term_ref = refs[2 * pairs + 1 : 2 * pairs + 3]
    scratch = refs[2 * pairs + 3 :]
    left_bufs, right_bufs = scratch[:pairs], scratch[pairs : 2 * pairs]
    rows_buf, stage = scratch[2 * pairs : 2 * pairs + 2]
    buffers = scratch[2 * pairs + 2 : -5]
    load_sem, rows_sem, store_sem, send_sem, recv_sem = scratch[-5:]
    copies = Copies(send_sem, recv_sem)
    rows_load = pltpu.make_async_copy(rows_ref, rows_buf, rows_sem)
    tiles = rows_ref.shape[1] // BACK_TILE
    width = left_refs[0].shape[1]

    def store(t):
        return pltpu.make_async_copy(
            stage.at[t % 2],
            term_ref.at[pl.ds(pl.multiple_of(t * BACK_TILE, 16), BACK_TILE)],
            store_sem.at[t % 2],
        )

    def beside():
        rows_load.wait()

        @pl.loop(0, tiles)
        def _(t):
            @pl.when(t >= 2)
            def _():
                store(t - 2).wait()

            columns = rows_buf[:, pl.ds(pl.multiple_of(t * BACK_TILE, BACK_TILE), BACK_TILE)]
            for j in range(pairs):
                term = contract_first(columns, left_bufs[j][...])
                stage[t % 2, :, pl.ds(j * width, width)] = term.astype(BF16)
            store(t).start()

    def start_rows():
        rows_load.start()

    summed = product_scatter_steps(
        left_refs,
        right_refs,
        left_bufs,
        right_bufs,
        buffers,
        load_sem,
        copies,
        offsets,
        step,
        (start_rows, beside),
    )

    @pl.loop(0, out_ref.shape[0] // ROW_CHUNK)
    def _(k):
        r = pl.ds(pl.multiple_of(k * ROW_CHUNK, ROW_CHUNK), ROW_CHUNK)
        out_ref[r] = summed(r)

    for t in range(tiles - 2, tiles):
        store(t).wait()
    copies.sent()


def product_scatter_back(lefts, rights, offsets, rows, step, collective_id):
    pairs = len(lefts)
    count, width = lefts[0].shape[0] // PLANE, rights[0].shape[0]
    columns = sum(value.shape[1] for value in lefts)
    return pl.pallas_call(
        partial(back_kernel, pairs=pairs, offsets=offsets, step=step),
        out_shape=(
            jax.ShapeDtypeStruct((count, width), F32),
            jax.ShapeDtypeStruct((rows.shape[1], columns), BF16),
        ),
        in_specs=[ANY] * (2 * pairs + 1),
        out_specs=(VMEM, ANY),
        scratch_shapes=[
            *[pltpu.VMEM(value.shape, BF16) for value in lefts],
            *[pltpu.VMEM((width, value.shape[1]), BF16) for value in lefts],
            pltpu.VMEM(rows.shape, BF16),
            pltpu.VMEM((2, BACK_TILE, columns), BF16),
            *scatter_buffers(count, width),
            DMA((pairs, W_TILES + 4)),
            DMA(()),
            DMA((2,)),
            DMA((SCATTER_COPIES,)),
            DMA((SCATTER_COPIES,)),
        ],
        compiler_params=pltpu.CompilerParams(
            collective_id=collective_id, has_side_effects=True, vmem_limit_bytes=62 << 20
        ),
        cost_estimate=cost(60),
        name="product_scatter_back",
    )(*lefts, *rights, rows)


def product_scatter_line_kernel(left_ref, right_ref, full_in, out_ref, full_ref, *refs, step):
    left_buf, right_buf = refs[:2]
    buffers, (load_sem, send_sem, recv_sem, line_send, line_recv) = refs[2:-5], refs[-5:]
    copies = Copies(send_sem, recv_sem)
    line = Line(full_ref, line_send, line_recv)
    summed = product_scatter_steps(
        [left_ref],
        [right_ref],
        [left_buf],
        [right_buf],
        buffers,
        load_sem,
        copies,
        [0],
        step,
        line=(line, line_hops(line.planes)[1]),
    )

    @pl.loop(0, out_ref.shape[0] // ROW_CHUNK)
    def _(k):
        r = pl.ds(pl.multiple_of(k * ROW_CHUNK, ROW_CHUNK), ROW_CHUNK)
        out_ref[r] = summed(r)

    copies.sent()


def product_scatter_line(left, right, full, step, collective_id):
    rows, width = left.shape[0] // PLANE, right.shape[0]
    return pl.pallas_call(
        partial(product_scatter_line_kernel, step=step),
        out_shape=(
            jax.ShapeDtypeStruct((rows, width), F32),
            jax.ShapeDtypeStruct(full.shape, full.dtype),
        ),
        in_specs=[ANY, ANY, ANY],
        out_specs=(VMEM, ANY),
        scratch_shapes=[
            pltpu.VMEM(left.shape, BF16),
            pltpu.VMEM(right.shape, BF16),
            *scatter_buffers(rows, width),
            DMA((1, W_TILES + 4)),
            DMA((SCATTER_COPIES,)),
            DMA((SCATTER_COPIES,)),
            *line_semaphores(line_hops(full.shape[0])[1]),
        ],
        input_output_aliases={2: 1},
        compiler_params=pltpu.CompilerParams(
            collective_id=collective_id, has_side_effects=True, vmem_limit_bytes=48 << 20
        ),
        cost_estimate=cost(50),
        name="product_scatter_line",
    )(left, right, full)


TURN_TILE = 768


def in_place(rows):
    return rows % 16 == 0


def turn_kernel(
    left_ref,
    right_ref,
    near_ref,
    gain_ref,
    grad_ref,
    raw_ref,
    full_ref,
    term_ref,
    *refs,
    planes,
    step,
):
    left_buf, right_buf, gathered, total, grad_own, stage = refs[:6]
    buffers, (load_sem, own_sem, store_sem, send_sem, recv_sem) = refs[6:-5], refs[-5:]
    rows, width = grad_ref.shape
    half = width // 2
    piece = half // planes
    copies = Copies(send_sem, recv_sem)
    summed = product_scatter_steps(
        [left_ref], [right_ref], [left_buf], [right_buf], buffers, load_sem, copies, [0], step
    )
    gain = gain_ref[...]

    @pl.loop(0, rows // ROW_CHUNK)
    def _(k):
        r = pl.ds(pl.multiple_of(k * ROW_CHUNK, ROW_CHUNK), ROW_CHUNK)
        far = summed(r)
        raw_ref[r] = far
        value = jnp.concatenate([near_ref[r], far], axis=1)
        scale = lax.rsqrt(jnp.mean(value * value, axis=1, keepdims=True) + EPSILON)
        scaled = (1.0 + gain) * grad_ref[r].astype(F32)
        inner = jnp.mean(value * scaled, axis=1, keepdims=True)
        grad_own[r] = (scale * scaled - value * (scale * scale * scale * inner)).astype(BF16)

    stores = []

    def store_term(side):
        for plane in range(planes):
            start = side * half + plane * piece
            target = plane * 2 * piece + side * piece if in_place(piece) else start
            pltpu.make_async_copy(
                stage.at[pl.ds(start, piece)] if in_place(piece) else stage.at[pl.ds(side * half, half)],
                term_ref.at[pl.ds(target, piece)]
                if in_place(piece)
                else term_ref.at[pl.ds(side * half, half)],
                store_sem.at[4],
            ).start()
            if not in_place(piece):
                break

    def on_rows(device):
        slot = len(stores)
        r = pl.ds(pl.multiple_of((place(device, step) // 2) * 2 * rows, 16), 2 * rows)
        store = pltpu.make_async_copy(gathered.at[r], full_ref.at[r], store_sem.at[slot])
        store.start()
        stores.append(store)
        right = left_buf[r]
        if slot < 3:

            @pl.loop(0, width // TURN_TILE)
            def _(t):
                w = pl.ds(pl.multiple_of(t * TURN_TILE, TURN_TILE), TURN_TILE)
                term = contract_first(gathered[r, w], right)
                if slot == 0:
                    total[w] = term
                else:
                    total[w] += term
        else:
            for side in range(2):

                @pl.loop(0, 3)
                def _(t):
                    w = pl.ds(
                        pl.multiple_of(side * half + t * (half // 3), half // 3), half // 3
                    )
                    term = contract_first(gathered[r, w], right)
                    stage[w] = (total[w] + term).astype(BF16)

                store_term(side)

    gather_steps(grad_own, gathered, copies, own_sem, step)(on_rows)
    pltpu.make_async_copy(stage, term_ref, store_sem.at[4]).wait()
    for store in stores:
        store.wait()
    copies.sent()


def turn(left, right, near, gain_row, grad, planes, step, collective_id):
    rows, width = grad.shape
    count = SCATTER_COPIES + GATHER_COPIES
    return pl.pallas_call(
        partial(turn_kernel, planes=planes, step=step),
        out_shape=(
            jax.ShapeDtypeStruct((rows, width // 2), F32),
            jax.ShapeDtypeStruct((PLANE * rows, width), BF16),
            jax.ShapeDtypeStruct((width, left.shape[1]), BF16),
        ),
        in_specs=[ANY, ANY, VMEM, VMEM, VMEM],
        out_specs=(VMEM, ANY, ANY),
        scratch_shapes=[
            pltpu.VMEM(left.shape, BF16),
            pltpu.VMEM(right.shape, BF16),
            pltpu.VMEM((PLANE * rows, width), BF16),
            pltpu.VMEM((width, left.shape[1]), F32),
            pltpu.VMEM((rows, width), BF16),
            pltpu.VMEM((width, left.shape[1]), BF16),
            *scatter_buffers(rows, width // 2),
            DMA((1, W_TILES + 4)),
            DMA(()),
            DMA((5,)),
            DMA((count,)),
            DMA((count,)),
        ],
        compiler_params=pltpu.CompilerParams(
            collective_id=collective_id, has_side_effects=True, vmem_limit_bytes=60 << 20
        ),
        cost_estimate=cost(50),
        name="turn",
    )(left, right, near, gain_row, grad)


def attn_columns(column):
    query_width = H * HD
    key_offset = query_width + (column % 2) * KVH * HD + (column // 2) * HD
    return (column * HD, key_offset, query_width + 2 * KVH * HD + column * HD)


def greet_all(peers):
    me = lax.axis_index(AXIS)
    barrier = pltpu.get_barrier_semaphore()

    @pl.loop(1, peers)
    def _(k):
        device = lax.rem(me + k, peers)
        pl.semaphore_signal(barrier, inc=1, device_id=(device,), device_id_type=MESH)

    pl.semaphore_wait(barrier, peers - 1)


def exchange_all(source_of, target_ref, send_sem, recv_sem):
    peers = target_ref.shape[0]
    me = lax.axis_index(AXIS)

    def copy(k):
        device = lax.rem(me + k, peers)
        return pltpu.make_async_remote_copy(
            src_ref=source_of(device),
            dst_ref=target_ref.at[me],
            send_sem=send_sem.at[k],
            recv_sem=recv_sem.at[k],
            device_id=(device,),
            device_id_type=MESH,
        )

    @pl.loop(1, peers)
    def _(k):
        copy(k).start()

    def finish():
        @pl.loop(1, peers)
        def _(k):
            copy(k).wait()

    return finish


ORDER = (6, 7, 2, 3, 4, 5, 1)


def swap_steps(pieces_of, targets, copies, own_sem, step):
    me = lax.axis_index(AXIS)
    moved = []
    for bits in ORDER:
        peer = partner(me, bits, step)
        for source, target in zip(pieces_of(place(peer, step)), targets):
            moved.append(copies.start(source, target, peer))
    owns = []
    for slot, (source, target) in enumerate(zip(pieces_of(place(me, step)), targets)):
        own = pltpu.make_async_copy(source, target, own_sem.at[slot])
        own.start()
        owns.append(own)

    def finish():
        for own in owns:
            own.wait()
        for copy in moved:
            copy.wait_recv()

    return finish


def swap_half_steps(piece_of, target, near, copies, own_sem, step):
    me = lax.axis_index(AXIS)
    low = (place(me, step) < PLANE // 2) == near
    moved = []
    for bits in ORDER:
        peer = partner(me, bits, step)
        copy = copies.prepare(piece_of(place(peer, step)), target, peer)
        moved.append((copy, low != bool(bits & 4)))
    own = pltpu.make_async_copy(piece_of(place(me, step)), target, own_sem)

    @pl.when(low)
    def _():
        for copy, unused in moved:
            copy.start()
        own.start()

    def finish():
        for copy, comes in moved:

            @pl.when(comes)
            def _():
                copy.wait_recv()

        @pl.when(low)
        def _():
            own.wait()
            for copy, unused in moved:
                copy.wait_send()

    return finish


def square(step):
    me = lax.axis_index(AXIS)
    return [partner(me, bits, step) for bits in ORDER]


def wide(offset):
    return pl.ds(pl.multiple_of(offset, 128), HD)


class Line:
    def __init__(self, full_ref, send_sem, recv_sem, own_ref=None):
        me = lax.axis_index(AXIS)
        self.own = own_ref
        self.full, self.planes = full_ref, full_ref.shape[0]
        self.send_sem, self.recv_sem = send_sem, recv_sem
        self.plane = me // PLANE
        peers = self.planes * PLANE
        self.devices = (lax.rem(me + PLANE, peers), lax.rem(me + peers - PLANE, peers))

    def copy(self, way, slot, source, first=False):
        return pltpu.make_async_remote_copy(
            src_ref=self.own if first and self.own is not None else self.full.at[source],
            dst_ref=self.full.at[source],
            send_sem=self.send_sem.at[way, slot],
            recv_sem=self.recv_sem.at[way, slot],
            device_id=(self.devices[way],),
            device_id_type=MESH,
        )

    def sends(self, way, hop):
        if way == 0:
            source = self.plane - (hop - 1)
            return (self.plane + 1 < self.planes) & (source >= 0), source
        source = self.plane + (hop - 1)
        return (self.plane >= 1) & (source < self.planes), source

    def greet(self):
        barrier = pltpu.get_barrier_semaphore()
        count = 0
        for way, there in enumerate((self.plane + 1 < self.planes, self.plane >= 1)):

            @pl.when(there)
            def _():
                pl.semaphore_signal(
                    barrier, inc=1, device_id=(self.devices[way],), device_id_type=MESH
                )

            count = count + there.astype(jnp.int32)
        return count

    def start(self, hop, slot):
        for way in range(2):
            there, source = self.sends(way, hop)

            @pl.when(there)
            def _():
                self.copy(way, slot, source, hop == 1).start()

    def arrived(self, hop, slot):
        for way in range(2):
            source = self.plane - hop if way == 0 else self.plane + hop

            @pl.when((source >= 0) & (source < self.planes))
            def _():
                self.copy(way, slot, source).wait_recv()

    def sent(self, hop, slot):
        for way in range(2):
            there, source = self.sends(way, hop)

            @pl.when(there)
            def _():
                self.copy(way, slot, source, hop == 1).wait_send()

    def greet_with(self, peers):
        greet_line(self, peers)

    def begin(self, hops):
        if hops:
            self.start(hops[0], 0)

    def run(self, hops):
        for slot, hop in enumerate(hops):
            self.arrived(hop, slot)
            if slot + 1 < len(hops):
                self.start(hop + 1, slot + 1)

    def end(self, hops):
        for slot, hop in enumerate(hops):
            self.sent(hop, slot)


def line_hops(planes):
    hops = list(range(1, planes))
    first = (2 * len(hops) + 2) // 3
    return hops[:first], hops[first:]


def line_semaphores(hops):
    count = max(1, len(hops))
    return [DMA((2, count)), DMA((2, count))]


def greet_line(line, peers):
    barrier = pltpu.get_barrier_semaphore()
    for peer in peers:
        pl.semaphore_signal(barrier, inc=1, device_id=(peer,), device_id_type=MESH)
    pl.semaphore_wait(barrier, len(peers) + line.greet())


def row_bands(weights_ref):
    return [weights_ref.at[:, pl.ds(start * HD, H * HD)] for start in (0, H + 2 * KVH)]


def spread_attn_kernel(weights_ref, kv_ref, q_ref, out_ref, own_sem, send_sem, recv_sem, *sems):
    me = lax.axis_index(AXIS)
    plane, here = me // PLANE, place(me, PLANE_STEP)
    q_rows, out_rows = row_bands(weights_ref)
    q_line = Line(q_ref, sems[0], sems[1], q_rows)
    out_line = Line(out_ref, sems[2], sems[3], out_rows)
    hops = line_hops(out_line.planes)[0]
    greet_line(out_line, square(PLANE_STEP))
    out_line.begin(hops)
    q_line.begin([1])
    owns = []
    for slot, (source, target) in enumerate(((q_rows, q_ref), (out_rows, out_ref))):
        own = pltpu.make_async_copy(source, target.at[plane], own_sem.at[1 + slot])
        own.start()
        owns.append(own)
    copies = Copies(send_sem, recv_sem)
    spread = swap_steps(
        lambda c: [weights_ref.at[:, wide(attn_columns(c)[1])]],
        [kv_ref.at[plane, here]],
        copies,
        own_sem,
        PLANE_STEP,
    )
    out_line.run(hops)
    q_line.run([1])
    spread()
    for own in owns:
        own.wait()
    out_line.end(hops)
    q_line.end([1])
    copies.sent()


def spread_attn(weights, planes):
    rows = weights.shape[0]
    return pl.pallas_call(
        spread_attn_kernel,
        out_shape=(
            jax.ShapeDtypeStruct((planes, PLANE, rows, HD), BF16),
            jax.ShapeDtypeStruct((planes, rows, H * HD), BF16),
            jax.ShapeDtypeStruct((planes, rows, H * HD), BF16),
        ),
        in_specs=[ANY],
        out_specs=(ANY, ANY, ANY),
        scratch_shapes=[
            DMA((3,)),
            DMA((7,)),
            DMA((7,)),
            *line_semaphores([1]),
            *line_semaphores(line_hops(planes)[0]),
        ],
        compiler_params=pltpu.CompilerParams(collective_id=3, has_side_effects=True),
        name="spread_attn",
    )(weights)


def spread_gu_kernel(
    weights_ref,
    gain_ref,
    kv_in,
    q_in,
    out_in,
    gu_ref,
    gains_ref,
    kv_ref,
    q_ref,
    out_ref,
    near_ref,
    own_sem,
    send_sem,
    recv_sem,
    gain_send,
    gain_recv,
    *sems,
):
    peers = gains_ref.shape[0]
    ffc = gu_ref.shape[2] // 2
    me = lax.axis_index(AXIS)
    here = place(me, PLANE_STEP)
    kv_line = Line(kv_ref, sems[0], sems[1])
    q_line = Line(q_ref, sems[2], sems[3])
    out_line = Line(out_ref, sems[4], sems[5])
    kv_hops, out_hops = line_hops(kv_line.planes)
    q_hops = list(range(2, kv_line.planes))
    greet_all(peers)
    q_line.begin(q_hops)
    out_line.begin(out_hops)
    kv_line.begin(kv_hops)
    gains_done = exchange_all(lambda device: gain_ref, gains_ref, gain_send, gain_recv)
    own = pltpu.make_async_copy(gain_ref, gains_ref.at[me], own_sem.at[2])
    own.start()
    copies = Copies(send_sem, recv_sem)
    spread = swap_steps(
        lambda c: [weights_ref.at[:, lanes(slot * PLANE + c, ffc)] for slot in range(2)],
        [gu_ref.at[here, :, pl.ds(slot * ffc, ffc)] for slot in range(2)],
        copies,
        own_sem,
        PLANE_STEP,
    )
    near = swap_half_steps(
        lambda c: weights_ref.at[:, lanes(2 * PLANE + c, ffc)],
        near_ref.at[me // PLANE, here % 4],
        True,
        copies,
        own_sem.at[3],
        PLANE_STEP,
    )
    q_line.run(q_hops)
    out_line.run(out_hops)
    kv_line.run(kv_hops)
    spread()
    near()
    own.wait()
    gains_done()
    for line, hops in ((q_line, q_hops), (out_line, out_hops), (kv_line, kv_hops)):
        line.end(hops)
    copies.sent()


def spread_gu(weights, gain_block, kv_full, q_rows, out_rows, peers):
    rows = weights.shape[0]
    ffc = weights.shape[1] // 3 // PLANE
    planes = kv_full.shape[0]
    kv_hops, out_hops = line_hops(planes)
    return pl.pallas_call(
        spread_gu_kernel,
        out_shape=(
            jax.ShapeDtypeStruct((PLANE, rows, 2 * ffc), BF16),
            jax.ShapeDtypeStruct((peers,) + gain_block.shape, gain_block.dtype),
            jax.ShapeDtypeStruct(kv_full.shape, kv_full.dtype),
            jax.ShapeDtypeStruct(q_rows.shape, q_rows.dtype),
            jax.ShapeDtypeStruct(out_rows.shape, out_rows.dtype),
            jax.ShapeDtypeStruct((planes, PLANE // 2, rows, ffc), BF16),
        ),
        in_specs=[ANY] * 5,
        out_specs=(ANY,) * 6,
        scratch_shapes=[
            DMA((4,)),
            DMA((21,)),
            DMA((21,)),
            DMA((peers,)),
            DMA((peers,)),
            *line_semaphores(kv_hops),
            *line_semaphores(range(2, planes)),
            *line_semaphores(out_hops),
        ],
        input_output_aliases={2: 2, 3: 3, 4: 4},
        compiler_params=pltpu.CompilerParams(collective_id=4, has_side_effects=True),
        cost_estimate=cost(38),
        name="spread_gu",
    )(weights, gain_block, kv_full, q_rows, out_rows)


def spread_down_kernel(
    weights_ref,
    block_ref,
    kv_in,
    rows_ref,
    near_in,
    far_ref,
    full_ref,
    kv_ref,
    q_ref,
    near_ref,
    own_sem,
    send_sem,
    recv_sem,
    *sems,
):
    ffc = far_ref.shape[2]
    here = place(lax.axis_index(AXIS), PLANE_STEP)
    line = Line(kv_ref, sems[0], sems[1])
    near_line = Line(near_ref, sems[2], sems[3])
    near_hops, hops = line_hops(line.planes)
    greet_line(line, square(PLANE_STEP))
    line.begin(hops)
    near_line.begin(near_hops)
    copies = Copies(send_sem, recv_sem)
    gathered = gather_steps(block_ref, full_ref, copies, own_sem.at[2], PLANE_STEP)
    spread = swap_steps(
        lambda c: [rows_ref.at[:, :, lanes(c, HD)]],
        [q_ref.at[:, here]],
        copies,
        own_sem,
        PLANE_STEP,
    )
    far = swap_half_steps(
        lambda c: weights_ref.at[:, lanes(2 * PLANE + c, ffc)],
        far_ref.at[here % 4],
        False,
        copies,
        own_sem.at[1],
        PLANE_STEP,
    )
    gathered()
    line.run(hops)
    near_line.run(near_hops)
    spread()
    far()
    line.end(hops)
    near_line.end(near_hops)
    copies.sent()


def spread_down(weights, block, kv_full, q_rows, near_full):
    rows = weights.shape[0]
    ffc = weights.shape[1] // 3 // PLANE
    planes = kv_full.shape[0]
    count = GATHER_COPIES + 14
    near_hops, hops = line_hops(planes)
    return pl.pallas_call(
        spread_down_kernel,
        out_shape=(
            jax.ShapeDtypeStruct((PLANE // 2, rows, ffc), BF16),
            jax.ShapeDtypeStruct((PLANE * block.shape[0], block.shape[1]), BF16),
            jax.ShapeDtypeStruct(kv_full.shape, kv_full.dtype),
            jax.ShapeDtypeStruct((planes, PLANE, rows, HD), BF16),
            jax.ShapeDtypeStruct(near_full.shape, near_full.dtype),
        ),
        in_specs=[ANY] * 5,
        out_specs=(ANY,) * 5,
        scratch_shapes=[
            DMA((3,)),
            DMA((count,)),
            DMA((count,)),
            *line_semaphores(hops),
            *line_semaphores(near_hops),
        ],
        input_output_aliases={2: 2, 4: 4},
        compiler_params=pltpu.CompilerParams(collective_id=5, has_side_effects=True),
        cost_estimate=cost(1),
        name="spread_down",
    )(weights, block, kv_full, q_rows, near_full)


def spread_out_kernel(rows_ref, full_ref, own_sem, send_sem, recv_sem):
    here = place(lax.axis_index(AXIS), PLANE_STEP)
    greet(square(PLANE_STEP))
    copies = Copies(send_sem, recv_sem)
    swap_steps(
        lambda c: [rows_ref.at[:, :, lanes(c, HD)]],
        [full_ref.at[:, here]],
        copies,
        own_sem,
        PLANE_STEP,
    )()
    copies.sent()


def spread_out(out_rows):
    planes, rows = out_rows.shape[:2]
    return pl.pallas_call(
        spread_out_kernel,
        out_shape=jax.ShapeDtypeStruct((planes, PLANE, rows, HD), BF16),
        in_specs=[ANY],
        out_specs=ANY,
        scratch_shapes=[DMA((1,)), DMA((7,)), DMA((7,))],
        compiler_params=pltpu.CompilerParams(collective_id=11, has_side_effects=True),
        cost_estimate=cost(0.1),
        name="spread_out",
    )(out_rows)


def collect_kernel(term_ref, rows_ref, own_sem, send_sem, recv_sem):
    here = place(lax.axis_index(AXIS), PLANE_STEP)
    count = own_sem.shape[0]
    ffc = term_ref.shape[2] // count
    greet(square(PLANE_STEP))
    copies = Copies(send_sem, recv_sem)
    swap_steps(
        lambda c: [term_ref.at[c, :, pl.ds(slot * ffc, ffc)] for slot in range(count)],
        [rows_ref.at[:, lanes(slot * PLANE + here, ffc)] for slot in range(count)],
        copies,
        own_sem,
        PLANE_STEP,
    )()
    copies.sent()


def collect(term, count, collective_id):
    rows, columns = term.shape[1:]
    return pl.pallas_call(
        collect_kernel,
        out_shape=jax.ShapeDtypeStruct((rows, PLANE * columns), BF16),
        in_specs=[ANY],
        out_specs=ANY,
        scratch_shapes=[DMA((count,)), DMA((7 * count,)), DMA((7 * count,))],
        compiler_params=pltpu.CompilerParams(collective_id=collective_id, has_side_effects=True),
        cost_estimate=cost(0.1),
        name="collect",
    )(term)


def collect_attn_kernel(term_ref, rows_ref, own_sem, send_sem, recv_sem):
    here = place(lax.axis_index(AXIS), PLANE_STEP)
    greet(square(PLANE_STEP))
    copies = Copies(send_sem, recv_sem)
    swap_steps(
        lambda c: [term_ref.at[c, :, pl.ds(slot * HD, HD)] for slot in range(3)],
        [rows_ref.at[:, wide(offset)] for offset in attn_columns(here)],
        copies,
        own_sem,
        PLANE_STEP,
    )()
    copies.sent()


def collect_attn(term):
    rows = term.shape[1]
    return pl.pallas_call(
        collect_attn_kernel,
        out_shape=jax.ShapeDtypeStruct((rows, PLANE * 3 * HD), BF16),
        in_specs=[ANY],
        out_specs=ANY,
        scratch_shapes=[DMA((3,)), DMA((21,)), DMA((21,))],
        compiler_params=pltpu.CompilerParams(collective_id=7, has_side_effects=True),
        name="collect_attn",
    )(term)


def collect_gains_kernel(gain_ref, gains_ref, own_sem, gain_send, gain_recv):
    me = lax.axis_index(AXIS)
    greet_all(gain_ref.shape[0])
    done = exchange_all(lambda device: gain_ref.at[device], gains_ref, gain_send, gain_recv)
    own = pltpu.make_async_copy(gain_ref.at[me], gains_ref.at[me], own_sem)
    own.start()
    own.wait()
    done()


def collect_gains(gain_blocks):
    peers = gain_blocks.shape[0]
    return pl.pallas_call(
        collect_gains_kernel,
        out_shape=jax.ShapeDtypeStruct(gain_blocks.shape, gain_blocks.dtype),
        in_specs=[ANY],
        out_specs=ANY,
        scratch_shapes=[DMA(()), DMA((peers,)), DMA((peers,))],
        compiler_params=pltpu.CompilerParams(collective_id=8, has_side_effects=True),
        name="collect_gains",
    )(gain_blocks)


def block_scores(q, k, start, first):
    scores = lax.dot_general(q, k, (((1,), (1,)), ((), ())), preferred_element_type=F32)
    bent = jnp.tanh(scores * (HD ** (-0.5) / SOFT_CAP))
    rows, span = scores.shape
    key_at = lax.broadcasted_iota(jnp.int32, (rows, span), 1)
    row_at = lax.broadcasted_iota(jnp.int32, (rows, span), 0)
    allowed = (key_at + first >= start) & (key_at <= row_at + LMAX)
    return (bent, jnp.where(allowed, jnp.exp(SOFT_CAP * bent), 0.0))


def attend_kernel(q_ref, k_ref, v_ref, start_ref, out_ref, inv_ref):
    first = pl.program_id(0) * QBLK
    keys = pl.ds(pl.multiple_of(first, QBLK), LMAX + QBLK)
    unused_bent, exponent = block_scores(q_ref[...], k_ref[keys], start_ref[...], first)
    inverse = 1.0 / jnp.sum(exponent, axis=-1, keepdims=True)
    weights = (exponent * inverse).astype(BF16)
    out_ref[...] = jnp.dot(weights, v_ref[keys], preferred_element_type=F32).astype(BF16)
    inv_ref[...] = inverse


def attend(queries, key_rows, value_rows, starts):
    rows = queries.shape[0]
    span = key_rows.shape[0]
    row_spec = pl.BlockSpec((QBLK, HD), lambda i: (i, 0))
    one_spec = pl.BlockSpec((QBLK, 1), lambda i: (i, 0))
    all_spec = pl.BlockSpec((span, HD), lambda i: (0, 0))
    return pl.pallas_call(
        attend_kernel,
        out_shape=(
            jax.ShapeDtypeStruct((rows, HD), BF16),
            jax.ShapeDtypeStruct((rows, 1), F32),
        ),
        grid=(rows // QBLK,),
        in_specs=[row_spec, all_spec, all_spec, one_spec],
        out_specs=(row_spec, one_spec),
        compiler_params=pltpu.CompilerParams(vmem_limit_bytes=40 << 20),
        cost_estimate=cost(1),
        name="attend",
    )(queries, key_rows, value_rows, starts)


GRAD_TILE = 256


def attn_grad_kernel(rows_ref, q_ref, kv_ref, proj_ref, attended_ref, out_ref):
    for slot, (left, right) in enumerate(
        ((rows_ref, q_ref), (rows_ref, kv_ref), (proj_ref, attended_ref))
    ):
        out_ref[:, pl.ds(slot * HD, HD)] = contract_first(left[...], right[...]).astype(BF16)


def attn_grad(rows, grad_q, grad_kv, grad_proj, attended):
    count, width = rows.shape
    tile = pl.BlockSpec((count, GRAD_TILE), lambda i: (0, i))
    whole = pl.BlockSpec((count, HD), lambda i: (0, 0))
    return pl.pallas_call(
        attn_grad_kernel,
        out_shape=jax.ShapeDtypeStruct((width, 3 * HD), BF16),
        grid=(width // GRAD_TILE,),
        in_specs=[tile, whole, whole, tile, whole],
        out_specs=pl.BlockSpec((GRAD_TILE, 3 * HD), lambda i: (i, 0)),
        compiler_params=pltpu.CompilerParams(vmem_limit_bytes=48 << 20),
        cost_estimate=cost(10),
        name="attn_grad",
    )(rows, grad_q, grad_kv, grad_proj, attended)


def attend_back_kernel(q_ref, k_ref, v_ref, start_ref, inv_ref, grad_ref, gq_ref, gk_ref, gv_ref):
    @pl.when(pl.program_id(0) == 0)
    def _():
        gk_ref[...] = jnp.zeros_like(gk_ref)
        gv_ref[...] = jnp.zeros_like(gv_ref)

    first = pl.program_id(0) * QBLK
    keys = pl.ds(pl.multiple_of(first, QBLK), LMAX + QBLK)
    q, k, v, grad = q_ref[...], k_ref[keys], v_ref[keys], grad_ref[...]
    bent, exponent = block_scores(q, k, start_ref[...], first)
    probability = exponent * inv_ref[...]
    grad_prob = lax.dot_general(grad, v, (((1,), (1,)), ((), ())), preferred_element_type=F32)
    inner = jnp.sum(probability * grad_prob, axis=-1, keepdims=True)
    grad_scores = (probability * (grad_prob - inner) * (1.0 - bent * bent)).astype(BF16)
    scale = HD ** (-0.5)
    gq_ref[...] = jnp.dot(grad_scores, k, preferred_element_type=F32) * scale
    over_rows = (((0,), (0,)), ((), ()))
    gk_ref[keys] += lax.dot_general(grad_scores, q, over_rows, preferred_element_type=F32) * scale
    gv_ref[keys] += lax.dot_general(
        probability.astype(BF16), grad, over_rows, preferred_element_type=F32
    )


def attend_back(queries, key_rows, value_rows, starts, inverse, grad):
    rows = queries.shape[0]
    span = key_rows.shape[0]
    row_spec = pl.BlockSpec((QBLK, HD), lambda i: (i, 0))
    one_spec = pl.BlockSpec((QBLK, 1), lambda i: (i, 0))
    all_spec = pl.BlockSpec((span, HD), lambda i: (0, 0))
    return pl.pallas_call(
        attend_back_kernel,
        out_shape=(
            jax.ShapeDtypeStruct((rows, HD), F32),
            jax.ShapeDtypeStruct((span, HD), F32),
            jax.ShapeDtypeStruct((span, HD), F32),
        ),
        grid=(rows // QBLK,),
        in_specs=[row_spec, all_spec, all_spec, one_spec, one_spec, row_spec],
        out_specs=(row_spec, all_spec, all_spec),
        compiler_params=pltpu.CompilerParams(vmem_limit_bytes=48 << 20),
        cost_estimate=cost(20),
        name="attend_back",
    )(queries, key_rows, value_rows, starts, inverse, grad)


def token_tables(seq_lengths, index_vec):
    count = seq_lengths.shape[0]
    order = jnp.arange(count, dtype=jnp.int32)
    seq_ends = jnp.sum(
        jnp.where(order[None, :] <= order[:, None], seq_lengths[None, :], 0), axis=1
    )
    after_end = index_vec[:, None] >= seq_ends[None, :]
    return index_vec - jnp.sum(jnp.where(after_end, seq_lengths[None, :], 0), axis=1)


def rms_parts(value):
    return lax.rsqrt(jnp.mean(value * value, axis=-1, keepdims=True) + EPSILON)


def rms_forward(value, gain_vec):
    return value * rms_parts(value) * (1.0 + gain_vec)


def rms_backward(value, gain_vec, grad):
    r = rms_parts(value)
    scaled = (1.0 + gain_vec) * grad
    inner = jnp.mean(value * scaled, axis=-1, keepdims=True)
    return (r * scaled - value * (r * r * r * inner), jnp.sum(grad * value * r, axis=0))


def rotate(value, cosine, sine_part):
    half_width = value.shape[-1] // 2
    first_half = value[..., :half_width]
    second_half = value[..., half_width:]
    return jnp.concatenate(
        [
            first_half * cosine - second_half * sine_part,
            second_half * cosine + first_half * sine_part,
        ],
        axis=-1,
    )


def contract_last(left_side, right_side):
    return lax.dot_general(
        left_side, right_side, (((1,), (1,)), ((), ())), preferred_element_type=F32
    )


def contract_first(left_side, right_side):
    return lax.dot_general(
        left_side, right_side, (((0,), (0,)), ((), ())), preferred_element_type=F32
    )


def matmul(left_side, right_side):
    return jnp.dot(left_side, right_side, preferred_element_type=F32)


def gelu_parts(gate):
    k0 = 0.7978845608028654
    k1 = 0.044715
    t = jnp.tanh(k0 * (gate + k1 * gate * gate * gate))
    value = 0.5 * gate * (1.0 + t)
    slope = 0.5 * (1.0 + t) + 0.5 * gate * (1.0 - t * t) * k0 * (1.0 + 3.0 * k1 * gate * gate)
    return (value, slope)


def local(tokens, attn_weights, mlp_weights, norm_gains, seq_lengths, cotangent):
    tok_rows, width = tokens.shape
    peers = lax.axis_size(AXIS)
    planes = peers // PLANE
    share = width // peers
    row_share = attn_weights.shape[0]
    ff = mlp_weights.shape[1] // 3
    ffc = ff // PLANE
    plane_rows = PLANE * tok_rows
    halo = LMAX
    across = [[p * PLANE + i for p in range(planes)] for i in range(PLANE)]
    sibling = [(i, i ^ 1) for i in range(peers)]
    to_next = [(i, i + PLANE) for i in range(peers - PLANE)]
    to_prev = [(i + PLANE, i) for i in range(peers - PLANE)]
    me = lax.axis_index(AXIS)
    is_even = (me % 2) == 0
    plane_start = (me // PLANE) * plane_rows

    def split_features(value):
        value = value.reshape(value.shape[0], planes, 2, width // planes // 2)
        return value.transpose(0, 2, 1, 3).reshape(value.shape[0], width)

    def join_features(value):
        value = value.reshape(value.shape[0], 2, planes, width // planes // 2)
        return value.transpose(0, 2, 1, 3).reshape(value.shape[0], width)

    def gather_across(value):
        return lax.all_gather(value, AXIS, axis=0, tiled=True, axis_index_groups=across)

    def scatter_across(value):
        part = lax.psum_scatter(
            value.astype(BF16), AXIS, scatter_dimension=0, tiled=True, axis_index_groups=across
        )
        return part.reshape(PLANE, -1, part.shape[1])

    kv_full, q_rows, out_rows, gain_rows = lax.optimization_barrier(
        (*spread_attn(attn_weights, planes), norm_gains)
    )
    gain_block = jnp.pad(gain_rows.astype(F32), ((0, 8 - 4), (0, -share % 128)))
    gu_part, gain_blocks, kv_full, q_rows, out_rows, near_full = spread_gu(
        mlp_weights, gain_block, kv_full, q_rows, out_rows, peers
    )
    gain_full = gain_blocks[:, :4, :share].transpose(1, 0, 2).reshape(4, width)
    inputs = tokens.astype(F32)
    far_part, normed, kv_full, q_full, near_full = spread_down(
        mlp_weights, rms_forward(inputs, gain_full[0]).astype(BF16), kv_full, q_rows, near_full
    )
    q_cols, kv_cols = q_full.reshape(width, HD), kv_full.reshape(width, HD)
    gu_cols = gather_across(gu_part.reshape(-1, 2 * ffc))
    down_far = gather_across(far_part.reshape(-1, ffc))

    query_index = plane_start + jnp.arange(plane_rows, dtype=jnp.int32)
    position = token_tables(seq_lengths, query_index)
    starts = (jnp.arange(plane_rows, dtype=jnp.int32) + halo - position)[:, None]
    frequency = 10000.0 ** (-jnp.arange(HD // 2, dtype=F32) * 2.0 / HD)
    angles = position.astype(F32)[:, None] * frequency[None, :]
    cosine, sine_part = jnp.cos(angles), jnp.sin(angles)
    kv_cosine = jnp.where(is_even, cosine, 1.0)
    kv_sine = jnp.where(is_even, sine_part, 0.0)

    kv_own = rotate(matmul(normed, kv_cols), kv_cosine, kv_sine).astype(BF16)
    kv_halo = lax.ppermute(kv_own[plane_rows - halo :], AXIS, to_next)
    kv_own, out_rows, q_cols = lax.optimization_barrier((kv_own, out_rows, q_cols))
    out_cols = spread_out(out_rows).reshape(width, HD)
    queries = rotate(matmul(normed, q_cols), cosine, sine_part).astype(BF16)
    kv_halo, out_cols, queries = lax.optimization_barrier((kv_halo, out_cols, queries))
    kv_mine = jnp.concatenate([kv_halo, kv_own], axis=0)
    kv_other = lax.ppermute(kv_mine, AXIS, sibling)
    key_rows = jnp.where(is_even, kv_mine, kv_other)
    value_rows = jnp.where(is_even, kv_other, kv_mine)
    attended, inverse = attend(queries, key_rows, value_rows, starts)
    attn_proj, near_full = product_scatter_line(attended, out_cols, near_full, PLANE_STEP, 2)
    down_near = near_full.reshape(width // 2, ffc)

    middle = inputs + rms_forward(attn_proj, gain_full[1])
    mid_low = gather_square(rms_forward(middle, gain_full[2]).astype(BF16), PLANE_STEP, 1)
    gate_up = matmul(mid_low, gu_cols)
    gate, up = gate_up[:, :ffc], gate_up[:, ffc:]
    gelu, slope = gelu_parts(gate)
    hidden = (gelu * up).astype(BF16)
    hidden, gain_split, grad_split = lax.optimization_barrier(
        (hidden, split_features(gain_full[3:4]), split_features(cotangent))
    )
    raw_near = product_scatter([hidden], [down_near], [0], PLANE_STEP, 14)
    raw_far, grad_raw_low, down_grad = turn(
        hidden, down_far, raw_near, gain_split, grad_split, planes, PLANE_STEP, 9
    )
    mlp_raw = join_features(jnp.concatenate([raw_near, raw_far], axis=1))
    if not in_place(width // planes // 2):
        down_grad = join_features(down_grad.T).T
    layer_output = (middle + rms_forward(mlp_raw, gain_full[3])).astype(BF16)

    grad_out = cotangent.astype(F32)
    gain_four = jnp.sum(grad_out * mlp_raw * rms_parts(mlp_raw), axis=0)
    down_term = scatter_across(down_grad)
    grad_hidden = matmul(grad_raw_low, jnp.concatenate([down_near, down_far], axis=0))
    grad_normed_mid, gu_grad = product_scatter_back(
        [(slope * up * grad_hidden).astype(BF16), (gelu * grad_hidden).astype(BF16)],
        [gu_cols, gu_cols],
        [0, ffc],
        mid_low,
        PLANE_STEP,
        10,
    )
    gu_term = scatter_across(gu_grad)
    grad_mid_part, gain_three = rms_backward(middle, gain_full[2], grad_normed_mid)
    grad_middle = grad_out + grad_mid_part

    grad_proj, gain_two = rms_backward(attn_proj, gain_full[1], grad_middle)
    grad_proj_own, down_term = lax.optimization_barrier((grad_proj.astype(BF16), down_term))
    grad_proj_low = gather_square(grad_proj_own, PLANE_STEP, 1)
    grad_att = matmul(grad_proj_low, out_cols).astype(BF16)
    grad_query, grad_keys, grad_values = attend_back(
        queries, key_rows, value_rows, starts, inverse, grad_att
    )
    grad_mine = jnp.where(is_even, grad_keys, grad_values)
    grad_give = jnp.where(is_even, grad_values, grad_keys).astype(BF16)
    grad_kv = grad_mine + lax.ppermute(grad_give, AXIS, sibling).astype(F32)
    grad_back = lax.ppermute(grad_kv[:halo].astype(BF16), AXIS, to_prev).astype(F32)
    down_term, grad_kv = lax.optimization_barrier((down_term, grad_kv))
    down_rows = collect(down_term, 1, 6)
    down_rows, grad_back = lax.optimization_barrier((down_rows, grad_back))
    grad_kv = grad_kv[halo:] + jnp.pad(grad_back, ((plane_rows - halo, 0), (0, 0)))
    grad_q = rotate(grad_query, cosine, -sine_part).astype(BF16)
    grad_kv = rotate(grad_kv, kv_cosine, -kv_sine).astype(BF16)
    attn_term, grad_q, grad_kv = lax.optimization_barrier(
        (attn_grad(normed, grad_q, grad_kv, grad_proj_low, attended), grad_q, grad_kv)
    )
    attn_term = scatter_across(attn_term)
    grad_normed = product_scatter([grad_q, grad_kv], [q_cols, kv_cols], [0, 0], PLANE_STEP, 12)
    grad_in_part, gain_one = rms_backward(inputs, gain_full[0], grad_normed)
    grad_tokens = (grad_middle + grad_in_part).astype(BF16)

    gain_term = jnp.stack([gain_one, gain_two, gain_three, gain_four], axis=0)
    gain_term = gain_term.reshape(4, peers, share).transpose(1, 0, 2)
    gain_term = jnp.pad(gain_term, ((0, 0), (0, 8 - 4), (0, -share % 128)))
    gain_recv = collect_gains(gain_term)
    gu_term, gain_recv = lax.optimization_barrier((gu_term, gain_recv))
    gu_rows = collect(gu_term, 2, 13)
    grad_mlp = jnp.concatenate([gu_rows, down_rows], axis=1).astype(F32)
    grad_mlp, attn_term = lax.optimization_barrier((grad_mlp, attn_term))
    grad_attn = collect_attn(attn_term).astype(F32)
    grad_gains = jnp.sum(gain_recv[:, :4, :share], axis=0)
    return (layer_output, grad_tokens, grad_attn, grad_mlp, grad_gains)


def solution(mesh):
    return jax.shard_map(
        local,
        mesh=mesh,
        in_specs=(
            P("fsdp", None),
            P("fsdp", None),
            P("fsdp", None),
            P(None, "fsdp"),
            P(),
            P("fsdp", None),
        ),
        out_specs=(
            P("fsdp", None),
            P("fsdp", None),
            P("fsdp", None),
            P("fsdp", None),
            P(None, "fsdp"),
        ),
        check_vma=False,
    )
```

```python
from functools import partial

import jax
import jax.numpy as jnp
from jax import lax
from jax.experimental import pallas as pl
from jax.experimental.pallas import tpu as pltpu
from jax.sharding import PartitionSpec as P

H = 8
KVH = 4
HD = 256
LMAX = 1024
PLANE = 8
QBLK = 128

EPSILON = 1e-06
SOFT_CAP = 50.0
AXIS = "fsdp"
F32 = jnp.float32
BF16 = jnp.bfloat16
MESH = pl.DeviceIdType.MESH
ANY = pl.BlockSpec(memory_space=pl.ANY)
VMEM = pl.BlockSpec(memory_space=pltpu.VMEM)
DMA = pltpu.SemaphoreType.DMA


def flip(index, step):
    return index + step - 2 * step * ((index // step) % 2)


PLANE_STEP = 4


def partner(index, bits, step):
    for bit, by in ((1, 1), (2, 2), (4, step)):
        if bits & bit:
            index = flip(index, by)
    return index


def place(device, step):
    return device % 4 + 4 * ((device // step) % 2)


def greet(peers):
    barrier = pltpu.get_barrier_semaphore()
    for peer in peers:
        pl.semaphore_signal(barrier, inc=1, device_id=(peer,), device_id_type=MESH)
    pl.semaphore_wait(barrier, len(peers))


class Copies:
    def __init__(self, send_sem, recv_sem):
        self.send_sem, self.recv_sem, self.made = send_sem, recv_sem, []

    def start(self, source, target, device):
        slot = len(self.made)
        copy = pltpu.make_async_remote_copy(
            src_ref=source,
            dst_ref=target,
            send_sem=self.send_sem.at[slot],
            recv_sem=self.recv_sem.at[slot],
            device_id=(device,),
            device_id_type=MESH,
        )
        copy.start()
        self.made.append(copy)
        return copy

    def sent(self):
        for copy in self.made:
            copy.wait_send()


def band(index, size):
    return pl.ds(pl.multiple_of(index * size, 8), size)


def lanes(index, size):
    return pl.ds(pl.multiple_of(index * size, 128), size)


def gather_steps(block_ref, full_ref, copies, own_sem, step):
    rows, width = block_ref.shape
    half = width // 2
    me = lax.axis_index(AXIS)
    sib, xn, yn = flip(me, 1), flip(me, 2), flip(me, step)
    diag = flip(xn, step)

    def at(device, side):
        return full_ref.at[band(place(device, step), rows), pl.ds(side * half, half)]

    def mine(side):
        return block_ref.at[:, pl.ds(side * half, half)]

    own_rows = full_ref.at[band(place(me, step), rows)]
    xa = copies.start(mine(0), at(me, 0), xn)
    ya = copies.start(mine(1), at(me, 1), yn)
    xb = copies.start(mine(1), at(me, 1), xn)
    yb = copies.start(mine(0), at(me, 0), yn)
    arriving = [copies.start(block_ref, own_rows, sib)]
    own = pltpu.make_async_copy(block_ref, own_rows, own_sem)
    own.start()

    def finish(on_rows=None):
        def to_sibling(device, side):
            arriving.append(copies.start(at(device, side), at(device, side), sib))

        def arrived(first, last, *devices):
            for copy in arriving[first:last]:
                copy.wait_recv()
            for device in devices:
                on_rows(device)

        if on_rows is not None:
            own.wait()
            arrived(0, 1, me)
        xa.wait_recv()
        yc = copies.start(at(xn, 0), at(xn, 0), yn)
        to_sibling(xn, 0)
        ya.wait_recv()
        xc = copies.start(at(yn, 1), at(yn, 1), xn)
        to_sibling(yn, 1)
        xb.wait_recv()
        to_sibling(xn, 1)
        yb.wait_recv()
        to_sibling(yn, 0)
        if on_rows is not None:
            arrived(1, 5, xn, yn)
        yc.wait_recv()
        to_sibling(diag, 0)
        xc.wait_recv()
        to_sibling(diag, 1)
        if on_rows is not None:
            arrived(5, 7, diag)
        else:
            arrived(0, 7)
            own.wait()

    return finish


GATHER_COPIES = 13


def cost(microseconds):
    return pl.CostEstimate(
        flops=int(microseconds * 1e7), transcendentals=0, bytes_accessed=int(microseconds * 3e4)
    )


def gather_kernel(block_ref, full_ref, own_sem, send_sem, recv_sem, *, step):
    me = lax.axis_index(AXIS)
    greet((flip(me, 1), flip(me, 2), flip(me, step)))
    copies = Copies(send_sem, recv_sem)
    gather_steps(block_ref, full_ref, copies, own_sem, step)()
    copies.sent()


def gather_square(block, step, collective_id):
    rows, width = block.shape
    return pl.pallas_call(
        partial(gather_kernel, step=step),
        out_shape=jax.ShapeDtypeStruct((PLANE * rows, width), block.dtype),
        in_specs=[ANY],
        out_specs=ANY,
        scratch_shapes=[DMA(()), DMA((GATHER_COPIES,)), DMA((GATHER_COPIES,))],
        compiler_params=pltpu.CompilerParams(collective_id=collective_id, has_side_effects=True),
        cost_estimate=cost(42),
        name="gather_square",
    )(block)


W_TILES = 2
SCATTER_COPIES = 14


def split_columns(width):
    left = (width // 2 + 127) // 128 * 128
    return pl.ds(0, left), pl.ds(left, width - left)


def product_scatter_steps(
    left_refs, right_refs, left_bufs, right_bufs, buffers, load_sem, copies, offsets, step, beside=None
):
    both, got, ra, rb, ra2, rb2 = buffers
    pairs = len(left_refs)
    rows, width = got.shape[1:]
    sides = split_columns(width)
    chunk = 48
    me = lax.axis_index(AXIS)
    core = me % 2
    sib, xn, yn = flip(me, 1), flip(me, 2), flip(me, step)
    order = (flip(xn, step), xn, yn, me)
    first, second = sides

    def chip_rows(device):
        return pl.ds(pl.multiple_of((place(device, step) // 2) * 2 * rows, 16), 2 * rows)

    def right_load(j, t):
        r = sides[t]
        source = right_refs[j].at[r, pl.ds(offsets[j], right_bufs[j].shape[1])]
        return pltpu.make_async_copy(source, right_bufs[j].at[r], load_sem.at[j, t])

    def left_load(j, i):
        r = chip_rows(order[i])
        return pltpu.make_async_copy(
            left_refs[j].at[r], left_bufs[j].at[r], load_sem.at[j, W_TILES + i]
        )

    for j in range(pairs):
        left_load(j, 0).start()
    for t in range(W_TILES):
        for j in range(pairs):
            right_load(j, t).start()
    for i in range(1, 4):
        for j in range(pairs):
            left_load(j, i).start()
    if beside is not None:
        beside[0]()
    greet((sib, xn, yn))

    def mine(i, cols):
        return both.at[i, band(core, rows), cols]

    def add(total, other):
        @pl.loop(0, rows // chunk)
        def _(k):
            r = pl.ds(pl.multiple_of(k * chunk, chunk), chunk)
            total[r] = (total[r].astype(F32) + other[r].astype(F32)).astype(total.dtype)

    loaded = set()

    def make(i, side):
        for j in range(pairs):
            if i not in loaded:
                left_load(j, i).wait()
            if i == 0:
                right_load(j, side).wait()
        loaded.add(i)
        r, cols = chip_rows(order[i]), sides[side]
        total = None
        for j in range(pairs):
            term = contract_last(left_bufs[j][r], right_bufs[j][cols])
            total = term if total is None else total + term
        both[i, :, cols] = total.astype(BF16)
        return copies.start(both.at[i, band(1 - core, rows), cols], got.at[i, :, cols], sib)

    def merge(crossing, i, side):
        cols = sides[side]
        crossing.wait_recv()
        add(mine(i, cols), got.at[i, :, cols])

    c0 = make(0, 0)
    c1 = make(0, 1)
    merge(c0, 0, 0)
    x0 = copies.start(mine(0, first), ra.at[0], xn)
    c2 = make(1, 0)
    merge(c1, 0, 1)
    y0 = copies.start(mine(0, second), rb.at[0], yn)
    c3 = make(2, 1)
    merge(c2, 1, 0)
    x1 = copies.start(mine(1, first), ra.at[1], xn)
    c4 = make(2, 0)
    merge(c3, 2, 1)
    y1 = copies.start(mine(2, second), rb.at[1], yn)
    c5 = make(1, 1)
    merge(c4, 2, 0)
    x0.wait_recv()
    add(mine(2, first), ra.at[0])
    y2 = copies.start(mine(2, first), ra2, yn)
    c6 = make(3, 0)
    merge(c5, 1, 1)
    y0.wait_recv()
    add(mine(1, second), rb.at[0])
    x2 = copies.start(mine(1, second), rb2, xn)
    c7 = make(3, 1)
    merge(c6, 3, 0)
    merge(c7, 3, 1)
    if beside is not None:
        beside[1]()
    for copy in (x1, y1, y2, x2):
        copy.wait_recv()
    own = both.at[3, band(core, rows)]

    def summed(r):
        return jnp.concatenate(
            [
                own[r, first].astype(F32) + ra[1, r].astype(F32) + ra2[r].astype(F32),
                own[r, second].astype(F32) + rb[1, r].astype(F32) + rb2[r].astype(F32),
            ],
            axis=1,
        )

    return summed


ROW_CHUNK = 48


def product_scatter_kernel(*refs, pairs, offsets, step):
    left_refs, right_refs, out_ref = refs[:pairs], refs[pairs : 2 * pairs], refs[2 * pairs]
    left_bufs = refs[2 * pairs + 1 : 3 * pairs + 1]
    right_bufs = refs[3 * pairs + 1 : 4 * pairs + 1]
    buffers, (load_sem, send_sem, recv_sem) = refs[4 * pairs + 1 : -3], refs[-3:]
    copies = Copies(send_sem, recv_sem)
    summed = product_scatter_steps(
        left_refs, right_refs, left_bufs, right_bufs, buffers, load_sem, copies, offsets, step
    )

    @pl.loop(0, out_ref.shape[0] // ROW_CHUNK)
    def _(k):
        r = pl.ds(pl.multiple_of(k * ROW_CHUNK, ROW_CHUNK), ROW_CHUNK)
        out_ref[r] = summed(r)

    copies.sent()


def scatter_buffers(rows, width):
    left, right = [side.size for side in split_columns(width)]
    return [
        pltpu.VMEM((4, 2 * rows, width), BF16),
        pltpu.VMEM((4, rows, width), BF16),
        pltpu.VMEM((2, rows, left), BF16),
        pltpu.VMEM((2, rows, right), BF16),
        pltpu.VMEM((rows, left), BF16),
        pltpu.VMEM((rows, right), BF16),
    ]


def product_scatter(lefts, rights, offsets, step, collective_id):
    pairs = len(lefts)
    rows, width = lefts[0].shape[0] // PLANE, rights[0].shape[0]
    return pl.pallas_call(
        partial(product_scatter_kernel, pairs=pairs, offsets=offsets, step=step),
        out_shape=jax.ShapeDtypeStruct((rows, width), F32),
        in_specs=[ANY] * (2 * pairs),
        out_specs=VMEM,
        scratch_shapes=[
            *[pltpu.VMEM(value.shape, BF16) for value in lefts],
            *[pltpu.VMEM((width, value.shape[1]), BF16) for value in lefts],
            *scatter_buffers(rows, width),
            DMA((pairs, W_TILES + 4)),
            DMA((SCATTER_COPIES,)),
            DMA((SCATTER_COPIES,)),
        ],
        compiler_params=pltpu.CompilerParams(
            collective_id=collective_id, has_side_effects=True, vmem_limit_bytes=56 << 20
        ),
        cost_estimate=cost(50),
        name="product_scatter",
    )(*lefts, *rights)


BACK_TILE = 384


def back_kernel(*refs, pairs, offsets, step):
    left_refs, right_refs, rows_ref = refs[:pairs], refs[pairs : 2 * pairs], refs[2 * pairs]
    out_ref, term_ref = refs[2 * pairs + 1 : 2 * pairs + 3]
    scratch = refs[2 * pairs + 3 :]
    left_bufs, right_bufs = scratch[:pairs], scratch[pairs : 2 * pairs]
    rows_buf, stage = scratch[2 * pairs : 2 * pairs + 2]
    buffers = scratch[2 * pairs + 2 : -5]
    load_sem, rows_sem, store_sem, send_sem, recv_sem = scratch[-5:]
    copies = Copies(send_sem, recv_sem)
    rows_load = pltpu.make_async_copy(rows_ref, rows_buf, rows_sem)
    tiles = rows_ref.shape[1] // BACK_TILE
    width = left_refs[0].shape[1]

    def store(t):
        return pltpu.make_async_copy(
            stage.at[t % 2],
            term_ref.at[pl.ds(pl.multiple_of(t * BACK_TILE, 16), BACK_TILE)],
            store_sem.at[t % 2],
        )

    def beside():
        rows_load.wait()

        @pl.loop(0, tiles)
        def _(t):
            @pl.when(t >= 2)
            def _():
                store(t - 2).wait()

            columns = rows_buf[:, pl.ds(pl.multiple_of(t * BACK_TILE, BACK_TILE), BACK_TILE)]
            for j in range(pairs):
                term = contract_first(columns, left_bufs[j][...])
                stage[t % 2, :, pl.ds(j * width, width)] = term.astype(BF16)
            store(t).start()

    def start_rows():
        rows_load.start()

    summed = product_scatter_steps(
        left_refs,
        right_refs,
        left_bufs,
        right_bufs,
        buffers,
        load_sem,
        copies,
        offsets,
        step,
        (start_rows, beside),
    )

    @pl.loop(0, out_ref.shape[0] // ROW_CHUNK)
    def _(k):
        r = pl.ds(pl.multiple_of(k * ROW_CHUNK, ROW_CHUNK), ROW_CHUNK)
        out_ref[r] = summed(r)

    for t in range(tiles - 2, tiles):
        store(t).wait()
    copies.sent()


def product_scatter_back(lefts, rights, offsets, rows, step, collective_id):
    pairs = len(lefts)
    count, width = lefts[0].shape[0] // PLANE, rights[0].shape[0]
    columns = sum(value.shape[1] for value in lefts)
    return pl.pallas_call(
        partial(back_kernel, pairs=pairs, offsets=offsets, step=step),
        out_shape=(
            jax.ShapeDtypeStruct((count, width), F32),
            jax.ShapeDtypeStruct((rows.shape[1], columns), BF16),
        ),
        in_specs=[ANY] * (2 * pairs + 1),
        out_specs=(VMEM, ANY),
        scratch_shapes=[
            *[pltpu.VMEM(value.shape, BF16) for value in lefts],
            *[pltpu.VMEM((width, value.shape[1]), BF16) for value in lefts],
            pltpu.VMEM(rows.shape, BF16),
            pltpu.VMEM((2, BACK_TILE, columns), BF16),
            *scatter_buffers(count, width),
            DMA((pairs, W_TILES + 4)),
            DMA(()),
            DMA((2,)),
            DMA((SCATTER_COPIES,)),
            DMA((SCATTER_COPIES,)),
        ],
        compiler_params=pltpu.CompilerParams(
            collective_id=collective_id, has_side_effects=True, vmem_limit_bytes=62 << 20
        ),
        cost_estimate=cost(60),
        name="product_scatter_back",
    )(*lefts, *rights, rows)


TURN_TILE = 768


def in_place(rows):
    return rows % 16 == 0


def turn_kernel(
    left_ref,
    right_ref,
    near_ref,
    gain_ref,
    grad_ref,
    raw_ref,
    full_ref,
    term_ref,
    *refs,
    planes,
    step,
):
    left_buf, right_buf, gathered, total, grad_own, stage = refs[:6]
    buffers, (load_sem, own_sem, store_sem, send_sem, recv_sem) = refs[6:-5], refs[-5:]
    rows, width = grad_ref.shape
    half = width // 2
    piece = half // planes
    copies = Copies(send_sem, recv_sem)
    summed = product_scatter_steps(
        [left_ref], [right_ref], [left_buf], [right_buf], buffers, load_sem, copies, [0], step
    )
    gain = gain_ref[...]

    @pl.loop(0, rows // ROW_CHUNK)
    def _(k):
        r = pl.ds(pl.multiple_of(k * ROW_CHUNK, ROW_CHUNK), ROW_CHUNK)
        far = summed(r)
        raw_ref[r] = far
        value = jnp.concatenate([near_ref[r], far], axis=1)
        scale = lax.rsqrt(jnp.mean(value * value, axis=1, keepdims=True) + EPSILON)
        scaled = (1.0 + gain) * grad_ref[r].astype(F32)
        inner = jnp.mean(value * scaled, axis=1, keepdims=True)
        grad_own[r] = (scale * scaled - value * (scale * scale * scale * inner)).astype(BF16)

    stores = []

    def store_term(side):
        for plane in range(planes):
            start = side * half + plane * piece
            target = plane * 2 * piece + side * piece if in_place(piece) else start
            pltpu.make_async_copy(
                stage.at[pl.ds(start, piece)] if in_place(piece) else stage.at[pl.ds(side * half, half)],
                term_ref.at[pl.ds(target, piece)]
                if in_place(piece)
                else term_ref.at[pl.ds(side * half, half)],
                store_sem.at[4],
            ).start()
            if not in_place(piece):
                break

    def on_rows(device):
        slot = len(stores)
        r = pl.ds(pl.multiple_of((place(device, step) // 2) * 2 * rows, 16), 2 * rows)
        store = pltpu.make_async_copy(gathered.at[r], full_ref.at[r], store_sem.at[slot])
        store.start()
        stores.append(store)
        right = left_buf[r]
        if slot < 3:

            @pl.loop(0, width // TURN_TILE)
            def _(t):
                w = pl.ds(pl.multiple_of(t * TURN_TILE, TURN_TILE), TURN_TILE)
                term = contract_first(gathered[r, w], right)
                if slot == 0:
                    total[w] = term
                else:
                    total[w] += term
        else:
            for side in range(2):

                @pl.loop(0, 3)
                def _(t):
                    w = pl.ds(
                        pl.multiple_of(side * half + t * (half // 3), half // 3), half // 3
                    )
                    term = contract_first(gathered[r, w], right)
                    stage[w] = (total[w] + term).astype(BF16)

                store_term(side)

    gather_steps(grad_own, gathered, copies, own_sem, step)(on_rows)
    pltpu.make_async_copy(stage, term_ref, store_sem.at[4]).wait()
    for store in stores:
        store.wait()
    copies.sent()


def turn(left, right, near, gain_row, grad, planes, step, collective_id):
    rows, width = grad.shape
    count = SCATTER_COPIES + GATHER_COPIES
    return pl.pallas_call(
        partial(turn_kernel, planes=planes, step=step),
        out_shape=(
            jax.ShapeDtypeStruct((rows, width // 2), F32),
            jax.ShapeDtypeStruct((PLANE * rows, width), BF16),
            jax.ShapeDtypeStruct((width, left.shape[1]), BF16),
        ),
        in_specs=[ANY, ANY, VMEM, VMEM, VMEM],
        out_specs=(VMEM, ANY, ANY),
        scratch_shapes=[
            pltpu.VMEM(left.shape, BF16),
            pltpu.VMEM(right.shape, BF16),
            pltpu.VMEM((PLANE * rows, width), BF16),
            pltpu.VMEM((width, left.shape[1]), F32),
            pltpu.VMEM((rows, width), BF16),
            pltpu.VMEM((width, left.shape[1]), BF16),
            *scatter_buffers(rows, width // 2),
            DMA((1, W_TILES + 4)),
            DMA(()),
            DMA((5,)),
            DMA((count,)),
            DMA((count,)),
        ],
        compiler_params=pltpu.CompilerParams(
            collective_id=collective_id, has_side_effects=True, vmem_limit_bytes=60 << 20
        ),
        cost_estimate=cost(50),
        name="turn",
    )(left, right, near, gain_row, grad)


def attn_columns(column):
    query_width = H * HD
    key_offset = query_width + (column % 2) * KVH * HD + (column // 2) * HD
    return (column * HD, key_offset, query_width + 2 * KVH * HD + column * HD)


def greet_all(peers):
    me = lax.axis_index(AXIS)
    barrier = pltpu.get_barrier_semaphore()

    @pl.loop(1, peers)
    def _(k):
        device = lax.rem(me + k, peers)
        pl.semaphore_signal(barrier, inc=1, device_id=(device,), device_id_type=MESH)

    pl.semaphore_wait(barrier, peers - 1)


def exchange_all(source_of, target_ref, send_sem, recv_sem):
    peers = target_ref.shape[0]
    me = lax.axis_index(AXIS)

    def copy(k):
        device = lax.rem(me + k, peers)
        return pltpu.make_async_remote_copy(
            src_ref=source_of(device),
            dst_ref=target_ref.at[me],
            send_sem=send_sem.at[k],
            recv_sem=recv_sem.at[k],
            device_id=(device,),
            device_id_type=MESH,
        )

    @pl.loop(1, peers)
    def _(k):
        copy(k).start()

    def finish():
        @pl.loop(1, peers)
        def _(k):
            copy(k).wait()

    return finish


ORDER = (6, 7, 2, 3, 4, 5, 1)


def swap_steps(pieces_of, targets, copies, own_sem, step):
    me = lax.axis_index(AXIS)
    moved = []
    for bits in ORDER:
        peer = partner(me, bits, step)
        for source, target in zip(pieces_of(place(peer, step)), targets):
            moved.append(copies.start(source, target, peer))
    owns = []
    for slot, (source, target) in enumerate(zip(pieces_of(place(me, step)), targets)):
        own = pltpu.make_async_copy(source, target, own_sem.at[slot])
        own.start()
        owns.append(own)

    def finish():
        for own in owns:
            own.wait()
        for copy in moved:
            copy.wait_recv()

    return finish


def square(step):
    me = lax.axis_index(AXIS)
    return [partner(me, bits, step) for bits in ORDER]


def wide(offset):
    return pl.ds(pl.multiple_of(offset, 128), HD)


class Line:
    def __init__(self, full_ref, send_sem, recv_sem, own_ref=None):
        me = lax.axis_index(AXIS)
        self.own = own_ref
        self.full, self.planes = full_ref, full_ref.shape[0]
        self.send_sem, self.recv_sem = send_sem, recv_sem
        self.plane = me // PLANE
        peers = self.planes * PLANE
        self.devices = (lax.rem(me + PLANE, peers), lax.rem(me + peers - PLANE, peers))

    def copy(self, way, slot, source, first=False):
        return pltpu.make_async_remote_copy(
            src_ref=self.own if first and self.own is not None else self.full.at[source],
            dst_ref=self.full.at[source],
            send_sem=self.send_sem.at[way, slot],
            recv_sem=self.recv_sem.at[way, slot],
            device_id=(self.devices[way],),
            device_id_type=MESH,
        )

    def sends(self, way, hop):
        if way == 0:
            source = self.plane - (hop - 1)
            return (self.plane + 1 < self.planes) & (source >= 0), source
        source = self.plane + (hop - 1)
        return (self.plane >= 1) & (source < self.planes), source

    def greet(self):
        barrier = pltpu.get_barrier_semaphore()
        count = 0
        for way, there in enumerate((self.plane + 1 < self.planes, self.plane >= 1)):

            @pl.when(there)
            def _():
                pl.semaphore_signal(
                    barrier, inc=1, device_id=(self.devices[way],), device_id_type=MESH
                )

            count = count + there.astype(jnp.int32)
        return count

    def start(self, hop, slot):
        for way in range(2):
            there, source = self.sends(way, hop)

            @pl.when(there)
            def _():
                self.copy(way, slot, source, hop == 1).start()

    def arrived(self, hop, slot):
        for way in range(2):
            source = self.plane - hop if way == 0 else self.plane + hop

            @pl.when((source >= 0) & (source < self.planes))
            def _():
                self.copy(way, slot, source).wait_recv()

    def sent(self, hop, slot):
        for way in range(2):
            there, source = self.sends(way, hop)

            @pl.when(there)
            def _():
                self.copy(way, slot, source, hop == 1).wait_send()

    def begin(self, hops):
        if hops:
            self.start(hops[0], 0)

    def run(self, hops):
        for slot, hop in enumerate(hops):
            self.arrived(hop, slot)
            if slot + 1 < len(hops):
                self.start(hop + 1, slot + 1)

    def end(self, hops):
        for slot, hop in enumerate(hops):
            self.sent(hop, slot)


def line_hops(planes):
    hops = list(range(1, planes))
    first = (2 * len(hops) + 2) // 3
    return hops[:first], hops[first:]


def line_semaphores(hops):
    count = max(1, len(hops))
    return [DMA((2, count)), DMA((2, count))]


def greet_line(line, peers):
    barrier = pltpu.get_barrier_semaphore()
    for peer in peers:
        pl.semaphore_signal(barrier, inc=1, device_id=(peer,), device_id_type=MESH)
    pl.semaphore_wait(barrier, len(peers) + line.greet())


def row_bands(weights_ref):
    return [weights_ref.at[:, pl.ds(start * HD, H * HD)] for start in (0, H + 2 * KVH)]


def spread_attn_kernel(weights_ref, kv_ref, q_ref, out_ref, own_sem, send_sem, recv_sem, *sems):
    me = lax.axis_index(AXIS)
    plane, here = me // PLANE, place(me, PLANE_STEP)
    q_rows, out_rows = row_bands(weights_ref)
    q_line = Line(q_ref, sems[0], sems[1], q_rows)
    out_line = Line(out_ref, sems[2], sems[3], out_rows)
    hops = line_hops(out_line.planes)[0]
    greet_line(out_line, square(PLANE_STEP))
    out_line.begin(hops)
    q_line.begin([1])
    owns = []
    for slot, (source, target) in enumerate(((q_rows, q_ref), (out_rows, out_ref))):
        own = pltpu.make_async_copy(source, target.at[plane], own_sem.at[1 + slot])
        own.start()
        owns.append(own)
    copies = Copies(send_sem, recv_sem)
    spread = swap_steps(
        lambda c: [weights_ref.at[:, wide(attn_columns(c)[1])]],
        [kv_ref.at[plane, here]],
        copies,
        own_sem,
        PLANE_STEP,
    )
    out_line.run(hops)
    q_line.run([1])
    spread()
    for own in owns:
        own.wait()
    out_line.end(hops)
    q_line.end([1])
    copies.sent()


def spread_attn(weights, planes):
    rows = weights.shape[0]
    return pl.pallas_call(
        spread_attn_kernel,
        out_shape=(
            jax.ShapeDtypeStruct((planes, PLANE, rows, HD), BF16),
            jax.ShapeDtypeStruct((planes, rows, H * HD), BF16),
            jax.ShapeDtypeStruct((planes, rows, H * HD), BF16),
        ),
        in_specs=[ANY],
        out_specs=(ANY, ANY, ANY),
        scratch_shapes=[
            DMA((3,)),
            DMA((7,)),
            DMA((7,)),
            *line_semaphores([1]),
            *line_semaphores(line_hops(planes)[0]),
        ],
        compiler_params=pltpu.CompilerParams(collective_id=3, has_side_effects=True),
        name="spread_attn",
    )(weights)


def spread_gu_kernel(
    weights_ref,
    gain_ref,
    kv_in,
    q_in,
    out_in,
    gu_ref,
    gains_ref,
    kv_ref,
    q_ref,
    out_ref,
    own_sem,
    send_sem,
    recv_sem,
    gain_send,
    gain_recv,
    *sems,
):
    peers = gains_ref.shape[0]
    ffc = gu_ref.shape[2] // 2
    me = lax.axis_index(AXIS)
    here = place(me, PLANE_STEP)
    kv_line = Line(kv_ref, sems[0], sems[1])
    q_line = Line(q_ref, sems[2], sems[3])
    out_line = Line(out_ref, sems[4], sems[5])
    kv_hops, out_hops = line_hops(kv_line.planes)
    q_hops = list(range(2, kv_line.planes))
    greet_all(peers)
    q_line.begin(q_hops)
    out_line.begin(out_hops)
    kv_line.begin(kv_hops)
    gains_done = exchange_all(lambda device: gain_ref, gains_ref, gain_send, gain_recv)
    own = pltpu.make_async_copy(gain_ref, gains_ref.at[me], own_sem.at[2])
    own.start()
    copies = Copies(send_sem, recv_sem)
    spread = swap_steps(
        lambda c: [weights_ref.at[:, lanes(slot * PLANE + c, ffc)] for slot in range(2)],
        [gu_ref.at[here, :, pl.ds(slot * ffc, ffc)] for slot in range(2)],
        copies,
        own_sem,
        PLANE_STEP,
    )
    q_line.run(q_hops)
    out_line.run(out_hops)
    kv_line.run(kv_hops)
    spread()
    own.wait()
    gains_done()
    for line, hops in ((q_line, q_hops), (out_line, out_hops), (kv_line, kv_hops)):
        line.end(hops)
    copies.sent()


def spread_gu(weights, gain_block, kv_full, q_rows, out_rows, peers):
    rows = weights.shape[0]
    ffc = weights.shape[1] // 3 // PLANE
    planes = kv_full.shape[0]
    kv_hops, out_hops = line_hops(planes)
    return pl.pallas_call(
        spread_gu_kernel,
        out_shape=(
            jax.ShapeDtypeStruct((PLANE, rows, 2 * ffc), BF16),
            jax.ShapeDtypeStruct((peers,) + gain_block.shape, gain_block.dtype),
            jax.ShapeDtypeStruct(kv_full.shape, kv_full.dtype),
            jax.ShapeDtypeStruct(q_rows.shape, q_rows.dtype),
            jax.ShapeDtypeStruct(out_rows.shape, out_rows.dtype),
        ),
        in_specs=[ANY] * 5,
        out_specs=(ANY,) * 5,
        scratch_shapes=[
            DMA((3,)),
            DMA((14,)),
            DMA((14,)),
            DMA((peers,)),
            DMA((peers,)),
            *line_semaphores(kv_hops),
            *line_semaphores(range(2, planes)),
            *line_semaphores(out_hops),
        ],
        input_output_aliases={2: 2, 3: 3, 4: 4},
        compiler_params=pltpu.CompilerParams(collective_id=4, has_side_effects=True),
        cost_estimate=cost(38),
        name="spread_gu",
    )(weights, gain_block, kv_full, q_rows, out_rows)


def spread_down_kernel(
    weights_ref,
    block_ref,
    kv_in,
    rows_ref,
    down_ref,
    full_ref,
    kv_ref,
    q_ref,
    own_sem,
    send_sem,
    recv_sem,
    line_send,
    line_recv,
):
    ffc = down_ref.shape[2]
    here = place(lax.axis_index(AXIS), PLANE_STEP)
    line = Line(kv_ref, line_send, line_recv)
    hops = line_hops(line.planes)[1]
    greet_line(line, square(PLANE_STEP))
    line.begin(hops)
    copies = Copies(send_sem, recv_sem)
    gathered = gather_steps(block_ref, full_ref, copies, own_sem.at[2], PLANE_STEP)
    spread = swap_steps(
        lambda c: [
            rows_ref.at[:, :, lanes(c, HD)],
            weights_ref.at[:, lanes(2 * PLANE + c, ffc)],
        ],
        [q_ref.at[:, here], down_ref.at[here]],
        copies,
        own_sem,
        PLANE_STEP,
    )
    gathered()
    line.run(hops)
    spread()
    line.end(hops)
    copies.sent()


def spread_down(weights, block, kv_full, q_rows):
    rows = weights.shape[0]
    ffc = weights.shape[1] // 3 // PLANE
    planes = kv_full.shape[0]
    count = GATHER_COPIES + 14
    return pl.pallas_call(
        spread_down_kernel,
        out_shape=(
            jax.ShapeDtypeStruct((PLANE, rows, ffc), BF16),
            jax.ShapeDtypeStruct((PLANE * block.shape[0], block.shape[1]), BF16),
            jax.ShapeDtypeStruct(kv_full.shape, kv_full.dtype),
            jax.ShapeDtypeStruct((planes, PLANE, rows, HD), BF16),
        ),
        in_specs=[ANY] * 4,
        out_specs=(ANY,) * 4,
        scratch_shapes=[
            DMA((3,)),
            DMA((count,)),
            DMA((count,)),
            *line_semaphores(line_hops(planes)[1]),
        ],
        input_output_aliases={2: 2},
        compiler_params=pltpu.CompilerParams(collective_id=5, has_side_effects=True),
        cost_estimate=cost(1),
        name="spread_down",
    )(weights, block, kv_full, q_rows)


def spread_out_kernel(rows_ref, full_ref, own_sem, send_sem, recv_sem):
    here = place(lax.axis_index(AXIS), PLANE_STEP)
    greet(square(PLANE_STEP))
    copies = Copies(send_sem, recv_sem)
    swap_steps(
        lambda c: [rows_ref.at[:, :, lanes(c, HD)]],
        [full_ref.at[:, here]],
        copies,
        own_sem,
        PLANE_STEP,
    )()
    copies.sent()


def spread_out(out_rows):
    planes, rows = out_rows.shape[:2]
    return pl.pallas_call(
        spread_out_kernel,
        out_shape=jax.ShapeDtypeStruct((planes, PLANE, rows, HD), BF16),
        in_specs=[ANY],
        out_specs=ANY,
        scratch_shapes=[DMA((1,)), DMA((7,)), DMA((7,))],
        compiler_params=pltpu.CompilerParams(collective_id=11, has_side_effects=True),
        cost_estimate=cost(0.1),
        name="spread_out",
    )(out_rows)


def collect_kernel(term_ref, rows_ref, own_sem, send_sem, recv_sem):
    here = place(lax.axis_index(AXIS), PLANE_STEP)
    count = own_sem.shape[0]
    ffc = term_ref.shape[2] // count
    greet(square(PLANE_STEP))
    copies = Copies(send_sem, recv_sem)
    swap_steps(
        lambda c: [term_ref.at[c, :, pl.ds(slot * ffc, ffc)] for slot in range(count)],
        [rows_ref.at[:, lanes(slot * PLANE + here, ffc)] for slot in range(count)],
        copies,
        own_sem,
        PLANE_STEP,
    )()
    copies.sent()


def collect(term, count, collective_id):
    rows, columns = term.shape[1:]
    return pl.pallas_call(
        collect_kernel,
        out_shape=jax.ShapeDtypeStruct((rows, PLANE * columns), BF16),
        in_specs=[ANY],
        out_specs=ANY,
        scratch_shapes=[DMA((count,)), DMA((7 * count,)), DMA((7 * count,))],
        compiler_params=pltpu.CompilerParams(collective_id=collective_id, has_side_effects=True),
        cost_estimate=cost(0.1),
        name="collect",
    )(term)


def collect_attn_kernel(term_ref, rows_ref, own_sem, send_sem, recv_sem):
    here = place(lax.axis_index(AXIS), PLANE_STEP)
    greet(square(PLANE_STEP))
    copies = Copies(send_sem, recv_sem)
    done = swap_steps(
        lambda c: [term_ref.at[c, :, pl.ds(slot * HD, HD)] for slot in range(2)],
        [rows_ref.at[:, wide(offset)] for offset in attn_columns(here)[:2]],
        copies,
        own_sem,
        PLANE_STEP,
    )
    owns = []
    for head in range(H):
        own = pltpu.make_async_copy(
            term_ref.at[head, :, pl.ds(2 * HD, HD)],
            rows_ref.at[:, pl.ds((H + 2 * KVH + head) * HD, HD)],
            own_sem.at[2 + head],
        )
        own.start()
        owns.append(own)
    done()
    for own in owns:
        own.wait()
    copies.sent()


def collect_attn(term):
    rows = term.shape[1]
    return pl.pallas_call(
        collect_attn_kernel,
        out_shape=jax.ShapeDtypeStruct((rows, PLANE * 3 * HD), BF16),
        in_specs=[ANY],
        out_specs=ANY,
        scratch_shapes=[DMA((2 + H,)), DMA((14,)), DMA((14,))],
        compiler_params=pltpu.CompilerParams(collective_id=7, has_side_effects=True),
        name="collect_attn",
    )(term)


def collect_out_kernel(grad_ref, term_ref, own_sem, send_sem, recv_sem):
    here = place(lax.axis_index(AXIS), PLANE_STEP)
    greet(square(PLANE_STEP))
    copies = Copies(send_sem, recv_sem)
    swap_steps(
        lambda c: [grad_ref.at[:, c]],
        [term_ref.at[:, here, :, pl.ds(2 * HD, HD)]],
        copies,
        own_sem,
        PLANE_STEP,
    )()
    copies.sent()


def collect_out(grad, planes):
    rows = grad.shape[0] // planes // PLANE
    return pl.pallas_call(
        collect_out_kernel,
        out_shape=jax.ShapeDtypeStruct((planes, PLANE, rows, 3 * HD), BF16),
        in_specs=[ANY],
        out_specs=ANY,
        scratch_shapes=[DMA((1,)), DMA((7,)), DMA((7,))],
        compiler_params=pltpu.CompilerParams(collective_id=15, has_side_effects=True),
        cost_estimate=cost(0.1),
        name="collect_out",
    )(grad.reshape(planes, PLANE, rows, HD))


def collect_gains_kernel(gain_ref, gains_ref, own_sem, gain_send, gain_recv):
    me = lax.axis_index(AXIS)
    greet_all(gain_ref.shape[0])
    done = exchange_all(lambda device: gain_ref.at[device], gains_ref, gain_send, gain_recv)
    own = pltpu.make_async_copy(gain_ref.at[me], gains_ref.at[me], own_sem)
    own.start()
    own.wait()
    done()


def collect_gains(gain_blocks):
    peers = gain_blocks.shape[0]
    return pl.pallas_call(
        collect_gains_kernel,
        out_shape=jax.ShapeDtypeStruct(gain_blocks.shape, gain_blocks.dtype),
        in_specs=[ANY],
        out_specs=ANY,
        scratch_shapes=[DMA(()), DMA((peers,)), DMA((peers,))],
        compiler_params=pltpu.CompilerParams(collective_id=8, has_side_effects=True),
        name="collect_gains",
    )(gain_blocks)


def block_scores(q, k, start, first):
    scores = lax.dot_general(q, k, (((1,), (1,)), ((), ())), preferred_element_type=F32)
    bent = jnp.tanh(scores * (HD ** (-0.5) / SOFT_CAP))
    rows, span = scores.shape
    key_at = lax.broadcasted_iota(jnp.int32, (rows, span), 1)
    row_at = lax.broadcasted_iota(jnp.int32, (rows, span), 0)
    allowed = (key_at + first >= start) & (key_at <= row_at + LMAX)
    return (bent, jnp.where(allowed, jnp.exp(SOFT_CAP * bent), 0.0))


def attend_kernel(q_ref, k_ref, v_ref, start_ref, out_ref, inv_ref):
    first = pl.program_id(0) * QBLK
    keys = pl.ds(pl.multiple_of(first, QBLK), LMAX + QBLK)
    unused_bent, exponent = block_scores(q_ref[...], k_ref[keys], start_ref[...], first)
    inverse = 1.0 / jnp.sum(exponent, axis=-1, keepdims=True)
    weights = (exponent * inverse).astype(BF16)
    out_ref[...] = jnp.dot(weights, v_ref[keys], preferred_element_type=F32).astype(BF16)
    inv_ref[...] = inverse


def attend(queries, key_rows, value_rows, starts):
    rows = queries.shape[0]
    span = key_rows.shape[0]
    row_spec = pl.BlockSpec((QBLK, HD), lambda i: (i, 0))
    one_spec = pl.BlockSpec((QBLK, 1), lambda i: (i, 0))
    all_spec = pl.BlockSpec((span, HD), lambda i: (0, 0))
    return pl.pallas_call(
        attend_kernel,
        out_shape=(
            jax.ShapeDtypeStruct((rows, HD), BF16),
            jax.ShapeDtypeStruct((rows, 1), F32),
        ),
        grid=(rows // QBLK,),
        in_specs=[row_spec, all_spec, all_spec, one_spec],
        out_specs=(row_spec, one_spec),
        compiler_params=pltpu.CompilerParams(vmem_limit_bytes=40 << 20),
        cost_estimate=cost(1),
        name="attend",
    )(queries, key_rows, value_rows, starts)


GRAD_TILE = 256


def attn_grad_kernel(rows_ref, q_ref, kv_ref, term_in, out_ref):
    for slot, right in enumerate((q_ref, kv_ref)):

        @pl.when(pl.program_id(1) == slot)
        def _():
            out_ref[...] = contract_first(rows_ref[...], right[...]).astype(BF16)


def attn_grad(rows, grad_q, grad_kv, term):
    count, width = rows.shape
    whole = pl.BlockSpec((count, HD), lambda i, j: (0, 0))
    return pl.pallas_call(
        attn_grad_kernel,
        out_shape=jax.ShapeDtypeStruct((width, 3 * HD), BF16),
        grid=(width // GRAD_TILE, 2),
        in_specs=[
            pl.BlockSpec((count, GRAD_TILE), lambda i, j: (0, i)),
            whole,
            whole,
            pl.BlockSpec(memory_space=pl.ANY),
        ],
        out_specs=pl.BlockSpec((GRAD_TILE, HD), lambda i, j: (i, j)),
        input_output_aliases={3: 0},
        compiler_params=pltpu.CompilerParams(vmem_limit_bytes=48 << 20),
        cost_estimate=cost(10),
        name="attn_grad",
    )(rows, grad_q, grad_kv, term.reshape(width, 3 * HD))


def attend_back_kernel(q_ref, k_ref, v_ref, start_ref, inv_ref, grad_ref, gq_ref, gk_ref, gv_ref):
    @pl.when(pl.program_id(0) == 0)
    def _():
        gk_ref[...] = jnp.zeros_like(gk_ref)
        gv_ref[...] = jnp.zeros_like(gv_ref)

    first = pl.program_id(0) * QBLK
    keys = pl.ds(pl.multiple_of(first, QBLK), LMAX + QBLK)
    q, k, v, grad = q_ref[...], k_ref[keys], v_ref[keys], grad_ref[...]
    bent, exponent = block_scores(q, k, start_ref[...], first)
    probability = exponent * inv_ref[...]
    grad_prob = lax.dot_general(grad, v, (((1,), (1,)), ((), ())), preferred_element_type=F32)
    inner = jnp.sum(probability * grad_prob, axis=-1, keepdims=True)
    grad_scores = (probability * (grad_prob - inner) * (1.0 - bent * bent)).astype(BF16)
    scale = HD ** (-0.5)
    gq_ref[...] = jnp.dot(grad_scores, k, preferred_element_type=F32) * scale
    over_rows = (((0,), (0,)), ((), ()))
    gk_ref[keys] += lax.dot_general(grad_scores, q, over_rows, preferred_element_type=F32) * scale
    gv_ref[keys] += lax.dot_general(
        probability.astype(BF16), grad, over_rows, preferred_element_type=F32
    )


def attend_back(queries, key_rows, value_rows, starts, inverse, grad):
    rows = queries.shape[0]
    span = key_rows.shape[0]
    row_spec = pl.BlockSpec((QBLK, HD), lambda i: (i, 0))
    one_spec = pl.BlockSpec((QBLK, 1), lambda i: (i, 0))
    all_spec = pl.BlockSpec((span, HD), lambda i: (0, 0))
    return pl.pallas_call(
        attend_back_kernel,
        out_shape=(
            jax.ShapeDtypeStruct((rows, HD), F32),
            jax.ShapeDtypeStruct((span, HD), F32),
            jax.ShapeDtypeStruct((span, HD), F32),
        ),
        grid=(rows // QBLK,),
        in_specs=[row_spec, all_spec, all_spec, one_spec, one_spec, row_spec],
        out_specs=(row_spec, all_spec, all_spec),
        compiler_params=pltpu.CompilerParams(vmem_limit_bytes=48 << 20),
        cost_estimate=cost(20),
        name="attend_back",
    )(queries, key_rows, value_rows, starts, inverse, grad)


def token_tables(seq_lengths, index_vec):
    count = seq_lengths.shape[0]
    order = jnp.arange(count, dtype=jnp.int32)
    seq_ends = jnp.sum(
        jnp.where(order[None, :] <= order[:, None], seq_lengths[None, :], 0), axis=1
    )
    after_end = index_vec[:, None] >= seq_ends[None, :]
    return index_vec - jnp.sum(jnp.where(after_end, seq_lengths[None, :], 0), axis=1)


def rms_parts(value):
    return lax.rsqrt(jnp.mean(value * value, axis=-1, keepdims=True) + EPSILON)


def rms_forward(value, gain_vec):
    return value * rms_parts(value) * (1.0 + gain_vec)


def rms_backward(value, gain_vec, grad):
    r = rms_parts(value)
    scaled = (1.0 + gain_vec) * grad
    inner = jnp.mean(value * scaled, axis=-1, keepdims=True)
    return (r * scaled - value * (r * r * r * inner), jnp.sum(grad * value * r, axis=0))


def rotate(value, cosine, sine_part):
    half_width = value.shape[-1] // 2
    first_half = value[..., :half_width]
    second_half = value[..., half_width:]
    return jnp.concatenate(
        [
            first_half * cosine - second_half * sine_part,
            second_half * cosine + first_half * sine_part,
        ],
        axis=-1,
    )


def contract_last(left_side, right_side):
    return lax.dot_general(
        left_side, right_side, (((1,), (1,)), ((), ())), preferred_element_type=F32
    )


def contract_first(left_side, right_side):
    return lax.dot_general(
        left_side, right_side, (((0,), (0,)), ((), ())), preferred_element_type=F32
    )


def matmul(left_side, right_side):
    return jnp.dot(left_side, right_side, preferred_element_type=F32)


def gelu_parts(gate):
    k0 = 0.7978845608028654
    k1 = 0.044715
    t = jnp.tanh(k0 * (gate + k1 * gate * gate * gate))
    value = 0.5 * gate * (1.0 + t)
    slope = 0.5 * (1.0 + t) + 0.5 * gate * (1.0 - t * t) * k0 * (1.0 + 3.0 * k1 * gate * gate)
    return (value, slope)


def local(tokens, attn_weights, mlp_weights, norm_gains, seq_lengths, cotangent):
    tok_rows, width = tokens.shape
    peers = lax.axis_size(AXIS)
    planes = peers // PLANE
    share = width // peers
    row_share = attn_weights.shape[0]
    ff = mlp_weights.shape[1] // 3
    ffc = ff // PLANE
    plane_rows = PLANE * tok_rows
    halo = LMAX
    across = [[p * PLANE + i for p in range(planes)] for i in range(PLANE)]
    sibling = [(i, i ^ 1) for i in range(peers)]
    to_next = [(i, i + PLANE) for i in range(peers - PLANE)]
    to_prev = [(i + PLANE, i) for i in range(peers - PLANE)]
    me = lax.axis_index(AXIS)
    is_even = (me % 2) == 0
    plane_start = (me // PLANE) * plane_rows

    def split_features(value):
        value = value.reshape(value.shape[0], planes, 2, width // planes // 2)
        return value.transpose(0, 2, 1, 3).reshape(value.shape[0], width)

    def join_features(value):
        value = value.reshape(value.shape[0], 2, planes, width // planes // 2)
        return value.transpose(0, 2, 1, 3).reshape(value.shape[0], width)

    def gather_across(value):
        return lax.all_gather(value, AXIS, axis=0, tiled=True, axis_index_groups=across)

    def scatter_across(value):
        part = lax.psum_scatter(
            value.astype(BF16), AXIS, scatter_dimension=0, tiled=True, axis_index_groups=across
        )
        return part.reshape(PLANE, -1, part.shape[1])

    kv_full, q_rows, out_rows, gain_rows = lax.optimization_barrier(
        (*spread_attn(attn_weights, planes), norm_gains)
    )
    gain_block = jnp.pad(gain_rows.astype(F32), ((0, 8 - 4), (0, -share % 128)))
    gu_part, gain_blocks, kv_full, q_rows, out_rows = spread_gu(
        mlp_weights, gain_block, kv_full, q_rows, out_rows, peers
    )
    gain_full = gain_blocks[:, :4, :share].transpose(1, 0, 2).reshape(4, width)
    inputs = tokens.astype(F32)
    down_part, normed, kv_full, q_full = spread_down(
        mlp_weights, rms_forward(inputs, gain_full[0]).astype(BF16), kv_full, q_rows
    )
    q_cols, kv_cols = q_full.reshape(width, HD), kv_full.reshape(width, HD)
    gu_cols = gather_across(gu_part.reshape(-1, 2 * ffc))
    down_near = gather_across(down_part[: PLANE // 2].reshape(-1, ffc))
    down_far = gather_across(down_part[PLANE // 2 :].reshape(-1, ffc))

    query_index = plane_start + jnp.arange(plane_rows, dtype=jnp.int32)
    position = token_tables(seq_lengths, query_index)
    starts = (jnp.arange(plane_rows, dtype=jnp.int32) + halo - position)[:, None]
    frequency = 10000.0 ** (-jnp.arange(HD // 2, dtype=F32) * 2.0 / HD)
    angles = position.astype(F32)[:, None] * frequency[None, :]
    cosine, sine_part = jnp.cos(angles), jnp.sin(angles)
    kv_cosine = jnp.where(is_even, cosine, 1.0)
    kv_sine = jnp.where(is_even, sine_part, 0.0)

    kv_own = rotate(matmul(normed, kv_cols), kv_cosine, kv_sine).astype(BF16)
    kv_halo = lax.ppermute(kv_own[plane_rows - halo :], AXIS, to_next)
    kv_own, out_rows, q_cols = lax.optimization_barrier((kv_own, out_rows, q_cols))
    out_cols = spread_out(out_rows).reshape(width, HD)
    queries = rotate(matmul(normed, q_cols), cosine, sine_part).astype(BF16)
    kv_halo, out_cols, queries = lax.optimization_barrier((kv_halo, out_cols, queries))
    kv_mine = jnp.concatenate([kv_halo, kv_own], axis=0)
    kv_other = lax.ppermute(kv_mine, AXIS, sibling)
    key_rows = jnp.where(is_even, kv_mine, kv_other)
    value_rows = jnp.where(is_even, kv_other, kv_mine)
    attended, inverse = attend(queries, key_rows, value_rows, starts)
    attn_proj = product_scatter([attended], [out_cols], [0], PLANE_STEP, 2)

    middle = inputs + rms_forward(attn_proj, gain_full[1])
    mid_low = gather_square(rms_forward(middle, gain_full[2]).astype(BF16), PLANE_STEP, 1)
    gate_up = matmul(mid_low, gu_cols)
    gate, up = gate_up[:, :ffc], gate_up[:, ffc:]
    gelu, slope = gelu_parts(gate)
    hidden = (gelu * up).astype(BF16)
    hidden, gain_split, grad_split = lax.optimization_barrier(
        (hidden, split_features(gain_full[3:4]), split_features(cotangent))
    )
    raw_near = product_scatter([hidden], [down_near], [0], PLANE_STEP, 14)
    raw_far, grad_raw_low, down_grad = turn(
        hidden, down_far, raw_near, gain_split, grad_split, planes, PLANE_STEP, 9
    )
    mlp_raw = join_features(jnp.concatenate([raw_near, raw_far], axis=1))
    if not in_place(width // planes // 2):
        down_grad = join_features(down_grad.T).T
    layer_output = (middle + rms_forward(mlp_raw, gain_full[3])).astype(BF16)

    grad_out = cotangent.astype(F32)
    gain_four = jnp.sum(grad_out * mlp_raw * rms_parts(mlp_raw), axis=0)
    down_term = scatter_across(down_grad)
    grad_hidden = matmul(grad_raw_low, jnp.concatenate([down_near, down_far], axis=0))
    grad_normed_mid, gu_grad = product_scatter_back(
        [(slope * up * grad_hidden).astype(BF16), (gelu * grad_hidden).astype(BF16)],
        [gu_cols, gu_cols],
        [0, ffc],
        mid_low,
        PLANE_STEP,
        10,
    )
    gu_term = scatter_across(gu_grad)
    grad_mid_part, gain_three = rms_backward(middle, gain_full[2], grad_normed_mid)
    grad_middle = grad_out + grad_mid_part

    grad_proj, gain_two = rms_backward(attn_proj, gain_full[1], grad_middle)
    grad_proj_own, down_term = lax.optimization_barrier((grad_proj.astype(BF16), down_term))
    grad_proj_low = gather_square(grad_proj_own, PLANE_STEP, 1)
    grad_att = matmul(grad_proj_low, out_cols).astype(BF16)
    grad_query, grad_keys, grad_values = attend_back(
        queries, key_rows, value_rows, starts, inverse, grad_att
    )
    grad_mine = jnp.where(is_even, grad_keys, grad_values)
    grad_give = jnp.where(is_even, grad_values, grad_keys).astype(BF16)
    grad_kv = grad_mine + lax.ppermute(grad_give, AXIS, sibling).astype(F32)
    grad_back = lax.ppermute(grad_kv[:halo].astype(BF16), AXIS, to_prev).astype(F32)
    down_term, grad_kv = lax.optimization_barrier((down_term, grad_kv))
    down_rows = collect(down_term, 1, 6)
    out_grad = contract_first(grad_proj_low, attended).astype(BF16)
    down_rows, out_grad = lax.optimization_barrier((down_rows, out_grad))
    attn_term = collect_out(out_grad, planes)
    attn_term, grad_back = lax.optimization_barrier((attn_term, grad_back))
    grad_kv = grad_kv[halo:] + jnp.pad(grad_back, ((plane_rows - halo, 0), (0, 0)))
    grad_q = rotate(grad_query, cosine, -sine_part).astype(BF16)
    grad_kv = rotate(grad_kv, kv_cosine, -kv_sine).astype(BF16)
    attn_term, grad_q, grad_kv = lax.optimization_barrier(
        (attn_grad(normed, grad_q, grad_kv, attn_term), grad_q, grad_kv)
    )
    attn_term = scatter_across(attn_term)
    grad_normed = product_scatter([grad_q, grad_kv], [q_cols, kv_cols], [0, 0], PLANE_STEP, 12)
    grad_in_part, gain_one = rms_backward(inputs, gain_full[0], grad_normed)
    grad_tokens = (grad_middle + grad_in_part).astype(BF16)

    gain_term = jnp.stack([gain_one, gain_two, gain_three, gain_four], axis=0)
    gain_term = gain_term.reshape(4, peers, share).transpose(1, 0, 2)
    gain_term = jnp.pad(gain_term, ((0, 0), (0, 8 - 4), (0, -share % 128)))
    gain_recv = collect_gains(gain_term)
    gu_term, gain_recv = lax.optimization_barrier((gu_term, gain_recv))
    gu_rows = collect(gu_term, 2, 13)
    grad_mlp = jnp.concatenate([gu_rows, down_rows], axis=1).astype(F32)
    grad_mlp, attn_term = lax.optimization_barrier((grad_mlp, attn_term))
    grad_attn = collect_attn(attn_term).astype(F32)
    grad_gains = jnp.sum(gain_recv[:, :4, :share], axis=0)
    return (layer_output, grad_tokens, grad_attn, grad_mlp, grad_gains)


def solution(mesh):
    return jax.shard_map(
        local,
        mesh=mesh,
        in_specs=(
            P("fsdp", None),
            P("fsdp", None),
            P("fsdp", None),
            P(None, "fsdp"),
            P(),
            P("fsdp", None),
        ),
        out_specs=(
            P("fsdp", None),
            P("fsdp", None),
            P("fsdp", None),
            P("fsdp", None),
            P(None, "fsdp"),
        ),
        check_vma=False,
    )
```

```python
from functools import partial

import jax
import jax.numpy as jnp
from jax import lax
from jax.experimental import pallas as pl
from jax.experimental.pallas import tpu as pltpu
from jax.sharding import PartitionSpec as P

H = 8
KVH = 4
HD = 256
LMAX = 1024
PLANE = 8
QBLK = 128

EPSILON = 1e-06
SOFT_CAP = 50.0
AXIS = "fsdp"
F32 = jnp.float32
BF16 = jnp.bfloat16
MESH = pl.DeviceIdType.MESH
ANY = pl.BlockSpec(memory_space=pl.ANY)
VMEM = pl.BlockSpec(memory_space=pltpu.VMEM)
DMA = pltpu.SemaphoreType.DMA


def flip(index, step):
    return index + step - 2 * step * ((index // step) % 2)


PLANE_STEP = 4


def partner(index, bits, step):
    for bit, by in ((1, 1), (2, 2), (4, step)):
        if bits & bit:
            index = flip(index, by)
    return index


def place(device, step):
    return device % 4 + 4 * ((device // step) % 2)


def greet(peers):
    barrier = pltpu.get_barrier_semaphore()
    for peer in peers:
        pl.semaphore_signal(barrier, inc=1, device_id=(peer,), device_id_type=MESH)
    pl.semaphore_wait(barrier, len(peers))


class Copies:
    def __init__(self, send_sem, recv_sem):
        self.send_sem, self.recv_sem, self.made = send_sem, recv_sem, []

    def start(self, source, target, device):
        slot = len(self.made)
        copy = pltpu.make_async_remote_copy(
            src_ref=source,
            dst_ref=target,
            send_sem=self.send_sem.at[slot],
            recv_sem=self.recv_sem.at[slot],
            device_id=(device,),
            device_id_type=MESH,
        )
        copy.start()
        self.made.append(copy)
        return copy

    def sent(self):
        for copy in self.made:
            copy.wait_send()


def band(index, size):
    return pl.ds(pl.multiple_of(index * size, 8), size)


def lanes(index, size):
    return pl.ds(pl.multiple_of(index * size, 128), size)


def gather_steps(block_ref, full_ref, copies, own_sem, step):
    rows, width = block_ref.shape
    half = width // 2
    me = lax.axis_index(AXIS)
    sib, xn, yn = flip(me, 1), flip(me, 2), flip(me, step)
    diag = flip(xn, step)

    def at(device, side):
        return full_ref.at[band(place(device, step), rows), pl.ds(side * half, half)]

    def mine(side):
        return block_ref.at[:, pl.ds(side * half, half)]

    own_rows = full_ref.at[band(place(me, step), rows)]
    xa = copies.start(mine(0), at(me, 0), xn)
    ya = copies.start(mine(1), at(me, 1), yn)
    xb = copies.start(mine(1), at(me, 1), xn)
    yb = copies.start(mine(0), at(me, 0), yn)
    arriving = [copies.start(block_ref, own_rows, sib)]
    own = pltpu.make_async_copy(block_ref, own_rows, own_sem)
    own.start()

    def finish(on_rows=None):
        def to_sibling(device, side):
            arriving.append(copies.start(at(device, side), at(device, side), sib))

        def arrived(first, last, *devices):
            for copy in arriving[first:last]:
                copy.wait_recv()
            for device in devices:
                on_rows(device)

        if on_rows is not None:
            own.wait()
            arrived(0, 1, me)
        xa.wait_recv()
        yc = copies.start(at(xn, 0), at(xn, 0), yn)
        to_sibling(xn, 0)
        ya.wait_recv()
        xc = copies.start(at(yn, 1), at(yn, 1), xn)
        to_sibling(yn, 1)
        xb.wait_recv()
        to_sibling(xn, 1)
        yb.wait_recv()
        to_sibling(yn, 0)
        if on_rows is not None:
            arrived(1, 5, xn, yn)
        yc.wait_recv()
        to_sibling(diag, 0)
        xc.wait_recv()
        to_sibling(diag, 1)
        if on_rows is not None:
            arrived(5, 7, diag)
        else:
            arrived(0, 7)
            own.wait()

    return finish


GATHER_COPIES = 13


def cost(microseconds):
    return pl.CostEstimate(
        flops=int(microseconds * 1e7), transcendentals=0, bytes_accessed=int(microseconds * 3e4)
    )


def gather_kernel(block_ref, full_ref, own_sem, send_sem, recv_sem, *, step):
    me = lax.axis_index(AXIS)
    greet((flip(me, 1), flip(me, 2), flip(me, step)))
    copies = Copies(send_sem, recv_sem)
    gather_steps(block_ref, full_ref, copies, own_sem, step)()
    copies.sent()


def gather_square(block, step, collective_id):
    rows, width = block.shape
    return pl.pallas_call(
        partial(gather_kernel, step=step),
        out_shape=jax.ShapeDtypeStruct((PLANE * rows, width), block.dtype),
        in_specs=[ANY],
        out_specs=ANY,
        scratch_shapes=[DMA(()), DMA((GATHER_COPIES,)), DMA((GATHER_COPIES,))],
        compiler_params=pltpu.CompilerParams(collective_id=collective_id, has_side_effects=True),
        cost_estimate=cost(42),
        name="gather_square",
    )(block)


W_TILES = 2
SCATTER_COPIES = 14


def split_columns(width):
    left = (width // 2 + 127) // 128 * 128
    return pl.ds(0, left), pl.ds(left, width - left)


def product_scatter_steps(
    left_refs, right_refs, left_bufs, right_bufs, buffers, load_sem, copies, offsets, step, beside=None
):
    both, got, ra, rb, ra2, rb2 = buffers
    pairs = len(left_refs)
    rows, width = got.shape[1:]
    sides = split_columns(width)
    chunk = 48
    me = lax.axis_index(AXIS)
    core = me % 2
    sib, xn, yn = flip(me, 1), flip(me, 2), flip(me, step)
    order = (flip(xn, step), xn, yn, me)
    first, second = sides

    def chip_rows(device):
        return pl.ds(pl.multiple_of((place(device, step) // 2) * 2 * rows, 16), 2 * rows)

    def right_load(j, t):
        r = sides[t]
        source = right_refs[j].at[r, pl.ds(offsets[j], right_bufs[j].shape[1])]
        return pltpu.make_async_copy(source, right_bufs[j].at[r], load_sem.at[j, t])

    def left_load(j, i):
        r = chip_rows(order[i])
        return pltpu.make_async_copy(
            left_refs[j].at[r], left_bufs[j].at[r], load_sem.at[j, W_TILES + i]
        )

    for j in range(pairs):
        left_load(j, 0).start()
    for t in range(W_TILES):
        for j in range(pairs):
            right_load(j, t).start()
    for i in range(1, 4):
        for j in range(pairs):
            left_load(j, i).start()
    if beside is not None:
        beside[0]()
    greet((sib, xn, yn))

    def mine(i, cols):
        return both.at[i, band(core, rows), cols]

    def add(total, other):
        @pl.loop(0, rows // chunk)
        def _(k):
            r = pl.ds(pl.multiple_of(k * chunk, chunk), chunk)
            total[r] = (total[r].astype(F32) + other[r].astype(F32)).astype(total.dtype)

    loaded = set()

    def make(i, side):
        for j in range(pairs):
            if i not in loaded:
                left_load(j, i).wait()
            if i == 0:
                right_load(j, side).wait()
        loaded.add(i)
        r, cols = chip_rows(order[i]), sides[side]
        total = None
        for j in range(pairs):
            term = contract_last(left_bufs[j][r], right_bufs[j][cols])
            total = term if total is None else total + term
        both[i, :, cols] = total.astype(BF16)
        return copies.start(both.at[i, band(1 - core, rows), cols], got.at[i, :, cols], sib)

    def merge(crossing, i, side):
        cols = sides[side]
        crossing.wait_recv()
        add(mine(i, cols), got.at[i, :, cols])

    c0 = make(0, 0)
    c1 = make(0, 1)
    merge(c0, 0, 0)
    x0 = copies.start(mine(0, first), ra.at[0], xn)
    c2 = make(1, 0)
    merge(c1, 0, 1)
    y0 = copies.start(mine(0, second), rb.at[0], yn)
    c3 = make(2, 1)
    merge(c2, 1, 0)
    x1 = copies.start(mine(1, first), ra.at[1], xn)
    c4 = make(2, 0)
    merge(c3, 2, 1)
    y1 = copies.start(mine(2, second), rb.at[1], yn)
    c5 = make(1, 1)
    merge(c4, 2, 0)
    x0.wait_recv()
    add(mine(2, first), ra.at[0])
    y2 = copies.start(mine(2, first), ra2, yn)
    c6 = make(3, 0)
    merge(c5, 1, 1)
    y0.wait_recv()
    add(mine(1, second), rb.at[0])
    x2 = copies.start(mine(1, second), rb2, xn)
    c7 = make(3, 1)
    merge(c6, 3, 0)
    merge(c7, 3, 1)
    if beside is not None:
        beside[1]()
    for copy in (x1, y1, y2, x2):
        copy.wait_recv()
    own = both.at[3, band(core, rows)]

    def summed(r):
        return jnp.concatenate(
            [
                own[r, first].astype(F32) + ra[1, r].astype(F32) + ra2[r].astype(F32),
                own[r, second].astype(F32) + rb[1, r].astype(F32) + rb2[r].astype(F32),
            ],
            axis=1,
        )

    return summed


ROW_CHUNK = 48


def product_scatter_kernel(*refs, pairs, offsets, step):
    left_refs, right_refs, out_ref = refs[:pairs], refs[pairs : 2 * pairs], refs[2 * pairs]
    left_bufs = refs[2 * pairs + 1 : 3 * pairs + 1]
    right_bufs = refs[3 * pairs + 1 : 4 * pairs + 1]
    buffers, (load_sem, send_sem, recv_sem) = refs[4 * pairs + 1 : -3], refs[-3:]
    copies = Copies(send_sem, recv_sem)
    summed = product_scatter_steps(
        left_refs, right_refs, left_bufs, right_bufs, buffers, load_sem, copies, offsets, step
    )

    @pl.loop(0, out_ref.shape[0] // ROW_CHUNK)
    def _(k):
        r = pl.ds(pl.multiple_of(k * ROW_CHUNK, ROW_CHUNK), ROW_CHUNK)
        out_ref[r] = summed(r)

    copies.sent()


def scatter_buffers(rows, width):
    left, right = [side.size for side in split_columns(width)]
    return [
        pltpu.VMEM((4, 2 * rows, width), BF16),
        pltpu.VMEM((4, rows, width), BF16),
        pltpu.VMEM((2, rows, left), BF16),
        pltpu.VMEM((2, rows, right), BF16),
        pltpu.VMEM((rows, left), BF16),
        pltpu.VMEM((rows, right), BF16),
    ]


def product_scatter(lefts, rights, offsets, step, collective_id):
    pairs = len(lefts)
    rows, width = lefts[0].shape[0] // PLANE, rights[0].shape[0]
    return pl.pallas_call(
        partial(product_scatter_kernel, pairs=pairs, offsets=offsets, step=step),
        out_shape=jax.ShapeDtypeStruct((rows, width), F32),
        in_specs=[ANY] * (2 * pairs),
        out_specs=VMEM,
        scratch_shapes=[
            *[pltpu.VMEM(value.shape, BF16) for value in lefts],
            *[pltpu.VMEM((width, value.shape[1]), BF16) for value in lefts],
            *scatter_buffers(rows, width),
            DMA((pairs, W_TILES + 4)),
            DMA((SCATTER_COPIES,)),
            DMA((SCATTER_COPIES,)),
        ],
        compiler_params=pltpu.CompilerParams(
            collective_id=collective_id, has_side_effects=True, vmem_limit_bytes=56 << 20
        ),
        cost_estimate=cost(50),
        name="product_scatter",
    )(*lefts, *rights)


BACK_TILE = 384


def back_kernel(*refs, pairs, offsets, step):
    left_refs, right_refs, rows_ref = refs[:pairs], refs[pairs : 2 * pairs], refs[2 * pairs]
    out_ref, term_ref = refs[2 * pairs + 1 : 2 * pairs + 3]
    scratch = refs[2 * pairs + 3 :]
    left_bufs, right_bufs = scratch[:pairs], scratch[pairs : 2 * pairs]
    rows_buf, stage = scratch[2 * pairs : 2 * pairs + 2]
    buffers = scratch[2 * pairs + 2 : -5]
    load_sem, rows_sem, store_sem, send_sem, recv_sem = scratch[-5:]
    copies = Copies(send_sem, recv_sem)
    rows_load = pltpu.make_async_copy(rows_ref, rows_buf, rows_sem)
    tiles = rows_ref.shape[1] // BACK_TILE
    width = left_refs[0].shape[1]

    def store(t):
        return pltpu.make_async_copy(
            stage.at[t % 2],
            term_ref.at[pl.ds(pl.multiple_of(t * BACK_TILE, 16), BACK_TILE)],
            store_sem.at[t % 2],
        )

    def beside():
        rows_load.wait()

        @pl.loop(0, tiles)
        def _(t):
            @pl.when(t >= 2)
            def _():
                store(t - 2).wait()

            columns = rows_buf[:, pl.ds(pl.multiple_of(t * BACK_TILE, BACK_TILE), BACK_TILE)]
            for j in range(pairs):
                term = contract_first(columns, left_bufs[j][...])
                stage[t % 2, :, pl.ds(j * width, width)] = term.astype(BF16)
            store(t).start()

    def start_rows():
        rows_load.start()

    summed = product_scatter_steps(
        left_refs,
        right_refs,
        left_bufs,
        right_bufs,
        buffers,
        load_sem,
        copies,
        offsets,
        step,
        (start_rows, beside),
    )

    @pl.loop(0, out_ref.shape[0] // ROW_CHUNK)
    def _(k):
        r = pl.ds(pl.multiple_of(k * ROW_CHUNK, ROW_CHUNK), ROW_CHUNK)
        out_ref[r] = summed(r)

    for t in range(tiles - 2, tiles):
        store(t).wait()
    copies.sent()


def product_scatter_back(lefts, rights, offsets, rows, step, collective_id):
    pairs = len(lefts)
    count, width = lefts[0].shape[0] // PLANE, rights[0].shape[0]
    columns = sum(value.shape[1] for value in lefts)
    return pl.pallas_call(
        partial(back_kernel, pairs=pairs, offsets=offsets, step=step),
        out_shape=(
            jax.ShapeDtypeStruct((count, width), F32),
            jax.ShapeDtypeStruct((rows.shape[1], columns), BF16),
        ),
        in_specs=[ANY] * (2 * pairs + 1),
        out_specs=(VMEM, ANY),
        scratch_shapes=[
            *[pltpu.VMEM(value.shape, BF16) for value in lefts],
            *[pltpu.VMEM((width, value.shape[1]), BF16) for value in lefts],
            pltpu.VMEM(rows.shape, BF16),
            pltpu.VMEM((2, BACK_TILE, columns), BF16),
            *scatter_buffers(count, width),
            DMA((pairs, W_TILES + 4)),
            DMA(()),
            DMA((2,)),
            DMA((SCATTER_COPIES,)),
            DMA((SCATTER_COPIES,)),
        ],
        compiler_params=pltpu.CompilerParams(
            collective_id=collective_id, has_side_effects=True, vmem_limit_bytes=62 << 20
        ),
        cost_estimate=cost(60),
        name="product_scatter_back",
    )(*lefts, *rights, rows)


TURN_TILE = 768


def in_place(rows):
    return rows % 16 == 0


def turn_kernel(
    left_ref,
    right_ref,
    near_ref,
    gain_ref,
    grad_ref,
    raw_ref,
    full_ref,
    term_ref,
    *refs,
    planes,
    step,
):
    left_buf, right_buf, gathered, total, grad_own, stage = refs[:6]
    buffers, (load_sem, own_sem, store_sem, send_sem, recv_sem) = refs[6:-5], refs[-5:]
    rows, width = grad_ref.shape
    half = width // 2
    piece = half // planes
    copies = Copies(send_sem, recv_sem)
    summed = product_scatter_steps(
        [left_ref], [right_ref], [left_buf], [right_buf], buffers, load_sem, copies, [0], step
    )
    gain = gain_ref[...]

    @pl.loop(0, rows // ROW_CHUNK)
    def _(k):
        r = pl.ds(pl.multiple_of(k * ROW_CHUNK, ROW_CHUNK), ROW_CHUNK)
        far = summed(r)
        raw_ref[r] = far
        value = jnp.concatenate([near_ref[r], far], axis=1)
        scale = lax.rsqrt(jnp.mean(value * value, axis=1, keepdims=True) + EPSILON)
        scaled = (1.0 + gain) * grad_ref[r].astype(F32)
        inner = jnp.mean(value * scaled, axis=1, keepdims=True)
        grad_own[r] = (scale * scaled - value * (scale * scale * scale * inner)).astype(BF16)

    stores = []

    def store_term(side):
        for plane in range(planes):
            start = side * half + plane * piece
            target = plane * 2 * piece + side * piece if in_place(piece) else start
            pltpu.make_async_copy(
                stage.at[pl.ds(start, piece)] if in_place(piece) else stage.at[pl.ds(side * half, half)],
                term_ref.at[pl.ds(target, piece)]
                if in_place(piece)
                else term_ref.at[pl.ds(side * half, half)],
                store_sem.at[4],
            ).start()
            if not in_place(piece):
                break

    def on_rows(device):
        slot = len(stores)
        r = pl.ds(pl.multiple_of((place(device, step) // 2) * 2 * rows, 16), 2 * rows)
        store = pltpu.make_async_copy(gathered.at[r], full_ref.at[r], store_sem.at[slot])
        store.start()
        stores.append(store)
        right = left_buf[r]
        if slot < 3:

            @pl.loop(0, width // TURN_TILE)
            def _(t):
                w = pl.ds(pl.multiple_of(t * TURN_TILE, TURN_TILE), TURN_TILE)
                term = contract_first(gathered[r, w], right)
                if slot == 0:
                    total[w] = term
                else:
                    total[w] += term
        else:
            for side in range(2):

                w = pl.ds(side * half, half)
                stage[w] = (total[w] + contract_first(gathered[r, w], right)).astype(BF16)
                store_term(side)

    gather_steps(grad_own, gathered, copies, own_sem, step)(on_rows)
    pltpu.make_async_copy(stage, term_ref, store_sem.at[4]).wait()
    for store in stores:
        store.wait()
    copies.sent()


def turn(left, right, near, gain_row, grad, planes, step, collective_id):
    rows, width = grad.shape
    count = SCATTER_COPIES + GATHER_COPIES
    return pl.pallas_call(
        partial(turn_kernel, planes=planes, step=step),
        out_shape=(
            jax.ShapeDtypeStruct((rows, width // 2), F32),
            jax.ShapeDtypeStruct((PLANE * rows, width), BF16),
            jax.ShapeDtypeStruct((width, left.shape[1]), BF16),
        ),
        in_specs=[ANY, ANY, VMEM, VMEM, VMEM],
        out_specs=(VMEM, ANY, ANY),
        scratch_shapes=[
            pltpu.VMEM(left.shape, BF16),
            pltpu.VMEM(right.shape, BF16),
            pltpu.VMEM((PLANE * rows, width), BF16),
            pltpu.VMEM((width, left.shape[1]), F32),
            pltpu.VMEM((rows, width), BF16),
            pltpu.VMEM((width, left.shape[1]), BF16),
            *scatter_buffers(rows, width // 2),
            DMA((1, W_TILES + 4)),
            DMA(()),
            DMA((5,)),
            DMA((count,)),
            DMA((count,)),
        ],
        compiler_params=pltpu.CompilerParams(
            collective_id=collective_id, has_side_effects=True, vmem_limit_bytes=60 << 20
        ),
        cost_estimate=cost(50),
        name="turn",
    )(left, right, near, gain_row, grad)


def attn_columns(column):
    query_width = H * HD
    key_offset = query_width + (column % 2) * KVH * HD + (column // 2) * HD
    return (column * HD, key_offset, query_width + 2 * KVH * HD + column * HD)


def greet_all(peers):
    me = lax.axis_index(AXIS)
    barrier = pltpu.get_barrier_semaphore()

    @pl.loop(1, peers)
    def _(k):
        device = lax.rem(me + k, peers)
        pl.semaphore_signal(barrier, inc=1, device_id=(device,), device_id_type=MESH)

    pl.semaphore_wait(barrier, peers - 1)


def exchange_all(source_of, target_ref, send_sem, recv_sem):
    peers = target_ref.shape[0]
    me = lax.axis_index(AXIS)

    def copy(k):
        device = lax.rem(me + k, peers)
        return pltpu.make_async_remote_copy(
            src_ref=source_of(device),
            dst_ref=target_ref.at[me],
            send_sem=send_sem.at[k],
            recv_sem=recv_sem.at[k],
            device_id=(device,),
            device_id_type=MESH,
        )

    @pl.loop(1, peers)
    def _(k):
        copy(k).start()

    def finish():
        @pl.loop(1, peers)
        def _(k):
            copy(k).wait()

    return finish


ORDER = (6, 7, 2, 3, 4, 5, 1)


def swap_steps(pieces_of, targets, copies, own_sem, step):
    me = lax.axis_index(AXIS)
    moved = []
    for bits in ORDER:
        peer = partner(me, bits, step)
        for source, target in zip(pieces_of(place(peer, step)), targets):
            moved.append(copies.start(source, target, peer))
    owns = []
    for slot, (source, target) in enumerate(zip(pieces_of(place(me, step)), targets)):
        own = pltpu.make_async_copy(source, target, own_sem.at[slot])
        own.start()
        owns.append(own)

    def finish():
        for own in owns:
            own.wait()
        for copy in moved:
            copy.wait_recv()

    return finish


def square(step):
    me = lax.axis_index(AXIS)
    return [partner(me, bits, step) for bits in ORDER]


def wide(offset):
    return pl.ds(pl.multiple_of(offset, 128), HD)


class Line:
    def __init__(self, full_ref, send_sem, recv_sem, own_ref=None):
        me = lax.axis_index(AXIS)
        self.own = own_ref
        self.full, self.planes = full_ref, full_ref.shape[0]
        self.send_sem, self.recv_sem = send_sem, recv_sem
        self.plane = me // PLANE
        peers = self.planes * PLANE
        self.devices = (lax.rem(me + PLANE, peers), lax.rem(me + peers - PLANE, peers))

    def copy(self, way, slot, source, first=False):
        return pltpu.make_async_remote_copy(
            src_ref=self.own if first and self.own is not None else self.full.at[source],
            dst_ref=self.full.at[source],
            send_sem=self.send_sem.at[way, slot],
            recv_sem=self.recv_sem.at[way, slot],
            device_id=(self.devices[way],),
            device_id_type=MESH,
        )

    def sends(self, way, hop):
        if way == 0:
            source = self.plane - (hop - 1)
            return (self.plane + 1 < self.planes) & (source >= 0), source
        source = self.plane + (hop - 1)
        return (self.plane >= 1) & (source < self.planes), source

    def greet(self):
        barrier = pltpu.get_barrier_semaphore()
        count = 0
        for way, there in enumerate((self.plane + 1 < self.planes, self.plane >= 1)):

            @pl.when(there)
            def _():
                pl.semaphore_signal(
                    barrier, inc=1, device_id=(self.devices[way],), device_id_type=MESH
                )

            count = count + there.astype(jnp.int32)
        return count

    def start(self, hop, slot):
        for way in range(2):
            there, source = self.sends(way, hop)

            @pl.when(there)
            def _():
                self.copy(way, slot, source, hop == 1).start()

    def arrived(self, hop, slot):
        for way in range(2):
            source = self.plane - hop if way == 0 else self.plane + hop

            @pl.when((source >= 0) & (source < self.planes))
            def _():
                self.copy(way, slot, source).wait_recv()

    def sent(self, hop, slot):
        for way in range(2):
            there, source = self.sends(way, hop)

            @pl.when(there)
            def _():
                self.copy(way, slot, source, hop == 1).wait_send()

    def begin(self, hops):
        if hops:
            self.start(hops[0], 0)

    def run(self, hops):
        for slot, hop in enumerate(hops):
            self.arrived(hop, slot)
            if slot + 1 < len(hops):
                self.start(hop + 1, slot + 1)

    def end(self, hops):
        for slot, hop in enumerate(hops):
            self.sent(hop, slot)


def line_hops(planes):
    hops = list(range(1, planes))
    first = (2 * len(hops) + 2) // 3
    return hops[:first], hops[first:]


def line_semaphores(hops):
    count = max(1, len(hops))
    return [DMA((2, count)), DMA((2, count))]


def greet_line(line, peers):
    barrier = pltpu.get_barrier_semaphore()
    for peer in peers:
        pl.semaphore_signal(barrier, inc=1, device_id=(peer,), device_id_type=MESH)
    pl.semaphore_wait(barrier, len(peers) + line.greet())


def row_bands(weights_ref):
    return [weights_ref.at[:, pl.ds(start * HD, H * HD)] for start in (0, H + 2 * KVH)]


def spread_attn_kernel(weights_ref, kv_ref, q_ref, out_ref, own_sem, send_sem, recv_sem, *sems):
    me = lax.axis_index(AXIS)
    plane, here = me // PLANE, place(me, PLANE_STEP)
    q_rows, out_rows = row_bands(weights_ref)
    q_line = Line(q_ref, sems[0], sems[1], q_rows)
    out_line = Line(out_ref, sems[2], sems[3], out_rows)
    hops = line_hops(out_line.planes)[0]
    greet_line(out_line, square(PLANE_STEP))
    out_line.begin(hops)
    q_line.begin([1])
    owns = []
    for slot, (source, target) in enumerate(((q_rows, q_ref), (out_rows, out_ref))):
        own = pltpu.make_async_copy(source, target.at[plane], own_sem.at[1 + slot])
        own.start()
        owns.append(own)
    copies = Copies(send_sem, recv_sem)
    spread = swap_steps(
        lambda c: [weights_ref.at[:, wide(attn_columns(c)[1])]],
        [kv_ref.at[plane, here]],
        copies,
        own_sem,
        PLANE_STEP,
    )
    out_line.run(hops)
    q_line.run([1])
    spread()
    for own in owns:
        own.wait()
    out_line.end(hops)
    q_line.end([1])
    copies.sent()


def spread_attn(weights, planes):
    rows = weights.shape[0]
    return pl.pallas_call(
        spread_attn_kernel,
        out_shape=(
            jax.ShapeDtypeStruct((planes, PLANE, rows, HD), BF16),
            jax.ShapeDtypeStruct((planes, rows, H * HD), BF16),
            jax.ShapeDtypeStruct((planes, rows, H * HD), BF16),
        ),
        in_specs=[ANY],
        out_specs=(ANY, ANY, ANY),
        scratch_shapes=[
            DMA((3,)),
            DMA((7,)),
            DMA((7,)),
            *line_semaphores([1]),
            *line_semaphores(line_hops(planes)[0]),
        ],
        compiler_params=pltpu.CompilerParams(collective_id=3, has_side_effects=True),
        name="spread_attn",
    )(weights)


def spread_gu_kernel(
    weights_ref,
    gain_ref,
    kv_in,
    q_in,
    out_in,
    gu_ref,
    gains_ref,
    kv_ref,
    q_ref,
    out_ref,
    own_sem,
    send_sem,
    recv_sem,
    gain_send,
    gain_recv,
    *sems,
):
    peers = gains_ref.shape[0]
    ffc = gu_ref.shape[2] // 2
    me = lax.axis_index(AXIS)
    here = place(me, PLANE_STEP)
    kv_line = Line(kv_ref, sems[0], sems[1])
    q_line = Line(q_ref, sems[2], sems[3])
    out_line = Line(out_ref, sems[4], sems[5])
    kv_hops, out_hops = line_hops(kv_line.planes)
    q_hops = list(range(2, kv_line.planes))
    greet_all(peers)
    q_line.begin(q_hops)
    out_line.begin(out_hops)
    kv_line.begin(kv_hops)
    gains_done = exchange_all(lambda device: gain_ref, gains_ref, gain_send, gain_recv)
    own = pltpu.make_async_copy(gain_ref, gains_ref.at[me], own_sem.at[2])
    own.start()
    copies = Copies(send_sem, recv_sem)
    spread = swap_steps(
        lambda c: [weights_ref.at[:, lanes(slot * PLANE + c, ffc)] for slot in range(2)],
        [gu_ref.at[here, :, pl.ds(slot * ffc, ffc)] for slot in range(2)],
        copies,
        own_sem,
        PLANE_STEP,
    )
    q_line.run(q_hops)
    out_line.run(out_hops)
    kv_line.run(kv_hops)
    spread()
    own.wait()
    gains_done()
    for line, hops in ((q_line, q_hops), (out_line, out_hops), (kv_line, kv_hops)):
        line.end(hops)
    copies.sent()


def spread_gu(weights, gain_block, kv_full, q_rows, out_rows, peers):
    rows = weights.shape[0]
    ffc = weights.shape[1] // 3 // PLANE
    planes = kv_full.shape[0]
    kv_hops, out_hops = line_hops(planes)
    return pl.pallas_call(
        spread_gu_kernel,
        out_shape=(
            jax.ShapeDtypeStruct((PLANE, rows, 2 * ffc), BF16),
            jax.ShapeDtypeStruct((peers,) + gain_block.shape, gain_block.dtype),
            jax.ShapeDtypeStruct(kv_full.shape, kv_full.dtype),
            jax.ShapeDtypeStruct(q_rows.shape, q_rows.dtype),
            jax.ShapeDtypeStruct(out_rows.shape, out_rows.dtype),
        ),
        in_specs=[ANY] * 5,
        out_specs=(ANY,) * 5,
        scratch_shapes=[
            DMA((3,)),
            DMA((14,)),
            DMA((14,)),
            DMA((peers,)),
            DMA((peers,)),
            *line_semaphores(kv_hops),
            *line_semaphores(range(2, planes)),
            *line_semaphores(out_hops),
        ],
        input_output_aliases={2: 2, 3: 3, 4: 4},
        compiler_params=pltpu.CompilerParams(collective_id=4, has_side_effects=True),
        cost_estimate=cost(38),
        name="spread_gu",
    )(weights, gain_block, kv_full, q_rows, out_rows)


def spread_down_kernel(
    weights_ref,
    block_ref,
    kv_in,
    rows_ref,
    down_ref,
    full_ref,
    kv_ref,
    q_ref,
    own_sem,
    send_sem,
    recv_sem,
    line_send,
    line_recv,
):
    ffc = down_ref.shape[2]
    here = place(lax.axis_index(AXIS), PLANE_STEP)
    line = Line(kv_ref, line_send, line_recv)
    hops = line_hops(line.planes)[1]
    greet_line(line, square(PLANE_STEP))
    line.begin(hops)
    copies = Copies(send_sem, recv_sem)
    gathered = gather_steps(block_ref, full_ref, copies, own_sem.at[2], PLANE_STEP)
    spread = swap_steps(
        lambda c: [
            rows_ref.at[:, :, lanes(c, HD)],
            weights_ref.at[:, lanes(2 * PLANE + c, ffc)],
        ],
        [q_ref.at[:, here], down_ref.at[here]],
        copies,
        own_sem,
        PLANE_STEP,
    )
    gathered()
    line.run(hops)
    spread()
    line.end(hops)
    copies.sent()


def spread_down(weights, block, kv_full, q_rows):
    rows = weights.shape[0]
    ffc = weights.shape[1] // 3 // PLANE
    planes = kv_full.shape[0]
    count = GATHER_COPIES + 14
    return pl.pallas_call(
        spread_down_kernel,
        out_shape=(
            jax.ShapeDtypeStruct((PLANE, rows, ffc), BF16),
            jax.ShapeDtypeStruct((PLANE * block.shape[0], block.shape[1]), BF16),
            jax.ShapeDtypeStruct(kv_full.shape, kv_full.dtype),
            jax.ShapeDtypeStruct((planes, PLANE, rows, HD), BF16),
        ),
        in_specs=[ANY] * 4,
        out_specs=(ANY,) * 4,
        scratch_shapes=[
            DMA((3,)),
            DMA((count,)),
            DMA((count,)),
            *line_semaphores(line_hops(planes)[1]),
        ],
        input_output_aliases={2: 2},
        compiler_params=pltpu.CompilerParams(collective_id=5, has_side_effects=True),
        cost_estimate=cost(1),
        name="spread_down",
    )(weights, block, kv_full, q_rows)


def spread_out_kernel(rows_ref, full_ref, own_sem, send_sem, recv_sem):
    here = place(lax.axis_index(AXIS), PLANE_STEP)
    greet(square(PLANE_STEP))
    copies = Copies(send_sem, recv_sem)
    swap_steps(
        lambda c: [rows_ref.at[:, :, lanes(c, HD)]],
        [full_ref.at[:, here]],
        copies,
        own_sem,
        PLANE_STEP,
    )()
    copies.sent()


def spread_out(out_rows):
    planes, rows = out_rows.shape[:2]
    return pl.pallas_call(
        spread_out_kernel,
        out_shape=jax.ShapeDtypeStruct((planes, PLANE, rows, HD), BF16),
        in_specs=[ANY],
        out_specs=ANY,
        scratch_shapes=[DMA((1,)), DMA((7,)), DMA((7,))],
        compiler_params=pltpu.CompilerParams(collective_id=11, has_side_effects=True),
        cost_estimate=cost(0.1),
        name="spread_out",
    )(out_rows)


def collect_kernel(term_ref, rows_ref, own_sem, send_sem, recv_sem):
    here = place(lax.axis_index(AXIS), PLANE_STEP)
    count = own_sem.shape[0]
    ffc = term_ref.shape[2] // count
    greet(square(PLANE_STEP))
    copies = Copies(send_sem, recv_sem)
    swap_steps(
        lambda c: [term_ref.at[c, :, pl.ds(slot * ffc, ffc)] for slot in range(count)],
        [rows_ref.at[:, lanes(slot * PLANE + here, ffc)] for slot in range(count)],
        copies,
        own_sem,
        PLANE_STEP,
    )()
    copies.sent()


def collect(term, count, collective_id):
    rows, columns = term.shape[1:]
    return pl.pallas_call(
        collect_kernel,
        out_shape=jax.ShapeDtypeStruct((rows, PLANE * columns), BF16),
        in_specs=[ANY],
        out_specs=ANY,
        scratch_shapes=[DMA((count,)), DMA((7 * count,)), DMA((7 * count,))],
        compiler_params=pltpu.CompilerParams(collective_id=collective_id, has_side_effects=True),
        cost_estimate=cost(0.1),
        name="collect",
    )(term)


def collect_attn_kernel(term_ref, rows_ref, own_sem, send_sem, recv_sem):
    here = place(lax.axis_index(AXIS), PLANE_STEP)
    greet(square(PLANE_STEP))
    copies = Copies(send_sem, recv_sem)
    swap_steps(
        lambda c: [term_ref.at[c, :, pl.ds(slot * HD, HD)] for slot in range(3)],
        [rows_ref.at[:, wide(offset)] for offset in attn_columns(here)],
        copies,
        own_sem,
        PLANE_STEP,
    )()
    copies.sent()


def collect_attn(term):
    rows = term.shape[1]
    return pl.pallas_call(
        collect_attn_kernel,
        out_shape=jax.ShapeDtypeStruct((rows, PLANE * 3 * HD), BF16),
        in_specs=[ANY],
        out_specs=ANY,
        scratch_shapes=[DMA((3,)), DMA((21,)), DMA((21,))],
        compiler_params=pltpu.CompilerParams(collective_id=7, has_side_effects=True),
        name="collect_attn",
    )(term)


def collect_gains_kernel(gain_ref, gains_ref, own_sem, gain_send, gain_recv):
    me = lax.axis_index(AXIS)
    greet_all(gain_ref.shape[0])
    done = exchange_all(lambda device: gain_ref.at[device], gains_ref, gain_send, gain_recv)
    own = pltpu.make_async_copy(gain_ref.at[me], gains_ref.at[me], own_sem)
    own.start()
    own.wait()
    done()


def collect_gains(gain_blocks):
    peers = gain_blocks.shape[0]
    return pl.pallas_call(
        collect_gains_kernel,
        out_shape=jax.ShapeDtypeStruct(gain_blocks.shape, gain_blocks.dtype),
        in_specs=[ANY],
        out_specs=ANY,
        scratch_shapes=[DMA(()), DMA((peers,)), DMA((peers,))],
        compiler_params=pltpu.CompilerParams(collective_id=8, has_side_effects=True),
        name="collect_gains",
    )(gain_blocks)


def block_scores(q, k, start, first):
    scores = lax.dot_general(q, k, (((1,), (1,)), ((), ())), preferred_element_type=F32)
    bent = jnp.tanh(scores * (HD ** (-0.5) / SOFT_CAP))
    rows, span = scores.shape
    key_at = lax.broadcasted_iota(jnp.int32, (rows, span), 1)
    row_at = lax.broadcasted_iota(jnp.int32, (rows, span), 0)
    allowed = (key_at + first >= start) & (key_at <= row_at + LMAX)
    return (bent, jnp.where(allowed, jnp.exp(SOFT_CAP * bent), 0.0))


def attend_kernel(q_ref, k_ref, v_ref, start_ref, out_ref, inv_ref):
    first = pl.program_id(0) * QBLK
    keys = pl.ds(pl.multiple_of(first, QBLK), LMAX + QBLK)
    unused_bent, exponent = block_scores(q_ref[...], k_ref[keys], start_ref[...], first)
    inverse = 1.0 / jnp.sum(exponent, axis=-1, keepdims=True)
    weights = (exponent * inverse).astype(BF16)
    out_ref[...] = jnp.dot(weights, v_ref[keys], preferred_element_type=F32).astype(BF16)
    inv_ref[...] = inverse


def attend(queries, key_rows, value_rows, starts):
    rows = queries.shape[0]
    span = key_rows.shape[0]
    row_spec = pl.BlockSpec((QBLK, HD), lambda i: (i, 0))
    one_spec = pl.BlockSpec((QBLK, 1), lambda i: (i, 0))
    all_spec = pl.BlockSpec((span, HD), lambda i: (0, 0))
    return pl.pallas_call(
        attend_kernel,
        out_shape=(
            jax.ShapeDtypeStruct((rows, HD), BF16),
            jax.ShapeDtypeStruct((rows, 1), F32),
        ),
        grid=(rows // QBLK,),
        in_specs=[row_spec, all_spec, all_spec, one_spec],
        out_specs=(row_spec, one_spec),
        compiler_params=pltpu.CompilerParams(vmem_limit_bytes=40 << 20),
        cost_estimate=cost(1),
        name="attend",
    )(queries, key_rows, value_rows, starts)


GRAD_TILE = 384


def attn_grad_kernel(rows_ref, q_ref, kv_ref, proj_ref, attended_ref, out_ref):
    for slot, (left, right) in enumerate(
        ((rows_ref, q_ref), (rows_ref, kv_ref), (proj_ref, attended_ref))
    ):
        out_ref[:, pl.ds(slot * HD, HD)] = contract_first(left[...], right[...]).astype(BF16)


def attn_grad(rows, grad_q, grad_kv, grad_proj, attended):
    count, width = rows.shape
    tile = pl.BlockSpec((count, GRAD_TILE), lambda i: (0, i))
    whole = pl.BlockSpec((count, HD), lambda i: (0, 0))
    return pl.pallas_call(
        attn_grad_kernel,
        out_shape=jax.ShapeDtypeStruct((width, 3 * HD), BF16),
        grid=(width // GRAD_TILE,),
        in_specs=[tile, whole, whole, tile, whole],
        out_specs=pl.BlockSpec((GRAD_TILE, 3 * HD), lambda i: (i, 0)),
        compiler_params=pltpu.CompilerParams(vmem_limit_bytes=48 << 20),
        cost_estimate=cost(10),
        name="attn_grad",
    )(rows, grad_q, grad_kv, grad_proj, attended)


def attend_back_kernel(q_ref, k_ref, v_ref, start_ref, inv_ref, grad_ref, gq_ref, gk_ref, gv_ref):
    @pl.when(pl.program_id(0) == 0)
    def _():
        gk_ref[...] = jnp.zeros_like(gk_ref)
        gv_ref[...] = jnp.zeros_like(gv_ref)

    first = pl.program_id(0) * QBLK
    keys = pl.ds(pl.multiple_of(first, QBLK), LMAX + QBLK)
    q, k, v, grad = q_ref[...], k_ref[keys], v_ref[keys], grad_ref[...]
    bent, exponent = block_scores(q, k, start_ref[...], first)
    probability = exponent * inv_ref[...]
    grad_prob = lax.dot_general(grad, v, (((1,), (1,)), ((), ())), preferred_element_type=F32)
    inner = jnp.sum(probability * grad_prob, axis=-1, keepdims=True)
    grad_scores = (probability * (grad_prob - inner) * (1.0 - bent * bent)).astype(BF16)
    scale = HD ** (-0.5)
    gq_ref[...] = jnp.dot(grad_scores, k, preferred_element_type=F32) * scale
    over_rows = (((0,), (0,)), ((), ()))
    gk_ref[keys] += lax.dot_general(grad_scores, q, over_rows, preferred_element_type=F32) * scale
    gv_ref[keys] += lax.dot_general(
        probability.astype(BF16), grad, over_rows, preferred_element_type=F32
    )


def attend_back(queries, key_rows, value_rows, starts, inverse, grad):
    rows = queries.shape[0]
    span = key_rows.shape[0]
    row_spec = pl.BlockSpec((QBLK, HD), lambda i: (i, 0))
    one_spec = pl.BlockSpec((QBLK, 1), lambda i: (i, 0))
    all_spec = pl.BlockSpec((span, HD), lambda i: (0, 0))
    return pl.pallas_call(
        attend_back_kernel,
        out_shape=(
            jax.ShapeDtypeStruct((rows, HD), F32),
            jax.ShapeDtypeStruct((span, HD), F32),
            jax.ShapeDtypeStruct((span, HD), F32),
        ),
        grid=(rows // QBLK,),
        in_specs=[row_spec, all_spec, all_spec, one_spec, one_spec, row_spec],
        out_specs=(row_spec, all_spec, all_spec),
        compiler_params=pltpu.CompilerParams(vmem_limit_bytes=48 << 20),
        cost_estimate=cost(20),
        name="attend_back",
    )(queries, key_rows, value_rows, starts, inverse, grad)


def token_tables(seq_lengths, index_vec):
    count = seq_lengths.shape[0]
    order = jnp.arange(count, dtype=jnp.int32)
    seq_ends = jnp.sum(
        jnp.where(order[None, :] <= order[:, None], seq_lengths[None, :], 0), axis=1
    )
    after_end = index_vec[:, None] >= seq_ends[None, :]
    return index_vec - jnp.sum(jnp.where(after_end, seq_lengths[None, :], 0), axis=1)


def rms_parts(value):
    return lax.rsqrt(jnp.mean(value * value, axis=-1, keepdims=True) + EPSILON)


def rms_forward(value, gain_vec):
    return value * rms_parts(value) * (1.0 + gain_vec)


def rms_backward(value, gain_vec, grad):
    r = rms_parts(value)
    scaled = (1.0 + gain_vec) * grad
    inner = jnp.mean(value * scaled, axis=-1, keepdims=True)
    return (r * scaled - value * (r * r * r * inner), jnp.sum(grad * value * r, axis=0))


def rotate(value, cosine, sine_part):
    half_width = value.shape[-1] // 2
    first_half = value[..., :half_width]
    second_half = value[..., half_width:]
    return jnp.concatenate(
        [
            first_half * cosine - second_half * sine_part,
            second_half * cosine + first_half * sine_part,
        ],
        axis=-1,
    )


def contract_last(left_side, right_side):
    return lax.dot_general(
        left_side, right_side, (((1,), (1,)), ((), ())), preferred_element_type=F32
    )


def contract_first(left_side, right_side):
    return lax.dot_general(
        left_side, right_side, (((0,), (0,)), ((), ())), preferred_element_type=F32
    )


def matmul(left_side, right_side):
    return jnp.dot(left_side, right_side, preferred_element_type=F32)


def gelu_parts(gate):
    k0 = 0.7978845608028654
    k1 = 0.044715
    t = jnp.tanh(k0 * (gate + k1 * gate * gate * gate))
    value = 0.5 * gate * (1.0 + t)
    slope = 0.5 * (1.0 + t) + 0.5 * gate * (1.0 - t * t) * k0 * (1.0 + 3.0 * k1 * gate * gate)
    return (value, slope)


def local(tokens, attn_weights, mlp_weights, norm_gains, seq_lengths, cotangent):
    tok_rows, width = tokens.shape
    peers = lax.axis_size(AXIS)
    planes = peers // PLANE
    share = width // peers
    row_share = attn_weights.shape[0]
    ff = mlp_weights.shape[1] // 3
    ffc = ff // PLANE
    plane_rows = PLANE * tok_rows
    halo = LMAX
    across = [[p * PLANE + i for p in range(planes)] for i in range(PLANE)]
    sibling = [(i, i ^ 1) for i in range(peers)]
    to_next = [(i, i + PLANE) for i in range(peers - PLANE)]
    to_prev = [(i + PLANE, i) for i in range(peers - PLANE)]
    me = lax.axis_index(AXIS)
    is_even = (me % 2) == 0
    plane_start = (me // PLANE) * plane_rows

    def split_features(value):
        value = value.reshape(value.shape[0], planes, 2, width // planes // 2)
        return value.transpose(0, 2, 1, 3).reshape(value.shape[0], width)

    def join_features(value):
        value = value.reshape(value.shape[0], 2, planes, width // planes // 2)
        return value.transpose(0, 2, 1, 3).reshape(value.shape[0], width)

    def gather_across(value):
        return lax.all_gather(value, AXIS, axis=0, tiled=True, axis_index_groups=across)

    def scatter_across(value):
        part = lax.psum_scatter(
            value.astype(BF16), AXIS, scatter_dimension=0, tiled=True, axis_index_groups=across
        )
        return part.reshape(PLANE, -1, part.shape[1])

    kv_full, q_rows, out_rows, gain_rows = lax.optimization_barrier(
        (*spread_attn(attn_weights, planes), norm_gains)
    )
    gain_block = jnp.pad(gain_rows.astype(F32), ((0, 8 - 4), (0, -share % 128)))
    gu_part, gain_blocks, kv_full, q_rows, out_rows = spread_gu(
        mlp_weights, gain_block, kv_full, q_rows, out_rows, peers
    )
    gain_full = gain_blocks[:, :4, :share].transpose(1, 0, 2).reshape(4, width)
    inputs = tokens.astype(F32)
    down_part, normed, kv_full, q_full = spread_down(
        mlp_weights, rms_forward(inputs, gain_full[0]).astype(BF16), kv_full, q_rows
    )
    q_cols, kv_cols = q_full.reshape(width, HD), kv_full.reshape(width, HD)
    gu_cols = gather_across(gu_part.reshape(-1, 2 * ffc))
    down_near = gather_across(down_part[: PLANE // 2].reshape(-1, ffc))
    down_far = gather_across(down_part[PLANE // 2 :].reshape(-1, ffc))

    query_index = plane_start + jnp.arange(plane_rows, dtype=jnp.int32)
    position = token_tables(seq_lengths, query_index)
    starts = (jnp.arange(plane_rows, dtype=jnp.int32) + halo - position)[:, None]
    frequency = 10000.0 ** (-jnp.arange(HD // 2, dtype=F32) * 2.0 / HD)
    angles = position.astype(F32)[:, None] * frequency[None, :]
    cosine, sine_part = jnp.cos(angles), jnp.sin(angles)
    kv_cosine = jnp.where(is_even, cosine, 1.0)
    kv_sine = jnp.where(is_even, sine_part, 0.0)

    kv_own = rotate(matmul(normed, kv_cols), kv_cosine, kv_sine).astype(BF16)
    kv_halo = lax.ppermute(kv_own[plane_rows - halo :], AXIS, to_next)
    kv_own, out_rows, q_cols = lax.optimization_barrier((kv_own, out_rows, q_cols))
    out_cols = spread_out(out_rows).reshape(width, HD)
    queries = rotate(matmul(normed, q_cols), cosine, sine_part).astype(BF16)
    kv_halo, out_cols, queries = lax.optimization_barrier((kv_halo, out_cols, queries))
    kv_mine = jnp.concatenate([kv_halo, kv_own], axis=0)
    kv_other = lax.ppermute(kv_mine, AXIS, sibling)
    key_rows = jnp.where(is_even, kv_mine, kv_other)
    value_rows = jnp.where(is_even, kv_other, kv_mine)
    attended, inverse = attend(queries, key_rows, value_rows, starts)
    attn_proj = product_scatter([attended], [out_cols], [0], PLANE_STEP, 2)

    middle = inputs + rms_forward(attn_proj, gain_full[1])
    mid_low = gather_square(rms_forward(middle, gain_full[2]).astype(BF16), PLANE_STEP, 1)
    gate_up = matmul(mid_low, gu_cols)
    gate, up = gate_up[:, :ffc], gate_up[:, ffc:]
    gelu, slope = gelu_parts(gate)
    hidden = (gelu * up).astype(BF16)
    hidden, gain_split, grad_split = lax.optimization_barrier(
        (hidden, split_features(gain_full[3:4]), split_features(cotangent))
    )
    raw_near = product_scatter([hidden], [down_near], [0], PLANE_STEP, 14)
    raw_far, grad_raw_low, down_grad = turn(
        hidden, down_far, raw_near, gain_split, grad_split, planes, PLANE_STEP, 9
    )
    mlp_raw = join_features(jnp.concatenate([raw_near, raw_far], axis=1))
    if not in_place(width // planes // 2):
        down_grad = join_features(down_grad.T).T
    layer_output = (middle + rms_forward(mlp_raw, gain_full[3])).astype(BF16)

    grad_out = cotangent.astype(F32)
    gain_four = jnp.sum(grad_out * mlp_raw * rms_parts(mlp_raw), axis=0)
    down_term = scatter_across(down_grad)
    grad_hidden = matmul(grad_raw_low, jnp.concatenate([down_near, down_far], axis=0))
    grad_normed_mid, gu_grad = product_scatter_back(
        [(slope * up * grad_hidden).astype(BF16), (gelu * grad_hidden).astype(BF16)],
        [gu_cols, gu_cols],
        [0, ffc],
        mid_low,
        PLANE_STEP,
        10,
    )
    gu_term = scatter_across(gu_grad)
    grad_mid_part, gain_three = rms_backward(middle, gain_full[2], grad_normed_mid)
    grad_middle = grad_out + grad_mid_part

    grad_proj, gain_two = rms_backward(attn_proj, gain_full[1], grad_middle)
    grad_proj_own, down_term = lax.optimization_barrier((grad_proj.astype(BF16), down_term))
    grad_proj_low = gather_square(grad_proj_own, PLANE_STEP, 1)
    grad_att = matmul(grad_proj_low, out_cols).astype(BF16)
    grad_query, grad_keys, grad_values = attend_back(
        queries, key_rows, value_rows, starts, inverse, grad_att
    )
    grad_mine = jnp.where(is_even, grad_keys, grad_values)
    grad_give = jnp.where(is_even, grad_values, grad_keys).astype(BF16)
    grad_kv = grad_mine + lax.ppermute(grad_give, AXIS, sibling).astype(F32)
    grad_back = lax.ppermute(grad_kv[:halo].astype(BF16), AXIS, to_prev).astype(F32)
    down_term, grad_kv = lax.optimization_barrier((down_term, grad_kv))
    down_rows = collect(down_term, 1, 6)
    down_rows, grad_back = lax.optimization_barrier((down_rows, grad_back))
    grad_kv = grad_kv[halo:] + jnp.pad(grad_back, ((plane_rows - halo, 0), (0, 0)))
    grad_q = rotate(grad_query, cosine, -sine_part).astype(BF16)
    grad_kv = rotate(grad_kv, kv_cosine, -kv_sine).astype(BF16)
    attn_term, grad_q, grad_kv = lax.optimization_barrier(
        (attn_grad(normed, grad_q, grad_kv, grad_proj_low, attended), grad_q, grad_kv)
    )
    attn_term = scatter_across(attn_term)
    grad_normed = product_scatter([grad_q, grad_kv], [q_cols, kv_cols], [0, 0], PLANE_STEP, 12)
    grad_in_part, gain_one = rms_backward(inputs, gain_full[0], grad_normed)
    grad_tokens = (grad_middle + grad_in_part).astype(BF16)

    gain_term = jnp.stack([gain_one, gain_two, gain_three, gain_four], axis=0)
    gain_term = gain_term.reshape(4, peers, share).transpose(1, 0, 2)
    gain_term = jnp.pad(gain_term, ((0, 0), (0, 8 - 4), (0, -share % 128)))
    gain_recv = collect_gains(gain_term)
    gu_term, gain_recv = lax.optimization_barrier((gu_term, gain_recv))
    gu_rows = collect(gu_term, 2, 13)
    grad_mlp = jnp.concatenate([gu_rows, down_rows], axis=1).astype(F32)
    grad_mlp, attn_term = lax.optimization_barrier((grad_mlp, attn_term))
    grad_attn = collect_attn(attn_term).astype(F32)
    grad_gains = jnp.sum(gain_recv[:, :4, :share], axis=0)
    return (layer_output, grad_tokens, grad_attn, grad_mlp, grad_gains)


def solution(mesh):
    return jax.shard_map(
        local,
        mesh=mesh,
        in_specs=(
            P("fsdp", None),
            P("fsdp", None),
            P("fsdp", None),
            P(None, "fsdp"),
            P(),
            P("fsdp", None),
        ),
        out_specs=(
            P("fsdp", None),
            P("fsdp", None),
            P("fsdp", None),
            P("fsdp", None),
            P(None, "fsdp"),
        ),
        check_vma=False,
    )
```

```python
from functools import partial

import jax
import jax.numpy as jnp
from jax import lax
from jax.experimental import pallas as pl
from jax.experimental.pallas import tpu as pltpu
from jax.sharding import PartitionSpec as P

H = 8
KVH = 4
HD = 256
LMAX = 1024
PLANE = 8
QBLK = 128

EPSILON = 1e-06
SOFT_CAP = 50.0
AXIS = "fsdp"
F32 = jnp.float32
BF16 = jnp.bfloat16
MESH = pl.DeviceIdType.MESH
ANY = pl.BlockSpec(memory_space=pl.ANY)
VMEM = pl.BlockSpec(memory_space=pltpu.VMEM)
DMA = pltpu.SemaphoreType.DMA


def flip(index, step):
    return index + step - 2 * step * ((index // step) % 2)


PLANE_STEP = 4


def partner(index, bits, step):
    for bit, by in ((1, 1), (2, 2), (4, step)):
        if bits & bit:
            index = flip(index, by)
    return index


def place(device, step):
    return device % 4 + 4 * ((device // step) % 2)


def greet(peers):
    barrier = pltpu.get_barrier_semaphore()
    for peer in peers:
        pl.semaphore_signal(barrier, inc=1, device_id=(peer,), device_id_type=MESH)
    pl.semaphore_wait(barrier, len(peers))


class Copies:
    def __init__(self, send_sem, recv_sem):
        self.send_sem, self.recv_sem, self.made = send_sem, recv_sem, []

    def start(self, source, target, device):
        slot = len(self.made)
        copy = pltpu.make_async_remote_copy(
            src_ref=source,
            dst_ref=target,
            send_sem=self.send_sem.at[slot],
            recv_sem=self.recv_sem.at[slot],
            device_id=(device,),
            device_id_type=MESH,
        )
        copy.start()
        self.made.append(copy)
        return copy

    def sent(self):
        for copy in self.made:
            copy.wait_send()


def band(index, size):
    return pl.ds(pl.multiple_of(index * size, 8), size)


def lanes(index, size):
    return pl.ds(pl.multiple_of(index * size, 128), size)


def gather_steps(block_ref, full_ref, copies, own_sem, step):
    rows, width = block_ref.shape
    half = width // 2
    me = lax.axis_index(AXIS)
    sib, xn, yn = flip(me, 1), flip(me, 2), flip(me, step)
    diag = flip(xn, step)

    def at(device, side):
        return full_ref.at[band(place(device, step), rows), pl.ds(side * half, half)]

    def mine(side):
        return block_ref.at[:, pl.ds(side * half, half)]

    own_rows = full_ref.at[band(place(me, step), rows)]
    xa = copies.start(mine(0), at(me, 0), xn)
    ya = copies.start(mine(1), at(me, 1), yn)
    xb = copies.start(mine(1), at(me, 1), xn)
    yb = copies.start(mine(0), at(me, 0), yn)
    arriving = [copies.start(block_ref, own_rows, sib)]
    own = pltpu.make_async_copy(block_ref, own_rows, own_sem)
    own.start()

    def finish(on_rows=None):
        def to_sibling(device, side):
            arriving.append(copies.start(at(device, side), at(device, side), sib))

        def arrived(first, last, *devices):
            for copy in arriving[first:last]:
                copy.wait_recv()
            for device in devices:
                on_rows(device)

        if on_rows is not None:
            own.wait()
            arrived(0, 1, me)
        xa.wait_recv()
        yc = copies.start(at(xn, 0), at(xn, 0), yn)
        to_sibling(xn, 0)
        ya.wait_recv()
        xc = copies.start(at(yn, 1), at(yn, 1), xn)
        to_sibling(yn, 1)
        xb.wait_recv()
        to_sibling(xn, 1)
        yb.wait_recv()
        to_sibling(yn, 0)
        if on_rows is not None:
            arrived(1, 5, xn, yn)
        yc.wait_recv()
        to_sibling(diag, 0)
        xc.wait_recv()
        to_sibling(diag, 1)
        if on_rows is not None:
            arrived(5, 7, diag)
        else:
            arrived(0, 7)
            own.wait()

    return finish


GATHER_COPIES = 13


def cost(microseconds):
    return pl.CostEstimate(
        flops=int(microseconds * 1e7), transcendentals=0, bytes_accessed=int(microseconds * 3e4)
    )


def gather_kernel(block_ref, full_ref, own_sem, send_sem, recv_sem, *, step):
    me = lax.axis_index(AXIS)
    greet((flip(me, 1), flip(me, 2), flip(me, step)))
    copies = Copies(send_sem, recv_sem)
    gather_steps(block_ref, full_ref, copies, own_sem, step)()
    copies.sent()


def gather_square(block, step, collective_id):
    rows, width = block.shape
    return pl.pallas_call(
        partial(gather_kernel, step=step),
        out_shape=jax.ShapeDtypeStruct((PLANE * rows, width), block.dtype),
        in_specs=[ANY],
        out_specs=ANY,
        scratch_shapes=[DMA(()), DMA((GATHER_COPIES,)), DMA((GATHER_COPIES,))],
        compiler_params=pltpu.CompilerParams(collective_id=collective_id, has_side_effects=True),
        cost_estimate=cost(42),
        name="gather_square",
    )(block)


W_TILES = 2
SCATTER_COPIES = 14


def split_columns(width):
    left = (width // 2 + 127) // 128 * 128
    return pl.ds(0, left), pl.ds(left, width - left)


def product_scatter_steps(
    left_refs, right_refs, left_bufs, right_bufs, buffers, load_sem, copies, offsets, step, beside=None
):
    both, got, ra, rb, ra2, rb2 = buffers
    pairs = len(left_refs)
    rows, width = got.shape[1:]
    sides = split_columns(width)
    chunk = 48
    me = lax.axis_index(AXIS)
    core = me % 2
    sib, xn, yn = flip(me, 1), flip(me, 2), flip(me, step)
    order = (flip(xn, step), xn, yn, me)
    first, second = sides

    def chip_rows(device):
        return pl.ds(pl.multiple_of((place(device, step) // 2) * 2 * rows, 16), 2 * rows)

    def right_load(j, t):
        r = sides[t]
        source = right_refs[j].at[r, pl.ds(offsets[j], right_bufs[j].shape[1])]
        return pltpu.make_async_copy(source, right_bufs[j].at[r], load_sem.at[j, t])

    def left_load(j, i):
        r = chip_rows(order[i])
        return pltpu.make_async_copy(
            left_refs[j].at[r], left_bufs[j].at[r], load_sem.at[j, W_TILES + i]
        )

    for j in range(pairs):
        left_load(j, 0).start()
    for t in range(W_TILES):
        for j in range(pairs):
            right_load(j, t).start()
    for i in range(1, 4):
        for j in range(pairs):
            left_load(j, i).start()
    if beside is not None:
        beside[0]()
    greet((sib, xn, yn))

    def mine(i, cols):
        return both.at[i, band(core, rows), cols]

    def add(total, other):
        @pl.loop(0, rows // chunk)
        def _(k):
            r = pl.ds(pl.multiple_of(k * chunk, chunk), chunk)
            total[r] = (total[r].astype(F32) + other[r].astype(F32)).astype(total.dtype)

    loaded = set()

    def make(i, side):
        for j in range(pairs):
            if i not in loaded:
                left_load(j, i).wait()
            if i == 0:
                right_load(j, side).wait()
        loaded.add(i)
        r, cols = chip_rows(order[i]), sides[side]
        total = None
        for j in range(pairs):
            term = contract_last(left_bufs[j][r], right_bufs[j][cols])
            total = term if total is None else total + term
        both[i, :, cols] = total.astype(BF16)
        return copies.start(both.at[i, band(1 - core, rows), cols], got.at[i, :, cols], sib)

    def merge(crossing, i, side):
        cols = sides[side]
        crossing.wait_recv()
        add(mine(i, cols), got.at[i, :, cols])

    c0 = make(0, 0)
    c1 = make(0, 1)
    merge(c0, 0, 0)
    x0 = copies.start(mine(0, first), ra.at[0], xn)
    c2 = make(1, 0)
    merge(c1, 0, 1)
    y0 = copies.start(mine(0, second), rb.at[0], yn)
    c3 = make(2, 1)
    merge(c2, 1, 0)
    x1 = copies.start(mine(1, first), ra.at[1], xn)
    c4 = make(2, 0)
    merge(c3, 2, 1)
    y1 = copies.start(mine(2, second), rb.at[1], yn)
    c5 = make(1, 1)
    merge(c4, 2, 0)
    x0.wait_recv()
    add(mine(2, first), ra.at[0])
    y2 = copies.start(mine(2, first), ra2, yn)
    c6 = make(3, 0)
    merge(c5, 1, 1)
    y0.wait_recv()
    add(mine(1, second), rb.at[0])
    x2 = copies.start(mine(1, second), rb2, xn)
    c7 = make(3, 1)
    merge(c6, 3, 0)
    merge(c7, 3, 1)
    if beside is not None:
        beside[1]()
    for copy in (x1, y1, y2, x2):
        copy.wait_recv()
    own = both.at[3, band(core, rows)]

    def summed(r):
        return jnp.concatenate(
            [
                own[r, first].astype(F32) + ra[1, r].astype(F32) + ra2[r].astype(F32),
                own[r, second].astype(F32) + rb[1, r].astype(F32) + rb2[r].astype(F32),
            ],
            axis=1,
        )

    return summed


ROW_CHUNK = 48


def product_scatter_kernel(*refs, pairs, offsets, step):
    left_refs, right_refs, out_ref = refs[:pairs], refs[pairs : 2 * pairs], refs[2 * pairs]
    left_bufs = refs[2 * pairs + 1 : 3 * pairs + 1]
    right_bufs = refs[3 * pairs + 1 : 4 * pairs + 1]
    buffers, (load_sem, send_sem, recv_sem) = refs[4 * pairs + 1 : -3], refs[-3:]
    copies = Copies(send_sem, recv_sem)
    summed = product_scatter_steps(
        left_refs, right_refs, left_bufs, right_bufs, buffers, load_sem, copies, offsets, step
    )

    @pl.loop(0, out_ref.shape[0] // ROW_CHUNK)
    def _(k):
        r = pl.ds(pl.multiple_of(k * ROW_CHUNK, ROW_CHUNK), ROW_CHUNK)
        out_ref[r] = summed(r)

    copies.sent()


def scatter_buffers(rows, width):
    left, right = [side.size for side in split_columns(width)]
    return [
        pltpu.VMEM((4, 2 * rows, width), BF16),
        pltpu.VMEM((4, rows, width), BF16),
        pltpu.VMEM((2, rows, left), BF16),
        pltpu.VMEM((2, rows, right), BF16),
        pltpu.VMEM((rows, left), BF16),
        pltpu.VMEM((rows, right), BF16),
    ]


def product_scatter(lefts, rights, offsets, step, collective_id):
    pairs = len(lefts)
    rows, width = lefts[0].shape[0] // PLANE, rights[0].shape[0]
    return pl.pallas_call(
        partial(product_scatter_kernel, pairs=pairs, offsets=offsets, step=step),
        out_shape=jax.ShapeDtypeStruct((rows, width), F32),
        in_specs=[ANY] * (2 * pairs),
        out_specs=VMEM,
        scratch_shapes=[
            *[pltpu.VMEM(value.shape, BF16) for value in lefts],
            *[pltpu.VMEM((width, value.shape[1]), BF16) for value in lefts],
            *scatter_buffers(rows, width),
            DMA((pairs, W_TILES + 4)),
            DMA((SCATTER_COPIES,)),
            DMA((SCATTER_COPIES,)),
        ],
        compiler_params=pltpu.CompilerParams(
            collective_id=collective_id, has_side_effects=True, vmem_limit_bytes=56 << 20
        ),
        cost_estimate=cost(50),
        name="product_scatter",
    )(*lefts, *rights)


BACK_TILE = 384


def back_kernel(*refs, pairs, offsets, step):
    left_refs, right_refs, rows_ref = refs[:pairs], refs[pairs : 2 * pairs], refs[2 * pairs]
    out_ref, term_ref = refs[2 * pairs + 1 : 2 * pairs + 3]
    scratch = refs[2 * pairs + 3 :]
    left_bufs, right_bufs = scratch[:pairs], scratch[pairs : 2 * pairs]
    rows_buf, stage = scratch[2 * pairs : 2 * pairs + 2]
    buffers = scratch[2 * pairs + 2 : -5]
    load_sem, rows_sem, store_sem, send_sem, recv_sem = scratch[-5:]
    copies = Copies(send_sem, recv_sem)
    rows_load = pltpu.make_async_copy(rows_ref, rows_buf, rows_sem)
    tiles = rows_ref.shape[1] // BACK_TILE
    width = left_refs[0].shape[1]

    def store(t):
        return pltpu.make_async_copy(
            stage.at[t % 2],
            term_ref.at[pl.ds(pl.multiple_of(t * BACK_TILE, 16), BACK_TILE)],
            store_sem.at[t % 2],
        )

    def beside():
        rows_load.wait()

        @pl.loop(0, tiles)
        def _(t):
            @pl.when(t >= 2)
            def _():
                store(t - 2).wait()

            columns = rows_buf[:, pl.ds(pl.multiple_of(t * BACK_TILE, BACK_TILE), BACK_TILE)]
            for j in range(pairs):
                term = contract_first(columns, left_bufs[j][...])
                stage[t % 2, :, pl.ds(j * width, width)] = term.astype(BF16)
            store(t).start()

    def start_rows():
        rows_load.start()

    summed = product_scatter_steps(
        left_refs,
        right_refs,
        left_bufs,
        right_bufs,
        buffers,
        load_sem,
        copies,
        offsets,
        step,
        (start_rows, beside),
    )

    @pl.loop(0, out_ref.shape[0] // ROW_CHUNK)
    def _(k):
        r = pl.ds(pl.multiple_of(k * ROW_CHUNK, ROW_CHUNK), ROW_CHUNK)
        out_ref[r] = summed(r)

    for t in range(tiles - 2, tiles):
        store(t).wait()
    copies.sent()


def product_scatter_back(lefts, rights, offsets, rows, step, collective_id):
    pairs = len(lefts)
    count, width = lefts[0].shape[0] // PLANE, rights[0].shape[0]
    columns = sum(value.shape[1] for value in lefts)
    return pl.pallas_call(
        partial(back_kernel, pairs=pairs, offsets=offsets, step=step),
        out_shape=(
            jax.ShapeDtypeStruct((count, width), F32),
            jax.ShapeDtypeStruct((rows.shape[1], columns), BF16),
        ),
        in_specs=[ANY] * (2 * pairs + 1),
        out_specs=(VMEM, ANY),
        scratch_shapes=[
            *[pltpu.VMEM(value.shape, BF16) for value in lefts],
            *[pltpu.VMEM((width, value.shape[1]), BF16) for value in lefts],
            pltpu.VMEM(rows.shape, BF16),
            pltpu.VMEM((2, BACK_TILE, columns), BF16),
            *scatter_buffers(count, width),
            DMA((pairs, W_TILES + 4)),
            DMA(()),
            DMA((2,)),
            DMA((SCATTER_COPIES,)),
            DMA((SCATTER_COPIES,)),
        ],
        compiler_params=pltpu.CompilerParams(
            collective_id=collective_id, has_side_effects=True, vmem_limit_bytes=62 << 20
        ),
        cost_estimate=cost(60),
        name="product_scatter_back",
    )(*lefts, *rights, rows)


TURN_TILE = 768


def in_place(rows):
    return rows % 16 == 0


def turn_kernel(
    left_ref,
    right_ref,
    near_ref,
    gain_ref,
    grad_ref,
    raw_ref,
    full_ref,
    term_ref,
    *refs,
    planes,
    step,
):
    left_buf, right_buf, gathered, total, grad_own, stage = refs[:6]
    buffers, (load_sem, own_sem, store_sem, send_sem, recv_sem) = refs[6:-5], refs[-5:]
    rows, width = grad_ref.shape
    half = width // 2
    piece = half // planes
    copies = Copies(send_sem, recv_sem)
    summed = product_scatter_steps(
        [left_ref], [right_ref], [left_buf], [right_buf], buffers, load_sem, copies, [0], step
    )
    gain = gain_ref[...]

    @pl.loop(0, rows // ROW_CHUNK)
    def _(k):
        r = pl.ds(pl.multiple_of(k * ROW_CHUNK, ROW_CHUNK), ROW_CHUNK)
        far = summed(r)
        raw_ref[r] = far
        value = jnp.concatenate([near_ref[r], far], axis=1)
        scale = lax.rsqrt(jnp.mean(value * value, axis=1, keepdims=True) + EPSILON)
        scaled = (1.0 + gain) * grad_ref[r].astype(F32)
        inner = jnp.mean(value * scaled, axis=1, keepdims=True)
        grad_own[r] = (scale * scaled - value * (scale * scale * scale * inner)).astype(BF16)

    stores = []

    def store_term(side):
        for plane in range(planes):
            start = side * half + plane * piece
            target = plane * 2 * piece + side * piece if in_place(piece) else start
            pltpu.make_async_copy(
                stage.at[pl.ds(start, piece)] if in_place(piece) else stage.at[pl.ds(side * half, half)],
                term_ref.at[pl.ds(target, piece)]
                if in_place(piece)
                else term_ref.at[pl.ds(side * half, half)],
                store_sem.at[4],
            ).start()
            if not in_place(piece):
                break

    def on_rows(device):
        slot = len(stores)
        r = pl.ds(pl.multiple_of((place(device, step) // 2) * 2 * rows, 16), 2 * rows)
        store = pltpu.make_async_copy(gathered.at[r], full_ref.at[r], store_sem.at[slot])
        store.start()
        stores.append(store)
        right = left_buf[r]
        if slot < 3:

            @pl.loop(0, width // TURN_TILE)
            def _(t):
                w = pl.ds(pl.multiple_of(t * TURN_TILE, TURN_TILE), TURN_TILE)
                term = contract_first(gathered[r, w], right)
                if slot == 0:
                    total[w] = term
                else:
                    total[w] += term
        else:
            for side in range(2):

                w = pl.ds(side * half, half)
                stage[w] = (total[w] + contract_first(gathered[r, w], right)).astype(BF16)
                store_term(side)

    gather_steps(grad_own, gathered, copies, own_sem, step)(on_rows)
    pltpu.make_async_copy(stage, term_ref, store_sem.at[4]).wait()
    for store in stores:
        store.wait()
    copies.sent()


def turn(left, right, near, gain_row, grad, planes, step, collective_id):
    rows, width = grad.shape
    count = SCATTER_COPIES + GATHER_COPIES
    return pl.pallas_call(
        partial(turn_kernel, planes=planes, step=step),
        out_shape=(
            jax.ShapeDtypeStruct((rows, width // 2), F32),
            jax.ShapeDtypeStruct((PLANE * rows, width), BF16),
            jax.ShapeDtypeStruct((width, left.shape[1]), BF16),
        ),
        in_specs=[ANY, ANY, VMEM, VMEM, VMEM],
        out_specs=(VMEM, ANY, ANY),
        scratch_shapes=[
            pltpu.VMEM(left.shape, BF16),
            pltpu.VMEM(right.shape, BF16),
            pltpu.VMEM((PLANE * rows, width), BF16),
            pltpu.VMEM((width, left.shape[1]), F32),
            pltpu.VMEM((rows, width), BF16),
            pltpu.VMEM((width, left.shape[1]), BF16),
            *scatter_buffers(rows, width // 2),
            DMA((1, W_TILES + 4)),
            DMA(()),
            DMA((5,)),
            DMA((count,)),
            DMA((count,)),
        ],
        compiler_params=pltpu.CompilerParams(
            collective_id=collective_id, has_side_effects=True, vmem_limit_bytes=60 << 20
        ),
        cost_estimate=cost(50),
        name="turn",
    )(left, right, near, gain_row, grad)


def attn_columns(column):
    query_width = H * HD
    key_offset = query_width + (column % 2) * KVH * HD + (column // 2) * HD
    return (column * HD, key_offset, query_width + 2 * KVH * HD + column * HD)


def greet_all(peers):
    me = lax.axis_index(AXIS)
    barrier = pltpu.get_barrier_semaphore()

    @pl.loop(1, peers)
    def _(k):
        device = lax.rem(me + k, peers)
        pl.semaphore_signal(barrier, inc=1, device_id=(device,), device_id_type=MESH)

    pl.semaphore_wait(barrier, peers - 1)


def exchange_all(source_of, target_ref, send_sem, recv_sem):
    peers = target_ref.shape[0]
    me = lax.axis_index(AXIS)

    def copy(k):
        device = lax.rem(me + k, peers)
        return pltpu.make_async_remote_copy(
            src_ref=source_of(device),
            dst_ref=target_ref.at[me],
            send_sem=send_sem.at[k],
            recv_sem=recv_sem.at[k],
            device_id=(device,),
            device_id_type=MESH,
        )

    @pl.loop(1, peers)
    def _(k):
        copy(k).start()

    def finish():
        @pl.loop(1, peers)
        def _(k):
            copy(k).wait()

    return finish


ORDER = (6, 7, 2, 3, 4, 5, 1)


def swap_steps(pieces_of, targets, copies, own_sem, step):
    me = lax.axis_index(AXIS)
    moved = []
    for bits in ORDER:
        peer = partner(me, bits, step)
        for source, target in zip(pieces_of(place(peer, step)), targets):
            moved.append(copies.start(source, target, peer))
    owns = []
    for slot, (source, target) in enumerate(zip(pieces_of(place(me, step)), targets)):
        own = pltpu.make_async_copy(source, target, own_sem.at[slot])
        own.start()
        owns.append(own)

    def finish():
        for own in owns:
            own.wait()
        for copy in moved:
            copy.wait_recv()

    return finish


def square(step):
    me = lax.axis_index(AXIS)
    return [partner(me, bits, step) for bits in ORDER]


def wide(offset):
    return pl.ds(pl.multiple_of(offset, 128), HD)


class Line:
    def __init__(self, full_ref, send_sem, recv_sem, own_ref=None):
        me = lax.axis_index(AXIS)
        self.own = own_ref
        self.full, self.planes = full_ref, full_ref.shape[0]
        self.send_sem, self.recv_sem = send_sem, recv_sem
        self.plane = me // PLANE
        peers = self.planes * PLANE
        self.devices = (lax.rem(me + PLANE, peers), lax.rem(me + peers - PLANE, peers))

    def copy(self, way, slot, source, first=False):
        return pltpu.make_async_remote_copy(
            src_ref=self.own if first and self.own is not None else self.full.at[source],
            dst_ref=self.full.at[source],
            send_sem=self.send_sem.at[way, slot],
            recv_sem=self.recv_sem.at[way, slot],
            device_id=(self.devices[way],),
            device_id_type=MESH,
        )

    def sends(self, way, hop):
        if way == 0:
            source = self.plane - (hop - 1)
            return (self.plane + 1 < self.planes) & (source >= 0), source
        source = self.plane + (hop - 1)
        return (self.plane >= 1) & (source < self.planes), source

    def greet(self):
        barrier = pltpu.get_barrier_semaphore()
        count = 0
        for way, there in enumerate((self.plane + 1 < self.planes, self.plane >= 1)):

            @pl.when(there)
            def _():
                pl.semaphore_signal(
                    barrier, inc=1, device_id=(self.devices[way],), device_id_type=MESH
                )

            count = count + there.astype(jnp.int32)
        return count

    def start(self, hop, slot):
        for way in range(2):
            there, source = self.sends(way, hop)

            @pl.when(there)
            def _():
                self.copy(way, slot, source, hop == 1).start()

    def arrived(self, hop, slot):
        for way in range(2):
            source = self.plane - hop if way == 0 else self.plane + hop

            @pl.when((source >= 0) & (source < self.planes))
            def _():
                self.copy(way, slot, source).wait_recv()

    def sent(self, hop, slot):
        for way in range(2):
            there, source = self.sends(way, hop)

            @pl.when(there)
            def _():
                self.copy(way, slot, source, hop == 1).wait_send()

    def begin(self, hops):
        if hops:
            self.start(hops[0], 0)

    def run(self, hops):
        for slot, hop in enumerate(hops):
            self.arrived(hop, slot)
            if slot + 1 < len(hops):
                self.start(hop + 1, slot + 1)

    def end(self, hops):
        for slot, hop in enumerate(hops):
            self.sent(hop, slot)


def line_hops(planes):
    hops = list(range(1, planes))
    first = (2 * len(hops) + 2) // 3
    return hops[:first], hops[first:]


def line_semaphores(hops):
    count = max(1, len(hops))
    return [DMA((2, count)), DMA((2, count))]


def greet_line(line, peers):
    barrier = pltpu.get_barrier_semaphore()
    for peer in peers:
        pl.semaphore_signal(barrier, inc=1, device_id=(peer,), device_id_type=MESH)
    pl.semaphore_wait(barrier, len(peers) + line.greet())


def row_bands(weights_ref):
    return [weights_ref.at[:, pl.ds(start * HD, H * HD)] for start in (0, H + 2 * KVH)]


def spread_attn_kernel(
    weights_ref,
    gain_ref,
    kv_ref,
    q_ref,
    out_ref,
    gains_ref,
    own_sem,
    send_sem,
    recv_sem,
    gain_send,
    gain_recv,
    *sems,
):
    me = lax.axis_index(AXIS)
    plane, here = me // PLANE, place(me, PLANE_STEP)
    q_rows, out_rows = row_bands(weights_ref)
    q_line = Line(q_ref, sems[0], sems[1], q_rows)
    out_line = Line(out_ref, sems[2], sems[3], out_rows)
    hops = line_hops(out_line.planes)[0]
    greet_all(gains_ref.shape[0])
    out_line.begin(hops)
    q_line.begin([1])
    gains_done = exchange_all(lambda device: gain_ref, gains_ref, gain_send, gain_recv)
    owns = [pltpu.make_async_copy(gain_ref, gains_ref.at[me], own_sem.at[3])]
    owns[0].start()
    for slot, (source, target) in enumerate(((q_rows, q_ref), (out_rows, out_ref))):
        own = pltpu.make_async_copy(source, target.at[plane], own_sem.at[1 + slot])
        own.start()
        owns.append(own)
    copies = Copies(send_sem, recv_sem)
    spread = swap_steps(
        lambda c: [weights_ref.at[:, wide(attn_columns(c)[1])]],
        [kv_ref.at[plane, here]],
        copies,
        own_sem,
        PLANE_STEP,
    )
    out_line.run(hops)
    q_line.run([1])
    spread()
    for own in owns:
        own.wait()
    gains_done()
    out_line.end(hops)
    q_line.end([1])
    copies.sent()


def spread_attn(weights, gain_block, planes):
    rows = weights.shape[0]
    peers = planes * PLANE
    return pl.pallas_call(
        spread_attn_kernel,
        out_shape=(
            jax.ShapeDtypeStruct((planes, PLANE, rows, HD), BF16),
            jax.ShapeDtypeStruct((planes, rows, H * HD), BF16),
            jax.ShapeDtypeStruct((planes, rows, H * HD), BF16),
            jax.ShapeDtypeStruct((peers,) + gain_block.shape, gain_block.dtype),
        ),
        in_specs=[ANY, ANY],
        out_specs=(ANY,) * 4,
        scratch_shapes=[
            DMA((4,)),
            DMA((7,)),
            DMA((7,)),
            DMA((peers,)),
            DMA((peers,)),
            *line_semaphores([1]),
            *line_semaphores(line_hops(planes)[0]),
        ],
        compiler_params=pltpu.CompilerParams(collective_id=3, has_side_effects=True),
        name="spread_attn",
    )(weights, gain_block)


def spread_gu_kernel(
    weights_ref,
    kv_in,
    q_in,
    out_in,
    gu_ref,
    kv_ref,
    q_ref,
    out_ref,
    own_sem,
    send_sem,
    recv_sem,
    *sems,
):
    ffc = gu_ref.shape[2] // 2
    me = lax.axis_index(AXIS)
    here = place(me, PLANE_STEP)
    kv_line = Line(kv_ref, sems[0], sems[1])
    q_line = Line(q_ref, sems[2], sems[3])
    out_line = Line(out_ref, sems[4], sems[5])
    kv_hops, out_hops = line_hops(kv_line.planes)
    q_hops = list(range(2, kv_line.planes))
    greet_line(kv_line, square(PLANE_STEP))
    q_line.begin(q_hops)
    out_line.begin(out_hops)
    kv_line.begin(kv_hops)
    copies = Copies(send_sem, recv_sem)
    spread = swap_steps(
        lambda c: [weights_ref.at[:, lanes(slot * PLANE + c, ffc)] for slot in range(2)],
        [gu_ref.at[here, :, pl.ds(slot * ffc, ffc)] for slot in range(2)],
        copies,
        own_sem,
        PLANE_STEP,
    )
    q_line.run(q_hops)
    out_line.run(out_hops)
    kv_line.run(kv_hops)
    spread()
    for line, hops in ((q_line, q_hops), (out_line, out_hops), (kv_line, kv_hops)):
        line.end(hops)
    copies.sent()


def spread_gu(weights, kv_full, q_rows, out_rows):
    rows = weights.shape[0]
    ffc = weights.shape[1] // 3 // PLANE
    planes = kv_full.shape[0]
    kv_hops, out_hops = line_hops(planes)
    return pl.pallas_call(
        spread_gu_kernel,
        out_shape=(
            jax.ShapeDtypeStruct((PLANE, rows, 2 * ffc), BF16),
            jax.ShapeDtypeStruct(kv_full.shape, kv_full.dtype),
            jax.ShapeDtypeStruct(q_rows.shape, q_rows.dtype),
            jax.ShapeDtypeStruct(out_rows.shape, out_rows.dtype),
        ),
        in_specs=[ANY] * 4,
        out_specs=(ANY,) * 4,
        scratch_shapes=[
            DMA((2,)),
            DMA((14,)),
            DMA((14,)),
            *line_semaphores(kv_hops),
            *line_semaphores(range(2, planes)),
            *line_semaphores(out_hops),
        ],
        input_output_aliases={1: 1, 2: 2, 3: 3},
        compiler_params=pltpu.CompilerParams(collective_id=4, has_side_effects=True),
        cost_estimate=cost(38),
        name="spread_gu",
    )(weights, kv_full, q_rows, out_rows)


def spread_down_kernel(
    weights_ref,
    block_ref,
    kv_in,
    rows_ref,
    down_ref,
    full_ref,
    kv_ref,
    q_ref,
    own_sem,
    send_sem,
    recv_sem,
    line_send,
    line_recv,
):
    ffc = down_ref.shape[2]
    here = place(lax.axis_index(AXIS), PLANE_STEP)
    line = Line(kv_ref, line_send, line_recv)
    hops = line_hops(line.planes)[1]
    greet_line(line, square(PLANE_STEP))
    line.begin(hops)
    copies = Copies(send_sem, recv_sem)
    gathered = gather_steps(block_ref, full_ref, copies, own_sem.at[2], PLANE_STEP)
    spread = swap_steps(
        lambda c: [
            rows_ref.at[:, :, lanes(c, HD)],
            weights_ref.at[:, lanes(2 * PLANE + c, ffc)],
        ],
        [q_ref.at[:, here], down_ref.at[here]],
        copies,
        own_sem,
        PLANE_STEP,
    )
    gathered()
    line.run(hops)
    spread()
    line.end(hops)
    copies.sent()


def spread_down(weights, block, kv_full, q_rows):
    rows = weights.shape[0]
    ffc = weights.shape[1] // 3 // PLANE
    planes = kv_full.shape[0]
    count = GATHER_COPIES + 14
    return pl.pallas_call(
        spread_down_kernel,
        out_shape=(
            jax.ShapeDtypeStruct((PLANE, rows, ffc), BF16),
            jax.ShapeDtypeStruct((PLANE * block.shape[0], block.shape[1]), BF16),
            jax.ShapeDtypeStruct(kv_full.shape, kv_full.dtype),
            jax.ShapeDtypeStruct((planes, PLANE, rows, HD), BF16),
        ),
        in_specs=[ANY] * 4,
        out_specs=(ANY,) * 4,
        scratch_shapes=[
            DMA((3,)),
            DMA((count,)),
            DMA((count,)),
            *line_semaphores(line_hops(planes)[1]),
        ],
        input_output_aliases={2: 2},
        compiler_params=pltpu.CompilerParams(collective_id=5, has_side_effects=True),
        cost_estimate=cost(1),
        name="spread_down",
    )(weights, block, kv_full, q_rows)


def spread_out_kernel(rows_ref, full_ref, own_sem, send_sem, recv_sem):
    here = place(lax.axis_index(AXIS), PLANE_STEP)
    greet(square(PLANE_STEP))
    copies = Copies(send_sem, recv_sem)
    swap_steps(
        lambda c: [rows_ref.at[:, :, lanes(c, HD)]],
        [full_ref.at[:, here]],
        copies,
        own_sem,
        PLANE_STEP,
    )()
    copies.sent()


def spread_out(out_rows):
    planes, rows = out_rows.shape[:2]
    return pl.pallas_call(
        spread_out_kernel,
        out_shape=jax.ShapeDtypeStruct((planes, PLANE, rows, HD), BF16),
        in_specs=[ANY],
        out_specs=ANY,
        scratch_shapes=[DMA((1,)), DMA((7,)), DMA((7,))],
        compiler_params=pltpu.CompilerParams(collective_id=11, has_side_effects=True),
        cost_estimate=cost(0.1),
        name="spread_out",
    )(out_rows)


def collect_kernel(term_ref, rows_ref, own_sem, send_sem, recv_sem):
    here = place(lax.axis_index(AXIS), PLANE_STEP)
    count = own_sem.shape[0]
    ffc = term_ref.shape[2] // count
    greet(square(PLANE_STEP))
    copies = Copies(send_sem, recv_sem)
    swap_steps(
        lambda c: [term_ref.at[c, :, pl.ds(slot * ffc, ffc)] for slot in range(count)],
        [rows_ref.at[:, lanes(slot * PLANE + here, ffc)] for slot in range(count)],
        copies,
        own_sem,
        PLANE_STEP,
    )()
    copies.sent()


def collect(term, count, collective_id):
    rows, columns = term.shape[1:]
    return pl.pallas_call(
        collect_kernel,
        out_shape=jax.ShapeDtypeStruct((rows, PLANE * columns), BF16),
        in_specs=[ANY],
        out_specs=ANY,
        scratch_shapes=[DMA((count,)), DMA((7 * count,)), DMA((7 * count,))],
        compiler_params=pltpu.CompilerParams(collective_id=collective_id, has_side_effects=True),
        cost_estimate=cost(0.1),
        name="collect",
    )(term)


def collect_attn_kernel(term_ref, rows_ref, own_sem, send_sem, recv_sem):
    here = place(lax.axis_index(AXIS), PLANE_STEP)
    greet(square(PLANE_STEP))
    copies = Copies(send_sem, recv_sem)
    swap_steps(
        lambda c: [term_ref.at[c, :, pl.ds(slot * HD, HD)] for slot in range(3)],
        [rows_ref.at[:, wide(offset)] for offset in attn_columns(here)],
        copies,
        own_sem,
        PLANE_STEP,
    )()
    copies.sent()


def collect_attn(term):
    rows = term.shape[1]
    return pl.pallas_call(
        collect_attn_kernel,
        out_shape=jax.ShapeDtypeStruct((rows, PLANE * 3 * HD), BF16),
        in_specs=[ANY],
        out_specs=ANY,
        scratch_shapes=[DMA((3,)), DMA((21,)), DMA((21,))],
        compiler_params=pltpu.CompilerParams(collective_id=7, has_side_effects=True),
        name="collect_attn",
    )(term)


def collect_gains_kernel(gain_ref, gains_ref, own_sem, gain_send, gain_recv):
    me = lax.axis_index(AXIS)
    greet_all(gain_ref.shape[0])
    done = exchange_all(lambda device: gain_ref.at[device], gains_ref, gain_send, gain_recv)
    own = pltpu.make_async_copy(gain_ref.at[me], gains_ref.at[me], own_sem)
    own.start()
    own.wait()
    done()


def collect_gains(gain_blocks):
    peers = gain_blocks.shape[0]
    return pl.pallas_call(
        collect_gains_kernel,
        out_shape=jax.ShapeDtypeStruct(gain_blocks.shape, gain_blocks.dtype),
        in_specs=[ANY],
        out_specs=ANY,
        scratch_shapes=[DMA(()), DMA((peers,)), DMA((peers,))],
        compiler_params=pltpu.CompilerParams(collective_id=8, has_side_effects=True),
        name="collect_gains",
    )(gain_blocks)


def block_scores(q, k, start, first):
    scores = lax.dot_general(q, k, (((1,), (1,)), ((), ())), preferred_element_type=F32)
    bent = jnp.tanh(scores * (HD ** (-0.5) / SOFT_CAP))
    rows, span = scores.shape
    key_at = lax.broadcasted_iota(jnp.int32, (rows, span), 1)
    row_at = lax.broadcasted_iota(jnp.int32, (rows, span), 0)
    allowed = (key_at + first >= start) & (key_at <= row_at + LMAX)
    return (bent, jnp.where(allowed, jnp.exp(SOFT_CAP * bent), 0.0))


def attend_kernel(q_ref, k_ref, v_ref, start_ref, out_ref, inv_ref):
    first = pl.program_id(0) * QBLK
    keys = pl.ds(pl.multiple_of(first, QBLK), LMAX + QBLK)
    unused_bent, exponent = block_scores(q_ref[...], k_ref[keys], start_ref[...], first)
    inverse = 1.0 / jnp.sum(exponent, axis=-1, keepdims=True)
    weights = (exponent * inverse).astype(BF16)
    out_ref[...] = jnp.dot(weights, v_ref[keys], preferred_element_type=F32).astype(BF16)
    inv_ref[...] = inverse


def attend(queries, key_rows, value_rows, starts):
    rows = queries.shape[0]
    span = key_rows.shape[0]
    row_spec = pl.BlockSpec((QBLK, HD), lambda i: (i, 0))
    one_spec = pl.BlockSpec((QBLK, 1), lambda i: (i, 0))
    all_spec = pl.BlockSpec((span, HD), lambda i: (0, 0))
    return pl.pallas_call(
        attend_kernel,
        out_shape=(
            jax.ShapeDtypeStruct((rows, HD), BF16),
            jax.ShapeDtypeStruct((rows, 1), F32),
        ),
        grid=(rows // QBLK,),
        in_specs=[row_spec, all_spec, all_spec, one_spec],
        out_specs=(row_spec, one_spec),
        compiler_params=pltpu.CompilerParams(vmem_limit_bytes=40 << 20),
        cost_estimate=cost(1),
        name="attend",
    )(queries, key_rows, value_rows, starts)


GRAD_TILE = 384


def attn_grad_kernel(rows_ref, q_ref, kv_ref, proj_ref, attended_ref, out_ref):
    for slot, (left, right) in enumerate(
        ((rows_ref, q_ref), (rows_ref, kv_ref), (proj_ref, attended_ref))
    ):
        out_ref[:, pl.ds(slot * HD, HD)] = contract_first(left[...], right[...]).astype(BF16)


def attn_grad(rows, grad_q, grad_kv, grad_proj, attended):
    count, width = rows.shape
    tile = pl.BlockSpec((count, GRAD_TILE), lambda i: (0, i))
    whole = pl.BlockSpec((count, HD), lambda i: (0, 0))
    return pl.pallas_call(
        attn_grad_kernel,
        out_shape=jax.ShapeDtypeStruct((width, 3 * HD), BF16),
        grid=(width // GRAD_TILE,),
        in_specs=[tile, whole, whole, tile, whole],
        out_specs=pl.BlockSpec((GRAD_TILE, 3 * HD), lambda i: (i, 0)),
        compiler_params=pltpu.CompilerParams(vmem_limit_bytes=48 << 20),
        cost_estimate=cost(10),
        name="attn_grad",
    )(rows, grad_q, grad_kv, grad_proj, attended)


def attend_back_kernel(q_ref, k_ref, v_ref, start_ref, inv_ref, grad_ref, gq_ref, gk_ref, gv_ref):
    @pl.when(pl.program_id(0) == 0)
    def _():
        gk_ref[...] = jnp.zeros_like(gk_ref)
        gv_ref[...] = jnp.zeros_like(gv_ref)

    first = pl.program_id(0) * QBLK
    keys = pl.ds(pl.multiple_of(first, QBLK), LMAX + QBLK)
    q, k, v, grad = q_ref[...], k_ref[keys], v_ref[keys], grad_ref[...]
    bent, exponent = block_scores(q, k, start_ref[...], first)
    probability = exponent * inv_ref[...]
    grad_prob = lax.dot_general(grad, v, (((1,), (1,)), ((), ())), preferred_element_type=F32)
    inner = jnp.sum(probability * grad_prob, axis=-1, keepdims=True)
    grad_scores = (probability * (grad_prob - inner) * (1.0 - bent * bent)).astype(BF16)
    scale = HD ** (-0.5)
    gq_ref[...] = jnp.dot(grad_scores, k, preferred_element_type=F32) * scale
    over_rows = (((0,), (0,)), ((), ()))
    gk_ref[keys] += lax.dot_general(grad_scores, q, over_rows, preferred_element_type=F32) * scale
    gv_ref[keys] += lax.dot_general(
        probability.astype(BF16), grad, over_rows, preferred_element_type=F32
    )


def attend_back(queries, key_rows, value_rows, starts, inverse, grad):
    rows = queries.shape[0]
    span = key_rows.shape[0]
    row_spec = pl.BlockSpec((QBLK, HD), lambda i: (i, 0))
    one_spec = pl.BlockSpec((QBLK, 1), lambda i: (i, 0))
    all_spec = pl.BlockSpec((span, HD), lambda i: (0, 0))
    return pl.pallas_call(
        attend_back_kernel,
        out_shape=(
            jax.ShapeDtypeStruct((rows, HD), F32),
            jax.ShapeDtypeStruct((span, HD), F32),
            jax.ShapeDtypeStruct((span, HD), F32),
        ),
        grid=(rows // QBLK,),
        in_specs=[row_spec, all_spec, all_spec, one_spec, one_spec, row_spec],
        out_specs=(row_spec, all_spec, all_spec),
        compiler_params=pltpu.CompilerParams(vmem_limit_bytes=48 << 20),
        cost_estimate=cost(20),
        name="attend_back",
    )(queries, key_rows, value_rows, starts, inverse, grad)


def token_tables(seq_lengths, index_vec):
    count = seq_lengths.shape[0]
    order = jnp.arange(count, dtype=jnp.int32)
    seq_ends = jnp.sum(
        jnp.where(order[None, :] <= order[:, None], seq_lengths[None, :], 0), axis=1
    )
    after_end = index_vec[:, None] >= seq_ends[None, :]
    return index_vec - jnp.sum(jnp.where(after_end, seq_lengths[None, :], 0), axis=1)


def rms_parts(value):
    return lax.rsqrt(jnp.mean(value * value, axis=-1, keepdims=True) + EPSILON)


def rms_forward(value, gain_vec):
    return value * rms_parts(value) * (1.0 + gain_vec)


def rms_backward(value, gain_vec, grad):
    r = rms_parts(value)
    scaled = (1.0 + gain_vec) * grad
    inner = jnp.mean(value * scaled, axis=-1, keepdims=True)
    return (r * scaled - value * (r * r * r * inner), jnp.sum(grad * value * r, axis=0))


def rotate(value, cosine, sine_part):
    half_width = value.shape[-1] // 2
    first_half = value[..., :half_width]
    second_half = value[..., half_width:]
    return jnp.concatenate(
        [
            first_half * cosine - second_half * sine_part,
            second_half * cosine + first_half * sine_part,
        ],
        axis=-1,
    )


def contract_last(left_side, right_side):
    return lax.dot_general(
        left_side, right_side, (((1,), (1,)), ((), ())), preferred_element_type=F32
    )


def contract_first(left_side, right_side):
    return lax.dot_general(
        left_side, right_side, (((0,), (0,)), ((), ())), preferred_element_type=F32
    )


def matmul(left_side, right_side):
    return jnp.dot(left_side, right_side, preferred_element_type=F32)


def gelu_parts(gate):
    k0 = 0.7978845608028654
    k1 = 0.044715
    t = jnp.tanh(k0 * (gate + k1 * gate * gate * gate))
    value = 0.5 * gate * (1.0 + t)
    slope = 0.5 * (1.0 + t) + 0.5 * gate * (1.0 - t * t) * k0 * (1.0 + 3.0 * k1 * gate * gate)
    return (value, slope)


def local(tokens, attn_weights, mlp_weights, norm_gains, seq_lengths, cotangent):
    tok_rows, width = tokens.shape
    peers = lax.axis_size(AXIS)
    planes = peers // PLANE
    share = width // peers
    row_share = attn_weights.shape[0]
    ff = mlp_weights.shape[1] // 3
    ffc = ff // PLANE
    plane_rows = PLANE * tok_rows
    halo = LMAX
    across = [[p * PLANE + i for p in range(planes)] for i in range(PLANE)]
    sibling = [(i, i ^ 1) for i in range(peers)]
    to_next = [(i, i + PLANE) for i in range(peers - PLANE)]
    to_prev = [(i + PLANE, i) for i in range(peers - PLANE)]
    me = lax.axis_index(AXIS)
    is_even = (me % 2) == 0
    plane_start = (me // PLANE) * plane_rows

    def split_features(value):
        value = value.reshape(value.shape[0], planes, 2, width // planes // 2)
        return value.transpose(0, 2, 1, 3).reshape(value.shape[0], width)

    def join_features(value):
        value = value.reshape(value.shape[0], 2, planes, width // planes // 2)
        return value.transpose(0, 2, 1, 3).reshape(value.shape[0], width)

    def gather_across(value):
        return lax.all_gather(value, AXIS, axis=0, tiled=True, axis_index_groups=across)

    def scatter_across(value):
        part = lax.psum_scatter(
            value.astype(BF16), AXIS, scatter_dimension=0, tiled=True, axis_index_groups=across
        )
        return part.reshape(PLANE, -1, part.shape[1])

    gain_block = jnp.pad(norm_gains.astype(F32), ((0, 8 - 4), (0, -share % 128)))
    kv_full, q_rows, out_rows, gain_blocks = spread_attn(attn_weights, gain_block, planes)
    gu_part, kv_full, q_rows, out_rows = spread_gu(mlp_weights, kv_full, q_rows, out_rows)
    gain_full = gain_blocks[:, :4, :share].transpose(1, 0, 2).reshape(4, width)
    inputs = tokens.astype(F32)
    down_part, normed, kv_full, q_full = spread_down(
        mlp_weights, rms_forward(inputs, gain_full[0]).astype(BF16), kv_full, q_rows
    )
    q_cols, kv_cols = q_full.reshape(width, HD), kv_full.reshape(width, HD)
    gu_cols = gather_across(gu_part.reshape(-1, 2 * ffc))
    down_near = gather_across(down_part[: PLANE // 2].reshape(-1, ffc))
    down_far = gather_across(down_part[PLANE // 2 :].reshape(-1, ffc))

    query_index = plane_start + jnp.arange(plane_rows, dtype=jnp.int32)
    position = token_tables(seq_lengths, query_index)
    starts = (jnp.arange(plane_rows, dtype=jnp.int32) + halo - position)[:, None]
    frequency = 10000.0 ** (-jnp.arange(HD // 2, dtype=F32) * 2.0 / HD)
    angles = position.astype(F32)[:, None] * frequency[None, :]
    cosine, sine_part = jnp.cos(angles), jnp.sin(angles)
    kv_cosine = jnp.where(is_even, cosine, 1.0)
    kv_sine = jnp.where(is_even, sine_part, 0.0)

    kv_own = rotate(matmul(normed, kv_cols), kv_cosine, kv_sine).astype(BF16)
    kv_halo = lax.ppermute(kv_own[plane_rows - halo :], AXIS, to_next)
    kv_own, out_rows, q_cols = lax.optimization_barrier((kv_own, out_rows, q_cols))
    out_cols = spread_out(out_rows).reshape(width, HD)
    queries = rotate(matmul(normed, q_cols), cosine, sine_part).astype(BF16)
    kv_halo, out_cols, queries = lax.optimization_barrier((kv_halo, out_cols, queries))
    kv_mine = jnp.concatenate([kv_halo, kv_own], axis=0)
    kv_other = lax.ppermute(kv_mine, AXIS, sibling)
    key_rows = jnp.where(is_even, kv_mine, kv_other)
    value_rows = jnp.where(is_even, kv_other, kv_mine)
    attended, inverse = attend(queries, key_rows, value_rows, starts)
    attn_proj = product_scatter([attended], [out_cols], [0], PLANE_STEP, 2)

    middle = inputs + rms_forward(attn_proj, gain_full[1])
    mid_low = gather_square(rms_forward(middle, gain_full[2]).astype(BF16), PLANE_STEP, 1)
    gate_up = matmul(mid_low, gu_cols)
    gate, up = gate_up[:, :ffc], gate_up[:, ffc:]
    gelu, slope = gelu_parts(gate)
    hidden = (gelu * up).astype(BF16)
    hidden, gain_split, grad_split = lax.optimization_barrier(
        (hidden, split_features(gain_full[3:4]), split_features(cotangent))
    )
    raw_near = product_scatter([hidden], [down_near], [0], PLANE_STEP, 14)
    raw_far, grad_raw_low, down_grad = turn(
        hidden, down_far, raw_near, gain_split, grad_split, planes, PLANE_STEP, 9
    )
    mlp_raw = join_features(jnp.concatenate([raw_near, raw_far], axis=1))
    if not in_place(width // planes // 2):
        down_grad = join_features(down_grad.T).T
    layer_output = (middle + rms_forward(mlp_raw, gain_full[3])).astype(BF16)

    grad_out = cotangent.astype(F32)
    gain_four = jnp.sum(grad_out * mlp_raw * rms_parts(mlp_raw), axis=0)
    down_term = scatter_across(down_grad)
    grad_hidden = matmul(grad_raw_low, jnp.concatenate([down_near, down_far], axis=0))
    grad_normed_mid, gu_grad = product_scatter_back(
        [(slope * up * grad_hidden).astype(BF16), (gelu * grad_hidden).astype(BF16)],
        [gu_cols, gu_cols],
        [0, ffc],
        mid_low,
        PLANE_STEP,
        10,
    )
    gu_term = scatter_across(gu_grad)
    grad_mid_part, gain_three = rms_backward(middle, gain_full[2], grad_normed_mid)
    grad_middle = grad_out + grad_mid_part

    grad_proj, gain_two = rms_backward(attn_proj, gain_full[1], grad_middle)
    grad_proj_own, down_term = lax.optimization_barrier((grad_proj.astype(BF16), down_term))
    grad_proj_low = gather_square(grad_proj_own, PLANE_STEP, 1)
    grad_att = matmul(grad_proj_low, out_cols).astype(BF16)
    grad_query, grad_keys, grad_values = attend_back(
        queries, key_rows, value_rows, starts, inverse, grad_att
    )
    grad_mine = jnp.where(is_even, grad_keys, grad_values)
    grad_give = jnp.where(is_even, grad_values, grad_keys).astype(BF16)
    grad_kv = grad_mine + lax.ppermute(grad_give, AXIS, sibling).astype(F32)
    grad_back = lax.ppermute(grad_kv[:halo].astype(BF16), AXIS, to_prev).astype(F32)
    down_term, grad_kv = lax.optimization_barrier((down_term, grad_kv))
    down_rows = collect(down_term, 1, 6)
    down_rows, grad_back = lax.optimization_barrier((down_rows, grad_back))
    grad_kv = grad_kv[halo:] + jnp.pad(grad_back, ((plane_rows - halo, 0), (0, 0)))
    grad_q = rotate(grad_query, cosine, -sine_part).astype(BF16)
    grad_kv = rotate(grad_kv, kv_cosine, -kv_sine).astype(BF16)
    attn_term, grad_q, grad_kv = lax.optimization_barrier(
        (attn_grad(normed, grad_q, grad_kv, grad_proj_low, attended), grad_q, grad_kv)
    )
    attn_term = scatter_across(attn_term)
    grad_normed = product_scatter([grad_q, grad_kv], [q_cols, kv_cols], [0, 0], PLANE_STEP, 12)
    grad_in_part, gain_one = rms_backward(inputs, gain_full[0], grad_normed)
    grad_tokens = (grad_middle + grad_in_part).astype(BF16)

    gain_term = jnp.stack([gain_one, gain_two, gain_three, gain_four], axis=0)
    gain_term = gain_term.reshape(4, peers, share).transpose(1, 0, 2)
    gain_term = jnp.pad(gain_term, ((0, 0), (0, 8 - 4), (0, -share % 128)))
    gain_recv = collect_gains(gain_term)
    gu_term, gain_recv = lax.optimization_barrier((gu_term, gain_recv))
    gu_rows = collect(gu_term, 2, 13)
    grad_mlp = jnp.concatenate([gu_rows, down_rows], axis=1).astype(F32)
    grad_mlp, attn_term = lax.optimization_barrier((grad_mlp, attn_term))
    grad_attn = collect_attn(attn_term).astype(F32)
    grad_gains = jnp.sum(gain_recv[:, :4, :share], axis=0)
    return (layer_output, grad_tokens, grad_attn, grad_mlp, grad_gains)


def solution(mesh):
    return jax.shard_map(
        local,
        mesh=mesh,
        in_specs=(
            P("fsdp", None),
            P("fsdp", None),
            P("fsdp", None),
            P(None, "fsdp"),
            P(),
            P("fsdp", None),
        ),
        out_specs=(
            P("fsdp", None),
            P("fsdp", None),
            P("fsdp", None),
            P("fsdp", None),
            P(None, "fsdp"),
        ),
        check_vma=False,
    )
```

```python
from functools import partial

import jax
import jax.numpy as jnp
from jax import lax
from jax.experimental import pallas as pl
from jax.experimental.pallas import tpu as pltpu
from jax.sharding import PartitionSpec as P

H = 8
KVH = 4
HD = 256
LMAX = 1024
PLANE = 8
QBLK = 128

EPSILON = 1e-06
SOFT_CAP = 50.0
AXIS = "fsdp"
F32 = jnp.float32
BF16 = jnp.bfloat16
MESH = pl.DeviceIdType.MESH
ANY = pl.BlockSpec(memory_space=pl.ANY)
VMEM = pl.BlockSpec(memory_space=pltpu.VMEM)
DMA = pltpu.SemaphoreType.DMA


def flip(index, step):
    return index + step - 2 * step * ((index // step) % 2)


PLANE_STEP = 4


def partner(index, bits, step):
    for bit, by in ((1, 1), (2, 2), (4, step)):
        if bits & bit:
            index = flip(index, by)
    return index


def place(device, step):
    return device % 4 + 4 * ((device // step) % 2)


def greet(peers):
    barrier = pltpu.get_barrier_semaphore()
    for peer in peers:
        pl.semaphore_signal(barrier, inc=1, device_id=(peer,), device_id_type=MESH)
    pl.semaphore_wait(barrier, len(peers))


class Copies:
    def __init__(self, send_sem, recv_sem):
        self.send_sem, self.recv_sem, self.made = send_sem, recv_sem, []

    def start(self, source, target, device):
        slot = len(self.made)
        copy = pltpu.make_async_remote_copy(
            src_ref=source,
            dst_ref=target,
            send_sem=self.send_sem.at[slot],
            recv_sem=self.recv_sem.at[slot],
            device_id=(device,),
            device_id_type=MESH,
        )
        copy.start()
        self.made.append(copy)
        return copy

    def sent(self):
        for copy in self.made:
            copy.wait_send()


def band(index, size):
    return pl.ds(pl.multiple_of(index * size, 8), size)


def lanes(index, size):
    return pl.ds(pl.multiple_of(index * size, 128), size)


def gather_steps(block_ref, full_ref, copies, own_sem, step):
    rows, width = block_ref.shape
    half = width // 2
    me = lax.axis_index(AXIS)
    sib, xn, yn = flip(me, 1), flip(me, 2), flip(me, step)
    diag = flip(xn, step)

    def at(device, side):
        return full_ref.at[band(place(device, step), rows), pl.ds(side * half, half)]

    def mine(side):
        return block_ref.at[:, pl.ds(side * half, half)]

    own_rows = full_ref.at[band(place(me, step), rows)]
    xa = copies.start(mine(0), at(me, 0), xn)
    ya = copies.start(mine(1), at(me, 1), yn)
    xb = copies.start(mine(1), at(me, 1), xn)
    yb = copies.start(mine(0), at(me, 0), yn)
    arriving = [copies.start(block_ref, own_rows, sib)]
    own = pltpu.make_async_copy(block_ref, own_rows, own_sem)
    own.start()

    def finish(on_rows=None):
        def to_sibling(device, side):
            arriving.append(copies.start(at(device, side), at(device, side), sib))

        def arrived(first, last, *devices):
            for copy in arriving[first:last]:
                copy.wait_recv()
            for device in devices:
                on_rows(device)

        if on_rows is not None:
            own.wait()
            arrived(0, 1, me)
        xa.wait_recv()
        yc = copies.start(at(xn, 0), at(xn, 0), yn)
        to_sibling(xn, 0)
        ya.wait_recv()
        xc = copies.start(at(yn, 1), at(yn, 1), xn)
        to_sibling(yn, 1)
        xb.wait_recv()
        to_sibling(xn, 1)
        yb.wait_recv()
        to_sibling(yn, 0)
        if on_rows is not None:
            arrived(1, 5, xn, yn)
        yc.wait_recv()
        to_sibling(diag, 0)
        xc.wait_recv()
        to_sibling(diag, 1)
        if on_rows is not None:
            arrived(5, 7, diag)
        else:
            arrived(0, 7)
            own.wait()

    return finish


GATHER_COPIES = 13


def cost(microseconds):
    return pl.CostEstimate(
        flops=int(microseconds * 1e7), transcendentals=0, bytes_accessed=int(microseconds * 3e4)
    )


def gather_kernel(block_ref, full_ref, own_sem, send_sem, recv_sem, *, step):
    me = lax.axis_index(AXIS)
    greet((flip(me, 1), flip(me, 2), flip(me, step)))
    copies = Copies(send_sem, recv_sem)
    gather_steps(block_ref, full_ref, copies, own_sem, step)()
    copies.sent()


def gather_square(block, step, collective_id):
    rows, width = block.shape
    return pl.pallas_call(
        partial(gather_kernel, step=step),
        out_shape=jax.ShapeDtypeStruct((PLANE * rows, width), block.dtype),
        in_specs=[ANY],
        out_specs=ANY,
        scratch_shapes=[DMA(()), DMA((GATHER_COPIES,)), DMA((GATHER_COPIES,))],
        compiler_params=pltpu.CompilerParams(collective_id=collective_id, has_side_effects=True),
        cost_estimate=cost(42),
        name="gather_square",
    )(block)


W_TILES = 2
SCATTER_COPIES = 14


def split_columns(width):
    left = (width // 2 + 127) // 128 * 128
    return pl.ds(0, left), pl.ds(left, width - left)


def product_scatter_steps(
    left_refs, right_refs, left_bufs, right_bufs, buffers, load_sem, copies, offsets, step, beside=None
):
    both, got, ra, rb, ra2, rb2 = buffers
    pairs = len(left_refs)
    rows, width = got.shape[1:]
    sides = split_columns(width)
    chunk = 48
    me = lax.axis_index(AXIS)
    core = me % 2
    sib, xn, yn = flip(me, 1), flip(me, 2), flip(me, step)
    order = (flip(xn, step), xn, yn, me)
    first, second = sides

    def chip_rows(device):
        return pl.ds(pl.multiple_of((place(device, step) // 2) * 2 * rows, 16), 2 * rows)

    def right_load(j, t):
        r = sides[t]
        source = right_refs[j].at[r, pl.ds(offsets[j], right_bufs[j].shape[1])]
        return pltpu.make_async_copy(source, right_bufs[j].at[r], load_sem.at[j, t])

    def left_load(j, i):
        r = chip_rows(order[i])
        return pltpu.make_async_copy(
            left_refs[j].at[r], left_bufs[j].at[r], load_sem.at[j, W_TILES + i]
        )

    for j in range(pairs):
        left_load(j, 0).start()
    for t in range(W_TILES):
        for j in range(pairs):
            right_load(j, t).start()
    for i in range(1, 4):
        for j in range(pairs):
            left_load(j, i).start()
    if beside is not None:
        beside[0]()
    greet((sib, xn, yn))

    def mine(i, cols):
        return both.at[i, band(core, rows), cols]

    def add(total, other):
        @pl.loop(0, rows // chunk)
        def _(k):
            r = pl.ds(pl.multiple_of(k * chunk, chunk), chunk)
            total[r] = (total[r].astype(F32) + other[r].astype(F32)).astype(total.dtype)

    loaded = set()

    def make(i, side):
        for j in range(pairs):
            if i not in loaded:
                left_load(j, i).wait()
            if i == 0:
                right_load(j, side).wait()
        loaded.add(i)
        r, cols = chip_rows(order[i]), sides[side]
        total = None
        for j in range(pairs):
            term = contract_last(left_bufs[j][r], right_bufs[j][cols])
            total = term if total is None else total + term
        both[i, :, cols] = total.astype(BF16)
        return copies.start(both.at[i, band(1 - core, rows), cols], got.at[i, :, cols], sib)

    def merge(crossing, i, side):
        cols = sides[side]
        crossing.wait_recv()
        add(mine(i, cols), got.at[i, :, cols])

    c0 = make(0, 0)
    c1 = make(0, 1)
    merge(c0, 0, 0)
    x0 = copies.start(mine(0, first), ra.at[0], xn)
    c2 = make(1, 0)
    merge(c1, 0, 1)
    y0 = copies.start(mine(0, second), rb.at[0], yn)
    c3 = make(2, 1)
    merge(c2, 1, 0)
    x1 = copies.start(mine(1, first), ra.at[1], xn)
    c4 = make(2, 0)
    merge(c3, 2, 1)
    y1 = copies.start(mine(2, second), rb.at[1], yn)
    c5 = make(1, 1)
    merge(c4, 2, 0)
    x0.wait_recv()
    add(mine(2, first), ra.at[0])
    y2 = copies.start(mine(2, first), ra2, yn)
    c6 = make(3, 0)
    merge(c5, 1, 1)
    y0.wait_recv()
    add(mine(1, second), rb.at[0])
    x2 = copies.start(mine(1, second), rb2, xn)
    c7 = make(3, 1)
    merge(c6, 3, 0)
    merge(c7, 3, 1)
    if beside is not None:
        beside[1]()
    for copy in (x1, y1, y2, x2):
        copy.wait_recv()
    own = both.at[3, band(core, rows)]

    def summed(r):
        return jnp.concatenate(
            [
                own[r, first].astype(F32) + ra[1, r].astype(F32) + ra2[r].astype(F32),
                own[r, second].astype(F32) + rb[1, r].astype(F32) + rb2[r].astype(F32),
            ],
            axis=1,
        )

    return summed


ROW_CHUNK = 48


def product_scatter_kernel(*refs, pairs, offsets, step):
    left_refs, right_refs, out_ref = refs[:pairs], refs[pairs : 2 * pairs], refs[2 * pairs]
    left_bufs = refs[2 * pairs + 1 : 3 * pairs + 1]
    right_bufs = refs[3 * pairs + 1 : 4 * pairs + 1]
    buffers, (load_sem, send_sem, recv_sem) = refs[4 * pairs + 1 : -3], refs[-3:]
    copies = Copies(send_sem, recv_sem)
    summed = product_scatter_steps(
        left_refs, right_refs, left_bufs, right_bufs, buffers, load_sem, copies, offsets, step
    )

    @pl.loop(0, out_ref.shape[0] // ROW_CHUNK)
    def _(k):
        r = pl.ds(pl.multiple_of(k * ROW_CHUNK, ROW_CHUNK), ROW_CHUNK)
        out_ref[r] = summed(r)

    copies.sent()


def scatter_buffers(rows, width):
    left, right = [side.size for side in split_columns(width)]
    return [
        pltpu.VMEM((4, 2 * rows, width), BF16),
        pltpu.VMEM((4, rows, width), BF16),
        pltpu.VMEM((2, rows, left), BF16),
        pltpu.VMEM((2, rows, right), BF16),
        pltpu.VMEM((rows, left), BF16),
        pltpu.VMEM((rows, right), BF16),
    ]


def product_scatter(lefts, rights, offsets, step, collective_id):
    pairs = len(lefts)
    rows, width = lefts[0].shape[0] // PLANE, rights[0].shape[0]
    return pl.pallas_call(
        partial(product_scatter_kernel, pairs=pairs, offsets=offsets, step=step),
        out_shape=jax.ShapeDtypeStruct((rows, width), F32),
        in_specs=[ANY] * (2 * pairs),
        out_specs=VMEM,
        scratch_shapes=[
            *[pltpu.VMEM(value.shape, BF16) for value in lefts],
            *[pltpu.VMEM((width, value.shape[1]), BF16) for value in lefts],
            *scatter_buffers(rows, width),
            DMA((pairs, W_TILES + 4)),
            DMA((SCATTER_COPIES,)),
            DMA((SCATTER_COPIES,)),
        ],
        compiler_params=pltpu.CompilerParams(
            collective_id=collective_id, has_side_effects=True, vmem_limit_bytes=56 << 20
        ),
        cost_estimate=cost(50),
        name="product_scatter",
    )(*lefts, *rights)


BACK_TILE = 384


def back_kernel(*refs, pairs, offsets, step):
    left_refs, right_refs, rows_ref = refs[:pairs], refs[pairs : 2 * pairs], refs[2 * pairs]
    out_ref, term_ref = refs[2 * pairs + 1 : 2 * pairs + 3]
    scratch = refs[2 * pairs + 3 :]
    left_bufs, right_bufs = scratch[:pairs], scratch[pairs : 2 * pairs]
    rows_buf, stage = scratch[2 * pairs : 2 * pairs + 2]
    buffers = scratch[2 * pairs + 2 : -5]
    load_sem, rows_sem, store_sem, send_sem, recv_sem = scratch[-5:]
    copies = Copies(send_sem, recv_sem)
    rows_load = pltpu.make_async_copy(rows_ref, rows_buf, rows_sem)
    tiles = rows_ref.shape[1] // BACK_TILE
    width = left_refs[0].shape[1]

    def store(t):
        return pltpu.make_async_copy(
            stage.at[t % 2],
            term_ref.at[pl.ds(pl.multiple_of(t * BACK_TILE, 16), BACK_TILE)],
            store_sem.at[t % 2],
        )

    def beside():
        rows_load.wait()

        @pl.loop(0, tiles)
        def _(t):
            @pl.when(t >= 2)
            def _():
                store(t - 2).wait()

            columns = rows_buf[:, pl.ds(pl.multiple_of(t * BACK_TILE, BACK_TILE), BACK_TILE)]
            for j in range(pairs):
                term = contract_first(columns, left_bufs[j][...])
                stage[t % 2, :, pl.ds(j * width, width)] = term.astype(BF16)
            store(t).start()

    def start_rows():
        rows_load.start()

    summed = product_scatter_steps(
        left_refs,
        right_refs,
        left_bufs,
        right_bufs,
        buffers,
        load_sem,
        copies,
        offsets,
        step,
        (start_rows, beside),
    )

    @pl.loop(0, out_ref.shape[0] // ROW_CHUNK)
    def _(k):
        r = pl.ds(pl.multiple_of(k * ROW_CHUNK, ROW_CHUNK), ROW_CHUNK)
        out_ref[r] = summed(r)

    for t in range(tiles - 2, tiles):
        store(t).wait()
    copies.sent()


def product_scatter_back(lefts, rights, offsets, rows, step, collective_id):
    pairs = len(lefts)
    count, width = lefts[0].shape[0] // PLANE, rights[0].shape[0]
    columns = sum(value.shape[1] for value in lefts)
    return pl.pallas_call(
        partial(back_kernel, pairs=pairs, offsets=offsets, step=step),
        out_shape=(
            jax.ShapeDtypeStruct((count, width), F32),
            jax.ShapeDtypeStruct((rows.shape[1], columns), BF16),
        ),
        in_specs=[ANY] * (2 * pairs + 1),
        out_specs=(VMEM, ANY),
        scratch_shapes=[
            *[pltpu.VMEM(value.shape, BF16) for value in lefts],
            *[pltpu.VMEM((width, value.shape[1]), BF16) for value in lefts],
            pltpu.VMEM(rows.shape, BF16),
            pltpu.VMEM((2, BACK_TILE, columns), BF16),
            *scatter_buffers(count, width),
            DMA((pairs, W_TILES + 4)),
            DMA(()),
            DMA((2,)),
            DMA((SCATTER_COPIES,)),
            DMA((SCATTER_COPIES,)),
        ],
        compiler_params=pltpu.CompilerParams(
            collective_id=collective_id, has_side_effects=True, vmem_limit_bytes=62 << 20
        ),
        cost_estimate=cost(60),
        name="product_scatter_back",
    )(*lefts, *rights, rows)


TURN_TILE = 768


def in_place(rows):
    return rows % 16 == 0


def turn_kernel(
    left_ref,
    right_ref,
    near_ref,
    gain_ref,
    grad_ref,
    raw_ref,
    full_ref,
    term_ref,
    *refs,
    planes,
    step,
):
    left_buf, right_buf, gathered, total, grad_own, stage = refs[:6]
    buffers, (load_sem, own_sem, store_sem, send_sem, recv_sem) = refs[6:-5], refs[-5:]
    rows, width = grad_ref.shape
    half = width // 2
    piece = half // planes
    copies = Copies(send_sem, recv_sem)
    summed = product_scatter_steps(
        [left_ref], [right_ref], [left_buf], [right_buf], buffers, load_sem, copies, [0], step
    )
    gain = gain_ref[...]

    @pl.loop(0, rows // ROW_CHUNK)
    def _(k):
        r = pl.ds(pl.multiple_of(k * ROW_CHUNK, ROW_CHUNK), ROW_CHUNK)
        far = summed(r)
        raw_ref[r] = far
        value = jnp.concatenate([near_ref[r], far], axis=1)
        scale = lax.rsqrt(jnp.mean(value * value, axis=1, keepdims=True) + EPSILON)
        scaled = (1.0 + gain) * grad_ref[r].astype(F32)
        inner = jnp.mean(value * scaled, axis=1, keepdims=True)
        grad_own[r] = (scale * scaled - value * (scale * scale * scale * inner)).astype(BF16)

    stores = []

    def store_term(side):
        for plane in range(planes):
            start = side * half + plane * piece
            target = plane * 2 * piece + side * piece if in_place(piece) else start
            pltpu.make_async_copy(
                stage.at[pl.ds(start, piece)] if in_place(piece) else stage.at[pl.ds(side * half, half)],
                term_ref.at[pl.ds(target, piece)]
                if in_place(piece)
                else term_ref.at[pl.ds(side * half, half)],
                store_sem.at[4],
            ).start()
            if not in_place(piece):
                break

    def on_rows(device):
        slot = len(stores)
        r = pl.ds(pl.multiple_of((place(device, step) // 2) * 2 * rows, 16), 2 * rows)
        store = pltpu.make_async_copy(gathered.at[r], full_ref.at[r], store_sem.at[slot])
        store.start()
        stores.append(store)
        right = left_buf[r]
        if slot < 3:

            @pl.loop(0, width // TURN_TILE)
            def _(t):
                w = pl.ds(pl.multiple_of(t * TURN_TILE, TURN_TILE), TURN_TILE)
                term = contract_first(gathered[r, w], right)
                if slot == 0:
                    total[w] = term
                else:
                    total[w] += term
        else:
            for side in range(2):

                w = pl.ds(side * half, half)
                stage[w] = (total[w] + contract_first(gathered[r, w], right)).astype(BF16)
                store_term(side)

    gather_steps(grad_own, gathered, copies, own_sem, step)(on_rows)
    pltpu.make_async_copy(stage, term_ref, store_sem.at[4]).wait()
    for store in stores:
        store.wait()
    copies.sent()


def turn(left, right, near, gain_row, grad, planes, step, collective_id):
    rows, width = grad.shape
    count = SCATTER_COPIES + GATHER_COPIES
    return pl.pallas_call(
        partial(turn_kernel, planes=planes, step=step),
        out_shape=(
            jax.ShapeDtypeStruct((rows, width // 2), F32),
            jax.ShapeDtypeStruct((PLANE * rows, width), BF16),
            jax.ShapeDtypeStruct((width, left.shape[1]), BF16),
        ),
        in_specs=[ANY, ANY, VMEM, VMEM, VMEM],
        out_specs=(VMEM, ANY, ANY),
        scratch_shapes=[
            pltpu.VMEM(left.shape, BF16),
            pltpu.VMEM(right.shape, BF16),
            pltpu.VMEM((PLANE * rows, width), BF16),
            pltpu.VMEM((width, left.shape[1]), F32),
            pltpu.VMEM((rows, width), BF16),
            pltpu.VMEM((width, left.shape[1]), BF16),
            *scatter_buffers(rows, width // 2),
            DMA((1, W_TILES + 4)),
            DMA(()),
            DMA((5,)),
            DMA((count,)),
            DMA((count,)),
        ],
        compiler_params=pltpu.CompilerParams(
            collective_id=collective_id, has_side_effects=True, vmem_limit_bytes=60 << 20
        ),
        cost_estimate=cost(50),
        name="turn",
    )(left, right, near, gain_row, grad)


def attn_columns(column):
    query_width = H * HD
    key_offset = query_width + (column % 2) * KVH * HD + (column // 2) * HD
    return (column * HD, key_offset, query_width + 2 * KVH * HD + column * HD)


def greet_all(peers):
    me = lax.axis_index(AXIS)
    barrier = pltpu.get_barrier_semaphore()

    @pl.loop(1, peers)
    def _(k):
        device = lax.rem(me + k, peers)
        pl.semaphore_signal(barrier, inc=1, device_id=(device,), device_id_type=MESH)

    pl.semaphore_wait(barrier, peers - 1)


def exchange_all(source_of, target_ref, send_sem, recv_sem):
    peers = target_ref.shape[0]
    me = lax.axis_index(AXIS)

    def copy(k):
        device = lax.rem(me + k, peers)
        return pltpu.make_async_remote_copy(
            src_ref=source_of(device),
            dst_ref=target_ref.at[me],
            send_sem=send_sem.at[k],
            recv_sem=recv_sem.at[k],
            device_id=(device,),
            device_id_type=MESH,
        )

    @pl.loop(1, peers)
    def _(k):
        copy(k).start()

    def finish():
        @pl.loop(1, peers)
        def _(k):
            copy(k).wait()

    return finish


ORDER = (6, 7, 2, 3, 4, 5, 1)


def swap_steps(pieces_of, targets, copies, own_sem, step):
    me = lax.axis_index(AXIS)
    owns, moved = [], []
    for slot, (source, target) in enumerate(zip(pieces_of(place(me, step)), targets)):
        own = pltpu.make_async_copy(source, target, own_sem.at[slot])
        own.start()
        owns.append(own)
    for bits in ORDER:
        peer = partner(me, bits, step)
        for source, target in zip(pieces_of(place(peer, step)), targets):
            moved.append(copies.start(source, target, peer))

    def finish():
        for own in owns:
            own.wait()
        for copy in moved:
            copy.wait_recv()

    return finish


def square(step):
    me = lax.axis_index(AXIS)
    return [partner(me, bits, step) for bits in ORDER]


def wide(offset):
    return pl.ds(pl.multiple_of(offset, 128), HD)


class Line:
    def __init__(self, full_ref, send_sem, recv_sem, own_ref=None):
        me = lax.axis_index(AXIS)
        self.own = own_ref
        self.full, self.planes = full_ref, full_ref.shape[0]
        self.send_sem, self.recv_sem = send_sem, recv_sem
        self.plane = me // PLANE
        peers = self.planes * PLANE
        self.devices = (lax.rem(me + PLANE, peers), lax.rem(me + peers - PLANE, peers))

    def copy(self, way, slot, source, first=False):
        return pltpu.make_async_remote_copy(
            src_ref=self.own if first and self.own is not None else self.full.at[source],
            dst_ref=self.full.at[source],
            send_sem=self.send_sem.at[way, slot],
            recv_sem=self.recv_sem.at[way, slot],
            device_id=(self.devices[way],),
            device_id_type=MESH,
        )

    def sends(self, way, hop):
        if way == 0:
            source = self.plane - (hop - 1)
            return (self.plane + 1 < self.planes) & (source >= 0), source
        source = self.plane + (hop - 1)
        return (self.plane >= 1) & (source < self.planes), source

    def greet(self):
        barrier = pltpu.get_barrier_semaphore()
        count = 0
        for way, there in enumerate((self.plane + 1 < self.planes, self.plane >= 1)):

            @pl.when(there)
            def _():
                pl.semaphore_signal(
                    barrier, inc=1, device_id=(self.devices[way],), device_id_type=MESH
                )

            count = count + there.astype(jnp.int32)
        return count

    def start(self, hop, slot):
        for way in range(2):
            there, source = self.sends(way, hop)

            @pl.when(there)
            def _():
                self.copy(way, slot, source, hop == 1).start()

    def arrived(self, hop, slot):
        for way in range(2):
            source = self.plane - hop if way == 0 else self.plane + hop

            @pl.when((source >= 0) & (source < self.planes))
            def _():
                self.copy(way, slot, source).wait_recv()

    def sent(self, hop, slot):
        for way in range(2):
            there, source = self.sends(way, hop)

            @pl.when(there)
            def _():
                self.copy(way, slot, source, hop == 1).wait_send()

    def begin(self, hops):
        if hops:
            self.start(hops[0], 0)

    def run(self, hops):
        for slot, hop in enumerate(hops):
            self.arrived(hop, slot)
            if slot + 1 < len(hops):
                self.start(hop + 1, slot + 1)

    def end(self, hops):
        for slot, hop in enumerate(hops):
            self.sent(hop, slot)


def line_hops(planes):
    hops = list(range(1, planes))
    first = (2 * len(hops) + 2) // 3
    return hops[:first], hops[first:]


def line_semaphores(hops):
    count = max(1, len(hops))
    return [DMA((2, count)), DMA((2, count))]


def greet_line(line, peers):
    barrier = pltpu.get_barrier_semaphore()
    for peer in peers:
        pl.semaphore_signal(barrier, inc=1, device_id=(peer,), device_id_type=MESH)
    pl.semaphore_wait(barrier, len(peers) + line.greet())


def row_bands(weights_ref):
    return [weights_ref.at[:, pl.ds(start * HD, H * HD)] for start in (0, H + 2 * KVH)]


def spread_attn_kernel(weights_ref, kv_ref, q_ref, out_ref, own_sem, send_sem, recv_sem, *sems):
    me = lax.axis_index(AXIS)
    plane, here = me // PLANE, place(me, PLANE_STEP)
    q_rows, out_rows = row_bands(weights_ref)
    q_line = Line(q_ref, sems[0], sems[1], q_rows)
    out_line = Line(out_ref, sems[2], sems[3], out_rows)
    hops = line_hops(out_line.planes)[0]
    greet_line(out_line, square(PLANE_STEP))
    out_line.begin(hops)
    q_line.begin([1])
    owns = []
    for slot, (source, target) in enumerate(((q_rows, q_ref), (out_rows, out_ref))):
        own = pltpu.make_async_copy(source, target.at[plane], own_sem.at[1 + slot])
        own.start()
        owns.append(own)
    copies = Copies(send_sem, recv_sem)
    spread = swap_steps(
        lambda c: [weights_ref.at[:, wide(attn_columns(c)[1])]],
        [kv_ref.at[plane, here]],
        copies,
        own_sem,
        PLANE_STEP,
    )
    out_line.run(hops)
    q_line.run([1])
    spread()
    for own in owns:
        own.wait()
    out_line.end(hops)
    q_line.end([1])
    copies.sent()


def spread_attn(weights, planes):
    rows = weights.shape[0]
    return pl.pallas_call(
        spread_attn_kernel,
        out_shape=(
            jax.ShapeDtypeStruct((planes, PLANE, rows, HD), BF16),
            jax.ShapeDtypeStruct((planes, rows, H * HD), BF16),
            jax.ShapeDtypeStruct((planes, rows, H * HD), BF16),
        ),
        in_specs=[ANY],
        out_specs=(ANY, ANY, ANY),
        scratch_shapes=[
            DMA((3,)),
            DMA((7,)),
            DMA((7,)),
            *line_semaphores([1]),
            *line_semaphores(line_hops(planes)[0]),
        ],
        compiler_params=pltpu.CompilerParams(collective_id=3, has_side_effects=True),
        name="spread_attn",
    )(weights)


def spread_gu_kernel(
    weights_ref,
    gain_ref,
    kv_in,
    q_in,
    out_in,
    gu_ref,
    gains_ref,
    kv_ref,
    q_ref,
    out_ref,
    own_sem,
    send_sem,
    recv_sem,
    gain_send,
    gain_recv,
    *sems,
):
    peers = gains_ref.shape[0]
    ffc = gu_ref.shape[2] // 2
    me = lax.axis_index(AXIS)
    here = place(me, PLANE_STEP)
    kv_line = Line(kv_ref, sems[0], sems[1])
    q_line = Line(q_ref, sems[2], sems[3])
    out_line = Line(out_ref, sems[4], sems[5])
    kv_hops, out_hops = line_hops(kv_line.planes)
    q_hops = list(range(2, kv_line.planes))
    greet_all(peers)
    q_line.begin(q_hops)
    out_line.begin(out_hops)
    kv_line.begin(kv_hops)
    gains_done = exchange_all(lambda device: gain_ref, gains_ref, gain_send, gain_recv)
    own = pltpu.make_async_copy(gain_ref, gains_ref.at[me], own_sem.at[2])
    own.start()
    copies = Copies(send_sem, recv_sem)
    spread = swap_steps(
        lambda c: [weights_ref.at[:, lanes(slot * PLANE + c, ffc)] for slot in range(2)],
        [gu_ref.at[here, :, pl.ds(slot * ffc, ffc)] for slot in range(2)],
        copies,
        own_sem,
        PLANE_STEP,
    )
    q_line.run(q_hops)
    out_line.run(out_hops)
    kv_line.run(kv_hops)
    spread()
    own.wait()
    gains_done()
    for line, hops in ((q_line, q_hops), (out_line, out_hops), (kv_line, kv_hops)):
        line.end(hops)
    copies.sent()


def spread_gu(weights, gain_block, kv_full, q_rows, out_rows, peers):
    rows = weights.shape[0]
    ffc = weights.shape[1] // 3 // PLANE
    planes = kv_full.shape[0]
    kv_hops, out_hops = line_hops(planes)
    return pl.pallas_call(
        spread_gu_kernel,
        out_shape=(
            jax.ShapeDtypeStruct((PLANE, rows, 2 * ffc), BF16),
            jax.ShapeDtypeStruct((peers,) + gain_block.shape, gain_block.dtype),
            jax.ShapeDtypeStruct(kv_full.shape, kv_full.dtype),
            jax.ShapeDtypeStruct(q_rows.shape, q_rows.dtype),
            jax.ShapeDtypeStruct(out_rows.shape, out_rows.dtype),
        ),
        in_specs=[ANY] * 5,
        out_specs=(ANY,) * 5,
        scratch_shapes=[
            DMA((3,)),
            DMA((14,)),
            DMA((14,)),
            DMA((peers,)),
            DMA((peers,)),
            *line_semaphores(kv_hops),
            *line_semaphores(range(2, planes)),
            *line_semaphores(out_hops),
        ],
        input_output_aliases={2: 2, 3: 3, 4: 4},
        compiler_params=pltpu.CompilerParams(collective_id=4, has_side_effects=True),
        cost_estimate=cost(38),
        name="spread_gu",
    )(weights, gain_block, kv_full, q_rows, out_rows)


def spread_down_kernel(
    weights_ref,
    block_ref,
    kv_in,
    rows_ref,
    down_ref,
    full_ref,
    kv_ref,
    q_ref,
    own_sem,
    send_sem,
    recv_sem,
    line_send,
    line_recv,
):
    ffc = down_ref.shape[2]
    here = place(lax.axis_index(AXIS), PLANE_STEP)
    line = Line(kv_ref, line_send, line_recv)
    hops = line_hops(line.planes)[1]
    greet_line(line, square(PLANE_STEP))
    line.begin(hops)
    copies = Copies(send_sem, recv_sem)
    gathered = gather_steps(block_ref, full_ref, copies, own_sem.at[2], PLANE_STEP)
    spread = swap_steps(
        lambda c: [
            rows_ref.at[:, :, lanes(c, HD)],
            weights_ref.at[:, lanes(2 * PLANE + c, ffc)],
        ],
        [q_ref.at[:, here], down_ref.at[here]],
        copies,
        own_sem,
        PLANE_STEP,
    )
    gathered()
    line.run(hops)
    spread()
    line.end(hops)
    copies.sent()


def spread_down(weights, block, kv_full, q_rows):
    rows = weights.shape[0]
    ffc = weights.shape[1] // 3 // PLANE
    planes = kv_full.shape[0]
    count = GATHER_COPIES + 14
    return pl.pallas_call(
        spread_down_kernel,
        out_shape=(
            jax.ShapeDtypeStruct((PLANE, rows, ffc), BF16),
            jax.ShapeDtypeStruct((PLANE * block.shape[0], block.shape[1]), BF16),
            jax.ShapeDtypeStruct(kv_full.shape, kv_full.dtype),
            jax.ShapeDtypeStruct((planes, PLANE, rows, HD), BF16),
        ),
        in_specs=[ANY] * 4,
        out_specs=(ANY,) * 4,
        scratch_shapes=[
            DMA((3,)),
            DMA((count,)),
            DMA((count,)),
            *line_semaphores(line_hops(planes)[1]),
        ],
        input_output_aliases={2: 2},
        compiler_params=pltpu.CompilerParams(collective_id=5, has_side_effects=True),
        cost_estimate=cost(1),
        name="spread_down",
    )(weights, block, kv_full, q_rows)


def spread_out_kernel(rows_ref, full_ref, own_sem, send_sem, recv_sem):
    here = place(lax.axis_index(AXIS), PLANE_STEP)
    greet(square(PLANE_STEP))
    copies = Copies(send_sem, recv_sem)
    swap_steps(
        lambda c: [rows_ref.at[:, :, lanes(c, HD)]],
        [full_ref.at[:, here]],
        copies,
        own_sem,
        PLANE_STEP,
    )()
    copies.sent()


def spread_out(out_rows):
    planes, rows = out_rows.shape[:2]
    return pl.pallas_call(
        spread_out_kernel,
        out_shape=jax.ShapeDtypeStruct((planes, PLANE, rows, HD), BF16),
        in_specs=[ANY],
        out_specs=ANY,
        scratch_shapes=[DMA((1,)), DMA((7,)), DMA((7,))],
        compiler_params=pltpu.CompilerParams(collective_id=11, has_side_effects=True),
        cost_estimate=cost(0.1),
        name="spread_out",
    )(out_rows)


def collect_kernel(term_ref, rows_ref, own_sem, send_sem, recv_sem):
    here = place(lax.axis_index(AXIS), PLANE_STEP)
    count = own_sem.shape[0]
    ffc = term_ref.shape[2] // count
    greet(square(PLANE_STEP))
    copies = Copies(send_sem, recv_sem)
    swap_steps(
        lambda c: [term_ref.at[c, :, pl.ds(slot * ffc, ffc)] for slot in range(count)],
        [rows_ref.at[:, lanes(slot * PLANE + here, ffc)] for slot in range(count)],
        copies,
        own_sem,
        PLANE_STEP,
    )()
    copies.sent()


def collect(term, count, collective_id):
    rows, columns = term.shape[1:]
    return pl.pallas_call(
        collect_kernel,
        out_shape=jax.ShapeDtypeStruct((rows, PLANE * columns), BF16),
        in_specs=[ANY],
        out_specs=ANY,
        scratch_shapes=[DMA((count,)), DMA((7 * count,)), DMA((7 * count,))],
        compiler_params=pltpu.CompilerParams(collective_id=collective_id, has_side_effects=True),
        cost_estimate=cost(0.1),
        name="collect",
    )(term)


def collect_attn_kernel(term_ref, rows_ref, own_sem, send_sem, recv_sem):
    here = place(lax.axis_index(AXIS), PLANE_STEP)
    greet(square(PLANE_STEP))
    copies = Copies(send_sem, recv_sem)
    swap_steps(
        lambda c: [term_ref.at[c, :, pl.ds(slot * HD, HD)] for slot in range(3)],
        [rows_ref.at[:, wide(offset)] for offset in attn_columns(here)],
        copies,
        own_sem,
        PLANE_STEP,
    )()
    copies.sent()


def collect_attn(term):
    rows = term.shape[1]
    return pl.pallas_call(
        collect_attn_kernel,
        out_shape=jax.ShapeDtypeStruct((rows, PLANE * 3 * HD), BF16),
        in_specs=[ANY],
        out_specs=ANY,
        scratch_shapes=[DMA((3,)), DMA((21,)), DMA((21,))],
        compiler_params=pltpu.CompilerParams(collective_id=7, has_side_effects=True),
        name="collect_attn",
    )(term)


def collect_gains_kernel(gain_ref, gains_ref, own_sem, gain_send, gain_recv):
    me = lax.axis_index(AXIS)
    greet_all(gain_ref.shape[0])
    done = exchange_all(lambda device: gain_ref.at[device], gains_ref, gain_send, gain_recv)
    own = pltpu.make_async_copy(gain_ref.at[me], gains_ref.at[me], own_sem)
    own.start()
    own.wait()
    done()


def collect_gains(gain_blocks):
    peers = gain_blocks.shape[0]
    return pl.pallas_call(
        collect_gains_kernel,
        out_shape=jax.ShapeDtypeStruct(gain_blocks.shape, gain_blocks.dtype),
        in_specs=[ANY],
        out_specs=ANY,
        scratch_shapes=[DMA(()), DMA((peers,)), DMA((peers,))],
        compiler_params=pltpu.CompilerParams(collective_id=8, has_side_effects=True),
        name="collect_gains",
    )(gain_blocks)


def block_scores(q, k, start, first):
    scores = lax.dot_general(q, k, (((1,), (1,)), ((), ())), preferred_element_type=F32)
    bent = jnp.tanh(scores * (HD ** (-0.5) / SOFT_CAP))
    rows, span = scores.shape
    key_at = lax.broadcasted_iota(jnp.int32, (rows, span), 1)
    row_at = lax.broadcasted_iota(jnp.int32, (rows, span), 0)
    allowed = (key_at + first >= start) & (key_at <= row_at + LMAX)
    return (bent, jnp.where(allowed, jnp.exp(SOFT_CAP * bent), 0.0))


def attend_kernel(q_ref, k_ref, v_ref, start_ref, out_ref, inv_ref):
    first = pl.program_id(0) * QBLK
    keys = pl.ds(pl.multiple_of(first, QBLK), LMAX + QBLK)
    unused_bent, exponent = block_scores(q_ref[...], k_ref[keys], start_ref[...], first)
    inverse = 1.0 / jnp.sum(exponent, axis=-1, keepdims=True)
    weights = (exponent * inverse).astype(BF16)
    out_ref[...] = jnp.dot(weights, v_ref[keys], preferred_element_type=F32).astype(BF16)
    inv_ref[...] = inverse


def attend(queries, key_rows, value_rows, starts):
    rows = queries.shape[0]
    span = key_rows.shape[0]
    row_spec = pl.BlockSpec((QBLK, HD), lambda i: (i, 0))
    one_spec = pl.BlockSpec((QBLK, 1), lambda i: (i, 0))
    all_spec = pl.BlockSpec((span, HD), lambda i: (0, 0))
    return pl.pallas_call(
        attend_kernel,
        out_shape=(
            jax.ShapeDtypeStruct((rows, HD), BF16),
            jax.ShapeDtypeStruct((rows, 1), F32),
        ),
        grid=(rows // QBLK,),
        in_specs=[row_spec, all_spec, all_spec, one_spec],
        out_specs=(row_spec, one_spec),
        compiler_params=pltpu.CompilerParams(vmem_limit_bytes=40 << 20),
        cost_estimate=cost(1),
        name="attend",
    )(queries, key_rows, value_rows, starts)


GRAD_TILE = 384


def attn_grad_kernel(rows_ref, q_ref, kv_ref, proj_ref, attended_ref, out_ref):
    for slot, (left, right) in enumerate(
        ((rows_ref, q_ref), (rows_ref, kv_ref), (proj_ref, attended_ref))
    ):
        out_ref[:, pl.ds(slot * HD, HD)] = contract_first(left[...], right[...]).astype(BF16)


def attn_grad(rows, grad_q, grad_kv, grad_proj, attended):
    count, width = rows.shape
    tile = pl.BlockSpec((count, GRAD_TILE), lambda i: (0, i))
    whole = pl.BlockSpec((count, HD), lambda i: (0, 0))
    return pl.pallas_call(
        attn_grad_kernel,
        out_shape=jax.ShapeDtypeStruct((width, 3 * HD), BF16),
        grid=(width // GRAD_TILE,),
        in_specs=[tile, whole, whole, tile, whole],
        out_specs=pl.BlockSpec((GRAD_TILE, 3 * HD), lambda i: (i, 0)),
        compiler_params=pltpu.CompilerParams(vmem_limit_bytes=48 << 20),
        cost_estimate=cost(10),
        name="attn_grad",
    )(rows, grad_q, grad_kv, grad_proj, attended)


def attend_back_kernel(q_ref, k_ref, v_ref, start_ref, inv_ref, grad_ref, gq_ref, gk_ref, gv_ref):
    @pl.when(pl.program_id(0) == 0)
    def _():
        gk_ref[...] = jnp.zeros_like(gk_ref)
        gv_ref[...] = jnp.zeros_like(gv_ref)

    first = pl.program_id(0) * QBLK
    keys = pl.ds(pl.multiple_of(first, QBLK), LMAX + QBLK)
    q, k, v, grad = q_ref[...], k_ref[keys], v_ref[keys], grad_ref[...]
    bent, exponent = block_scores(q, k, start_ref[...], first)
    probability = exponent * inv_ref[...]
    grad_prob = lax.dot_general(grad, v, (((1,), (1,)), ((), ())), preferred_element_type=F32)
    inner = jnp.sum(probability * grad_prob, axis=-1, keepdims=True)
    grad_scores = (probability * (grad_prob - inner) * (1.0 - bent * bent)).astype(BF16)
    scale = HD ** (-0.5)
    gq_ref[...] = jnp.dot(grad_scores, k, preferred_element_type=F32) * scale
    over_rows = (((0,), (0,)), ((), ()))
    gk_ref[keys] += lax.dot_general(grad_scores, q, over_rows, preferred_element_type=F32) * scale
    gv_ref[keys] += lax.dot_general(
        probability.astype(BF16), grad, over_rows, preferred_element_type=F32
    )


def attend_back(queries, key_rows, value_rows, starts, inverse, grad):
    rows = queries.shape[0]
    span = key_rows.shape[0]
    row_spec = pl.BlockSpec((QBLK, HD), lambda i: (i, 0))
    one_spec = pl.BlockSpec((QBLK, 1), lambda i: (i, 0))
    all_spec = pl.BlockSpec((span, HD), lambda i: (0, 0))
    return pl.pallas_call(
        attend_back_kernel,
        out_shape=(
            jax.ShapeDtypeStruct((rows, HD), F32),
            jax.ShapeDtypeStruct((span, HD), F32),
            jax.ShapeDtypeStruct((span, HD), F32),
        ),
        grid=(rows // QBLK,),
        in_specs=[row_spec, all_spec, all_spec, one_spec, one_spec, row_spec],
        out_specs=(row_spec, all_spec, all_spec),
        compiler_params=pltpu.CompilerParams(vmem_limit_bytes=48 << 20),
        cost_estimate=cost(20),
        name="attend_back",
    )(queries, key_rows, value_rows, starts, inverse, grad)


def token_tables(seq_lengths, index_vec):
    count = seq_lengths.shape[0]
    order = jnp.arange(count, dtype=jnp.int32)
    seq_ends = jnp.sum(
        jnp.where(order[None, :] <= order[:, None], seq_lengths[None, :], 0), axis=1
    )
    after_end = index_vec[:, None] >= seq_ends[None, :]
    return index_vec - jnp.sum(jnp.where(after_end, seq_lengths[None, :], 0), axis=1)


def rms_parts(value):
    return lax.rsqrt(jnp.mean(value * value, axis=-1, keepdims=True) + EPSILON)


def rms_forward(value, gain_vec):
    return value * rms_parts(value) * (1.0 + gain_vec)


def rms_backward(value, gain_vec, grad):
    r = rms_parts(value)
    scaled = (1.0 + gain_vec) * grad
    inner = jnp.mean(value * scaled, axis=-1, keepdims=True)
    return (r * scaled - value * (r * r * r * inner), jnp.sum(grad * value * r, axis=0))


def rotate(value, cosine, sine_part):
    half_width = value.shape[-1] // 2
    first_half = value[..., :half_width]
    second_half = value[..., half_width:]
    return jnp.concatenate(
        [
            first_half * cosine - second_half * sine_part,
            second_half * cosine + first_half * sine_part,
        ],
        axis=-1,
    )


def contract_last(left_side, right_side):
    return lax.dot_general(
        left_side, right_side, (((1,), (1,)), ((), ())), preferred_element_type=F32
    )


def contract_first(left_side, right_side):
    return lax.dot_general(
        left_side, right_side, (((0,), (0,)), ((), ())), preferred_element_type=F32
    )


def matmul(left_side, right_side):
    return jnp.dot(left_side, right_side, preferred_element_type=F32)


def gelu_parts(gate):
    k0 = 0.7978845608028654
    k1 = 0.044715
    t = jnp.tanh(k0 * (gate + k1 * gate * gate * gate))
    value = 0.5 * gate * (1.0 + t)
    slope = 0.5 * (1.0 + t) + 0.5 * gate * (1.0 - t * t) * k0 * (1.0 + 3.0 * k1 * gate * gate)
    return (value, slope)


def local(tokens, attn_weights, mlp_weights, norm_gains, seq_lengths, cotangent):
    tok_rows, width = tokens.shape
    peers = lax.axis_size(AXIS)
    planes = peers // PLANE
    share = width // peers
    row_share = attn_weights.shape[0]
    ff = mlp_weights.shape[1] // 3
    ffc = ff // PLANE
    plane_rows = PLANE * tok_rows
    halo = LMAX
    across = [[p * PLANE + i for p in range(planes)] for i in range(PLANE)]
    sibling = [(i, i ^ 1) for i in range(peers)]
    to_next = [(i, i + PLANE) for i in range(peers - PLANE)]
    to_prev = [(i + PLANE, i) for i in range(peers - PLANE)]
    me = lax.axis_index(AXIS)
    is_even = (me % 2) == 0
    plane_start = (me // PLANE) * plane_rows

    def split_features(value):
        value = value.reshape(value.shape[0], planes, 2, width // planes // 2)
        return value.transpose(0, 2, 1, 3).reshape(value.shape[0], width)

    def join_features(value):
        value = value.reshape(value.shape[0], 2, planes, width // planes // 2)
        return value.transpose(0, 2, 1, 3).reshape(value.shape[0], width)

    def gather_across(value):
        return lax.all_gather(value, AXIS, axis=0, tiled=True, axis_index_groups=across)

    def scatter_across(value):
        part = lax.psum_scatter(
            value.astype(BF16), AXIS, scatter_dimension=0, tiled=True, axis_index_groups=across
        )
        return part.reshape(PLANE, -1, part.shape[1])

    kv_full, q_rows, out_rows, gain_rows = lax.optimization_barrier(
        (*spread_attn(attn_weights, planes), norm_gains)
    )
    gain_block = jnp.pad(gain_rows.astype(F32), ((0, 8 - 4), (0, -share % 128)))
    gu_part, gain_blocks, kv_full, q_rows, out_rows = spread_gu(
        mlp_weights, gain_block, kv_full, q_rows, out_rows, peers
    )
    gain_full = gain_blocks[:, :4, :share].transpose(1, 0, 2).reshape(4, width)
    inputs = tokens.astype(F32)
    down_part, normed, kv_full, q_full = spread_down(
        mlp_weights, rms_forward(inputs, gain_full[0]).astype(BF16), kv_full, q_rows
    )
    q_cols, kv_cols = q_full.reshape(width, HD), kv_full.reshape(width, HD)
    gu_cols = gather_across(gu_part.reshape(-1, 2 * ffc))
    down_near = gather_across(down_part[: PLANE // 2].reshape(-1, ffc))
    down_far = gather_across(down_part[PLANE // 2 :].reshape(-1, ffc))

    query_index = plane_start + jnp.arange(plane_rows, dtype=jnp.int32)
    position = token_tables(seq_lengths, query_index)
    starts = (jnp.arange(plane_rows, dtype=jnp.int32) + halo - position)[:, None]
    frequency = 10000.0 ** (-jnp.arange(HD // 2, dtype=F32) * 2.0 / HD)
    angles = position.astype(F32)[:, None] * frequency[None, :]
    cosine, sine_part = jnp.cos(angles), jnp.sin(angles)
    kv_cosine = jnp.where(is_even, cosine, 1.0)
    kv_sine = jnp.where(is_even, sine_part, 0.0)

    kv_own = rotate(matmul(normed, kv_cols), kv_cosine, kv_sine).astype(BF16)
    kv_halo = lax.ppermute(kv_own[plane_rows - halo :], AXIS, to_next)
    kv_own, out_rows, q_cols = lax.optimization_barrier((kv_own, out_rows, q_cols))
    out_cols = spread_out(out_rows).reshape(width, HD)
    queries = rotate(matmul(normed, q_cols), cosine, sine_part).astype(BF16)
    kv_halo, out_cols, queries = lax.optimization_barrier((kv_halo, out_cols, queries))
    kv_mine = jnp.concatenate([kv_halo, kv_own], axis=0)
    kv_other = lax.ppermute(kv_mine, AXIS, sibling)
    key_rows = jnp.where(is_even, kv_mine, kv_other)
    value_rows = jnp.where(is_even, kv_other, kv_mine)
    attended, inverse = attend(queries, key_rows, value_rows, starts)
    attn_proj = product_scatter([attended], [out_cols], [0], PLANE_STEP, 2)

    middle = inputs + rms_forward(attn_proj, gain_full[1])
    mid_low = gather_square(rms_forward(middle, gain_full[2]).astype(BF16), PLANE_STEP, 1)
    gate_up = matmul(mid_low, gu_cols)
    gate, up = gate_up[:, :ffc], gate_up[:, ffc:]
    gelu, slope = gelu_parts(gate)
    hidden = (gelu * up).astype(BF16)
    hidden, gain_split, grad_split = lax.optimization_barrier(
        (hidden, split_features(gain_full[3:4]), split_features(cotangent))
    )
    raw_near = product_scatter([hidden], [down_near], [0], PLANE_STEP, 14)
    raw_far, grad_raw_low, down_grad = turn(
        hidden, down_far, raw_near, gain_split, grad_split, planes, PLANE_STEP, 9
    )
    mlp_raw = join_features(jnp.concatenate([raw_near, raw_far], axis=1))
    if not in_place(width // planes // 2):
        down_grad = join_features(down_grad.T).T
    layer_output = (middle + rms_forward(mlp_raw, gain_full[3])).astype(BF16)

    grad_out = cotangent.astype(F32)
    gain_four = jnp.sum(grad_out * mlp_raw * rms_parts(mlp_raw), axis=0)
    down_term = scatter_across(down_grad)
    grad_hidden = matmul(grad_raw_low, jnp.concatenate([down_near, down_far], axis=0))
    grad_normed_mid, gu_grad = product_scatter_back(
        [(slope * up * grad_hidden).astype(BF16), (gelu * grad_hidden).astype(BF16)],
        [gu_cols, gu_cols],
        [0, ffc],
        mid_low,
        PLANE_STEP,
        10,
    )
    gu_term = scatter_across(gu_grad)
    grad_mid_part, gain_three = rms_backward(middle, gain_full[2], grad_normed_mid)
    grad_middle = grad_out + grad_mid_part

    grad_proj, gain_two = rms_backward(attn_proj, gain_full[1], grad_middle)
    grad_proj_own, down_term = lax.optimization_barrier((grad_proj.astype(BF16), down_term))
    grad_proj_low = gather_square(grad_proj_own, PLANE_STEP, 1)
    grad_att = matmul(grad_proj_low, out_cols).astype(BF16)
    grad_query, grad_keys, grad_values = attend_back(
        queries, key_rows, value_rows, starts, inverse, grad_att
    )
    grad_mine = jnp.where(is_even, grad_keys, grad_values)
    grad_give = jnp.where(is_even, grad_values, grad_keys).astype(BF16)
    grad_kv = grad_mine + lax.ppermute(grad_give, AXIS, sibling).astype(F32)
    grad_back = lax.ppermute(grad_kv[:halo].astype(BF16), AXIS, to_prev).astype(F32)
    down_term, grad_kv = lax.optimization_barrier((down_term, grad_kv))
    down_rows = collect(down_term, 1, 6)
    down_rows, grad_back = lax.optimization_barrier((down_rows, grad_back))
    grad_kv = grad_kv[halo:] + jnp.pad(grad_back, ((plane_rows - halo, 0), (0, 0)))
    grad_q = rotate(grad_query, cosine, -sine_part).astype(BF16)
    grad_kv = rotate(grad_kv, kv_cosine, -kv_sine).astype(BF16)
    attn_term, grad_q, grad_kv = lax.optimization_barrier(
        (attn_grad(normed, grad_q, grad_kv, grad_proj_low, attended), grad_q, grad_kv)
    )
    attn_term = scatter_across(attn_term)
    grad_normed = product_scatter([grad_q, grad_kv], [q_cols, kv_cols], [0, 0], PLANE_STEP, 12)
    grad_in_part, gain_one = rms_backward(inputs, gain_full[0], grad_normed)
    grad_tokens = (grad_middle + grad_in_part).astype(BF16)

    gain_term = jnp.stack([gain_one, gain_two, gain_three, gain_four], axis=0)
    gain_term = gain_term.reshape(4, peers, share).transpose(1, 0, 2)
    gain_term = jnp.pad(gain_term, ((0, 0), (0, 8 - 4), (0, -share % 128)))
    gain_recv = collect_gains(gain_term)
    gu_term, gain_recv = lax.optimization_barrier((gu_term, gain_recv))
    gu_rows = collect(gu_term, 2, 13)
    grad_mlp = jnp.concatenate([gu_rows, down_rows], axis=1).astype(F32)
    grad_mlp, attn_term = lax.optimization_barrier((grad_mlp, attn_term))
    grad_attn = collect_attn(attn_term).astype(F32)
    grad_gains = jnp.sum(gain_recv[:, :4, :share], axis=0)
    return (layer_output, grad_tokens, grad_attn, grad_mlp, grad_gains)


def solution(mesh):
    return jax.shard_map(
        local,
        mesh=mesh,
        in_specs=(
            P("fsdp", None),
            P("fsdp", None),
            P("fsdp", None),
            P(None, "fsdp"),
            P(),
            P("fsdp", None),
        ),
        out_specs=(
            P("fsdp", None),
            P("fsdp", None),
            P("fsdp", None),
            P("fsdp", None),
            P(None, "fsdp"),
        ),
        check_vma=False,
    )
```
